32 devices in a mesh: dp: 16 (over z, x, core), mp: 2 (over y).
Axes of the slice: x: 2, y: 2, z: 4, core: 2. Of those that a mesh axis runs over, the one named last changes fastest.
Arguments:
- tokens: bfloat16 [2, 16384, 768], P(None, ('dp', 'mp')), may hold values from -6 to 6
- lengths: int32 [16, 4], P('dp'), may hold values from 1 to 682, 1024 in all within a row
- block_size: int32 [1], replicated, may hold values from 4 to 16
- cotangent: bfloat16 [2, 16384, 768], P(None, ('dp', 'mp')), may hold values from -6 to 6
- ln1_gain: float32 [768], replicated, may hold values from 0.5 to 1.5
- ln1_bias: float32 [768], replicated, may hold values from -1.5 to 1.5
- w_qkv: bfloat16 [768, 3, 768], P(None, None, 'mp'), may hold values from -0.21875 to 0.21875
- w_out: bfloat16 [768, 768], P('mp'), may hold values from -0.875 to 0.875
- ln2_gain: float32 [768], replicated, may hold values from 0.5 to 1.5
- ln2_bias: float32 [768], replicated, may hold values from -1.5 to 1.5
- w_up: bfloat16 [768, 3072], P(None, 'mp'), may hold values from -0.21875 to 0.21875
- b_up: bfloat16 [3072], P('mp'), may hold values from -1.5 to 1.5
- w_down: bfloat16 [3072, 768], P('mp'), may hold values from -0.109375 to 0.109375
- b_down: float32 [768], replicated, may hold values from -1.5 to 1.5
Outputs:
- out: bfloat16 [2, 16384, 768], P(None, ('dp', 'mp'))
- grad_tokens: float32 [2, 16384, 768], P(None, ('dp', 'mp'))
- grad_ln1_gain: float32 [768], replicated
- grad_ln1_bias: float32 [768], replicated
- grad_w_qkv: float32 [768, 3, 768], P(None, None, 'mp')
- grad_w_out: float32 [768, 768], P('mp')
- grad_ln2_gain: float32 [768], replicated
- grad_ln2_bias: float32 [768], replicated
- grad_w_up: float32 [768, 3072], P(None, 'mp')
- grad_b_up: float32 [3072], P('mp')
- grad_w_down: float32 [3072, 768], P('mp')
- grad_b_down: float32 [768], replicated
The draws below stay inside these ranges and needn't reach their ends.
Inputs may be any that keep to these rules, and one draw needn't show every extreme that they name: Each row lists the lengths of the 4 sequences packed in order into one pack of 1024 tokens; they sum to 1024 and the longest of each row is exactly 682.
All inputs are finite; a program needn't handle non-finite values.
Results may differ from the reference program's by a relative error of at most 0.011.
Values may be sent and summed in bfloat16 or wider, within the bound.
A program may use at most 256 MiB of HBM per device.

```python
import math
import jax
import jax.numpy as jnp
import numpy as np
from jax import lax

D = 768
HEADS = 12
HD = 64
FF = 3072
TOK_DEV = 1024
SEQS_DEV = 4
MAXLEN = 682
PACKS = 16
TOKENS = 16384


def steps_of(key, shape, cuts, low, top_value):
    loudness = 1.0
    for dim, parts in cuts:
        steps = jax.random.uniform(jax.random.fold_in(jax.random.fold_in(key, 6), dim), (parts,), jnp.float32, low / len(cuts), top_value / len(cuts))
        loudness = loudness * jnp.repeat(jnp.exp(steps), shape[dim] // parts).reshape((-1,) + (1,) * (len(shape) - 1 - dim))
    return loudness


def split_up(number_of, total, bound, skew):
    weights = [(1 << 20) // math.isqrt(grade ** skew) + 1 for grade in range(2, number_of + 1)]
    surplus, given = total - bound - (number_of - 1), [1] * (number_of - 1)
    while surplus > 0:
        free = [i for i in range(number_of - 1) if given[i] < bound]
        pool, remaining = sum([weights[i] for i in free]), surplus
        for i in free:
            more = min(bound - given[i], max(1, remaining * weights[i] // pool), surplus)
            given[i] = given[i] + more
            surplus = surplus - more
    return np.array([bound] + given)


def ragged(key, number_of, total, bound, lean):
    if number_of == 2:
        one = jax.random.randint(key, (), max(1, total - bound), min(bound, total - 1) + 1)
        return jnp.stack([one, total - one])
    tallies = jnp.asarray(split_up(number_of, total, bound, lean), jnp.int32)
    pairs = (number_of - 1) // 2
    donor, sink = tallies[1:1 + 2 * pairs:2], tallies[2:2 + 2 * pairs:2]
    room = jnp.minimum(donor - 1, bound - sink)
    shifted = jax.random.randint(jax.random.fold_in(key, 1), (pairs,), 0, 1 << 20) % (room + 1)
    tallies = tallies.at[1:1 + 2 * pairs:2].set(donor - shifted).at[2:2 + 2 * pairs:2].set(sink + shifted)
    return tallies[jax.random.permutation(jax.random.fold_in(key, 2), number_of)]


def scatter_about(key, dims, width, bound, shards=(), held_as=jnp.bfloat16):
    drawn = width * jax.random.normal(key, dims, jnp.float32)
    if shards:
        drawn = drawn * steps_of(key, dims, shards, -0.22, 0.18)
    return jnp.clip(drawn, -bound, bound).astype(held_as)


def setup_inputs(seed: int = 0) -> dict:
    splits = jax.random.split(jax.random.key(seed), 15)
    tokens = scatter_about(splits[0], (2, TOKENS, D), 1.0, 6.0, ((1, 32),))
    lengths = jax.vmap(lambda own: ragged(own, SEQS_DEV, TOK_DEV, MAXLEN, 2))(jax.random.split(splits[1], PACKS)).reshape((PACKS, SEQS_DEV)).astype(jnp.int32)
    block_size = jax.random.randint(splits[2], (1,), 4, 17).astype(jnp.int32)
    cotangent = scatter_about(splits[3], (2, TOKENS, D), 1.0, 6.0, ((1, 32),))
    ln1_gain = jnp.clip(1.0 + 0.1 * jax.random.normal(splits[4], (D,), jnp.float32), 0.5, 1.5)
    ln1_bias = scatter_about(splits[5], (D,), 0.3, 1.5, (), jnp.float32)
    w_qkv = scatter_about(splits[6], (D, 3, HEADS * HD), D ** -0.5, 0.21875, ((2, 2),))
    w_out = scatter_about(splits[7], (HEADS * HD, D), (HEADS * HD // 16) ** -0.5, 0.875, ((0, 2),))
    ln2_gain = jnp.clip(1.0 + 0.1 * jax.random.normal(splits[8], (D,), jnp.float32), 0.5, 1.5)
    ln2_bias = scatter_about(splits[9], (D,), 0.3, 1.5, (), jnp.float32)
    w_up = scatter_about(splits[10], (D, FF), D ** -0.5, 0.21875, ((1, 2),))
    b_up = scatter_about(splits[11], (FF,), 0.3, 1.5, ((0, 2),))
    w_down = scatter_about(splits[12], (FF, D), FF ** -0.5, 0.109375, ((0, 2),))
    b_down = scatter_about(splits[13], (D,), 0.3, 1.5, (), jnp.float32)
    return {"tokens": tokens, "lengths": lengths, "block_size": block_size, "cotangent": cotangent, "ln1_gain": ln1_gain, "ln1_bias": ln1_bias, "w_qkv": w_qkv, "w_out": w_out, "ln2_gain": ln2_gain, "ln2_bias": ln2_bias, "w_up": w_up, "b_up": b_up, "w_down": w_down, "b_down": b_down}


@jax.custom_vjp
def low(v):
    return lax.optimization_barrier(v.astype(jnp.bfloat16)).astype(jnp.float32)

@jax.custom_vjp
def low_back(v):
    return v

def low_keep(v):
    return (low(v), None)

def low_pass(kept, grad):
    return (grad,)

def back_keep(v):
    return (v, None)

def back_low(kept, grad):
    return (low(grad),)
low.defvjp(low_keep, low_pass)
low_back.defvjp(back_keep, back_low)
epsilon = 1e-05
neg_large = -1e+30
highest = lax.Precision.HIGHEST

def layer_norm(values, norm_gain, norm_bias):
    average = lax.optimization_barrier(jnp.mean(values, axis=-1, keepdims=True))
    centred = values - average
    variance = lax.optimization_barrier(jnp.mean(centred * centred, axis=-1, keepdims=True))
    return centred * lax.rsqrt(variance + epsilon) * norm_gain + norm_bias

def gelu_tanh(values):
    inner = 0.7978845608028654 * (values + 0.044715 * values * values * values)
    return 0.5 * values * (1.0 + jnp.tanh(inner))

def pack_layout(seq_lengths, block_len, tokens_count):
    token_index = jnp.arange(tokens_count, dtype=jnp.int32)
    seq_ends = jnp.cumsum(seq_lengths).astype(jnp.int32)
    passed = token_index[:, None] >= seq_ends[None, :]
    doc_ids = lax.optimization_barrier(jnp.sum(passed.astype(jnp.int32), axis=1)).astype(jnp.int32)
    starts = lax.optimization_barrier(jnp.sum(jnp.where(passed, seq_lengths[None, :], 0), axis=1)).astype(jnp.int32)
    positions = token_index - starts
    blocks = (positions // block_len).astype(jnp.int32)
    return (doc_ids, positions, blocks)

def rotary_tables(positions, head_dim):
    half_dim = head_dim // 2
    frequency = jnp.exp(jnp.arange(half_dim, dtype=jnp.float32) * (-math.log(10000.0) / half_dim))
    angles = positions.astype(jnp.float32)[:, None] * frequency[None, :]
    return (jnp.cos(angles), jnp.sin(angles))

def rotate(field, cosine, sine):
    half_dim = field.shape[-1] // 2
    first = field[..., :half_dim]
    second = field[..., half_dim:]
    cos_rows = cosine[:, None, :]
    sin_rows = sine[:, None, :]
    return jnp.concatenate([first * cos_rows - second * sin_rows, second * cos_rows + first * sin_rows], axis=-1)

def allowed_keys(query_noisy, query_doc, query_block, key_noisy, key_doc, key_block):
    same_doc = query_doc[:, None] == key_doc[None, :]
    key_flag = key_noisy[None, :]
    noisy_rule = jnp.where(key_flag, key_block[None, :] == query_block[:, None], key_block[None, :] < query_block[:, None])
    clean_rule = jnp.logical_and(jnp.logical_not(key_flag), key_block[None, :] <= query_block[:, None])
    return jnp.logical_and(same_doc, jnp.where(query_noisy[:, None], noisy_rule, clean_rule))

def forward(x_pack, ln1_gain, ln1_bias, w_qkv, w_out, ln2_gain, ln2_bias, w_up, b_up, w_down, b_down, row_doc, row_block, row_noisy, row_cos, row_sin):
    row_count = 2 * TOK_DEV
    rows_in = x_pack.reshape(row_count, D)
    normed1 = low(layer_norm(rows_in, ln1_gain, ln1_bias))
    qkv = low_back(jnp.einsum('rd,dcf->rcf', normed1, w_qkv, precision=highest))
    query = low(rotate(qkv[:, 0].reshape(row_count, HEADS, HD), row_cos, row_sin))
    keys = low(rotate(qkv[:, 1].reshape(row_count, HEADS, HD), row_cos, row_sin))
    values = low(qkv[:, 2].reshape(row_count, HEADS, HD))
    block_rows = min(512, TOK_DEV)
    count = row_count // block_rows

    def attend(item):
        query_blk, doc_blk, block_blk, noisy_blk = item
        raw = jnp.einsum('qhe,khe->hqk', query_blk, keys, precision=highest)
        scores = low_back(raw) * 0.125
        mask = allowed_keys(noisy_blk, doc_blk, block_blk, row_noisy, row_doc, row_block)
        masked = jnp.where(mask[None], scores, neg_large)
        row_top = lax.optimization_barrier(jnp.max(masked, axis=-1, keepdims=True))
        expo = jnp.exp(masked - row_top)
        probs = low(expo / lax.optimization_barrier(jnp.sum(expo, axis=-1, keepdims=True)))
        return jnp.einsum('hqk,khe->qhe', probs, values, precision=highest)
    items = (query.reshape(count, block_rows, HEADS, HD), row_doc.reshape(count, block_rows), row_block.reshape(count, block_rows), row_noisy.reshape(count, block_rows))
    attended = lax.map(jax.checkpoint(attend), items)
    attended = low(low_back(attended.reshape(row_count, HEADS * HD)))
    branch = low_back(jnp.dot(attended, w_out, precision=highest))
    mid = rows_in + branch
    normed2 = low(layer_norm(mid, ln2_gain, ln2_bias))
    pre = low_back(jnp.dot(normed2, w_up, precision=highest) + b_up)
    act = low(gelu_tanh(pre))
    down = low_back(jnp.dot(act, w_down, precision=highest))
    return (mid + down + b_down).reshape(2, TOK_DEV, D)

def reference(tokens, lengths, block_size, cotangent, ln1_gain, ln1_bias, w_qkv, w_out, ln2_gain, ln2_bias, w_up, b_up, w_down, b_down):
    params = tuple((value.astype(jnp.float32) for value in (ln1_gain, ln1_bias, w_qkv, w_out, ln2_gain, ln2_bias, w_up, b_up, w_down, b_down)))
    block_len = block_size[0]
    x_packs = tokens.astype(jnp.float32).reshape(2, PACKS, TOK_DEV, D).transpose(1, 0, 2, 3)
    d_packs = cotangent.astype(jnp.float32).reshape(2, PACKS, TOK_DEV, D).transpose(1, 0, 2, 3)

    def one_pack(totals, item):
        x_pack, d_pack, seq_lengths = item
        doc_ids, positions, blocks = pack_layout(seq_lengths, block_len, TOK_DEV)
        cosine, sine = rotary_tables(positions, HD)
        row_doc = jnp.concatenate([doc_ids, doc_ids])
        row_block = jnp.concatenate([blocks, blocks])
        row_noisy = jnp.arange(2 * TOK_DEV, dtype=jnp.int32) < TOK_DEV
        row_cos = jnp.concatenate([cosine, cosine])
        row_sin = jnp.concatenate([sine, sine])

        def layer(x_value, *weights):
            return forward(x_value, *weights, row_doc, row_block, row_noisy, row_cos, row_sin)
        out_pack, pullback = jax.vjp(layer, x_pack, *params)
        grads = pullback(d_pack)
        totals = tuple((left + right for left, right in zip(totals, grads[1:])))
        return (totals, (out_pack, grads[0]))
    zeros = tuple((jnp.zeros_like(value) for value in params))
    totals, (outs, d_tokens) = lax.scan(one_pack, zeros, (x_packs, d_packs, lengths))
    out = outs.transpose(1, 0, 2, 3).reshape(2, TOKENS, D).astype(jnp.bfloat16)
    grad_tokens = d_tokens.transpose(1, 0, 2, 3).reshape(2, TOKENS, D)
    return (out, grad_tokens, totals[0], totals[1], totals[2], totals[3], totals[4], totals[5], totals[6], totals[7], totals[8], totals[9])
```

```python
import functools
import math

import jax
import jax.numpy as jnp
from jax import lax
from jax.experimental import pallas as pl
from jax.experimental.pallas import tpu as pltpu
from jax.sharding import PartitionSpec as P

HD = 64
TOK_DEV = 1024
HALF = TOK_DEV // 2
EDGE = 16
CLEAN_OWN = HALF
NOISY_BASE = 2 * HALF + EDGE
NOISY_OWN = NOISY_BASE + EDGE
KEY_ROWS = NOISY_OWN + HALF + EDGE
TILE = 128
TILES = HALF // TILE
WINDOW = TILE + 2 * EDGE
KEY_TILE = 256
LANES = 128

epsilon = 1e-05
neg_large = -1e30
to_base2 = 0.125 * math.log2(math.e)
f32 = jnp.float32
bf16 = jnp.bfloat16

NN = (((1,), (0,)), ((), ()))
NT = (((1,), (1,)), ((), ()))


def dot(left, right, dims=NN):
    return lax.dot_general(left, right, dims, preferred_element_type=f32)


def layer_norm(values, norm_gain, norm_bias):
    average = jnp.mean(values, axis=-1, keepdims=True)
    centred = values - average
    variance = jnp.mean(centred * centred, axis=-1, keepdims=True)
    return centred * lax.rsqrt(variance + epsilon) * norm_gain + norm_bias


def gelu_tanh(values):
    inner = 0.7978845608028654 * (values + 0.044715 * values * values * values)
    return 0.5 * values * (1.0 + jnp.tanh(inner))


def low_lanes(shape):
    return lax.broadcasted_iota(jnp.int32, shape, 1) < HD


def turn(values, cosine, sine):
    lane = lax.broadcasted_iota(jnp.int32, values.shape, 1)
    first_half = (lane & (HD - 1)) < HD // 2
    swapped = jnp.where(
        first_half,
        pltpu.roll(values, LANES - HD // 2, 1),
        pltpu.roll(values, HD // 2, 1),
    )
    return values * cosine + swapped * sine


def project_kernel(rows_ref, w_ref, cos_ref, sin_ref, q_ref, k_ref, v_ref):
    rows = rows_ref[...]
    cosine, sine = cos_ref[...], sin_ref[...]
    for part, out_ref in ((0, q_ref), (1, k_ref)):
        field = dot(rows, w_ref[part])
        for pair in range(field.shape[1] // LANES):
            cols = slice(pair * LANES, (pair + 1) * LANES)
            out_ref[:, cols] = turn(field[:, cols], cosine, sine).astype(bf16)
    v_ref[...] = dot(rows, w_ref[2]).astype(bf16)


def project(rows, weights, cosine, sine):
    count, width = rows.shape
    cols = weights.shape[2]
    step = count // 9
    row_spec = pl.BlockSpec((step, width), lambda i: (i, 0))
    table_spec = pl.BlockSpec((step, LANES), lambda i: (i, 0))
    out_spec = pl.BlockSpec((step, cols), lambda i: (i, 0))
    shape = jax.ShapeDtypeStruct((count, cols), bf16)
    return pl.pallas_call(
        project_kernel,
        grid=(9,),
        in_specs=[
            row_spec,
            pl.BlockSpec(weights.shape, lambda i: (0, 0, 0)),
            table_spec,
            table_spec,
        ],
        out_specs=[out_spec] * 3,
        out_shape=[shape] * 3,
        name="project",
        cost_estimate=pl.CostEstimate(
            flops=2 * count * width * 3 * cols,
            bytes_accessed=2 * (count * (width + 3 * cols) + 3 * width * cols),
            transcendentals=0,
        ),
    )(rows, weights, cosine, sine)


def split_heads(rows):
    low = low_lanes(rows.shape)
    zero = jnp.zeros_like(rows)
    return jnp.where(low, rows, zero), jnp.where(low, zero, rows)


def between(shape, offset, low, high):
    index = lax.broadcasted_iota(jnp.int32, shape, 0) + offset
    return jnp.logical_and(index >= low, index < high)


def forward_kernel(
    span_ref, clean_ref, noisy_ref, q_ref, k_ref, v_ref, out_ref, lse_ref
):
    def one_tile(t, _):
        clean_at = pl.multiple_of(CLEAN_OWN + t * TILE, TILE)
        noisy_at = pl.multiple_of(NOISY_OWN + t * TILE, EDGE)
        window_at = pl.multiple_of(NOISY_BASE + t * TILE, EDGE)
        query = jnp.concatenate(
            [q_ref[pl.ds(noisy_at, TILE), :], q_ref[pl.ds(clean_at, TILE), :]], axis=0
        )
        queries = split_heads(query)
        key_low, key_high = clean_ref[t, 0:1, :], clean_ref[t, 1:2, :]
        own_low, own_high = noisy_ref[t, 0:1, :], noisy_ref[t, 1:2, :]
        keys = k_ref[pl.ds(window_at, WINDOW), :]
        values_t = v_ref[pl.ds(window_at, WINDOW), :].T
        allowed = between((WINDOW, TILE), 0, own_low, own_high)
        state = []
        for head in range(2):
            scores = dot(keys, queries[head][:TILE], NT) * to_base2
            scores = jnp.where(allowed, scores, neg_large)
            top = jnp.max(scores, axis=0, keepdims=True)
            expo = jnp.exp2(scores - top)
            total = jnp.sum(expo, axis=0, keepdims=True)
            mixed = dot(values_t[head * HD : (head + 1) * HD], expo.astype(bf16))
            blank = jnp.zeros((1, TILE), f32)
            state += [
                jnp.concatenate([top, blank + neg_large], axis=1),
                jnp.concatenate([total, blank], axis=1),
                jnp.concatenate([mixed, jnp.zeros((HD, TILE), f32)], axis=1),
            ]
        first_key, trips = span_ref[t, 0], span_ref[t, 1]

        def one_step(j, state):
            at = pl.multiple_of(first_key + j * KEY_TILE, EDGE)
            keys = k_ref[pl.ds(at, KEY_TILE), :]
            values_t = v_ref[pl.ds(at, KEY_TILE), :].T
            allowed = between((KEY_TILE, 2 * TILE), at, key_low, key_high)
            after = []
            for head in range(2):
                top, total, mixed = state[3 * head : 3 * head + 3]
                scores = dot(keys, queries[head], NT) * to_base2
                scores = jnp.where(allowed, scores, neg_large)
                new_top = jnp.maximum(top, jnp.max(scores, axis=0, keepdims=True))
                keep = jnp.exp2(top - new_top)
                expo = jnp.exp2(scores - new_top)
                after += [
                    new_top,
                    total * keep + jnp.sum(expo, axis=0, keepdims=True),
                    mixed * keep
                    + dot(values_t[head * HD : (head + 1) * HD], expo.astype(bf16)),
                ]
            return tuple(after)

        state = lax.fori_loop(0, trips, one_step, tuple(state))
        pair = jnp.concatenate(
            [state[2] / state[1], state[5] / state[4]], axis=0
        ).T.astype(bf16)
        out_at = pl.multiple_of(t * TILE, TILE)
        out_ref[pl.ds(out_at, TILE), :] = pair[:TILE]
        out_ref[pl.ds(pl.multiple_of(HALF + t * TILE, TILE), TILE), :] = pair[TILE:]
        lse_ref[0, t, 0:1, :] = state[0] + jnp.log2(state[1])
        lse_ref[0, t, 1:2, :] = state[3] + jnp.log2(state[4])
        return 0

    lax.fori_loop(0, TILES, one_tile, 0)


def attend_forward(spans, clean_bounds, noisy_bounds, query, keys, values):
    count, cols = query.shape
    pairs = cols // LANES
    whole3 = lambda array: pl.BlockSpec(array.shape, lambda p, s: (0, 0, 0))
    row_spec = pl.BlockSpec((count, LANES), lambda p, s: (0, p))
    work = pairs * 2 * 2 * HALF * TOK_DEV
    return pl.pallas_call(
        forward_kernel,
        grid_spec=pltpu.PrefetchScalarGridSpec(
            num_scalar_prefetch=1,
            grid=(pairs,),
            in_specs=[whole3(clean_bounds), whole3(noisy_bounds)] + [row_spec] * 3,
            out_specs=[
                pl.BlockSpec((TOK_DEV, LANES), lambda p, s: (0, p)),
                pl.BlockSpec((1, TILES, 2, 2 * TILE), lambda p, s: (p, 0, 0, 0)),
            ],
        ),
        out_shape=[
            jax.ShapeDtypeStruct((TOK_DEV, cols), bf16),
            jax.ShapeDtypeStruct((pairs, TILES, 2, 2 * TILE), f32),
        ],
        name="attend_forward",
        cost_estimate=pl.CostEstimate(
            flops=4 * work * HD, bytes_accessed=8 * count * cols, transcendentals=work
        ),
    )(spans, clean_bounds, noisy_bounds, query, keys, values)


def backward_kernel(
    span_ref,
    clean_ref,
    noisy_ref,
    q_ref,
    k_ref,
    v_ref,
    o_ref,
    d_ref,
    lse_ref,
    cos_ref,
    sin_ref,
    out_ref,
    dk_ref,
    dv_ref,
):
    dk_ref[...] = jnp.zeros_like(dk_ref)
    dv_ref[...] = jnp.zeros_like(dv_ref)
    out_ref[0] = jnp.zeros_like(out_ref[0])

    def one_tile(t, _):
        clean_at = pl.multiple_of(CLEAN_OWN + t * TILE, TILE)
        noisy_at = pl.multiple_of(NOISY_OWN + t * TILE, EDGE)
        window_at = pl.multiple_of(NOISY_BASE + t * TILE, EDGE)
        low_at = pl.multiple_of(t * TILE, TILE)
        high_at = pl.multiple_of(HALF + t * TILE, TILE)

        def both(ref, low, high):
            return jnp.concatenate(
                [ref[pl.ds(low, TILE), :], ref[pl.ds(high, TILE), :]], axis=0
            )

        query = split_heads(both(q_ref, noisy_at, clean_at))
        d_rows = both(d_ref, low_at, high_at)
        o_rows = both(o_ref, low_at, high_at)
        product = (d_rows.astype(f32) * o_rows.astype(f32)).T
        d_out = split_heads(d_rows)
        inner = [
            jnp.sum(product[head * HD : (head + 1) * HD], axis=0, keepdims=True)
            for head in range(2)
        ]
        lse = [lse_ref[0, t, head : head + 1, :] for head in range(2)]
        key_low, key_high = clean_ref[t, 0:1, :], clean_ref[t, 1:2, :]
        own_low, own_high = noisy_ref[t, 0:1, :], noisy_ref[t, 1:2, :]

        def accumulate(at, rows, cols, allowed, d_query):
            keys = k_ref[pl.ds(at, rows), :]
            values = v_ref[pl.ds(at, rows), :]
            keys_t = keys.T
            weights, d_scores, after = [], [], []
            for head in range(2):
                scores = dot(keys, query[head][:cols], NT) * to_base2
                scores = jnp.where(allowed, scores - lse[head][:, :cols], neg_large)
                probs = jnp.exp2(scores)
                d_probs = dot(values, d_out[head][:cols], NT)
                d_score = (probs * (d_probs - inner[head][:, :cols]) * 0.125).astype(bf16)
                weights.append(probs.astype(bf16))
                d_scores.append(d_score)
                after.append(
                    d_query[head] + dot(keys_t[head * HD : (head + 1) * HD], d_score)
                )
            stack = lambda parts: jnp.concatenate([part[:cols] for part in parts], axis=0)
            dv_ref[pl.ds(at, rows), :] += dot(
                jnp.concatenate(weights, axis=1), stack(d_out)
            )
            dk_ref[pl.ds(at, rows), :] += dot(
                jnp.concatenate(d_scores, axis=1), stack(query)
            )
            return tuple(after)

        allowed = between((WINDOW, TILE), 0, own_low, own_high)
        zero = jnp.zeros((HD, TILE), f32)
        start = accumulate(window_at, WINDOW, TILE, allowed, (zero, zero))
        start = tuple(jnp.concatenate([part, zero], axis=1) for part in start)
        first_key, trips = span_ref[t, 0], span_ref[t, 1]

        def one_step(j, d_query):
            at = pl.multiple_of(first_key + j * KEY_TILE, EDGE)
            allowed = between((KEY_TILE, 2 * TILE), at, key_low, key_high)
            return accumulate(at, KEY_TILE, 2 * TILE, allowed, d_query)

        d_query = lax.fori_loop(0, trips, one_step, start)
        d_query = jnp.concatenate(d_query, axis=0).T
        for at, part in ((noisy_at, d_query[:TILE]), (clean_at, d_query[TILE:])):
            turned = turn(part, cos_ref[pl.ds(at, TILE), :], -sin_ref[pl.ds(at, TILE), :])
            out_ref[0, pl.ds(at, TILE), :] = turned.astype(bf16)
        return 0

    lax.fori_loop(0, TILES, one_tile, 0)
    step = KEY_ROWS // 9

    def finish(i, _):
        rows = pl.ds(pl.multiple_of(i * step, EDGE), step)
        out_ref[1, rows, :] = turn(dk_ref[rows, :], cos_ref[rows, :], -sin_ref[rows, :]).astype(
            bf16
        )
        out_ref[2, rows, :] = dv_ref[rows, :].astype(bf16)
        return 0

    lax.fori_loop(0, 9, finish, 0)


def attend_backward(
    spans, clean_bounds, noisy_bounds, query, keys, values, attended, d_attended, lse, cosine, sine
):
    count, cols = query.shape
    pairs = cols // LANES
    whole2 = lambda array: pl.BlockSpec(array.shape, lambda p, s: (0, 0))
    whole3 = lambda array: pl.BlockSpec(array.shape, lambda p, s: (0, 0, 0))
    row_spec = pl.BlockSpec((count, LANES), lambda p, s: (0, p))
    own_spec = pl.BlockSpec((TOK_DEV, LANES), lambda p, s: (0, p))
    work = pairs * 2 * 2 * HALF * TOK_DEV
    return pl.pallas_call(
        backward_kernel,
        grid_spec=pltpu.PrefetchScalarGridSpec(
            num_scalar_prefetch=1,
            grid=(pairs,),
            in_specs=[whole3(clean_bounds), whole3(noisy_bounds)]
            + [row_spec] * 3
            + [own_spec] * 2
            + [
                pl.BlockSpec((1, TILES, 2, 2 * TILE), lambda p, s: (p, 0, 0, 0)),
                whole2(cosine),
                whole2(sine),
            ],
            out_specs=pl.BlockSpec((3, count, LANES), lambda p, s: (0, 0, p)),
            scratch_shapes=[pltpu.VMEM((count, LANES), f32)] * 2,
        ),
        out_shape=jax.ShapeDtypeStruct((3, count, cols), bf16),
        name="attend_backward",
        cost_estimate=pl.CostEstimate(
            flops=10 * work * HD, bytes_accessed=16 * count * cols, transcendentals=work
        ),
    )(
        spans,
        clean_bounds,
        noisy_bounds,
        query,
        keys,
        values,
        attended,
        d_attended,
        lse,
        cosine,
        sine,
    )


def key_layout(seq_lengths, block_len, part):
    index = jnp.arange(KEY_ROWS, dtype=jnp.int32)
    own = part * HALF
    token = jnp.where(
        index < NOISY_BASE, index + (own - HALF), index - NOISY_BASE + (own - EDGE)
    )
    ends = jnp.cumsum(seq_lengths)
    passed = token[:, None] >= ends[None, :]
    starts = jnp.sum(jnp.where(passed, seq_lengths[None, :], 0), axis=1)
    lengths_here = jnp.where(passed, 0, ends[None, :])
    stops = jnp.min(jnp.where(passed, TOK_DEV, lengths_here), axis=1)
    positions = token - starts
    block_start = starts + positions // block_len * block_len
    block_stop = jnp.minimum(block_start + block_len, stops)
    mine = slice(CLEAN_OWN, CLEAN_OWN + HALF)
    low, start, stop = starts[mine], block_start[mine], block_stop[mine]
    to_clean = own - HALF
    tiles = lambda column: column.reshape(TILES, 1, TILE)
    clean_bounds = jnp.concatenate(
        [
            jnp.concatenate([tiles(low - to_clean), tiles(low - to_clean)], axis=2),
            jnp.concatenate([tiles(start - to_clean), tiles(stop - to_clean)], axis=2),
        ],
        axis=1,
    )
    to_window = own - EDGE + TILE * jnp.arange(TILES, dtype=jnp.int32)[:, None, None]
    noisy_bounds = jnp.concatenate(
        [tiles(start) - to_window, tiles(stop) - to_window], axis=1
    )
    first = jnp.min(clean_bounds[:, 0], axis=1) // EDGE * EDGE
    last = jnp.max(clean_bounds[:, 1], axis=1)
    trips = (last - first + KEY_TILE - 1) // KEY_TILE
    spans = jnp.stack([first, trips], axis=1)
    lane = jnp.arange(LANES, dtype=jnp.int32)
    frequency = jnp.exp(
        (lane % (HD // 2)).astype(f32) * (-math.log(10000.0) / (HD // 2))
    )
    angles = positions.astype(f32)[:, None] * frequency[None, :]
    sign = jnp.where(lane % HD < HD // 2, -1.0, 1.0)
    return spans, clean_bounds, noisy_bounds, jnp.cos(angles), jnp.sin(angles) * sign


def half_of(array, which):
    size = array.shape[0] // 2
    return lax.dynamic_slice_in_dim(array, which * size, size, 0)


def in_order(bit, mine, theirs):
    flip = bit == 0
    return jnp.concatenate(
        [jnp.where(flip, mine, theirs), jnp.where(flip, theirs, mine)], axis=0
    )


def local(
    dp_size,
    tokens,
    lengths,
    block_size,
    cotangent,
    ln1_gain,
    ln1_bias,
    w_qkv,
    w_out,
    ln2_gain,
    ln2_bias,
    w_up,
    b_up,
    w_down,
    b_down,
):
    width = tokens.shape[2]
    part = lax.axis_index("mp")
    place = lax.axis_index("dp")
    bits = dp_size.bit_length() - 1
    across = [(0, 1), (1, 0)]
    flips = [[(i, i ^ (1 << b)) for i in range(dp_size)] for b in range(bits)]
    my_bit = [(place >> b) & 1 for b in range(bits)]

    def to_partner(array):
        return lax.ppermute(array, "mp", across)

    def to_flip(array, b):
        return lax.ppermute(array, "dp", flips[b])

    def fetch(weights):
        here = to_partner(half_of(weights, my_bit[0]))
        there = to_flip(here, 0)
        return in_order(my_bit[0], here, there)

    def reduce_over_all(mine, others):
        core = my_bit[0]
        got = to_flip(half_of(others, 1 - core).astype(bf16), 0)
        crossing = half_of(others, core) + got.astype(f32)
        got_own = to_flip(half_of(mine, 1 - core).astype(bf16), 0)
        total = half_of(mine, core) + got_own.astype(f32)
        total = total + to_partner(crossing.astype(bf16)).astype(f32)
        for b in range(1, bits):
            got = to_flip(half_of(total, 1 - my_bit[b]).astype(bf16), b)
            total = half_of(total, my_bit[b]) + got.astype(f32)
        total = total.astype(bf16)
        for b in reversed(range(bits)):
            total = in_order(my_bit[b], total, to_flip(total, b))
        return total.astype(f32)

    edge = jnp.where(part == 0, tokens[0, HALF - EDGE :], tokens[0, :EDGE])
    context = to_partner(jnp.concatenate([tokens[1], edge], axis=0))
    qkv_mine = w_qkv.transpose(1, 0, 2)
    qkv_other = fetch(w_qkv.transpose(1, 0, 2).reshape(-1, w_qkv.shape[2])).reshape(
        qkv_mine.shape
    )
    out_other = fetch(w_out)
    up_other = fetch(w_up)
    bias_other = to_partner(b_up)
    down_other = fetch(w_down)

    spans, clean_bounds, noisy_bounds, cosine, sine = key_layout(lengths[0], block_size[0], part)
    clean_other, edge_other = context[:HALF], context[HALF:]
    key_tokens = jnp.concatenate(
        [clean_other, tokens[1], clean_other[:EDGE], edge_other, tokens[0], edge_other], axis=0
    )
    normed1_keys = layer_norm(key_tokens.astype(f32), ln1_gain, ln1_bias).astype(bf16)

    saved = []
    for weights in (qkv_mine, qkv_other):
        query, keys, values = project(normed1_keys, weights, cosine, sine)
        attended, lse = attend_forward(spans, clean_bounds, noisy_bounds, query, keys, values)
        saved.append((query, keys, values, attended, lse))

    x_rows = tokens.astype(f32).reshape(TOK_DEV, width)
    branch = dot(saved[0][3], w_out) + dot(saved[1][3], out_other)
    mid = x_rows + branch
    normed2, norm2_back = jax.vjp(layer_norm, mid, ln2_gain, ln2_bias)
    mlp_rows = normed2.astype(bf16)
    d_low = cotangent.reshape(TOK_DEV, width)
    d_out_rows = d_low.astype(f32)
    grad_b_down = jnp.sum(d_out_rows, axis=0)
    down = 0.0
    d_normed2 = 0.0
    grad_down, grad_up, grad_up_bias = [], [], []
    for up, bias, down_w in ((w_up, b_up, w_down), (up_other, bias_other, down_other)):
        pre = dot(mlp_rows, up) + bias.astype(f32)
        act_low = gelu_tanh(pre).astype(bf16)
        down = down + dot(act_low, down_w)
        d_act = dot(d_low, down_w, NT)
        d_pre = jax.vjp(gelu_tanh, pre)[1](d_act)[0].astype(bf16)
        grad_down.append(jnp.einsum("rf,rd->fd", act_low, d_low, preferred_element_type=f32))
        grad_up.append(jnp.einsum("rd,rf->df", mlp_rows, d_pre, preferred_element_type=f32))
        grad_up_bias.append(jnp.sum(d_pre.astype(f32), axis=0))
        d_normed2 = d_normed2 + dot(d_pre, up, NT)
    out = (mid + down + b_down).astype(bf16).reshape(tokens.shape)
    grad_down = reduce_over_all(*grad_down)
    grad_up = reduce_over_all(*grad_up)

    d_mid_norm, grad_ln2_gain, grad_ln2_bias = norm2_back(d_normed2)
    d_mid = d_out_rows + d_mid_norm
    d_branch = d_mid.astype(bf16)
    grad_out = []
    d_attended = []
    for item, weights in zip(saved, (w_out, out_other)):
        grad_out.append(jnp.einsum("rf,rd->fd", item[3], d_branch, preferred_element_type=f32))
        d_attended.append(dot(d_branch, weights, NT).astype(bf16))
    grad_out = reduce_over_all(*grad_out)

    grad_qkv = [None, None]
    d_normed1_keys = 0.0
    for group, weights in ((1, qkv_other), (0, qkv_mine)):
        query, keys, values, attended, lse = saved[group]
        d_qkv = attend_backward(
            spans,
            clean_bounds,
            noisy_bounds,
            query,
            keys,
            values,
            attended,
            d_attended[group],
            lse,
            cosine,
            sine,
        )
        grad_qkv[group] = jnp.einsum(
            "rd,crf->cdf", normed1_keys, d_qkv, preferred_element_type=f32
        ).reshape(-1, d_qkv.shape[2])
        d_normed1_keys = d_normed1_keys + jnp.einsum(
            "crf,cdf->rd", d_qkv, weights, preferred_element_type=f32
        )
    grad_qkv = reduce_over_all(*grad_qkv).reshape(qkv_mine.shape).transpose(1, 0, 2)

    clean_back = d_normed1_keys[:HALF]
    clean_back = clean_back.at[:EDGE].add(d_normed1_keys[2 * HALF : 2 * HALF + EDGE])
    edge_back = d_normed1_keys[NOISY_BASE:NOISY_OWN] + d_normed1_keys[NOISY_OWN + HALF :]
    back = to_partner(jnp.concatenate([clean_back, edge_back], axis=0).astype(bf16)).astype(f32)
    at_end = jnp.concatenate([jnp.zeros((HALF - EDGE, width), f32), back[HALF:]], axis=0)
    at_start = jnp.concatenate([back[HALF:], jnp.zeros((HALF - EDGE, width), f32)], axis=0)
    d_normed1 = jnp.concatenate(
        [
            d_normed1_keys[NOISY_OWN : NOISY_OWN + HALF]
            + jnp.where(part == 0, at_end, at_start),
            d_normed1_keys[CLEAN_OWN : CLEAN_OWN + HALF] + back[:HALF],
        ],
        axis=0,
    )
    norm1_back = jax.vjp(layer_norm, x_rows, ln1_gain, ln1_bias)[1]
    d_x_norm, grad_ln1_gain, grad_ln1_bias = norm1_back(d_normed1)
    grad_tokens = (d_mid + d_x_norm).reshape(tokens.shape)

    bias_sum = to_partner(grad_up_bias[1]) + grad_up_bias[0]
    hidden = bias_sum.shape[0]
    own_bias = jnp.concatenate([jnp.where(part == 0, bias_sum, 0.0), jnp.where(part == 0, 0.0, bias_sum)])
    small = lax.psum(
        jnp.concatenate(
            [own_bias, grad_ln1_gain, grad_ln1_bias, grad_ln2_gain, grad_ln2_bias, grad_b_down]
        ),
        ("dp", "mp"),
    )
    grad_up_bias = lax.dynamic_slice_in_dim(small, part * hidden, hidden, 0)
    rest = [small[2 * hidden + i * width : 2 * hidden + (i + 1) * width] for i in range(5)]
    return (
        out,
        grad_tokens,
        rest[0],
        rest[1],
        grad_qkv,
        grad_out,
        rest[2],
        rest[3],
        grad_up,
        grad_up_bias,
        grad_down,
        rest[4],
    )


def solution(mesh):
    in_specs = (
        P(None, ("dp", "mp"), None),
        P("dp", None),
        P(),
        P(None, ("dp", "mp"), None),
        P(),
        P(),
        P(None, None, "mp"),
        P("mp", None),
        P(),
        P(),
        P(None, "mp"),
        P("mp"),
        P("mp", None),
        P(),
    )
    out_specs = (
        P(None, ("dp", "mp"), None),
        P(None, ("dp", "mp"), None),
        P(),
        P(),
        P(None, None, "mp"),
        P("mp", None),
        P(),
        P(),
        P(None, "mp"),
        P("mp"),
        P("mp", None),
        P(),
    )
    return jax.shard_map(
        functools.partial(local, mesh.shape["dp"]),
        mesh=mesh,
        in_specs=in_specs,
        out_specs=out_specs,
        check_vma=False,
    )
```

```python
import functools
import math

import jax
import jax.numpy as jnp
from jax import lax
from jax.experimental import pallas as pl
from jax.experimental.pallas import tpu as pltpu
from jax.sharding import PartitionSpec as P

HD = 64
TOK_DEV = 1024
HALF = TOK_DEV // 2
EDGE = 16
CLEAN_OWN = HALF
NOISY_BASE = 2 * HALF + EDGE
NOISY_OWN = NOISY_BASE + EDGE
KEY_ROWS = NOISY_OWN + HALF + EDGE
TILE = 128
TILES = HALF // TILE
WINDOW = TILE + 2 * EDGE
KEY_TILE = 256
LANES = 128

epsilon = 1e-05
neg_large = -1e30
to_base2 = 0.125 * math.log2(math.e)
f32 = jnp.float32
bf16 = jnp.bfloat16

NN = (((1,), (0,)), ((), ()))
NT = (((1,), (1,)), ((), ()))


def dot(left, right, dims=NN):
    return lax.dot_general(left, right, dims, preferred_element_type=f32)


def layer_norm(values, norm_gain, norm_bias):
    average = jnp.mean(values, axis=-1, keepdims=True)
    centred = values - average
    variance = jnp.mean(centred * centred, axis=-1, keepdims=True)
    return centred * lax.rsqrt(variance + epsilon) * norm_gain + norm_bias


def gelu_tanh(values):
    inner = 0.7978845608028654 * (values + 0.044715 * values * values * values)
    return 0.5 * values * (1.0 + jnp.tanh(inner))


def low_lanes(shape):
    return lax.broadcasted_iota(jnp.int32, shape, 1) < HD


def turn(values, cosine, sine):
    lane = lax.broadcasted_iota(jnp.int32, values.shape, 1)
    first_half = (lane & (HD - 1)) < HD // 2
    swapped = jnp.where(
        first_half,
        pltpu.roll(values, LANES - HD // 2, 1),
        pltpu.roll(values, HD // 2, 1),
    )
    return values * cosine + swapped * sine


def project_kernel(rows_ref, w_ref, cos_ref, sin_ref, q_ref, k_ref, v_ref):
    rows = rows_ref[...]
    cosine, sine = cos_ref[...], sin_ref[...]
    for part, out_ref in ((0, q_ref), (1, k_ref)):
        field = dot(rows, w_ref[part])
        for pair in range(field.shape[1] // LANES):
            cols = slice(pair * LANES, (pair + 1) * LANES)
            out_ref[:, cols] = turn(field[:, cols], cosine, sine).astype(bf16)
    v_ref[...] = dot(rows, w_ref[2]).astype(bf16)


def project(rows, weights, cosine, sine):
    count, width = rows.shape
    cols = weights.shape[2]
    step = count // 9
    row_spec = pl.BlockSpec((step, width), lambda i: (i, 0))
    table_spec = pl.BlockSpec((step, LANES), lambda i: (i, 0))
    out_spec = pl.BlockSpec((step, cols), lambda i: (i, 0))
    shape = jax.ShapeDtypeStruct((count, cols), bf16)
    return pl.pallas_call(
        project_kernel,
        grid=(9,),
        in_specs=[
            row_spec,
            pl.BlockSpec(weights.shape, lambda i: (0, 0, 0)),
            table_spec,
            table_spec,
        ],
        out_specs=[out_spec] * 3,
        out_shape=[shape] * 3,
        name="project",
        cost_estimate=pl.CostEstimate(
            flops=2 * count * width * 3 * cols,
            bytes_accessed=2 * (count * (width + 3 * cols) + 3 * width * cols),
            transcendentals=0,
        ),
    )(rows, weights, cosine, sine)


def split_heads(rows):
    low = low_lanes(rows.shape)
    zero = jnp.zeros_like(rows)
    return jnp.where(low, rows, zero), jnp.where(low, zero, rows)


def between(shape, offset, low, high):
    index = lax.broadcasted_iota(jnp.int32, shape, 0) + offset
    return jnp.logical_and(index >= low, index < high)


def forward_kernel(
    span_ref, clean_ref, noisy_ref, q_ref, k_ref, v_ref, out_ref, lse_ref
):
    def one_tile(t, _):
        clean_at = pl.multiple_of(CLEAN_OWN + t * TILE, TILE)
        noisy_at = pl.multiple_of(NOISY_OWN + t * TILE, EDGE)
        window_at = pl.multiple_of(NOISY_BASE + t * TILE, EDGE)
        query = jnp.concatenate(
            [q_ref[pl.ds(noisy_at, TILE), :], q_ref[pl.ds(clean_at, TILE), :]], axis=0
        )
        queries = split_heads(query)
        key_low, key_high = clean_ref[t, 0:1, :], clean_ref[t, 1:2, :]
        own_low, own_high = noisy_ref[t, 0:1, :], noisy_ref[t, 1:2, :]
        keys = k_ref[pl.ds(window_at, WINDOW), :]
        values_t = v_ref[pl.ds(window_at, WINDOW), :].T
        allowed = between((WINDOW, TILE), 0, own_low, own_high)
        state = []
        for head in range(2):
            scores = dot(keys, queries[head][:TILE], NT) * to_base2
            scores = jnp.where(allowed, scores, neg_large)
            top = jnp.max(scores, axis=0, keepdims=True)
            expo = jnp.exp2(scores - top)
            total = jnp.sum(expo, axis=0, keepdims=True)
            mixed = dot(values_t[head * HD : (head + 1) * HD], expo.astype(bf16))
            blank = jnp.zeros((1, TILE), f32)
            state += [
                jnp.concatenate([top, blank + neg_large], axis=1),
                jnp.concatenate([total, blank], axis=1),
                jnp.concatenate([mixed, jnp.zeros((HD, TILE), f32)], axis=1),
            ]
        first_key, trips = span_ref[t, 0], span_ref[t, 1]

        def one_step(j, state):
            at = pl.multiple_of(first_key + j * KEY_TILE, EDGE)
            keys = k_ref[pl.ds(at, KEY_TILE), :]
            values_t = v_ref[pl.ds(at, KEY_TILE), :].T
            allowed = between((KEY_TILE, 2 * TILE), at, key_low, key_high)
            after = []
            for head in range(2):
                top, total, mixed = state[3 * head : 3 * head + 3]
                scores = dot(keys, queries[head], NT) * to_base2
                scores = jnp.where(allowed, scores, neg_large)
                new_top = jnp.maximum(top, jnp.max(scores, axis=0, keepdims=True))
                keep = jnp.exp2(top - new_top)
                expo = jnp.exp2(scores - new_top)
                after += [
                    new_top,
                    total * keep + jnp.sum(expo, axis=0, keepdims=True),
                    mixed * keep
                    + dot(values_t[head * HD : (head + 1) * HD], expo.astype(bf16)),
                ]
            return tuple(after)

        state = lax.fori_loop(0, trips, one_step, tuple(state))
        pair = jnp.concatenate(
            [state[2] / state[1], state[5] / state[4]], axis=0
        ).T.astype(bf16)
        out_at = pl.multiple_of(t * TILE, TILE)
        out_ref[pl.ds(out_at, TILE), :] = pair[:TILE]
        out_ref[pl.ds(pl.multiple_of(HALF + t * TILE, TILE), TILE), :] = pair[TILE:]
        lse_ref[0, t, 0:1, :] = state[0] + jnp.log2(state[1])
        lse_ref[0, t, 1:2, :] = state[3] + jnp.log2(state[4])
        return 0

    lax.fori_loop(0, TILES, one_tile, 0)


def attend_forward(spans, clean_bounds, noisy_bounds, query, keys, values):
    count, cols = query.shape
    pairs = cols // LANES
    whole3 = lambda array: pl.BlockSpec(array.shape, lambda p, s: (0, 0, 0))
    row_spec = pl.BlockSpec((count, LANES), lambda p, s: (0, p))
    work = pairs * 2 * 2 * HALF * TOK_DEV
    return pl.pallas_call(
        forward_kernel,
        grid_spec=pltpu.PrefetchScalarGridSpec(
            num_scalar_prefetch=1,
            grid=(pairs,),
            in_specs=[whole3(clean_bounds), whole3(noisy_bounds)] + [row_spec] * 3,
            out_specs=[
                pl.BlockSpec((TOK_DEV, LANES), lambda p, s: (0, p)),
                pl.BlockSpec((1, TILES, 2, 2 * TILE), lambda p, s: (p, 0, 0, 0)),
            ],
        ),
        out_shape=[
            jax.ShapeDtypeStruct((TOK_DEV, cols), bf16),
            jax.ShapeDtypeStruct((pairs, TILES, 2, 2 * TILE), f32),
        ],
        name="attend_forward",
        cost_estimate=pl.CostEstimate(
            flops=4 * work * HD, bytes_accessed=8 * count * cols, transcendentals=work
        ),
    )(spans, clean_bounds, noisy_bounds, query, keys, values)


def backward_kernel(
    span_ref,
    clean_ref,
    noisy_ref,
    q_ref,
    k_ref,
    v_ref,
    o_ref,
    d_ref,
    lse_ref,
    cos_ref,
    sin_ref,
    rows_ref,
    out_ref,
    grad_ref,
    dk_ref,
    dv_ref,
):
    dk_ref[...] = jnp.zeros_like(dk_ref)
    dv_ref[...] = jnp.zeros_like(dv_ref)
    out_ref[:, :LANES] = jnp.zeros((KEY_ROWS, LANES), bf16)

    def one_tile(t, _):
        clean_at = pl.multiple_of(CLEAN_OWN + t * TILE, TILE)
        noisy_at = pl.multiple_of(NOISY_OWN + t * TILE, EDGE)
        window_at = pl.multiple_of(NOISY_BASE + t * TILE, EDGE)
        low_at = pl.multiple_of(t * TILE, TILE)
        high_at = pl.multiple_of(HALF + t * TILE, TILE)

        def both(ref, low, high):
            return jnp.concatenate(
                [ref[pl.ds(low, TILE), :], ref[pl.ds(high, TILE), :]], axis=0
            )

        query = split_heads(both(q_ref, noisy_at, clean_at))
        d_rows = both(d_ref, low_at, high_at)
        o_rows = both(o_ref, low_at, high_at)
        product = (d_rows.astype(f32) * o_rows.astype(f32)).T
        d_out = split_heads(d_rows)
        inner = [
            jnp.sum(product[head * HD : (head + 1) * HD], axis=0, keepdims=True)
            for head in range(2)
        ]
        lse = [lse_ref[0, t, head : head + 1, :] for head in range(2)]
        key_low, key_high = clean_ref[t, 0:1, :], clean_ref[t, 1:2, :]
        own_low, own_high = noisy_ref[t, 0:1, :], noisy_ref[t, 1:2, :]

        def accumulate(at, rows, cols, allowed, d_query):
            keys = k_ref[pl.ds(at, rows), :]
            values = v_ref[pl.ds(at, rows), :]
            keys_t = keys.T
            weights, d_scores, after = [], [], []
            for head in range(2):
                scores = dot(keys, query[head][:cols], NT) * to_base2
                scores = jnp.where(allowed, scores - lse[head][:, :cols], neg_large)
                probs = jnp.exp2(scores)
                d_probs = dot(values, d_out[head][:cols], NT)
                d_score = (probs * (d_probs - inner[head][:, :cols]) * 0.125).astype(bf16)
                weights.append(probs.astype(bf16))
                d_scores.append(d_score)
                after.append(
                    d_query[head] + dot(keys_t[head * HD : (head + 1) * HD], d_score)
                )
            stack = lambda parts: jnp.concatenate([part[:cols] for part in parts], axis=0)
            dv_ref[pl.ds(at, rows), :] += dot(
                jnp.concatenate(weights, axis=1), stack(d_out)
            )
            dk_ref[pl.ds(at, rows), :] += dot(
                jnp.concatenate(d_scores, axis=1), stack(query)
            )
            return tuple(after)

        allowed = between((WINDOW, TILE), 0, own_low, own_high)
        zero = jnp.zeros((HD, TILE), f32)
        start = accumulate(window_at, WINDOW, TILE, allowed, (zero, zero))
        start = tuple(jnp.concatenate([part, zero], axis=1) for part in start)
        first_key, trips = span_ref[t, 0], span_ref[t, 1]

        def one_step(j, d_query):
            at = pl.multiple_of(first_key + j * KEY_TILE, EDGE)
            allowed = between((KEY_TILE, 2 * TILE), at, key_low, key_high)
            return accumulate(at, KEY_TILE, 2 * TILE, allowed, d_query)

        d_query = lax.fori_loop(0, trips, one_step, start)
        d_query = jnp.concatenate(d_query, axis=0).T
        for at, part in ((noisy_at, d_query[:TILE]), (clean_at, d_query[TILE:])):
            turned = turn(part, cos_ref[pl.ds(at, TILE), :], -sin_ref[pl.ds(at, TILE), :])
            out_ref[pl.ds(at, TILE), :LANES] = turned.astype(bf16)
        return 0

    lax.fori_loop(0, TILES, one_tile, 0)
    step = KEY_ROWS // 9

    def finish(i, _):
        rows = pl.ds(pl.multiple_of(i * step, EDGE), step)
        out_ref[rows, LANES : 2 * LANES] = turn(
            dk_ref[rows, :], cos_ref[rows, :], -sin_ref[rows, :]
        ).astype(bf16)
        out_ref[rows, 2 * LANES :] = dv_ref[rows, :].astype(bf16)
        return 0

    lax.fori_loop(0, 9, finish, 0)

    def weight_rows(i, _):
        rows = pl.ds(pl.multiple_of(i * LANES, LANES), LANES)
        grad = dot(rows_ref[rows, :], out_ref[...])
        for c in range(3):
            grad_ref[c, rows, :] = grad[:, c * LANES : (c + 1) * LANES]
        return 0

    lax.fori_loop(0, rows_ref.shape[0] // LANES, weight_rows, 0)


def attend_backward(
    pair,
    spans,
    clean_bounds,
    noisy_bounds,
    query,
    keys,
    values,
    attended,
    d_attended,
    lse,
    cosine,
    sine,
    rows_t,
):
    count = query.shape[0]
    width = rows_t.shape[0]
    whole2 = lambda array: pl.BlockSpec(array.shape, lambda i, s: (0, 0))
    whole3 = lambda array: pl.BlockSpec(array.shape, lambda i, s: (0, 0, 0))
    row_spec = pl.BlockSpec((count, LANES), lambda i, s: (0, pair))
    own_spec = pl.BlockSpec((TOK_DEV, LANES), lambda i, s: (0, pair))
    return pl.pallas_call(
        backward_kernel,
        grid_spec=pltpu.PrefetchScalarGridSpec(
            num_scalar_prefetch=1,
            grid=(1,),
            in_specs=[whole3(clean_bounds), whole3(noisy_bounds)]
            + [row_spec] * 3
            + [own_spec] * 2
            + [
                pl.BlockSpec((1, TILES, 2, 2 * TILE), lambda i, s: (pair, 0, 0, 0)),
                whole2(cosine),
                whole2(sine),
                whole2(rows_t),
            ],
            out_specs=[
                pl.BlockSpec((count, 3 * LANES), lambda i, s: (0, 0)),
                pl.BlockSpec((3, width, LANES), lambda i, s: (0, 0, 0)),
            ],
            scratch_shapes=[pltpu.VMEM((count, LANES), f32)] * 2,
        ),
        out_shape=[
            jax.ShapeDtypeStruct((count, 3 * LANES), bf16),
            jax.ShapeDtypeStruct((3, width, LANES), f32),
        ],
        name="attend_backward",
        cost_estimate=pl.CostEstimate(
            flops=12 * 10**9, bytes_accessed=12 * 10**6, transcendentals=2 * 10**6
        ),
    )(
        spans,
        clean_bounds,
        noisy_bounds,
        query,
        keys,
        values,
        attended,
        d_attended,
        lse,
        cosine,
        sine,
        rows_t,
    )


def rows_back_kernel(*refs):
    *grads, weights, out_ref = refs
    total = dot(grads[0][...], weights[0], NT)
    for i, grad in enumerate(grads[1:]):
        total = total + dot(grad[...], weights[i + 1], NT)
    out_ref[...] = total


def rows_back(grads, weights):
    count, cols = grads[0].shape
    step = count // 9
    width = weights.shape[1]
    return pl.pallas_call(
        rows_back_kernel,
        grid=(9,),
        in_specs=[pl.BlockSpec((step, cols), lambda i: (i, 0))] * len(grads)
        + [pl.BlockSpec(weights.shape, lambda i: (0, 0, 0))],
        out_specs=pl.BlockSpec((step, width), lambda i: (i, 0)),
        out_shape=jax.ShapeDtypeStruct((count, width), f32),
        name="rows_back",
        cost_estimate=pl.CostEstimate(
            flops=2 * count * cols * width * len(grads),
            bytes_accessed=16 * 10**6,
            transcendentals=0,
        ),
    )(*grads, weights)


def key_layout(seq_lengths, block_len, part):
    index = jnp.arange(KEY_ROWS, dtype=jnp.int32)
    own = part * HALF
    token = jnp.where(
        index < NOISY_BASE, index + (own - HALF), index - NOISY_BASE + (own - EDGE)
    )
    ends = jnp.cumsum(seq_lengths)
    passed = token[:, None] >= ends[None, :]
    starts = jnp.sum(jnp.where(passed, seq_lengths[None, :], 0), axis=1)
    lengths_here = jnp.where(passed, 0, ends[None, :])
    stops = jnp.min(jnp.where(passed, TOK_DEV, lengths_here), axis=1)
    positions = token - starts
    block_start = starts + positions // block_len * block_len
    block_stop = jnp.minimum(block_start + block_len, stops)
    mine = slice(CLEAN_OWN, CLEAN_OWN + HALF)
    low, start, stop = starts[mine], block_start[mine], block_stop[mine]
    to_clean = own - HALF
    tiles = lambda column: column.reshape(TILES, 1, TILE)
    clean_bounds = jnp.concatenate(
        [
            jnp.concatenate([tiles(low - to_clean), tiles(low - to_clean)], axis=2),
            jnp.concatenate([tiles(start - to_clean), tiles(stop - to_clean)], axis=2),
        ],
        axis=1,
    )
    to_window = own - EDGE + TILE * jnp.arange(TILES, dtype=jnp.int32)[:, None, None]
    noisy_bounds = jnp.concatenate(
        [tiles(start) - to_window, tiles(stop) - to_window], axis=1
    )
    first = jnp.min(clean_bounds[:, 0], axis=1) // EDGE * EDGE
    last = jnp.max(clean_bounds[:, 1], axis=1)
    trips = (last - first + KEY_TILE - 1) // KEY_TILE
    spans = jnp.stack([first, trips], axis=1)
    lane = jnp.arange(LANES, dtype=jnp.int32)
    frequency = jnp.exp(
        (lane % (HD // 2)).astype(f32) * (-math.log(10000.0) / (HD // 2))
    )
    angles = positions.astype(f32)[:, None] * frequency[None, :]
    sign = jnp.where(lane % HD < HD // 2, -1.0, 1.0)
    return spans, clean_bounds, noisy_bounds, jnp.cos(angles), jnp.sin(angles) * sign


def half_of(array, which):
    size = array.shape[0] // 2
    return lax.dynamic_slice_in_dim(array, which * size, size, 0)


def in_order(bit, mine, theirs):
    flip = bit == 0
    return jnp.concatenate(
        [jnp.where(flip, mine, theirs), jnp.where(flip, theirs, mine)], axis=0
    )


def low(array):
    return array.astype(bf16)


class Job:
    def __init__(self, steps):
        self.steps = steps
        self.pending = None
        self.result = None
        self.routes = None


def tie(first, second):
    return lax.optimization_barrier((first, second))


def local(
    dp_size,
    tokens,
    lengths,
    block_size,
    cotangent,
    ln1_gain,
    ln1_bias,
    w_qkv,
    w_out,
    ln2_gain,
    ln2_bias,
    w_up,
    b_up,
    w_down,
    b_down,
):
    width = tokens.shape[2]
    part = lax.axis_index("mp")
    place = lax.axis_index("dp")
    bits = dp_size.bit_length() - 1
    my_bit = [(place >> b) & 1 for b in range(bits)]

    def send(array, route):
        mask, cross = route
        if cross:
            return lax.ppermute(array, "mp", [(0, 1), (1, 0)])
        return lax.ppermute(array, "dp", [(i, i ^ mask) for i in range(dp_size)])

    across, sibling, beside = (0, 1), (1, 0), (2, 0)

    def fetch(half):
        here = send(half, across)
        return here, send(here, sibling)

    def cross_steps(others):
        core = my_bit[0]
        (got,) = yield [(low(half_of(others, 1 - core)), sibling)]
        (got,) = yield [(low(half_of(others, core) + got.astype(f32)), across)]
        return got

    def sum_steps(mine, crossed):
        core = my_bit[0]
        (got,) = yield [(low(half_of(mine, 1 - core)), sibling)]
        total = half_of(mine, core) + got.astype(f32) + crossed().astype(f32)
        (got,) = yield [(low(half_of(total, 1 - my_bit[1])), beside)]
        total = half_of(total, my_bit[1]) + got.astype(f32)
        spans = [(b, min(2, bits - b)) for b in range(2, bits, 2)]
        for b, n in spans:
            size = total.shape[0] >> n
            spot = (place >> b) & ((1 << n) - 1)
            piece = lambda s: lax.dynamic_slice_in_dim(total, s * size, size, 0)
            got = yield [(low(piece(spot ^ k)), (k << b, 0)) for k in range(1, 1 << n)]
            total = piece(spot)
            for item in got:
                total = total + item.astype(f32)
        total = low(total)
        for b, n in reversed(spans):
            got = yield [(total, (k << b, 0)) for k in range(1, 1 << n)]
            if n == 1:
                total = in_order(my_bit[b], total, got[0])
            else:
                total = in_order(
                    my_bit[b + 1],
                    in_order(my_bit[b], total, got[0]),
                    in_order(my_bit[b], got[1], got[2]),
                )
        (got,) = yield [(total, beside)]
        total = in_order(my_bit[1], total, got)
        (got,) = yield [(total, sibling)]
        return in_order(my_bit[0], total, got).astype(f32)

    def small_steps(mine, others):
        (got,) = yield [(others, across)]
        total = mine + got
        for b in range(bits):
            (got,) = yield [(total, (1 << b, 0))]
            total = total + got
        return total

    def advance(after, before, jobs):
        arrived = [job.pending for job in jobs]
        after, arrived = tie(after, arrived)
        outgoing = []
        for job, got in zip(jobs, arrived):
            job.pending = None
            try:
                orders = job.steps.send(got)
                job.routes = [route for _, route in orders]
                outgoing.append([array for array, _ in orders])
            except StopIteration as stop:
                job.result = stop.value
                job.routes = []
                outgoing.append([])
        before, outgoing = tie(before, outgoing)
        for job, arrays in zip(jobs, outgoing):
            job.pending = [send(array, route) for array, route in zip(arrays, job.routes)]
        return before

    def finish(job):
        if job.result is None:
            while True:
                try:
                    orders = job.steps.send(job.pending)
                except StopIteration as stop:
                    job.result = stop.value
                    break
                job.pending = [send(array, route) for array, route in orders]
        return job.result

    core = my_bit[0]
    edge = jnp.where(part == 0, tokens[0, HALF - EDGE :], tokens[0, :EDGE])
    context = send(jnp.concatenate([tokens[1], edge], axis=0), across)
    qkv_mine = w_qkv.transpose(1, 0, 2)
    halves = [
        half_of(qkv_mine.reshape(-1, w_qkv.shape[2]), core),
        half_of(w_out, core),
        half_of(w_up, core),
        half_of(w_down, core),
    ]
    context, halves = tie(context, halves)
    fetched = [fetch(half) for half in halves]
    bias_other = send(b_up, across)

    spans, clean_bounds, noisy_bounds, cosine, sine = key_layout(lengths[0], block_size[0], part)
    clean_other, edge_other = context[:HALF], context[HALF:]
    key_tokens = jnp.concatenate(
        [clean_other, tokens[1], clean_other[:EDGE], edge_other, tokens[0], edge_other], axis=0
    )
    normed1_keys = layer_norm(key_tokens.astype(f32), ln1_gain, ln1_bias).astype(bf16)
    normed1_t = normed1_keys.T

    def attention(weights):
        query, keys, values = project(normed1_keys, weights, cosine, sine)
        attended, lse = attend_forward(spans, clean_bounds, noisy_bounds, query, keys, values)
        return (query, keys, values, attended, lse)

    mine = attention(qkv_mine)
    fetched[0] = tie(fetched[0], mine[3])[0]
    qkv_other = in_order(core, *fetched[0]).reshape(qkv_mine.shape)
    other = attention(qkv_other)
    fetched[1:] = tie(fetched[1:], other[3])[0]
    out_other, up_other, down_other = [in_order(core, *pieces) for pieces in fetched[1:]]
    saved = (mine, other)

    x_rows = tokens.astype(f32).reshape(TOK_DEV, width)
    branch = dot(mine[3], w_out) + dot(other[3], out_other)
    mid = x_rows + branch
    normed2, norm2_back = jax.vjp(layer_norm, mid, ln2_gain, ln2_bias)
    mlp_rows = normed2.astype(bf16)
    d_low = cotangent.reshape(TOK_DEV, width)
    d_out_rows = d_low.astype(f32)
    grad_b_down = jnp.sum(d_out_rows, axis=0)

    def hidden_units(mlp_rows, d_low, up, bias, down_w):
        pre = dot(mlp_rows, up) + bias.astype(f32)
        act_low = gelu_tanh(pre).astype(bf16)
        down = dot(act_low, down_w)
        d_act = dot(d_low, down_w, NT)
        d_pre = jax.vjp(gelu_tanh, pre)[1](d_act)[0].astype(bf16)
        grad_down = jnp.einsum("rf,rd->fd", act_low, d_low, preferred_element_type=f32)
        grad_up = jnp.einsum("rd,rf->df", mlp_rows, d_pre, preferred_element_type=f32)
        grad_bias = jnp.sum(d_pre.astype(f32), axis=0)
        return down, dot(d_pre, up, NT), grad_down, grad_up, grad_bias

    down2, d_two, down_o, up_o, bias_o = hidden_units(
        mlp_rows, d_low, up_other, bias_other, down_other
    )
    down_cross, up_cross = Job(cross_steps(down_o)), Job(cross_steps(up_o))
    rows_here, d_here = advance(
        [d_two, down2], (mlp_rows, d_low), [down_cross, up_cross]
    )
    down1, d_one, down_m, up_m, bias_m = hidden_units(rows_here, d_here, w_up, b_up, w_down)
    out = (mid + (down1 + down2) + b_down).astype(bf16).reshape(tokens.shape)
    d_normed2 = d_one + d_two
    down_sum = Job(sum_steps(down_m, lambda: down_cross.result))
    up_sum = Job(sum_steps(up_m, lambda: up_cross.result))
    d_normed2 = advance([d_normed2], d_normed2, [down_cross, up_cross, down_sum, up_sum])

    d_mid_norm, grad_ln2_gain, grad_ln2_bias = norm2_back(d_normed2)
    d_mid = d_out_rows + d_mid_norm
    d_branch = d_mid.astype(bf16)
    grad_out = []
    d_attended = []
    for item, weights in zip(saved, (w_out, out_other)):
        grad_out.append(jnp.einsum("rf,rd->fd", item[3], d_branch, preferred_element_type=f32))
        d_attended.append(dot(d_branch, weights, NT).astype(bf16))
    out_cross = Job(cross_steps(grad_out[1]))
    out_sum = Job(sum_steps(grad_out[0], lambda: out_cross.result))
    norms = jnp.concatenate([grad_ln2_gain, grad_ln2_bias, grad_b_down])
    small = Job(
        small_steps(
            jnp.concatenate([bias_m, norms]), jnp.concatenate([bias_o, norms])
        )
    )
    pairs = mine[0].shape[1] // LANES
    qkv_cross, qkv_sum = [], []
    plan = [
        [out_cross, out_sum, small],
        [down_cross, down_sum, out_cross, small],
        [up_cross, up_sum, down_sum, small, "cross"],
        [down_sum, up_sum, out_cross, out_sum, small, "cross"],
        [down_sum, up_sum, out_sum, small, "cross", "sum"],
        [down_sum, up_sum, out_sum, small, "cross", "sum"],
        [down_sum, up_sum, out_sum, small, "cross", "sum"],
    ]
    token = spans
    token = advance(d_attended, token, plan[0])
    d_qkv = [[], []]
    grad_qkv = [[], []]
    turn_at = 0
    for group in (1, 0):
        query, keys, values, attended, lse = saved[group]
        for pair in range(pairs):
            d_fields, grad = attend_backward(
                pair,
                token,
                clean_bounds,
                noisy_bounds,
                query,
                keys,
                values,
                attended,
                d_attended[group],
                lse,
                cosine,
                sine,
                normed1_t,
            )
            d_qkv[group].append(d_fields)
            turn_at += 1
            flat = grad.reshape(-1, LANES)
            if group == 1:
                qkv_cross.append(Job(cross_steps(flat)))
            else:
                cross = qkv_cross[pair]
                qkv_sum.append(Job(sum_steps(flat, lambda cross=cross: cross.result)))
            jobs = []
            for item in plan[turn_at]:
                if item == "cross":
                    jobs += [job for job in qkv_cross if job.result is None]
                elif item == "sum":
                    jobs += qkv_sum
                elif item.result is None:
                    jobs.append(item)
            token = advance([d_fields], token, jobs)

    def by_pair(weights):
        split = weights.reshape(3, width, pairs, LANES)
        return split.transpose(2, 1, 0, 3).reshape(pairs, width, 3 * LANES)

    d_normed1_keys = rows_back(
        d_qkv[0] + d_qkv[1],
        jnp.concatenate([by_pair(qkv_mine), by_pair(qkv_other)], axis=0),
    )
    clean_back = d_normed1_keys[:HALF]
    clean_back = clean_back.at[:EDGE].add(d_normed1_keys[2 * HALF : 2 * HALF + EDGE])
    edge_back = d_normed1_keys[NOISY_BASE:NOISY_OWN] + d_normed1_keys[NOISY_OWN + HALF :]
    back = send(low(jnp.concatenate([clean_back, edge_back], axis=0)), across).astype(f32)
    at_end = jnp.concatenate([jnp.zeros((HALF - EDGE, width), f32), back[HALF:]], axis=0)
    at_start = jnp.concatenate([back[HALF:], jnp.zeros((HALF - EDGE, width), f32)], axis=0)
    d_normed1 = jnp.concatenate(
        [
            d_normed1_keys[NOISY_OWN : NOISY_OWN + HALF]
            + jnp.where(part == 0, at_end, at_start),
            d_normed1_keys[CLEAN_OWN : CLEAN_OWN + HALF] + back[:HALF],
        ],
        axis=0,
    )
    norm1_back = jax.vjp(layer_norm, x_rows, ln1_gain, ln1_bias)[1]
    d_x_norm, grad_ln1_gain, grad_ln1_bias = norm1_back(d_normed1)
    grad_tokens = (d_mid + d_x_norm).reshape(tokens.shape)
    norms1 = jnp.concatenate([grad_ln1_gain, grad_ln1_bias])
    first_norm = finish(Job(small_steps(norms1, norms1)))

    grad_down, grad_up, grad_out = finish(down_sum), finish(up_sum), finish(out_sum)
    small = finish(small)
    grad_qkv = jnp.concatenate(
        [finish(job).reshape(3, width, LANES) for job in qkv_sum], axis=2
    ).transpose(1, 0, 2)
    hidden = b_up.shape[0]
    rest = [small[hidden + i * width : hidden + (i + 1) * width] for i in range(3)]
    return (
        out,
        grad_tokens,
        first_norm[:width],
        first_norm[width:],
        grad_qkv,
        grad_out,
        rest[0],
        rest[1],
        grad_up,
        small[:hidden],
        grad_down,
        rest[2],
    )


def solution(mesh):
    in_specs = (
        P(None, ("dp", "mp"), None),
        P("dp", None),
        P(),
        P(None, ("dp", "mp"), None),
        P(),
        P(),
        P(None, None, "mp"),
        P("mp", None),
        P(),
        P(),
        P(None, "mp"),
        P("mp"),
        P("mp", None),
        P(),
    )
    out_specs = (
        P(None, ("dp", "mp"), None),
        P(None, ("dp", "mp"), None),
        P(),
        P(),
        P(None, None, "mp"),
        P("mp", None),
        P(),
        P(),
        P(None, "mp"),
        P("mp"),
        P("mp", None),
        P(),
    )
    return jax.shard_map(
        functools.partial(local, mesh.shape["dp"]),
        mesh=mesh,
        in_specs=in_specs,
        out_specs=out_specs,
        check_vma=False,
    )
```

```python
import functools
import math

import jax
import jax.numpy as jnp
from jax import lax
from jax.experimental import pallas as pl
from jax.experimental.pallas import tpu as pltpu
from jax.sharding import PartitionSpec as P

HD = 64
TOK_DEV = 1024
HALF = TOK_DEV // 2
EDGE = 16
CLEAN_OWN = HALF
NOISY_BASE = 2 * HALF + EDGE
NOISY_OWN = NOISY_BASE + EDGE
KEY_ROWS = NOISY_OWN + HALF + EDGE
TILE = 128
TILES = HALF // TILE
WINDOW = TILE + 2 * EDGE
KEY_TILE = 256
LANES = 128

epsilon = 1e-05
neg_large = -1e30
to_base2 = 0.125 * math.log2(math.e)
f32 = jnp.float32
bf16 = jnp.bfloat16

NN = (((1,), (0,)), ((), ()))
NT = (((1,), (1,)), ((), ()))


def dot(left, right, dims=NN):
    return lax.dot_general(left, right, dims, preferred_element_type=f32)


def layer_norm(values, norm_gain, norm_bias):
    average = jnp.mean(values, axis=-1, keepdims=True)
    centred = values - average
    variance = jnp.mean(centred * centred, axis=-1, keepdims=True)
    return centred * lax.rsqrt(variance + epsilon) * norm_gain + norm_bias


def low_lanes(shape):
    return lax.broadcasted_iota(jnp.int32, shape, 1) < HD


def turn(values, cosine, sine):
    lane = lax.broadcasted_iota(jnp.int32, values.shape, 1)
    first_half = (lane & (HD - 1)) < HD // 2
    swapped = jnp.where(
        first_half,
        pltpu.roll(values, LANES - HD // 2, 1),
        pltpu.roll(values, HD // 2, 1),
    )
    return values * cosine + swapped * sine


def project_kernel(rows_ref, w_ref, cos_ref, sin_ref, q_ref, k_ref, v_ref):
    rows = rows_ref[...]
    cosine, sine = cos_ref[...], sin_ref[...]
    for part, out_ref in ((0, q_ref), (1, k_ref)):
        field = dot(rows, w_ref[part])
        for pair in range(field.shape[1] // LANES):
            cols = slice(pair * LANES, (pair + 1) * LANES)
            out_ref[:, cols] = turn(field[:, cols], cosine, sine).astype(bf16)
    v_ref[...] = dot(rows, w_ref[2]).astype(bf16)


def project(rows, weights, cosine, sine):
    count, width = rows.shape
    cols = weights.shape[2]
    step = count // 9
    row_spec = pl.BlockSpec((step, width), lambda i: (i, 0))
    table_spec = pl.BlockSpec((step, LANES), lambda i: (i, 0))
    out_spec = pl.BlockSpec((step, cols), lambda i: (i, 0))
    shape = jax.ShapeDtypeStruct((count, cols), bf16)
    return pl.pallas_call(
        project_kernel,
        grid=(9,),
        in_specs=[
            row_spec,
            pl.BlockSpec(weights.shape, lambda i: (0, 0, 0)),
            table_spec,
            table_spec,
        ],
        out_specs=[out_spec] * 3,
        out_shape=[shape] * 3,
        name="project",
        cost_estimate=pl.CostEstimate(
            flops=2 * count * width * 3 * cols,
            bytes_accessed=2 * (count * (width + 3 * cols) + 3 * width * cols),
            transcendentals=0,
        ),
    )(rows, weights, cosine, sine)


def split_heads(rows):
    low = low_lanes(rows.shape)
    zero = jnp.zeros_like(rows)
    return jnp.where(low, rows, zero), jnp.where(low, zero, rows)


def between(shape, offset, low, high):
    index = lax.broadcasted_iota(jnp.int32, shape, 0) + offset
    return jnp.logical_and(index >= low, index < high)


def forward_kernel(
    span_ref, clean_ref, noisy_ref, q_ref, k_ref, v_ref, out_ref, lse_ref
):
    def one_tile(t, _):
        clean_at = pl.multiple_of(CLEAN_OWN + t * TILE, TILE)
        noisy_at = pl.multiple_of(NOISY_OWN + t * TILE, EDGE)
        window_at = pl.multiple_of(NOISY_BASE + t * TILE, EDGE)
        query = jnp.concatenate(
            [q_ref[pl.ds(noisy_at, TILE), :], q_ref[pl.ds(clean_at, TILE), :]], axis=0
        )
        queries = split_heads(query)
        key_low, key_high = clean_ref[t, 0:1, :], clean_ref[t, 1:2, :]
        own_low, own_high = noisy_ref[t, 0:1, :], noisy_ref[t, 1:2, :]
        keys = k_ref[pl.ds(window_at, WINDOW), :]
        values_t = v_ref[pl.ds(window_at, WINDOW), :].T
        allowed = between((WINDOW, TILE), 0, own_low, own_high)
        state = []
        for head in range(2):
            scores = dot(keys, queries[head][:TILE], NT) * to_base2
            scores = jnp.where(allowed, scores, neg_large)
            top = jnp.max(scores, axis=0, keepdims=True)
            expo = jnp.exp2(scores - top)
            total = jnp.sum(expo, axis=0, keepdims=True)
            mixed = dot(values_t[head * HD : (head + 1) * HD], expo.astype(bf16))
            blank = jnp.zeros((1, TILE), f32)
            state += [
                jnp.concatenate([top, blank + neg_large], axis=1),
                jnp.concatenate([total, blank], axis=1),
                jnp.concatenate([mixed, jnp.zeros((HD, TILE), f32)], axis=1),
            ]
        first_key, trips = span_ref[t, 0], span_ref[t, 1]

        def one_step(j, state):
            at = pl.multiple_of(first_key + j * KEY_TILE, EDGE)
            keys = k_ref[pl.ds(at, KEY_TILE), :]
            values_t = v_ref[pl.ds(at, KEY_TILE), :].T
            allowed = between((KEY_TILE, 2 * TILE), at, key_low, key_high)
            after = []
            for head in range(2):
                top, total, mixed = state[3 * head : 3 * head + 3]
                scores = dot(keys, queries[head], NT) * to_base2
                scores = jnp.where(allowed, scores, neg_large)
                new_top = jnp.maximum(top, jnp.max(scores, axis=0, keepdims=True))
                keep = jnp.exp2(top - new_top)
                expo = jnp.exp2(scores - new_top)
                after += [
                    new_top,
                    total * keep + jnp.sum(expo, axis=0, keepdims=True),
                    mixed * keep
                    + dot(values_t[head * HD : (head + 1) * HD], expo.astype(bf16)),
                ]
            return tuple(after)

        state = lax.fori_loop(0, trips, one_step, tuple(state))
        pair = jnp.concatenate(
            [state[2] / state[1], state[5] / state[4]], axis=0
        ).T.astype(bf16)
        out_at = pl.multiple_of(t * TILE, TILE)
        out_ref[pl.ds(out_at, TILE), :] = pair[:TILE]
        out_ref[pl.ds(pl.multiple_of(HALF + t * TILE, TILE), TILE), :] = pair[TILE:]
        lse_ref[0, t, 0:1, :] = state[0] + jnp.log2(state[1])
        lse_ref[0, t, 1:2, :] = state[3] + jnp.log2(state[4])
        return 0

    lax.fori_loop(0, TILES, one_tile, 0)


def attend_forward(spans, clean_bounds, noisy_bounds, query, keys, values):
    count, cols = query.shape
    pairs = cols // LANES
    whole3 = lambda array: pl.BlockSpec(array.shape, lambda p, s: (0, 0, 0))
    row_spec = pl.BlockSpec((count, LANES), lambda p, s: (0, p))
    work = pairs * 2 * 2 * HALF * TOK_DEV
    return pl.pallas_call(
        forward_kernel,
        grid_spec=pltpu.PrefetchScalarGridSpec(
            num_scalar_prefetch=1,
            grid=(pairs,),
            in_specs=[whole3(clean_bounds), whole3(noisy_bounds)] + [row_spec] * 3,
            out_specs=[
                pl.BlockSpec((TOK_DEV, LANES), lambda p, s: (0, p)),
                pl.BlockSpec((1, TILES, 2, 2 * TILE), lambda p, s: (p, 0, 0, 0)),
            ],
        ),
        out_shape=[
            jax.ShapeDtypeStruct((TOK_DEV, cols), bf16),
            jax.ShapeDtypeStruct((pairs, TILES, 2, 2 * TILE), f32),
        ],
        name="attend_forward",
        cost_estimate=pl.CostEstimate(
            flops=4 * work * HD, bytes_accessed=8 * count * cols, transcendentals=work
        ),
    )(spans, clean_bounds, noisy_bounds, query, keys, values)


def backward_kernel(
    span_ref,
    clean_ref,
    noisy_ref,
    q_ref,
    k_ref,
    v_ref,
    o_ref,
    d_ref,
    lse_ref,
    cos_ref,
    sin_ref,
    rows_ref,
    out_ref,
    grad_ref,
    dk_ref,
    dv_ref,
):
    dk_ref[...] = jnp.zeros_like(dk_ref)
    dv_ref[...] = jnp.zeros_like(dv_ref)
    out_ref[0, :, :LANES] = jnp.zeros((KEY_ROWS, LANES), bf16)

    def one_tile(t, _):
        clean_at = pl.multiple_of(CLEAN_OWN + t * TILE, TILE)
        noisy_at = pl.multiple_of(NOISY_OWN + t * TILE, EDGE)
        window_at = pl.multiple_of(NOISY_BASE + t * TILE, EDGE)
        low_at = pl.multiple_of(t * TILE, TILE)
        high_at = pl.multiple_of(HALF + t * TILE, TILE)

        def both(ref, low, high):
            return jnp.concatenate(
                [ref[pl.ds(low, TILE), :], ref[pl.ds(high, TILE), :]], axis=0
            )

        query = split_heads(both(q_ref, noisy_at, clean_at))
        d_rows = both(d_ref, low_at, high_at)
        o_rows = both(o_ref, low_at, high_at)
        product = (d_rows.astype(f32) * o_rows.astype(f32)).T
        d_out = split_heads(d_rows)
        inner = [
            jnp.sum(product[head * HD : (head + 1) * HD], axis=0, keepdims=True)
            for head in range(2)
        ]
        lse = [lse_ref[0, t, head : head + 1, :] for head in range(2)]
        key_low, key_high = clean_ref[t, 0:1, :], clean_ref[t, 1:2, :]
        own_low, own_high = noisy_ref[t, 0:1, :], noisy_ref[t, 1:2, :]

        def accumulate(at, rows, cols, allowed, d_query):
            keys = k_ref[pl.ds(at, rows), :]
            values = v_ref[pl.ds(at, rows), :]
            keys_t = keys.T
            weights, d_scores, after = [], [], []
            for head in range(2):
                scores = dot(keys, query[head][:cols], NT) * to_base2
                scores = jnp.where(allowed, scores - lse[head][:, :cols], neg_large)
                probs = jnp.exp2(scores)
                d_probs = dot(values, d_out[head][:cols], NT)
                d_score = (probs * (d_probs - inner[head][:, :cols]) * 0.125).astype(bf16)
                weights.append(probs.astype(bf16))
                d_scores.append(d_score)
                after.append(
                    d_query[head] + dot(keys_t[head * HD : (head + 1) * HD], d_score)
                )
            stack = lambda parts: jnp.concatenate([part[:cols] for part in parts], axis=0)
            dv_ref[pl.ds(at, rows), :] += dot(
                jnp.concatenate(weights, axis=1), stack(d_out)
            )
            dk_ref[pl.ds(at, rows), :] += dot(
                jnp.concatenate(d_scores, axis=1), stack(query)
            )
            return tuple(after)

        allowed = between((WINDOW, TILE), 0, own_low, own_high)
        zero = jnp.zeros((HD, TILE), f32)
        start = accumulate(window_at, WINDOW, TILE, allowed, (zero, zero))
        start = tuple(jnp.concatenate([part, zero], axis=1) for part in start)
        first_key, trips = span_ref[t, 0], span_ref[t, 1]

        def one_step(j, d_query):
            at = pl.multiple_of(first_key + j * KEY_TILE, EDGE)
            allowed = between((KEY_TILE, 2 * TILE), at, key_low, key_high)
            return accumulate(at, KEY_TILE, 2 * TILE, allowed, d_query)

        d_query = lax.fori_loop(0, trips, one_step, start)
        d_query = jnp.concatenate(d_query, axis=0).T
        for at, part in ((noisy_at, d_query[:TILE]), (clean_at, d_query[TILE:])):
            turned = turn(part, cos_ref[pl.ds(at, TILE), :], -sin_ref[pl.ds(at, TILE), :])
            out_ref[0, pl.ds(at, TILE), :LANES] = turned.astype(bf16)
        return 0

    lax.fori_loop(0, TILES, one_tile, 0)
    step = KEY_ROWS // 9

    def finish(i, _):
        rows = pl.ds(pl.multiple_of(i * step, EDGE), step)
        out_ref[0, rows, LANES : 2 * LANES] = turn(
            dk_ref[rows, :], cos_ref[rows, :], -sin_ref[rows, :]
        ).astype(bf16)
        out_ref[0, rows, 2 * LANES :] = dv_ref[rows, :].astype(bf16)
        return 0

    lax.fori_loop(0, 9, finish, 0)

    def weight_rows(i, _):
        rows = pl.ds(pl.multiple_of(i * LANES, LANES), LANES)
        grad_ref[0, rows, :] = dot(rows_ref[rows, :], out_ref[0]).astype(bf16)
        return 0

    lax.fori_loop(0, rows_ref.shape[0] // LANES, weight_rows, 0)


def attend_backward(
    spans,
    clean_bounds,
    noisy_bounds,
    query,
    keys,
    values,
    attended,
    d_attended,
    lse,
    cosine,
    sine,
    rows_t,
):
    count, cols = query.shape
    pairs = cols // LANES
    width = rows_t.shape[0]
    whole2 = lambda array: pl.BlockSpec(array.shape, lambda p, s: (0, 0))
    whole3 = lambda array: pl.BlockSpec(array.shape, lambda p, s: (0, 0, 0))
    row_spec = pl.BlockSpec((count, LANES), lambda p, s: (0, p))
    own_spec = pl.BlockSpec((TOK_DEV, LANES), lambda p, s: (0, p))
    return pl.pallas_call(
        backward_kernel,
        grid_spec=pltpu.PrefetchScalarGridSpec(
            num_scalar_prefetch=1,
            grid=(pairs,),
            in_specs=[whole3(clean_bounds), whole3(noisy_bounds)]
            + [row_spec] * 3
            + [own_spec] * 2
            + [
                pl.BlockSpec((1, TILES, 2, 2 * TILE), lambda p, s: (p, 0, 0, 0)),
                whole2(cosine),
                whole2(sine),
                whole2(rows_t),
            ],
            out_specs=[
                pl.BlockSpec((1, count, 3 * LANES), lambda p, s: (p, 0, 0)),
                pl.BlockSpec((1, width, 3 * LANES), lambda p, s: (p, 0, 0)),
            ],
            scratch_shapes=[pltpu.VMEM((count, LANES), f32)] * 2,
        ),
        out_shape=[
            jax.ShapeDtypeStruct((pairs, count, 3 * LANES), bf16),
            jax.ShapeDtypeStruct((pairs, width, 3 * LANES), bf16),
        ],
        name="attend_backward",
        cost_estimate=pl.CostEstimate(
            flops=36 * 10**9, bytes_accessed=36 * 10**6, transcendentals=6 * 10**6
        ),
    )(
        spans,
        clean_bounds,
        noisy_bounds,
        query,
        keys,
        values,
        attended,
        d_attended,
        lse,
        cosine,
        sine,
        rows_t,
    )


def rows_back_kernel(grads_ref, grads2_ref, w_ref, w2_ref, out_ref):
    total = 0.0
    for grads, weights in ((grads_ref, w_ref), (grads2_ref, w2_ref)):
        for pair in range(grads.shape[0]):
            total = total + dot(grads[pair], weights[pair], NT)
    out_ref[...] = total


def rows_back(grads, grads2, weights, weights2):
    pairs, count, cols = grads.shape
    step = count // 9
    width = weights.shape[1]
    grad_spec = pl.BlockSpec((pairs, step, cols), lambda i: (0, i, 0))
    w_spec = pl.BlockSpec(weights.shape, lambda i: (0, 0, 0))
    return pl.pallas_call(
        rows_back_kernel,
        grid=(9,),
        in_specs=[grad_spec, grad_spec, w_spec, w_spec],
        out_specs=pl.BlockSpec((step, width), lambda i: (i, 0)),
        out_shape=jax.ShapeDtypeStruct((count, width), f32),
        name="rows_back",
        cost_estimate=pl.CostEstimate(
            flops=4 * pairs * count * cols * width,
            bytes_accessed=16 * 10**6,
            transcendentals=0,
        ),
    )(grads, grads2, weights, weights2)


PIECES = 16
MESH = pl.DeviceIdType.MESH


def flip(value, mask):
    result = value
    for b in range(mask.bit_length()):
        if mask >> b & 1:
            result = result + (1 << b) * (1 - 2 * ((value // (1 << b)) % 2))
    return result


class Exchange:
    names = ("a", "b", "c", "d", "e", "f", "g")

    def __init__(self, bits, count, rows, width):
        self.bits, self.count, self.rows, self.width = bits, count, rows, width
        self.half, self.quarter, self.piece = rows // 2, rows // 4, rows // PIECES
        self.extra = list(range(4, bits))

    def scratch(self):
        k, w = self.count, self.width
        shapes = [
            pltpu.VMEM((k, 2, self.half, w), bf16),
            pltpu.VMEM((k, self.half, w), bf16),
            pltpu.VMEM((k, self.half, w), bf16),
            pltpu.VMEM((k, self.quarter, w), bf16),
            pltpu.VMEM((k, self.quarter, w), bf16),
            pltpu.VMEM((k, self.quarter, w), f32),
            pltpu.VMEM((k, 3, self.piece, w), bf16),
            pltpu.VMEM((k, 3, self.piece, w), bf16),
        ]
        for lanes in (2, 1, 1, 3, 3, 1, 1):
            shapes += [pltpu.SemaphoreType.DMA((k, lanes))] * 2
        if self.extra:
            n = len(self.extra)
            shapes += [pltpu.VMEM((k, 2 * n, self.piece, w), bf16)]
            shapes += [pltpu.SemaphoreType.DMA((k, n))] * 2
        return shapes

    def bind(self, place, part, refs):
        (self.a_in, self.b_out, self.b_in, self.c_out, self.c_in, self.keep) = refs[:6]
        self.d_out, self.d_in = refs[6:8]
        self.sems = {
            name: (refs[8 + 2 * i], refs[9 + 2 * i]) for i, name in enumerate(self.names)
        }
        if self.extra:
            self.x_buf, self.x_send, self.x_recv = refs[22:25]
        self.place, self.part = place, part
        self.core, self.x, self.z = place % 2, (place // 2) % 2, (place // 4) % 4
        self.sibling = {"dp": flip(place, 1)}
        self.beside = {"dp": flip(place, 2)}
        self.across = {"mp": 1 - part}
        self.peers = [{"dp": flip(place, j << 2)} for j in range(1, 4)]
        self.partners = [self.sibling, self.beside, self.across] + self.peers
        self.partners += [{"dp": flip(place, 1 << b)} for b in self.extra]
        return self

    def greet(self):
        barrier = pltpu.get_barrier_semaphore()
        for partner in self.partners:
            pl.semaphore_signal(barrier, inc=1, device_id=partner, device_id_type=MESH)
        pl.semaphore_wait(barrier, len(self.partners))

    def copy(self, name, k, lane, source, target, device):
        out, into = self.sems[name]
        return pltpu.make_async_remote_copy(
            src_ref=source,
            dst_ref=target,
            send_sem=out.at[k, lane],
            recv_sem=into.at[k, lane],
            device_id=device,
            device_id_type=MESH,
        )

    def rows_at(self, start, size):
        return pl.ds(pl.multiple_of(start, PIECES), size)

    def copy_a(self, k, lane, grads):
        source = grads.at[k, self.rows_at((1 - self.core) * self.half, self.half)]
        return self.copy("a", k, lane, source, self.a_in.at[k, lane], self.sibling)

    def copy_b(self, k):
        return self.copy("b", k, 0, self.b_out.at[k], self.b_in.at[k], self.across)

    def copy_c(self, k):
        return self.copy("c", k, 0, self.c_out.at[k], self.c_in.at[k], self.beside)

    def copy_d(self, k, j):
        return self.copy("d", k, j, self.d_out.at[k, j], self.d_in.at[k, j], self.peers[j])

    def spot(self, change=0):
        start = self.core * self.half + self.x * self.quarter
        return self.rows_at(start + flip(self.z, change) * self.piece, self.piece)

    def copy_e(self, k, j, full):
        rows = full.at[k, self.spot()]
        return self.copy("e", k, j, rows, rows, self.peers[j])

    def copy_f(self, k, full):
        start = self.core * self.half + self.x * self.quarter
        rows = full.at[k, self.rows_at(start, self.quarter)]
        return self.copy("f", k, 0, rows, rows, self.beside)

    def copy_g(self, k, full):
        rows = full.at[k, self.rows_at(self.core * self.half, self.half)]
        return self.copy("g", k, 0, rows, rows, self.sibling)

    def start_a(self, k, lane, grads):
        self.copy_a(k, lane, grads).start()

    def stage_b(self, k, others):
        self.copy_a(k, 0, others).wait()
        mine = others[k, self.rows_at(self.core * self.half, self.half), :].astype(f32)
        self.b_out[k] = (mine + self.a_in[k, 0].astype(f32)).astype(bf16)
        self.copy_b(k).start()

    def stage_c(self, k, grads):
        self.copy_a(k, 1, grads).wait()
        self.copy_b(k).wait()

        def total(which):
            inner = which * self.quarter
            rows = self.rows_at(inner, self.quarter)
            mine = grads[k, self.rows_at(self.core * self.half + inner, self.quarter), :]
            got = self.a_in[k, 1, rows, :].astype(f32) + self.b_in[k, rows, :].astype(f32)
            return mine.astype(f32) + got

        self.c_out[k] = total(1 - self.x).astype(bf16)
        self.copy_c(k).start()
        self.keep[k] = total(self.x)

    def stage_d(self, k):
        self.copy_c(k).wait()
        for j in range(4):
            rows = self.rows_at(flip(self.z, j) * self.piece, self.piece)
            total = self.keep[k, rows, :] + self.c_in[k, rows, :].astype(f32)
            if j:
                self.d_out[k, j - 1] = total.astype(bf16)
                self.copy_d(k, j - 1).start()
            else:
                self.keep[k, rows, :] = total

    def stage_e(self, k, full):
        rows = self.rows_at(self.z * self.piece, self.piece)
        total = self.keep[k, rows, :]
        for j in range(3):
            self.copy_d(k, j).wait()
            total = total + self.d_in[k, j].astype(f32)
        for i, b in enumerate(self.extra):
            mine = self.x_buf.at[k, 2 * i]
            mine[...] = total.astype(bf16)
            swap = pltpu.make_async_remote_copy(
                src_ref=mine,
                dst_ref=self.x_buf.at[k, 2 * i + 1],
                send_sem=self.x_send.at[k, i],
                recv_sem=self.x_recv.at[k, i],
                device_id={"dp": flip(self.place, 1 << b)},
                device_id_type=MESH,
            )
            swap.start()
            swap.wait()
            total = total.astype(bf16).astype(f32) + self.x_buf[k, 2 * i + 1].astype(f32)
        full[k, self.spot(), :] = total.astype(bf16)
        for j in range(3):
            self.copy_e(k, j, full).start()

    def stage_f(self, k, full):
        for j in range(3):
            self.copy_e(k, j, full).wait()
        self.copy_f(k, full).start()

    def stage_g(self, k, full):
        self.copy_f(k, full).wait()
        self.copy_g(k, full).start()

    def stage_h(self, k, full):
        self.copy_g(k, full).wait()


def at_step(step, count, action):
    @pl.when(jnp.logical_and(step >= 0, step < count))
    def _():
        action(step)


HIDDEN_TILE = 256
ROW_TILE = 256


def normal(values):
    average = jnp.mean(values, axis=-1, keepdims=True)
    centred = values - average
    variance = jnp.mean(centred * centred, axis=-1, keepdims=True)
    scale = lax.rsqrt(variance + epsilon)
    return centred * scale, scale


def middle_kernel(exchange, tiles, *refs):
    (
        x_ref,
        att_ref,
        att2_ref,
        wout_ref,
        wout2_ref,
        dy_ref,
        gain_ref,
        shift_ref,
        bdown_ref,
        bup_ref,
        up_hbm,
        down_hbm,
        out_ref,
        mid_ref,
        datt_ref,
        datt2_ref,
        gout_ref,
        gout2_ref,
        gbup_ref,
        small_ref,
        full_ref,
        up_buf,
        down_buf,
        load_sem,
        n2_ref,
        total_ref,
        dn2_ref,
        act_ref,
        dpre_ref,
        grad_ref,
        *rest,
    ) = refs
    place, part = lax.axis_index("dp"), lax.axis_index("mp")
    ex = exchange.bind(place, part, rest)
    count = ex.count
    rows_all = x_ref.shape[0]
    blocks = rows_all // ROW_TILE
    width = x_ref.shape[1]

    def loads(i):
        slot = i % 2
        cols = pl.ds(pl.multiple_of(i * HIDDEN_TILE, HIDDEN_TILE), HIDDEN_TILE)
        return (
            pltpu.make_async_copy(up_hbm.at[:, cols], up_buf.at[slot], load_sem.at[slot, 0]),
            pltpu.make_async_copy(down_hbm.at[cols, :], down_buf.at[slot], load_sem.at[slot, 1]),
        )

    for load in loads(0):
        load.start()
    ex.greet()

    def prologue(r, _):
        rows = pl.ds(pl.multiple_of(r * ROW_TILE, ROW_TILE), ROW_TILE)
        branch = dot(att_ref[rows, :], wout_ref[...]) + dot(att2_ref[rows, :], wout2_ref[...])
        mid = x_ref[rows, :].astype(f32) + branch
        mid_ref[rows, :] = mid
        n2_ref[rows, :] = (normal(mid)[0] * gain_ref[...] + shift_ref[...]).astype(bf16)
        total_ref[rows, :] = mid + bdown_ref[...]
        dn2_ref[rows, :] = jnp.zeros((ROW_TILE, width), f32)
        return 0

    lax.fori_loop(0, blocks, prologue, 0)

    def tile(i):
        slot = i % 2
        for load in loads(i):
            load.wait()

        @pl.when(i + 1 < tiles)
        def _():
            for load in loads(i + 1):
                load.start()

        up, down = up_buf.at[slot], down_buf.at[slot]
        bias_grad = jnp.zeros((1, HIDDEN_TILE), f32)
        for r in range(blocks):
            rows = slice(r * ROW_TILE, (r + 1) * ROW_TILE)
            pre = dot(n2_ref[rows, :], up[...]) + bup_ref[i]
            square = pre * pre
            bend = jnp.tanh(0.7978845608028654 * (pre + 0.044715 * square * pre))
            part_one = 0.5 * (1.0 + bend)
            act = (pre * part_one).astype(bf16)
            slope = part_one + (0.5 * pre) * (1.0 - bend * bend) * (
                0.7978845608028654 * (1.0 + 3.0 * 0.044715 * square)
            )
            d_act = dot(dy_ref[rows, :], down[...], NT)
            d_pre = (d_act * slope).astype(bf16)
            act_ref[rows, :] = act
            dpre_ref[rows, :] = d_pre
            bias_grad = bias_grad + jnp.sum(d_pre.astype(f32), axis=0, keepdims=True)
            total_ref[rows, :] += dot(act, down[...])
            dn2_ref[rows, :] += dot(d_pre, up[...], NT)
        gbup_ref[i] = bias_grad
        k = i % count
        grad_ref[k, :, :width] = dot(act_ref[...].T, dy_ref[...]).astype(bf16)
        grad_ref[k, :, width:] = dot(dpre_ref[...].T, n2_ref[...]).astype(bf16)

    def steps(i, lanes):
        at_step(i - count - 7, count, lambda k: ex.stage_h(k, full_ref))
        at_step(i - count - 6, count, lambda k: ex.stage_g(k, full_ref))
        at_step(i - count - 5, count, lambda k: ex.stage_f(k, full_ref))
        at_step(i - count - 4, count, lambda k: ex.stage_e(k, full_ref))
        at_step(i - count - 3, count, lambda k: ex.stage_d(k))
        at_step(i - count - 2, count, lambda k: ex.stage_c(k, grad_ref))
        at_step(i - 1, count, lambda k: ex.stage_b(k, grad_ref))

    def main(i, _):
        tile(i)
        at_step(i, count, lambda k: ex.start_a(k, 0, grad_ref))
        at_step(i - count, count, lambda k: ex.start_a(k, 1, grad_ref))
        steps(i, None)
        return 0

    lax.fori_loop(0, tiles, main, 0)

    def epilogue(r, sums):
        rows = pl.ds(pl.multiple_of(r * ROW_TILE, ROW_TILE), ROW_TILE)
        out_ref[rows, :] = total_ref[rows, :].astype(bf16)
        unit, scale = normal(mid_ref[rows, :])
        d_rows = dn2_ref[rows, :]
        dy = dy_ref[rows, :].astype(f32)
        lean = d_rows * gain_ref[...]
        d_mid = dy + scale * (
            lean
            - jnp.mean(lean, axis=-1, keepdims=True)
            - unit * jnp.mean(lean * unit, axis=-1, keepdims=True)
        )
        mid_ref[rows, :] = d_mid
        d_branch = d_mid.astype(bf16)
        n2_ref[rows, :] = d_branch
        datt_ref[rows, :] = dot(d_branch, wout_ref[...], NT).astype(bf16)
        datt2_ref[rows, :] = dot(d_branch, wout2_ref[...], NT).astype(bf16)
        add = lambda values: jnp.sum(values, axis=0, keepdims=True)
        return (sums[0] + add(d_rows * unit), sums[1] + add(d_rows), sums[2] + add(dy))

    zero = jnp.zeros((1, width), f32)
    sums = lax.fori_loop(0, blocks, epilogue, (zero, zero, zero))
    for j in range(3):
        small_ref[j : j + 1, :] = sums[j]
    gout_ref[...] = dot(att_ref[...].T, n2_ref[...]).astype(bf16)
    gout2_ref[...] = dot(att2_ref[...].T, n2_ref[...]).astype(bf16)

    def drain(i, _):
        steps(i, None)
        return 0

    lax.fori_loop(tiles, tiles + count + 2, drain, 0)


def middle(bits, x, att, att2, wout, wout2, dy, gain, shift, bdown, bup, up, down):
    rows, width = x.shape
    hidden = up.shape[1]
    tiles = hidden // HIDDEN_TILE
    count = tiles // 2
    exchange = Exchange(bits, count, HIDDEN_TILE, 2 * width)
    vmem = pl.BlockSpec(memory_space=pltpu.VMEM)
    hbm = pl.BlockSpec(memory_space=pl.ANY)
    shape = jax.ShapeDtypeStruct
    return pl.pallas_call(
        functools.partial(middle_kernel, exchange, tiles),
        in_specs=[vmem] * 10 + [hbm] * 2,
        out_specs=[vmem] * 9,
        out_shape=[
            shape((rows, width), bf16),
            shape((rows, width), f32),
            shape(att.shape, bf16),
            shape(att2.shape, bf16),
            shape(wout.shape, bf16),
            shape(wout2.shape, bf16),
            shape((tiles, 1, HIDDEN_TILE), f32),
            shape((8, width), f32),
            shape((count, HIDDEN_TILE, 2 * width), bf16),
        ],
        scratch_shapes=[
            pltpu.VMEM((2, width, HIDDEN_TILE), bf16),
            pltpu.VMEM((2, HIDDEN_TILE, width), bf16),
            pltpu.SemaphoreType.DMA((2, 2)),
            pltpu.VMEM((rows, width), bf16),
            pltpu.VMEM((rows, width), f32),
            pltpu.VMEM((rows, width), f32),
            pltpu.VMEM((rows, HIDDEN_TILE), bf16),
            pltpu.VMEM((rows, HIDDEN_TILE), bf16),
            pltpu.VMEM((count, HIDDEN_TILE, 2 * width), bf16),
        ]
        + exchange.scratch(),
        compiler_params=pltpu.CompilerParams(
            collective_id=0, has_side_effects=True, vmem_limit_bytes=67043328
        ),
        name="middle",
        cost_estimate=pl.CostEstimate(
            flops=40 * 10**9, bytes_accessed=40 * 10**6, transcendentals=4 * 10**6
        ),
    )(x, att, att2, wout, wout2, dy, gain, shift, bdown, bup, up, down)


def sum_kernel(
    exchange, mine_ref, others_ref, small_ref, small2_ref, full_ref, sums_ref, got_ref, work_ref, small_send, small_recv, *rest
):
    place, part = lax.axis_index("dp"), lax.axis_index("mp")
    ex = exchange.bind(place, part, rest)
    count, bits = ex.count, ex.bits
    ex.greet()

    def small_copy(s):
        source = small2_ref if s == 0 else work_ref.at[s - 1]
        device = ex.across if s == 0 else {"dp": flip(place, 1 << (s - 1))}
        return pltpu.make_async_remote_copy(
            src_ref=source,
            dst_ref=got_ref.at[s],
            send_sem=small_send.at[s],
            recv_sem=small_recv.at[s],
            device_id=device,
            device_id_type=MESH,
        )

    def small_step(s):
        small_copy(s).wait()
        before = small_ref[...] if s == 0 else work_ref[s - 1]
        work_ref[s] = before + got_ref[s]
        if s < bits:
            small_copy(s + 1).start()
        else:
            sums_ref[...] = work_ref[s]

    def begin(k, _):
        ex.start_a(k, 0, others_ref)
        return 0

    lax.fori_loop(0, count, begin, 0)
    small_copy(0).start()

    def second(k, _):
        ex.start_a(k, 1, mine_ref)
        return 0

    lax.fori_loop(0, count, second, 0)

    def cross(k, _):
        ex.stage_b(k, others_ref)
        return 0

    lax.fori_loop(0, count, cross, 0)

    def steps(i, _):
        at_step(i - 5, count, lambda k: ex.stage_h(k, full_ref))
        at_step(i - 4, count, lambda k: ex.stage_g(k, full_ref))
        at_step(i - 3, count, lambda k: ex.stage_f(k, full_ref))
        at_step(i - 2, count, lambda k: ex.stage_e(k, full_ref))
        at_step(i - 1, count, lambda k: ex.stage_d(k))
        at_step(i, count, lambda k: ex.stage_c(k, mine_ref))
        for s in range(bits + 1):
            pl.when(i == s + 1)(functools.partial(small_step, s))
        return 0

    lax.fori_loop(0, count + 6, steps, 0)


def sum_chunks(bits, mine, others, small, small2):
    count, rows, width = mine.shape
    exchange = Exchange(bits, count, rows, width)
    vmem = pl.BlockSpec(memory_space=pltpu.VMEM)
    return pl.pallas_call(
        functools.partial(sum_kernel, exchange),
        in_specs=[vmem] * 4,
        out_specs=[vmem] * 2,
        out_shape=[
            jax.ShapeDtypeStruct(mine.shape, bf16),
            jax.ShapeDtypeStruct(small.shape, f32),
        ],
        scratch_shapes=[
            pltpu.VMEM((bits + 1,) + small.shape, f32),
            pltpu.VMEM((bits + 1,) + small.shape, f32),
            pltpu.SemaphoreType.DMA((bits + 1,)),
            pltpu.SemaphoreType.DMA((bits + 1,)),
        ]
        + exchange.scratch(),
        compiler_params=pltpu.CompilerParams(
            collective_id=1, has_side_effects=True, vmem_limit_bytes=67043328
        ),
        name="sum_chunks",
        cost_estimate=pl.CostEstimate(
            flops=40 * 10**9, bytes_accessed=40 * 10**6, transcendentals=0
        ),
    )(mine, others, small, small2)


def key_layout(seq_lengths, block_len, part):
    index = jnp.arange(KEY_ROWS, dtype=jnp.int32)
    own = part * HALF
    token = jnp.where(
        index < NOISY_BASE, index + (own - HALF), index - NOISY_BASE + (own - EDGE)
    )
    ends = jnp.cumsum(seq_lengths)
    passed = token[:, None] >= ends[None, :]
    starts = jnp.sum(jnp.where(passed, seq_lengths[None, :], 0), axis=1)
    lengths_here = jnp.where(passed, 0, ends[None, :])
    stops = jnp.min(jnp.where(passed, TOK_DEV, lengths_here), axis=1)
    positions = token - starts
    block_start = starts + positions // block_len * block_len
    block_stop = jnp.minimum(block_start + block_len, stops)
    mine = slice(CLEAN_OWN, CLEAN_OWN + HALF)
    low, start, stop = starts[mine], block_start[mine], block_stop[mine]
    to_clean = own - HALF
    tiles = lambda column: column.reshape(TILES, 1, TILE)
    clean_bounds = jnp.concatenate(
        [
            jnp.concatenate([tiles(low - to_clean), tiles(low - to_clean)], axis=2),
            jnp.concatenate([tiles(start - to_clean), tiles(stop - to_clean)], axis=2),
        ],
        axis=1,
    )
    to_window = own - EDGE + TILE * jnp.arange(TILES, dtype=jnp.int32)[:, None, None]
    noisy_bounds = jnp.concatenate(
        [tiles(start) - to_window, tiles(stop) - to_window], axis=1
    )
    first = jnp.min(clean_bounds[:, 0], axis=1) // EDGE * EDGE
    last = jnp.max(clean_bounds[:, 1], axis=1)
    trips = (last - first + KEY_TILE - 1) // KEY_TILE
    spans = jnp.stack([first, trips], axis=1)
    lane = jnp.arange(LANES, dtype=jnp.int32)
    frequency = jnp.exp(
        (lane % (HD // 2)).astype(f32) * (-math.log(10000.0) / (HD // 2))
    )
    angles = positions.astype(f32)[:, None] * frequency[None, :]
    sign = jnp.where(lane % HD < HD // 2, -1.0, 1.0)
    return spans, clean_bounds, noisy_bounds, jnp.cos(angles), jnp.sin(angles) * sign


def half_of(array, which):
    size = array.shape[0] // 2
    return lax.dynamic_slice_in_dim(array, which * size, size, 0)


def in_order(bit, mine, theirs):
    flip = bit == 0
    return jnp.concatenate(
        [jnp.where(flip, mine, theirs), jnp.where(flip, theirs, mine)], axis=0
    )


def tie(first, second):
    return lax.optimization_barrier((first, second))


def local(
    dp_size,
    tokens,
    lengths,
    block_size,
    cotangent,
    ln1_gain,
    ln1_bias,
    w_qkv,
    w_out,
    ln2_gain,
    ln2_bias,
    w_up,
    b_up,
    w_down,
    b_down,
):
    width = tokens.shape[2]
    part = lax.axis_index("mp")
    place = lax.axis_index("dp")
    bits = dp_size.bit_length() - 1

    def across(array):
        return lax.ppermute(array, "mp", [(0, 1), (1, 0)])

    def sibling(array):
        return lax.ppermute(array, "dp", [(i, i ^ 1) for i in range(dp_size)])

    def fetch(half):
        here = across(half)
        return here, sibling(here)

    core = place & 1
    edge = jnp.where(part == 0, tokens[0, HALF - EDGE :], tokens[0, :EDGE])
    context = across(jnp.concatenate([tokens[1], edge], axis=0))
    qkv_mine = w_qkv.transpose(1, 0, 2)
    halves = [
        half_of(qkv_mine.reshape(-1, w_qkv.shape[2]), core),
        half_of(w_out, core),
        half_of(w_up, core),
        half_of(w_down, core),
    ]
    context, halves = tie(context, halves)
    fetched = [fetch(half) for half in halves]
    bias_other = across(b_up)

    spans, clean_bounds, noisy_bounds, cosine, sine = key_layout(lengths[0], block_size[0], part)
    clean_other, edge_other = context[:HALF], context[HALF:]
    key_tokens = jnp.concatenate(
        [clean_other, tokens[1], clean_other[:EDGE], edge_other, tokens[0], edge_other], axis=0
    )
    normed1_keys = layer_norm(key_tokens.astype(f32), ln1_gain, ln1_bias).astype(bf16)
    normed1_t = normed1_keys.T

    def attention(weights):
        query, keys, values = project(normed1_keys, weights, cosine, sine)
        attended, lse = attend_forward(spans, clean_bounds, noisy_bounds, query, keys, values)
        return (query, keys, values, attended, lse)

    mine = attention(qkv_mine)
    fetched[0] = tie(fetched[0], mine[3])[0]
    qkv_other = in_order(core, *fetched[0]).reshape(qkv_mine.shape)
    other = attention(qkv_other)
    fetched[1:] = tie(fetched[1:], other[3])[0]
    out_other, up_other, down_other = [in_order(core, *pieces) for pieces in fetched[1:]]
    up_all = jnp.concatenate([up_other, w_up], axis=1)
    down_all = jnp.concatenate([down_other, w_down], axis=0)
    bias_all = jnp.concatenate([bias_other, b_up]).astype(f32).reshape(-1, 1, HIDDEN_TILE)

    as_row = lambda vector: vector.reshape(1, -1)
    out, d_mid, d_att, d_att2, grad_out, grad_out2, grad_bias, norms, full = middle(
        bits,
        tokens.reshape(TOK_DEV, width),
        mine[3],
        other[3],
        w_out,
        out_other,
        cotangent.reshape(TOK_DEV, width),
        as_row(ln2_gain),
        as_row(ln2_bias),
        as_row(b_down),
        bias_all,
        up_all,
        down_all,
    )
    hidden = b_up.shape[0]
    grad_down = full[:, :, :width].reshape(hidden, width).astype(f32)
    grad_up = full[:, :, width:].reshape(hidden, width).T.astype(f32)

    d_qkv, grad_qkv = [], []
    for saved, d_attended in ((other, d_att2), (mine, d_att)):
        query, keys, values, attended, lse = saved
        d_fields, grad = attend_backward(
            spans,
            clean_bounds,
            noisy_bounds,
            query,
            keys,
            values,
            attended,
            d_attended,
            lse,
            cosine,
            sine,
            normed1_t,
        )
        d_qkv.append(d_fields)
        grad_qkv.append(grad)
    pairs = mine[0].shape[1] // LANES

    def by_pair(weights):
        split = weights.reshape(3, width, pairs, LANES)
        return split.transpose(2, 1, 0, 3).reshape(pairs, width, 3 * LANES)

    d_normed1_keys = rows_back(d_qkv[1], d_qkv[0], by_pair(qkv_mine), by_pair(qkv_other))
    clean_back = d_normed1_keys[:HALF]
    clean_back = clean_back.at[:EDGE].add(d_normed1_keys[2 * HALF : 2 * HALF + EDGE])
    edge_back = d_normed1_keys[NOISY_BASE:NOISY_OWN] + d_normed1_keys[NOISY_OWN + HALF :]
    back = across(jnp.concatenate([clean_back, edge_back], axis=0).astype(bf16)).astype(f32)
    at_end = jnp.concatenate([jnp.zeros((HALF - EDGE, width), f32), back[HALF:]], axis=0)
    at_start = jnp.concatenate([back[HALF:], jnp.zeros((HALF - EDGE, width), f32)], axis=0)
    d_normed1 = jnp.concatenate(
        [
            d_normed1_keys[NOISY_OWN : NOISY_OWN + HALF]
            + jnp.where(part == 0, at_end, at_start),
            d_normed1_keys[CLEAN_OWN : CLEAN_OWN + HALF] + back[:HALF],
        ],
        axis=0,
    )
    x_rows = tokens.astype(f32).reshape(TOK_DEV, width)
    norm1_back = jax.vjp(layer_norm, x_rows, ln1_gain, ln1_bias)[1]
    d_x_norm, grad_ln1_gain, grad_ln1_bias = norm1_back(d_normed1)
    grad_tokens = (d_mid + d_x_norm).reshape(tokens.shape)
    shared = jnp.concatenate(
        [norms[:3], as_row(grad_ln1_gain), as_row(grad_ln1_bias), jnp.zeros((1, width), f32)],
        axis=0,
    )
    bias2, bias1 = grad_bias.reshape(2, hidden // width, width)

    def chunks(of_qkv, of_out):
        lanes = 3 * LANES
        flat = jnp.concatenate([of_out[:, :lanes], of_out[:, lanes:]], axis=0)
        return jnp.concatenate(
            [of_qkv.reshape(-1, ROW_TILE, lanes), flat.reshape(-1, ROW_TILE, lanes)], axis=0
        )

    full2, sums = sum_chunks(
        bits,
        chunks(grad_qkv[1], grad_out),
        chunks(grad_qkv[0], grad_out2),
        jnp.concatenate([bias1, shared], axis=0),
        jnp.concatenate([bias2, shared], axis=0),
    )
    split = pairs * width // ROW_TILE
    grad_qkv = full2[:split].reshape(pairs, width, 3, LANES).transpose(1, 2, 0, 3)
    grad_qkv = grad_qkv.reshape(w_qkv.shape).astype(f32)
    flat = full2[split:].reshape(2, w_out.shape[0], 3 * LANES)
    grad_out = jnp.concatenate([flat[0], flat[1]], axis=1).astype(f32)
    lead = hidden // width
    return (
        out.reshape(tokens.shape),
        grad_tokens,
        sums[lead + 3],
        sums[lead + 4],
        grad_qkv,
        grad_out,
        sums[lead],
        sums[lead + 1],
        grad_up,
        sums[:lead].reshape(hidden),
        grad_down,
        sums[lead + 2],
    )


def solution(mesh):
    in_specs = (
        P(None, ("dp", "mp"), None),
        P("dp", None),
        P(),
        P(None, ("dp", "mp"), None),
        P(),
        P(),
        P(None, None, "mp"),
        P("mp", None),
        P(),
        P(),
        P(None, "mp"),
        P("mp"),
        P("mp", None),
        P(),
    )
    out_specs = (
        P(None, ("dp", "mp"), None),
        P(None, ("dp", "mp"), None),
        P(),
        P(),
        P(None, None, "mp"),
        P("mp", None),
        P(),
        P(),
        P(None, "mp"),
        P("mp"),
        P("mp", None),
        P(),
    )
    return jax.shard_map(
        functools.partial(local, mesh.shape["dp"]),
        mesh=mesh,
        in_specs=in_specs,
        out_specs=out_specs,
        check_vma=False,
    )
```

```python
import functools
import math

import jax
import jax.numpy as jnp
from jax import lax
from jax.experimental import pallas as pl
from jax.experimental.pallas import tpu as pltpu
from jax.sharding import PartitionSpec as P

HD = 64
TOK_DEV = 1024
HALF = TOK_DEV // 2
EDGE = 16
CLEAN_OWN = HALF
NOISY_BASE = 2 * HALF + EDGE
NOISY_OWN = NOISY_BASE + EDGE
KEY_ROWS = NOISY_OWN + HALF + EDGE
TILE = 128
TILES = HALF // TILE
WINDOW = TILE + 2 * EDGE
KEY_TILE = 256
LANES = 128
HIDDEN_TILE = 256
ROW_TILE = 256

epsilon = 1e-05
neg_large = -1e30
to_base2 = 0.125 * math.log2(math.e)
f32 = jnp.float32
bf16 = jnp.bfloat16

NN = (((1,), (0,)), ((), ()))
NT = (((1,), (1,)), ((), ()))


def dot(left, right, dims=NN):
    return lax.dot_general(left, right, dims, preferred_element_type=f32)


def low_lanes(shape):
    return lax.broadcasted_iota(jnp.int32, shape, 1) < HD


def turn(values, cosine, sine):
    lane = lax.broadcasted_iota(jnp.int32, values.shape, 1)
    first_half = (lane & (HD - 1)) < HD // 2
    swapped = jnp.where(
        first_half,
        pltpu.roll(values, LANES - HD // 2, 1),
        pltpu.roll(values, HD // 2, 1),
    )
    return values * cosine + swapped * sine


def project_rows(rows, w_ref, cosine, sine, q_ref, k_ref, v_ref, at):
    for part, out_ref in ((0, q_ref), (1, k_ref)):
        field = dot(rows, w_ref[part])
        for pair in range(field.shape[1] // LANES):
            cols = slice(pair * LANES, (pair + 1) * LANES)
            out_ref[at, cols] = turn(field[:, cols], cosine, sine).astype(bf16)
    v_ref[at, :] = dot(rows, w_ref[2]).astype(bf16)


def project_kernel(rows_ref, w_ref, cos_ref, sin_ref, q_ref, k_ref, v_ref):
    at = slice(0, rows_ref.shape[0])
    project_rows(rows_ref[...], w_ref, cos_ref[...], sin_ref[...], q_ref, k_ref, v_ref, at)


def project(rows, weights, cosine, sine):
    count, width = rows.shape
    cols = weights.shape[2]
    step = count // 3
    row_spec = pl.BlockSpec((step, width), lambda i: (i, 0))
    table_spec = pl.BlockSpec((step, LANES), lambda i: (i, 0))
    out_spec = pl.BlockSpec((step, cols), lambda i: (i, 0))
    shape = jax.ShapeDtypeStruct((count, cols), bf16)
    return pl.pallas_call(
        project_kernel,
        grid=(3,),
        in_specs=[
            row_spec,
            pl.BlockSpec(weights.shape, lambda i: (0, 0, 0)),
            table_spec,
            table_spec,
        ],
        out_specs=[out_spec] * 3,
        out_shape=[shape] * 3,
        name="project",
        cost_estimate=pl.CostEstimate(
            flops=2 * count * width * 3 * cols,
            bytes_accessed=2 * (count * (width + 3 * cols) + 3 * width * cols),
            transcendentals=0,
        ),
    )(rows, weights, cosine, sine)


def normal(values):
    average = jnp.mean(values, axis=-1, keepdims=True)
    centred = values - average
    variance = jnp.mean(centred * centred, axis=-1, keepdims=True)
    scale = lax.rsqrt(variance + epsilon)
    return centred * scale, scale


def enter_kernel(
    tokens_ref,
    context_ref,
    gain_ref,
    shift_ref,
    w_ref,
    cos_ref,
    sin_ref,
    rows_ref,
    rows_t_ref,
    q_ref,
    k_ref,
    v_ref,
):
    def norm(values):
        return (normal(values.astype(f32))[0] * gain_ref[...] + shift_ref[...]).astype(bf16)

    def blocks(i, _):
        source = pl.ds(pl.multiple_of(i * TILE, TILE), TILE)
        rows_ref[source, :] = norm(context_ref[source, :])
        at = pl.ds(pl.multiple_of(CLEAN_OWN + i * TILE, TILE), TILE)
        rows_ref[at, :] = norm(tokens_ref[1, source, :])
        at = pl.ds(pl.multiple_of(NOISY_OWN + i * TILE, EDGE), TILE)
        rows_ref[at, :] = norm(tokens_ref[0, source, :])
        return 0

    lax.fori_loop(0, TILES, blocks, 0)
    rows_ref[2 * HALF : NOISY_BASE, :] = rows_ref[:EDGE, :]
    edge = norm(context_ref[HALF:, :])
    rows_ref[NOISY_BASE:NOISY_OWN, :] = edge
    rows_ref[NOISY_OWN + HALF :, :] = edge
    step = KEY_ROWS // 3

    def fields(i, _):
        at = pl.ds(pl.multiple_of(i * step, EDGE), step)
        project_rows(
            rows_ref[at, :], w_ref, cos_ref[at, :], sin_ref[at, :], q_ref, k_ref, v_ref, at
        )
        return 0

    lax.fori_loop(0, 3, fields, 0)
    for c in range(rows_t_ref.shape[0] // LANES):
        cols = slice(c * LANES, (c + 1) * LANES)
        rows_t_ref[cols, :] = rows_ref[:, cols].T


def enter(tokens, context, gain, shift, weights, cosine, sine):
    width, cols = weights.shape[1:]
    vmem = pl.BlockSpec(memory_space=pltpu.VMEM)
    shape = jax.ShapeDtypeStruct
    field = shape((KEY_ROWS, cols), bf16)
    return pl.pallas_call(
        enter_kernel,
        in_specs=[vmem] * 7,
        out_specs=[vmem] * 5,
        out_shape=[shape((KEY_ROWS, width), bf16), shape((width, KEY_ROWS), bf16)] + [field] * 3,
        name="enter",
        cost_estimate=pl.CostEstimate(
            flops=10**10, bytes_accessed=16 * 10**6, transcendentals=0
        ),
    )(tokens, context, gain, shift, weights, cosine, sine)


def split_heads(rows):
    low = low_lanes(rows.shape)
    zero = jnp.zeros_like(rows)
    return jnp.where(low, rows, zero), jnp.where(low, zero, rows)


def between(shape, offset, low, high):
    index = lax.broadcasted_iota(jnp.int32, shape, 0) + offset
    return jnp.logical_and(index >= low, index < high)


def forward_kernel(
    span_ref, clean_ref, noisy_ref, q_ref, k_ref, v_ref, out_ref, lse_ref
):
    def one_tile(t, _):
        clean_at = pl.multiple_of(CLEAN_OWN + t * TILE, TILE)
        noisy_at = pl.multiple_of(NOISY_OWN + t * TILE, EDGE)
        window_at = pl.multiple_of(NOISY_BASE + t * TILE, EDGE)
        query = jnp.concatenate(
            [q_ref[pl.ds(noisy_at, TILE), :], q_ref[pl.ds(clean_at, TILE), :]], axis=0
        )
        queries = split_heads(query)
        key_low, key_high = clean_ref[t, 0:1, :], clean_ref[t, 1:2, :]
        own_low, own_high = noisy_ref[t, 0:1, :], noisy_ref[t, 1:2, :]
        keys = k_ref[pl.ds(window_at, WINDOW), :]
        values_t = v_ref[pl.ds(window_at, WINDOW), :].T
        allowed = between((WINDOW, TILE), 0, own_low, own_high)
        state = []
        for head in range(2):
            scores = dot(keys, queries[head][:TILE], NT) * to_base2
            scores = jnp.where(allowed, scores, neg_large)
            top = jnp.max(scores, axis=0, keepdims=True)
            expo = jnp.exp2(scores - top)
            total = jnp.sum(expo, axis=0, keepdims=True)
            mixed = dot(values_t[head * HD : (head + 1) * HD], expo.astype(bf16))
            blank = jnp.zeros((1, TILE), f32)
            state += [
                jnp.concatenate([top, blank + neg_large], axis=1),
                jnp.concatenate([total, blank], axis=1),
                jnp.concatenate([mixed, jnp.zeros((HD, TILE), f32)], axis=1),
            ]
        first_key, trips = span_ref[t, 0], span_ref[t, 1]

        def one_step(j, state):
            at = pl.multiple_of(first_key + j * KEY_TILE, EDGE)
            keys = k_ref[pl.ds(at, KEY_TILE), :]
            values_t = v_ref[pl.ds(at, KEY_TILE), :].T
            allowed = between((KEY_TILE, 2 * TILE), at, key_low, key_high)
            after = []
            for head in range(2):
                top, total, mixed = state[3 * head : 3 * head + 3]
                scores = dot(keys, queries[head], NT) * to_base2
                scores = jnp.where(allowed, scores, neg_large)
                new_top = jnp.maximum(top, jnp.max(scores, axis=0, keepdims=True))
                keep = jnp.exp2(top - new_top)
                expo = jnp.exp2(scores - new_top)
                after += [
                    new_top,
                    total * keep + jnp.sum(expo, axis=0, keepdims=True),
                    mixed * keep
                    + dot(values_t[head * HD : (head + 1) * HD], expo.astype(bf16)),
                ]
            return tuple(after)

        state = lax.fori_loop(0, trips, one_step, tuple(state))
        pair = jnp.concatenate(
            [state[2] / state[1], state[5] / state[4]], axis=0
        ).T.astype(bf16)
        out_at = pl.multiple_of(t * TILE, TILE)
        out_ref[pl.ds(out_at, TILE), :] = pair[:TILE]
        out_ref[pl.ds(pl.multiple_of(HALF + t * TILE, TILE), TILE), :] = pair[TILE:]
        lse_ref[0, t, 0:1, :] = state[0] + jnp.log2(state[1])
        lse_ref[0, t, 1:2, :] = state[3] + jnp.log2(state[4])
        return 0

    lax.fori_loop(0, TILES, one_tile, 0)


def attend_forward(spans, clean_bounds, noisy_bounds, query, keys, values):
    count, cols = query.shape
    pairs = cols // LANES
    whole3 = lambda array: pl.BlockSpec(array.shape, lambda p, s: (0, 0, 0))
    row_spec = pl.BlockSpec((count, LANES), lambda p, s: (0, p))
    work = pairs * 2 * 2 * HALF * TOK_DEV
    return pl.pallas_call(
        forward_kernel,
        grid_spec=pltpu.PrefetchScalarGridSpec(
            num_scalar_prefetch=1,
            grid=(pairs,),
            in_specs=[whole3(clean_bounds), whole3(noisy_bounds)] + [row_spec] * 3,
            out_specs=[
                pl.BlockSpec((TOK_DEV, LANES), lambda p, s: (0, p)),
                pl.BlockSpec((1, TILES, 2, 2 * TILE), lambda p, s: (p, 0, 0, 0)),
            ],
        ),
        out_shape=[
            jax.ShapeDtypeStruct((TOK_DEV, cols), bf16),
            jax.ShapeDtypeStruct((pairs, TILES, 2, 2 * TILE), f32),
        ],
        name="attend_forward",
        cost_estimate=pl.CostEstimate(
            flops=4 * work * HD, bytes_accessed=8 * count * cols, transcendentals=work
        ),
    )(spans, clean_bounds, noisy_bounds, query, keys, values)


def backward_kernel(
    span_ref,
    clean_ref,
    noisy_ref,
    q_ref,
    k_ref,
    v_ref,
    o_ref,
    d_ref,
    lse_ref,
    cos_ref,
    sin_ref,
    rows_ref,
    out_ref,
    grad_ref,
    dk_ref,
    dv_ref,
    fields_ref,
):
    dk_ref[...] = jnp.zeros_like(dk_ref)
    dv_ref[...] = jnp.zeros_like(dv_ref)
    fields_ref[:, :LANES] = jnp.zeros((KEY_ROWS, LANES), bf16)

    def one_tile(t, _):
        clean_at = pl.multiple_of(CLEAN_OWN + t * TILE, TILE)
        noisy_at = pl.multiple_of(NOISY_OWN + t * TILE, EDGE)
        window_at = pl.multiple_of(NOISY_BASE + t * TILE, EDGE)
        low_at = pl.multiple_of(t * TILE, TILE)
        high_at = pl.multiple_of(HALF + t * TILE, TILE)

        def both(ref, low, high):
            return jnp.concatenate(
                [ref[pl.ds(low, TILE), :], ref[pl.ds(high, TILE), :]], axis=0
            )

        query = split_heads(both(q_ref, noisy_at, clean_at))
        d_rows = both(d_ref, low_at, high_at)
        o_rows = both(o_ref, low_at, high_at)
        product = (d_rows.astype(f32) * o_rows.astype(f32)).T
        d_out = split_heads(d_rows)
        inner = [
            jnp.sum(product[head * HD : (head + 1) * HD], axis=0, keepdims=True)
            for head in range(2)
        ]
        lse = [lse_ref[0, t, head : head + 1, :] for head in range(2)]
        key_low, key_high = clean_ref[t, 0:1, :], clean_ref[t, 1:2, :]
        own_low, own_high = noisy_ref[t, 0:1, :], noisy_ref[t, 1:2, :]

        def accumulate(at, rows, cols, allowed, d_query):
            keys = k_ref[pl.ds(at, rows), :]
            values = v_ref[pl.ds(at, rows), :]
            keys_t = keys.T
            weights, d_scores, after = [], [], []
            for head in range(2):
                scores = dot(keys, query[head][:cols], NT) * to_base2
                scores = jnp.where(allowed, scores - lse[head][:, :cols], neg_large)
                probs = jnp.exp2(scores)
                d_probs = dot(values, d_out[head][:cols], NT)
                d_score = (probs * (d_probs - inner[head][:, :cols]) * 0.125).astype(bf16)
                weights.append(probs.astype(bf16))
                d_scores.append(d_score)
                after.append(
                    d_query[head] + dot(keys_t[head * HD : (head + 1) * HD], d_score)
                )
            stack = lambda parts: jnp.concatenate([part[:cols] for part in parts], axis=0)
            dv_ref[pl.ds(at, rows), :] += dot(
                jnp.concatenate(weights, axis=1), stack(d_out)
            )
            dk_ref[pl.ds(at, rows), :] += dot(
                jnp.concatenate(d_scores, axis=1), stack(query)
            )
            return tuple(after)

        allowed = between((WINDOW, TILE), 0, own_low, own_high)
        zero = jnp.zeros((HD, TILE), f32)
        start = accumulate(window_at, WINDOW, TILE, allowed, (zero, zero))
        start = tuple(jnp.concatenate([part, zero], axis=1) for part in start)
        first_key, trips = span_ref[t, 0], span_ref[t, 1]

        def one_step(j, d_query):
            at = pl.multiple_of(first_key + j * KEY_TILE, EDGE)
            allowed = between((KEY_TILE, 2 * TILE), at, key_low, key_high)
            return accumulate(at, KEY_TILE, 2 * TILE, allowed, d_query)

        d_query = lax.fori_loop(0, trips, one_step, start)
        d_query = jnp.concatenate(d_query, axis=0).T
        for at, part in ((noisy_at, d_query[:TILE]), (clean_at, d_query[TILE:])):
            turned = turn(part, cos_ref[pl.ds(at, TILE), :], -sin_ref[pl.ds(at, TILE), :])
            fields_ref[pl.ds(at, TILE), :LANES] = turned.astype(bf16)
        return 0

    lax.fori_loop(0, TILES, one_tile, 0)
    step = KEY_ROWS // 9

    def finish(i, _):
        rows = pl.ds(pl.multiple_of(i * step, EDGE), step)
        fields_ref[rows, LANES : 2 * LANES] = turn(
            dk_ref[rows, :], cos_ref[rows, :], -sin_ref[rows, :]
        ).astype(bf16)
        fields_ref[rows, 2 * LANES :] = dv_ref[rows, :].astype(bf16)
        for c in range(3):
            out_ref[c, rows, :] = fields_ref[rows, c * LANES : (c + 1) * LANES]
        return 0

    lax.fori_loop(0, 9, finish, 0)

    def weight_rows(i, _):
        rows = pl.ds(pl.multiple_of(i * ROW_TILE, LANES), ROW_TILE)
        grad = dot(rows_ref[rows, :], fields_ref[...]).astype(bf16)
        for c in range(3):
            grad_ref[c, rows, :] = grad[:, c * LANES : (c + 1) * LANES]
        return 0

    lax.fori_loop(0, rows_ref.shape[0] // ROW_TILE, weight_rows, 0)


def attend_backward(
    spans,
    clean_bounds,
    noisy_bounds,
    query,
    keys,
    values,
    attended,
    d_attended,
    lse,
    cosine,
    sine,
    rows_t,
):
    count, cols = query.shape
    pairs = cols // LANES
    width = rows_t.shape[0]
    whole2 = lambda array: pl.BlockSpec(array.shape, lambda p, s: (0, 0))
    whole3 = lambda array: pl.BlockSpec(array.shape, lambda p, s: (0, 0, 0))
    row_spec = pl.BlockSpec((count, LANES), lambda p, s: (0, p))
    own_spec = pl.BlockSpec((TOK_DEV, LANES), lambda p, s: (0, p))
    return pl.pallas_call(
        backward_kernel,
        grid_spec=pltpu.PrefetchScalarGridSpec(
            num_scalar_prefetch=1,
            grid=(pairs,),
            in_specs=[whole3(clean_bounds), whole3(noisy_bounds)]
            + [row_spec] * 3
            + [own_spec] * 2
            + [
                pl.BlockSpec((1, TILES, 2, 2 * TILE), lambda p, s: (p, 0, 0, 0)),
                whole2(cosine),
                whole2(sine),
                whole2(rows_t),
            ],
            out_specs=[
                pl.BlockSpec((3, count, LANES), lambda p, s: (0, 0, p)),
                pl.BlockSpec((3, width, LANES), lambda p, s: (0, 0, p)),
            ],
            scratch_shapes=[pltpu.VMEM((count, LANES), f32)] * 2
            + [pltpu.VMEM((count, 3 * LANES), bf16)],
        ),
        out_shape=[
            jax.ShapeDtypeStruct((3, count, cols), bf16),
            jax.ShapeDtypeStruct((3, width, cols), bf16),
        ],
        name="attend_backward",
        cost_estimate=pl.CostEstimate(
            flops=36 * 10**9, bytes_accessed=36 * 10**6, transcendentals=6 * 10**6
        ),
    )(
        spans,
        clean_bounds,
        noisy_bounds,
        query,
        keys,
        values,
        attended,
        d_attended,
        lse,
        cosine,
        sine,
        rows_t,
    )


PIECES = 16
MESH = pl.DeviceIdType.MESH


def flip(value, mask):
    result = value
    for b in range(mask.bit_length()):
        if mask >> b & 1:
            result = result + (1 << b) * (1 - 2 * ((value // (1 << b)) % 2))
    return result


class Exchange:
    names = ("a", "b", "c", "d", "e", "f", "g")

    def __init__(self, bits, count, rows, width):
        self.bits, self.count, self.rows, self.width = bits, count, rows, width
        self.half, self.quarter, self.piece = rows // 2, rows // 4, rows // PIECES
        self.extra = list(range(4, bits))

    def scratch(self):
        k, w = self.count, self.width
        shapes = [
            pltpu.VMEM((k, 2, self.half, w), bf16),
            pltpu.VMEM((k, self.half, w), bf16),
            pltpu.VMEM((k, self.half, w), bf16),
            pltpu.VMEM((k, self.quarter, w), bf16),
            pltpu.VMEM((k, self.quarter, w), bf16),
            pltpu.VMEM((k, self.quarter, w), f32),
            pltpu.VMEM((k, 3, self.piece, w), bf16),
            pltpu.VMEM((k, 3, self.piece, w), bf16),
        ]
        for lanes in (2, 1, 1, 3, 3, 1, 1):
            shapes += [pltpu.SemaphoreType.DMA((k, lanes))] * 2
        if self.extra:
            n = len(self.extra)
            shapes += [pltpu.VMEM((k, 2 * n, self.piece, w), bf16)]
            shapes += [pltpu.SemaphoreType.DMA((k, n))] * 2
        return shapes

    def bind(self, place, part, refs):
        (self.a_in, self.b_out, self.b_in, self.c_out, self.c_in, self.keep) = refs[:6]
        self.d_out, self.d_in = refs[6:8]
        self.sems = {
            name: (refs[8 + 2 * i], refs[9 + 2 * i]) for i, name in enumerate(self.names)
        }
        if self.extra:
            self.x_buf, self.x_send, self.x_recv = refs[22:25]
        self.place, self.part = place, part
        self.core, self.x, self.z = place % 2, (place // 2) % 2, (place // 4) % 4
        self.sibling = {"dp": flip(place, 1)}
        self.beside = {"dp": flip(place, 2)}
        self.across = {"mp": 1 - part}
        self.peers = [{"dp": flip(place, j << 2)} for j in range(1, 4)]
        self.partners = [self.sibling, self.beside, self.across] + self.peers
        self.partners += [{"dp": flip(place, 1 << b)} for b in self.extra]
        return self

    def greet(self):
        barrier = pltpu.get_barrier_semaphore()
        for partner in self.partners:
            pl.semaphore_signal(barrier, inc=1, device_id=partner, device_id_type=MESH)
        pl.semaphore_wait(barrier, len(self.partners))

    def copy(self, name, k, lane, source, target, device):
        out, into = self.sems[name]
        return pltpu.make_async_remote_copy(
            src_ref=source,
            dst_ref=target,
            send_sem=out.at[k, lane],
            recv_sem=into.at[k, lane],
            device_id=device,
            device_id_type=MESH,
        )

    def rows_at(self, start, size):
        return pl.ds(pl.multiple_of(start, PIECES), size)

    def copy_a(self, k, lane, grads):
        source = grads.at[k, self.rows_at((1 - self.core) * self.half, self.half)]
        return self.copy("a", k, lane, source, self.a_in.at[k, lane], self.sibling)

    def copy_b(self, k):
        return self.copy("b", k, 0, self.b_out.at[k], self.b_in.at[k], self.across)

    def copy_c(self, k):
        return self.copy("c", k, 0, self.c_out.at[k], self.c_in.at[k], self.beside)

    def copy_d(self, k, j):
        return self.copy("d", k, j, self.d_out.at[k, j], self.d_in.at[k, j], self.peers[j])

    def spot(self, change=0):
        start = self.core * self.half + self.x * self.quarter
        return self.rows_at(start + flip(self.z, change) * self.piece, self.piece)

    def copy_e(self, k, j, full):
        rows = full.at[k, self.spot()]
        return self.copy("e", k, j, rows, rows, self.peers[j])

    def copy_f(self, k, full):
        start = self.core * self.half + self.x * self.quarter
        rows = full.at[k, self.rows_at(start, self.quarter)]
        return self.copy("f", k, 0, rows, rows, self.beside)

    def copy_g(self, k, full):
        rows = full.at[k, self.rows_at(self.core * self.half, self.half)]
        return self.copy("g", k, 0, rows, rows, self.sibling)

    def start_a(self, k, lane, grads):
        self.copy_a(k, lane, grads).start()

    def stage_b(self, k, others):
        self.copy_a(k, 0, others).wait()
        mine = others[k, self.rows_at(self.core * self.half, self.half), :].astype(f32)
        self.b_out[k] = (mine + self.a_in[k, 0].astype(f32)).astype(bf16)
        self.copy_b(k).start()

    def stage_c(self, k, grads, crossed=True):
        self.copy_a(k, 1, grads).wait()
        if crossed:
            self.copy_b(k).wait()

        def total(which):
            inner = which * self.quarter
            rows = self.rows_at(inner, self.quarter)
            mine = grads[k, self.rows_at(self.core * self.half + inner, self.quarter), :]
            got = self.a_in[k, 1, rows, :].astype(f32)
            if crossed:
                got = got + self.b_in[k, rows, :].astype(f32)
            return mine.astype(f32) + got

        self.c_out[k] = total(1 - self.x).astype(bf16)
        self.copy_c(k).start()
        self.keep[k] = total(self.x)

    def stage_d(self, k):
        self.copy_c(k).wait()
        for j in range(4):
            rows = self.rows_at(flip(self.z, j) * self.piece, self.piece)
            total = self.keep[k, rows, :] + self.c_in[k, rows, :].astype(f32)
            if j:
                self.d_out[k, j - 1] = total.astype(bf16)
                self.copy_d(k, j - 1).start()
            else:
                self.keep[k, rows, :] = total

    def stage_e(self, k, full):
        rows = self.rows_at(self.z * self.piece, self.piece)
        total = self.keep[k, rows, :]
        for j in range(3):
            self.copy_d(k, j).wait()
            total = total + self.d_in[k, j].astype(f32)
        for i, b in enumerate(self.extra):
            mine = self.x_buf.at[k, 2 * i]
            mine[...] = total.astype(bf16)
            swap = pltpu.make_async_remote_copy(
                src_ref=mine,
                dst_ref=self.x_buf.at[k, 2 * i + 1],
                send_sem=self.x_send.at[k, i],
                recv_sem=self.x_recv.at[k, i],
                device_id={"dp": flip(self.place, 1 << b)},
                device_id_type=MESH,
            )
            swap.start()
            swap.wait()
            total = total.astype(bf16).astype(f32) + self.x_buf[k, 2 * i + 1].astype(f32)
        full[k, self.spot(), :] = total.astype(bf16)
        for j in range(3):
            self.copy_e(k, j, full).start()

    def stage_f(self, k, full):
        for j in range(3):
            self.copy_e(k, j, full).wait()
        self.copy_f(k, full).start()

    def stage_g(self, k, full):
        self.copy_f(k, full).wait()
        self.copy_g(k, full).start()

    def stage_h(self, k, full):
        self.copy_g(k, full).wait()


def at_step(step, count, action):
    @pl.when(jnp.logical_and(step >= 0, step < count))
    def _():
        action(step)


SPLIT = 4


def middle_kernel(exchange, tiles, *refs):
    (
        x_ref,
        att_ref,
        att2_ref,
        wout_ref,
        wout2_ref,
        dy_ref,
        gain_ref,
        shift_ref,
        bdown_ref,
        bup_ref,
        up_mine,
        up_here,
        up_there,
        down_mine,
        down_here,
        down_there,
        out_ref,
        mid_ref,
        datt_ref,
        datt2_ref,
        gout_ref,
        gout2_ref,
        gbup_ref,
        small_ref,
        gdown_ref,
        gup_ref,
        full_ref,
        up_buf,
        down_buf,
        load_sem,
        n2_ref,
        total_ref,
        dn2_ref,
        act_ref,
        dpre_ref,
        grad_ref,
        *rest,
    ) = refs
    place, part = lax.axis_index("dp"), lax.axis_index("mp")
    ex = exchange.bind(place, part, rest)
    core = ex.core
    count = tiles // 2
    rows_all = x_ref.shape[0]
    blocks = rows_all // ROW_TILE
    width = x_ref.shape[1]
    lanes = width // 2

    def which(i):
        other = jnp.logical_or(i == 0, jnp.logical_and(i % 2 == 1, i < tiles - 1))
        mine = jnp.where(i == tiles - 1, count - 1, i // 2 - 1)
        return other, jnp.where(other, (i + 1) // 2, mine)

    def load(i, up_source, down_source, h):
        slot = i % 2
        sems = load_sem.at[slot]
        if h is None:
            return pltpu.make_async_copy(down_source, down_buf.at[slot], sems.at[2])
        target = up_buf.at[slot, h * lanes : (h + 1) * lanes]
        return pltpu.make_async_copy(up_source, target, sems.at[h])

    def start_loads(i):
        other, k = which(i)
        cols = pl.ds(pl.multiple_of(k * HIDDEN_TILE, HIDDEN_TILE), HIDDEN_TILE)
        inner = k % (count // 2)
        rows = pl.ds(pl.multiple_of(inner * HIDDEN_TILE, HIDDEN_TILE), HIDDEN_TILE)

        def put(condition, source, h):
            @pl.when(condition)
            def _():
                if h is None:
                    load(i, None, source, None).start()
                else:
                    load(i, source, None, h).start()

        mine = jnp.logical_not(other)
        for h in range(2):
            put(mine, up_mine.at[h * lanes : (h + 1) * lanes, cols], h)
            put(jnp.logical_and(other, core == h), up_here.at[:, cols], h)
            put(jnp.logical_and(other, core != h), up_there.at[:, cols], h)
        held = k // (count // 2) == core
        put(mine, down_mine.at[cols, :], None)
        put(jnp.logical_and(other, held), down_here.at[rows, :], None)
        put(jnp.logical_and(other, jnp.logical_not(held)), down_there.at[rows, :], None)

    def wait_loads(i):
        for h in range(2):
            load(i, up_mine.at[:lanes, :HIDDEN_TILE], None, h).wait()
        load(i, None, down_mine.at[:HIDDEN_TILE, :], None).wait()

    start_loads(0)
    ex.greet()

    def prologue(r, _):
        rows = pl.ds(pl.multiple_of(r * ROW_TILE, ROW_TILE), ROW_TILE)
        branch = dot(att_ref[rows, :], wout_ref[...]) + dot(att2_ref[rows, :], wout2_ref[...])
        mid = x_ref[rows, :].astype(f32) + branch
        mid_ref[rows, :] = mid
        n2_ref[rows, :] = (normal(mid)[0] * gain_ref[...] + shift_ref[...]).astype(bf16)
        total_ref[rows, :] = mid + bdown_ref[...]
        dn2_ref[rows, :] = jnp.zeros((ROW_TILE, width), f32)
        return 0

    lax.fori_loop(0, blocks, prologue, 0)

    def tile(i):
        other, k = which(i)
        slot = i % 2
        wait_loads(i)

        @pl.when(i + 1 < tiles)
        def _():
            start_loads(i + 1)

        up, down = up_buf.at[slot], down_buf.at[slot]
        bias_at = jnp.where(other, k, count + k)
        bias_grad = jnp.zeros((1, HIDDEN_TILE), f32)
        for r in range(blocks):
            rows = slice(r * ROW_TILE, (r + 1) * ROW_TILE)
            pre = dot(n2_ref[rows, :], up[...]) + bup_ref[bias_at]
            square = pre * pre
            bend = jnp.tanh(0.7978845608028654 * (pre + 0.044715 * square * pre))
            part_one = 0.5 * (1.0 + bend)
            act = (pre * part_one).astype(bf16)
            slope = part_one + (0.5 * pre) * (1.0 - bend * bend) * (
                0.7978845608028654 * (1.0 + 3.0 * 0.044715 * square)
            )
            d_act = dot(dy_ref[rows, :], down[...], NT)
            d_pre = (d_act * slope).astype(bf16)
            act_ref[rows, :] = act
            dpre_ref[rows, :] = d_pre
            bias_grad = bias_grad + jnp.sum(d_pre.astype(f32), axis=0, keepdims=True)
            total_ref[rows, :] += dot(act, down[...])
            dn2_ref[rows, :] += dot(d_pre, up[...], NT)
        gbup_ref[bias_at] = bias_grad
        grads = (
            dot(act_ref[...].T, dy_ref[...]).astype(bf16),
            dot(dpre_ref[...].T, n2_ref[...]).astype(bf16),
        )
        for c in range(SPLIT):
            cols = slice(c % 2 * lanes, (c % 2 + 1) * lanes)
            grad_ref[k * SPLIT + c] = grads[c // 2][:, cols]

        @pl.when(other)
        def _():
            for c in range(SPLIT):
                ex.start_a(k * SPLIT + c, 0, grad_ref)

        @pl.when(jnp.logical_not(other))
        def _():
            for c in range(SPLIT):
                ex.start_a(k * SPLIT + c, 1, grad_ref)

    def group(k, when, action):
        @pl.when(jnp.logical_and(when, jnp.logical_and(k >= 0, k < count)))
        def _():
            lax.fori_loop(0, SPLIT, lambda c, _: (action(k * SPLIT + c), 0)[1], 0)

    def arrive(k):
        for c in range(SPLIT):
            ex.stage_h(k * SPLIT + c, full_ref)
        hidden = pl.ds(pl.multiple_of(k * HIDDEN_TILE, HIDDEN_TILE), HIDDEN_TILE)
        for c in range(2):
            cols = slice(c * lanes, (c + 1) * lanes)
            gdown_ref[hidden, cols] = full_ref[k * SPLIT + c]
            gup_ref[cols, hidden] = full_ref[k * SPLIT + 2 + c].T

    def steps(i):
        even = i % 2 == 0
        odd = jnp.logical_not(even)
        last = (i - 9) // 2

        @pl.when(jnp.logical_and(odd, jnp.logical_and(last >= 0, last < count)))
        def _():
            arrive(last)

        group((i - 8) // 2, even, lambda k: ex.stage_g(k, full_ref))
        group((i - 7) // 2, odd, lambda k: ex.stage_f(k, full_ref))
        group((i - 6) // 2, even, lambda k: ex.stage_e(k, full_ref))
        group((i - 5) // 2, odd, lambda k: ex.stage_d(k))
        group((i - 4) // 2, even, lambda k: ex.stage_c(k, grad_ref))
        crossing = jnp.logical_or(i == 1, jnp.logical_and(even, i >= 2))
        group(i // 2, crossing, lambda k: ex.stage_b(k, grad_ref))

    def main(i, _):
        tile(i)
        steps(i)
        return 0

    lax.fori_loop(0, tiles, main, 0)

    def epilogue(r, sums):
        rows = pl.ds(pl.multiple_of(r * ROW_TILE, ROW_TILE), ROW_TILE)
        out_ref[rows, :] = total_ref[rows, :].astype(bf16)
        unit, scale = normal(mid_ref[rows, :])
        d_rows = dn2_ref[rows, :]
        dy = dy_ref[rows, :].astype(f32)
        lean = d_rows * gain_ref[...]
        d_mid = dy + scale * (
            lean
            - jnp.mean(lean, axis=-1, keepdims=True)
            - unit * jnp.mean(lean * unit, axis=-1, keepdims=True)
        )
        mid_ref[rows, :] = d_mid
        d_branch = d_mid.astype(bf16)
        n2_ref[rows, :] = d_branch
        datt_ref[rows, :] = dot(d_branch, wout_ref[...], NT).astype(bf16)
        datt2_ref[rows, :] = dot(d_branch, wout2_ref[...], NT).astype(bf16)
        add = lambda values: jnp.sum(values, axis=0, keepdims=True)
        sums = (sums[0] + add(d_rows * unit), sums[1] + add(d_rows), sums[2] + add(dy))
        steps(tiles + r)
        return sums

    zero = jnp.zeros((1, width), f32)
    sums = lax.fori_loop(0, blocks, epilogue, (zero, zero, zero))
    for j in range(3):
        small_ref[j : j + 1, :] = sums[j]
    depth = wout_ref.shape[0]
    for source, target in ((att_ref, gout_ref), (att2_ref, gout2_ref)):
        grad = dot(source[...].T, n2_ref[...]).astype(bf16)
        target[:depth, :] = grad[:, :lanes]
        target[depth:, :] = grad[:, lanes:]

    def drain(i, _):
        steps(i)
        return 0

    lax.fori_loop(tiles + blocks, 2 * count + 8, drain, 0)


def middle(bits, x, att, att2, wout, wout2, dy, gain, shift, bdown, bup, ups, downs):
    rows, width = x.shape
    hidden = ups[0].shape[1]
    count = hidden // HIDDEN_TILE
    tiles = 2 * count
    exchange = Exchange(bits, count * SPLIT, HIDDEN_TILE, width // 2)
    vmem = pl.BlockSpec(memory_space=pltpu.VMEM)
    hbm = pl.BlockSpec(memory_space=pl.ANY)
    shape = jax.ShapeDtypeStruct
    depth = wout.shape[0]
    return pl.pallas_call(
        functools.partial(middle_kernel, exchange, tiles),
        in_specs=[vmem] * 10 + [hbm] * 6,
        out_specs=[vmem] * 10,
        out_shape=[
            shape((rows, width), bf16),
            shape((rows, width), f32),
            shape(att.shape, bf16),
            shape(att2.shape, bf16),
            shape((2 * depth, width // 2), bf16),
            shape((2 * depth, width // 2), bf16),
            shape((tiles, 1, HIDDEN_TILE), f32),
            shape((8, width), f32),
            shape((hidden, width), bf16),
            shape((width, hidden), bf16),
        ],
        scratch_shapes=[
            pltpu.VMEM((count * SPLIT, HIDDEN_TILE, width // 2), bf16),
            pltpu.VMEM((2, width, HIDDEN_TILE), bf16),
            pltpu.VMEM((2, HIDDEN_TILE, width), bf16),
            pltpu.SemaphoreType.DMA((2, 3)),
            pltpu.VMEM((rows, width), bf16),
            pltpu.VMEM((rows, width), f32),
            pltpu.VMEM((rows, width), f32),
            pltpu.VMEM((rows, HIDDEN_TILE), bf16),
            pltpu.VMEM((rows, HIDDEN_TILE), bf16),
            pltpu.VMEM((count * SPLIT, HIDDEN_TILE, width // 2), bf16),
        ]
        + exchange.scratch(),
        compiler_params=pltpu.CompilerParams(
            collective_id=0, has_side_effects=True, vmem_limit_bytes=67043328
        ),
        name="middle",
        cost_estimate=pl.CostEstimate(
            flops=60 * 10**9, bytes_accessed=40 * 10**6, transcendentals=4 * 10**6
        ),
    )(x, att, att2, wout, wout2, dy, gain, shift, bdown, bup, *ups, *downs)


def leave_kernel(exchange, *refs):
    (
        mine_ref,
        mine_out_ref,
        crossed_ref,
        crossed_out_ref,
        d_ref,
        d2_ref,
        w_ref,
        w2_ref,
        tokens_ref,
        gain_ref,
        dmid_ref,
        small_ref,
        small2_ref,
        full_ref,
        back_ref,
        sums_ref,
        sum_buf,
        rows_ref,
        give_ref,
        take_ref,
        swap_sem,
        got_ref,
        work_ref,
        small_send,
        small_recv,
        *rest,
    ) = refs
    place, part = lax.axis_index("dp"), lax.axis_index("mp")
    ex = exchange.bind(place, part, rest)
    count, bits = ex.count, ex.bits
    first = mine_ref.shape[0]
    ex.greet()

    def begin(k, _):
        total = mine_ref[k].astype(f32) + crossed_ref[k].astype(f32)
        sum_buf[k] = total.astype(bf16)
        ex.start_a(k, 1, sum_buf)
        return 0

    lax.fori_loop(0, first, begin, 0)

    def begin_out(k, _):
        total = mine_out_ref[k].astype(f32) + crossed_out_ref[k].astype(f32)
        sum_buf[first + k] = total.astype(bf16)
        ex.start_a(first + k, 1, sum_buf)
        return 0

    lax.fori_loop(0, count - first, begin_out, 0)

    def back_of(rows):
        total = 0.0
        for grads, weights in ((d_ref, w_ref), (d2_ref, w2_ref)):
            for c in range(3):
                total = total + dot(grads[c, rows, :], weights[c], NT)
        return total

    for r in range(HALF // ROW_TILE):
        rows = slice(r * ROW_TILE, (r + 1) * ROW_TILE)
        given = back_of(rows)
        if r == 0:
            edges = back_of(slice(2 * HALF, NOISY_OWN))
            give_ref[EDGE:ROW_TILE, :] = given[EDGE:].astype(bf16)
            give_ref[:EDGE, :] = (given[:EDGE] + edges[:EDGE]).astype(bf16)
            last = back_of(slice(NOISY_OWN + HALF, KEY_ROWS))
            give_ref[HALF:, :] = (edges[EDGE:] + last).astype(bf16)
        else:
            give_ref[rows, :] = given.astype(bf16)
    swap = pltpu.make_async_remote_copy(
        src_ref=give_ref,
        dst_ref=take_ref,
        send_sem=swap_sem.at[0],
        recv_sem=swap_sem.at[1],
        device_id=ex.across,
        device_id_type=MESH,
    )
    swap.start()

    def steps(i):
        at_step(i - 15, count, lambda k: ex.stage_h(k, full_ref))
        at_step(i - 12, count, lambda k: ex.stage_g(k, full_ref))
        at_step(i - 9, count, lambda k: ex.stage_f(k, full_ref))
        at_step(i - 6, count, lambda k: ex.stage_e(k, full_ref))
        at_step(i - 3, count, lambda k: ex.stage_d(k))
        at_step(i, count, lambda k: ex.stage_c(k, sum_buf, False))

    parts = 2 * TILES

    def own_rows(b, _):
        noisy = NOISY_OWN + b * TILE
        clean = CLEAN_OWN + (b - TILES) * TILE
        start = jnp.where(b < TILES, noisy, clean)
        rows_ref[pl.ds(pl.multiple_of(b * TILE, TILE), TILE), :] = back_of(
            pl.ds(pl.multiple_of(start, EDGE), TILE)
        )
        steps(2 * b)
        steps(2 * b + 1)
        return 0

    lax.fori_loop(0, parts, own_rows, 0)
    swap.wait()
    rows_ref[HALF:, :] += take_ref[:HALF, :].astype(f32)
    edge = pl.ds(pl.multiple_of((1 - part) * (HALF - EDGE), EDGE), EDGE)
    rows_ref[edge, :] += take_ref[HALF:, :].astype(f32)

    def norm_back(b, sums):
        rows = pl.ds(pl.multiple_of(b * TILE, TILE), TILE)
        unit, scale = normal(tokens_ref[rows, :].astype(f32))
        d_rows = rows_ref[rows, :]
        lean = d_rows * gain_ref[...]
        back_ref[rows, :] = dmid_ref[rows, :] + scale * (
            lean
            - jnp.mean(lean, axis=-1, keepdims=True)
            - unit * jnp.mean(lean * unit, axis=-1, keepdims=True)
        )
        add = lambda values: jnp.sum(values, axis=0, keepdims=True)
        steps(2 * parts + b)
        return (sums[0] + add(d_rows * unit), sums[1] + add(d_rows))

    width = tokens_ref.shape[1]
    zero = jnp.zeros((1, width), f32)
    sums = lax.fori_loop(0, parts, norm_back, (zero, zero))
    lead = small_ref.shape[0] - 2

    def small_copy(s):
        device = ex.across if s == 0 else {"dp": flip(place, 1 << (s - 1))}
        return pltpu.make_async_remote_copy(
            src_ref=work_ref.at[s],
            dst_ref=got_ref.at[s],
            send_sem=small_send.at[s],
            recv_sem=small_recv.at[s],
            device_id=device,
            device_id_type=MESH,
        )

    work_ref[0, :lead, :] = small2_ref[:lead, :]
    for j in range(2):
        work_ref[0, lead + j : lead + j + 1, :] = sums[j]
    small_copy(0).start()
    for s in range(bits + 1):
        steps(3 * parts + s)
        small_copy(s).wait()
        if s == 0:
            work_ref[1, :lead, :] = small_ref[:lead, :] + got_ref[0, :lead, :]
            work_ref[1, lead:, :] = work_ref[0, lead:, :] + got_ref[0, lead:, :]
        else:
            work_ref[s + 1] = work_ref[s] + got_ref[s]
        if s < bits:
            small_copy(s + 1).start()
    sums_ref[...] = work_ref[bits + 1]

    def drain(i, _):
        steps(i)
        return 0

    lax.fori_loop(3 * parts + bits + 1, 3 * parts + bits + 1 + 15, drain, 0)


def leave(bits, mine, crossed, d_fields, weights, tokens, gain, d_mid, small, small2):
    total = mine[0].shape[0] + mine[1].shape[0]
    rows, cols = mine[0].shape[1:]
    exchange = Exchange(bits, total, rows, cols)
    count, width = tokens.shape
    vmem = pl.BlockSpec(memory_space=pltpu.VMEM)
    shape = jax.ShapeDtypeStruct
    return pl.pallas_call(
        functools.partial(leave_kernel, exchange),
        in_specs=[vmem] * 13,
        out_specs=[vmem] * 3,
        out_shape=[
            shape((total, rows, cols), bf16),
            shape((count, width), f32),
            shape(small.shape, f32),
        ],
        scratch_shapes=[
            pltpu.VMEM((total, rows, cols), bf16),
            pltpu.VMEM((count, width), f32),
            pltpu.VMEM((HALF + EDGE, width), bf16),
            pltpu.VMEM((HALF + EDGE, width), bf16),
            pltpu.SemaphoreType.DMA((2,)),
            pltpu.VMEM((bits + 1,) + small.shape, f32),
            pltpu.VMEM((bits + 2,) + small.shape, f32),
            pltpu.SemaphoreType.DMA((bits + 1,)),
            pltpu.SemaphoreType.DMA((bits + 1,)),
        ]
        + exchange.scratch(),
        compiler_params=pltpu.CompilerParams(
            collective_id=1, has_side_effects=True, vmem_limit_bytes=67043328
        ),
        name="leave",
        cost_estimate=pl.CostEstimate(
            flops=40 * 10**9, bytes_accessed=40 * 10**6, transcendentals=0
        ),
    )(*mine, *crossed, *d_fields, *weights, tokens, gain, d_mid, small, small2)


def key_layout(seq_lengths, block_len, part):
    index = jnp.arange(KEY_ROWS, dtype=jnp.int32)
    own = part * HALF
    token = jnp.where(
        index < NOISY_BASE, index + (own - HALF), index - NOISY_BASE + (own - EDGE)
    )
    ends = jnp.cumsum(seq_lengths)
    passed = token[:, None] >= ends[None, :]
    starts = jnp.sum(jnp.where(passed, seq_lengths[None, :], 0), axis=1)
    lengths_here = jnp.where(passed, 0, ends[None, :])
    stops = jnp.min(jnp.where(passed, TOK_DEV, lengths_here), axis=1)
    positions = token - starts
    block_start = starts + positions // block_len * block_len
    block_stop = jnp.minimum(block_start + block_len, stops)
    mine = slice(CLEAN_OWN, CLEAN_OWN + HALF)
    low, start, stop = starts[mine], block_start[mine], block_stop[mine]
    to_clean = own - HALF
    tiles = lambda column: column.reshape(TILES, 1, TILE)
    clean_bounds = jnp.concatenate(
        [
            jnp.concatenate([tiles(low - to_clean), tiles(low - to_clean)], axis=2),
            jnp.concatenate([tiles(start - to_clean), tiles(stop - to_clean)], axis=2),
        ],
        axis=1,
    )
    to_window = own - EDGE + TILE * jnp.arange(TILES, dtype=jnp.int32)[:, None, None]
    noisy_bounds = jnp.concatenate(
        [tiles(start) - to_window, tiles(stop) - to_window], axis=1
    )
    first = jnp.min(clean_bounds[:, 0], axis=1) // EDGE * EDGE
    last = jnp.max(clean_bounds[:, 1], axis=1)
    trips = (last - first + KEY_TILE - 1) // KEY_TILE
    spans = jnp.stack([first, trips], axis=1)
    lane = jnp.arange(LANES, dtype=jnp.int32)
    frequency = jnp.exp(
        (lane % (HD // 2)).astype(f32) * (-math.log(10000.0) / (HD // 2))
    )
    angles = positions.astype(f32)[:, None] * frequency[None, :]
    sign = jnp.where(lane % HD < HD // 2, -1.0, 1.0)
    return spans, clean_bounds, noisy_bounds, jnp.cos(angles), jnp.sin(angles) * sign


def half_of(array, which, axis=0):
    size = array.shape[axis] // 2
    return lax.dynamic_slice_in_dim(array, which * size, size, axis)


def in_order(bit, mine, theirs, axis=0):
    order = bit == 0
    return jnp.concatenate(
        [jnp.where(order, mine, theirs), jnp.where(order, theirs, mine)], axis=axis
    )


def tie(first, second):
    return lax.optimization_barrier((first, second))


def as_row(vector):
    return vector.reshape(1, -1)


def local(
    dp_size,
    tokens,
    lengths,
    block_size,
    cotangent,
    ln1_gain,
    ln1_bias,
    w_qkv,
    w_out,
    ln2_gain,
    ln2_bias,
    w_up,
    b_up,
    w_down,
    b_down,
):
    width = tokens.shape[2]
    part = lax.axis_index("mp")
    place = lax.axis_index("dp")
    bits = dp_size.bit_length() - 1
    core = place & 1

    def across(array):
        return lax.ppermute(array, "mp", [(0, 1), (1, 0)])

    def sibling(array):
        return lax.ppermute(array, "dp", [(i, i ^ 1) for i in range(dp_size)])

    def fetch(half):
        here = across(half)
        return here, sibling(here)

    edge = jnp.where(part == 0, tokens[0, HALF - EDGE :], tokens[0, :EDGE])
    context = across(jnp.concatenate([tokens[1], edge], axis=0))
    qkv_mine = w_qkv.transpose(1, 0, 2)
    halves = [
        half_of(qkv_mine, core, 1),
        half_of(w_out, core),
        half_of(w_up, core),
        half_of(w_down, core),
    ]
    context, halves = tie(context, halves)
    fetched = [fetch(half) for half in halves]
    bias_other = across(b_up)

    spans, clean_bounds, noisy_bounds, cosine, sine = key_layout(lengths[0], block_size[0], part)
    normed1, normed1_t, *fields = enter(
        tokens, context, as_row(ln1_gain), as_row(ln1_bias), qkv_mine, cosine, sine
    )
    mine = [*fields, *attend_forward(spans, clean_bounds, noisy_bounds, *fields)]
    fetched[0] = tie(fetched[0], mine[3])[0]
    qkv_other = in_order(core, *fetched[0], axis=1)
    fields = project(normed1, qkv_other, cosine, sine)
    other = [*fields, *attend_forward(spans, clean_bounds, noisy_bounds, *fields)]
    fetched[1:] = tie(fetched[1:], other[3])[0]
    bias_all = jnp.concatenate([bias_other, b_up]).astype(f32).reshape(-1, 1, HIDDEN_TILE)

    x_rows = tokens.reshape(TOK_DEV, width)
    out, d_mid, d_att, d_att2, grad_out, grad_out2, grad_bias, norms, grad_down, grad_up = middle(
        bits,
        x_rows,
        mine[3],
        other[3],
        w_out,
        in_order(core, *fetched[1]),
        cotangent.reshape(TOK_DEV, width),
        as_row(ln2_gain),
        as_row(ln2_bias),
        as_row(b_down),
        bias_all,
        (w_up,) + fetched[2],
        (w_down,) + fetched[3],
    )
    hidden = b_up.shape[0]

    d_qkv, grad_qkv = [], []
    for saved, d_attended in ((other, d_att2), (mine, d_att)):
        query, keys, values, attended, lse = saved
        d_fields, grad = attend_backward(
            spans,
            clean_bounds,
            noisy_bounds,
            query,
            keys,
            values,
            attended,
            d_attended,
            lse,
            cosine,
            sine,
            normed1_t,
        )
        spans = tie(spans, grad)[0]
        d_qkv.append(d_fields)
        grad_qkv.append(grad.reshape(-1, ROW_TILE, grad.shape[2]))
    crossed_out = across(grad_out2)
    crossed = across(grad_qkv[0])
    lead = hidden // width
    bias2, bias1 = grad_bias.reshape(2, lead, width)
    shared = jnp.concatenate([norms[:3], jnp.zeros((2, width), f32)], axis=0)
    full, grad_tokens, sums = leave(
        bits,
        (grad_qkv[1], grad_out.reshape(-1, ROW_TILE, grad_out.shape[1])),
        (crossed, crossed_out.reshape(-1, ROW_TILE, grad_out.shape[1])),
        (d_qkv[1], d_qkv[0]),
        (qkv_mine, qkv_other),
        x_rows,
        as_row(ln1_gain),
        d_mid,
        jnp.concatenate([bias1, shared], axis=0),
        jnp.concatenate([bias2, shared], axis=0),
    )
    split = 3 * width // ROW_TILE
    grad_qkv = full[:split].reshape(qkv_mine.shape).transpose(1, 0, 2).astype(f32)
    flat = full[split:].reshape(2, w_out.shape[0], width // 2)
    grad_out = jnp.concatenate([flat[0], flat[1]], axis=1).astype(f32)
    return (
        out.reshape(tokens.shape),
        grad_tokens.reshape(tokens.shape),
        sums[lead + 3],
        sums[lead + 4],
        grad_qkv,
        grad_out,
        sums[lead],
        sums[lead + 1],
        grad_up.astype(f32),
        sums[:lead].reshape(hidden),
        grad_down.astype(f32),
        sums[lead + 2],
    )


def solution(mesh):
    in_specs = (
        P(None, ("dp", "mp"), None),
        P("dp", None),
        P(),
        P(None, ("dp", "mp"), None),
        P(),
        P(),
        P(None, None, "mp"),
        P("mp", None),
        P(),
        P(),
        P(None, "mp"),
        P("mp"),
        P("mp", None),
        P(),
    )
    out_specs = (
        P(None, ("dp", "mp"), None),
        P(None, ("dp", "mp"), None),
        P(),
        P(),
        P(None, None, "mp"),
        P("mp", None),
        P(),
        P(),
        P(None, "mp"),
        P("mp"),
        P("mp", None),
        P(),
    )
    return jax.shard_map(
        functools.partial(local, mesh.shape["dp"]),
        mesh=mesh,
        in_specs=in_specs,
        out_specs=out_specs,
        check_vma=False,
    )
```

```python
import functools
import math

import jax
import jax.numpy as jnp
from jax import lax
from jax.experimental import pallas as pl
from jax.experimental.pallas import tpu as pltpu
from jax.sharding import PartitionSpec as P

HD = 64
TOK_DEV = 1024
HALF = TOK_DEV // 2
EDGE = 16
CLEAN_OWN = HALF
NOISY_BASE = 2 * HALF + EDGE
NOISY_OWN = NOISY_BASE + EDGE
KEY_ROWS = NOISY_OWN + HALF + EDGE
TILE = 128
TILES = HALF // TILE
WINDOW = TILE + 2 * EDGE
KEY_TILE = 256
LANES = 128
HIDDEN_TILE = 256
ROW_TILE = 256

epsilon = 1e-05
neg_large = -1e30
to_base2 = 0.125 * math.log2(math.e)
f32 = jnp.float32
bf16 = jnp.bfloat16

NN = (((1,), (0,)), ((), ()))
NT = (((1,), (1,)), ((), ()))


def dot(left, right, dims=NN):
    return lax.dot_general(left, right, dims, preferred_element_type=f32)


def low_lanes(shape):
    return lax.broadcasted_iota(jnp.int32, shape, 1) < HD


def turn(values, cosine, sine):
    lane = lax.broadcasted_iota(jnp.int32, values.shape, 1)
    first_half = (lane & (HD - 1)) < HD // 2
    swapped = jnp.where(
        first_half,
        pltpu.roll(values, LANES - HD // 2, 1),
        pltpu.roll(values, HD // 2, 1),
    )
    return values * cosine + swapped * sine


def project_rows(rows, w_ref, cosine, sine, q_ref, k_ref, v_ref, at):
    for part, out_ref in ((0, q_ref), (1, k_ref)):
        field = dot(rows, w_ref[part])
        for pair in range(field.shape[1] // LANES):
            cols = slice(pair * LANES, (pair + 1) * LANES)
            out_ref[at, cols] = turn(field[:, cols], cosine, sine).astype(bf16)
    v_ref[at, :] = dot(rows, w_ref[2]).astype(bf16)


def project_kernel(rows_ref, w_ref, cos_ref, sin_ref, q_ref, k_ref, v_ref):
    at = slice(0, rows_ref.shape[0])
    project_rows(rows_ref[...], w_ref, cos_ref[...], sin_ref[...], q_ref, k_ref, v_ref, at)


def project(rows, weights, cosine, sine):
    count, width = rows.shape
    cols = weights.shape[2]
    step = count // 3
    row_spec = pl.BlockSpec((step, width), lambda i: (i, 0))
    table_spec = pl.BlockSpec((step, LANES), lambda i: (i, 0))
    out_spec = pl.BlockSpec((step, cols), lambda i: (i, 0))
    shape = jax.ShapeDtypeStruct((count, cols), bf16)
    return pl.pallas_call(
        project_kernel,
        grid=(3,),
        in_specs=[
            row_spec,
            pl.BlockSpec(weights.shape, lambda i: (0, 0, 0)),
            table_spec,
            table_spec,
        ],
        out_specs=[out_spec] * 3,
        out_shape=[shape] * 3,
        name="project",
        cost_estimate=pl.CostEstimate(
            flops=2 * count * width * 3 * cols,
            bytes_accessed=2 * (count * (width + 3 * cols) + 3 * width * cols),
            transcendentals=0,
        ),
    )(rows, weights, cosine, sine)


def normal(values):
    average = jnp.mean(values, axis=-1, keepdims=True)
    centred = values - average
    variance = jnp.mean(centred * centred, axis=-1, keepdims=True)
    scale = lax.rsqrt(variance + epsilon)
    return centred * scale, scale


def enter_kernel(
    tokens_ref,
    context_ref,
    vectors_ref,
    w_ref,
    cos_ref,
    sin_ref,
    rows_ref,
    rows_t_ref,
    q_ref,
    k_ref,
    v_ref,
):
    def norm(values):
        unit = normal(values.astype(f32))[0]
        return (unit * vectors_ref[0:1, :] + vectors_ref[1:2, :]).astype(bf16)

    def blocks(i, _):
        source = pl.ds(pl.multiple_of(i * TILE, TILE), TILE)
        rows_ref[source, :] = norm(context_ref[source, :])
        at = pl.ds(pl.multiple_of(CLEAN_OWN + i * TILE, TILE), TILE)
        rows_ref[at, :] = norm(tokens_ref[1, source, :])
        at = pl.ds(pl.multiple_of(NOISY_OWN + i * TILE, EDGE), TILE)
        rows_ref[at, :] = norm(tokens_ref[0, source, :])
        return 0

    lax.fori_loop(0, TILES, blocks, 0)
    rows_ref[2 * HALF : NOISY_BASE, :] = rows_ref[:EDGE, :]
    edge = norm(context_ref[HALF:, :])
    rows_ref[NOISY_BASE:NOISY_OWN, :] = edge
    rows_ref[NOISY_OWN + HALF :, :] = edge
    step = KEY_ROWS // 3

    def fields(i, _):
        at = pl.ds(pl.multiple_of(i * step, EDGE), step)
        project_rows(
            rows_ref[at, :], w_ref, cos_ref[at, :], sin_ref[at, :], q_ref, k_ref, v_ref, at
        )
        return 0

    lax.fori_loop(0, 3, fields, 0)
    for c in range(rows_t_ref.shape[0] // LANES):
        cols = slice(c * LANES, (c + 1) * LANES)
        rows_t_ref[cols, :] = rows_ref[:, cols].T


def enter(tokens, context, vectors, weights, cosine, sine):
    width, cols = weights.shape[1:]
    vmem = pl.BlockSpec(memory_space=pltpu.VMEM)
    shape = jax.ShapeDtypeStruct
    field = shape((KEY_ROWS, cols), bf16)
    return pl.pallas_call(
        enter_kernel,
        in_specs=[vmem] * 6,
        out_specs=[vmem] * 5,
        out_shape=[shape((KEY_ROWS, width), bf16), shape((width, KEY_ROWS), bf16)] + [field] * 3,
        name="enter",
        cost_estimate=pl.CostEstimate(
            flops=10**10, bytes_accessed=16 * 10**6, transcendentals=0
        ),
    )(tokens, context, vectors, weights, cosine, sine)


def split_heads(rows):
    low = low_lanes(rows.shape)
    zero = jnp.zeros_like(rows)
    return jnp.where(low, rows, zero), jnp.where(low, zero, rows)


def between(shape, offset, low, high):
    index = lax.broadcasted_iota(jnp.int32, shape, 0) + offset
    return jnp.logical_and(index >= low, index < high)


def forward_kernel(
    span_ref, clean_ref, noisy_ref, q_ref, k_ref, v_ref, out_ref, lse_ref
):
    def one_tile(t, _):
        clean_at = pl.multiple_of(CLEAN_OWN + t * TILE, TILE)
        noisy_at = pl.multiple_of(NOISY_OWN + t * TILE, EDGE)
        window_at = pl.multiple_of(NOISY_BASE + t * TILE, EDGE)
        query = jnp.concatenate(
            [q_ref[pl.ds(noisy_at, TILE), :], q_ref[pl.ds(clean_at, TILE), :]], axis=0
        )
        queries = split_heads(query)
        key_low, key_high = clean_ref[t, 0:1, :], clean_ref[t, 1:2, :]
        own_low, own_high = noisy_ref[t, 0:1, :], noisy_ref[t, 1:2, :]
        keys = k_ref[pl.ds(window_at, WINDOW), :]
        values_t = v_ref[pl.ds(window_at, WINDOW), :].T
        allowed = between((WINDOW, TILE), 0, own_low, own_high)
        state = []
        for head in range(2):
            scores = dot(keys, queries[head][:TILE], NT) * to_base2
            scores = jnp.where(allowed, scores, neg_large)
            top = jnp.max(scores, axis=0, keepdims=True)
            expo = jnp.exp2(scores - top)
            total = jnp.sum(expo, axis=0, keepdims=True)
            mixed = dot(values_t[head * HD : (head + 1) * HD], expo.astype(bf16))
            blank = jnp.zeros((1, TILE), f32)
            state += [
                jnp.concatenate([top, blank + neg_large], axis=1),
                jnp.concatenate([total, blank], axis=1),
                jnp.concatenate([mixed, jnp.zeros((HD, TILE), f32)], axis=1),
            ]
        first_key, trips = span_ref[t, 0], span_ref[t, 1]

        def one_step(j, state):
            at = pl.multiple_of(first_key + j * KEY_TILE, EDGE)
            keys = k_ref[pl.ds(at, KEY_TILE), :]
            values_t = v_ref[pl.ds(at, KEY_TILE), :].T
            allowed = between((KEY_TILE, 2 * TILE), at, key_low, key_high)
            after = []
            for head in range(2):
                top, total, mixed = state[3 * head : 3 * head + 3]
                scores = dot(keys, queries[head], NT) * to_base2
                scores = jnp.where(allowed, scores, neg_large)
                new_top = jnp.maximum(top, jnp.max(scores, axis=0, keepdims=True))
                keep = jnp.exp2(top - new_top)
                expo = jnp.exp2(scores - new_top)
                after += [
                    new_top,
                    total * keep + jnp.sum(expo, axis=0, keepdims=True),
                    mixed * keep
                    + dot(values_t[head * HD : (head + 1) * HD], expo.astype(bf16)),
                ]
            return tuple(after)

        state = lax.fori_loop(0, trips, one_step, tuple(state))
        pair = jnp.concatenate(
            [state[2] / state[1], state[5] / state[4]], axis=0
        ).T.astype(bf16)
        out_at = pl.multiple_of(t * TILE, TILE)
        out_ref[pl.ds(out_at, TILE), :] = pair[:TILE]
        out_ref[pl.ds(pl.multiple_of(HALF + t * TILE, TILE), TILE), :] = pair[TILE:]
        lse_ref[0, t, 0:1, :] = state[0] + jnp.log2(state[1])
        lse_ref[0, t, 1:2, :] = state[3] + jnp.log2(state[4])
        return 0

    lax.fori_loop(0, TILES, one_tile, 0)


def attend_forward(spans, clean_bounds, noisy_bounds, query, keys, values):
    count, cols = query.shape
    pairs = cols // LANES
    whole3 = lambda array: pl.BlockSpec(array.shape, lambda p, s: (0, 0, 0))
    row_spec = pl.BlockSpec((count, LANES), lambda p, s: (0, p))
    work = pairs * 2 * 2 * HALF * TOK_DEV
    return pl.pallas_call(
        forward_kernel,
        grid_spec=pltpu.PrefetchScalarGridSpec(
            num_scalar_prefetch=1,
            grid=(pairs,),
            in_specs=[whole3(clean_bounds), whole3(noisy_bounds)] + [row_spec] * 3,
            out_specs=[
                pl.BlockSpec((TOK_DEV, LANES), lambda p, s: (0, p)),
                pl.BlockSpec((1, TILES, 2, 2 * TILE), lambda p, s: (p, 0, 0, 0)),
            ],
        ),
        out_shape=[
            jax.ShapeDtypeStruct((TOK_DEV, cols), bf16),
            jax.ShapeDtypeStruct((pairs, TILES, 2, 2 * TILE), f32),
        ],
        name="attend_forward",
        cost_estimate=pl.CostEstimate(
            flops=4 * work * HD, bytes_accessed=8 * count * cols, transcendentals=work
        ),
    )(spans, clean_bounds, noisy_bounds, query, keys, values)


def backward_kernel(
    span_ref,
    clean_ref,
    noisy_ref,
    q_ref,
    k_ref,
    v_ref,
    o_ref,
    d_ref,
    lse_ref,
    cos_ref,
    sin_ref,
    rows_ref,
    out_ref,
    grad_ref,
    dk_ref,
    dv_ref,
    fields_ref,
):
    dk_ref[...] = jnp.zeros_like(dk_ref)
    dv_ref[...] = jnp.zeros_like(dv_ref)
    fields_ref[:, :LANES] = jnp.zeros((KEY_ROWS, LANES), bf16)

    def one_tile(t, _):
        clean_at = pl.multiple_of(CLEAN_OWN + t * TILE, TILE)
        noisy_at = pl.multiple_of(NOISY_OWN + t * TILE, EDGE)
        window_at = pl.multiple_of(NOISY_BASE + t * TILE, EDGE)
        low_at = pl.multiple_of(t * TILE, TILE)
        high_at = pl.multiple_of(HALF + t * TILE, TILE)

        def both(ref, low, high):
            return jnp.concatenate(
                [ref[pl.ds(low, TILE), :], ref[pl.ds(high, TILE), :]], axis=0
            )

        query = split_heads(both(q_ref, noisy_at, clean_at))
        d_rows = both(d_ref, low_at, high_at)
        o_rows = both(o_ref, low_at, high_at)
        product = (d_rows.astype(f32) * o_rows.astype(f32)).T
        d_out = split_heads(d_rows)
        inner = [
            jnp.sum(product[head * HD : (head + 1) * HD], axis=0, keepdims=True)
            for head in range(2)
        ]
        lse = [lse_ref[0, t, head : head + 1, :] for head in range(2)]
        key_low, key_high = clean_ref[t, 0:1, :], clean_ref[t, 1:2, :]
        own_low, own_high = noisy_ref[t, 0:1, :], noisy_ref[t, 1:2, :]

        def accumulate(at, rows, cols, allowed, d_query):
            keys = k_ref[pl.ds(at, rows), :]
            values = v_ref[pl.ds(at, rows), :]
            keys_t = keys.T
            weights, d_scores, after = [], [], []
            for head in range(2):
                scores = dot(keys, query[head][:cols], NT) * to_base2
                scores = jnp.where(allowed, scores - lse[head][:, :cols], neg_large)
                probs = jnp.exp2(scores)
                d_probs = dot(values, d_out[head][:cols], NT)
                d_score = (probs * (d_probs - inner[head][:, :cols]) * 0.125).astype(bf16)
                weights.append(probs.astype(bf16))
                d_scores.append(d_score)
                after.append(
                    d_query[head] + dot(keys_t[head * HD : (head + 1) * HD], d_score)
                )
            stack = lambda parts: jnp.concatenate([part[:cols] for part in parts], axis=0)
            dv_ref[pl.ds(at, rows), :] += dot(
                jnp.concatenate(weights, axis=1), stack(d_out)
            )
            dk_ref[pl.ds(at, rows), :] += dot(
                jnp.concatenate(d_scores, axis=1), stack(query)
            )
            return tuple(after)

        allowed = between((WINDOW, TILE), 0, own_low, own_high)
        zero = jnp.zeros((HD, TILE), f32)
        start = accumulate(window_at, WINDOW, TILE, allowed, (zero, zero))
        start = tuple(jnp.concatenate([part, zero], axis=1) for part in start)
        first_key, trips = span_ref[t, 0], span_ref[t, 1]

        def one_step(j, d_query):
            at = pl.multiple_of(first_key + j * KEY_TILE, EDGE)
            allowed = between((KEY_TILE, 2 * TILE), at, key_low, key_high)
            return accumulate(at, KEY_TILE, 2 * TILE, allowed, d_query)

        d_query = lax.fori_loop(0, trips, one_step, start)
        d_query = jnp.concatenate(d_query, axis=0).T
        for at, part in ((noisy_at, d_query[:TILE]), (clean_at, d_query[TILE:])):
            turned = turn(part, cos_ref[pl.ds(at, TILE), :], -sin_ref[pl.ds(at, TILE), :])
            fields_ref[pl.ds(at, TILE), :LANES] = turned.astype(bf16)
        return 0

    lax.fori_loop(0, TILES, one_tile, 0)
    step = KEY_ROWS // 9

    def finish(i, _):
        rows = pl.ds(pl.multiple_of(i * step, EDGE), step)
        fields_ref[rows, LANES : 2 * LANES] = turn(
            dk_ref[rows, :], cos_ref[rows, :], -sin_ref[rows, :]
        ).astype(bf16)
        fields_ref[rows, 2 * LANES :] = dv_ref[rows, :].astype(bf16)
        for c in range(3):
            out_ref[c, rows, :] = fields_ref[rows, c * LANES : (c + 1) * LANES]
        return 0

    lax.fori_loop(0, 9, finish, 0)

    def weight_rows(i, _):
        rows = pl.ds(pl.multiple_of(i * ROW_TILE, LANES), ROW_TILE)
        grad = dot(rows_ref[rows, :], fields_ref[...]).astype(bf16)
        for c in range(3):
            grad_ref[c, rows, :] = grad[:, c * LANES : (c + 1) * LANES]
        return 0

    lax.fori_loop(0, rows_ref.shape[0] // ROW_TILE, weight_rows, 0)


def attend_backward(
    spans,
    clean_bounds,
    noisy_bounds,
    query,
    keys,
    values,
    attended,
    d_attended,
    lse,
    cosine,
    sine,
    rows_t,
):
    count, cols = query.shape
    pairs = cols // LANES
    width = rows_t.shape[0]
    whole2 = lambda array: pl.BlockSpec(array.shape, lambda p, s: (0, 0))
    whole3 = lambda array: pl.BlockSpec(array.shape, lambda p, s: (0, 0, 0))
    row_spec = pl.BlockSpec((count, LANES), lambda p, s: (0, p))
    own_spec = pl.BlockSpec((TOK_DEV, LANES), lambda p, s: (0, p))
    return pl.pallas_call(
        backward_kernel,
        grid_spec=pltpu.PrefetchScalarGridSpec(
            num_scalar_prefetch=1,
            grid=(pairs,),
            in_specs=[whole3(clean_bounds), whole3(noisy_bounds)]
            + [row_spec] * 3
            + [own_spec] * 2
            + [
                pl.BlockSpec((1, TILES, 2, 2 * TILE), lambda p, s: (p, 0, 0, 0)),
                whole2(cosine),
                whole2(sine),
                whole2(rows_t),
            ],
            out_specs=[
                pl.BlockSpec((3, count, LANES), lambda p, s: (0, 0, p)),
                pl.BlockSpec((3, width, LANES), lambda p, s: (0, 0, p)),
            ],
            scratch_shapes=[pltpu.VMEM((count, LANES), f32)] * 2
            + [pltpu.VMEM((count, 3 * LANES), bf16)],
        ),
        out_shape=[
            jax.ShapeDtypeStruct((3, count, cols), bf16),
            jax.ShapeDtypeStruct((3, width, cols), bf16),
        ],
        name="attend_backward",
        cost_estimate=pl.CostEstimate(
            flops=36 * 10**9, bytes_accessed=36 * 10**6, transcendentals=6 * 10**6
        ),
    )(
        spans,
        clean_bounds,
        noisy_bounds,
        query,
        keys,
        values,
        attended,
        d_attended,
        lse,
        cosine,
        sine,
        rows_t,
    )


PIECES = 16
MESH = pl.DeviceIdType.MESH


def flip(value, mask):
    result = value
    for b in range(mask.bit_length()):
        if mask >> b & 1:
            result = result + (1 << b) * (1 - 2 * ((value // (1 << b)) % 2))
    return result


class Exchange:
    names = ("a", "b", "c", "d", "e", "f", "g")

    def __init__(self, bits, count, rows, width):
        self.bits, self.count, self.rows, self.width = bits, count, rows, width
        self.half, self.quarter, self.piece = rows // 2, rows // 4, rows // PIECES
        self.extra = list(range(4, bits))

    def scratch(self):
        k, w = self.count, self.width
        shapes = [
            pltpu.VMEM((k, 2, self.half, w), bf16),
            pltpu.VMEM((k, self.half, w), bf16),
            pltpu.VMEM((k, self.half, w), bf16),
            pltpu.VMEM((k, self.quarter, w), bf16),
            pltpu.VMEM((k, self.quarter, w), bf16),
            pltpu.VMEM((k, self.quarter, w), f32),
            pltpu.VMEM((k, 3, self.piece, w), bf16),
            pltpu.VMEM((k, 3, self.piece, w), bf16),
        ]
        for lanes in (2, 1, 1, 3, 3, 1, 1):
            shapes += [pltpu.SemaphoreType.DMA((k, lanes))] * 2
        if self.extra:
            n = len(self.extra)
            shapes += [pltpu.VMEM((k, 2 * n, self.piece, w), bf16)]
            shapes += [pltpu.SemaphoreType.DMA((k, n))] * 2
        return shapes

    def bind(self, place, part, refs):
        (self.a_in, self.b_out, self.b_in, self.c_out, self.c_in, self.keep) = refs[:6]
        self.d_out, self.d_in = refs[6:8]
        self.sems = {
            name: (refs[8 + 2 * i], refs[9 + 2 * i]) for i, name in enumerate(self.names)
        }
        if self.extra:
            self.x_buf, self.x_send, self.x_recv = refs[22:25]
        self.place, self.part = place, part
        self.core, self.x, self.z = place % 2, (place // 2) % 2, (place // 4) % 4
        self.sibling = {"dp": flip(place, 1)}
        self.beside = {"dp": flip(place, 2)}
        self.across = {"mp": 1 - part}
        self.peers = [{"dp": flip(place, j << 2)} for j in range(1, 4)]
        self.partners = [self.sibling, self.beside, self.across] + self.peers
        self.partners += [{"dp": flip(place, 1 << b)} for b in self.extra]
        return self

    def greet(self):
        barrier = pltpu.get_barrier_semaphore()
        for partner in self.partners:
            pl.semaphore_signal(barrier, inc=1, device_id=partner, device_id_type=MESH)
        pl.semaphore_wait(barrier, len(self.partners))

    def copy(self, name, k, lane, source, target, device):
        out, into = self.sems[name]
        return pltpu.make_async_remote_copy(
            src_ref=source,
            dst_ref=target,
            send_sem=out.at[k, lane],
            recv_sem=into.at[k, lane],
            device_id=device,
            device_id_type=MESH,
        )

    def rows_at(self, start, size):
        return pl.ds(pl.multiple_of(start, PIECES), size)

    def copy_a(self, k, lane, grads):
        source = grads.at[k, self.rows_at((1 - self.core) * self.half, self.half)]
        return self.copy("a", k, lane, source, self.a_in.at[k, lane], self.sibling)

    def copy_b(self, k):
        return self.copy("b", k, 0, self.b_out.at[k], self.b_in.at[k], self.across)

    def copy_c(self, k):
        return self.copy("c", k, 0, self.c_out.at[k], self.c_in.at[k], self.beside)

    def copy_d(self, k, j):
        return self.copy("d", k, j, self.d_out.at[k, j], self.d_in.at[k, j], self.peers[j])

    def spot(self, change=0):
        start = self.core * self.half + self.x * self.quarter
        return self.rows_at(start + flip(self.z, change) * self.piece, self.piece)

    def copy_e(self, k, j, full):
        rows = full.at[k, self.spot()]
        return self.copy("e", k, j, rows, rows, self.peers[j])

    def copy_f(self, k, full):
        start = self.core * self.half + self.x * self.quarter
        rows = full.at[k, self.rows_at(start, self.quarter)]
        return self.copy("f", k, 0, rows, rows, self.beside)

    def copy_g(self, k, full):
        rows = full.at[k, self.rows_at(self.core * self.half, self.half)]
        return self.copy("g", k, 0, rows, rows, self.sibling)

    def start_a(self, k, lane, grads):
        self.copy_a(k, lane, grads).start()

    def stage_b(self, k, others):
        self.copy_a(k, 0, others).wait()
        mine = others[k, self.rows_at(self.core * self.half, self.half), :].astype(f32)
        self.b_out[k] = (mine + self.a_in[k, 0].astype(f32)).astype(bf16)
        self.copy_b(k).start()

    def stage_c(self, k, grads, crossed=True):
        self.copy_a(k, 1, grads).wait()
        if crossed:
            self.copy_b(k).wait()

        def total(which):
            inner = which * self.quarter
            rows = self.rows_at(inner, self.quarter)
            mine = grads[k, self.rows_at(self.core * self.half + inner, self.quarter), :]
            got = self.a_in[k, 1, rows, :].astype(f32)
            if crossed:
                got = got + self.b_in[k, rows, :].astype(f32)
            return mine.astype(f32) + got

        self.c_out[k] = total(1 - self.x).astype(bf16)
        self.copy_c(k).start()
        self.keep[k] = total(self.x)

    def stage_d(self, k):
        self.copy_c(k).wait()
        for j in range(4):
            rows = self.rows_at(flip(self.z, j) * self.piece, self.piece)
            total = self.keep[k, rows, :] + self.c_in[k, rows, :].astype(f32)
            if j:
                self.d_out[k, j - 1] = total.astype(bf16)
                self.copy_d(k, j - 1).start()
            else:
                self.keep[k, rows, :] = total

    def stage_e(self, k, full):
        rows = self.rows_at(self.z * self.piece, self.piece)
        total = self.keep[k, rows, :]
        for j in range(3):
            self.copy_d(k, j).wait()
            total = total + self.d_in[k, j].astype(f32)
        for i, b in enumerate(self.extra):
            mine = self.x_buf.at[k, 2 * i]
            mine[...] = total.astype(bf16)
            swap = pltpu.make_async_remote_copy(
                src_ref=mine,
                dst_ref=self.x_buf.at[k, 2 * i + 1],
                send_sem=self.x_send.at[k, i],
                recv_sem=self.x_recv.at[k, i],
                device_id={"dp": flip(self.place, 1 << b)},
                device_id_type=MESH,
            )
            swap.start()
            swap.wait()
            total = total.astype(bf16).astype(f32) + self.x_buf[k, 2 * i + 1].astype(f32)
        full[k, self.spot(), :] = total.astype(bf16)
        for j in range(3):
            self.copy_e(k, j, full).start()

    def stage_f(self, k, full):
        for j in range(3):
            self.copy_e(k, j, full).wait()
        self.copy_f(k, full).start()

    def stage_g(self, k, full):
        self.copy_f(k, full).wait()
        self.copy_g(k, full).start()

    def stage_h(self, k, full):
        self.copy_g(k, full).wait()


def at_step(step, count, action):
    @pl.when(jnp.logical_and(step >= 0, step < count))
    def _():
        action(step)


SPLIT = 4


def middle_kernel(exchange, tiles, *refs):
    (
        x_ref,
        att_ref,
        att2_ref,
        wout_ref,
        wout2_ref,
        dy_ref,
        vectors_ref,
        bup_ref,
        up_mine,
        up_here,
        down_mine,
        down_here,
        out_ref,
        mid_ref,
        datt_ref,
        datt2_ref,
        gout_ref,
        gout2_ref,
        gbup_ref,
        small_ref,
        gdown_ref,
        gup_ref,
        full_ref,
        up_there,
        down_there,
        pass_up,
        pass_down,
        up_buf,
        down_buf,
        load_sem,
        n2_ref,
        total_ref,
        dn2_ref,
        act_ref,
        dpre_ref,
        grad_ref,
        *rest,
    ) = refs
    place, part = lax.axis_index("dp"), lax.axis_index("mp")
    ex = exchange.bind(place, part, rest)
    core = ex.core
    count = tiles // 2
    rows_all = x_ref.shape[0]
    blocks = rows_all // ROW_TILE
    width = x_ref.shape[1]
    lanes = width // 2

    def which(i):
        other = jnp.logical_or(i == 0, jnp.logical_and(i % 2 == 1, i < tiles - 1))
        mine = jnp.where(i == tiles - 1, count - 1, i // 2 - 1)
        return other, jnp.where(other, (i + 1) // 2, mine)

    def load(i, up_source, down_source, h):
        slot = i % 2
        sems = load_sem.at[slot]
        if h is None:
            return pltpu.make_async_copy(down_source, down_buf.at[slot], sems.at[2])
        target = up_buf.at[slot, h * lanes : (h + 1) * lanes]
        return pltpu.make_async_copy(up_source, target, sems.at[h])

    def hand_up(k):
        cols = pl.ds(pl.multiple_of(k * HIDDEN_TILE, HIDDEN_TILE), HIDDEN_TILE)
        return pltpu.make_async_remote_copy(
            src_ref=up_here.at[:, cols],
            dst_ref=up_there.at[k],
            send_sem=pass_up.at[k, 0],
            recv_sem=pass_up.at[k, 1],
            device_id=ex.sibling,
            device_id_type=MESH,
        )

    def hand_down(k):
        rows = pl.ds(pl.multiple_of(k * HIDDEN_TILE, HIDDEN_TILE), HIDDEN_TILE)
        return pltpu.make_async_remote_copy(
            src_ref=down_here.at[rows, :],
            dst_ref=down_there.at[k],
            send_sem=pass_down.at[k, 0],
            recv_sem=pass_down.at[k, 1],
            device_id=ex.sibling,
            device_id_type=MESH,
        )

    def start_loads(i):
        other, k = which(i)
        held = k // (count // 2) == core

        @pl.when(other)
        def _():
            hand_up(k).wait()

        @pl.when(jnp.logical_and(other, jnp.logical_not(held)))
        def _():
            hand_down(k % (count // 2)).wait()

        cols = pl.ds(pl.multiple_of(k * HIDDEN_TILE, HIDDEN_TILE), HIDDEN_TILE)
        inner = k % (count // 2)
        rows = pl.ds(pl.multiple_of(inner * HIDDEN_TILE, HIDDEN_TILE), HIDDEN_TILE)

        def put(condition, source, h):
            @pl.when(condition)
            def _():
                if h is None:
                    load(i, None, source, None).start()
                else:
                    load(i, source, None, h).start()

        mine = jnp.logical_not(other)
        for h in range(2):
            put(mine, up_mine.at[h * lanes : (h + 1) * lanes, cols], h)
            put(jnp.logical_and(other, core == h), up_here.at[:, cols], h)
            put(jnp.logical_and(other, core != h), up_there.at[k], h)
        put(mine, down_mine.at[cols, :], None)
        put(jnp.logical_and(other, held), down_here.at[rows, :], None)
        put(jnp.logical_and(other, jnp.logical_not(held)), down_there.at[inner], None)

    def wait_loads(i):
        for h in range(2):
            load(i, up_mine.at[:lanes, :HIDDEN_TILE], None, h).wait()
        load(i, None, down_mine.at[:HIDDEN_TILE, :], None).wait()

    ex.greet()

    def hand(k, _):
        hand_up(k).start()

        @pl.when(k < count // 2)
        def _():
            hand_down(k).start()

        return 0

    lax.fori_loop(0, count, hand, 0)

    def prologue(r, _):
        rows = pl.ds(pl.multiple_of(r * ROW_TILE, ROW_TILE), ROW_TILE)
        branch = dot(att_ref[rows, :], wout_ref[...]) + dot(att2_ref[rows, :], wout2_ref[...])
        mid = x_ref[rows, :].astype(f32) + branch
        mid_ref[rows, :] = mid
        unit = normal(mid)[0]
        n2_ref[rows, :] = (unit * vectors_ref[2:3, :] + vectors_ref[3:4, :]).astype(bf16)
        total_ref[rows, :] = mid + vectors_ref[4:5, :]
        dn2_ref[rows, :] = jnp.zeros((ROW_TILE, width), f32)
        return 0

    lax.fori_loop(0, blocks, prologue, 0)
    start_loads(0)

    def tile(i):
        other, k = which(i)
        slot = i % 2
        wait_loads(i)

        @pl.when(i + 1 < tiles)
        def _():
            start_loads(i + 1)

        up, down = up_buf.at[slot], down_buf.at[slot]
        bias_at = jnp.where(other, k, count + k)
        bias_grad = jnp.zeros((1, HIDDEN_TILE), f32)
        for r in range(blocks):
            rows = slice(r * ROW_TILE, (r + 1) * ROW_TILE)
            pre = dot(n2_ref[rows, :], up[...]) + bup_ref[bias_at]
            square = pre * pre
            bend = jnp.tanh(0.7978845608028654 * (pre + 0.044715 * square * pre))
            part_one = 0.5 * (1.0 + bend)
            act = (pre * part_one).astype(bf16)
            slope = part_one + (0.5 * pre) * (1.0 - bend * bend) * (
                0.7978845608028654 * (1.0 + 3.0 * 0.044715 * square)
            )
            d_act = dot(dy_ref[rows, :], down[...], NT)
            d_pre = (d_act * slope).astype(bf16)
            act_ref[rows, :] = act
            dpre_ref[rows, :] = d_pre
            bias_grad = bias_grad + jnp.sum(d_pre.astype(f32), axis=0, keepdims=True)
            total_ref[rows, :] += dot(act, down[...])
            dn2_ref[rows, :] += dot(d_pre, up[...], NT)
        gbup_ref[bias_at] = bias_grad
        grads = (
            dot(act_ref[...].T, dy_ref[...]).astype(bf16),
            dot(dpre_ref[...].T, n2_ref[...]).astype(bf16),
        )
        for c in range(SPLIT):
            cols = slice(c % 2 * lanes, (c % 2 + 1) * lanes)
            grad_ref[k * SPLIT + c] = grads[c // 2][:, cols]

        @pl.when(other)
        def _():
            for c in range(SPLIT):
                ex.start_a(k * SPLIT + c, 0, grad_ref)

        @pl.when(jnp.logical_not(other))
        def _():
            for c in range(SPLIT):
                ex.start_a(k * SPLIT + c, 1, grad_ref)

    def group(k, when, action):
        @pl.when(jnp.logical_and(when, jnp.logical_and(k >= 0, k < count)))
        def _():
            lax.fori_loop(0, SPLIT, lambda c, _: (action(k * SPLIT + c), 0)[1], 0)

    def arrive(c):
        ex.stage_h(c, full_ref)
        k, lane = c // SPLIT, c % SPLIT
        hidden = pl.ds(pl.multiple_of(k * HIDDEN_TILE, HIDDEN_TILE), HIDDEN_TILE)
        cols = pl.ds(pl.multiple_of(lane % 2 * lanes, LANES), lanes)

        @pl.when(lane < 2)
        def _():
            gdown_ref[hidden, cols] = full_ref[c]

        @pl.when(lane >= 2)
        def _():
            gup_ref[cols, hidden] = full_ref[c].T

    def steps(i):
        even = i % 2 == 0
        odd = jnp.logical_not(even)
        group((i - 9) // 2, odd, arrive)
        group((i - 8) // 2, even, lambda k: ex.stage_g(k, full_ref))
        group((i - 7) // 2, odd, lambda k: ex.stage_f(k, full_ref))
        group((i - 6) // 2, even, lambda k: ex.stage_e(k, full_ref))
        group((i - 5) // 2, odd, lambda k: ex.stage_d(k))
        group((i - 4) // 2, even, lambda k: ex.stage_c(k, grad_ref))
        crossing = jnp.logical_or(i == 1, jnp.logical_and(even, i >= 2))
        group(i // 2, crossing, lambda k: ex.stage_b(k, grad_ref))

    def tick(d):
        total = count * SPLIT

        def due(c, least, action):
            @pl.when(jnp.logical_and(c >= least, c < total))
            def _():
                action(c)

        done = [
            (tiles + 1 - lag) // 2 * SPLIT if lag % 2 == 0 else (tiles - lag + 1) // 2 * SPLIT
            for lag in (9, 8, 7, 6, 5, 4)
        ]
        first = done[5]
        due(first - 10 + d, done[0], arrive)
        due(first - 8 + d, done[1], lambda c: ex.stage_g(c, full_ref))
        due(first - 6 + d, done[2], lambda c: ex.stage_f(c, full_ref))
        due(first - 4 + d, done[3], lambda c: ex.stage_e(c, full_ref))
        due(first - 2 + d, done[4], lambda c: ex.stage_d(c))
        due(first + d, done[5], lambda c: ex.stage_c(c, grad_ref))

    def main(i, _):
        tile(i)
        steps(i)
        return 0

    lax.fori_loop(0, tiles, main, 0)

    def epilogue(r, sums):
        rows = pl.ds(pl.multiple_of(r * ROW_TILE, ROW_TILE), ROW_TILE)
        out_ref[rows, :] = total_ref[rows, :].astype(bf16)
        unit, scale = normal(mid_ref[rows, :])
        d_rows = dn2_ref[rows, :]
        dy = dy_ref[rows, :].astype(f32)
        lean = d_rows * vectors_ref[2:3, :]
        d_mid = dy + scale * (
            lean
            - jnp.mean(lean, axis=-1, keepdims=True)
            - unit * jnp.mean(lean * unit, axis=-1, keepdims=True)
        )
        mid_ref[rows, :] = d_mid
        d_branch = d_mid.astype(bf16)
        n2_ref[rows, :] = d_branch
        datt_ref[rows, :] = dot(d_branch, wout_ref[...], NT).astype(bf16)
        datt2_ref[rows, :] = dot(d_branch, wout2_ref[...], NT).astype(bf16)
        add = lambda values: jnp.sum(values, axis=0, keepdims=True)
        sums = (sums[0] + add(d_rows * unit), sums[1] + add(d_rows), sums[2] + add(dy))
        tick(2 * r)
        tick(2 * r + 1)
        return sums

    zero = jnp.zeros((1, width), f32)
    sums = lax.fori_loop(0, blocks, epilogue, (zero, zero, zero))
    for j in range(3):
        small_ref[j : j + 1, :] = sums[j]
    depth = wout_ref.shape[0]
    for source, target in ((att_ref, gout_ref), (att2_ref, gout2_ref)):
        grad = dot(source[...].T, n2_ref[...]).astype(bf16)
        target[:depth, :] = grad[:, :lanes]
        target[depth:, :] = grad[:, lanes:]

    def drain(d, _):
        tick(d)
        return 0

    lax.fori_loop(2 * blocks, 2 * SPLIT + 10, drain, 0)


def middle(bits, x, att, att2, wout, wout2, dy, vectors, bup, ups, downs):
    rows, width = x.shape
    hidden = ups[0].shape[1]
    count = hidden // HIDDEN_TILE
    tiles = 2 * count
    exchange = Exchange(bits, count * SPLIT, HIDDEN_TILE, width // 2)
    vmem = pl.BlockSpec(memory_space=pltpu.VMEM)
    hbm = pl.BlockSpec(memory_space=pl.ANY)
    shape = jax.ShapeDtypeStruct
    depth = wout.shape[0]
    return pl.pallas_call(
        functools.partial(middle_kernel, exchange, tiles),
        in_specs=[vmem] * 8 + [hbm] * 4,
        out_specs=[vmem] * 10,
        out_shape=[
            shape((rows, width), bf16),
            shape((rows, width), f32),
            shape(att.shape, bf16),
            shape(att2.shape, bf16),
            shape((2 * depth, width // 2), bf16),
            shape((2 * depth, width // 2), bf16),
            shape((tiles, 1, HIDDEN_TILE), f32),
            shape((8, width), f32),
            shape((hidden, width), bf16),
            shape((width, hidden), bf16),
        ],
        scratch_shapes=[
            pltpu.VMEM((count * SPLIT, HIDDEN_TILE, width // 2), bf16),
            pltpu.VMEM((count, width // 2, HIDDEN_TILE), bf16),
            pltpu.VMEM((count // 2, HIDDEN_TILE, width), bf16),
            pltpu.SemaphoreType.DMA((count, 2)),
            pltpu.SemaphoreType.DMA((count // 2, 2)),
            pltpu.VMEM((2, width, HIDDEN_TILE), bf16),
            pltpu.VMEM((2, HIDDEN_TILE, width), bf16),
            pltpu.SemaphoreType.DMA((2, 3)),
            pltpu.VMEM((rows, width), bf16),
            pltpu.VMEM((rows, width), f32),
            pltpu.VMEM((rows, width), f32),
            pltpu.VMEM((rows, HIDDEN_TILE), bf16),
            pltpu.VMEM((rows, HIDDEN_TILE), bf16),
            pltpu.VMEM((count * SPLIT, HIDDEN_TILE, width // 2), bf16),
        ]
        + exchange.scratch(),
        compiler_params=pltpu.CompilerParams(
            collective_id=0, has_side_effects=True, vmem_limit_bytes=67043328
        ),
        name="middle",
        cost_estimate=pl.CostEstimate(
            flops=60 * 10**9, bytes_accessed=40 * 10**6, transcendentals=4 * 10**6
        ),
    )(x, att, att2, wout, wout2, dy, vectors, bup, *ups, *downs)


def leave_kernel(exchange, *refs):
    (
        mine_ref,
        mine_out_ref,
        crossed_ref,
        crossed_out_ref,
        d_ref,
        d2_ref,
        w_ref,
        w2_ref,
        tokens_ref,
        vectors_ref,
        dmid_ref,
        small_ref,
        small2_ref,
        full_ref,
        back_ref,
        sums_ref,
        sum_buf,
        rows_ref,
        give_ref,
        take_ref,
        swap_sem,
        near_ref,
        far_ref,
        near_sem,
        far_sem,
        *rest,
    ) = refs
    place, part = lax.axis_index("dp"), lax.axis_index("mp")
    ex = exchange.bind(place, part, rest)
    count, bits = ex.count, ex.bits
    first = mine_ref.shape[0]
    near_id = part * 4 + place % 4
    near = [
        {"dp": flip(place, j % 4), "mp": part if j < 4 else 1 - part} for j in range(1, 8)
    ]
    ex.partners += [near[j - 1] for j in (3, 5, 6, 7)]
    ex.greet()

    def begin(k, _):
        total = mine_ref[k].astype(f32) + crossed_ref[k].astype(f32)
        sum_buf[k] = total.astype(bf16)
        ex.start_a(k, 1, sum_buf)
        return 0

    lax.fori_loop(0, first, begin, 0)

    def begin_out(k, _):
        total = mine_out_ref[k].astype(f32) + crossed_out_ref[k].astype(f32)
        sum_buf[first + k] = total.astype(bf16)
        ex.start_a(first + k, 1, sum_buf)
        return 0

    lax.fori_loop(0, count - first, begin_out, 0)

    def back_of(rows):
        total = 0.0
        for grads, weights in ((d_ref, w_ref), (d2_ref, w2_ref)):
            for c in range(3):
                total = total + dot(grads[c, rows, :], weights[c], NT)
        return total

    def steps(i):
        at_step(i - 10, count, lambda k: ex.stage_h(k, full_ref))
        at_step(i - 8, count, lambda k: ex.stage_g(k, full_ref))
        at_step(i - 6, count, lambda k: ex.stage_f(k, full_ref))
        at_step(i - 4, count, lambda k: ex.stage_e(k, full_ref))
        at_step(i - 2, count, lambda k: ex.stage_d(k))
        at_step(i, count, lambda k: ex.stage_c(k, sum_buf, False))

    def many(low, high):
        lax.fori_loop(low, high, lambda i, _: (steps(i), 0)[1], 0)

    tail = back_of(slice(2 * HALF, KEY_ROWS))
    own = NOISY_OWN - 2 * HALF
    rows_ref[:HALF, :] = tail[own : own + HALF]
    give_ref[HALF:, :] = (tail[EDGE:own] + tail[own + HALF :]).astype(bf16)
    rows_ref[HALF : HALF + EDGE, :] = tail[:EDGE]
    many(0, 3)
    given = back_of(slice(0, HALF))
    give_ref[EDGE:HALF, :] = given[EDGE:].astype(bf16)
    give_ref[:EDGE, :] = (given[:EDGE] + rows_ref[HALF : HALF + EDGE, :]).astype(bf16)
    swap = pltpu.make_async_remote_copy(
        src_ref=give_ref,
        dst_ref=take_ref,
        send_sem=swap_sem.at[0],
        recv_sem=swap_sem.at[1],
        device_id=ex.across,
        device_id_type=MESH,
    )
    swap.start()
    many(3, 6)
    rows_ref[HALF:, :] = back_of(slice(CLEAN_OWN, CLEAN_OWN + HALF))
    many(6, 10)
    swap.wait()
    rows_ref[HALF:, :] += take_ref[:HALF, :].astype(f32)
    edge = pl.ds(pl.multiple_of((1 - part) * (HALF - EDGE), EDGE), EDGE)
    rows_ref[edge, :] += take_ref[HALF:, :].astype(f32)

    def norm_back(b, sums):
        rows = pl.ds(pl.multiple_of(b * ROW_TILE, TILE), ROW_TILE)
        unit, scale = normal(tokens_ref[rows, :].astype(f32))
        d_rows = rows_ref[rows, :]
        lean = d_rows * vectors_ref[0:1, :]
        back_ref[rows, :] = dmid_ref[rows, :] + scale * (
            lean
            - jnp.mean(lean, axis=-1, keepdims=True)
            - unit * jnp.mean(lean * unit, axis=-1, keepdims=True)
        )
        add = lambda values: jnp.sum(values, axis=0, keepdims=True)
        steps(10 + b)
        return (sums[0] + add(d_rows * unit), sums[1] + add(d_rows))

    width = tokens_ref.shape[1]
    parts = tokens_ref.shape[0] // ROW_TILE
    zero = jnp.zeros((1, width), f32)
    sums = lax.fori_loop(0, parts, norm_back, (zero, zero))
    lead = small_ref.shape[0] - 2
    bias = lead - 3
    mine = near_ref.at[near_id]
    mine[:lead, :] = small_ref[:lead, :]
    for j in range(2):
        mine[lead + j : lead + j + 1, :] = sums[j]
    mine[lead + 2 : lead + 2 + bias, :] = small2_ref[:bias, :]
    rest_rows = 16 - lead - 2 - bias
    mine[16 - rest_rows :, :] = jnp.zeros((rest_rows, width), f32)

    def near_copy(j):
        return pltpu.make_async_remote_copy(
            src_ref=near_ref.at[near_id],
            dst_ref=near_ref.at[near_id],
            send_sem=near_sem.at[j, 0],
            recv_sem=near_sem.at[j, 1],
            device_id=near[j - 1],
            device_id_type=MESH,
        )

    def near_got(j):
        came = (part + j // 4) % 2 * 4 + flip(place % 4, j % 4)
        return pltpu.make_async_remote_copy(
            src_ref=near_ref.at[came],
            dst_ref=near_ref.at[came],
            send_sem=near_sem.at[j, 0],
            recv_sem=near_sem.at[j, 1],
            device_id=near[j - 1],
            device_id_type=MESH,
        )

    for j in range(1, 8):
        near_copy(j).start()
    many(10 + parts, 13 + parts)
    for j in range(1, 8):
        near_copy(j).wait_send()
        near_got(j).wait_recv()
    total = near_ref[0]
    for j in range(1, 8):
        total = total + near_ref[j]
    plane = near_ref[part * 4]
    other = near_ref[(1 - part) * 4]
    for j in range(1, 4):
        plane = plane + near_ref[part * 4 + j]
        other = other + near_ref[(1 - part) * 4 + j]
    spot = far_ref.at[ex.z]
    spot[...] = total
    spot[:bias, :] = plane[:bias] + other[lead + 2 : lead + 2 + bias]

    def far_copy(j, at):
        return pltpu.make_async_remote_copy(
            src_ref=far_ref.at[at],
            dst_ref=far_ref.at[at],
            send_sem=far_sem.at[j, 0],
            recv_sem=far_sem.at[j, 1],
            device_id=ex.peers[j - 1],
            device_id_type=MESH,
        )

    for j in range(1, 4):
        far_copy(j, ex.z).start()
    many(13 + parts, 16 + parts)
    for j in range(1, 4):
        far_copy(j, ex.z).wait_send()
        far_copy(j, flip(ex.z, j)).wait_recv()
    total = far_ref[0]
    for j in range(1, 4):
        total = total + far_ref[j]
    for i, b in enumerate(ex.extra):
        far_ref[4 + 2 * i] = total
        trade = pltpu.make_async_remote_copy(
            src_ref=far_ref.at[4 + 2 * i],
            dst_ref=far_ref.at[5 + 2 * i],
            send_sem=far_sem.at[4 + i, 0],
            recv_sem=far_sem.at[4 + i, 1],
            device_id={"dp": flip(place, 1 << b)},
            device_id_type=MESH,
        )
        trade.start()
        trade.wait()
        total = total + far_ref[5 + 2 * i]
    sums_ref[...] = total
    many(16 + parts, count + 10)


def leave(bits, mine, crossed, d_fields, weights, tokens, vectors, d_mid, small, small2):
    total = mine[0].shape[0] + mine[1].shape[0]
    rows, cols = mine[0].shape[1:]
    exchange = Exchange(bits, total, rows, cols)
    count, width = tokens.shape
    vmem = pl.BlockSpec(memory_space=pltpu.VMEM)
    shape = jax.ShapeDtypeStruct
    return pl.pallas_call(
        functools.partial(leave_kernel, exchange),
        in_specs=[vmem] * 13,
        out_specs=[vmem] * 3,
        out_shape=[
            shape((total, rows, cols), bf16),
            shape((count, width), f32),
            shape((16, width), f32),
        ],
        scratch_shapes=[
            pltpu.VMEM((total, rows, cols), bf16),
            pltpu.VMEM((count, width), f32),
            pltpu.VMEM((HALF + EDGE, width), bf16),
            pltpu.VMEM((HALF + EDGE, width), bf16),
            pltpu.SemaphoreType.DMA((2,)),
            pltpu.VMEM((8, 16, width), f32),
            pltpu.VMEM((4 + 2 * len(exchange.extra), 16, width), f32),
            pltpu.SemaphoreType.DMA((8, 2)),
            pltpu.SemaphoreType.DMA((4 + len(exchange.extra), 2)),
        ]
        + exchange.scratch(),
        compiler_params=pltpu.CompilerParams(
            collective_id=1, has_side_effects=True, vmem_limit_bytes=67043328
        ),
        name="leave",
        cost_estimate=pl.CostEstimate(
            flops=40 * 10**9, bytes_accessed=40 * 10**6, transcendentals=0
        ),
    )(*mine, *crossed, *d_fields, *weights, tokens, vectors, d_mid, small, small2)


def key_layout(seq_lengths, block_len, part):
    index = jnp.arange(KEY_ROWS, dtype=jnp.int32)
    own = part * HALF
    token = jnp.where(
        index < NOISY_BASE, index + (own - HALF), index - NOISY_BASE + (own - EDGE)
    )
    ends = jnp.cumsum(seq_lengths)
    passed = token[:, None] >= ends[None, :]
    starts = jnp.sum(jnp.where(passed, seq_lengths[None, :], 0), axis=1)
    lengths_here = jnp.where(passed, 0, ends[None, :])
    stops = jnp.min(jnp.where(passed, TOK_DEV, lengths_here), axis=1)
    positions = token - starts
    block_start = starts + positions // block_len * block_len
    block_stop = jnp.minimum(block_start + block_len, stops)
    mine = slice(CLEAN_OWN, CLEAN_OWN + HALF)
    low, start, stop = starts[mine], block_start[mine], block_stop[mine]
    to_clean = own - HALF
    tiles = lambda column: column.reshape(TILES, 1, TILE)
    clean_bounds = jnp.concatenate(
        [
            jnp.concatenate([tiles(low - to_clean), tiles(low - to_clean)], axis=2),
            jnp.concatenate([tiles(start - to_clean), tiles(stop - to_clean)], axis=2),
        ],
        axis=1,
    )
    to_window = own - EDGE + TILE * jnp.arange(TILES, dtype=jnp.int32)[:, None, None]
    noisy_bounds = jnp.concatenate(
        [tiles(start) - to_window, tiles(stop) - to_window], axis=1
    )
    first = jnp.min(clean_bounds[:, 0], axis=1) // EDGE * EDGE
    last = jnp.max(clean_bounds[:, 1], axis=1)
    trips = (last - first + KEY_TILE - 1) // KEY_TILE
    spans = jnp.stack([first, trips], axis=1)
    lane = jnp.arange(LANES, dtype=jnp.int32)
    frequency = jnp.exp(
        (lane % (HD // 2)).astype(f32) * (-math.log(10000.0) / (HD // 2))
    )
    angles = positions.astype(f32)[:, None] * frequency[None, :]
    sign = jnp.where(lane % HD < HD // 2, -1.0, 1.0)
    return spans, clean_bounds, noisy_bounds, jnp.cos(angles), jnp.sin(angles) * sign


def half_of(array, which, axis=0):
    size = array.shape[axis] // 2
    return lax.dynamic_slice_in_dim(array, which * size, size, axis)


def in_order(bit, mine, theirs, axis=0):
    order = bit == 0
    return jnp.concatenate(
        [jnp.where(order, mine, theirs), jnp.where(order, theirs, mine)], axis=axis
    )


def tie(first, second):
    return lax.optimization_barrier((first, second))


def local(
    dp_size,
    tokens,
    lengths,
    block_size,
    cotangent,
    ln1_gain,
    ln1_bias,
    w_qkv,
    w_out,
    ln2_gain,
    ln2_bias,
    w_up,
    b_up,
    w_down,
    b_down,
):
    width = tokens.shape[2]
    part = lax.axis_index("mp")
    place = lax.axis_index("dp")
    bits = dp_size.bit_length() - 1
    core = place & 1

    def across(array):
        return lax.ppermute(array, "mp", [(0, 1), (1, 0)])

    def sibling(array):
        return lax.ppermute(array, "dp", [(i, i ^ 1) for i in range(dp_size)])

    edge = jnp.where(part == 0, tokens[0, HALF - EDGE :], tokens[0, :EDGE])
    context = across(jnp.concatenate([tokens[1], edge], axis=0))
    qkv_mine = w_qkv.transpose(1, 0, 2)
    halves = [
        half_of(qkv_mine, core, 1),
        half_of(w_out, core),
        half_of(w_up, core),
        half_of(w_down, core),
    ]
    layout = key_layout(lengths[0], block_size[0], part)
    vectors = jnp.stack([ln1_gain, ln1_bias, ln2_gain, ln2_bias, b_down])
    context, (halves, layout, vectors) = tie(context, (halves, layout, vectors))
    qkv_here, out_here, up_here, down_here = [across(half) for half in halves]
    bias_other = across(b_up)

    spans, clean_bounds, noisy_bounds, cosine, sine = layout
    normed1, normed1_t, *fields = enter(tokens, context, vectors, qkv_mine, cosine, sine)
    mine = [*fields, *attend_forward(spans, clean_bounds, noisy_bounds, *fields)]
    (qkv_here, out_here), _ = tie((qkv_here, out_here), mine[3])
    qkv_other = in_order(core, qkv_here, sibling(qkv_here), axis=1)
    out_there = sibling(out_here)
    fields = project(normed1, qkv_other, cosine, sine)
    other = [*fields, *attend_forward(spans, clean_bounds, noisy_bounds, *fields)]
    (out_here, out_there, up_here, down_here, bias_other), _ = tie(
        (out_here, out_there, up_here, down_here, bias_other), other[3]
    )
    bias_all = jnp.concatenate([bias_other, b_up]).astype(f32).reshape(-1, 1, HIDDEN_TILE)

    x_rows = tokens.reshape(TOK_DEV, width)
    out, d_mid, d_att, d_att2, grad_out, grad_out2, grad_bias, norms, grad_down, grad_up = middle(
        bits,
        x_rows,
        mine[3],
        other[3],
        w_out,
        in_order(core, out_here, out_there),
        cotangent.reshape(TOK_DEV, width),
        vectors,
        bias_all,
        (w_up, up_here),
        (w_down, down_here),
    )
    hidden = b_up.shape[0]

    d_qkv, grad_qkv = [], []
    for saved, d_attended in ((other, d_att2), (mine, d_att)):
        query, keys, values, attended, lse = saved
        d_fields, grad = attend_backward(
            spans,
            clean_bounds,
            noisy_bounds,
            query,
            keys,
            values,
            attended,
            d_attended,
            lse,
            cosine,
            sine,
            normed1_t,
        )
        spans = tie(spans, grad)[0]
        d_qkv.append(d_fields)
        grad_qkv.append(grad.reshape(-1, ROW_TILE, grad.shape[2]))
    crossed_out = across(grad_out2)
    crossed = across(grad_qkv[0])
    lead = hidden // width
    bias2, bias1 = grad_bias.reshape(2, lead, width)
    shared = jnp.concatenate([norms[:3], jnp.zeros((2, width), f32)], axis=0)
    full, grad_tokens, sums = leave(
        bits,
        (grad_qkv[1], grad_out.reshape(-1, ROW_TILE, grad_out.shape[1])),
        (crossed, crossed_out.reshape(-1, ROW_TILE, grad_out.shape[1])),
        (d_qkv[1], d_qkv[0]),
        (qkv_mine, qkv_other),
        x_rows,
        vectors,
        d_mid,
        jnp.concatenate([bias1, shared], axis=0),
        jnp.concatenate([bias2, shared], axis=0),
    )
    split = 3 * width // ROW_TILE
    grad_qkv = full[:split].reshape(qkv_mine.shape).transpose(1, 0, 2).astype(f32)
    flat = full[split:].reshape(2, w_out.shape[0], width // 2)
    grad_out = jnp.concatenate([flat[0], flat[1]], axis=1).astype(f32)
    return (
        out.reshape(tokens.shape),
        grad_tokens.reshape(tokens.shape),
        sums[lead + 3],
        sums[lead + 4],
        grad_qkv,
        grad_out,
        sums[lead],
        sums[lead + 1],
        grad_up.astype(f32),
        sums[:lead].reshape(hidden),
        grad_down.astype(f32),
        sums[lead + 2],
    )


def solution(mesh):
    in_specs = (
        P(None, ("dp", "mp"), None),
        P("dp", None),
        P(),
        P(None, ("dp", "mp"), None),
        P(),
        P(),
        P(None, None, "mp"),
        P("mp", None),
        P(),
        P(),
        P(None, "mp"),
        P("mp"),
        P("mp", None),
        P(),
    )
    out_specs = (
        P(None, ("dp", "mp"), None),
        P(None, ("dp", "mp"), None),
        P(),
        P(),
        P(None, None, "mp"),
        P("mp", None),
        P(),
        P(),
        P(None, "mp"),
        P("mp"),
        P("mp", None),
        P(),
    )
    return jax.shard_map(
        functools.partial(local, mesh.shape["dp"]),
        mesh=mesh,
        in_specs=in_specs,
        out_specs=out_specs,
        check_vma=False,
    )
```

```python
import functools
import math

import jax
import jax.numpy as jnp
from jax import lax
from jax.experimental import pallas as pl
from jax.experimental.pallas import tpu as pltpu
from jax.sharding import PartitionSpec as P

HD = 64
TOK_DEV = 1024
HALF = TOK_DEV // 2
EDGE = 16
CLEAN_OWN = HALF
NOISY_BASE = 2 * HALF + EDGE
NOISY_OWN = NOISY_BASE + EDGE
KEY_ROWS = NOISY_OWN + HALF + EDGE
TILE = 128
TILES = HALF // TILE
WINDOW = TILE + 2 * EDGE
KEY_TILE = 192
LANES = 128
HIDDEN_TILE = 256
ROW_TILE = 256

epsilon = 1e-05
neg_large = -1e30
to_base2 = 0.125 * math.log2(math.e)
f32 = jnp.float32
bf16 = jnp.bfloat16

NN = (((1,), (0,)), ((), ()))
NT = (((1,), (1,)), ((), ()))


def dot(left, right, dims=NN):
    return lax.dot_general(left, right, dims, preferred_element_type=f32)


def low_lanes(shape):
    return lax.broadcasted_iota(jnp.int32, shape, 1) < HD


def turn(values, cosine, sine):
    lane = lax.broadcasted_iota(jnp.int32, values.shape, 1)
    first_half = (lane & (HD - 1)) < HD // 2
    swapped = jnp.where(
        first_half,
        pltpu.roll(values, LANES - HD // 2, 1),
        pltpu.roll(values, HD // 2, 1),
    )
    return values * cosine + swapped * sine


def project_rows(rows, w_ref, cosine, sine, q_ref, k_ref, v_ref, at):
    for part, out_ref in ((0, q_ref), (1, k_ref)):
        field = dot(rows, w_ref[part])
        for pair in range(field.shape[1] // LANES):
            cols = slice(pair * LANES, (pair + 1) * LANES)
            out_ref[at, cols] = turn(field[:, cols], cosine, sine).astype(bf16)
    v_ref[at, :] = dot(rows, w_ref[2]).astype(bf16)


def project_kernel(rows_ref, w_ref, cos_ref, sin_ref, q_ref, k_ref, v_ref):
    at = slice(0, rows_ref.shape[0])
    project_rows(rows_ref[...], w_ref, cos_ref[...], sin_ref[...], q_ref, k_ref, v_ref, at)


def project(rows, weights, cosine, sine):
    count, width = rows.shape
    cols = weights.shape[2]
    step = count // 3
    row_spec = pl.BlockSpec((step, width), lambda i: (i, 0))
    table_spec = pl.BlockSpec((step, LANES), lambda i: (i, 0))
    out_spec = pl.BlockSpec((step, cols), lambda i: (i, 0))
    shape = jax.ShapeDtypeStruct((count, cols), bf16)
    return pl.pallas_call(
        project_kernel,
        grid=(3,),
        in_specs=[
            row_spec,
            pl.BlockSpec(weights.shape, lambda i: (0, 0, 0)),
            table_spec,
            table_spec,
        ],
        out_specs=[out_spec] * 3,
        out_shape=[shape] * 3,
        name="project",
        cost_estimate=pl.CostEstimate(
            flops=2 * count * width * 3 * cols,
            bytes_accessed=2 * (count * (width + 3 * cols) + 3 * width * cols),
            transcendentals=0,
        ),
    )(rows, weights, cosine, sine)


def normal(values):
    average = jnp.mean(values, axis=-1, keepdims=True)
    centred = values - average
    variance = jnp.mean(centred * centred, axis=-1, keepdims=True)
    scale = lax.rsqrt(variance + epsilon)
    return centred * scale, scale


def enter_kernel(
    tokens_ref,
    context_ref,
    vectors_ref,
    w_ref,
    cos_ref,
    sin_ref,
    rows_ref,
    rows_t_ref,
    q_ref,
    k_ref,
    v_ref,
):
    def norm(values):
        unit = normal(values.astype(f32))[0]
        return (unit * vectors_ref[0:1, :] + vectors_ref[1:2, :]).astype(bf16)

    def blocks(i, _):
        source = pl.ds(pl.multiple_of(i * TILE, TILE), TILE)
        rows_ref[source, :] = norm(context_ref[source, :])
        at = pl.ds(pl.multiple_of(CLEAN_OWN + i * TILE, TILE), TILE)
        rows_ref[at, :] = norm(tokens_ref[1, source, :])
        at = pl.ds(pl.multiple_of(NOISY_OWN + i * TILE, EDGE), TILE)
        rows_ref[at, :] = norm(tokens_ref[0, source, :])
        return 0

    lax.fori_loop(0, TILES, blocks, 0)
    rows_ref[2 * HALF : NOISY_BASE, :] = rows_ref[:EDGE, :]
    edge = norm(context_ref[HALF:, :])
    rows_ref[NOISY_BASE:NOISY_OWN, :] = edge
    rows_ref[NOISY_OWN + HALF :, :] = edge
    step = KEY_ROWS // 3

    def fields(i, _):
        at = pl.ds(pl.multiple_of(i * step, EDGE), step)
        project_rows(
            rows_ref[at, :], w_ref, cos_ref[at, :], sin_ref[at, :], q_ref, k_ref, v_ref, at
        )
        return 0

    lax.fori_loop(0, 3, fields, 0)
    for c in range(rows_t_ref.shape[0] // LANES):
        cols = slice(c * LANES, (c + 1) * LANES)
        rows_t_ref[cols, :] = rows_ref[:, cols].T


def enter(tokens, context, vectors, weights, cosine, sine):
    width, cols = weights.shape[1:]
    vmem = pl.BlockSpec(memory_space=pltpu.VMEM)
    shape = jax.ShapeDtypeStruct
    field = shape((KEY_ROWS, cols), bf16)
    return pl.pallas_call(
        enter_kernel,
        in_specs=[vmem] * 6,
        out_specs=[vmem] * 5,
        out_shape=[shape((KEY_ROWS, width), bf16), shape((width, KEY_ROWS), bf16)] + [field] * 3,
        name="enter",
        cost_estimate=pl.CostEstimate(
            flops=10**10, bytes_accessed=16 * 10**6, transcendentals=0
        ),
    )(tokens, context, vectors, weights, cosine, sine)


def split_heads(rows):
    low = low_lanes(rows.shape)
    zero = jnp.zeros_like(rows)
    return jnp.where(low, rows, zero), jnp.where(low, zero, rows)


def between(shape, offset, low, high):
    index = lax.broadcasted_iota(jnp.int32, shape, 0) + offset
    return jnp.logical_and(index >= low, index < high)


def fold(values, combine):
    rows, cols = values.shape
    groups = values.reshape(rows // 8, 8, cols)
    return combine(groups, axis=0)


def forward_kernel(
    span_ref, clean_ref, noisy_ref, q_ref, k_ref, v_ref, out_ref, lse_ref, bias_ref, window_ref
):
    pairs = q_ref.shape[1] // LANES
    lanes = [slice(p * LANES, (p + 1) * LANES) for p in range(pairs)]

    def one_tile(t, _):
        clean_at = pl.multiple_of(CLEAN_OWN + t * TILE, TILE)
        noisy_at = pl.multiple_of(NOISY_OWN + t * TILE, EDGE)
        window_at = pl.multiple_of(NOISY_BASE + t * TILE, EDGE)
        key_low, key_high = clean_ref[t, 0:1, :], clean_ref[t, 1:2, :]
        own_low, own_high = noisy_ref[t, 0:1, :], noisy_ref[t, 1:2, :]
        allowed = between((WINDOW, TILE), 0, own_low, own_high)
        window_ref[...] = jnp.where(allowed, 0.0, neg_large)
        first_key, trips = span_ref[t, 0], span_ref[t, 1]
        queries, tops = [], []
        for cols in lanes:
            query = jnp.concatenate(
                [q_ref[pl.ds(noisy_at, TILE), cols], q_ref[pl.ds(clean_at, TILE), cols]], axis=0
            )
            heads = split_heads(query)
            queries += heads
            keys = k_ref[pl.ds(window_at, WINDOW), cols]
            for head in range(2):
                scores = dot(keys, heads[head][:TILE], NT) + window_ref[...]
                top = fold(scores, jnp.max)
                tops.append(
                    jnp.concatenate([top, jnp.full((8, TILE), neg_large, f32)], axis=1)
                )

        def first_pass(j, tops):
            at = pl.multiple_of(first_key + j * KEY_TILE, EDGE)
            allowed = between((KEY_TILE, 2 * TILE), at, key_low, key_high)
            bias_ref[j] = jnp.where(allowed, 0.0, neg_large)
            after = []
            for p, cols in enumerate(lanes):
                keys = k_ref[pl.ds(at, KEY_TILE), cols]
                for head in range(2):
                    scores = dot(keys, queries[2 * p + head], NT) + bias_ref[j]
                    after.append(jnp.maximum(tops[2 * p + head], fold(scores, jnp.max)))
            return tuple(after)

        tops = lax.fori_loop(0, trips, first_pass, tuple(tops))
        tops = [jnp.max(top, axis=0, keepdims=True) * to_base2 for top in tops]
        state = []
        keys = [k_ref[pl.ds(window_at, WINDOW), cols] for cols in lanes]
        values_t = [v_ref[pl.ds(window_at, WINDOW), cols].T for cols in lanes]
        scores = dot(keys[0], queries[0][:TILE], NT)
        late = None
        for h in range(2 * pairs):
            if h + 1 < 2 * pairs:
                ahead = dot(keys[(h + 1) // 2], queries[h + 1][:TILE], NT)
            expo = jnp.exp2(scores * to_base2 - tops[h][:, :TILE] + window_ref[...])
            if late is not None:
                state.append(jnp.concatenate([late, jnp.zeros((HD, TILE), f32)], axis=1))
            total = fold(expo, jnp.sum)
            state.append(jnp.concatenate([total, jnp.zeros((8, TILE), f32)], axis=1))
            side = slice(h % 2 * HD, (h % 2 + 1) * HD)
            late = dot(values_t[h // 2][side], expo.astype(bf16))
            scores = ahead
        state.append(jnp.concatenate([late, jnp.zeros((HD, TILE), f32)], axis=1))

        def second_pass(j, state):
            at = pl.multiple_of(first_key + j * KEY_TILE, EDGE)
            keys = [k_ref[pl.ds(at, KEY_TILE), cols] for cols in lanes]
            values_t = [v_ref[pl.ds(at, KEY_TILE), cols].T for cols in lanes]
            after = list(state)
            scores = dot(keys[0], queries[0], NT)
            late = None
            for h in range(2 * pairs):
                ahead = dot(keys[(h + 1) // 2], queries[h + 1], NT) if h + 1 < 2 * pairs else None
                expo = jnp.exp2(scores * to_base2 - tops[h] + bias_ref[j])
                after[2 * h] = state[2 * h] + fold(expo, jnp.sum)
                if late is not None:
                    after[2 * h - 1] = state[2 * h - 1] + late
                side = slice(h % 2 * HD, (h % 2 + 1) * HD)
                late = dot(values_t[h // 2][side], expo.astype(bf16))
                scores = ahead
            after[-1] = state[-1] + late
            return tuple(after)

        state = lax.fori_loop(0, trips, second_pass, tuple(state))
        low_at = pl.ds(pl.multiple_of(t * TILE, TILE), TILE)
        high_at = pl.ds(pl.multiple_of(HALF + t * TILE, TILE), TILE)
        for p, cols in enumerate(lanes):
            halves = []
            for head in range(2):
                h = 2 * p + head
                total = jnp.sum(state[2 * h], axis=0, keepdims=True)
                halves.append(state[2 * h + 1] / total)
                lse_ref[p, t, head : head + 1, :] = tops[h] + jnp.log2(total)
            pair = jnp.concatenate(halves, axis=0).T.astype(bf16)
            out_ref[low_at, cols] = pair[:TILE]
            out_ref[high_at, cols] = pair[TILE:]
        return 0

    lax.fori_loop(0, TILES, one_tile, 0)


def attend_forward(spans, clean_bounds, noisy_bounds, query, keys, values):
    count, cols = query.shape
    pairs = cols // LANES
    vmem = pl.BlockSpec(memory_space=pltpu.VMEM)
    work = pairs * 2 * 2 * HALF * TOK_DEV
    return pl.pallas_call(
        forward_kernel,
        in_specs=[pl.BlockSpec(memory_space=pltpu.SMEM)] + [vmem] * 5,
        out_specs=[vmem] * 2,
        out_shape=[
            jax.ShapeDtypeStruct((TOK_DEV, cols), bf16),
            jax.ShapeDtypeStruct((pairs, TILES, 2, 2 * TILE), f32),
        ],
        scratch_shapes=[
            pltpu.VMEM((NOISY_BASE // KEY_TILE + 1, KEY_TILE, 2 * TILE), f32),
            pltpu.VMEM((WINDOW, TILE), f32),
        ],
        name="attend_forward",
        cost_estimate=pl.CostEstimate(
            flops=4 * work * HD, bytes_accessed=8 * count * cols, transcendentals=work
        ),
    )(spans, clean_bounds, noisy_bounds, query, keys, values)


def backward_kernel(
    span_ref,
    clean_ref,
    noisy_ref,
    q_ref,
    k_ref,
    v_ref,
    o_ref,
    d_ref,
    lse_ref,
    cos_ref,
    sin_ref,
    rows_ref,
    out_ref,
    grad_ref,
    dk_ref,
    dv_ref,
    bias_ref,
):
    pairs = q_ref.shape[1] // LANES
    lanes = [slice(p * LANES, (p + 1) * LANES) for p in range(pairs)]
    dk_ref[...] = jnp.zeros_like(dk_ref)
    dv_ref[...] = jnp.zeros_like(dv_ref)
    out_ref[0] = jnp.zeros_like(out_ref[0])

    def one_tile(t, _):
        clean_at = pl.multiple_of(CLEAN_OWN + t * TILE, TILE)
        noisy_at = pl.multiple_of(NOISY_OWN + t * TILE, EDGE)
        window_at = pl.multiple_of(NOISY_BASE + t * TILE, EDGE)
        low_at = pl.multiple_of(t * TILE, TILE)
        high_at = pl.multiple_of(HALF + t * TILE, TILE)
        key_low, key_high = clean_ref[t, 0:1, :], clean_ref[t, 1:2, :]
        own_low, own_high = noisy_ref[t, 0:1, :], noisy_ref[t, 1:2, :]
        queries, d_outs, inners, lses = [], [], [], []
        for p, cols in enumerate(lanes):

            def both(ref, low, high):
                return jnp.concatenate(
                    [ref[pl.ds(low, TILE), cols], ref[pl.ds(high, TILE), cols]], axis=0
                )

            queries.append(split_heads(both(q_ref, noisy_at, clean_at)))
            d_rows = both(d_ref, low_at, high_at)
            o_rows = both(o_ref, low_at, high_at)
            product = (d_rows.astype(f32) * o_rows.astype(f32)).T
            d_outs.append(split_heads(d_rows))
            inners.append(
                [
                    jnp.sum(product[head * HD : (head + 1) * HD], axis=0, keepdims=True) * 0.125
                    for head in range(2)
                ]
            )
            lses.append([lse_ref[p, t, head : head + 1, :] for head in range(2)])

        def accumulate(at, rows, cols, allowed, d_query):
            bias_ref[:rows, :cols] = jnp.where(allowed, 0.0, neg_large)
            after = list(d_query)
            keys = [k_ref[pl.ds(at, rows), span] for span in lanes]
            eighth = [v_ref[pl.ds(at, rows), span] * jnp.asarray(0.125, bf16) for span in lanes]
            keys_t = [part.T for part in keys]
            stack = lambda parts: jnp.concatenate([part[:cols] for part in parts], axis=0)

            def begin(h):
                p, head = h // 2, h % 2
                return (
                    dot(keys[p], queries[p][head][:cols], NT),
                    dot(eighth[p], d_outs[p][head][:cols], NT),
                )

            def finish_pair(p, weights, d_scores):
                span = lanes[p]
                for head in range(2):
                    side = slice(head * HD, (head + 1) * HD)
                    h = 2 * p + head
                    after[h] = d_query[h] + dot(keys_t[p][side], d_scores[head])
                dv_ref[pl.ds(at, rows), span] += dot(
                    jnp.concatenate(weights, axis=1), stack(d_outs[p])
                )
                dk_ref[pl.ds(at, rows), span] += dot(
                    jnp.concatenate(d_scores, axis=1), stack(queries[p])
                )

            ready = begin(0)
            held = None
            weights, d_scores = [], []
            for h in range(2 * pairs):
                ahead = begin(h + 1) if h + 1 < 2 * pairs else None
                p, head = h // 2, h % 2
                scores = ready[0] * to_base2 - lses[p][head][:, :cols] + bias_ref[:rows, :cols]
                probs = jnp.exp2(scores)
                d_score = (probs * (ready[1] - inners[p][head][:, :cols])).astype(bf16)
                weights.append(probs.astype(bf16))
                d_scores.append(d_score)
                if held is not None:
                    finish_pair(*held)
                    held = None
                if head == 1:
                    held = (p, weights, d_scores)
                    weights, d_scores = [], []
                ready = ahead
            finish_pair(*held)
            return tuple(after)

        allowed = between((WINDOW, TILE), 0, own_low, own_high)
        zero = jnp.zeros((HD, TILE), f32)
        start = accumulate(window_at, WINDOW, TILE, allowed, (zero,) * (2 * pairs))
        start = tuple(jnp.concatenate([part, zero], axis=1) for part in start)
        first_key, trips = span_ref[t, 0], span_ref[t, 1]

        def one_step(j, d_query):
            at = pl.multiple_of(first_key + j * KEY_TILE, EDGE)
            allowed = between((KEY_TILE, 2 * TILE), at, key_low, key_high)
            return accumulate(at, KEY_TILE, 2 * TILE, allowed, d_query)

        d_query = lax.fori_loop(0, trips, one_step, start)
        for p, span in enumerate(lanes):
            pair = jnp.concatenate(d_query[2 * p : 2 * p + 2], axis=0).T
            for at, part in ((noisy_at, pair[:TILE]), (clean_at, pair[TILE:])):
                turned = turn(part, cos_ref[pl.ds(at, TILE), :], -sin_ref[pl.ds(at, TILE), :])
                out_ref[0, pl.ds(at, TILE), span] = turned.astype(bf16)
        return 0

    lax.fori_loop(0, TILES, one_tile, 0)
    step = KEY_ROWS // 9

    def finish(i, _):
        rows = pl.ds(pl.multiple_of(i * step, EDGE), step)
        for span in lanes:
            out_ref[1, rows, span] = turn(
                dk_ref[rows, span], cos_ref[rows, :], -sin_ref[rows, :]
            ).astype(bf16)
        out_ref[2, rows, :] = dv_ref[rows, :].astype(bf16)
        return 0

    lax.fori_loop(0, 9, finish, 0)

    def weight_rows(i, _):
        rows = pl.ds(pl.multiple_of(i * ROW_TILE, LANES), ROW_TILE)
        for c in range(3):
            grad_ref[c, rows, :] = dot(rows_ref[rows, :], out_ref[c]).astype(bf16)
        return 0

    lax.fori_loop(0, rows_ref.shape[0] // ROW_TILE, weight_rows, 0)


def attend_backward(
    spans,
    clean_bounds,
    noisy_bounds,
    query,
    keys,
    values,
    attended,
    d_attended,
    lse,
    cosine,
    sine,
    rows_t,
):
    count, cols = query.shape
    width = rows_t.shape[0]
    vmem = pl.BlockSpec(memory_space=pltpu.VMEM)
    return pl.pallas_call(
        backward_kernel,
        in_specs=[pl.BlockSpec(memory_space=pltpu.SMEM)] + [vmem] * 11,
        out_specs=[vmem] * 2,
        scratch_shapes=[
            pltpu.VMEM((count, cols), f32),
            pltpu.VMEM((count, cols), f32),
            pltpu.VMEM((max(KEY_TILE, WINDOW), 2 * TILE), f32),
        ],
        out_shape=[
            jax.ShapeDtypeStruct((3, count, cols), bf16),
            jax.ShapeDtypeStruct((3, width, cols), bf16),
        ],
        name="attend_backward",
        cost_estimate=pl.CostEstimate(
            flops=36 * 10**9, bytes_accessed=36 * 10**6, transcendentals=6 * 10**6
        ),
    )(
        spans,
        clean_bounds,
        noisy_bounds,
        query,
        keys,
        values,
        attended,
        d_attended,
        lse,
        cosine,
        sine,
        rows_t,
    )


PIECES = 16
MESH = pl.DeviceIdType.MESH


def flip(value, mask):
    result = value
    for b in range(mask.bit_length()):
        if mask >> b & 1:
            result = result + (1 << b) * (1 - 2 * ((value // (1 << b)) % 2))
    return result


class Exchange:
    names = ("a", "b", "c", "d", "e", "f", "g")

    def __init__(self, bits, count, rows, width):
        self.bits, self.count, self.rows, self.width = bits, count, rows, width
        self.half, self.quarter, self.piece = rows // 2, rows // 4, rows // PIECES
        self.extra = list(range(4, bits))

    def scratch(self):
        k, w = self.count, self.width
        shapes = [
            pltpu.VMEM((k, 2, self.half, w), bf16),
            pltpu.VMEM((k, self.half, w), bf16),
            pltpu.VMEM((k, self.half, w), bf16),
            pltpu.VMEM((k, self.quarter, w), bf16),
            pltpu.VMEM((k, self.quarter, w), bf16),
            pltpu.VMEM((k, self.quarter, w), f32),
            pltpu.VMEM((k, 3, self.piece, w), bf16),
            pltpu.VMEM((k, 3, self.piece, w), bf16),
        ]
        for lanes in (2, 1, 1, 3, 3, 1, 1):
            shapes += [pltpu.SemaphoreType.DMA((k, lanes))] * 2
        if self.extra:
            n = len(self.extra)
            shapes += [pltpu.VMEM((k, 2 * n, self.piece, w), bf16)]
            shapes += [pltpu.SemaphoreType.DMA((k, n))] * 2
        return shapes

    def bind(self, place, part, refs):
        (self.a_in, self.b_out, self.b_in, self.c_out, self.c_in, self.keep) = refs[:6]
        self.d_out, self.d_in = refs[6:8]
        self.sems = {
            name: (refs[8 + 2 * i], refs[9 + 2 * i]) for i, name in enumerate(self.names)
        }
        if self.extra:
            self.x_buf, self.x_send, self.x_recv = refs[22:25]
        self.place, self.part = place, part
        self.core, self.x, self.z = place % 2, (place // 2) % 2, (place // 4) % 4
        self.sibling = {"dp": flip(place, 1)}
        self.beside = {"dp": flip(place, 2)}
        self.across = {"mp": 1 - part}
        self.peers = [{"dp": flip(place, j << 2)} for j in range(1, 4)]
        self.partners = [self.sibling, self.beside, self.across] + self.peers
        self.partners += [{"dp": flip(place, 1 << b)} for b in self.extra]
        return self

    def greet(self):
        barrier = pltpu.get_barrier_semaphore()
        for partner in self.partners:
            pl.semaphore_signal(barrier, inc=1, device_id=partner, device_id_type=MESH)
        pl.semaphore_wait(barrier, len(self.partners))

    def copy(self, name, k, lane, source, target, device):
        out, into = self.sems[name]
        return pltpu.make_async_remote_copy(
            src_ref=source,
            dst_ref=target,
            send_sem=out.at[k, lane],
            recv_sem=into.at[k, lane],
            device_id=device,
            device_id_type=MESH,
        )

    def rows_at(self, start, size):
        return pl.ds(pl.multiple_of(start, PIECES), size)

    def copy_a(self, k, lane, grads):
        source = grads.at[k, self.rows_at((1 - self.core) * self.half, self.half)]
        return self.copy("a", k, lane, source, self.a_in.at[k, lane], self.sibling)

    def copy_b(self, k):
        return self.copy("b", k, 0, self.b_out.at[k], self.b_in.at[k], self.across)

    def copy_c(self, k):
        return self.copy("c", k, 0, self.c_out.at[k], self.c_in.at[k], self.beside)

    def copy_d(self, k, j):
        return self.copy("d", k, j, self.d_out.at[k, j], self.d_in.at[k, j], self.peers[j])

    def spot(self, change=0):
        start = self.core * self.half + self.x * self.quarter
        return self.rows_at(start + flip(self.z, change) * self.piece, self.piece)

    def copy_e(self, k, j, full):
        rows = full.at[k, self.spot()]
        return self.copy("e", k, j, rows, rows, self.peers[j])

    def copy_f(self, k, full):
        start = self.core * self.half + self.x * self.quarter
        rows = full.at[k, self.rows_at(start, self.quarter)]
        return self.copy("f", k, 0, rows, rows, self.beside)

    def copy_g(self, k, full):
        rows = full.at[k, self.rows_at(self.core * self.half, self.half)]
        return self.copy("g", k, 0, rows, rows, self.sibling)

    def start_a(self, k, lane, grads):
        self.copy_a(k, lane, grads).start()

    def stage_b(self, k, others):
        self.copy_a(k, 0, others).wait()
        mine = others[k, self.rows_at(self.core * self.half, self.half), :].astype(f32)
        self.b_out[k] = (mine + self.a_in[k, 0].astype(f32)).astype(bf16)
        self.copy_b(k).start()

    def stage_c(self, k, grads, crossed=True):
        self.copy_a(k, 1, grads).wait()
        if crossed:
            self.copy_b(k).wait()

        def total(which):
            inner = which * self.quarter
            rows = self.rows_at(inner, self.quarter)
            mine = grads[k, self.rows_at(self.core * self.half + inner, self.quarter), :]
            got = self.a_in[k, 1, rows, :].astype(f32)
            if crossed:
                got = got + self.b_in[k, rows, :].astype(f32)
            return mine.astype(f32) + got

        self.c_out[k] = total(1 - self.x).astype(bf16)
        self.copy_c(k).start()
        self.keep[k] = total(self.x)

    def stage_d(self, k):
        self.copy_c(k).wait()
        for j in range(4):
            rows = self.rows_at(flip(self.z, j) * self.piece, self.piece)
            total = self.keep[k, rows, :] + self.c_in[k, rows, :].astype(f32)
            if j:
                self.d_out[k, j - 1] = total.astype(bf16)
                self.copy_d(k, j - 1).start()
            else:
                self.keep[k, rows, :] = total

    def stage_e(self, k, full):
        rows = self.rows_at(self.z * self.piece, self.piece)
        total = self.keep[k, rows, :]
        for j in range(3):
            self.copy_d(k, j).wait()
            total = total + self.d_in[k, j].astype(f32)
        for i, b in enumerate(self.extra):
            mine = self.x_buf.at[k, 2 * i]
            mine[...] = total.astype(bf16)
            swap = pltpu.make_async_remote_copy(
                src_ref=mine,
                dst_ref=self.x_buf.at[k, 2 * i + 1],
                send_sem=self.x_send.at[k, i],
                recv_sem=self.x_recv.at[k, i],
                device_id={"dp": flip(self.place, 1 << b)},
                device_id_type=MESH,
            )
            swap.start()
            swap.wait()
            total = total.astype(bf16).astype(f32) + self.x_buf[k, 2 * i + 1].astype(f32)
        full[k, self.spot(), :] = total.astype(bf16)
        for j in range(3):
            self.copy_e(k, j, full).start()

    def stage_f(self, k, full):
        for j in range(3):
            self.copy_e(k, j, full).wait()
        self.copy_f(k, full).start()

    def stage_g(self, k, full):
        self.copy_f(k, full).wait()
        self.copy_g(k, full).start()

    def stage_h(self, k, full):
        self.copy_g(k, full).wait()


def at_step(step, count, action):
    @pl.when(jnp.logical_and(step >= 0, step < count))
    def _():
        action(step)


SPLIT = 4


def middle_kernel(exchange, tiles, *refs):
    (
        x_ref,
        att_ref,
        att2_ref,
        wout_ref,
        wout2_ref,
        dy_ref,
        vectors_ref,
        bup_ref,
        up_mine,
        up_here,
        up_beside,
        down_mine,
        down_here,
        down_beside,
        out_ref,
        mid_ref,
        datt_ref,
        datt2_ref,
        gout_ref,
        gout2_ref,
        gbup_ref,
        small_ref,
        gdown_ref,
        gup_ref,
        full_ref,
        up_there,
        down_there,
        pass_up,
        pass_down,
        up_buf,
        down_buf,
        load_sem,
        n2_ref,
        total_ref,
        dn2_ref,
        act_ref,
        dpre_ref,
        grad_ref,
        *rest,
    ) = refs
    place, part = lax.axis_index("dp"), lax.axis_index("mp")
    ex = exchange.bind(place, part, rest)
    core = ex.core
    count = tiles // 2
    rows_all = x_ref.shape[0]
    blocks = rows_all // ROW_TILE
    width = x_ref.shape[1]
    lanes = width // 2

    def which(i):
        other = jnp.logical_or(i == 0, jnp.logical_and(i % 2 == 1, i < tiles - 1))
        mine = jnp.where(i == tiles - 1, count - 1, i // 2 - 1)
        return other, jnp.where(other, (i + 1) // 2, mine)

    quarter = width // 4
    strip = HIDDEN_TILE // 2
    held = 2 * core + ex.x
    kept = 2 * core + 1 - ex.x

    def load_up(i, source, h):
        target = up_buf.at[i % 2, h * quarter : (h + 1) * quarter]
        return pltpu.make_async_copy(source, target, load_sem.at[i % 2, h])

    def load_down(i, source, h):
        target = down_buf.at[i % 2, h * strip : (h + 1) * strip]
        return pltpu.make_async_copy(source, target, load_sem.at[i % 2, 4 + h])

    def hand_up(k, part_of):
        cols = pl.ds(pl.multiple_of(k * HIDDEN_TILE, HIDDEN_TILE), HIDDEN_TILE)
        side = ex.x if part_of == 0 else 1 - ex.x
        rows = pl.ds(pl.multiple_of(side * quarter, EDGE), quarter)
        return pltpu.make_async_remote_copy(
            src_ref=(up_here, up_beside)[part_of].at[:, cols],
            dst_ref=up_there.at[k, rows],
            send_sem=pass_up.at[k, 2 * part_of],
            recv_sem=pass_up.at[k, 2 * part_of + 1],
            device_id=ex.sibling,
            device_id_type=MESH,
        )

    def hand_down(b, part_of):
        side = ex.x if part_of == 0 else 1 - ex.x
        return pltpu.make_async_remote_copy(
            src_ref=(down_here, down_beside)[part_of].at[strip_rows(b)],
            dst_ref=down_there.at[side * (count // 2) + b],
            send_sem=pass_down.at[side * (count // 2) + b, 0],
            recv_sem=pass_down.at[side * (count // 2) + b, 1],
            device_id=ex.sibling,
            device_id_type=MESH,
        )

    def strip_rows(b):
        return pl.ds(pl.multiple_of(b * strip, strip), strip)

    def got_down(slot):
        return pltpu.make_async_remote_copy(
            src_ref=down_there.at[slot],
            dst_ref=down_there.at[slot],
            send_sem=pass_down.at[slot, 0],
            recv_sem=pass_down.at[slot, 1],
            device_id=ex.sibling,
            device_id_type=MESH,
        )

    def start_loads(i):
        other, k = which(i)
        mine = jnp.logical_not(other)
        cols = pl.ds(pl.multiple_of(k * HIDDEN_TILE, HIDDEN_TILE), HIDDEN_TILE)
        span = count // 2

        @pl.when(other)
        def _():
            hand_up(k, 0).wait()
            hand_up(k, 1).wait()

        for h in range(4):

            @pl.when(mine)
            def _():
                load_up(i, up_mine.at[h * quarter : (h + 1) * quarter, cols], h).start()

            @pl.when(jnp.logical_and(other, held == h))
            def _():
                load_up(i, up_here.at[:, cols], h).start()

            @pl.when(jnp.logical_and(other, kept == h))
            def _():
                load_up(i, up_beside.at[:, cols], h).start()

            @pl.when(jnp.logical_and(other, core != h // 2))
            def _():
                rows = slice(h % 2 * quarter, (h % 2 + 1) * quarter)
                load_up(i, up_there.at[k, rows], h).start()

        for h in range(2):
            b = 2 * k + h
            piece, inner = b // span, b % span

            @pl.when(mine)
            def _():
                load_down(i, down_mine.at[strip_rows(b), :], h).start()

            @pl.when(jnp.logical_and(other, held == piece))
            def _():
                load_down(i, down_here.at[strip_rows(inner), :], h).start()

            @pl.when(jnp.logical_and(other, kept == piece))
            def _():
                load_down(i, down_beside.at[strip_rows(inner), :], h).start()

            @pl.when(jnp.logical_and(other, core != piece // 2))
            def _():
                slot = piece % 2 * span + inner
                got_down(slot).wait_recv()
                load_down(i, down_there.at[slot], h).start()

    def wait_loads(i):
        for h in range(4):
            load_up(i, up_mine.at[:quarter, :HIDDEN_TILE], h).wait()
        for h in range(2):
            load_down(i, down_mine.at[:strip, :], h).wait()

    ex.greet()

    def hand(k, _):
        hand_up(k, 0).start()
        hand_up(k, 1).start()

        @pl.when(k < count // 2)
        def _():
            hand_down(k, 0).start()
            hand_down(k, 1).start()

        return 0

    lax.fori_loop(0, count, hand, 0)

    def prologue(r, _):
        rows = pl.ds(pl.multiple_of(r * ROW_TILE, ROW_TILE), ROW_TILE)
        branch = dot(att_ref[rows, :], wout_ref[...]) + dot(att2_ref[rows, :], wout2_ref[...])
        mid = x_ref[rows, :].astype(f32) + branch
        mid_ref[rows, :] = mid
        unit = normal(mid)[0]
        n2_ref[rows, :] = (unit * vectors_ref[2:3, :] + vectors_ref[3:4, :]).astype(bf16)
        total_ref[rows, :] = mid + vectors_ref[4:5, :]
        dn2_ref[rows, :] = jnp.zeros((ROW_TILE, width), f32)
        return 0

    lax.fori_loop(0, blocks, prologue, 0)
    start_loads(0)

    def tile(i):
        other, k = which(i)
        slot = i % 2
        wait_loads(i)

        @pl.when(i + 1 < tiles)
        def _():
            start_loads(i + 1)

        up, down = up_buf.at[slot], down_buf.at[slot]
        bias_at = jnp.where(other, k, count + k)
        bias_grad = jnp.zeros((1, HIDDEN_TILE), f32)
        block = lambda r: slice(r * ROW_TILE, (r + 1) * ROW_TILE)

        def begin(r):
            return dot(n2_ref[block(r), :], up[...]), dot(dy_ref[block(r), :], down[...], NT)

        ready = begin(0)
        for r in range(blocks):
            rows = block(r)
            ahead = begin(r + 1) if r + 1 < blocks else None
            pre = ready[0] + bup_ref[bias_at]
            square = pre * pre
            bend = jnp.tanh(0.7978845608028654 * (pre + 0.044715 * square * pre))
            part_one = 0.5 * (1.0 + bend)
            act = (pre * part_one).astype(bf16)
            slope = part_one + (0.5 * pre) * (1.0 - bend * bend) * (
                0.7978845608028654 * (1.0 + 3.0 * 0.044715 * square)
            )
            d_pre = (ready[1] * slope).astype(bf16)
            act_ref[rows, :] = act
            dpre_ref[rows, :] = d_pre
            bias_grad = bias_grad + jnp.sum(d_pre.astype(f32), axis=0, keepdims=True)
            total_ref[rows, :] += dot(act, down[...])
            dn2_ref[rows, :] += dot(d_pre, up[...], NT)
            ready = ahead
        gbup_ref[bias_at] = bias_grad
        grads = (
            dot(act_ref[...].T, dy_ref[...]).astype(bf16),
            dot(dpre_ref[...].T, n2_ref[...]).astype(bf16),
        )
        for c in range(SPLIT):
            cols = slice(c % 2 * lanes, (c % 2 + 1) * lanes)
            grad_ref[k * SPLIT + c] = grads[c // 2][:, cols]

        @pl.when(other)
        def _():
            for c in range(SPLIT):
                ex.start_a(k * SPLIT + c, 0, grad_ref)

        @pl.when(jnp.logical_not(other))
        def _():
            for c in range(SPLIT):
                ex.start_a(k * SPLIT + c, 1, grad_ref)

    def group(k, when, action):
        @pl.when(jnp.logical_and(when, jnp.logical_and(k >= 0, k < count)))
        def _():
            lax.fori_loop(0, SPLIT, lambda c, _: (action(k * SPLIT + c), 0)[1], 0)

    def arrive(c):
        ex.stage_h(c, full_ref)
        k, lane = c // SPLIT, c % SPLIT
        hidden = pl.ds(pl.multiple_of(k * HIDDEN_TILE, HIDDEN_TILE), HIDDEN_TILE)
        cols = pl.ds(pl.multiple_of(lane % 2 * lanes, LANES), lanes)

        @pl.when(lane < 2)
        def _():
            gdown_ref[hidden, cols] = full_ref[c]

        @pl.when(lane >= 2)
        def _():
            gup_ref[cols, hidden] = full_ref[c].T

    def steps(i):
        even = i % 2 == 0
        odd = jnp.logical_not(even)
        group((i - 9) // 2, odd, arrive)
        group((i - 8) // 2, even, lambda k: ex.stage_g(k, full_ref))
        group((i - 7) // 2, odd, lambda k: ex.stage_f(k, full_ref))
        group((i - 6) // 2, even, lambda k: ex.stage_e(k, full_ref))
        group((i - 5) // 2, odd, lambda k: ex.stage_d(k))
        group((i - 4) // 2, even, lambda k: ex.stage_c(k, grad_ref))
        crossing = jnp.logical_or(i == 1, jnp.logical_and(even, i >= 2))
        group(i // 2, crossing, lambda k: ex.stage_b(k, grad_ref))

    def tick(d):
        total = count * SPLIT

        def due(c, least, action):
            @pl.when(jnp.logical_and(c >= least, c < total))
            def _():
                action(c)

        done = [
            (tiles + 1 - lag) // 2 * SPLIT if lag % 2 == 0 else (tiles - lag + 1) // 2 * SPLIT
            for lag in (9, 8, 7, 6, 5, 4)
        ]
        first = done[5]
        due(first - 10 + d, done[0], arrive)
        due(first - 8 + d, done[1], lambda c: ex.stage_g(c, full_ref))
        due(first - 6 + d, done[2], lambda c: ex.stage_f(c, full_ref))
        due(first - 4 + d, done[3], lambda c: ex.stage_e(c, full_ref))
        due(first - 2 + d, done[4], lambda c: ex.stage_d(c))
        due(first + d, done[5], lambda c: ex.stage_c(c, grad_ref))

    def main(i, _):
        tile(i)
        steps(i)
        return 0

    lax.fori_loop(0, tiles, main, 0)

    def handed(slot, _):
        got_down(slot).wait_send()
        return 0

    lax.fori_loop(0, count, handed, 0)

    def epilogue(r, sums):
        rows = pl.ds(pl.multiple_of(r * ROW_TILE, ROW_TILE), ROW_TILE)
        out_ref[rows, :] = total_ref[rows, :].astype(bf16)
        unit, scale = normal(mid_ref[rows, :])
        d_rows = dn2_ref[rows, :]
        dy = dy_ref[rows, :].astype(f32)
        lean = d_rows * vectors_ref[2:3, :]
        d_mid = dy + scale * (
            lean
            - jnp.mean(lean, axis=-1, keepdims=True)
            - unit * jnp.mean(lean * unit, axis=-1, keepdims=True)
        )
        mid_ref[rows, :] = d_mid
        d_branch = d_mid.astype(bf16)
        n2_ref[rows, :] = d_branch
        datt_ref[rows, :] = dot(d_branch, wout_ref[...], NT).astype(bf16)
        datt2_ref[rows, :] = dot(d_branch, wout2_ref[...], NT).astype(bf16)
        add = lambda values: jnp.sum(values, axis=0, keepdims=True)
        sums = (sums[0] + add(d_rows * unit), sums[1] + add(d_rows), sums[2] + add(dy))
        tick(2 * r)
        tick(2 * r + 1)
        return sums

    zero = jnp.zeros((1, width), f32)
    sums = lax.fori_loop(0, blocks, epilogue, (zero, zero, zero))
    for j in range(3):
        small_ref[j : j + 1, :] = sums[j]
    depth = wout_ref.shape[0]
    for source, target in ((att_ref, gout_ref), (att2_ref, gout2_ref)):
        grad = dot(source[...].T, n2_ref[...]).astype(bf16)
        target[:depth, :] = grad[:, :lanes]
        target[depth:, :] = grad[:, lanes:]

    def drain(d, _):
        tick(d)
        return 0

    lax.fori_loop(2 * blocks, 2 * SPLIT + 10, drain, 0)


def middle(bits, x, att, att2, wout, wout2, dy, vectors, bup, ups, downs):
    rows, width = x.shape
    hidden = ups[0].shape[1]
    count = hidden // HIDDEN_TILE
    tiles = 2 * count
    exchange = Exchange(bits, count * SPLIT, HIDDEN_TILE, width // 2)
    vmem = pl.BlockSpec(memory_space=pltpu.VMEM)
    hbm = pl.BlockSpec(memory_space=pl.ANY)
    shape = jax.ShapeDtypeStruct
    depth = wout.shape[0]
    return pl.pallas_call(
        functools.partial(middle_kernel, exchange, tiles),
        in_specs=[vmem] * 8 + [hbm] * 6,
        out_specs=[vmem] * 10,
        out_shape=[
            shape((rows, width), bf16),
            shape((rows, width), f32),
            shape(att.shape, bf16),
            shape(att2.shape, bf16),
            shape((2 * depth, width // 2), bf16),
            shape((2 * depth, width // 2), bf16),
            shape((tiles, 1, HIDDEN_TILE), f32),
            shape((8, width), f32),
            shape((hidden, width), bf16),
            shape((width, hidden), bf16),
        ],
        scratch_shapes=[
            pltpu.VMEM((count * SPLIT, HIDDEN_TILE, width // 2), bf16),
            pltpu.VMEM((count, width // 2, HIDDEN_TILE), bf16),
            pltpu.VMEM((count, HIDDEN_TILE // 2, width), bf16),
            pltpu.SemaphoreType.DMA((count, 4)),
            pltpu.SemaphoreType.DMA((count, 2)),
            pltpu.VMEM((2, width, HIDDEN_TILE), bf16),
            pltpu.VMEM((2, HIDDEN_TILE, width), bf16),
            pltpu.SemaphoreType.DMA((2, 6)),
            pltpu.VMEM((rows, width), bf16),
            pltpu.VMEM((rows, width), f32),
            pltpu.VMEM((rows, width), f32),
            pltpu.VMEM((rows, HIDDEN_TILE), bf16),
            pltpu.VMEM((rows, HIDDEN_TILE), bf16),
            pltpu.VMEM((count * SPLIT, HIDDEN_TILE, width // 2), bf16),
        ]
        + exchange.scratch(),
        compiler_params=pltpu.CompilerParams(
            collective_id=0, has_side_effects=True, vmem_limit_bytes=67043328
        ),
        name="middle",
        cost_estimate=pl.CostEstimate(
            flops=60 * 10**9, bytes_accessed=40 * 10**6, transcendentals=4 * 10**6
        ),
    )(x, att, att2, wout, wout2, dy, vectors, bup, *ups, *downs)


def leave_kernel(exchange, *refs):
    (
        mine_ref,
        mine_out_ref,
        crossed_ref,
        crossed_out_ref,
        d_ref,
        d2_ref,
        w_ref,
        w2_ref,
        tokens_ref,
        vectors_ref,
        dmid_ref,
        small_ref,
        small2_ref,
        full_ref,
        back_ref,
        sums_ref,
        sum_buf,
        rows_ref,
        give_ref,
        take_ref,
        swap_sem,
        near_ref,
        far_ref,
        near_sem,
        far_sem,
        *rest,
    ) = refs
    place, part = lax.axis_index("dp"), lax.axis_index("mp")
    ex = exchange.bind(place, part, rest)
    count, bits = ex.count, ex.bits
    first = mine_ref.shape[0]
    near_id = part * 4 + place % 4
    near = [
        {"dp": flip(place, j % 4), "mp": part if j < 4 else 1 - part} for j in range(1, 8)
    ]
    ex.partners += [near[j - 1] for j in (3, 5, 6, 7)]
    ex.greet()

    def begin(k, _):
        total = mine_ref[k].astype(f32) + crossed_ref[k].astype(f32)
        sum_buf[k] = total.astype(bf16)
        ex.start_a(k, 1, sum_buf)
        return 0

    lax.fori_loop(0, first, begin, 0)

    def begin_out(k, _):
        total = mine_out_ref[k].astype(f32) + crossed_out_ref[k].astype(f32)
        sum_buf[first + k] = total.astype(bf16)
        ex.start_a(first + k, 1, sum_buf)
        return 0

    lax.fori_loop(0, count - first, begin_out, 0)

    def back_of(rows):
        total = 0.0
        for grads, weights in ((d_ref, w_ref), (d2_ref, w2_ref)):
            for c in range(3):
                total = total + dot(grads[c, rows, :], weights[c], NT)
        return total

    def steps(i):
        at_step(i - 10, count, lambda k: ex.stage_h(k, full_ref))
        at_step(i - 8, count, lambda k: ex.stage_g(k, full_ref))
        at_step(i - 6, count, lambda k: ex.stage_f(k, full_ref))
        at_step(i - 4, count, lambda k: ex.stage_e(k, full_ref))
        at_step(i - 2, count, lambda k: ex.stage_d(k))
        at_step(i, count, lambda k: ex.stage_c(k, sum_buf, False))

    def many(low, high):
        lax.fori_loop(low, high, lambda i, _: (steps(i), 0)[1], 0)

    tail = back_of(slice(2 * HALF, KEY_ROWS))
    own = NOISY_OWN - 2 * HALF
    rows_ref[:HALF, :] = tail[own : own + HALF]
    give_ref[HALF:, :] = (tail[EDGE:own] + tail[own + HALF :]).astype(bf16)
    rows_ref[HALF : HALF + EDGE, :] = tail[:EDGE]
    many(0, 3)
    given = back_of(slice(0, HALF))
    give_ref[EDGE:HALF, :] = given[EDGE:].astype(bf16)
    give_ref[:EDGE, :] = (given[:EDGE] + rows_ref[HALF : HALF + EDGE, :]).astype(bf16)
    swap = pltpu.make_async_remote_copy(
        src_ref=give_ref,
        dst_ref=take_ref,
        send_sem=swap_sem.at[0],
        recv_sem=swap_sem.at[1],
        device_id=ex.across,
        device_id_type=MESH,
    )
    swap.start()
    many(3, 6)
    rows_ref[HALF:, :] = back_of(slice(CLEAN_OWN, CLEAN_OWN + HALF))
    many(6, 10)
    swap.wait()
    rows_ref[HALF:, :] += take_ref[:HALF, :].astype(f32)
    edge = pl.ds(pl.multiple_of((1 - part) * (HALF - EDGE), EDGE), EDGE)
    rows_ref[edge, :] += take_ref[HALF:, :].astype(f32)

    def norm_back(b, sums):
        rows = pl.ds(pl.multiple_of(b * ROW_TILE, TILE), ROW_TILE)
        unit, scale = normal(tokens_ref[rows, :].astype(f32))
        d_rows = rows_ref[rows, :]
        lean = d_rows * vectors_ref[0:1, :]
        back_ref[rows, :] = dmid_ref[rows, :] + scale * (
            lean
            - jnp.mean(lean, axis=-1, keepdims=True)
            - unit * jnp.mean(lean * unit, axis=-1, keepdims=True)
        )
        add = lambda values: jnp.sum(values, axis=0, keepdims=True)
        steps(10 + b)
        return (sums[0] + add(d_rows * unit), sums[1] + add(d_rows))

    width = tokens_ref.shape[1]
    parts = tokens_ref.shape[0] // ROW_TILE
    zero = jnp.zeros((1, width), f32)
    sums = lax.fori_loop(0, parts, norm_back, (zero, zero))
    lead = small_ref.shape[0] - 2
    bias = lead - 3
    mine = near_ref.at[near_id]
    mine[:lead, :] = small_ref[:lead, :]
    for j in range(2):
        mine[lead + j : lead + j + 1, :] = sums[j]
    mine[lead + 2 : lead + 2 + bias, :] = small2_ref[:bias, :]
    rest_rows = 16 - lead - 2 - bias
    mine[16 - rest_rows :, :] = jnp.zeros((rest_rows, width), f32)

    def near_copy(j):
        return pltpu.make_async_remote_copy(
            src_ref=near_ref.at[near_id],
            dst_ref=near_ref.at[near_id],
            send_sem=near_sem.at[j, 0],
            recv_sem=near_sem.at[j, 1],
            device_id=near[j - 1],
            device_id_type=MESH,
        )

    def near_got(j):
        came = (part + j // 4) % 2 * 4 + flip(place % 4, j % 4)
        return pltpu.make_async_remote_copy(
            src_ref=near_ref.at[came],
            dst_ref=near_ref.at[came],
            send_sem=near_sem.at[j, 0],
            recv_sem=near_sem.at[j, 1],
            device_id=near[j - 1],
            device_id_type=MESH,
        )

    for j in range(1, 8):
        near_copy(j).start()
    many(10 + parts, 13 + parts)
    for j in range(1, 8):
        near_copy(j).wait_send()
        near_got(j).wait_recv()
    total = near_ref[0]
    for j in range(1, 8):
        total = total + near_ref[j]
    plane = near_ref[part * 4]
    other = near_ref[(1 - part) * 4]
    for j in range(1, 4):
        plane = plane + near_ref[part * 4 + j]
        other = other + near_ref[(1 - part) * 4 + j]
    spot = far_ref.at[ex.z]
    spot[...] = total
    spot[:bias, :] = plane[:bias] + other[lead + 2 : lead + 2 + bias]

    def far_copy(j, at):
        return pltpu.make_async_remote_copy(
            src_ref=far_ref.at[at],
            dst_ref=far_ref.at[at],
            send_sem=far_sem.at[j, 0],
            recv_sem=far_sem.at[j, 1],
            device_id=ex.peers[j - 1],
            device_id_type=MESH,
        )

    for j in range(1, 4):
        far_copy(j, ex.z).start()
    many(13 + parts, 16 + parts)
    for j in range(1, 4):
        far_copy(j, ex.z).wait_send()
        far_copy(j, flip(ex.z, j)).wait_recv()
    total = far_ref[0]
    for j in range(1, 4):
        total = total + far_ref[j]
    for i, b in enumerate(ex.extra):
        far_ref[4 + 2 * i] = total
        trade = pltpu.make_async_remote_copy(
            src_ref=far_ref.at[4 + 2 * i],
            dst_ref=far_ref.at[5 + 2 * i],
            send_sem=far_sem.at[4 + i, 0],
            recv_sem=far_sem.at[4 + i, 1],
            device_id={"dp": flip(place, 1 << b)},
            device_id_type=MESH,
        )
        trade.start()
        trade.wait()
        total = total + far_ref[5 + 2 * i]
    sums_ref[...] = total
    many(16 + parts, count + 10)


def leave(bits, mine, crossed, d_fields, weights, tokens, vectors, d_mid, small, small2):
    total = mine[0].shape[0] + mine[1].shape[0]
    rows, cols = mine[0].shape[1:]
    exchange = Exchange(bits, total, rows, cols)
    count, width = tokens.shape
    vmem = pl.BlockSpec(memory_space=pltpu.VMEM)
    shape = jax.ShapeDtypeStruct
    return pl.pallas_call(
        functools.partial(leave_kernel, exchange),
        in_specs=[vmem] * 13,
        out_specs=[vmem] * 3,
        out_shape=[
            shape((total, rows, cols), bf16),
            shape((count, width), f32),
            shape((16, width), f32),
        ],
        scratch_shapes=[
            pltpu.VMEM((total, rows, cols), bf16),
            pltpu.VMEM((count, width), f32),
            pltpu.VMEM((HALF + EDGE, width), bf16),
            pltpu.VMEM((HALF + EDGE, width), bf16),
            pltpu.SemaphoreType.DMA((2,)),
            pltpu.VMEM((8, 16, width), f32),
            pltpu.VMEM((4 + 2 * len(exchange.extra), 16, width), f32),
            pltpu.SemaphoreType.DMA((8, 2)),
            pltpu.SemaphoreType.DMA((4 + len(exchange.extra), 2)),
        ]
        + exchange.scratch(),
        compiler_params=pltpu.CompilerParams(
            collective_id=1, has_side_effects=True, vmem_limit_bytes=67043328
        ),
        name="leave",
        cost_estimate=pl.CostEstimate(
            flops=40 * 10**9, bytes_accessed=40 * 10**6, transcendentals=0
        ),
    )(*mine, *crossed, *d_fields, *weights, tokens, vectors, d_mid, small, small2)


def key_layout(seq_lengths, block_len, part):
    index = jnp.arange(KEY_ROWS, dtype=jnp.int32)
    own = part * HALF
    token = jnp.where(
        index < NOISY_BASE, index + (own - HALF), index - NOISY_BASE + (own - EDGE)
    )
    ends = jnp.cumsum(seq_lengths)
    passed = token[:, None] >= ends[None, :]
    starts = jnp.sum(jnp.where(passed, seq_lengths[None, :], 0), axis=1)
    lengths_here = jnp.where(passed, 0, ends[None, :])
    stops = jnp.min(jnp.where(passed, TOK_DEV, lengths_here), axis=1)
    positions = token - starts
    block_start = starts + positions // block_len * block_len
    block_stop = jnp.minimum(block_start + block_len, stops)
    mine = slice(CLEAN_OWN, CLEAN_OWN + HALF)
    low, start, stop = starts[mine], block_start[mine], block_stop[mine]
    to_clean = own - HALF
    tiles = lambda column: column.reshape(TILES, 1, TILE)
    clean_bounds = jnp.concatenate(
        [
            jnp.concatenate([tiles(low - to_clean), tiles(low - to_clean)], axis=2),
            jnp.concatenate([tiles(start - to_clean), tiles(stop - to_clean)], axis=2),
        ],
        axis=1,
    )
    to_window = own - EDGE + TILE * jnp.arange(TILES, dtype=jnp.int32)[:, None, None]
    noisy_bounds = jnp.concatenate(
        [tiles(start) - to_window, tiles(stop) - to_window], axis=1
    )
    first = jnp.min(clean_bounds[:, 0], axis=1) // EDGE * EDGE
    last = jnp.max(clean_bounds[:, 1], axis=1)
    trips = (last - first + KEY_TILE - 1) // KEY_TILE
    spans = jnp.stack([first, trips], axis=1)
    lane = jnp.arange(LANES, dtype=jnp.int32)
    frequency = jnp.exp(
        (lane % (HD // 2)).astype(f32) * (-math.log(10000.0) / (HD // 2))
    )
    angles = positions.astype(f32)[:, None] * frequency[None, :]
    sign = jnp.where(lane % HD < HD // 2, -1.0, 1.0)
    return spans, clean_bounds, noisy_bounds, jnp.cos(angles), jnp.sin(angles) * sign


def in_order(bit, mine, theirs, axis=0):
    order = bit == 0
    return jnp.concatenate(
        [jnp.where(order, mine, theirs), jnp.where(order, theirs, mine)], axis=axis
    )


def tie(first, second):
    return lax.optimization_barrier((first, second))


def local(
    dp_size,
    tokens,
    lengths,
    block_size,
    cotangent,
    ln1_gain,
    ln1_bias,
    w_qkv,
    w_out,
    ln2_gain,
    ln2_bias,
    w_up,
    b_up,
    w_down,
    b_down,
):
    width = tokens.shape[2]
    part = lax.axis_index("mp")
    place = lax.axis_index("dp")
    bits = dp_size.bit_length() - 1
    core = place & 1

    def across(array):
        return lax.ppermute(array, "mp", [(0, 1), (1, 0)])

    def sibling(array):
        return lax.ppermute(array, "dp", [(i, i ^ 1) for i in range(dp_size)])

    def beside(array):
        return lax.ppermute(array, "dp", [(i, i ^ 2) for i in range(dp_size)])

    edge = jnp.where(part == 0, tokens[0, HALF - EDGE :], tokens[0, :EDGE])
    context = across(jnp.concatenate([tokens[1], edge], axis=0))
    qkv_mine = w_qkv.transpose(1, 0, 2)
    side = (place >> 1) & 1

    def quarter_of(array, axis=0):
        size = array.shape[axis] // 4
        return lax.dynamic_slice_in_dim(array, (2 * core + side) * size, size, axis)

    quarters = [
        quarter_of(qkv_mine, 1),
        quarter_of(w_up),
        quarter_of(w_down),
        quarter_of(w_out),
    ]
    layout = key_layout(lengths[0], block_size[0], part)
    vectors = jnp.stack([ln1_gain, ln1_bias, ln2_gain, ln2_bias, b_down])
    context, (quarters, layout, vectors) = tie(context, (quarters, layout, vectors))
    qkv_here, up_here, down_here, out_here = [across(piece) for piece in quarters]
    bias_other = across(b_up)

    spans, clean_bounds, noisy_bounds, cosine, sine = layout
    normed1, normed1_t, *fields = enter(tokens, context, vectors, qkv_mine, cosine, sine)
    qkv_here, fields = tie(qkv_here, fields)
    qkv_beside = beside(qkv_here)
    mine = [*fields, *attend_forward(spans, clean_bounds, noisy_bounds, *fields)]
    (qkv_here, qkv_beside, up_here), _ = tie((qkv_here, qkv_beside, up_here), mine[3])
    qkv_half = in_order(side, qkv_here, qkv_beside, axis=1)
    qkv_other = in_order(core, qkv_half, sibling(qkv_half), axis=1)
    up_beside = beside(up_here)
    fields = project(normed1, qkv_other, cosine, sine)
    (down_here, out_here), fields = tie((down_here, out_here), fields)
    out_beside = beside(out_here)
    down_beside = beside(down_here)
    other = [*fields, *attend_forward(spans, clean_bounds, noisy_bounds, *fields)]
    (out_here, out_beside, up_here, up_beside, down_here, down_beside, bias_other), _ = tie(
        (out_here, out_beside, up_here, up_beside, down_here, down_beside, bias_other), other[3]
    )
    out_half = in_order(side, out_here, out_beside)
    out_other = in_order(core, out_half, sibling(out_half))
    bias_all = jnp.concatenate([bias_other, b_up]).astype(f32).reshape(-1, 1, HIDDEN_TILE)

    x_rows = tokens.reshape(TOK_DEV, width)
    out, d_mid, d_att, d_att2, grad_out, grad_out2, grad_bias, norms, grad_down, grad_up = middle(
        bits,
        x_rows,
        mine[3],
        other[3],
        w_out,
        out_other,
        cotangent.reshape(TOK_DEV, width),
        vectors,
        bias_all,
        (w_up, up_here, up_beside),
        (w_down, down_here, down_beside),
    )
    hidden = b_up.shape[0]

    d_qkv, grad_qkv = [], []
    for saved, d_attended in ((other, d_att2), (mine, d_att)):
        query, keys, values, attended, lse = saved
        d_fields, grad = attend_backward(
            spans,
            clean_bounds,
            noisy_bounds,
            query,
            keys,
            values,
            attended,
            d_attended,
            lse,
            cosine,
            sine,
            normed1_t,
        )
        spans = tie(spans, grad)[0]
        d_qkv.append(d_fields)
        grad_qkv.append(grad.reshape(-1, ROW_TILE, grad.shape[2]))
    crossed_out = across(grad_out2)
    crossed = across(grad_qkv[0])
    lead = hidden // width
    bias2, bias1 = grad_bias.reshape(2, lead, width)
    shared = jnp.concatenate([norms[:3], jnp.zeros((2, width), f32)], axis=0)
    full, grad_tokens, sums = leave(
        bits,
        (grad_qkv[1], grad_out.reshape(-1, ROW_TILE, grad_out.shape[1])),
        (crossed, crossed_out.reshape(-1, ROW_TILE, grad_out.shape[1])),
        (d_qkv[1], d_qkv[0]),
        (qkv_mine, qkv_other),
        x_rows,
        vectors,
        d_mid,
        jnp.concatenate([bias1, shared], axis=0),
        jnp.concatenate([bias2, shared], axis=0),
    )
    split = 3 * width // ROW_TILE
    grad_qkv = full[:split].reshape(qkv_mine.shape).transpose(1, 0, 2).astype(f32)
    flat = full[split:].reshape(2, w_out.shape[0], width // 2)
    grad_out = jnp.concatenate([flat[0], flat[1]], axis=1).astype(f32)
    return (
        out.reshape(tokens.shape),
        grad_tokens.reshape(tokens.shape),
        sums[lead + 3],
        sums[lead + 4],
        grad_qkv,
        grad_out,
        sums[lead],
        sums[lead + 1],
        grad_up.astype(f32),
        sums[:lead].reshape(hidden),
        grad_down.astype(f32),
        sums[lead + 2],
    )


def solution(mesh):
    in_specs = (
        P(None, ("dp", "mp"), None),
        P("dp", None),
        P(),
        P(None, ("dp", "mp"), None),
        P(),
        P(),
        P(None, None, "mp"),
        P("mp", None),
        P(),
        P(),
        P(None, "mp"),
        P("mp"),
        P("mp", None),
        P(),
    )
    out_specs = (
        P(None, ("dp", "mp"), None),
        P(None, ("dp", "mp"), None),
        P(),
        P(),
        P(None, None, "mp"),
        P("mp", None),
        P(),
        P(),
        P(None, "mp"),
        P("mp"),
        P("mp", None),
        P(),
    )
    return jax.shard_map(
        functools.partial(local, mesh.shape["dp"]),
        mesh=mesh,
        in_specs=in_specs,
        out_specs=out_specs,
        check_vma=False,
    )
```

```python
import functools
import math

import jax
import jax.numpy as jnp
from jax import lax
from jax.experimental import pallas as pl
from jax.experimental.pallas import tpu as pltpu
from jax.sharding import PartitionSpec as P

HD = 64
TOK_DEV = 1024
HALF = TOK_DEV // 2
EDGE = 16
CLEAN_OWN = HALF
NOISY_BASE = 2 * HALF + EDGE
NOISY_OWN = NOISY_BASE + EDGE
KEY_ROWS = NOISY_OWN + HALF + EDGE
TILE = 128
TILES = HALF // TILE
WINDOW = TILE + 2 * EDGE
KEY_TILE = 192
LANES = 128
HIDDEN_TILE = 256
ROW_TILE = 256

epsilon = 1e-05
neg_large = -1e30
to_base2 = 0.125 * math.log2(math.e)
f32 = jnp.float32
bf16 = jnp.bfloat16

NN = (((1,), (0,)), ((), ()))
NT = (((1,), (1,)), ((), ()))


def dot(left, right, dims=NN):
    return lax.dot_general(left, right, dims, preferred_element_type=f32)


def low_lanes(shape):
    return lax.broadcasted_iota(jnp.int32, shape, 1) < HD


def turn(values, cosine, sine):
    lane = lax.broadcasted_iota(jnp.int32, values.shape, 1)
    first_half = (lane & (HD - 1)) < HD // 2
    swapped = jnp.where(
        first_half,
        pltpu.roll(values, LANES - HD // 2, 1),
        pltpu.roll(values, HD // 2, 1),
    )
    return values * cosine + swapped * sine


def project_rows(rows, w_ref, cosine, sine, q_ref, k_ref, v_ref, at):
    for part, out_ref in ((0, q_ref), (1, k_ref)):
        field = dot(rows, w_ref[part])
        for pair in range(field.shape[1] // LANES):
            cols = slice(pair * LANES, (pair + 1) * LANES)
            out_ref[at, cols] = turn(field[:, cols], cosine, sine).astype(bf16)
    v_ref[at, :] = dot(rows, w_ref[2]).astype(bf16)


def project_kernel(rows_ref, w_ref, cos_ref, sin_ref, q_ref, k_ref, v_ref):
    at = slice(0, rows_ref.shape[0])
    project_rows(rows_ref[...], w_ref, cos_ref[...], sin_ref[...], q_ref, k_ref, v_ref, at)


def project(rows, weights, cosine, sine):
    count, width = rows.shape
    cols = weights.shape[2]
    step = count // 3
    row_spec = pl.BlockSpec((step, width), lambda i: (i, 0))
    table_spec = pl.BlockSpec((step, LANES), lambda i: (i, 0))
    out_spec = pl.BlockSpec((step, cols), lambda i: (i, 0))
    shape = jax.ShapeDtypeStruct((count, cols), bf16)
    return pl.pallas_call(
        project_kernel,
        grid=(3,),
        in_specs=[
            row_spec,
            pl.BlockSpec(weights.shape, lambda i: (0, 0, 0)),
            table_spec,
            table_spec,
        ],
        out_specs=[out_spec] * 3,
        out_shape=[shape] * 3,
        name="project",
        cost_estimate=pl.CostEstimate(
            flops=2 * count * width * 3 * cols,
            bytes_accessed=2 * (count * (width + 3 * cols) + 3 * width * cols),
            transcendentals=0,
        ),
    )(rows, weights, cosine, sine)


def normal(values):
    average = jnp.mean(values, axis=-1, keepdims=True)
    centred = values - average
    variance = jnp.mean(centred * centred, axis=-1, keepdims=True)
    scale = lax.rsqrt(variance + epsilon)
    return centred * scale, scale


def enter_kernel(
    tokens_ref,
    context_ref,
    vectors_ref,
    w_ref,
    cos_ref,
    sin_ref,
    rows_ref,
    rows_t_ref,
    q_ref,
    k_ref,
    v_ref,
):
    def norm(values):
        unit = normal(values.astype(f32))[0]
        return (unit * vectors_ref[0:1, :] + vectors_ref[1:2, :]).astype(bf16)

    def blocks(i, _):
        source = pl.ds(pl.multiple_of(i * TILE, TILE), TILE)
        rows_ref[source, :] = norm(context_ref[source, :])
        at = pl.ds(pl.multiple_of(CLEAN_OWN + i * TILE, TILE), TILE)
        rows_ref[at, :] = norm(tokens_ref[1, source, :])
        at = pl.ds(pl.multiple_of(NOISY_OWN + i * TILE, EDGE), TILE)
        rows_ref[at, :] = norm(tokens_ref[0, source, :])
        return 0

    lax.fori_loop(0, TILES, blocks, 0)
    rows_ref[2 * HALF : NOISY_BASE, :] = rows_ref[:EDGE, :]
    edge = norm(context_ref[HALF:, :])
    rows_ref[NOISY_BASE:NOISY_OWN, :] = edge
    rows_ref[NOISY_OWN + HALF :, :] = edge
    step = KEY_ROWS // 3

    def fields(i, _):
        at = pl.ds(pl.multiple_of(i * step, EDGE), step)
        project_rows(
            rows_ref[at, :], w_ref, cos_ref[at, :], sin_ref[at, :], q_ref, k_ref, v_ref, at
        )
        return 0

    lax.fori_loop(0, 3, fields, 0)
    for c in range(rows_t_ref.shape[0] // LANES):
        cols = slice(c * LANES, (c + 1) * LANES)
        rows_t_ref[cols, :] = rows_ref[:, cols].T


def enter(tokens, context, vectors, weights, cosine, sine):
    width, cols = weights.shape[1:]
    vmem = pl.BlockSpec(memory_space=pltpu.VMEM)
    shape = jax.ShapeDtypeStruct
    field = shape((KEY_ROWS, cols), bf16)
    return pl.pallas_call(
        enter_kernel,
        in_specs=[vmem] * 6,
        out_specs=[vmem] * 5,
        out_shape=[shape((KEY_ROWS, width), bf16), shape((width, KEY_ROWS), bf16)] + [field] * 3,
        name="enter",
        cost_estimate=pl.CostEstimate(
            flops=10**10, bytes_accessed=16 * 10**6, transcendentals=0
        ),
    )(tokens, context, vectors, weights, cosine, sine)


def split_heads(rows):
    low = low_lanes(rows.shape)
    zero = jnp.zeros_like(rows)
    return jnp.where(low, rows, zero), jnp.where(low, zero, rows)


def between(shape, offset, low, high):
    index = lax.broadcasted_iota(jnp.int32, shape, 0) + offset
    return jnp.logical_and(index >= low, index < high)


def fold(values, combine):
    rows, cols = values.shape
    groups = values.reshape(rows // 8, 8, cols)
    return combine(groups, axis=0)


def forward_kernel(
    span_ref, clean_ref, noisy_ref, q_ref, k_ref, v_ref, out_ref, lse_ref, bias_ref, window_ref
):
    pairs = q_ref.shape[1] // LANES
    lanes = [slice(p * LANES, (p + 1) * LANES) for p in range(pairs)]

    def one_tile(t, _):
        clean_at = pl.multiple_of(CLEAN_OWN + t * TILE, TILE)
        noisy_at = pl.multiple_of(NOISY_OWN + t * TILE, EDGE)
        window_at = pl.multiple_of(NOISY_BASE + t * TILE, EDGE)
        key_low, key_high = clean_ref[t, 0:1, :], clean_ref[t, 1:2, :]
        own_low, own_high = noisy_ref[t, 0:1, :], noisy_ref[t, 1:2, :]
        allowed = between((WINDOW, TILE), 0, own_low, own_high)
        window_ref[...] = jnp.where(allowed, 0.0, neg_large)
        first_key, trips = span_ref[t, 0], span_ref[t, 1]
        queries, tops = [], []
        for cols in lanes:
            query = jnp.concatenate(
                [q_ref[pl.ds(noisy_at, TILE), cols], q_ref[pl.ds(clean_at, TILE), cols]], axis=0
            )
            heads = split_heads(query)
            queries += heads
            keys = k_ref[pl.ds(window_at, WINDOW), cols]
            for head in range(2):
                scores = dot(keys, heads[head][:TILE], NT) + window_ref[...]
                top = fold(scores, jnp.max)
                tops.append(
                    jnp.concatenate([top, jnp.full((8, TILE), neg_large, f32)], axis=1)
                )

        def first_pass(j, tops):
            at = pl.multiple_of(first_key + j * KEY_TILE, EDGE)
            allowed = between((KEY_TILE, 2 * TILE), at, key_low, key_high)
            bias_ref[j] = jnp.where(allowed, 0.0, neg_large)
            after = []
            for p, cols in enumerate(lanes):
                keys = k_ref[pl.ds(at, KEY_TILE), cols]
                for head in range(2):
                    scores = dot(keys, queries[2 * p + head], NT) + bias_ref[j]
                    after.append(jnp.maximum(tops[2 * p + head], fold(scores, jnp.max)))
            return tuple(after)

        tops = lax.fori_loop(0, trips, first_pass, tuple(tops))
        tops = [jnp.max(top, axis=0, keepdims=True) * to_base2 for top in tops]
        state = []
        keys = [k_ref[pl.ds(window_at, WINDOW), cols] for cols in lanes]
        values_t = [v_ref[pl.ds(window_at, WINDOW), cols].T for cols in lanes]
        scores = dot(keys[0], queries[0][:TILE], NT)
        late = None
        for h in range(2 * pairs):
            if h + 1 < 2 * pairs:
                ahead = dot(keys[(h + 1) // 2], queries[h + 1][:TILE], NT)
            expo = jnp.exp2(scores * to_base2 - tops[h][:, :TILE] + window_ref[...])
            if late is not None:
                state.append(jnp.concatenate([late, jnp.zeros((HD, TILE), f32)], axis=1))
            total = fold(expo, jnp.sum)
            state.append(jnp.concatenate([total, jnp.zeros((8, TILE), f32)], axis=1))
            side = slice(h % 2 * HD, (h % 2 + 1) * HD)
            late = dot(values_t[h // 2][side], expo.astype(bf16))
            scores = ahead
        state.append(jnp.concatenate([late, jnp.zeros((HD, TILE), f32)], axis=1))

        def second_pass(j, state):
            at = pl.multiple_of(first_key + j * KEY_TILE, EDGE)
            keys = [k_ref[pl.ds(at, KEY_TILE), cols] for cols in lanes]
            values_t = [v_ref[pl.ds(at, KEY_TILE), cols].T for cols in lanes]
            after = list(state)
            scores = dot(keys[0], queries[0], NT)
            late = None
            for h in range(2 * pairs):
                ahead = dot(keys[(h + 1) // 2], queries[h + 1], NT) if h + 1 < 2 * pairs else None
                expo = jnp.exp2(scores * to_base2 - tops[h] + bias_ref[j])
                after[2 * h] = state[2 * h] + fold(expo, jnp.sum)
                if late is not None:
                    after[2 * h - 1] = state[2 * h - 1] + late
                side = slice(h % 2 * HD, (h % 2 + 1) * HD)
                late = dot(values_t[h // 2][side], expo.astype(bf16))
                scores = ahead
            after[-1] = state[-1] + late
            return tuple(after)

        state = lax.fori_loop(0, trips, second_pass, tuple(state))
        low_at = pl.ds(pl.multiple_of(t * TILE, TILE), TILE)
        high_at = pl.ds(pl.multiple_of(HALF + t * TILE, TILE), TILE)
        for p, cols in enumerate(lanes):
            halves = []
            for head in range(2):
                h = 2 * p + head
                total = jnp.sum(state[2 * h], axis=0, keepdims=True)
                halves.append(state[2 * h + 1] / total)
                lse_ref[p, t, head : head + 1, :] = tops[h] + jnp.log2(total)
            pair = jnp.concatenate(halves, axis=0).T.astype(bf16)
            out_ref[low_at, cols] = pair[:TILE]
            out_ref[high_at, cols] = pair[TILE:]
        return 0

    lax.fori_loop(0, TILES, one_tile, 0)


def attend_forward(spans, clean_bounds, noisy_bounds, query, keys, values):
    count, cols = query.shape
    pairs = cols // LANES
    vmem = pl.BlockSpec(memory_space=pltpu.VMEM)
    work = pairs * 2 * 2 * HALF * TOK_DEV
    return pl.pallas_call(
        forward_kernel,
        in_specs=[pl.BlockSpec(memory_space=pltpu.SMEM)] + [vmem] * 5,
        out_specs=[vmem] * 2,
        out_shape=[
            jax.ShapeDtypeStruct((TOK_DEV, cols), bf16),
            jax.ShapeDtypeStruct((pairs, TILES, 2, 2 * TILE), f32),
        ],
        scratch_shapes=[
            pltpu.VMEM((NOISY_BASE // KEY_TILE + 1, KEY_TILE, 2 * TILE), f32),
            pltpu.VMEM((WINDOW, TILE), f32),
        ],
        name="attend_forward",
        cost_estimate=pl.CostEstimate(
            flops=4 * work * HD, bytes_accessed=8 * count * cols, transcendentals=work
        ),
    )(spans, clean_bounds, noisy_bounds, query, keys, values)


def backward_kernel(
    span_ref,
    clean_ref,
    noisy_ref,
    q_ref,
    k_ref,
    v_ref,
    o_ref,
    d_ref,
    lse_ref,
    cos_ref,
    sin_ref,
    rows_ref,
    out_ref,
    grad_ref,
    dk_ref,
    dv_ref,
    bias_ref,
):
    pairs = q_ref.shape[1] // LANES
    lanes = [slice(p * LANES, (p + 1) * LANES) for p in range(pairs)]
    dk_ref[...] = jnp.zeros_like(dk_ref)
    dv_ref[...] = jnp.zeros_like(dv_ref)
    out_ref[0] = jnp.zeros_like(out_ref[0])

    def one_tile(t, _):
        clean_at = pl.multiple_of(CLEAN_OWN + t * TILE, TILE)
        noisy_at = pl.multiple_of(NOISY_OWN + t * TILE, EDGE)
        window_at = pl.multiple_of(NOISY_BASE + t * TILE, EDGE)
        low_at = pl.multiple_of(t * TILE, TILE)
        high_at = pl.multiple_of(HALF + t * TILE, TILE)
        key_low, key_high = clean_ref[t, 0:1, :], clean_ref[t, 1:2, :]
        own_low, own_high = noisy_ref[t, 0:1, :], noisy_ref[t, 1:2, :]
        queries, d_outs, inners, lses = [], [], [], []
        for p, cols in enumerate(lanes):

            def both(ref, low, high):
                return jnp.concatenate(
                    [ref[pl.ds(low, TILE), cols], ref[pl.ds(high, TILE), cols]], axis=0
                )

            queries.append(split_heads(both(q_ref, noisy_at, clean_at)))
            d_rows = both(d_ref, low_at, high_at)
            o_rows = both(o_ref, low_at, high_at)
            product = (d_rows.astype(f32) * o_rows.astype(f32)).T
            d_outs.append(split_heads(d_rows))
            inners.append(
                [
                    jnp.sum(product[head * HD : (head + 1) * HD], axis=0, keepdims=True) * 0.125
                    for head in range(2)
                ]
            )
            lses.append([lse_ref[p, t, head : head + 1, :] for head in range(2)])

        def accumulate(at, rows, cols, allowed, d_query):
            bias_ref[:rows, :cols] = jnp.where(allowed, 0.0, neg_large)
            after = list(d_query)
            keys = [k_ref[pl.ds(at, rows), span] for span in lanes]
            eighth = [v_ref[pl.ds(at, rows), span] * jnp.asarray(0.125, bf16) for span in lanes]
            keys_t = [part.T for part in keys]
            stack = lambda parts: jnp.concatenate([part[:cols] for part in parts], axis=0)

            def begin(h):
                p, head = h // 2, h % 2
                return (
                    dot(keys[p], queries[p][head][:cols], NT),
                    dot(eighth[p], d_outs[p][head][:cols], NT),
                )

            def finish_pair(p, weights, d_scores):
                span = lanes[p]
                for head in range(2):
                    side = slice(head * HD, (head + 1) * HD)
                    h = 2 * p + head
                    after[h] = d_query[h] + dot(keys_t[p][side], d_scores[head])
                dv_ref[pl.ds(at, rows), span] += dot(
                    jnp.concatenate(weights, axis=1), stack(d_outs[p])
                )
                dk_ref[pl.ds(at, rows), span] += dot(
                    jnp.concatenate(d_scores, axis=1), stack(queries[p])
                )

            ready = begin(0)
            held = None
            weights, d_scores = [], []
            for h in range(2 * pairs):
                ahead = begin(h + 1) if h + 1 < 2 * pairs else None
                p, head = h // 2, h % 2
                scores = ready[0] * to_base2 - lses[p][head][:, :cols] + bias_ref[:rows, :cols]
                probs = jnp.exp2(scores)
                d_score = (probs * (ready[1] - inners[p][head][:, :cols])).astype(bf16)
                weights.append(probs.astype(bf16))
                d_scores.append(d_score)
                if held is not None:
                    finish_pair(*held)
                    held = None
                if head == 1:
                    held = (p, weights, d_scores)
                    weights, d_scores = [], []
                ready = ahead
            finish_pair(*held)
            return tuple(after)

        allowed = between((WINDOW, TILE), 0, own_low, own_high)
        zero = jnp.zeros((HD, TILE), f32)
        start = accumulate(window_at, WINDOW, TILE, allowed, (zero,) * (2 * pairs))
        start = tuple(jnp.concatenate([part, zero], axis=1) for part in start)
        first_key, trips = span_ref[t, 0], span_ref[t, 1]

        def one_step(j, d_query):
            at = pl.multiple_of(first_key + j * KEY_TILE, EDGE)
            allowed = between((KEY_TILE, 2 * TILE), at, key_low, key_high)
            return accumulate(at, KEY_TILE, 2 * TILE, allowed, d_query)

        d_query = lax.fori_loop(0, trips, one_step, start)
        for p, span in enumerate(lanes):
            pair = jnp.concatenate(d_query[2 * p : 2 * p + 2], axis=0).T
            for at, part in ((noisy_at, pair[:TILE]), (clean_at, pair[TILE:])):
                turned = turn(part, cos_ref[pl.ds(at, TILE), :], -sin_ref[pl.ds(at, TILE), :])
                out_ref[0, pl.ds(at, TILE), span] = turned.astype(bf16)
        return 0

    lax.fori_loop(0, TILES, one_tile, 0)
    step = KEY_ROWS // 9

    def finish(i, _):
        rows = pl.ds(pl.multiple_of(i * step, EDGE), step)
        for span in lanes:
            out_ref[1, rows, span] = turn(
                dk_ref[rows, span], cos_ref[rows, :], -sin_ref[rows, :]
            ).astype(bf16)
        out_ref[2, rows, :] = dv_ref[rows, :].astype(bf16)
        return 0

    lax.fori_loop(0, 9, finish, 0)

    def weight_rows(i, _):
        rows = pl.ds(pl.multiple_of(i * ROW_TILE, LANES), ROW_TILE)
        for c in range(3):
            grad_ref[c, rows, :] = dot(rows_ref[rows, :], out_ref[c]).astype(bf16)
        return 0

    lax.fori_loop(0, rows_ref.shape[0] // ROW_TILE, weight_rows, 0)


def attend_backward(
    spans,
    clean_bounds,
    noisy_bounds,
    query,
    keys,
    values,
    attended,
    d_attended,
    lse,
    cosine,
    sine,
    rows_t,
):
    count, cols = query.shape
    width = rows_t.shape[0]
    vmem = pl.BlockSpec(memory_space=pltpu.VMEM)
    return pl.pallas_call(
        backward_kernel,
        in_specs=[pl.BlockSpec(memory_space=pltpu.SMEM)] + [vmem] * 11,
        out_specs=[vmem] * 2,
        scratch_shapes=[
            pltpu.VMEM((count, cols), f32),
            pltpu.VMEM((count, cols), f32),
            pltpu.VMEM((max(KEY_TILE, WINDOW), 2 * TILE), f32),
        ],
        out_shape=[
            jax.ShapeDtypeStruct((3, count, cols), bf16),
            jax.ShapeDtypeStruct((3, width, cols), bf16),
        ],
        name="attend_backward",
        cost_estimate=pl.CostEstimate(
            flops=36 * 10**9, bytes_accessed=36 * 10**6, transcendentals=6 * 10**6
        ),
    )(
        spans,
        clean_bounds,
        noisy_bounds,
        query,
        keys,
        values,
        attended,
        d_attended,
        lse,
        cosine,
        sine,
        rows_t,
    )


PIECES = 16
MESH = pl.DeviceIdType.MESH


def flip(value, mask):
    result = value
    for b in range(mask.bit_length()):
        if mask >> b & 1:
            result = result + (1 << b) * (1 - 2 * ((value // (1 << b)) % 2))
    return result


class Exchange:
    def __init__(self, bits, count, rows, width, back=True):
        self.bits, self.count, self.rows, self.width = bits, count, rows, width
        self.back = back
        self.half, self.quarter, self.piece = rows // 2, rows // 4, rows // PIECES
        self.extra = list(range(4, bits))

    def slots(self):
        return 8 + 2 * (6 if self.back else 4) + (3 if self.extra else 0)

    def scratch(self):
        k, w = self.count, self.width
        cross = k if not self.back else 1
        shapes = [
            pltpu.VMEM((k, 2 - self.back, self.half, w), bf16),
            pltpu.VMEM((cross, self.half, w), bf16),
            pltpu.VMEM((cross, self.half, w), bf16),
            pltpu.VMEM((k, self.quarter, w), bf16),
            pltpu.VMEM((k, self.quarter, w), bf16),
            pltpu.VMEM((k, self.quarter, w), f32),
            pltpu.VMEM((k, 3, self.piece, w), bf16),
            pltpu.VMEM((k, 3, self.piece, w), bf16),
        ]
        lanes_of = (1, 0, 1, 3, 3, 1, 1) if self.back else (2, 1, 1, 3, 0, 0, 0)
        for lanes in [lanes for lanes in lanes_of if lanes]:
            shapes += [pltpu.SemaphoreType.DMA((k, lanes))] * 2
        if self.extra:
            n = len(self.extra)
            shapes += [pltpu.VMEM((k, 2 * n, self.piece, w), bf16)]
            shapes += [pltpu.SemaphoreType.DMA((k, n))] * 2
        return shapes

    def bind(self, place, part, refs):
        (self.a_in, self.b_out, self.b_in, self.c_out, self.c_in, self.keep) = refs[:6]
        self.d_out, self.d_in = refs[6:8]
        names = "acdefg" if self.back else "abcd"
        self.sems = {name: (refs[8 + 2 * i], refs[9 + 2 * i]) for i, name in enumerate(names)}
        if self.extra:
            at = 8 + 2 * len(names)
            self.x_buf, self.x_send, self.x_recv = refs[at : at + 3]
        self.place, self.part = place, part
        self.core, self.x, self.z = place % 2, (place // 2) % 2, (place // 4) % 4
        self.sibling = {"dp": flip(place, 1)}
        self.beside = {"dp": flip(place, 2)}
        self.across = {"mp": 1 - part}
        self.peers = [{"dp": flip(place, j << 2)} for j in range(1, 4)]
        self.partners = [self.sibling, self.beside, self.across] + self.peers
        self.partners += [{"dp": flip(place, 1 << b)} for b in self.extra]
        return self

    def greet(self):
        barrier = pltpu.get_barrier_semaphore()
        for partner in self.partners:
            pl.semaphore_signal(barrier, inc=1, device_id=partner, device_id_type=MESH)
        pl.semaphore_wait(barrier, len(self.partners))

    def copy(self, name, k, lane, source, target, device):
        out, into = self.sems[name]
        return pltpu.make_async_remote_copy(
            src_ref=source,
            dst_ref=target,
            send_sem=out.at[k, lane],
            recv_sem=into.at[k, lane],
            device_id=device,
            device_id_type=MESH,
        )

    def rows_at(self, start, size):
        return pl.ds(pl.multiple_of(start, PIECES), size)

    def copy_a(self, k, lane, grads):
        source = grads.at[k, self.rows_at((1 - self.core) * self.half, self.half)]
        return self.copy("a", k, lane, source, self.a_in.at[k, lane], self.sibling)

    def copy_b(self, k):
        return self.copy("b", k, 0, self.b_out.at[k], self.b_in.at[k], self.across)

    def copy_c(self, k):
        return self.copy("c", k, 0, self.c_out.at[k], self.c_in.at[k], self.beside)

    def copy_d(self, k, j):
        return self.copy("d", k, j, self.d_out.at[k, j], self.d_in.at[k, j], self.peers[j])

    def spot(self, change=0):
        start = self.core * self.half + self.x * self.quarter
        return self.rows_at(start + flip(self.z, change) * self.piece, self.piece)

    def copy_e(self, k, j, full):
        rows = full.at[k, self.spot()]
        return self.copy("e", k, j, rows, rows, self.peers[j])

    def copy_f(self, k, full):
        start = self.core * self.half + self.x * self.quarter
        rows = full.at[k, self.rows_at(start, self.quarter)]
        return self.copy("f", k, 0, rows, rows, self.beside)

    def copy_g(self, k, full):
        rows = full.at[k, self.rows_at(self.core * self.half, self.half)]
        return self.copy("g", k, 0, rows, rows, self.sibling)

    def start_a(self, k, lane, grads):
        self.copy_a(k, lane, grads).start()

    def stage_b(self, k, others):
        self.copy_a(k, 0, others).wait()
        mine = others[k, self.rows_at(self.core * self.half, self.half), :].astype(f32)
        self.b_out[k] = (mine + self.a_in[k, 0].astype(f32)).astype(bf16)
        self.copy_b(k).start()

    def stage_c(self, k, grads, crossed=None):
        lane = 0 if self.back else 1
        self.copy_a(k, lane, grads).wait()
        if not self.back:
            self.copy_b(k).wait()

        def total(which):
            inner = which * self.quarter
            rows = self.rows_at(inner, self.quarter)
            mine = grads[k, self.rows_at(self.core * self.half + inner, self.quarter), :]
            got = self.a_in[k, lane, rows, :].astype(f32)
            if not self.back:
                got = got + self.b_in[k, rows, :].astype(f32)
            elif crossed is not None:
                got = got + crossed(rows)
            return mine.astype(f32) + got

        self.c_out[k] = total(1 - self.x).astype(bf16)
        self.copy_c(k).start()
        self.keep[k] = total(self.x)

    def stage_d(self, k):
        self.copy_c(k).wait()
        for j in range(4):
            rows = self.rows_at(flip(self.z, j) * self.piece, self.piece)
            total = self.keep[k, rows, :] + self.c_in[k, rows, :].astype(f32)
            if j:
                self.d_out[k, j - 1] = total.astype(bf16)
                self.copy_d(k, j - 1).start()
            else:
                self.keep[k, rows, :] = total

    def gather_d(self, k):
        rows = self.rows_at(self.z * self.piece, self.piece)
        total = self.keep[k, rows, :]
        for j in range(3):
            self.copy_d(k, j).wait()
            total = total + self.d_in[k, j].astype(f32)
        for i, b in enumerate(self.extra):
            mine = self.x_buf.at[k, 2 * i]
            mine[...] = total.astype(bf16)
            swap = pltpu.make_async_remote_copy(
                src_ref=mine,
                dst_ref=self.x_buf.at[k, 2 * i + 1],
                send_sem=self.x_send.at[k, i],
                recv_sem=self.x_recv.at[k, i],
                device_id={"dp": flip(self.place, 1 << b)},
                device_id_type=MESH,
            )
            swap.start()
            swap.wait()
            total = total.astype(bf16).astype(f32) + self.x_buf[k, 2 * i + 1].astype(f32)
        return total.astype(bf16)

    def stage_e(self, k, full):
        full[k, self.spot(), :] = self.gather_d(k)
        for j in range(3):
            self.copy_e(k, j, full).start()

    def stage_f(self, k, full):
        for j in range(3):
            self.copy_e(k, j, full).wait()
        self.copy_f(k, full).start()

    def stage_g(self, k, full):
        self.copy_f(k, full).wait()
        self.copy_g(k, full).start()

    def stage_h(self, k, full):
        self.copy_g(k, full).wait()


def at_step(step, count, action):
    @pl.when(jnp.logical_and(step >= 0, step < count))
    def _():
        action(step)


def middle_kernel(exchanges, tiles, *refs):
    (
        x_ref,
        att_ref,
        att2_ref,
        wout_ref,
        wout2_ref,
        dy_ref,
        vectors_ref,
        bup_ref,
        up_mine,
        up_here,
        up_beside,
        down_mine,
        down_here,
        down_beside,
        out_ref,
        mid_ref,
        datt_ref,
        datt2_ref,
        gout_ref,
        gout2_ref,
        gbup_ref,
        small_ref,
        pieces_ref,
        up_there,
        down_there,
        pass_up,
        pass_down,
        up_buf,
        down_buf,
        load_sem,
        n2_ref,
        total_ref,
        dn2_ref,
        act_ref,
        dpre_ref,
        n2_t,
        down_grad,
        up_grad,
        *rest,
    ) = refs
    place, part = lax.axis_index("dp"), lax.axis_index("mp")
    ex = exchanges[0].bind(place, part, rest)
    ex_up = exchanges[1].bind(place, part, rest[exchanges[0].slots() :])
    sides = ((ex, down_grad), (ex_up, up_grad))
    core = ex.core
    count = tiles // 2
    rows_all = x_ref.shape[0]
    blocks = rows_all // ROW_TILE
    width = x_ref.shape[1]
    lanes = width // 2

    def which(i):
        other = jnp.logical_or(i == 0, jnp.logical_and(i % 2 == 1, i < tiles - 1))
        mine = jnp.where(i == tiles - 1, count - 1, i // 2 - 1)
        return other, jnp.where(other, (i + 1) // 2, mine)

    quarter = width // 4
    strip = HIDDEN_TILE // 2
    held = 2 * core + ex.x
    kept = 2 * core + 1 - ex.x

    def load_up(i, source, h):
        target = up_buf.at[i % 2, h * quarter : (h + 1) * quarter]
        return pltpu.make_async_copy(source, target, load_sem.at[i % 2, h])

    def load_down(i, source, h):
        target = down_buf.at[i % 2, h * strip : (h + 1) * strip]
        return pltpu.make_async_copy(source, target, load_sem.at[i % 2, 4 + h])

    def hand_up(k, part_of):
        cols = pl.ds(pl.multiple_of(k * HIDDEN_TILE, HIDDEN_TILE), HIDDEN_TILE)
        side = ex.x if part_of == 0 else 1 - ex.x
        rows = pl.ds(pl.multiple_of(side * quarter, EDGE), quarter)
        return pltpu.make_async_remote_copy(
            src_ref=(up_here, up_beside)[part_of].at[:, cols],
            dst_ref=up_there.at[k, rows],
            send_sem=pass_up.at[k, 2 * part_of],
            recv_sem=pass_up.at[k, 2 * part_of + 1],
            device_id=ex.sibling,
            device_id_type=MESH,
        )

    def hand_down(b, part_of):
        side = ex.x if part_of == 0 else 1 - ex.x
        return pltpu.make_async_remote_copy(
            src_ref=(down_here, down_beside)[part_of].at[strip_rows(b)],
            dst_ref=down_there.at[side * (count // 2) + b],
            send_sem=pass_down.at[side * (count // 2) + b, 0],
            recv_sem=pass_down.at[side * (count // 2) + b, 1],
            device_id=ex.sibling,
            device_id_type=MESH,
        )

    def strip_rows(b):
        return pl.ds(pl.multiple_of(b * strip, strip), strip)

    def got_down(slot):
        return pltpu.make_async_remote_copy(
            src_ref=down_there.at[slot],
            dst_ref=down_there.at[slot],
            send_sem=pass_down.at[slot, 0],
            recv_sem=pass_down.at[slot, 1],
            device_id=ex.sibling,
            device_id_type=MESH,
        )

    def start_loads(i):
        other, k = which(i)
        mine = jnp.logical_not(other)
        cols = pl.ds(pl.multiple_of(k * HIDDEN_TILE, HIDDEN_TILE), HIDDEN_TILE)
        span = count // 2

        @pl.when(other)
        def _():
            hand_up(k, 0).wait()
            hand_up(k, 1).wait()

        for h in range(4):

            @pl.when(mine)
            def _():
                load_up(i, up_mine.at[h * quarter : (h + 1) * quarter, cols], h).start()

            @pl.when(jnp.logical_and(other, held == h))
            def _():
                load_up(i, up_here.at[:, cols], h).start()

            @pl.when(jnp.logical_and(other, kept == h))
            def _():
                load_up(i, up_beside.at[:, cols], h).start()

            @pl.when(jnp.logical_and(other, core != h // 2))
            def _():
                rows = slice(h % 2 * quarter, (h % 2 + 1) * quarter)
                load_up(i, up_there.at[k, rows], h).start()

        for h in range(2):
            b = 2 * k + h
            piece, inner = b // span, b % span

            @pl.when(mine)
            def _():
                load_down(i, down_mine.at[strip_rows(b), :], h).start()

            @pl.when(jnp.logical_and(other, held == piece))
            def _():
                load_down(i, down_here.at[strip_rows(inner), :], h).start()

            @pl.when(jnp.logical_and(other, kept == piece))
            def _():
                load_down(i, down_beside.at[strip_rows(inner), :], h).start()

            @pl.when(jnp.logical_and(other, core != piece // 2))
            def _():
                slot = piece % 2 * span + inner
                got_down(slot).wait_recv()
                load_down(i, down_there.at[slot], h).start()

    def wait_loads(i):
        for h in range(4):
            load_up(i, up_mine.at[:quarter, :HIDDEN_TILE], h).wait()
        for h in range(2):
            load_down(i, down_mine.at[:strip, :], h).wait()

    ex.greet()

    def hand(k, _):
        hand_up(k, 0).start()
        hand_up(k, 1).start()

        @pl.when(k < count // 2)
        def _():
            hand_down(k, 0).start()
            hand_down(k, 1).start()

        return 0

    lax.fori_loop(0, count, hand, 0)

    def prologue(r, _):
        rows = pl.ds(pl.multiple_of(r * ROW_TILE, ROW_TILE), ROW_TILE)
        branch = dot(att_ref[rows, :], wout_ref[...]) + dot(att2_ref[rows, :], wout2_ref[...])
        mid = x_ref[rows, :].astype(f32) + branch
        mid_ref[rows, :] = mid
        unit = normal(mid)[0]
        n2_ref[rows, :] = (unit * vectors_ref[2:3, :] + vectors_ref[3:4, :]).astype(bf16)
        total_ref[rows, :] = mid + vectors_ref[4:5, :]
        dn2_ref[rows, :] = jnp.zeros((ROW_TILE, width), f32)
        return 0

    lax.fori_loop(0, blocks, prologue, 0)
    start_loads(0)
    for c in range(width // LANES):
        cols = slice(c * LANES, (c + 1) * LANES)
        n2_t[cols, :] = n2_ref[:, cols].T

    def tile(i):
        other, k = which(i)
        slot = i % 2
        wait_loads(i)

        @pl.when(i + 1 < tiles)
        def _():
            start_loads(i + 1)

        up, down = up_buf.at[slot], down_buf.at[slot]
        bias_at = jnp.where(other, k, count + k)
        bias_grad = jnp.zeros((1, HIDDEN_TILE), f32)
        block = lambda r: slice(r * ROW_TILE, (r + 1) * ROW_TILE)

        def begin(r):
            return dot(n2_ref[block(r), :], up[...]), dot(dy_ref[block(r), :], down[...], NT)

        ready = begin(0)
        for r in range(blocks):
            rows = block(r)
            ahead = begin(r + 1) if r + 1 < blocks else None
            pre = ready[0] + bup_ref[bias_at]
            square = pre * pre
            bend = jnp.tanh(0.7978845608028654 * (pre + 0.044715 * square * pre))
            part_one = 0.5 * (1.0 + bend)
            act = (pre * part_one).astype(bf16)
            slope = part_one + (0.5 * pre) * (1.0 - bend * bend) * (
                0.7978845608028654 * (1.0 + 3.0 * 0.044715 * square)
            )
            d_pre = (ready[1] * slope).astype(bf16)
            act_ref[rows, :] = act
            dpre_ref[rows, :] = d_pre
            bias_grad = bias_grad + jnp.sum(d_pre.astype(f32), axis=0, keepdims=True)
            total_ref[rows, :] += dot(act, down[...])
            dn2_ref[rows, :] += dot(d_pre, up[...], NT)
            ready = ahead
        gbup_ref[bias_at] = bias_grad
        down_grad[k] = dot(act_ref[...].T, dy_ref[...]).astype(bf16)

        def start(lane):
            for side, grad in sides:
                side.start_a(k, lane, grad)

        up_grad[k] = dot(n2_t[...], dpre_ref[...]).astype(bf16)
        pl.when(other)(functools.partial(start, 0))
        pl.when(jnp.logical_not(other))(functools.partial(start, 1))

    def each(k, when, action):
        @pl.when(jnp.logical_and(when, jnp.logical_and(k >= 0, k < count)))
        def _():
            for n, (side, grad) in enumerate(sides):
                action(n, side, grad, k)

    def stage_b(n, side, grad, k):
        side.stage_b(k, grad)

    def stage_c(n, side, grad, k):
        side.stage_c(k, grad)

    def stage_d(n, side, grad, k):
        side.stage_d(k)

    def arrive(n, side, grad, k):
        piece = side.gather_d(k)
        if n == 0:
            pieces_ref[k] = piece
        else:
            for c in range(width // HIDDEN_TILE):
                cols = slice(c * HIDDEN_TILE, (c + 1) * HIDDEN_TILE)
                pieces_ref[count + k, :, cols] = piece[c * PIECES : (c + 1) * PIECES]

    def steps(i):
        even = i % 2 == 0
        odd = jnp.logical_not(even)
        each((i - 6) // 2, even, arrive)
        each((i - 5) // 2, odd, stage_d)
        each((i - 4) // 2, even, stage_c)
        crossing = jnp.logical_or(i == 1, jnp.logical_and(even, i >= 2))
        each(i // 2, crossing, stage_b)

    def epilogue(r, _):
        rows = pl.ds(pl.multiple_of(r * ROW_TILE, ROW_TILE), ROW_TILE)
        out_ref[rows, :] = total_ref[rows, :].astype(bf16)
        unit, scale = normal(mid_ref[rows, :])
        d_rows = dn2_ref[rows, :]
        dy = dy_ref[rows, :].astype(f32)
        lean = d_rows * vectors_ref[2:3, :]
        d_mid = dy + scale * (
            lean
            - jnp.mean(lean, axis=-1, keepdims=True)
            - unit * jnp.mean(lean * unit, axis=-1, keepdims=True)
        )
        mid_ref[rows, :] = d_mid
        d_branch = d_mid.astype(bf16)
        n2_ref[rows, :] = d_branch
        datt_ref[rows, :] = dot(d_branch, wout_ref[...], NT).astype(bf16)
        datt2_ref[rows, :] = dot(d_branch, wout2_ref[...], NT).astype(bf16)
        add = lambda values: jnp.sum(values, axis=0, keepdims=True)
        small_ref[0:1, :] += add(d_rows * unit)
        small_ref[1:2, :] += add(d_rows)
        small_ref[2:3, :] += add(dy)
        return 0

    def out_grads():
        depth = wout_ref.shape[0]
        for source, target in ((att_ref, gout_ref), (att2_ref, gout2_ref)):
            grad = dot(source[...].T, n2_ref[...]).astype(bf16)
            target[:depth, :] = grad[:, :lanes]
            target[depth:, :] = grad[:, lanes:]

    def main(i, _):
        pl.when(i < tiles)(functools.partial(tile, i))

        @pl.when(jnp.logical_and(i >= tiles, i < tiles + 2))
        def _():
            first = (i - tiles) * (blocks // 2)
            lax.fori_loop(first, first + blocks // 2, epilogue, 0)

        pl.when(i == tiles + 2)(out_grads)
        steps(i)
        return 0

    small_ref[...] = jnp.zeros_like(small_ref)
    lax.fori_loop(0, tiles + 5, main, 0)

    def handed(slot, _):
        got_down(slot).wait_send()
        return 0

    lax.fori_loop(0, count, handed, 0)


def middle(bits, x, att, att2, wout, wout2, dy, vectors, bup, ups, downs):
    rows, width = x.shape
    hidden = ups[0].shape[1]
    count = hidden // HIDDEN_TILE
    tiles = 2 * count
    exchanges = (
        Exchange(bits, count, HIDDEN_TILE, width, False),
        Exchange(bits, count, width, HIDDEN_TILE, False),
    )
    vmem = pl.BlockSpec(memory_space=pltpu.VMEM)
    hbm = pl.BlockSpec(memory_space=pl.ANY)
    shape = jax.ShapeDtypeStruct
    depth = wout.shape[0]
    return pl.pallas_call(
        functools.partial(middle_kernel, exchanges, tiles),
        in_specs=[vmem] * 8 + [hbm] * 6,
        out_specs=[vmem] * 9,
        out_shape=[
            shape((rows, width), bf16),
            shape((rows, width), f32),
            shape(att.shape, bf16),
            shape(att2.shape, bf16),
            shape((2 * depth, width // 2), bf16),
            shape((2 * depth, width // 2), bf16),
            shape((tiles, 1, HIDDEN_TILE), f32),
            shape((8, width), f32),
            shape((2 * count, PIECES, width), bf16),
        ],
        scratch_shapes=[
            pltpu.VMEM((count, width // 2, HIDDEN_TILE), bf16),
            pltpu.VMEM((count, HIDDEN_TILE // 2, width), bf16),
            pltpu.SemaphoreType.DMA((count, 4)),
            pltpu.SemaphoreType.DMA((count, 2)),
            pltpu.VMEM((2, width, HIDDEN_TILE), bf16),
            pltpu.VMEM((2, HIDDEN_TILE, width), bf16),
            pltpu.SemaphoreType.DMA((2, 6)),
            pltpu.VMEM((rows, width), bf16),
            pltpu.VMEM((rows, width), f32),
            pltpu.VMEM((rows, width), f32),
            pltpu.VMEM((rows, HIDDEN_TILE), bf16),
            pltpu.VMEM((rows, HIDDEN_TILE), bf16),
            pltpu.VMEM((width, rows), bf16),
            pltpu.VMEM((count, HIDDEN_TILE, width), bf16),
            pltpu.VMEM((count, width, HIDDEN_TILE), bf16),
        ]
        + exchanges[0].scratch()
        + exchanges[1].scratch(),
        compiler_params=pltpu.CompilerParams(
            collective_id=0, has_side_effects=True, vmem_limit_bytes=67043328
        ),
        name="middle",
        cost_estimate=pl.CostEstimate(
            flops=60 * 10**9, bytes_accessed=40 * 10**6, transcendentals=4 * 10**6
        ),
    )(x, att, att2, wout, wout2, dy, vectors, bup, *ups, *downs)


def leave_kernel(exchange, *refs):
    (
        mine_ref,
        mine_out_ref,
        crossed_ref,
        crossed_out_ref,
        d_hbm,
        d2_hbm,
        w_hbm,
        w2_hbm,
        tokens_ref,
        context_ref,
        vectors_ref,
        dmid_hbm,
        small_ref,
        small2_ref,
        full_ref,
        back_ref,
        sums_ref,
        out_buf,
        d_ref,
        d2_ref,
        w_ref,
        w2_ref,
        dmid_ref,
        load_sem,
        rows_ref,
        give_ref,
        take_ref,
        swap_sem,
        norm_ref,
        near_ref,
        far_ref,
        near_sem,
        far_sem,
        *rest,
    ) = refs
    place, part = lax.axis_index("dp"), lax.axis_index("mp")
    ex = exchange.bind(place, part, rest)
    count, bits = ex.count, ex.bits
    first = mine_ref.shape[0]
    loads = [
        pltpu.make_async_copy(source, target, load_sem.at[n])
        for n, (source, target) in enumerate(
            ((w_hbm, w_ref), (d_hbm, d_ref), (w2_hbm, w2_ref), (d2_hbm, d2_ref), (dmid_hbm, dmid_ref))
        )
    ]
    for load in loads:
        load.start()
    near_id = part * 4 + place % 4
    near = [
        {"dp": flip(place, j % 4), "mp": part if j < 4 else 1 - part} for j in range(1, 8)
    ]
    ex.partners += [near[j - 1] for j in (3, 5, 6, 7)]
    ex.greet()

    def begin(k, _):
        ex.start_a(k, 0, mine_ref)
        return 0

    lax.fori_loop(0, first, begin, 0)

    def begin_out(k, _):
        total = mine_out_ref[k].astype(f32) + crossed_out_ref[k].astype(f32)
        out_buf[first + k] = total.astype(bf16)
        ex.start_a(first + k, 0, out_buf)
        return 0

    lax.fori_loop(0, count - first, begin_out, 0)

    def back_of(rows):
        total = 0.0
        for grads, weights in ((d_ref, w_ref), (d2_ref, w2_ref)):
            for c in range(3):
                total = total + dot(grads[c, rows, :], weights[c], NT)
        return total

    def stage_c(k):
        @pl.when(k < first)
        def _():
            ex.stage_c(k, mine_ref, lambda rows: crossed_ref[k, rows, :].astype(f32))

        @pl.when(k >= first)
        def _():
            ex.stage_c(k, out_buf)

    def steps(i):
        at_step(i - 10, count, lambda k: ex.stage_h(k, full_ref))
        at_step(i - 8, count, lambda k: ex.stage_g(k, full_ref))
        at_step(i - 6, count, lambda k: ex.stage_f(k, full_ref))
        at_step(i - 4, count, lambda k: ex.stage_e(k, full_ref))
        at_step(i - 2, count, lambda k: ex.stage_d(k))
        at_step(i, count, stage_c)

    width = tokens_ref.shape[1]

    def swap(rows, lane):
        return pltpu.make_async_remote_copy(
            src_ref=give_ref.at[rows],
            dst_ref=take_ref.at[rows],
            send_sem=swap_sem.at[lane, 0],
            recv_sem=swap_sem.at[lane, 1],
            device_id=ex.across,
            device_id_type=MESH,
        )

    def sums_of(d_rows, units):
        add = lambda values: jnp.sum(values, axis=0, keepdims=True)
        norm_ref[0:1, :] += add(d_rows * units)
        norm_ref[1:2, :] += add(d_rows)

    main = slice(0, HALF)
    edges = slice(HALF, HALF + 2 * EDGE)
    parts = tokens_ref.shape[0] // TILE
    own = NOISY_OWN - 2 * HALF
    lead = small_ref.shape[0] - 2
    bias = lead - 3
    norm_ref[...] = jnp.zeros_like(norm_ref)

    def give_main():
        for load in loads[:4]:
            load.wait()
        given = back_of(main)
        give_ref[main, :] = given.astype(bf16)
        rows_ref[:HALF, :] = given
        swap(main, 0).start()

    def give_edges():
        def context_sums(b, _):
            rows = pl.ds(pl.multiple_of(b * TILE, TILE), TILE)
            sums_of(rows_ref[rows, :], normal(context_ref[rows, :].astype(f32))[0])
            return 0

        lax.fori_loop(0, HALF // TILE, context_sums, 0)
        tail = back_of(slice(2 * HALF, KEY_ROWS))
        rows_ref[:HALF, :] = tail[own : own + HALF]
        side = tail[EDGE:own] + tail[own + HALF :]
        give_ref[HALF : HALF + EDGE, :] = tail[:EDGE].astype(bf16)
        give_ref[HALF + EDGE :, :] = side.astype(bf16)
        swap(edges, 1).start()
        sums_of(tail[:EDGE], normal(context_ref[:EDGE, :].astype(f32))[0])
        sums_of(side, normal(context_ref[HALF:, :].astype(f32))[0])

    def own_clean():
        rows_ref[HALF:, :] = back_of(slice(CLEAN_OWN, CLEAN_OWN + HALF))

    def tell_near():
        def own_sums(b, _):
            rows = pl.ds(pl.multiple_of(b * TILE, TILE), TILE)
            sums_of(rows_ref[rows, :], normal(tokens_ref[rows, :].astype(f32))[0])
            return 0

        lax.fori_loop(0, parts, own_sums, 0)
        mine = near_ref.at[near_id]
        mine[:lead, :] = small_ref[:lead, :]
        mine[lead : lead + 2, :] = norm_ref[:2, :]
        mine[lead + 2 : lead + 2 + bias, :] = small2_ref[:bias, :]
        rest_rows = 16 - lead - 2 - bias
        mine[16 - rest_rows :, :] = jnp.zeros((rest_rows, width), f32)
        for j in range(1, 8):
            near_copy(j).start()

    def near_copy(j):
        return pltpu.make_async_remote_copy(
            src_ref=near_ref.at[near_id],
            dst_ref=near_ref.at[near_id],
            send_sem=near_sem.at[j, 0],
            recv_sem=near_sem.at[j, 1],
            device_id=near[j - 1],
            device_id_type=MESH,
        )

    def near_got(j):
        came = (part + j // 4) % 2 * 4 + flip(place % 4, j % 4)
        return pltpu.make_async_remote_copy(
            src_ref=near_ref.at[came],
            dst_ref=near_ref.at[came],
            send_sem=near_sem.at[j, 0],
            recv_sem=near_sem.at[j, 1],
            device_id=near[j - 1],
            device_id_type=MESH,
        )

    def far_copy(j, at):
        return pltpu.make_async_remote_copy(
            src_ref=far_ref.at[at],
            dst_ref=far_ref.at[at],
            send_sem=far_sem.at[j, 0],
            recv_sem=far_sem.at[j, 1],
            device_id=ex.peers[j - 1],
            device_id_type=MESH,
        )

    def tell_far():
        for j in range(1, 8):
            near_copy(j).wait_send()
            near_got(j).wait_recv()
        total = near_ref[0]
        for j in range(1, 8):
            total = total + near_ref[j]
        plane = near_ref[part * 4]
        other = near_ref[(1 - part) * 4]
        for j in range(1, 4):
            plane = plane + near_ref[part * 4 + j]
            other = other + near_ref[(1 - part) * 4 + j]
        spot = far_ref.at[ex.z]
        spot[...] = total
        spot[:bias, :] = plane[:bias] + other[lead + 2 : lead + 2 + bias]
        for j in range(1, 4):
            far_copy(j, ex.z).start()

    def take_back():
        loads[4].wait()
        swap(main, 0).wait()
        swap(edges, 1).wait()
        rows_ref[HALF:, :] += take_ref[main, :].astype(f32)
        rows_ref[HALF : HALF + EDGE, :] += take_ref[HALF : HALF + EDGE, :].astype(f32)
        edge = pl.ds(pl.multiple_of((1 - part) * (HALF - EDGE), EDGE), EDGE)
        rows_ref[edge, :] += take_ref[HALF + EDGE :, :].astype(f32)

    def norm_back(b):
        rows = pl.ds(pl.multiple_of(b * TILE, TILE), TILE)
        unit, scale = normal(tokens_ref[rows, :].astype(f32))
        lean = rows_ref[rows, :] * vectors_ref[0:1, :]
        back_ref[rows, :] = dmid_ref[rows, :] + scale * (
            lean
            - jnp.mean(lean, axis=-1, keepdims=True)
            - unit * jnp.mean(lean * unit, axis=-1, keepdims=True)
        )

    def end_far():
        for j in range(1, 4):
            far_copy(j, ex.z).wait_send()
            far_copy(j, flip(ex.z, j)).wait_recv()
        total = far_ref[0]
        for j in range(1, 4):
            total = total + far_ref[j]
        for i, b in enumerate(ex.extra):
            far_ref[4 + 2 * i] = total
            trade = pltpu.make_async_remote_copy(
                src_ref=far_ref.at[4 + 2 * i],
                dst_ref=far_ref.at[5 + 2 * i],
                send_sem=far_sem.at[4 + i, 0],
                recv_sem=far_sem.at[4 + i, 1],
                device_id={"dp": flip(place, 1 << b)},
                device_id_type=MESH,
            )
            trade.start()
            trade.wait()
            total = total + far_ref[5 + 2 * i]
        sums_ref[...] = total

    actions = [give_main, give_edges, own_clean, tell_near, tell_far, take_back]
    ticks = [0, 2, 5, 8, 12, 13]

    def phase(p, _):
        for n, action in enumerate(actions):
            pl.when(p == n)(action)
        block = p - len(actions)

        @pl.when(jnp.logical_and(block >= 0, block < parts))
        def _():
            norm_back(block)

        pl.when(block == parts)(end_far)
        low = jnp.maximum(block, 0) + ticks[-1]
        high = low + 1
        for n in reversed(range(len(actions))):
            low = jnp.where(p == n, ticks[n], low)
            high = jnp.where(p == n, ticks[n + 1] if n + 1 < len(ticks) else ticks[n], high)
        lax.fori_loop(low, high, lambda i, _: (steps(i), 0)[1], 0)
        return 0

    lax.fori_loop(0, len(actions) + count + 10 - ticks[-1], phase, 0)


def leave(bits, mine, crossed, d_fields, weights, tokens, context, vectors, d_mid, small, small2):
    total = mine[0].shape[0] + mine[1].shape[0]
    rows, cols = mine[0].shape[1:]
    exchange = Exchange(bits, total, rows, cols)
    count, width = tokens.shape
    vmem = pl.BlockSpec(memory_space=pltpu.VMEM)
    hbm = pl.BlockSpec(memory_space=pl.ANY)
    shape = jax.ShapeDtypeStruct
    return pl.pallas_call(
        functools.partial(leave_kernel, exchange),
        in_specs=[vmem] * 4 + [hbm] * 4 + [vmem] * 3 + [hbm] + [vmem] * 2,
        out_specs=[vmem] * 3,
        out_shape=[
            shape((total, rows, cols), bf16),
            shape((count, width), f32),
            shape((16, width), f32),
        ],
        scratch_shapes=[
            pltpu.VMEM((total, rows, cols), bf16),
            pltpu.VMEM(d_fields[0].shape, bf16),
            pltpu.VMEM(d_fields[1].shape, bf16),
            pltpu.VMEM(weights[0].shape, bf16),
            pltpu.VMEM(weights[1].shape, bf16),
            pltpu.VMEM(d_mid.shape, f32),
            pltpu.SemaphoreType.DMA((5,)),
            pltpu.VMEM((count, width), f32),
            pltpu.VMEM((HALF + 2 * EDGE, width), bf16),
            pltpu.VMEM((HALF + 2 * EDGE, width), bf16),
            pltpu.SemaphoreType.DMA((2, 2)),
            pltpu.VMEM((8, width), f32),
            pltpu.VMEM((8, 16, width), f32),
            pltpu.VMEM((4 + 2 * len(exchange.extra), 16, width), f32),
            pltpu.SemaphoreType.DMA((8, 2)),
            pltpu.SemaphoreType.DMA((4 + len(exchange.extra), 2)),
        ]
        + exchange.scratch(),
        compiler_params=pltpu.CompilerParams(
            collective_id=1, has_side_effects=True, vmem_limit_bytes=67043328
        ),
        name="leave",
        cost_estimate=pl.CostEstimate(
            flops=40 * 10**9, bytes_accessed=40 * 10**6, transcendentals=0
        ),
    )(
        *mine, *crossed, *d_fields, *weights, tokens, context, vectors, d_mid, small, small2
    )


def key_layout(seq_lengths, block_len, part):
    index = jnp.arange(KEY_ROWS, dtype=jnp.int32)
    own = part * HALF
    token = jnp.where(
        index < NOISY_BASE, index + (own - HALF), index - NOISY_BASE + (own - EDGE)
    )
    ends = jnp.cumsum(seq_lengths)
    passed = token[:, None] >= ends[None, :]
    starts = jnp.sum(jnp.where(passed, seq_lengths[None, :], 0), axis=1)
    lengths_here = jnp.where(passed, 0, ends[None, :])
    stops = jnp.min(jnp.where(passed, TOK_DEV, lengths_here), axis=1)
    positions = token - starts
    block_start = starts + positions // block_len * block_len
    block_stop = jnp.minimum(block_start + block_len, stops)
    mine = slice(CLEAN_OWN, CLEAN_OWN + HALF)
    low, start, stop = starts[mine], block_start[mine], block_stop[mine]
    to_clean = own - HALF
    tiles = lambda column: column.reshape(TILES, 1, TILE)
    clean_bounds = jnp.concatenate(
        [
            jnp.concatenate([tiles(low - to_clean), tiles(low - to_clean)], axis=2),
            jnp.concatenate([tiles(start - to_clean), tiles(stop - to_clean)], axis=2),
        ],
        axis=1,
    )
    to_window = own - EDGE + TILE * jnp.arange(TILES, dtype=jnp.int32)[:, None, None]
    noisy_bounds = jnp.concatenate(
        [tiles(start) - to_window, tiles(stop) - to_window], axis=1
    )
    first = jnp.min(clean_bounds[:, 0], axis=1) // EDGE * EDGE
    last = jnp.max(clean_bounds[:, 1], axis=1)
    trips = (last - first + KEY_TILE - 1) // KEY_TILE
    spans = jnp.stack([first, trips], axis=1)
    lane = jnp.arange(LANES, dtype=jnp.int32)
    frequency = jnp.exp(
        (lane % (HD // 2)).astype(f32) * (-math.log(10000.0) / (HD // 2))
    )
    angles = positions.astype(f32)[:, None] * frequency[None, :]
    sign = jnp.where(lane % HD < HD // 2, -1.0, 1.0)
    return spans, clean_bounds, noisy_bounds, jnp.cos(angles), jnp.sin(angles) * sign


def in_order(bit, mine, theirs, axis=0):
    order = bit == 0
    return jnp.concatenate(
        [jnp.where(order, mine, theirs), jnp.where(order, theirs, mine)], axis=axis
    )


def tie(first, second):
    return lax.optimization_barrier((first, second))


def local(
    dp_size,
    tokens,
    lengths,
    block_size,
    cotangent,
    ln1_gain,
    ln1_bias,
    w_qkv,
    w_out,
    ln2_gain,
    ln2_bias,
    w_up,
    b_up,
    w_down,
    b_down,
):
    width = tokens.shape[2]
    part = lax.axis_index("mp")
    place = lax.axis_index("dp")
    bits = dp_size.bit_length() - 1
    core = place & 1

    def across(array):
        return lax.ppermute(array, "mp", [(0, 1), (1, 0)])

    def sibling(array):
        return lax.ppermute(array, "dp", [(i, i ^ 1) for i in range(dp_size)])

    def beside(array):
        return lax.ppermute(array, "dp", [(i, i ^ 2) for i in range(dp_size)])

    edge = jnp.where(part == 0, tokens[0, HALF - EDGE :], tokens[0, :EDGE])
    context = across(jnp.concatenate([tokens[1], edge], axis=0))
    qkv_mine = w_qkv.transpose(1, 0, 2)
    side = (place >> 1) & 1

    def quarter_of(array, axis=0):
        size = array.shape[axis] // 4
        return lax.dynamic_slice_in_dim(array, (2 * core + side) * size, size, axis)

    quarters = [
        quarter_of(qkv_mine, 1),
        quarter_of(w_up),
        quarter_of(w_down),
        quarter_of(w_out),
    ]
    layout = key_layout(lengths[0], block_size[0], part)
    vectors = jnp.stack([ln1_gain, ln1_bias, ln2_gain, ln2_bias, b_down])
    context, (quarters, layout, vectors) = tie(context, (quarters, layout, vectors))
    qkv_here, up_here, down_here, out_here = [across(piece) for piece in quarters]
    bias_other = across(b_up)

    spans, clean_bounds, noisy_bounds, cosine, sine = layout
    normed1, normed1_t, *fields = enter(tokens, context, vectors, qkv_mine, cosine, sine)
    qkv_here, fields = tie(qkv_here, fields)
    qkv_beside = beside(qkv_here)
    mine = [*fields, *attend_forward(spans, clean_bounds, noisy_bounds, *fields)]
    (qkv_here, qkv_beside, up_here), _ = tie((qkv_here, qkv_beside, up_here), mine[3])
    qkv_half = in_order(side, qkv_here, qkv_beside, axis=1)
    qkv_other = in_order(core, qkv_half, sibling(qkv_half), axis=1)
    up_beside = beside(up_here)
    fields = project(normed1, qkv_other, cosine, sine)
    (down_here, out_here), fields = tie((down_here, out_here), fields)
    out_beside = beside(out_here)
    down_beside = beside(down_here)
    other = [*fields, *attend_forward(spans, clean_bounds, noisy_bounds, *fields)]
    (out_here, out_beside, up_here, up_beside, down_here, down_beside, bias_other), _ = tie(
        (out_here, out_beside, up_here, up_beside, down_here, down_beside, bias_other), other[3]
    )
    out_half = in_order(side, out_here, out_beside)
    out_other = in_order(core, out_half, sibling(out_half))
    bias_all = jnp.concatenate([bias_other, b_up]).astype(f32).reshape(-1, 1, HIDDEN_TILE)

    x_rows = tokens.reshape(TOK_DEV, width)
    out, d_mid, d_att, d_att2, grad_out, grad_out2, grad_bias, norms, pieces = middle(
        bits,
        x_rows,
        mine[3],
        other[3],
        w_out,
        out_other,
        cotangent.reshape(TOK_DEV, width),
        vectors,
        bias_all,
        (w_up, up_here, up_beside),
        (w_down, down_here, down_beside),
    )
    hidden = b_up.shape[0]

    crossed_out = across(grad_out2)
    spread = [(b, min(2, min(bits, 4) - b)) for b in range(2, min(bits, 4), 2)]
    gathered = pieces
    ((first_bit, n),) = spread
    moved = [
        lax.ppermute(gathered, "dp", [(i, i ^ (k << first_bit)) for i in range(dp_size)])
        for k in range(1, 1 << n)
    ]

    def backward(saved, d_attended, spans):
        query, keys, values, attended, lse = saved
        return attend_backward(
            spans,
            clean_bounds,
            noisy_bounds,
            query,
            keys,
            values,
            attended,
            d_attended,
            lse,
            cosine,
            sine,
            normed1_t,
        )

    d_fields2, grad2 = backward(other, d_att2, spans)
    grad2 = grad2.reshape(-1, ROW_TILE, grad2.shape[2])
    low_bit, high_bit = (place >> 2) & 1, (place >> 3) & 1
    moved, _ = tie(moved, grad2)
    gathered = in_order(
        high_bit,
        in_order(low_bit, gathered, moved[0], 1),
        in_order(low_bit, moved[1], moved[2], 1),
        1,
    )
    half = ROW_TILE // 2
    part_of = lambda array, which: lax.dynamic_slice_in_dim(array, which * half, half, 1)
    got = sibling(part_of(grad2, 1 - core))
    crossing = (part_of(grad2, core).astype(f32) + got.astype(f32)).astype(bf16)
    (crossing, gathered), spans = tie((crossing, gathered), spans)
    crossed = across(crossing)
    moved = beside(gathered)
    d_fields1, grad1 = backward(mine, d_att, spans)
    grad1 = grad1.reshape(-1, ROW_TILE, grad1.shape[2])
    moved, grad1 = tie(moved, grad1)
    gathered = in_order(side, gathered, moved, 1)
    gathered, grad1 = tie(gathered, grad1)
    moved = sibling(gathered)
    lead = hidden // width
    bias2, bias1 = grad_bias.reshape(2, lead, width)
    shared = jnp.concatenate([norms[:3], jnp.zeros((2, width), f32)], axis=0)
    full, grad_tokens, sums = leave(
        bits,
        (grad1, grad_out.reshape(-1, ROW_TILE, grad_out.shape[1])),
        (crossed, crossed_out.reshape(-1, ROW_TILE, grad_out.shape[1])),
        (d_fields1, d_fields2),
        (qkv_mine, qkv_other),
        x_rows,
        context,
        vectors,
        d_mid,
        jnp.concatenate([bias1, shared], axis=0),
        jnp.concatenate([bias2, shared], axis=0),
    )
    moved, _ = tie(moved, full)
    gathered = in_order(core, gathered, moved, 1)
    count = hidden // HIDDEN_TILE
    grad_down = gathered[:count].reshape(hidden, width).astype(f32)
    grad_up = gathered[count:].reshape(count, PIECES, PIECES, width // HIDDEN_TILE, HIDDEN_TILE)
    grad_up = grad_up.transpose(1, 3, 2, 0, 4).reshape(width, hidden).astype(f32)
    split = 3 * width // ROW_TILE
    grad_qkv = full[:split].reshape(qkv_mine.shape).transpose(1, 0, 2).astype(f32)
    flat = full[split:].reshape(2, w_out.shape[0], width // 2)
    grad_out = jnp.concatenate([flat[0], flat[1]], axis=1).astype(f32)
    return (
        out.reshape(tokens.shape),
        grad_tokens.reshape(tokens.shape),
        sums[lead + 3],
        sums[lead + 4],
        grad_qkv,
        grad_out,
        sums[lead],
        sums[lead + 1],
        grad_up,
        sums[:lead].reshape(hidden),
        grad_down,
        sums[lead + 2],
    )


def solution(mesh):
    in_specs = (
        P(None, ("dp", "mp"), None),
        P("dp", None),
        P(),
        P(None, ("dp", "mp"), None),
        P(),
        P(),
        P(None, None, "mp"),
        P("mp", None),
        P(),
        P(),
        P(None, "mp"),
        P("mp"),
        P("mp", None),
        P(),
    )
    out_specs = (
        P(None, ("dp", "mp"), None),
        P(None, ("dp", "mp"), None),
        P(),
        P(),
        P(None, None, "mp"),
        P("mp", None),
        P(),
        P(),
        P(None, "mp"),
        P("mp"),
        P("mp", None),
        P(),
    )
    return jax.shard_map(
        functools.partial(local, mesh.shape["dp"]),
        mesh=mesh,
        in_specs=in_specs,
        out_specs=out_specs,
        check_vma=False,
    )
```

```python
import functools
import math

import jax
import jax.numpy as jnp
from jax import lax
from jax.experimental import pallas as pl
from jax.experimental.pallas import tpu as pltpu
from jax.sharding import PartitionSpec as P

HD = 64
TOK_DEV = 1024
HALF = TOK_DEV // 2
EDGE = 16
CLEAN_OWN = HALF
NOISY_BASE = 2 * HALF + EDGE
NOISY_OWN = NOISY_BASE + EDGE
KEY_ROWS = NOISY_OWN + HALF + EDGE
TILE = 128
TILES = HALF // TILE
WINDOW = TILE + 2 * EDGE
KEY_TILE = 192
LANES = 128
HIDDEN_TILE = 256
ROW_TILE = 256

epsilon = 1e-05
neg_large = -1e30
to_base2 = 0.125 * math.log2(math.e)
f32 = jnp.float32
bf16 = jnp.bfloat16

NN = (((1,), (0,)), ((), ()))
NT = (((1,), (1,)), ((), ()))


def dot(left, right, dims=NN):
    return lax.dot_general(left, right, dims, preferred_element_type=f32)


def low_lanes(shape):
    return lax.broadcasted_iota(jnp.int32, shape, 1) < HD


def turn(values, cosine, sine):
    lane = lax.broadcasted_iota(jnp.int32, values.shape, 1)
    first_half = (lane & (HD - 1)) < HD // 2
    swapped = jnp.where(
        first_half,
        pltpu.roll(values, LANES - HD // 2, 1),
        pltpu.roll(values, HD // 2, 1),
    )
    return values * cosine + swapped * sine


def project_rows(rows, w_ref, cosine, sine, q_ref, k_ref, v_ref, at):
    for part, out_ref in ((0, q_ref), (1, k_ref)):
        field = dot(rows, w_ref[part])
        for pair in range(field.shape[1] // LANES):
            cols = slice(pair * LANES, (pair + 1) * LANES)
            out_ref[at, cols] = turn(field[:, cols], cosine, sine).astype(bf16)
    v_ref[at, :] = dot(rows, w_ref[2]).astype(bf16)


def project_kernel(rows_ref, w_ref, cos_ref, sin_ref, q_ref, k_ref, v_ref):
    at = slice(0, rows_ref.shape[0])
    project_rows(rows_ref[...], w_ref, cos_ref[...], sin_ref[...], q_ref, k_ref, v_ref, at)


def project(rows, weights, cosine, sine):
    count, width = rows.shape
    cols = weights.shape[2]
    step = count // 3
    row_spec = pl.BlockSpec((step, width), lambda i: (i, 0))
    table_spec = pl.BlockSpec((step, LANES), lambda i: (i, 0))
    out_spec = pl.BlockSpec((step, cols), lambda i: (i, 0))
    shape = jax.ShapeDtypeStruct((count, cols), bf16)
    return pl.pallas_call(
        project_kernel,
        grid=(3,),
        in_specs=[
            row_spec,
            pl.BlockSpec(weights.shape, lambda i: (0, 0, 0)),
            table_spec,
            table_spec,
        ],
        out_specs=[out_spec] * 3,
        out_shape=[shape] * 3,
        name="project",
        cost_estimate=pl.CostEstimate(
            flops=2 * count * width * 3 * cols,
            bytes_accessed=2 * (count * (width + 3 * cols) + 3 * width * cols),
            transcendentals=0,
        ),
    )(rows, weights, cosine, sine)


def normal(values):
    average = jnp.mean(values, axis=-1, keepdims=True)
    centred = values - average
    variance = jnp.mean(centred * centred, axis=-1, keepdims=True)
    scale = lax.rsqrt(variance + epsilon)
    return centred * scale, scale


def enter_kernel(
    tokens_ref,
    context_ref,
    vectors_ref,
    w_ref,
    cos_ref,
    sin_ref,
    rows_ref,
    rows_t_ref,
    q_ref,
    k_ref,
    v_ref,
):
    def norm(values):
        unit = normal(values.astype(f32))[0]
        return (unit * vectors_ref[0:1, :] + vectors_ref[1:2, :]).astype(bf16)

    def blocks(i, _):
        source = pl.ds(pl.multiple_of(i * TILE, TILE), TILE)
        rows_ref[source, :] = norm(context_ref[source, :])
        at = pl.ds(pl.multiple_of(CLEAN_OWN + i * TILE, TILE), TILE)
        rows_ref[at, :] = norm(tokens_ref[1, source, :])
        at = pl.ds(pl.multiple_of(NOISY_OWN + i * TILE, EDGE), TILE)
        rows_ref[at, :] = norm(tokens_ref[0, source, :])
        return 0

    lax.fori_loop(0, TILES, blocks, 0)
    rows_ref[2 * HALF : NOISY_BASE, :] = rows_ref[:EDGE, :]
    edge = norm(context_ref[HALF:, :])
    rows_ref[NOISY_BASE:NOISY_OWN, :] = edge
    rows_ref[NOISY_OWN + HALF :, :] = edge
    step = KEY_ROWS // 3

    def fields(i, _):
        at = pl.ds(pl.multiple_of(i * step, EDGE), step)
        project_rows(
            rows_ref[at, :], w_ref, cos_ref[at, :], sin_ref[at, :], q_ref, k_ref, v_ref, at
        )
        return 0

    lax.fori_loop(0, 3, fields, 0)
    for c in range(rows_t_ref.shape[0] // LANES):
        cols = slice(c * LANES, (c + 1) * LANES)
        rows_t_ref[cols, :] = rows_ref[:, cols].T


def enter(tokens, context, vectors, weights, cosine, sine):
    width, cols = weights.shape[1:]
    vmem = pl.BlockSpec(memory_space=pltpu.VMEM)
    shape = jax.ShapeDtypeStruct
    field = shape((KEY_ROWS, cols), bf16)
    return pl.pallas_call(
        enter_kernel,
        in_specs=[vmem] * 6,
        out_specs=[vmem] * 5,
        out_shape=[shape((KEY_ROWS, width), bf16), shape((width, KEY_ROWS), bf16)] + [field] * 3,
        name="enter",
        cost_estimate=pl.CostEstimate(
            flops=10**10, bytes_accessed=16 * 10**6, transcendentals=0
        ),
    )(tokens, context, vectors, weights, cosine, sine)


def split_heads(rows):
    low = low_lanes(rows.shape)
    zero = jnp.zeros_like(rows)
    return jnp.where(low, rows, zero), jnp.where(low, zero, rows)


def between(shape, offset, low, high):
    index = lax.broadcasted_iota(jnp.int32, shape, 0) + offset
    return jnp.logical_and(index >= low, index < high)


def fold(values, combine):
    rows, cols = values.shape
    groups = values.reshape(rows // 8, 8, cols)
    return combine(groups, axis=0)


def forward_kernel(
    span_ref, clean_ref, noisy_ref, q_ref, k_ref, v_ref, out_ref, lse_ref, bias_ref, window_ref
):
    pairs = q_ref.shape[1] // LANES
    lanes = [slice(p * LANES, (p + 1) * LANES) for p in range(pairs)]

    def one_tile(t, _):
        clean_at = pl.multiple_of(CLEAN_OWN + t * TILE, TILE)
        noisy_at = pl.multiple_of(NOISY_OWN + t * TILE, EDGE)
        window_at = pl.multiple_of(NOISY_BASE + t * TILE, EDGE)
        key_low, key_high = clean_ref[t, 0:1, :], clean_ref[t, 1:2, :]
        own_low, own_high = noisy_ref[t, 0:1, :], noisy_ref[t, 1:2, :]
        allowed = between((WINDOW, TILE), 0, own_low, own_high)
        window_ref[...] = jnp.where(allowed, 0.0, neg_large)
        first_key, trips = span_ref[t, 0], span_ref[t, 1]
        queries, tops = [], []
        for cols in lanes:
            query = jnp.concatenate(
                [q_ref[pl.ds(noisy_at, TILE), cols], q_ref[pl.ds(clean_at, TILE), cols]], axis=0
            )
            heads = split_heads(query)
            queries += heads
            keys = k_ref[pl.ds(window_at, WINDOW), cols]
            for head in range(2):
                scores = dot(keys, heads[head][:TILE], NT) + window_ref[...]
                top = fold(scores, jnp.max)
                tops.append(
                    jnp.concatenate([top, jnp.full((8, TILE), neg_large, f32)], axis=1)
                )

        def first_pass(j, tops):
            at = pl.multiple_of(first_key + j * KEY_TILE, EDGE)
            allowed = between((KEY_TILE, 2 * TILE), at, key_low, key_high)
            bias_ref[j] = jnp.where(allowed, 0.0, neg_large)
            after = []
            for p, cols in enumerate(lanes):
                keys = k_ref[pl.ds(at, KEY_TILE), cols]
                for head in range(2):
                    scores = dot(keys, queries[2 * p + head], NT) + bias_ref[j]
                    after.append(jnp.maximum(tops[2 * p + head], fold(scores, jnp.max)))
            return tuple(after)

        tops = lax.fori_loop(0, trips, first_pass, tuple(tops))
        tops = [jnp.max(top, axis=0, keepdims=True) * to_base2 for top in tops]
        state = []
        keys = [k_ref[pl.ds(window_at, WINDOW), cols] for cols in lanes]
        values_t = [v_ref[pl.ds(window_at, WINDOW), cols].T for cols in lanes]
        scores = dot(keys[0], queries[0][:TILE], NT)
        late = None
        for h in range(2 * pairs):
            if h + 1 < 2 * pairs:
                ahead = dot(keys[(h + 1) // 2], queries[h + 1][:TILE], NT)
            expo = jnp.exp2(scores * to_base2 - tops[h][:, :TILE] + window_ref[...])
            if late is not None:
                state.append(jnp.concatenate([late, jnp.zeros((HD, TILE), f32)], axis=1))
            total = fold(expo, jnp.sum)
            state.append(jnp.concatenate([total, jnp.zeros((8, TILE), f32)], axis=1))
            side = slice(h % 2 * HD, (h % 2 + 1) * HD)
            late = dot(values_t[h // 2][side], expo.astype(bf16))
            scores = ahead
        state.append(jnp.concatenate([late, jnp.zeros((HD, TILE), f32)], axis=1))

        def second_pass(j, state):
            at = pl.multiple_of(first_key + j * KEY_TILE, EDGE)
            keys = [k_ref[pl.ds(at, KEY_TILE), cols] for cols in lanes]
            values_t = [v_ref[pl.ds(at, KEY_TILE), cols].T for cols in lanes]
            after = list(state)
            scores = dot(keys[0], queries[0], NT)
            late = None
            for h in range(2 * pairs):
                ahead = dot(keys[(h + 1) // 2], queries[h + 1], NT) if h + 1 < 2 * pairs else None
                expo = jnp.exp2(scores * to_base2 - tops[h] + bias_ref[j])
                after[2 * h] = state[2 * h] + fold(expo, jnp.sum)
                if late is not None:
                    after[2 * h - 1] = state[2 * h - 1] + late
                side = slice(h % 2 * HD, (h % 2 + 1) * HD)
                late = dot(values_t[h // 2][side], expo.astype(bf16))
                scores = ahead
            after[-1] = state[-1] + late
            return tuple(after)

        state = lax.fori_loop(0, trips, second_pass, tuple(state))
        low_at = pl.ds(pl.multiple_of(t * TILE, TILE), TILE)
        high_at = pl.ds(pl.multiple_of(HALF + t * TILE, TILE), TILE)
        for p, cols in enumerate(lanes):
            halves = []
            for head in range(2):
                h = 2 * p + head
                total = jnp.sum(state[2 * h], axis=0, keepdims=True)
                halves.append(state[2 * h + 1] / total)
                lse_ref[p, t, head : head + 1, :] = tops[h] + jnp.log2(total)
            pair = jnp.concatenate(halves, axis=0).T.astype(bf16)
            out_ref[low_at, cols] = pair[:TILE]
            out_ref[high_at, cols] = pair[TILE:]
        return 0

    lax.fori_loop(0, TILES, one_tile, 0)


def attend_forward(spans, clean_bounds, noisy_bounds, query, keys, values):
    count, cols = query.shape
    pairs = cols // LANES
    vmem = pl.BlockSpec(memory_space=pltpu.VMEM)
    work = pairs * 2 * 2 * HALF * TOK_DEV
    return pl.pallas_call(
        forward_kernel,
        in_specs=[pl.BlockSpec(memory_space=pltpu.SMEM)] + [vmem] * 5,
        out_specs=[vmem] * 2,
        out_shape=[
            jax.ShapeDtypeStruct((TOK_DEV, cols), bf16),
            jax.ShapeDtypeStruct((pairs, TILES, 2, 2 * TILE), f32),
        ],
        scratch_shapes=[
            pltpu.VMEM((NOISY_BASE // KEY_TILE + 1, KEY_TILE, 2 * TILE), f32),
            pltpu.VMEM((WINDOW, TILE), f32),
        ],
        name="attend_forward",
        cost_estimate=pl.CostEstimate(
            flops=4 * work * HD, bytes_accessed=8 * count * cols, transcendentals=work
        ),
    )(spans, clean_bounds, noisy_bounds, query, keys, values)


def backward_kernel(
    span_ref,
    clean_ref,
    noisy_ref,
    q_ref,
    k_ref,
    v_ref,
    o_ref,
    d_ref,
    lse_ref,
    cos_ref,
    sin_ref,
    *refs,
):
    rows_ref, out_ref, grad_ref, dk_ref, dv_ref, bias_ref = refs if len(refs) == 6 else (
        None,
        refs[0],
        None,
        *refs[1:],
    )
    pairs = q_ref.shape[1] // LANES
    lanes = [slice(p * LANES, (p + 1) * LANES) for p in range(pairs)]
    dk_ref[...] = jnp.zeros_like(dk_ref)
    dv_ref[...] = jnp.zeros_like(dv_ref)
    out_ref[0] = jnp.zeros_like(out_ref[0])

    def one_tile(t, _):
        clean_at = pl.multiple_of(CLEAN_OWN + t * TILE, TILE)
        noisy_at = pl.multiple_of(NOISY_OWN + t * TILE, EDGE)
        window_at = pl.multiple_of(NOISY_BASE + t * TILE, EDGE)
        low_at = pl.multiple_of(t * TILE, TILE)
        high_at = pl.multiple_of(HALF + t * TILE, TILE)
        key_low, key_high = clean_ref[t, 0:1, :], clean_ref[t, 1:2, :]
        own_low, own_high = noisy_ref[t, 0:1, :], noisy_ref[t, 1:2, :]
        queries, d_outs, inners, lses = [], [], [], []
        for p, cols in enumerate(lanes):

            def both(ref, low, high):
                return jnp.concatenate(
                    [ref[pl.ds(low, TILE), cols], ref[pl.ds(high, TILE), cols]], axis=0
                )

            queries.append(split_heads(both(q_ref, noisy_at, clean_at)))
            d_rows = both(d_ref, low_at, high_at)
            o_rows = both(o_ref, low_at, high_at)
            product = (d_rows.astype(f32) * o_rows.astype(f32)).T
            d_outs.append(split_heads(d_rows))
            inners.append(
                [
                    jnp.sum(product[head * HD : (head + 1) * HD], axis=0, keepdims=True) * 0.125
                    for head in range(2)
                ]
            )
            lses.append([lse_ref[p, t, head : head + 1, :] for head in range(2)])

        def accumulate(at, rows, cols, allowed, d_query):
            bias_ref[:rows, :cols] = jnp.where(allowed, 0.0, neg_large)
            after = list(d_query)
            keys = [k_ref[pl.ds(at, rows), span] for span in lanes]
            eighth = [v_ref[pl.ds(at, rows), span] * jnp.asarray(0.125, bf16) for span in lanes]
            keys_t = [part.T for part in keys]
            stack = lambda parts: jnp.concatenate([part[:cols] for part in parts], axis=0)

            def begin(h):
                p, head = h // 2, h % 2
                return (
                    dot(keys[p], queries[p][head][:cols], NT),
                    dot(eighth[p], d_outs[p][head][:cols], NT),
                )

            def finish_pair(p, weights, d_scores):
                span = lanes[p]
                for head in range(2):
                    side = slice(head * HD, (head + 1) * HD)
                    h = 2 * p + head
                    after[h] = d_query[h] + dot(keys_t[p][side], d_scores[head])
                dv_ref[pl.ds(at, rows), span] += dot(
                    jnp.concatenate(weights, axis=1), stack(d_outs[p])
                )
                dk_ref[pl.ds(at, rows), span] += dot(
                    jnp.concatenate(d_scores, axis=1), stack(queries[p])
                )

            ready = begin(0)
            held = None
            weights, d_scores = [], []
            for h in range(2 * pairs):
                ahead = begin(h + 1) if h + 1 < 2 * pairs else None
                p, head = h // 2, h % 2
                scores = ready[0] * to_base2 - lses[p][head][:, :cols] + bias_ref[:rows, :cols]
                probs = jnp.exp2(scores)
                d_score = (probs * (ready[1] - inners[p][head][:, :cols])).astype(bf16)
                weights.append(probs.astype(bf16))
                d_scores.append(d_score)
                if held is not None:
                    finish_pair(*held)
                    held = None
                if head == 1:
                    held = (p, weights, d_scores)
                    weights, d_scores = [], []
                ready = ahead
            finish_pair(*held)
            return tuple(after)

        allowed = between((WINDOW, TILE), 0, own_low, own_high)
        zero = jnp.zeros((HD, TILE), f32)
        start = accumulate(window_at, WINDOW, TILE, allowed, (zero,) * (2 * pairs))
        start = tuple(jnp.concatenate([part, zero], axis=1) for part in start)
        first_key, trips = span_ref[t, 0], span_ref[t, 1]

        def one_step(j, d_query):
            at = pl.multiple_of(first_key + j * KEY_TILE, EDGE)
            allowed = between((KEY_TILE, 2 * TILE), at, key_low, key_high)
            return accumulate(at, KEY_TILE, 2 * TILE, allowed, d_query)

        d_query = lax.fori_loop(0, trips, one_step, start)
        for p, span in enumerate(lanes):
            pair = jnp.concatenate(d_query[2 * p : 2 * p + 2], axis=0).T
            for at, part in ((noisy_at, pair[:TILE]), (clean_at, pair[TILE:])):
                turned = turn(part, cos_ref[pl.ds(at, TILE), :], -sin_ref[pl.ds(at, TILE), :])
                out_ref[0, pl.ds(at, TILE), span] = turned.astype(bf16)
        return 0

    lax.fori_loop(0, TILES, one_tile, 0)
    step = KEY_ROWS // 9

    def finish(i, _):
        rows = pl.ds(pl.multiple_of(i * step, EDGE), step)
        for span in lanes:
            out_ref[1, rows, span] = turn(
                dk_ref[rows, span], cos_ref[rows, :], -sin_ref[rows, :]
            ).astype(bf16)
        out_ref[2, rows, :] = dv_ref[rows, :].astype(bf16)
        return 0

    lax.fori_loop(0, 9, finish, 0)

    def weight_rows(i, _):
        rows = pl.ds(pl.multiple_of(i * ROW_TILE, LANES), ROW_TILE)
        for c in range(3):
            grad_ref[c, rows, :] = dot(rows_ref[rows, :], out_ref[c]).astype(bf16)
        return 0

    if rows_ref is not None:
        lax.fori_loop(0, rows_ref.shape[0] // ROW_TILE, weight_rows, 0)


def attend_backward(
    spans,
    clean_bounds,
    noisy_bounds,
    query,
    keys,
    values,
    attended,
    d_attended,
    lse,
    cosine,
    sine,
    *rows_t,
):
    count, cols = query.shape
    vmem = pl.BlockSpec(memory_space=pltpu.VMEM)
    return pl.pallas_call(
        backward_kernel,
        in_specs=[pl.BlockSpec(memory_space=pltpu.SMEM)] + [vmem] * (10 + len(rows_t)),
        out_specs=[vmem] * (1 + len(rows_t)),
        scratch_shapes=[
            pltpu.VMEM((count, cols), f32),
            pltpu.VMEM((count, cols), f32),
            pltpu.VMEM((max(KEY_TILE, WINDOW), 2 * TILE), f32),
        ],
        out_shape=[
            jax.ShapeDtypeStruct((3, count, cols), bf16),
            *[jax.ShapeDtypeStruct((3, rows.shape[0], cols), bf16) for rows in rows_t],
        ],
        name="attend_backward",
        cost_estimate=pl.CostEstimate(
            flops=36 * 10**9, bytes_accessed=36 * 10**6, transcendentals=6 * 10**6
        ),
    )(
        spans,
        clean_bounds,
        noisy_bounds,
        query,
        keys,
        values,
        attended,
        d_attended,
        lse,
        cosine,
        sine,
        *rows_t,
    )


PIECES = 16
MESH = pl.DeviceIdType.MESH


def flip(value, mask):
    result = value
    for b in range(mask.bit_length()):
        if mask >> b & 1:
            result = result + (1 << b) * (1 - 2 * ((value // (1 << b)) % 2))
    return result


class Exchange:
    def __init__(self, bits, count, rows, width, back=True):
        self.bits, self.count, self.rows, self.width = bits, count, rows, width
        self.back = back
        self.half, self.quarter, self.piece = rows // 2, rows // 4, rows // PIECES
        self.extra = list(range(4, bits))

    def slots(self):
        return 8 + 2 * (6 if self.back else 4) + (3 if self.extra else 0)

    def scratch(self):
        k, w = self.count, self.width
        cross = k if not self.back else 1
        shapes = [
            pltpu.VMEM((k, 2 - self.back, self.half, w), bf16),
            pltpu.VMEM((cross, self.half, w), bf16),
            pltpu.VMEM((cross, self.half, w), bf16),
            pltpu.VMEM((k, self.quarter, w), bf16),
            pltpu.VMEM((k, self.quarter, w), bf16),
            pltpu.VMEM((k, self.quarter, w), f32),
            pltpu.VMEM((k, 3, self.piece, w), bf16),
            pltpu.VMEM((k, 3, self.piece, w), bf16),
        ]
        lanes_of = (1, 0, 1, 3, 3, 1, 1) if self.back else (2, 1, 1, 3, 0, 0, 0)
        for lanes in [lanes for lanes in lanes_of if lanes]:
            shapes += [pltpu.SemaphoreType.DMA((k, lanes))] * 2
        if self.extra:
            n = len(self.extra)
            shapes += [pltpu.VMEM((k, 2 * n, self.piece, w), bf16)]
            shapes += [pltpu.SemaphoreType.DMA((k, n))] * 2
        return shapes

    def bind(self, place, part, refs):
        (self.a_in, self.b_out, self.b_in, self.c_out, self.c_in, self.keep) = refs[:6]
        self.d_out, self.d_in = refs[6:8]
        names = "acdefg" if self.back else "abcd"
        self.sems = {name: (refs[8 + 2 * i], refs[9 + 2 * i]) for i, name in enumerate(names)}
        if self.extra:
            at = 8 + 2 * len(names)
            self.x_buf, self.x_send, self.x_recv = refs[at : at + 3]
        self.place, self.part = place, part
        self.core, self.x, self.z = place % 2, (place // 2) % 2, (place // 4) % 4
        self.sibling = {"dp": flip(place, 1)}
        self.beside = {"dp": flip(place, 2)}
        self.across = {"mp": 1 - part}
        self.peers = [{"dp": flip(place, j << 2)} for j in range(1, 4)]
        self.partners = [self.sibling, self.beside, self.across] + self.peers
        self.partners += [{"dp": flip(place, 1 << b)} for b in self.extra]
        return self

    def greet(self):
        barrier = pltpu.get_barrier_semaphore()
        for partner in self.partners:
            pl.semaphore_signal(barrier, inc=1, device_id=partner, device_id_type=MESH)
        pl.semaphore_wait(barrier, len(self.partners))

    def copy(self, name, k, lane, source, target, device):
        out, into = self.sems[name]
        return pltpu.make_async_remote_copy(
            src_ref=source,
            dst_ref=target,
            send_sem=out.at[k, lane],
            recv_sem=into.at[k, lane],
            device_id=device,
            device_id_type=MESH,
        )

    def rows_at(self, start, size):
        return pl.ds(pl.multiple_of(start, PIECES), size)

    def copy_a(self, k, lane, grads):
        source = grads.at[k, self.rows_at((1 - self.core) * self.half, self.half)]
        return self.copy("a", k, lane, source, self.a_in.at[k, lane], self.sibling)

    def copy_b(self, k):
        return self.copy("b", k, 0, self.b_out.at[k], self.b_in.at[k], self.across)

    def copy_c(self, k):
        return self.copy("c", k, 0, self.c_out.at[k], self.c_in.at[k], self.beside)

    def copy_d(self, k, j):
        return self.copy("d", k, j, self.d_out.at[k, j], self.d_in.at[k, j], self.peers[j])

    def spot(self, change=0):
        start = self.core * self.half + self.x * self.quarter
        return self.rows_at(start + flip(self.z, change) * self.piece, self.piece)

    def copy_e(self, k, j, full):
        rows = full.at[k, self.spot()]
        return self.copy("e", k, j, rows, rows, self.peers[j])

    def copy_f(self, k, full):
        start = self.core * self.half + self.x * self.quarter
        rows = full.at[k, self.rows_at(start, self.quarter)]
        return self.copy("f", k, 0, rows, rows, self.beside)

    def copy_g(self, k, full):
        rows = full.at[k, self.rows_at(self.core * self.half, self.half)]
        return self.copy("g", k, 0, rows, rows, self.sibling)

    def start_a(self, k, lane, grads):
        self.copy_a(k, lane, grads).start()

    def stage_b(self, k, others):
        self.copy_a(k, 0, others).wait()
        mine = others[k, self.rows_at(self.core * self.half, self.half), :].astype(f32)
        self.b_out[k] = (mine + self.a_in[k, 0].astype(f32)).astype(bf16)
        self.copy_b(k).start()

    def stage_c(self, k, grads, crossed=None):
        lane = 0 if self.back else 1
        self.copy_a(k, lane, grads).wait()
        if not self.back:
            self.copy_b(k).wait()

        def total(which):
            inner = which * self.quarter
            rows = self.rows_at(inner, self.quarter)
            mine = grads[k, self.rows_at(self.core * self.half + inner, self.quarter), :]
            got = self.a_in[k, lane, rows, :].astype(f32)
            if not self.back:
                got = got + self.b_in[k, rows, :].astype(f32)
            elif crossed is not None:
                got = got + crossed(rows)
            return mine.astype(f32) + got

        self.c_out[k] = total(1 - self.x).astype(bf16)
        self.copy_c(k).start()
        self.keep[k] = total(self.x)

    def stage_d(self, k):
        self.copy_c(k).wait()
        for j in range(4):
            rows = self.rows_at(flip(self.z, j) * self.piece, self.piece)
            total = self.keep[k, rows, :] + self.c_in[k, rows, :].astype(f32)
            if j:
                self.d_out[k, j - 1] = total.astype(bf16)
                self.copy_d(k, j - 1).start()
            else:
                self.keep[k, rows, :] = total

    def gather_d(self, k):
        rows = self.rows_at(self.z * self.piece, self.piece)
        total = self.keep[k, rows, :]
        for j in range(3):
            self.copy_d(k, j).wait()
            total = total + self.d_in[k, j].astype(f32)
        for i, b in enumerate(self.extra):
            mine = self.x_buf.at[k, 2 * i]
            mine[...] = total.astype(bf16)
            swap = pltpu.make_async_remote_copy(
                src_ref=mine,
                dst_ref=self.x_buf.at[k, 2 * i + 1],
                send_sem=self.x_send.at[k, i],
                recv_sem=self.x_recv.at[k, i],
                device_id={"dp": flip(self.place, 1 << b)},
                device_id_type=MESH,
            )
            swap.start()
            swap.wait()
            total = total.astype(bf16).astype(f32) + self.x_buf[k, 2 * i + 1].astype(f32)
        return total.astype(bf16)

    def stage_e(self, k, full):
        full[k, self.spot(), :] = self.gather_d(k)
        for j in range(3):
            self.copy_e(k, j, full).start()

    def stage_f(self, k, full):
        for j in range(3):
            self.copy_e(k, j, full).wait()
        self.copy_f(k, full).start()

    def stage_g(self, k, full):
        self.copy_f(k, full).wait()
        self.copy_g(k, full).start()

    def stage_h(self, k, full):
        self.copy_g(k, full).wait()


def at_step(step, count, action):
    @pl.when(jnp.logical_and(step >= 0, step < count))
    def _():
        action(step)


def middle_kernel(exchanges, tiles, *refs):
    (
        x_ref,
        att_ref,
        att2_ref,
        wout_ref,
        wout2_ref,
        dy_ref,
        vectors_ref,
        bup_ref,
        up_mine,
        up_here,
        up_beside,
        down_mine,
        down_here,
        down_beside,
        out_ref,
        mid_ref,
        datt_ref,
        datt2_ref,
        gout_ref,
        gout2_ref,
        gbup_ref,
        small_ref,
        pieces_ref,
        up_there,
        down_there,
        pass_up,
        pass_down,
        up_buf,
        down_buf,
        load_sem,
        n2_ref,
        total_ref,
        dn2_ref,
        act_ref,
        dpre_ref,
        n2_t,
        bup_other,
        bias_sem,
        down_grad,
        up_grad,
        *rest,
    ) = refs
    place, part = lax.axis_index("dp"), lax.axis_index("mp")
    ex = exchanges[0].bind(place, part, rest)
    ex_up = exchanges[1].bind(place, part, rest[exchanges[0].slots() :])
    sides = ((ex, down_grad), (ex_up, up_grad))
    core = ex.core
    count = tiles // 2
    rows_all = x_ref.shape[0]
    blocks = rows_all // ROW_TILE
    width = x_ref.shape[1]
    lanes = width // 2

    def which(i):
        other = jnp.logical_or(i == 0, jnp.logical_and(i % 2 == 1, i < tiles - 1))
        mine = jnp.where(i == tiles - 1, count - 1, i // 2 - 1)
        return other, jnp.where(other, (i + 1) // 2, mine)

    quarter = width // 4
    strip = HIDDEN_TILE // 2
    held = 2 * core + ex.x
    kept = 2 * core + 1 - ex.x

    def load_up(i, source, h):
        target = up_buf.at[i % 2, h * quarter : (h + 1) * quarter]
        return pltpu.make_async_copy(source, target, load_sem.at[i % 2, h])

    def load_down(i, source, h):
        target = down_buf.at[i % 2, h * strip : (h + 1) * strip]
        return pltpu.make_async_copy(source, target, load_sem.at[i % 2, 4 + h])

    def hand_up(k, part_of):
        cols = pl.ds(pl.multiple_of(k * HIDDEN_TILE, HIDDEN_TILE), HIDDEN_TILE)
        side = ex.x if part_of == 0 else 1 - ex.x
        rows = pl.ds(pl.multiple_of(side * quarter, EDGE), quarter)
        return pltpu.make_async_remote_copy(
            src_ref=(up_here, up_beside)[part_of].at[:, cols],
            dst_ref=up_there.at[k, rows],
            send_sem=pass_up.at[k, 2 * part_of],
            recv_sem=pass_up.at[k, 2 * part_of + 1],
            device_id=ex.sibling,
            device_id_type=MESH,
        )

    def hand_down(b, part_of):
        side = ex.x if part_of == 0 else 1 - ex.x
        return pltpu.make_async_remote_copy(
            src_ref=(down_here, down_beside)[part_of].at[strip_rows(b)],
            dst_ref=down_there.at[side * (count // 2) + b],
            send_sem=pass_down.at[side * (count // 2) + b, 0],
            recv_sem=pass_down.at[side * (count // 2) + b, 1],
            device_id=ex.sibling,
            device_id_type=MESH,
        )

    def strip_rows(b):
        return pl.ds(pl.multiple_of(b * strip, strip), strip)

    def got_down(slot):
        return pltpu.make_async_remote_copy(
            src_ref=down_there.at[slot],
            dst_ref=down_there.at[slot],
            send_sem=pass_down.at[slot, 0],
            recv_sem=pass_down.at[slot, 1],
            device_id=ex.sibling,
            device_id_type=MESH,
        )

    def start_loads(i):
        other, k = which(i)
        mine = jnp.logical_not(other)
        cols = pl.ds(pl.multiple_of(k * HIDDEN_TILE, HIDDEN_TILE), HIDDEN_TILE)
        span = count // 2

        @pl.when(other)
        def _():
            hand_up(k, 0).wait()
            hand_up(k, 1).wait()

        for h in range(4):

            @pl.when(mine)
            def _():
                load_up(i, up_mine.at[h * quarter : (h + 1) * quarter, cols], h).start()

            @pl.when(jnp.logical_and(other, held == h))
            def _():
                load_up(i, up_here.at[:, cols], h).start()

            @pl.when(jnp.logical_and(other, kept == h))
            def _():
                load_up(i, up_beside.at[:, cols], h).start()

            @pl.when(jnp.logical_and(other, core != h // 2))
            def _():
                rows = slice(h % 2 * quarter, (h % 2 + 1) * quarter)
                load_up(i, up_there.at[k, rows], h).start()

        for h in range(2):
            b = 2 * k + h
            piece, inner = b // span, b % span

            @pl.when(mine)
            def _():
                load_down(i, down_mine.at[strip_rows(b), :], h).start()

            @pl.when(jnp.logical_and(other, held == piece))
            def _():
                load_down(i, down_here.at[strip_rows(inner), :], h).start()

            @pl.when(jnp.logical_and(other, kept == piece))
            def _():
                load_down(i, down_beside.at[strip_rows(inner), :], h).start()

            @pl.when(jnp.logical_and(other, core != piece // 2))
            def _():
                slot = piece % 2 * span + inner
                got_down(slot).wait_recv()
                load_down(i, down_there.at[slot], h).start()

    def wait_loads(i):
        for h in range(4):
            load_up(i, up_mine.at[:quarter, :HIDDEN_TILE], h).wait()
        for h in range(2):
            load_down(i, down_mine.at[:strip, :], h).wait()

    ex.greet()
    bias_swap = pltpu.make_async_remote_copy(
        src_ref=bup_ref,
        dst_ref=bup_other,
        send_sem=bias_sem.at[0],
        recv_sem=bias_sem.at[1],
        device_id=ex.across,
        device_id_type=MESH,
    )
    bias_swap.start()

    def hand(k, _):
        hand_up(k, 0).start()
        hand_up(k, 1).start()

        @pl.when(k < count // 2)
        def _():
            hand_down(k, 0).start()
            hand_down(k, 1).start()

        return 0

    lax.fori_loop(0, count, hand, 0)

    def prologue(r, _):
        rows = pl.ds(pl.multiple_of(r * ROW_TILE, ROW_TILE), ROW_TILE)
        branch = dot(att_ref[rows, :], wout_ref[...]) + dot(att2_ref[rows, :], wout2_ref[...])
        mid = x_ref[rows, :].astype(f32) + branch
        mid_ref[rows, :] = mid
        unit = normal(mid)[0]
        n2_ref[rows, :] = (unit * vectors_ref[2:3, :] + vectors_ref[3:4, :]).astype(bf16)
        total_ref[rows, :] = mid + vectors_ref[4:5, :]
        dn2_ref[rows, :] = jnp.zeros((ROW_TILE, width), f32)
        return 0

    lax.fori_loop(0, blocks, prologue, 0)
    start_loads(0)
    for c in range(width // LANES):
        cols = slice(c * LANES, (c + 1) * LANES)
        n2_t[cols, :] = n2_ref[:, cols].T
    n2_t[width:, :] = jnp.ones((PIECES, rows_all), bf16)
    bias_swap.wait()

    def tile(i):
        other, k = which(i)
        slot = i % 2
        wait_loads(i)

        @pl.when(i + 1 < tiles)
        def _():
            start_loads(i + 1)

        up, down = up_buf.at[slot], down_buf.at[slot]
        bias_at = jnp.where(other, k, count + k)
        bias = jnp.where(other, bup_other[k], bup_ref[k])
        linear = 0.7978845608028654
        cubic = linear * 0.044715
        block = lambda r: slice(r * ROW_TILE, (r + 1) * ROW_TILE)

        def begin(r):
            return dot(n2_ref[block(r), :], up[...]), dot(dy_ref[block(r), :], down[...], NT)

        ready = begin(0)
        for r in range(blocks):
            rows = block(r)
            ahead = begin(r + 1) if r + 1 < blocks else None
            pre = ready[0] + bias
            square = pre * pre
            bend = jnp.tanh(pre * (square * cubic + linear))
            gate = 0.5 * bend + 0.5
            full_act = pre * gate
            slope = gate + (full_act - full_act * gate) * (square * (6.0 * cubic) + 2.0 * linear)
            act = full_act.astype(bf16)
            d_pre = (ready[1] * slope).astype(bf16)
            act_ref[rows, :] = act
            dpre_ref[rows, :] = d_pre
            total_ref[rows, :] += dot(act, down[...])
            dn2_ref[rows, :] += dot(d_pre, up[...], NT)
            ready = ahead
        down_grad[k] = dot(act_ref[...].T, dy_ref[...]).astype(bf16)

        def start(lane):
            for side, grad in sides:
                side.start_a(k, lane, grad)

        by_rows = dot(n2_t[...], dpre_ref[...])
        up_grad[k] = by_rows[:width].astype(bf16)
        gbup_ref[bias_at] = by_rows[width : width + 1]
        pl.when(other)(functools.partial(start, 0))
        pl.when(jnp.logical_not(other))(functools.partial(start, 1))

    def each(k, when, action):
        @pl.when(jnp.logical_and(when, jnp.logical_and(k >= 0, k < count)))
        def _():
            for n, (side, grad) in enumerate(sides):
                action(n, side, grad, k)

    def stage_b(n, side, grad, k):
        side.stage_b(k, grad)

    def stage_c(n, side, grad, k):
        side.stage_c(k, grad)

    def stage_d(n, side, grad, k):
        side.stage_d(k)

    def arrive(n, side, grad, k):
        piece = side.gather_d(k)
        if n == 0:
            pieces_ref[k] = piece
        else:
            for c in range(width // HIDDEN_TILE):
                cols = slice(c * HIDDEN_TILE, (c + 1) * HIDDEN_TILE)
                pieces_ref[count + k, :, cols] = piece[c * PIECES : (c + 1) * PIECES]

    def steps(i):
        even = i % 2 == 0
        odd = jnp.logical_not(even)
        each((i - 6) // 2, even, arrive)
        each((i - 5) // 2, odd, stage_d)
        each((i - 4) // 2, even, stage_c)
        each(i // 2, even, stage_b)

    def epilogue(r, _):
        rows = pl.ds(pl.multiple_of(r * ROW_TILE, ROW_TILE), ROW_TILE)
        out_ref[rows, :] = total_ref[rows, :].astype(bf16)
        unit, scale = normal(mid_ref[rows, :])
        d_rows = dn2_ref[rows, :]
        dy = dy_ref[rows, :].astype(f32)
        lean = d_rows * vectors_ref[2:3, :]
        d_mid = dy + scale * (
            lean
            - jnp.mean(lean, axis=-1, keepdims=True)
            - unit * jnp.mean(lean * unit, axis=-1, keepdims=True)
        )
        mid_ref[rows, :] = d_mid
        d_branch = d_mid.astype(bf16)
        n2_ref[rows, :] = d_branch
        datt_ref[rows, :] = dot(d_branch, wout_ref[...], NT).astype(bf16)
        datt2_ref[rows, :] = dot(d_branch, wout2_ref[...], NT).astype(bf16)
        add = lambda values: jnp.sum(values, axis=0, keepdims=True)
        small_ref[0:1, :] += add(d_rows * unit)
        small_ref[1:2, :] += add(d_rows)
        small_ref[2:3, :] += add(dy)
        return 0

    def out_grads():
        depth = wout_ref.shape[0]
        for source, target in ((att_ref, gout_ref), (att2_ref, gout2_ref)):
            grad = dot(source[...].T, n2_ref[...]).astype(bf16)
            target[:depth, :] = grad[:, :lanes]
            target[depth:, :] = grad[:, lanes:]

    def main(i, _):
        pl.when(i < tiles)(functools.partial(tile, i))

        @pl.when(jnp.logical_and(i >= tiles, i < tiles + 2))
        def _():
            first = (i - tiles) * (blocks // 2)
            lax.fori_loop(first, first + blocks // 2, epilogue, 0)

        pl.when(i == tiles + 2)(out_grads)
        steps(i)
        return 0

    small_ref[...] = jnp.zeros_like(small_ref)
    lax.fori_loop(0, tiles + 5, main, 0)

    def handed(slot, _):
        got_down(slot).wait_send()
        return 0

    lax.fori_loop(0, count, handed, 0)


def middle(bits, x, att, att2, wout, wout2, dy, vectors, bup, ups, downs):
    rows, width = x.shape
    hidden = ups[0].shape[1]
    count = hidden // HIDDEN_TILE
    tiles = 2 * count
    exchanges = (
        Exchange(bits, count, HIDDEN_TILE, width, False),
        Exchange(bits, count, width, HIDDEN_TILE, False),
    )
    vmem = pl.BlockSpec(memory_space=pltpu.VMEM)
    hbm = pl.BlockSpec(memory_space=pl.ANY)
    shape = jax.ShapeDtypeStruct
    depth = wout.shape[0]
    return pl.pallas_call(
        functools.partial(middle_kernel, exchanges, tiles),
        in_specs=[vmem] * 8 + [hbm] * 6,
        out_specs=[vmem] * 9,
        out_shape=[
            shape((rows, width), bf16),
            shape((rows, width), f32),
            shape(att.shape, bf16),
            shape(att2.shape, bf16),
            shape((2 * depth, width // 2), bf16),
            shape((2 * depth, width // 2), bf16),
            shape((tiles, 1, HIDDEN_TILE), f32),
            shape((8, width), f32),
            shape((2 * count, PIECES, width), bf16),
        ],
        scratch_shapes=[
            pltpu.VMEM((count, width // 2, HIDDEN_TILE), bf16),
            pltpu.VMEM((count, HIDDEN_TILE // 2, width), bf16),
            pltpu.SemaphoreType.DMA((count, 4)),
            pltpu.SemaphoreType.DMA((count, 2)),
            pltpu.VMEM((2, width, HIDDEN_TILE), bf16),
            pltpu.VMEM((2, HIDDEN_TILE, width), bf16),
            pltpu.SemaphoreType.DMA((2, 6)),
            pltpu.VMEM((rows, width), bf16),
            pltpu.VMEM((rows, width), f32),
            pltpu.VMEM((rows, width), f32),
            pltpu.VMEM((rows, HIDDEN_TILE), bf16),
            pltpu.VMEM((rows, HIDDEN_TILE), bf16),
            pltpu.VMEM((width + PIECES, rows), bf16),
            pltpu.VMEM(bup.shape, f32),
            pltpu.SemaphoreType.DMA((2,)),
            pltpu.VMEM((count, HIDDEN_TILE, width), bf16),
            pltpu.VMEM((count, width, HIDDEN_TILE), bf16),
        ]
        + exchanges[0].scratch()
        + exchanges[1].scratch(),
        compiler_params=pltpu.CompilerParams(
            collective_id=0, has_side_effects=True, vmem_limit_bytes=67043328
        ),
        name="middle",
        cost_estimate=pl.CostEstimate(
            flops=60 * 10**9, bytes_accessed=40 * 10**6, transcendentals=4 * 10**6
        ),
    )(x, att, att2, wout, wout2, dy, vectors, bup, *ups, *downs)


def leave_kernel(exchange, *refs):
    (
        rows_hbm,
        mine_out_ref,
        crossed_ref,
        crossed_out_ref,
        d_hbm,
        d2_hbm,
        w_hbm,
        w2_hbm,
        tokens_ref,
        context_ref,
        vectors_ref,
        dmid_hbm,
        small_ref,
        small2_ref,
        full_ref,
        back_ref,
        sums_ref,
        out_buf,
        rows_t_ref,
        d_ref,
        d2_ref,
        w_ref,
        w2_ref,
        dmid_ref,
        load_sem,
        rows_ref,
        give_ref,
        take_ref,
        swap_sem,
        norm_ref,
        near_ref,
        far_ref,
        near_sem,
        far_sem,
        *rest,
    ) = refs
    place, part = lax.axis_index("dp"), lax.axis_index("mp")
    ex = exchange.bind(place, part, rest)
    count, bits = ex.count, ex.bits
    first = mine_out_ref.shape[0]
    loads = [
        pltpu.make_async_copy(source, target, load_sem.at[n])
        for n, (source, target) in enumerate(
            (
                (w_hbm, w_ref),
                (d_hbm, d_ref),
                (w2_hbm, w2_ref),
                (d2_hbm, d2_ref),
                (rows_hbm, rows_t_ref),
                (dmid_hbm, dmid_ref),
            )
        )
    ]
    for load in loads:
        load.start()
    near_id = part * 4 + place % 4
    near = [
        {"dp": flip(place, j % 4), "mp": part if j < 4 else 1 - part} for j in range(1, 8)
    ]
    ex.partners += [near[j - 1] for j in (3, 5, 6, 7)]
    ex.greet()

    def begin_out(k, _):
        total = mine_out_ref[k].astype(f32) + crossed_out_ref[k].astype(f32)
        out_buf[k] = total.astype(bf16)
        ex.start_a(k, 0, out_buf)
        return 0

    lax.fori_loop(0, first, begin_out, 0)
    step = KEY_ROWS // 3

    def back_rows(n):
        rows = pl.ds(pl.multiple_of(n * step, EDGE), step)
        total = 0.0
        for grads, weights in ((d_ref, w_ref), (d2_ref, w2_ref)):
            for c in range(3):
                total = total + dot(grads[c, rows, :], weights[c], NT)
        rows_ref[rows, :] = total

    def grad_chunk(j):
        parts = rows_t_ref.shape[0] // ROW_TILE
        rows = pl.ds(pl.multiple_of(j % parts * ROW_TILE, ROW_TILE), ROW_TILE)
        out_buf[first + j] = dot(rows_t_ref[rows, :], d_ref[j // parts]).astype(bf16)
        ex.start_a(first + j, 0, out_buf)

    def stage_c(k):
        @pl.when(k >= first)
        def _():
            ex.stage_c(k, out_buf, lambda rows: crossed_ref[k - first, rows, :].astype(f32))

        @pl.when(k < first)
        def _():
            ex.stage_c(k, out_buf)

    def steps(i):
        at_step(i - 10, count, lambda k: ex.stage_h(k, full_ref))
        at_step(i - 8, count, lambda k: ex.stage_g(k, full_ref))
        at_step(i - 6, count, lambda k: ex.stage_f(k, full_ref))
        at_step(i - 4, count, lambda k: ex.stage_e(k, full_ref))
        at_step(i - 2, count, lambda k: ex.stage_d(k))
        at_step(i, count, stage_c)

    width = tokens_ref.shape[1]

    def swap(rows, lane):
        return pltpu.make_async_remote_copy(
            src_ref=give_ref.at[rows],
            dst_ref=take_ref.at[rows],
            send_sem=swap_sem.at[lane, 0],
            recv_sem=swap_sem.at[lane, 1],
            device_id=ex.across,
            device_id_type=MESH,
        )

    def sums_of(d_rows, units):
        add = lambda values: jnp.sum(values, axis=0, keepdims=True)
        norm_ref[0:1, :] += add(d_rows * units)
        norm_ref[1:2, :] += add(d_rows)

    main = slice(0, HALF)
    edges = slice(HALF, HALF + 2 * EDGE)
    parts = tokens_ref.shape[0] // TILE
    lead = small_ref.shape[0] - 2
    bias = lead - 3
    norm_ref[...] = jnp.zeros_like(norm_ref)
    for load in loads[:4]:
        load.wait()

    def own_at(b):
        start = jnp.where(b < TILES, NOISY_OWN + b * TILE, CLEAN_OWN + (b - TILES) * TILE)
        return pl.ds(pl.multiple_of(start, EDGE), TILE)

    def tokens_at(b):
        return pl.ds(pl.multiple_of(b * TILE, TILE), TILE)

    def give_main():
        give_ref[main, :] = rows_ref[main, :].astype(bf16)
        swap(main, 0).start()
        loads[4].wait()

    def give_edges():
        side = rows_ref[NOISY_BASE:NOISY_OWN, :] + rows_ref[NOISY_OWN + HALF :, :]
        after = rows_ref[2 * HALF : NOISY_BASE, :]
        give_ref[HALF : HALF + EDGE, :] = after.astype(bf16)
        give_ref[HALF + EDGE :, :] = side.astype(bf16)
        swap(edges, 1).start()
        sums_of(after, normal(context_ref[:EDGE, :].astype(f32))[0])
        sums_of(side, normal(context_ref[HALF:, :].astype(f32))[0])

    def tell_near():
        def context_sums(b, _):
            rows = tokens_at(b)
            sums_of(rows_ref[rows, :], normal(context_ref[rows, :].astype(f32))[0])
            return 0

        lax.fori_loop(0, HALF // TILE, context_sums, 0)

        def own_sums(b, _):
            sums_of(rows_ref[own_at(b), :], normal(tokens_ref[tokens_at(b), :].astype(f32))[0])
            return 0

        lax.fori_loop(0, parts, own_sums, 0)
        mine = near_ref.at[near_id]
        mine[:lead, :] = small_ref[:lead, :]
        mine[lead : lead + 2, :] = norm_ref[:2, :]
        mine[lead + 2 : lead + 2 + bias, :] = small2_ref[:bias, :]
        rest_rows = 16 - lead - 2 - bias
        mine[16 - rest_rows :, :] = jnp.zeros((rest_rows, width), f32)
        for j in range(1, 8):
            near_copy(j).start()

    def near_copy(j):
        return pltpu.make_async_remote_copy(
            src_ref=near_ref.at[near_id],
            dst_ref=near_ref.at[near_id],
            send_sem=near_sem.at[j, 0],
            recv_sem=near_sem.at[j, 1],
            device_id=near[j - 1],
            device_id_type=MESH,
        )

    def near_got(j):
        came = (part + j // 4) % 2 * 4 + flip(place % 4, j % 4)
        return pltpu.make_async_remote_copy(
            src_ref=near_ref.at[came],
            dst_ref=near_ref.at[came],
            send_sem=near_sem.at[j, 0],
            recv_sem=near_sem.at[j, 1],
            device_id=near[j - 1],
            device_id_type=MESH,
        )

    def far_copy(j, at):
        return pltpu.make_async_remote_copy(
            src_ref=far_ref.at[at],
            dst_ref=far_ref.at[at],
            send_sem=far_sem.at[j, 0],
            recv_sem=far_sem.at[j, 1],
            device_id=ex.peers[j - 1],
            device_id_type=MESH,
        )

    def tell_far():
        for j in range(1, 8):
            near_copy(j).wait_send()
            near_got(j).wait_recv()
        total = near_ref[0]
        for j in range(1, 8):
            total = total + near_ref[j]
        plane = near_ref[part * 4]
        other = near_ref[(1 - part) * 4]
        for j in range(1, 4):
            plane = plane + near_ref[part * 4 + j]
            other = other + near_ref[(1 - part) * 4 + j]
        spot = far_ref.at[ex.z]
        spot[...] = total
        spot[:bias, :] = plane[:bias] + other[lead + 2 : lead + 2 + bias]
        for j in range(1, 4):
            far_copy(j, ex.z).start()

    def take_back():
        loads[5].wait()
        swap(main, 0).wait()
        swap(edges, 1).wait()
        clean = slice(CLEAN_OWN, CLEAN_OWN + HALF)
        rows_ref[clean, :] += take_ref[main, :].astype(f32)
        begin = slice(CLEAN_OWN, CLEAN_OWN + EDGE)
        rows_ref[begin, :] += take_ref[HALF : HALF + EDGE, :].astype(f32)
        edge = pl.ds(pl.multiple_of(NOISY_OWN + (1 - part) * (HALF - EDGE), EDGE), EDGE)
        rows_ref[edge, :] += take_ref[HALF + EDGE :, :].astype(f32)

    def norm_back(b):
        rows = tokens_at(b)
        unit, scale = normal(tokens_ref[rows, :].astype(f32))
        lean = rows_ref[own_at(b), :] * vectors_ref[0:1, :]
        back_ref[rows, :] = dmid_ref[rows, :] + scale * (
            lean
            - jnp.mean(lean, axis=-1, keepdims=True)
            - unit * jnp.mean(lean * unit, axis=-1, keepdims=True)
        )

    def end_far():
        for j in range(1, 4):
            far_copy(j, ex.z).wait_send()
            far_copy(j, flip(ex.z, j)).wait_recv()
        total = far_ref[0]
        for j in range(1, 4):
            total = total + far_ref[j]
        for i, b in enumerate(ex.extra):
            far_ref[4 + 2 * i] = total
            trade = pltpu.make_async_remote_copy(
                src_ref=far_ref.at[4 + 2 * i],
                dst_ref=far_ref.at[5 + 2 * i],
                send_sem=far_sem.at[4 + i, 0],
                recv_sem=far_sem.at[4 + i, 1],
                device_id={"dp": flip(place, 1 << b)},
                device_id_type=MESH,
            )
            trade.start()
            trade.wait()
            total = total + far_ref[5 + 2 * i]
        sums_ref[...] = total

    chunks = count - first
    begin_chunks, end_chunks = 1, 1 + chunks
    actions = {
        0: give_main,
        end_chunks + 1: give_edges,
        end_chunks + 2: tell_near,
        end_chunks + 3: tell_far,
        end_chunks + 4: take_back,
    }
    begin_back = end_chunks + 5

    def phase(p, _):
        back = jnp.logical_or(p == 0, jnp.logical_or(p == end_chunks, p == end_chunks + 1))

        @pl.when(back)
        def _():
            back_rows(jnp.where(p == 0, 0, p - end_chunks + 1))

        @pl.when(jnp.logical_and(p >= begin_chunks, p < end_chunks))
        def _():
            grad_chunk(p - begin_chunks)

        for n, action in actions.items():
            pl.when(p == n)(action)
        block = p - begin_back

        @pl.when(jnp.logical_and(block >= 0, block < parts))
        def _():
            norm_back(block)

        pl.when(block == parts)(end_far)
        steps(p - 1)
        return 0

    lax.fori_loop(0, max(begin_back + parts + 1, count + 11), phase, 0)


def leave(bits, rows_t, mine, crossed, d_fields, weights, tokens, context, vectors, d_mid, small, small2):
    total = mine.shape[0] + crossed[0].shape[0]
    rows, cols = mine.shape[1:]
    exchange = Exchange(bits, total, rows, cols)
    count, width = tokens.shape
    vmem = pl.BlockSpec(memory_space=pltpu.VMEM)
    hbm = pl.BlockSpec(memory_space=pl.ANY)
    shape = jax.ShapeDtypeStruct
    return pl.pallas_call(
        functools.partial(leave_kernel, exchange),
        in_specs=[hbm] + [vmem] * 3 + [hbm] * 4 + [vmem] * 3 + [hbm] + [vmem] * 2,
        out_specs=[vmem] * 3,
        out_shape=[
            shape((total, rows, cols), bf16),
            shape((count, width), f32),
            shape((16, width), f32),
        ],
        scratch_shapes=[
            pltpu.VMEM((total, rows, cols), bf16),
            pltpu.VMEM(rows_t.shape, bf16),
            pltpu.VMEM(d_fields[0].shape, bf16),
            pltpu.VMEM(d_fields[1].shape, bf16),
            pltpu.VMEM(weights[0].shape, bf16),
            pltpu.VMEM(weights[1].shape, bf16),
            pltpu.VMEM(d_mid.shape, f32),
            pltpu.SemaphoreType.DMA((6,)),
            pltpu.VMEM((KEY_ROWS, width), f32),
            pltpu.VMEM((HALF + 2 * EDGE, width), bf16),
            pltpu.VMEM((HALF + 2 * EDGE, width), bf16),
            pltpu.SemaphoreType.DMA((2, 2)),
            pltpu.VMEM((8, width), f32),
            pltpu.VMEM((8, 16, width), f32),
            pltpu.VMEM((4 + 2 * len(exchange.extra), 16, width), f32),
            pltpu.SemaphoreType.DMA((8, 2)),
            pltpu.SemaphoreType.DMA((4 + len(exchange.extra), 2)),
        ]
        + exchange.scratch(),
        compiler_params=pltpu.CompilerParams(
            collective_id=1, has_side_effects=True, vmem_limit_bytes=67043328
        ),
        name="leave",
        cost_estimate=pl.CostEstimate(
            flops=40 * 10**9, bytes_accessed=40 * 10**6, transcendentals=0
        ),
    )(
        rows_t, mine, *crossed, *d_fields, *weights, tokens, context, vectors, d_mid, small, small2
    )


def assemble_kernel(core_ref, down_mine, up_mine, down_got, up_got, down_ref, up_ref):
    core = core_ref[0]
    block = down_mine.shape[1]
    lanes = up_ref.shape[1]
    parts = down_mine.shape[2] // lanes
    deep = block * parts
    for side, down, up in ((core, down_mine, up_mine), (1 - core, down_got, up_got)):
        rows = pl.ds(pl.multiple_of(side * block, block), block)
        down_ref[rows, :] = down[0].astype(f32)
        for n in range(block // PIECES):
            for c in range(parts):
                at = side * deep + (n * parts + c) * PIECES
                rows = pl.ds(pl.multiple_of(at, PIECES), PIECES)
                piece = up[0, n * PIECES : (n + 1) * PIECES, c * lanes : (c + 1) * lanes]
                up_ref[rows, :] = piece.astype(f32)


def assemble(core, gathered, moved):
    tiles, half, width = gathered.shape
    count = tiles // 2
    down_spec = pl.BlockSpec((1, half, width), lambda k, c: (k, 0, 0))
    up_spec = pl.BlockSpec((1, half, width), lambda k, c: (count + k, 0, 0))
    hidden = count * 2 * half
    return pl.pallas_call(
        assemble_kernel,
        grid_spec=pltpu.PrefetchScalarGridSpec(
            num_scalar_prefetch=1,
            grid=(count,),
            in_specs=[down_spec, up_spec, down_spec, up_spec],
            out_specs=[
                pl.BlockSpec((2 * half, width), lambda k, c: (k, 0)),
                pl.BlockSpec((width, 2 * half), lambda k, c: (0, k)),
            ],
        ),
        out_shape=[
            jax.ShapeDtypeStruct((hidden, width), f32),
            jax.ShapeDtypeStruct((width, hidden), f32),
        ],
        name="assemble",
        cost_estimate=pl.CostEstimate(
            flops=10**6, bytes_accessed=14 * 10**6, transcendentals=0
        ),
    )(core, gathered, gathered, moved, moved)


def key_layout(seq_lengths, block_len, part):
    index = jnp.arange(KEY_ROWS, dtype=jnp.int32)
    own = part * HALF
    token = jnp.where(
        index < NOISY_BASE, index + (own - HALF), index - NOISY_BASE + (own - EDGE)
    )
    ends = jnp.cumsum(seq_lengths)
    passed = token[:, None] >= ends[None, :]
    starts = jnp.sum(jnp.where(passed, seq_lengths[None, :], 0), axis=1)
    lengths_here = jnp.where(passed, 0, ends[None, :])
    stops = jnp.min(jnp.where(passed, TOK_DEV, lengths_here), axis=1)
    positions = token - starts
    block_start = starts + positions // block_len * block_len
    block_stop = jnp.minimum(block_start + block_len, stops)
    mine = slice(CLEAN_OWN, CLEAN_OWN + HALF)
    low, start, stop = starts[mine], block_start[mine], block_stop[mine]
    to_clean = own - HALF
    tiles = lambda column: column.reshape(TILES, 1, TILE)
    clean_bounds = jnp.concatenate(
        [
            jnp.concatenate([tiles(low - to_clean), tiles(low - to_clean)], axis=2),
            jnp.concatenate([tiles(start - to_clean), tiles(stop - to_clean)], axis=2),
        ],
        axis=1,
    )
    to_window = own - EDGE + TILE * jnp.arange(TILES, dtype=jnp.int32)[:, None, None]
    noisy_bounds = jnp.concatenate(
        [tiles(start) - to_window, tiles(stop) - to_window], axis=1
    )
    first = jnp.min(clean_bounds[:, 0], axis=1) // EDGE * EDGE
    last = jnp.max(clean_bounds[:, 1], axis=1)
    trips = (last - first + KEY_TILE - 1) // KEY_TILE
    spans = jnp.stack([first, trips], axis=1)
    lane = jnp.arange(LANES, dtype=jnp.int32)
    frequency = jnp.exp(
        (lane % (HD // 2)).astype(f32) * (-math.log(10000.0) / (HD // 2))
    )
    angles = positions.astype(f32)[:, None] * frequency[None, :]
    sign = jnp.where(lane % HD < HD // 2, -1.0, 1.0)
    return spans, clean_bounds, noisy_bounds, jnp.cos(angles), jnp.sin(angles) * sign


def in_order(bit, mine, theirs, axis=0):
    order = bit == 0
    return jnp.concatenate(
        [jnp.where(order, mine, theirs), jnp.where(order, theirs, mine)], axis=axis
    )


def tie(first, second):
    return lax.optimization_barrier((first, second))


def local(
    dp_size,
    tokens,
    lengths,
    block_size,
    cotangent,
    ln1_gain,
    ln1_bias,
    w_qkv,
    w_out,
    ln2_gain,
    ln2_bias,
    w_up,
    b_up,
    w_down,
    b_down,
):
    width = tokens.shape[2]
    part = lax.axis_index("mp")
    place = lax.axis_index("dp")
    bits = dp_size.bit_length() - 1
    core = place & 1

    def across(array):
        return lax.ppermute(array, "mp", [(0, 1), (1, 0)])

    def sibling(array):
        return lax.ppermute(array, "dp", [(i, i ^ 1) for i in range(dp_size)])

    def beside(array):
        return lax.ppermute(array, "dp", [(i, i ^ 2) for i in range(dp_size)])

    edge = jnp.where(part == 0, tokens[0, HALF - EDGE :], tokens[0, :EDGE])
    context = across(jnp.concatenate([tokens[1], edge], axis=0))
    qkv_mine = w_qkv.transpose(1, 0, 2)
    side = (place >> 1) & 1

    def quarter_of(array, axis=0):
        size = array.shape[axis] // 4
        return lax.dynamic_slice_in_dim(array, (2 * core + side) * size, size, axis)

    quarters = [
        quarter_of(qkv_mine, 1),
        quarter_of(w_up),
        quarter_of(w_down),
        quarter_of(w_out),
    ]
    layout = key_layout(lengths[0], block_size[0], part)
    vectors = jnp.stack([ln1_gain, ln1_bias, ln2_gain, ln2_bias, b_down])
    context, (quarters, layout, vectors) = tie(context, (quarters, layout, vectors))
    qkv_here, up_here, down_here, out_here = [across(piece) for piece in quarters]

    spans, clean_bounds, noisy_bounds, cosine, sine = layout
    normed1, normed1_t, *fields = enter(tokens, context, vectors, qkv_mine, cosine, sine)
    qkv_here, fields = tie(qkv_here, fields)
    qkv_beside = beside(qkv_here)
    mine = [*fields, *attend_forward(spans, clean_bounds, noisy_bounds, *fields)]
    (qkv_here, qkv_beside, up_here), _ = tie((qkv_here, qkv_beside, up_here), mine[3])
    qkv_half = in_order(side, qkv_here, qkv_beside, axis=1)
    qkv_other = in_order(core, qkv_half, sibling(qkv_half), axis=1)
    up_beside = beside(up_here)
    fields = project(normed1, qkv_other, cosine, sine)
    (down_here, out_here), fields = tie((down_here, out_here), fields)
    out_beside = beside(out_here)
    down_beside = beside(down_here)
    other = [*fields, *attend_forward(spans, clean_bounds, noisy_bounds, *fields)]
    (out_here, out_beside, up_here, up_beside, down_here, down_beside), _ = tie(
        (out_here, out_beside, up_here, up_beside, down_here, down_beside), other[3]
    )
    out_half = in_order(side, out_here, out_beside)
    out_other = in_order(core, out_half, sibling(out_half))
    bias_all = b_up.astype(f32).reshape(-1, 1, HIDDEN_TILE)

    x_rows = tokens.reshape(TOK_DEV, width)
    out, d_mid, d_att, d_att2, grad_out, grad_out2, grad_bias, norms, pieces = middle(
        bits,
        x_rows,
        mine[3],
        other[3],
        w_out,
        out_other,
        cotangent.reshape(TOK_DEV, width),
        vectors,
        bias_all,
        (w_up, up_here, up_beside),
        (w_down, down_here, down_beside),
    )
    hidden = b_up.shape[0]

    crossed_out = across(grad_out2)
    spread = [(b, min(2, min(bits, 4) - b)) for b in range(2, min(bits, 4), 2)]
    gathered = pieces
    ((first_bit, n),) = spread
    moved = [
        lax.ppermute(gathered, "dp", [(i, i ^ (k << first_bit)) for i in range(dp_size)])
        for k in range(1, 1 << n)
    ]

    def backward(saved, d_attended, spans, *rows_t):
        query, keys, values, attended, lse = saved
        return attend_backward(
            spans,
            clean_bounds,
            noisy_bounds,
            query,
            keys,
            values,
            attended,
            d_attended,
            lse,
            cosine,
            sine,
            *rows_t,
        )

    d_fields2, grad2 = backward(other, d_att2, spans, normed1_t)
    grad2 = grad2.reshape(-1, ROW_TILE, grad2.shape[2])
    low_bit, high_bit = (place >> 2) & 1, (place >> 3) & 1
    moved, _ = tie(moved, grad2)
    gathered = in_order(
        high_bit,
        in_order(low_bit, gathered, moved[0], 1),
        in_order(low_bit, moved[1], moved[2], 1),
        1,
    )
    half = ROW_TILE // 2
    part_of = lambda array, which: lax.dynamic_slice_in_dim(array, which * half, half, 1)
    got = sibling(part_of(grad2, 1 - core))
    crossing = (part_of(grad2, core).astype(f32) + got.astype(f32)).astype(bf16)
    (crossing, gathered), spans = tie((crossing, gathered), spans)
    crossed = across(crossing)
    moved = beside(gathered)
    (d_fields1,) = backward(mine, d_att, spans)
    moved, d_fields1 = tie(moved, d_fields1)
    gathered = in_order(side, gathered, moved, 1)
    gathered, d_fields1 = tie(gathered, d_fields1)
    moved = sibling(gathered)
    lead = hidden // width
    bias2, bias1 = grad_bias.reshape(2, lead, width)
    shared = jnp.concatenate([norms[:3], jnp.zeros((2, width), f32)], axis=0)
    full, grad_tokens, sums = leave(
        bits,
        normed1_t,
        grad_out.reshape(-1, ROW_TILE, grad_out.shape[1]),
        (crossed, crossed_out.reshape(-1, ROW_TILE, grad_out.shape[1])),
        (d_fields1, d_fields2),
        (qkv_mine, qkv_other),
        x_rows,
        context,
        vectors,
        d_mid,
        jnp.concatenate([bias1, shared], axis=0),
        jnp.concatenate([bias2, shared], axis=0),
    )
    moved, _ = tie(moved, full)
    grad_down, grad_up = assemble(core.reshape(1), gathered, moved)
    split = grad_out.shape[0] // ROW_TILE
    flat = full[:split].reshape(2, w_out.shape[0], width // 2)
    grad_out = jnp.concatenate([flat[0], flat[1]], axis=1).astype(f32)
    grad_qkv = full[split:].reshape(qkv_mine.shape).transpose(1, 0, 2).astype(f32)
    return (
        out.reshape(tokens.shape),
        grad_tokens.reshape(tokens.shape),
        sums[lead + 3],
        sums[lead + 4],
        grad_qkv,
        grad_out,
        sums[lead],
        sums[lead + 1],
        grad_up,
        sums[:lead].reshape(hidden),
        grad_down,
        sums[lead + 2],
    )


def solution(mesh):
    in_specs = (
        P(None, ("dp", "mp"), None),
        P("dp", None),
        P(),
        P(None, ("dp", "mp"), None),
        P(),
        P(),
        P(None, None, "mp"),
        P("mp", None),
        P(),
        P(),
        P(None, "mp"),
        P("mp"),
        P("mp", None),
        P(),
    )
    out_specs = (
        P(None, ("dp", "mp"), None),
        P(None, ("dp", "mp"), None),
        P(),
        P(),
        P(None, None, "mp"),
        P("mp", None),
        P(),
        P(),
        P(None, "mp"),
        P("mp"),
        P("mp", None),
        P(),
    )
    return jax.shard_map(
        functools.partial(local, mesh.shape["dp"]),
        mesh=mesh,
        in_specs=in_specs,
        out_specs=out_specs,
        check_vma=False,
    )
```

```python
import functools
import math

import jax
import jax.numpy as jnp
from jax import lax
from jax.experimental import pallas as pl
from jax.experimental.pallas import tpu as pltpu
from jax.sharding import PartitionSpec as P

HD = 64
TOK_DEV = 1024
HALF = TOK_DEV // 2
EDGE = 16
CLEAN_OWN = HALF
NOISY_BASE = 2 * HALF + EDGE
NOISY_OWN = NOISY_BASE + EDGE
KEY_ROWS = NOISY_OWN + HALF + EDGE
TILE = 128
TILES = HALF // TILE
WINDOW = TILE + 2 * EDGE
KEY_TILE = 192
LANES = 128
HIDDEN_TILE = 256
ROW_TILE = 256

epsilon = 1e-05
neg_large = -1e30
to_base2 = 0.125 * math.log2(math.e)
f32 = jnp.float32
bf16 = jnp.bfloat16

NN = (((1,), (0,)), ((), ()))
NT = (((1,), (1,)), ((), ()))


def dot(left, right, dims=NN):
    return lax.dot_general(left, right, dims, preferred_element_type=f32)


def low_lanes(shape):
    return lax.broadcasted_iota(jnp.int32, shape, 1) < HD


def turn(values, cosine, sine):
    lane = lax.broadcasted_iota(jnp.int32, values.shape, 1)
    first_half = (lane & (HD - 1)) < HD // 2
    swapped = jnp.where(
        first_half,
        pltpu.roll(values, LANES - HD // 2, 1),
        pltpu.roll(values, HD // 2, 1),
    )
    return values * cosine + swapped * sine


def project_rows(rows, w_ref, cosine, sine, q_ref, k_ref, v_ref, at):
    for part, out_ref in ((0, q_ref), (1, k_ref)):
        field = dot(rows, w_ref[part])
        for pair in range(field.shape[1] // LANES):
            cols = slice(pair * LANES, (pair + 1) * LANES)
            out_ref[at, cols] = turn(field[:, cols], cosine, sine).astype(bf16)
    v_ref[at, :] = dot(rows, w_ref[2]).astype(bf16)


def project_kernel(rows_ref, w_ref, cos_ref, sin_ref, q_ref, k_ref, v_ref):
    at = slice(0, rows_ref.shape[0])
    project_rows(rows_ref[...], w_ref, cos_ref[...], sin_ref[...], q_ref, k_ref, v_ref, at)


def project(rows, weights, cosine, sine):
    count, width = rows.shape
    cols = weights.shape[2]
    step = count // 3
    row_spec = pl.BlockSpec((step, width), lambda i: (i, 0))
    table_spec = pl.BlockSpec((step, LANES), lambda i: (i, 0))
    out_spec = pl.BlockSpec((step, cols), lambda i: (i, 0))
    shape = jax.ShapeDtypeStruct((count, cols), bf16)
    return pl.pallas_call(
        project_kernel,
        grid=(3,),
        in_specs=[
            row_spec,
            pl.BlockSpec(weights.shape, lambda i: (0, 0, 0)),
            table_spec,
            table_spec,
        ],
        out_specs=[out_spec] * 3,
        out_shape=[shape] * 3,
        name="project",
        cost_estimate=pl.CostEstimate(
            flops=2 * count * width * 3 * cols,
            bytes_accessed=2 * (count * (width + 3 * cols) + 3 * width * cols),
            transcendentals=0,
        ),
    )(rows, weights, cosine, sine)


def normal(values):
    average = jnp.mean(values, axis=-1, keepdims=True)
    centred = values - average
    variance = jnp.mean(centred * centred, axis=-1, keepdims=True)
    scale = lax.rsqrt(variance + epsilon)
    return centred * scale, scale


def enter_kernel(
    tokens_ref,
    context_ref,
    vectors_ref,
    w_ref,
    cos_ref,
    sin_ref,
    rows_ref,
    rows_t_ref,
    q_ref,
    k_ref,
    v_ref,
):
    def norm(values):
        unit = normal(values.astype(f32))[0]
        return (unit * vectors_ref[0:1, :] + vectors_ref[1:2, :]).astype(bf16)

    def blocks(i, _):
        source = pl.ds(pl.multiple_of(i * TILE, TILE), TILE)
        rows_ref[source, :] = norm(context_ref[source, :])
        at = pl.ds(pl.multiple_of(CLEAN_OWN + i * TILE, TILE), TILE)
        rows_ref[at, :] = norm(tokens_ref[1, source, :])
        at = pl.ds(pl.multiple_of(NOISY_OWN + i * TILE, EDGE), TILE)
        rows_ref[at, :] = norm(tokens_ref[0, source, :])
        return 0

    lax.fori_loop(0, TILES, blocks, 0)
    rows_ref[2 * HALF : NOISY_BASE, :] = rows_ref[:EDGE, :]
    edge = norm(context_ref[HALF:, :])
    rows_ref[NOISY_BASE:NOISY_OWN, :] = edge
    rows_ref[NOISY_OWN + HALF :, :] = edge
    step = KEY_ROWS // 3

    def fields(i, _):
        at = pl.ds(pl.multiple_of(i * step, EDGE), step)
        project_rows(
            rows_ref[at, :], w_ref, cos_ref[at, :], sin_ref[at, :], q_ref, k_ref, v_ref, at
        )
        return 0

    lax.fori_loop(0, 3, fields, 0)
    for c in range(rows_t_ref.shape[0] // LANES):
        cols = slice(c * LANES, (c + 1) * LANES)
        rows_t_ref[cols, :] = rows_ref[:, cols].T


def enter(tokens, context, vectors, weights, cosine, sine):
    width, cols = weights.shape[1:]
    vmem = pl.BlockSpec(memory_space=pltpu.VMEM)
    shape = jax.ShapeDtypeStruct
    field = shape((KEY_ROWS, cols), bf16)
    return pl.pallas_call(
        enter_kernel,
        in_specs=[vmem] * 6,
        out_specs=[vmem] * 5,
        out_shape=[shape((KEY_ROWS, width), bf16), shape((width, KEY_ROWS), bf16)] + [field] * 3,
        name="enter",
        cost_estimate=pl.CostEstimate(
            flops=10**10, bytes_accessed=16 * 10**6, transcendentals=0
        ),
    )(tokens, context, vectors, weights, cosine, sine)


def split_heads(rows):
    low = low_lanes(rows.shape)
    zero = jnp.zeros_like(rows)
    return jnp.where(low, rows, zero), jnp.where(low, zero, rows)


def between(shape, offset, low, high):
    index = lax.broadcasted_iota(jnp.int32, shape, 0) + offset
    return jnp.logical_and(index >= low, index < high)


def fold(values, combine):
    rows, cols = values.shape
    groups = values.reshape(rows // 8, 8, cols)
    return combine(groups, axis=0)


def forward_kernel(
    span_ref, clean_ref, noisy_ref, q_ref, k_ref, v_ref, out_ref, lse_ref, bias_ref, window_ref
):
    pairs = q_ref.shape[1] // LANES
    lanes = [slice(p * LANES, (p + 1) * LANES) for p in range(pairs)]

    def one_tile(t, _):
        clean_at = pl.multiple_of(CLEAN_OWN + t * TILE, TILE)
        noisy_at = pl.multiple_of(NOISY_OWN + t * TILE, EDGE)
        window_at = pl.multiple_of(NOISY_BASE + t * TILE, EDGE)
        key_low, key_high = clean_ref[t, 0:1, :], clean_ref[t, 1:2, :]
        own_low, own_high = noisy_ref[t, 0:1, :], noisy_ref[t, 1:2, :]
        allowed = between((WINDOW, TILE), 0, own_low, own_high)
        window_ref[...] = jnp.where(allowed, 0.0, neg_large)
        first_key, trips = span_ref[t, 0], span_ref[t, 1]
        queries, tops = [], []
        for cols in lanes:
            query = jnp.concatenate(
                [q_ref[pl.ds(noisy_at, TILE), cols], q_ref[pl.ds(clean_at, TILE), cols]], axis=0
            )
            heads = split_heads(query)
            queries += heads
            keys = k_ref[pl.ds(window_at, WINDOW), cols]
            for head in range(2):
                scores = dot(keys, heads[head][:TILE], NT) + window_ref[...]
                top = fold(scores, jnp.max)
                tops.append(
                    jnp.concatenate([top, jnp.full((8, TILE), neg_large, f32)], axis=1)
                )

        def first_pass(j, tops):
            at = pl.multiple_of(first_key + j * KEY_TILE, EDGE)
            allowed = between((KEY_TILE, 2 * TILE), at, key_low, key_high)
            bias_ref[j] = jnp.where(allowed, 0.0, neg_large)
            after = []
            for p, cols in enumerate(lanes):
                keys = k_ref[pl.ds(at, KEY_TILE), cols]
                for head in range(2):
                    scores = dot(keys, queries[2 * p + head], NT) + bias_ref[j]
                    after.append(jnp.maximum(tops[2 * p + head], fold(scores, jnp.max)))
            return tuple(after)

        tops = lax.fori_loop(0, trips, first_pass, tuple(tops))
        tops = [jnp.max(top, axis=0, keepdims=True) * to_base2 for top in tops]
        state = []
        keys = [k_ref[pl.ds(window_at, WINDOW), cols] for cols in lanes]
        values_t = [v_ref[pl.ds(window_at, WINDOW), cols].T for cols in lanes]
        scores = dot(keys[0], queries[0][:TILE], NT)
        late = None
        for h in range(2 * pairs):
            if h + 1 < 2 * pairs:
                ahead = dot(keys[(h + 1) // 2], queries[h + 1][:TILE], NT)
            expo = jnp.exp2(scores * to_base2 - tops[h][:, :TILE] + window_ref[...])
            if late is not None:
                state.append(jnp.concatenate([late, jnp.zeros((HD, TILE), f32)], axis=1))
            total = fold(expo, jnp.sum)
            state.append(jnp.concatenate([total, jnp.zeros((8, TILE), f32)], axis=1))
            side = slice(h % 2 * HD, (h % 2 + 1) * HD)
            late = dot(values_t[h // 2][side], expo.astype(bf16))
            scores = ahead
        state.append(jnp.concatenate([late, jnp.zeros((HD, TILE), f32)], axis=1))

        def second_pass(j, state):
            at = pl.multiple_of(first_key + j * KEY_TILE, EDGE)
            keys = [k_ref[pl.ds(at, KEY_TILE), cols] for cols in lanes]
            values_t = [v_ref[pl.ds(at, KEY_TILE), cols].T for cols in lanes]
            after = list(state)
            scores = dot(keys[0], queries[0], NT)
            late = None
            for h in range(2 * pairs):
                ahead = dot(keys[(h + 1) // 2], queries[h + 1], NT) if h + 1 < 2 * pairs else None
                expo = jnp.exp2(scores * to_base2 - tops[h] + bias_ref[j])
                after[2 * h] = state[2 * h] + fold(expo, jnp.sum)
                if late is not None:
                    after[2 * h - 1] = state[2 * h - 1] + late
                side = slice(h % 2 * HD, (h % 2 + 1) * HD)
                late = dot(values_t[h // 2][side], expo.astype(bf16))
                scores = ahead
            after[-1] = state[-1] + late
            return tuple(after)

        state = lax.fori_loop(0, trips, second_pass, tuple(state))
        low_at = pl.ds(pl.multiple_of(t * TILE, TILE), TILE)
        high_at = pl.ds(pl.multiple_of(HALF + t * TILE, TILE), TILE)
        for p, cols in enumerate(lanes):
            halves = []
            for head in range(2):
                h = 2 * p + head
                total = jnp.sum(state[2 * h], axis=0, keepdims=True)
                halves.append(state[2 * h + 1] / total)
                lse_ref[p, t, head : head + 1, :] = tops[h] + jnp.log2(total)
            pair = jnp.concatenate(halves, axis=0).T.astype(bf16)
            out_ref[low_at, cols] = pair[:TILE]
            out_ref[high_at, cols] = pair[TILE:]
        return 0

    lax.fori_loop(0, TILES, one_tile, 0)


def attend_forward(spans, clean_bounds, noisy_bounds, query, keys, values):
    count, cols = query.shape
    pairs = cols // LANES
    vmem = pl.BlockSpec(memory_space=pltpu.VMEM)
    work = pairs * 2 * 2 * HALF * TOK_DEV
    return pl.pallas_call(
        forward_kernel,
        in_specs=[pl.BlockSpec(memory_space=pltpu.SMEM)] + [vmem] * 5,
        out_specs=[vmem] * 2,
        out_shape=[
            jax.ShapeDtypeStruct((TOK_DEV, cols), bf16),
            jax.ShapeDtypeStruct((pairs, TILES, 2, 2 * TILE), f32),
        ],
        scratch_shapes=[
            pltpu.VMEM((NOISY_BASE // KEY_TILE + 1, KEY_TILE, 2 * TILE), f32),
            pltpu.VMEM((WINDOW, TILE), f32),
        ],
        name="attend_forward",
        cost_estimate=pl.CostEstimate(
            flops=4 * work * HD, bytes_accessed=8 * count * cols, transcendentals=work
        ),
    )(spans, clean_bounds, noisy_bounds, query, keys, values)


def backward_kernel(
    span_ref,
    clean_ref,
    noisy_ref,
    q_ref,
    k_ref,
    v_ref,
    o_ref,
    d_ref,
    lse_ref,
    cos_ref,
    sin_ref,
    *refs,
):
    rows_ref, out_ref, grad_ref, dk_ref, dv_ref, bias_ref = refs if len(refs) == 6 else (
        None,
        refs[0],
        None,
        *refs[1:],
    )
    pairs = q_ref.shape[1] // LANES
    lanes = [slice(p * LANES, (p + 1) * LANES) for p in range(pairs)]
    dk_ref[...] = jnp.zeros_like(dk_ref)
    dv_ref[...] = jnp.zeros_like(dv_ref)
    out_ref[0] = jnp.zeros_like(out_ref[0])

    def one_tile(t, _):
        clean_at = pl.multiple_of(CLEAN_OWN + t * TILE, TILE)
        noisy_at = pl.multiple_of(NOISY_OWN + t * TILE, EDGE)
        window_at = pl.multiple_of(NOISY_BASE + t * TILE, EDGE)
        low_at = pl.multiple_of(t * TILE, TILE)
        high_at = pl.multiple_of(HALF + t * TILE, TILE)
        key_low, key_high = clean_ref[t, 0:1, :], clean_ref[t, 1:2, :]
        own_low, own_high = noisy_ref[t, 0:1, :], noisy_ref[t, 1:2, :]
        queries, d_outs, inners, lses = [], [], [], []
        for p, cols in enumerate(lanes):

            def both(ref, low, high):
                return jnp.concatenate(
                    [ref[pl.ds(low, TILE), cols], ref[pl.ds(high, TILE), cols]], axis=0
                )

            queries.append(split_heads(both(q_ref, noisy_at, clean_at)))
            d_rows = both(d_ref, low_at, high_at)
            o_rows = both(o_ref, low_at, high_at)
            product = (d_rows.astype(f32) * o_rows.astype(f32)).T
            d_outs.append(split_heads(d_rows))
            inners.append(
                [
                    jnp.sum(product[head * HD : (head + 1) * HD], axis=0, keepdims=True) * 0.125
                    for head in range(2)
                ]
            )
            lses.append([lse_ref[p, t, head : head + 1, :] for head in range(2)])

        def accumulate(at, rows, cols, allowed, d_query):
            bias_ref[:rows, :cols] = jnp.where(allowed, 0.0, neg_large)
            after = list(d_query)
            keys = [k_ref[pl.ds(at, rows), span] for span in lanes]
            eighth = [v_ref[pl.ds(at, rows), span] * jnp.asarray(0.125, bf16) for span in lanes]
            keys_t = [part.T for part in keys]
            stack = lambda parts: jnp.concatenate([part[:cols] for part in parts], axis=0)

            def begin(h):
                p, head = h // 2, h % 2
                return (
                    dot(keys[p], queries[p][head][:cols], NT),
                    dot(eighth[p], d_outs[p][head][:cols], NT),
                )

            def finish_pair(p, weights, d_scores):
                span = lanes[p]
                for head in range(2):
                    side = slice(head * HD, (head + 1) * HD)
                    h = 2 * p + head
                    after[h] = d_query[h] + dot(keys_t[p][side], d_scores[head])
                dv_ref[pl.ds(at, rows), span] += dot(
                    jnp.concatenate(weights, axis=1), stack(d_outs[p])
                )
                dk_ref[pl.ds(at, rows), span] += dot(
                    jnp.concatenate(d_scores, axis=1), stack(queries[p])
                )

            ready = begin(0)
            held = None
            weights, d_scores = [], []
            for h in range(2 * pairs):
                ahead = begin(h + 1) if h + 1 < 2 * pairs else None
                p, head = h // 2, h % 2
                scores = ready[0] * to_base2 - lses[p][head][:, :cols] + bias_ref[:rows, :cols]
                probs = jnp.exp2(scores)
                d_score = (probs * (ready[1] - inners[p][head][:, :cols])).astype(bf16)
                weights.append(probs.astype(bf16))
                d_scores.append(d_score)
                if held is not None:
                    finish_pair(*held)
                    held = None
                if head == 1:
                    held = (p, weights, d_scores)
                    weights, d_scores = [], []
                ready = ahead
            finish_pair(*held)
            return tuple(after)

        allowed = between((WINDOW, TILE), 0, own_low, own_high)
        zero = jnp.zeros((HD, TILE), f32)
        start = accumulate(window_at, WINDOW, TILE, allowed, (zero,) * (2 * pairs))
        start = tuple(jnp.concatenate([part, zero], axis=1) for part in start)
        first_key, trips = span_ref[t, 0], span_ref[t, 1]

        def one_step(j, d_query):
            at = pl.multiple_of(first_key + j * KEY_TILE, EDGE)
            allowed = between((KEY_TILE, 2 * TILE), at, key_low, key_high)
            return accumulate(at, KEY_TILE, 2 * TILE, allowed, d_query)

        d_query = lax.fori_loop(0, trips, one_step, start)
        for p, span in enumerate(lanes):
            pair = jnp.concatenate(d_query[2 * p : 2 * p + 2], axis=0).T
            for at, part in ((noisy_at, pair[:TILE]), (clean_at, pair[TILE:])):
                turned = turn(part, cos_ref[pl.ds(at, TILE), :], -sin_ref[pl.ds(at, TILE), :])
                out_ref[0, pl.ds(at, TILE), span] = turned.astype(bf16)
        return 0

    lax.fori_loop(0, TILES, one_tile, 0)
    step = KEY_ROWS // 9

    def finish(i, _):
        rows = pl.ds(pl.multiple_of(i * step, EDGE), step)
        for span in lanes:
            out_ref[1, rows, span] = turn(
                dk_ref[rows, span], cos_ref[rows, :], -sin_ref[rows, :]
            ).astype(bf16)
        out_ref[2, rows, :] = dv_ref[rows, :].astype(bf16)
        return 0

    lax.fori_loop(0, 9, finish, 0)

    def weight_rows(i, _):
        rows = pl.ds(pl.multiple_of(i * ROW_TILE, LANES), ROW_TILE)
        cols = q_ref.shape[1]
        spread = pl.ds(pl.multiple_of(i * cols, LANES), cols)
        for c in range(3):
            grad_ref[c, :, spread] = dot(rows_ref[rows, :], out_ref[c]).astype(bf16)
        return 0

    if rows_ref is not None:
        lax.fori_loop(0, rows_ref.shape[0] // ROW_TILE, weight_rows, 0)


def attend_backward(
    spans,
    clean_bounds,
    noisy_bounds,
    query,
    keys,
    values,
    attended,
    d_attended,
    lse,
    cosine,
    sine,
    *rows_t,
):
    count, cols = query.shape
    vmem = pl.BlockSpec(memory_space=pltpu.VMEM)
    return pl.pallas_call(
        backward_kernel,
        in_specs=[pl.BlockSpec(memory_space=pltpu.SMEM)] + [vmem] * (10 + len(rows_t)),
        out_specs=[vmem] * (1 + len(rows_t)),
        scratch_shapes=[
            pltpu.VMEM((count, cols), f32),
            pltpu.VMEM((count, cols), f32),
            pltpu.VMEM((max(KEY_TILE, WINDOW), 2 * TILE), f32),
        ],
        out_shape=[
            jax.ShapeDtypeStruct((3, count, cols), bf16),
            *[
                jax.ShapeDtypeStruct((3, ROW_TILE, rows.shape[0] // ROW_TILE * cols), bf16)
                for rows in rows_t
            ],
        ],
        name="attend_backward",
        cost_estimate=pl.CostEstimate(
            flops=36 * 10**9, bytes_accessed=36 * 10**6, transcendentals=6 * 10**6
        ),
    )(
        spans,
        clean_bounds,
        noisy_bounds,
        query,
        keys,
        values,
        attended,
        d_attended,
        lse,
        cosine,
        sine,
        *rows_t,
    )


PIECES = 16
MESH = pl.DeviceIdType.MESH


def flip(value, mask):
    result = value
    for b in range(mask.bit_length()):
        if mask >> b & 1:
            result = result + (1 << b) * (1 - 2 * ((value // (1 << b)) % 2))
    return result


class Exchange:
    def __init__(self, bits, count, rows, width, back=True):
        self.bits, self.count, self.rows, self.width = bits, count, rows, width
        self.back = back
        self.half, self.quarter, self.piece = rows // 2, rows // 4, rows // PIECES
        self.extra = list(range(4, bits))

    def slots(self):
        return 8 + 2 * (6 if self.back else 4) + (3 if self.extra else 0)

    def scratch(self):
        k, w = self.count, self.width
        cross = k if not self.back else 1
        shapes = [
            pltpu.VMEM((k, 2 - self.back, self.half, w), bf16),
            pltpu.VMEM((cross, self.half, w), bf16),
            pltpu.VMEM((cross, self.half, w), bf16),
            pltpu.VMEM((k, self.quarter, w), bf16),
            pltpu.VMEM((k, self.quarter, w), bf16),
            pltpu.VMEM((k, self.quarter, w), f32),
            pltpu.VMEM((k, 3, self.piece, w), bf16),
            pltpu.VMEM((k, 3, self.piece, w), bf16),
        ]
        lanes_of = (1, 0, 1, 3, 3, 1, 1) if self.back else (2, 1, 1, 3, 0, 0, 0)
        for lanes in [lanes for lanes in lanes_of if lanes]:
            shapes += [pltpu.SemaphoreType.DMA((k, lanes))] * 2
        if self.extra:
            n = len(self.extra)
            shapes += [pltpu.VMEM((k, 2 * n, self.piece, w), bf16)]
            shapes += [pltpu.SemaphoreType.DMA((k, n))] * 2
        return shapes

    def bind(self, place, part, refs):
        (self.a_in, self.b_out, self.b_in, self.c_out, self.c_in, self.keep) = refs[:6]
        self.d_out, self.d_in = refs[6:8]
        names = "acdefg" if self.back else "abcd"
        self.sems = {name: (refs[8 + 2 * i], refs[9 + 2 * i]) for i, name in enumerate(names)}
        if self.extra:
            at = 8 + 2 * len(names)
            self.x_buf, self.x_send, self.x_recv = refs[at : at + 3]
        self.place, self.part = place, part
        self.core, self.x, self.z = place % 2, (place // 2) % 2, (place // 4) % 4
        self.sibling = {"dp": flip(place, 1)}
        self.beside = {"dp": flip(place, 2)}
        self.across = {"mp": 1 - part}
        self.peers = [{"dp": flip(place, j << 2)} for j in range(1, 4)]
        self.partners = [self.sibling, self.beside, self.across] + self.peers
        self.partners += [{"dp": flip(place, 1 << b)} for b in self.extra]
        return self

    def greet(self):
        barrier = pltpu.get_barrier_semaphore()
        for partner in self.partners:
            pl.semaphore_signal(barrier, inc=1, device_id=partner, device_id_type=MESH)
        pl.semaphore_wait(barrier, len(self.partners))

    def copy(self, name, k, lane, source, target, device):
        out, into = self.sems[name]
        return pltpu.make_async_remote_copy(
            src_ref=source,
            dst_ref=target,
            send_sem=out.at[k, lane],
            recv_sem=into.at[k, lane],
            device_id=device,
            device_id_type=MESH,
        )

    def rows_at(self, start, size):
        return pl.ds(pl.multiple_of(start, PIECES), size)

    def copy_a(self, k, lane, grads):
        source = grads.at[k, self.rows_at((1 - self.core) * self.half, self.half)]
        return self.copy("a", k, lane, source, self.a_in.at[k, lane], self.sibling)

    def copy_b(self, k):
        return self.copy("b", k, 0, self.b_out.at[k], self.b_in.at[k], self.across)

    def copy_c(self, k):
        return self.copy("c", k, 0, self.c_out.at[k], self.c_in.at[k], self.beside)

    def copy_d(self, k, j):
        return self.copy("d", k, j, self.d_out.at[k, j], self.d_in.at[k, j], self.peers[j])

    def spot(self, change=0):
        start = self.core * self.half + self.x * self.quarter
        return self.rows_at(start + flip(self.z, change) * self.piece, self.piece)

    def copy_e(self, k, j, full):
        rows = full.at[k, self.spot()]
        return self.copy("e", k, j, rows, rows, self.peers[j])

    def copy_f(self, k, full):
        start = self.core * self.half + self.x * self.quarter
        rows = full.at[k, self.rows_at(start, self.quarter)]
        return self.copy("f", k, 0, rows, rows, self.beside)

    def copy_g(self, k, full):
        rows = full.at[k, self.rows_at(self.core * self.half, self.half)]
        return self.copy("g", k, 0, rows, rows, self.sibling)

    def start_a(self, k, lane, grads):
        self.copy_a(k, lane, grads).start()

    def stage_b(self, k, others):
        self.copy_a(k, 0, others).wait()
        mine = others[k, self.rows_at(self.core * self.half, self.half), :].astype(f32)
        self.b_out[k] = (mine + self.a_in[k, 0].astype(f32)).astype(bf16)
        self.copy_b(k).start()

    def stage_c(self, k, grads, crossed=None):
        lane = 0 if self.back else 1
        self.copy_a(k, lane, grads).wait()
        if not self.back:
            self.copy_b(k).wait()

        def total(which):
            inner = which * self.quarter
            rows = self.rows_at(inner, self.quarter)
            mine = grads[k, self.rows_at(self.core * self.half + inner, self.quarter), :]
            got = self.a_in[k, lane, rows, :].astype(f32)
            if not self.back:
                got = got + self.b_in[k, rows, :].astype(f32)
            elif crossed is not None:
                got = got + crossed(rows)
            return mine.astype(f32) + got

        self.c_out[k] = total(1 - self.x).astype(bf16)
        self.copy_c(k).start()
        self.keep[k] = total(self.x)

    def stage_d(self, k):
        self.copy_c(k).wait()
        for j in range(4):
            rows = self.rows_at(flip(self.z, j) * self.piece, self.piece)
            total = self.keep[k, rows, :] + self.c_in[k, rows, :].astype(f32)
            if j:
                self.d_out[k, j - 1] = total.astype(bf16)
                self.copy_d(k, j - 1).start()
            else:
                self.keep[k, rows, :] = total

    def gather_d(self, k):
        rows = self.rows_at(self.z * self.piece, self.piece)
        total = self.keep[k, rows, :]
        for j in range(3):
            self.copy_d(k, j).wait()
            total = total + self.d_in[k, j].astype(f32)
        for i, b in enumerate(self.extra):
            mine = self.x_buf.at[k, 2 * i]
            mine[...] = total.astype(bf16)
            swap = pltpu.make_async_remote_copy(
                src_ref=mine,
                dst_ref=self.x_buf.at[k, 2 * i + 1],
                send_sem=self.x_send.at[k, i],
                recv_sem=self.x_recv.at[k, i],
                device_id={"dp": flip(self.place, 1 << b)},
                device_id_type=MESH,
            )
            swap.start()
            swap.wait()
            total = total.astype(bf16).astype(f32) + self.x_buf[k, 2 * i + 1].astype(f32)
        return total.astype(bf16)

    def stage_e(self, k, full):
        full[k, self.spot(), :] = self.gather_d(k)
        for j in range(3):
            self.copy_e(k, j, full).start()

    def stage_f(self, k, full):
        for j in range(3):
            self.copy_e(k, j, full).wait()
        self.copy_f(k, full).start()

    def stage_g(self, k, full):
        self.copy_f(k, full).wait()
        self.copy_g(k, full).start()

    def stage_h(self, k, full):
        self.copy_g(k, full).wait()


def at_step(step, count, action):
    @pl.when(jnp.logical_and(step >= 0, step < count))
    def _():
        action(step)


def middle_kernel(exchanges, tiles, *refs):
    (
        x_ref,
        att_ref,
        att2_ref,
        wout_ref,
        wout2_ref,
        dy_ref,
        vectors_ref,
        bup_ref,
        up_mine,
        up_here,
        up_beside,
        down_mine,
        down_here,
        out_ref,
        mid_ref,
        datt_ref,
        datt2_ref,
        gout_ref,
        gout2_ref,
        gbup_ref,
        small_ref,
        pieces_ref,
        up_there,
        down_there,
        pass_up,
        pass_down,
        up_buf,
        down_buf,
        load_sem,
        n2_ref,
        total_ref,
        dn2_ref,
        act_ref,
        dpre_ref,
        n2_t,
        bup_other,
        bias_sem,
        down_grad,
        up_grad,
        *rest,
    ) = refs
    place, part = lax.axis_index("dp"), lax.axis_index("mp")
    ex = exchanges[0].bind(place, part, rest)
    ex_up = exchanges[1].bind(place, part, rest[exchanges[0].slots() :])
    sides = ((ex, down_grad), (ex_up, up_grad))
    core = ex.core
    count = tiles // 2
    rows_all = x_ref.shape[0]
    blocks = rows_all // ROW_TILE
    width = x_ref.shape[1]
    lanes = width // 2

    def which(i):
        other = jnp.logical_or(i == 0, jnp.logical_and(i % 2 == 1, i < tiles - 1))
        mine = jnp.where(i == tiles - 1, count - 1, i // 2 - 1)
        return other, jnp.where(other, (i + 1) // 2, mine)

    quarter = width // 4
    strip = HIDDEN_TILE // 2
    held = 2 * core + ex.x
    kept = 2 * core + 1 - ex.x

    def load_up(i, source, h):
        target = up_buf.at[i % 2, h * quarter : (h + 1) * quarter]
        return pltpu.make_async_copy(source, target, load_sem.at[i % 2, h])

    def load_down(i, source, h):
        target = down_buf.at[i % 2, h * strip : (h + 1) * strip]
        return pltpu.make_async_copy(source, target, load_sem.at[i % 2, 4 + h])

    def hand_up(k, part_of):
        cols = pl.ds(pl.multiple_of(k * HIDDEN_TILE, HIDDEN_TILE), HIDDEN_TILE)
        side = ex.x if part_of == 0 else 1 - ex.x
        rows = pl.ds(pl.multiple_of(side * quarter, EDGE), quarter)
        return pltpu.make_async_remote_copy(
            src_ref=(up_here, up_beside)[part_of].at[:, cols],
            dst_ref=up_there.at[k, rows],
            send_sem=pass_up.at[k, 2 * part_of],
            recv_sem=pass_up.at[k, 2 * part_of + 1],
            device_id=ex.sibling,
            device_id_type=MESH,
        )

    def hand_down(b):
        return pltpu.make_async_remote_copy(
            src_ref=down_here.at[strip_rows(b)],
            dst_ref=down_there.at[b],
            send_sem=pass_down.at[b, 0],
            recv_sem=pass_down.at[b, 1],
            device_id=ex.sibling,
            device_id_type=MESH,
        )

    def strip_rows(b):
        return pl.ds(pl.multiple_of(b * strip, strip), strip)

    def start_loads(i):
        other, k = which(i)
        mine = jnp.logical_not(other)
        cols = pl.ds(pl.multiple_of(k * HIDDEN_TILE, HIDDEN_TILE), HIDDEN_TILE)

        @pl.when(other)
        def _():
            hand_up(k, 0).wait()
            hand_up(k, 1).wait()

        for h in range(4):

            @pl.when(mine)
            def _():
                load_up(i, up_mine.at[h * quarter : (h + 1) * quarter, cols], h).start()

            @pl.when(jnp.logical_and(other, held == h))
            def _():
                load_up(i, up_here.at[:, cols], h).start()

            @pl.when(jnp.logical_and(other, kept == h))
            def _():
                load_up(i, up_beside.at[:, cols], h).start()

            @pl.when(jnp.logical_and(other, core != h // 2))
            def _():
                rows = slice(h % 2 * quarter, (h % 2 + 1) * quarter)
                load_up(i, up_there.at[k, rows], h).start()

        for h in range(2):
            b = 2 * k + h
            inner = b % count

            @pl.when(mine)
            def _():
                load_down(i, down_mine.at[strip_rows(b), :], h).start()

            @pl.when(jnp.logical_and(other, core == b // count))
            def _():
                load_down(i, down_here.at[strip_rows(inner), :], h).start()

            @pl.when(jnp.logical_and(other, core != b // count))
            def _():
                hand_down(inner).wait_recv()
                load_down(i, down_there.at[inner], h).start()

    def wait_loads(i):
        for h in range(4):
            load_up(i, up_mine.at[:quarter, :HIDDEN_TILE], h).wait()
        for h in range(2):
            load_down(i, down_mine.at[:strip, :], h).wait()

    ex.greet()
    bias_swap = pltpu.make_async_remote_copy(
        src_ref=bup_ref,
        dst_ref=bup_other,
        send_sem=bias_sem.at[0],
        recv_sem=bias_sem.at[1],
        device_id=ex.across,
        device_id_type=MESH,
    )
    bias_swap.start()

    def hand(k, _):
        hand_up(k, 0).start()
        hand_up(k, 1).start()
        hand_down(k).start()
        return 0

    lax.fori_loop(0, count, hand, 0)

    def prologue(r, _):
        rows = pl.ds(pl.multiple_of(r * ROW_TILE, ROW_TILE), ROW_TILE)
        branch = dot(att_ref[rows, :], wout_ref[...]) + dot(att2_ref[rows, :], wout2_ref[...])
        mid = x_ref[rows, :].astype(f32) + branch
        mid_ref[rows, :] = mid
        unit = normal(mid)[0]
        n2_ref[rows, :] = (unit * vectors_ref[2:3, :] + vectors_ref[3:4, :]).astype(bf16)
        total_ref[rows, :] = mid + vectors_ref[4:5, :]
        dn2_ref[rows, :] = jnp.zeros((ROW_TILE, width), f32)
        return 0

    lax.fori_loop(0, blocks, prologue, 0)
    start_loads(0)
    for c in range(width // LANES):
        cols = slice(c * LANES, (c + 1) * LANES)
        n2_t[cols, :] = n2_ref[:, cols].T
    n2_t[width:, :] = jnp.ones((PIECES, rows_all), bf16)
    bias_swap.wait()

    def tile(i):
        other, k = which(i)
        slot = i % 2
        wait_loads(i)

        @pl.when(i + 1 < tiles)
        def _():
            start_loads(i + 1)

        up, down = up_buf.at[slot], down_buf.at[slot]
        bias_at = jnp.where(other, k, count + k)
        bias = jnp.where(other, bup_other[k], bup_ref[k])
        linear = 0.7978845608028654
        cubic = linear * 0.044715
        for r in range(blocks):
            rows = slice(r * ROW_TILE, (r + 1) * ROW_TILE)
            pre = dot(n2_ref[rows, :], up[...]) + bias
            d_act = dot(dy_ref[rows, :], down[...], NT)
            square = pre * pre
            bend = jnp.tanh(pre * (square * cubic + linear))
            gate = 0.5 * bend + 0.5
            full_act = pre * gate
            slope = gate + (full_act - full_act * gate) * (square * (6.0 * cubic) + 2.0 * linear)
            act_ref[rows, :] = full_act.astype(bf16)
            dpre_ref[rows, :] = (d_act * slope).astype(bf16)
        total_ref[...] += dot(act_ref[...], down[...])
        dn2_ref[...] += dot(dpre_ref[...], up[...], NT)
        down_grad[k] = dot(act_ref[...].T, dy_ref[...]).astype(bf16)

        def start(lane):
            for side, grad in sides:
                side.start_a(k, lane, grad)

        by_rows = dot(n2_t[...], dpre_ref[...])
        up_grad[k] = by_rows[:width].astype(bf16)
        gbup_ref[bias_at] = by_rows[width : width + 1]
        pl.when(other)(functools.partial(start, 0))
        pl.when(jnp.logical_not(other))(functools.partial(start, 1))

    def each(k, when, action):
        @pl.when(jnp.logical_and(when, jnp.logical_and(k >= 0, k < count)))
        def _():
            for n, (side, grad) in enumerate(sides):
                action(n, side, grad, k)

    def stage_b(n, side, grad, k):
        side.stage_b(k, grad)

    def stage_c(n, side, grad, k):
        side.stage_c(k, grad)

    def stage_d(n, side, grad, k):
        side.stage_d(k)

    def arrive(n, side, grad, k):
        piece = side.gather_d(k)
        if n == 0:
            pieces_ref[k] = piece
        else:
            for c in range(width // HIDDEN_TILE):
                cols = slice(c * HIDDEN_TILE, (c + 1) * HIDDEN_TILE)
                pieces_ref[count + k, :, cols] = piece[c * PIECES : (c + 1) * PIECES]

    def steps(i):
        even = i % 2 == 0
        odd = jnp.logical_not(even)
        each((i - 6) // 2, even, arrive)
        each((i - 5) // 2, odd, stage_d)
        each((i - 4) // 2, even, stage_c)
        each(i // 2, even, stage_b)

    def epilogue(r, _):
        rows = pl.ds(pl.multiple_of(r * ROW_TILE, ROW_TILE), ROW_TILE)
        out_ref[rows, :] = total_ref[rows, :].astype(bf16)
        unit, scale = normal(mid_ref[rows, :])
        d_rows = dn2_ref[rows, :]
        dy = dy_ref[rows, :].astype(f32)
        lean = d_rows * vectors_ref[2:3, :]
        d_mid = dy + scale * (
            lean
            - jnp.mean(lean, axis=-1, keepdims=True)
            - unit * jnp.mean(lean * unit, axis=-1, keepdims=True)
        )
        mid_ref[rows, :] = d_mid
        d_branch = d_mid.astype(bf16)
        n2_ref[rows, :] = d_branch
        datt_ref[rows, :] = dot(d_branch, wout_ref[...], NT).astype(bf16)
        datt2_ref[rows, :] = dot(d_branch, wout2_ref[...], NT).astype(bf16)
        add = lambda values: jnp.sum(values, axis=0, keepdims=True)
        small_ref[0:1, :] += add(d_rows * unit)
        small_ref[1:2, :] += add(d_rows)
        small_ref[2:3, :] += add(dy)
        return 0

    def out_grads():
        for source, target in ((att_ref, gout_ref), (att2_ref, gout2_ref)):
            grad = dot(source[...].T, n2_ref[...]).astype(bf16)
            for a in range(wout_ref.shape[0] // LANES):
                for b in range(2):
                    rows = slice(a * LANES, (a + 1) * LANES)
                    cols = slice(b * lanes, (b + 1) * lanes)
                    spread = slice(a * lanes, (a + 1) * lanes)
                    target[b * LANES : (b + 1) * LANES, spread] = grad[rows, cols]

    def main(i, _):
        pl.when(i < tiles)(functools.partial(tile, i))

        @pl.when(jnp.logical_and(i >= tiles, i < tiles + 2))
        def _():
            first = (i - tiles) * (blocks // 2)
            lax.fori_loop(first, first + blocks // 2, epilogue, 0)

        pl.when(i == tiles + 2)(out_grads)
        steps(i)
        return 0

    small_ref[...] = jnp.zeros_like(small_ref)
    lax.fori_loop(0, tiles + 5, main, 0)

    def handed(slot, _):
        hand_down(slot).wait_send()
        return 0

    lax.fori_loop(0, count, handed, 0)


def middle(bits, x, att, att2, wout, wout2, dy, vectors, bup, ups, downs):
    rows, width = x.shape
    hidden = ups[0].shape[1]
    count = hidden // HIDDEN_TILE
    tiles = 2 * count
    exchanges = (
        Exchange(bits, count, HIDDEN_TILE, width, False),
        Exchange(bits, count, width, HIDDEN_TILE, False),
    )
    vmem = pl.BlockSpec(memory_space=pltpu.VMEM)
    hbm = pl.BlockSpec(memory_space=pl.ANY)
    shape = jax.ShapeDtypeStruct
    depth = wout.shape[0]
    return pl.pallas_call(
        functools.partial(middle_kernel, exchanges, tiles),
        in_specs=[vmem] * 8 + [hbm] * 5,
        out_specs=[vmem] * 9,
        out_shape=[
            shape((rows, width), bf16),
            shape((rows, width), f32),
            shape(att.shape, bf16),
            shape(att2.shape, bf16),
            shape((2 * LANES, depth // LANES * width // 2), bf16),
            shape((2 * LANES, depth // LANES * width // 2), bf16),
            shape((tiles, 1, HIDDEN_TILE), f32),
            shape((8, width), f32),
            shape((2 * count, PIECES, width), bf16),
        ],
        scratch_shapes=[
            pltpu.VMEM((count, width // 2, HIDDEN_TILE), bf16),
            pltpu.VMEM((count, HIDDEN_TILE // 2, width), bf16),
            pltpu.SemaphoreType.DMA((count, 4)),
            pltpu.SemaphoreType.DMA((count, 2)),
            pltpu.VMEM((2, width, HIDDEN_TILE), bf16),
            pltpu.VMEM((2, HIDDEN_TILE, width), bf16),
            pltpu.SemaphoreType.DMA((2, 6)),
            pltpu.VMEM((rows, width), bf16),
            pltpu.VMEM((rows, width), f32),
            pltpu.VMEM((rows, width), f32),
            pltpu.VMEM((rows, HIDDEN_TILE), bf16),
            pltpu.VMEM((rows, HIDDEN_TILE), bf16),
            pltpu.VMEM((width + PIECES, rows), bf16),
            pltpu.VMEM(bup.shape, f32),
            pltpu.SemaphoreType.DMA((2,)),
            pltpu.VMEM((count, HIDDEN_TILE, width), bf16),
            pltpu.VMEM((count, width, HIDDEN_TILE), bf16),
        ]
        + exchanges[0].scratch()
        + exchanges[1].scratch(),
        compiler_params=pltpu.CompilerParams(
            collective_id=0, has_side_effects=True, vmem_limit_bytes=67043328
        ),
        name="middle",
        cost_estimate=pl.CostEstimate(
            flops=60 * 10**9, bytes_accessed=40 * 10**6, transcendentals=4 * 10**6
        ),
    )(x, att, att2, wout, wout2, dy, vectors, bup, *ups, *downs)


def leave_kernel(exchange, *refs):
    (
        rows_hbm,
        mine_out_ref,
        crossed_ref,
        crossed_out_ref,
        d_hbm,
        d2_hbm,
        w_hbm,
        w2_hbm,
        tokens_ref,
        context_ref,
        vectors_ref,
        dmid_hbm,
        small_ref,
        small2_ref,
        gqkv_ref,
        gout_ref,
        back_ref,
        sums_ref,
        full_ref,
        out_buf,
        rows_t_ref,
        d_ref,
        d2_ref,
        w_ref,
        w2_ref,
        dmid_ref,
        load_sem,
        rows_ref,
        give_ref,
        take_ref,
        swap_sem,
        norm_ref,
        near_ref,
        far_ref,
        near_sem,
        far_sem,
        *rest,
    ) = refs
    place, part = lax.axis_index("dp"), lax.axis_index("mp")
    ex = exchange.bind(place, part, rest)
    count, bits = ex.count, ex.bits
    loads = [
        pltpu.make_async_copy(source, target, load_sem.at[n])
        for n, (source, target) in enumerate(
            (
                (w_hbm, w_ref),
                (d_hbm, d_ref),
                (w2_hbm, w2_ref),
                (d2_hbm, d2_ref),
                (rows_hbm, rows_t_ref),
                (dmid_hbm, dmid_ref),
            )
        )
    ]
    for load in loads:
        load.start()
    near_id = part * 4 + place % 4
    near = [
        {"dp": flip(place, j % 4), "mp": part if j < 4 else 1 - part} for j in range(1, 8)
    ]
    ex.partners += [near[j - 1] for j in (3, 5, 6, 7)]
    ex.greet()

    total = mine_out_ref[...].astype(f32) + crossed_out_ref[...].astype(f32)
    out_buf[0] = total.astype(bf16)
    ex.start_a(0, 0, out_buf)
    step = KEY_ROWS // 3

    def back_rows(n):
        rows = pl.ds(pl.multiple_of(n * step, EDGE), step)
        total = 0.0
        for grads, weights in ((d_ref, w_ref), (d2_ref, w2_ref)):
            for c in range(3):
                total = total + dot(grads[c, rows, :], weights[c], NT)
        rows_ref[rows, :] = total

    lanes = d_ref.shape[2]

    def grad_chunk(c):
        for r in range(rows_t_ref.shape[0] // ROW_TILE):
            rows = slice(r * ROW_TILE, (r + 1) * ROW_TILE)
            grad = dot(rows_t_ref[rows, :], d_ref[c]).astype(bf16)
            out_buf[c + 1, :, r * lanes : (r + 1) * lanes] = grad
        ex.start_a(c + 1, 0, out_buf)

    def stage_c(k):
        @pl.when(k >= 1)
        def _():
            ex.stage_c(k, out_buf, lambda rows: crossed_ref[k - 1, rows, :].astype(f32))

        @pl.when(k == 0)
        def _():
            ex.stage_c(k, out_buf)

    def arrive(k):
        ex.stage_h(k, full_ref)

        @pl.when(k == 0)
        def _():
            for a in range(gout_ref.shape[0] // LANES):
                for b in range(2):
                    spread = slice(a * lanes, (a + 1) * lanes)
                    rows = slice(a * LANES, (a + 1) * LANES)
                    piece = full_ref[0, b * LANES : (b + 1) * LANES, spread]
                    gout_ref[rows, b * lanes : (b + 1) * lanes] = piece

        @pl.when(k > 0)
        def _():
            for r in range(rows_t_ref.shape[0] // ROW_TILE):
                rows = slice(r * ROW_TILE, (r + 1) * ROW_TILE)
                gqkv_ref[k - 1, rows, :] = full_ref[k, :, r * lanes : (r + 1) * lanes]

    def steps(i):
        at_step(i - 6, count, arrive)
        at_step(i - 5, count, lambda k: ex.stage_g(k, full_ref))
        at_step(i - 4, count, lambda k: ex.stage_f(k, full_ref))
        at_step(i - 3, count, lambda k: ex.stage_e(k, full_ref))
        at_step(i - 2, count, lambda k: ex.stage_d(k))
        at_step(i - 1, count, stage_c)

    width = tokens_ref.shape[1]

    def swap(rows, lane):
        return pltpu.make_async_remote_copy(
            src_ref=give_ref.at[rows],
            dst_ref=take_ref.at[rows],
            send_sem=swap_sem.at[lane, 0],
            recv_sem=swap_sem.at[lane, 1],
            device_id=ex.across,
            device_id_type=MESH,
        )

    def sums_of(d_rows, units):
        add = lambda values: jnp.sum(values, axis=0, keepdims=True)
        norm_ref[0:1, :] += add(d_rows * units)
        norm_ref[1:2, :] += add(d_rows)

    main = slice(0, HALF)
    edges = slice(HALF, HALF + 2 * EDGE)
    parts = tokens_ref.shape[0] // TILE
    lead = small_ref.shape[0] - 2
    bias = lead - 3
    norm_ref[...] = jnp.zeros_like(norm_ref)
    for load in loads[:4]:
        load.wait()

    def own_at(b):
        start = jnp.where(b < TILES, NOISY_OWN + b * TILE, CLEAN_OWN + (b - TILES) * TILE)
        return pl.ds(pl.multiple_of(start, EDGE), TILE)

    def tokens_at(b):
        return pl.ds(pl.multiple_of(b * TILE, TILE), TILE)

    def give_main():
        give_ref[main, :] = rows_ref[main, :].astype(bf16)
        swap(main, 0).start()
        loads[4].wait()

    def give_edges():
        side = rows_ref[NOISY_BASE:NOISY_OWN, :] + rows_ref[NOISY_OWN + HALF :, :]
        after = rows_ref[2 * HALF : NOISY_BASE, :]
        give_ref[HALF : HALF + EDGE, :] = after.astype(bf16)
        give_ref[HALF + EDGE :, :] = side.astype(bf16)
        swap(edges, 1).start()
        sums_of(after, normal(context_ref[:EDGE, :].astype(f32))[0])
        sums_of(side, normal(context_ref[HALF:, :].astype(f32))[0])

    def tell_near():
        def context_sums(b, _):
            rows = tokens_at(b)
            sums_of(rows_ref[rows, :], normal(context_ref[rows, :].astype(f32))[0])
            return 0

        lax.fori_loop(0, HALF // TILE, context_sums, 0)

        def own_sums(b, _):
            sums_of(rows_ref[own_at(b), :], normal(tokens_ref[tokens_at(b), :].astype(f32))[0])
            return 0

        lax.fori_loop(0, parts, own_sums, 0)
        mine = near_ref.at[near_id]
        mine[:lead, :] = small_ref[:lead, :]
        mine[lead : lead + 2, :] = norm_ref[:2, :]
        mine[lead + 2 : lead + 2 + bias, :] = small2_ref[:bias, :]
        rest_rows = 16 - lead - 2 - bias
        mine[16 - rest_rows :, :] = jnp.zeros((rest_rows, width), f32)
        for j in range(1, 8):
            near_copy(j).start()

    def near_copy(j):
        return pltpu.make_async_remote_copy(
            src_ref=near_ref.at[near_id],
            dst_ref=near_ref.at[near_id],
            send_sem=near_sem.at[j, 0],
            recv_sem=near_sem.at[j, 1],
            device_id=near[j - 1],
            device_id_type=MESH,
        )

    def near_got(j):
        came = (part + j // 4) % 2 * 4 + flip(place % 4, j % 4)
        return pltpu.make_async_remote_copy(
            src_ref=near_ref.at[came],
            dst_ref=near_ref.at[came],
            send_sem=near_sem.at[j, 0],
            recv_sem=near_sem.at[j, 1],
            device_id=near[j - 1],
            device_id_type=MESH,
        )

    def far_copy(j, at):
        return pltpu.make_async_remote_copy(
            src_ref=far_ref.at[at],
            dst_ref=far_ref.at[at],
            send_sem=far_sem.at[j, 0],
            recv_sem=far_sem.at[j, 1],
            device_id=ex.peers[j - 1],
            device_id_type=MESH,
        )

    def tell_far():
        for j in range(1, 8):
            near_copy(j).wait_send()
            near_got(j).wait_recv()
        total = near_ref[0]
        for j in range(1, 8):
            total = total + near_ref[j]
        plane = near_ref[part * 4]
        other = near_ref[(1 - part) * 4]
        for j in range(1, 4):
            plane = plane + near_ref[part * 4 + j]
            other = other + near_ref[(1 - part) * 4 + j]
        spot = far_ref.at[ex.z]
        spot[...] = total
        spot[:bias, :] = plane[:bias] + other[lead + 2 : lead + 2 + bias]
        for j in range(1, 4):
            far_copy(j, ex.z).start()

    def take_back():
        loads[5].wait()
        swap(main, 0).wait()
        swap(edges, 1).wait()
        clean = slice(CLEAN_OWN, CLEAN_OWN + HALF)
        rows_ref[clean, :] += take_ref[main, :].astype(f32)
        begin = slice(CLEAN_OWN, CLEAN_OWN + EDGE)
        rows_ref[begin, :] += take_ref[HALF : HALF + EDGE, :].astype(f32)
        edge = pl.ds(pl.multiple_of(NOISY_OWN + (1 - part) * (HALF - EDGE), EDGE), EDGE)
        rows_ref[edge, :] += take_ref[HALF + EDGE :, :].astype(f32)

    def norm_back(b):
        rows = tokens_at(b)
        unit, scale = normal(tokens_ref[rows, :].astype(f32))
        lean = rows_ref[own_at(b), :] * vectors_ref[0:1, :]
        back_ref[rows, :] = dmid_ref[rows, :] + scale * (
            lean
            - jnp.mean(lean, axis=-1, keepdims=True)
            - unit * jnp.mean(lean * unit, axis=-1, keepdims=True)
        )

    def end_far():
        for j in range(1, 4):
            far_copy(j, ex.z).wait_send()
            far_copy(j, flip(ex.z, j)).wait_recv()
        total = far_ref[0]
        for j in range(1, 4):
            total = total + far_ref[j]
        for i, b in enumerate(ex.extra):
            far_ref[4 + 2 * i] = total
            trade = pltpu.make_async_remote_copy(
                src_ref=far_ref.at[4 + 2 * i],
                dst_ref=far_ref.at[5 + 2 * i],
                send_sem=far_sem.at[4 + i, 0],
                recv_sem=far_sem.at[4 + i, 1],
                device_id={"dp": flip(place, 1 << b)},
                device_id_type=MESH,
            )
            trade.start()
            trade.wait()
            total = total + far_ref[5 + 2 * i]
        sums_ref[...] = total

    groups = count - 1
    actions = {
        0: give_main,
        groups + 2: give_edges,
        groups + 3: tell_near,
        groups + 4: tell_far,
        groups + 5: take_back,
    }
    begin_back = groups + 6

    def phase(p, _):
        later = jnp.logical_or(p == groups + 1, p == groups + 2)

        @pl.when(jnp.logical_or(p == 0, later))
        def _():
            back_rows(jnp.where(p == 0, 0, p - groups))

        @pl.when(jnp.logical_and(p >= 1, p <= groups))
        def _():
            grad_chunk(p - 1)

        for n, action in actions.items():
            pl.when(p == n)(action)
        block = 2 * (p - begin_back)

        @pl.when(jnp.logical_and(block >= 0, block < parts))
        def _():
            lax.fori_loop(block, block + 2, lambda b, _: (norm_back(b), 0)[1], 0)

        pl.when(block == parts)(end_far)
        steps(p)
        return 0

    lax.fori_loop(0, begin_back + parts // 2 + 1, phase, 0)


def leave(bits, rows_t, mine, crossed, d_fields, weights, tokens, context, vectors, d_mid, small, small2):
    total = 1 + crossed[0].shape[0]
    rows, cols = mine.shape
    exchange = Exchange(bits, total, rows, cols)
    count, width = tokens.shape
    vmem = pl.BlockSpec(memory_space=pltpu.VMEM)
    hbm = pl.BlockSpec(memory_space=pl.ANY)
    shape = jax.ShapeDtypeStruct
    return pl.pallas_call(
        functools.partial(leave_kernel, exchange),
        in_specs=[hbm] + [vmem] * 3 + [hbm] * 4 + [vmem] * 3 + [hbm] + [vmem] * 2,
        out_specs=[vmem] * 4,
        out_shape=[
            shape(weights[0].shape, bf16),
            shape((d_fields[0].shape[2], width), bf16),
            shape((count, width), f32),
            shape((16, width), f32),
        ],
        scratch_shapes=[
            pltpu.VMEM((total, rows, cols), bf16),
            pltpu.VMEM((total, rows, cols), bf16),
            pltpu.VMEM(rows_t.shape, bf16),
            pltpu.VMEM(d_fields[0].shape, bf16),
            pltpu.VMEM(d_fields[1].shape, bf16),
            pltpu.VMEM(weights[0].shape, bf16),
            pltpu.VMEM(weights[1].shape, bf16),
            pltpu.VMEM(d_mid.shape, f32),
            pltpu.SemaphoreType.DMA((6,)),
            pltpu.VMEM((KEY_ROWS, width), f32),
            pltpu.VMEM((HALF + 2 * EDGE, width), bf16),
            pltpu.VMEM((HALF + 2 * EDGE, width), bf16),
            pltpu.SemaphoreType.DMA((2, 2)),
            pltpu.VMEM((8, width), f32),
            pltpu.VMEM((8, 16, width), f32),
            pltpu.VMEM((4 + 2 * len(exchange.extra), 16, width), f32),
            pltpu.SemaphoreType.DMA((8, 2)),
            pltpu.SemaphoreType.DMA((4 + len(exchange.extra), 2)),
        ]
        + exchange.scratch(),
        compiler_params=pltpu.CompilerParams(
            collective_id=1, has_side_effects=True, vmem_limit_bytes=67043328
        ),
        name="leave",
        cost_estimate=pl.CostEstimate(
            flops=40 * 10**9, bytes_accessed=40 * 10**6, transcendentals=0
        ),
    )(
        rows_t, mine, *crossed, *d_fields, *weights, tokens, context, vectors, d_mid, small, small2
    )


def assemble_kernel(core_ref, down_mine, up_mine, down_got, up_got, down_ref, up_ref):
    core = core_ref[0]
    block = down_mine.shape[1]
    lanes = up_ref.shape[1]
    parts = down_mine.shape[2] // lanes
    deep = block * parts
    for side, down, up in ((core, down_mine, up_mine), (1 - core, down_got, up_got)):
        rows = pl.ds(pl.multiple_of(side * block, block), block)
        down_ref[rows, :] = down[0].astype(f32)
        for n in range(block // PIECES):
            for c in range(parts):
                at = side * deep + (n * parts + c) * PIECES
                rows = pl.ds(pl.multiple_of(at, PIECES), PIECES)
                piece = up[0, n * PIECES : (n + 1) * PIECES, c * lanes : (c + 1) * lanes]
                up_ref[rows, :] = piece.astype(f32)


def assemble(core, gathered, moved):
    tiles, half, width = gathered.shape
    count = tiles // 2
    down_spec = pl.BlockSpec((1, half, width), lambda k, c: (k, 0, 0))
    up_spec = pl.BlockSpec((1, half, width), lambda k, c: (count + k, 0, 0))
    hidden = count * 2 * half
    return pl.pallas_call(
        assemble_kernel,
        grid_spec=pltpu.PrefetchScalarGridSpec(
            num_scalar_prefetch=1,
            grid=(count,),
            in_specs=[down_spec, up_spec, down_spec, up_spec],
            out_specs=[
                pl.BlockSpec((2 * half, width), lambda k, c: (k, 0)),
                pl.BlockSpec((width, 2 * half), lambda k, c: (0, k)),
            ],
        ),
        out_shape=[
            jax.ShapeDtypeStruct((hidden, width), f32),
            jax.ShapeDtypeStruct((width, hidden), f32),
        ],
        name="assemble",
        cost_estimate=pl.CostEstimate(
            flops=10**6, bytes_accessed=14 * 10**6, transcendentals=0
        ),
    )(core, gathered, gathered, moved, moved)


def key_layout(seq_lengths, block_len, part):
    index = jnp.arange(KEY_ROWS, dtype=jnp.int32)
    own = part * HALF
    token = jnp.where(
        index < NOISY_BASE, index + (own - HALF), index - NOISY_BASE + (own - EDGE)
    )
    ends = jnp.cumsum(seq_lengths)
    passed = token[:, None] >= ends[None, :]
    starts = jnp.sum(jnp.where(passed, seq_lengths[None, :], 0), axis=1)
    lengths_here = jnp.where(passed, 0, ends[None, :])
    stops = jnp.min(jnp.where(passed, TOK_DEV, lengths_here), axis=1)
    positions = token - starts
    block_start = starts + positions // block_len * block_len
    block_stop = jnp.minimum(block_start + block_len, stops)
    mine = slice(CLEAN_OWN, CLEAN_OWN + HALF)
    low, start, stop = starts[mine], block_start[mine], block_stop[mine]
    to_clean = own - HALF
    tiles = lambda column: column.reshape(TILES, 1, TILE)
    clean_bounds = jnp.concatenate(
        [
            jnp.concatenate([tiles(low - to_clean), tiles(low - to_clean)], axis=2),
            jnp.concatenate([tiles(start - to_clean), tiles(stop - to_clean)], axis=2),
        ],
        axis=1,
    )
    to_window = own - EDGE + TILE * jnp.arange(TILES, dtype=jnp.int32)[:, None, None]
    noisy_bounds = jnp.concatenate(
        [tiles(start) - to_window, tiles(stop) - to_window], axis=1
    )
    first = jnp.min(clean_bounds[:, 0], axis=1) // EDGE * EDGE
    last = jnp.max(clean_bounds[:, 1], axis=1)
    trips = (last - first + KEY_TILE - 1) // KEY_TILE
    spans = jnp.stack([first, trips], axis=1)
    lane = jnp.arange(LANES, dtype=jnp.int32)
    frequency = jnp.exp(
        (lane % (HD // 2)).astype(f32) * (-math.log(10000.0) / (HD // 2))
    )
    angles = positions.astype(f32)[:, None] * frequency[None, :]
    sign = jnp.where(lane % HD < HD // 2, -1.0, 1.0)
    return spans, clean_bounds, noisy_bounds, jnp.cos(angles), jnp.sin(angles) * sign


def in_order(bit, mine, theirs, axis=0):
    order = bit == 0
    return jnp.concatenate(
        [jnp.where(order, mine, theirs), jnp.where(order, theirs, mine)], axis=axis
    )


def tie(first, second):
    return lax.optimization_barrier((first, second))


def local(
    dp_size,
    tokens,
    lengths,
    block_size,
    cotangent,
    ln1_gain,
    ln1_bias,
    w_qkv,
    w_out,
    ln2_gain,
    ln2_bias,
    w_up,
    b_up,
    w_down,
    b_down,
):
    width = tokens.shape[2]
    part = lax.axis_index("mp")
    place = lax.axis_index("dp")
    bits = dp_size.bit_length() - 1
    core = place & 1

    def across(array):
        return lax.ppermute(array, "mp", [(0, 1), (1, 0)])

    def sibling(array):
        return lax.ppermute(array, "dp", [(i, i ^ 1) for i in range(dp_size)])

    def beside(array):
        return lax.ppermute(array, "dp", [(i, i ^ 2) for i in range(dp_size)])

    edge = jnp.where(part == 0, tokens[0, HALF - EDGE :], tokens[0, :EDGE])
    context = across(jnp.concatenate([tokens[1], edge], axis=0))
    qkv_mine = w_qkv.transpose(1, 0, 2)
    side = (place >> 1) & 1

    def quarter_of(array, axis=0):
        size = array.shape[axis] // 4
        return lax.dynamic_slice_in_dim(array, (2 * core + side) * size, size, axis)

    def half_of(array):
        size = array.shape[0] // 2
        return lax.dynamic_slice_in_dim(array, core * size, size, 0)

    quarters = [quarter_of(qkv_mine, 1), quarter_of(w_up), half_of(w_down), half_of(w_out)]
    layout = key_layout(lengths[0], block_size[0], part)
    vectors = jnp.stack([ln1_gain, ln1_bias, ln2_gain, ln2_bias, b_down])
    context, (quarters, layout, vectors) = tie(context, (quarters, layout, vectors))
    qkv_here, up_here, down_here, out_here = [across(piece) for piece in quarters]

    spans, clean_bounds, noisy_bounds, cosine, sine = layout
    normed1, normed1_t, *fields = enter(tokens, context, vectors, qkv_mine, cosine, sine)
    qkv_here, fields = tie(qkv_here, fields)
    qkv_beside = beside(qkv_here)
    mine = [*fields, *attend_forward(spans, clean_bounds, noisy_bounds, *fields)]
    (qkv_here, qkv_beside, up_here), _ = tie((qkv_here, qkv_beside, up_here), mine[3])
    qkv_half = in_order(side, qkv_here, qkv_beside, axis=1)
    qkv_other = in_order(core, qkv_half, sibling(qkv_half), axis=1)
    up_beside = beside(up_here)
    fields = project(normed1, qkv_other, cosine, sine)
    other = [*fields, *attend_forward(spans, clean_bounds, noisy_bounds, *fields)]
    (out_here, up_here, up_beside, down_here), _ = tie(
        (out_here, up_here, up_beside, down_here), other[3]
    )
    out_other = in_order(core, out_here, sibling(out_here))
    bias_all = b_up.astype(f32).reshape(-1, 1, HIDDEN_TILE)

    x_rows = tokens.reshape(TOK_DEV, width)
    out, d_mid, d_att, d_att2, grad_out, grad_out2, grad_bias, norms, pieces = middle(
        bits,
        x_rows,
        mine[3],
        other[3],
        w_out,
        out_other,
        cotangent.reshape(TOK_DEV, width),
        vectors,
        bias_all,
        (w_up, up_here, up_beside),
        (w_down, down_here),
    )
    hidden = b_up.shape[0]

    crossed_out = across(grad_out2)
    spread = [(b, min(2, min(bits, 4) - b)) for b in range(2, min(bits, 4), 2)]
    gathered = pieces
    ((first_bit, n),) = spread
    moved = [
        lax.ppermute(gathered, "dp", [(i, i ^ (k << first_bit)) for i in range(dp_size)])
        for k in range(1, 1 << n)
    ]

    def backward(saved, d_attended, spans, *rows_t):
        query, keys, values, attended, lse = saved
        return attend_backward(
            spans,
            clean_bounds,
            noisy_bounds,
            query,
            keys,
            values,
            attended,
            d_attended,
            lse,
            cosine,
            sine,
            *rows_t,
        )

    d_fields2, grad2 = backward(other, d_att2, spans, normed1_t)
    low_bit, high_bit = (place >> 2) & 1, (place >> 3) & 1
    moved, _ = tie(moved, grad2)
    gathered = in_order(
        high_bit,
        in_order(low_bit, gathered, moved[0], 1),
        in_order(low_bit, moved[1], moved[2], 1),
        1,
    )
    half = ROW_TILE // 2
    part_of = lambda array, which: lax.dynamic_slice_in_dim(array, which * half, half, 1)
    got = sibling(part_of(grad2, 1 - core))
    crossing = (part_of(grad2, core).astype(f32) + got.astype(f32)).astype(bf16)
    (crossing, gathered), spans = tie((crossing, gathered), spans)
    crossed = across(crossing)
    moved = beside(gathered)
    (d_fields1,) = backward(mine, d_att, spans)
    moved, d_fields1 = tie(moved, d_fields1)
    gathered = in_order(side, gathered, moved, 1)
    gathered, d_fields1 = tie(gathered, d_fields1)
    moved = sibling(gathered)
    lead = hidden // width
    bias2, bias1 = grad_bias.reshape(2, lead, width)
    shared = jnp.concatenate([norms[:3], jnp.zeros((2, width), f32)], axis=0)
    grad_qkv, grad_out, grad_tokens, sums = leave(
        bits,
        normed1_t,
        grad_out,
        (crossed, crossed_out),
        (d_fields1, d_fields2),
        (qkv_mine, qkv_other),
        x_rows,
        context,
        vectors,
        d_mid,
        jnp.concatenate([bias1, shared], axis=0),
        jnp.concatenate([bias2, shared], axis=0),
    )
    moved, _ = tie(moved, grad_qkv)
    grad_down, grad_up = assemble(core.reshape(1), gathered, moved)
    return (
        out.reshape(tokens.shape),
        grad_tokens.reshape(tokens.shape),
        sums[lead + 3],
        sums[lead + 4],
        grad_qkv.transpose(1, 0, 2).astype(f32),
        grad_out.astype(f32),
        sums[lead],
        sums[lead + 1],
        grad_up,
        sums[:lead].reshape(hidden),
        grad_down,
        sums[lead + 2],
    )


def solution(mesh):
    in_specs = (
        P(None, ("dp", "mp"), None),
        P("dp", None),
        P(),
        P(None, ("dp", "mp"), None),
        P(),
        P(),
        P(None, None, "mp"),
        P("mp", None),
        P(),
        P(),
        P(None, "mp"),
        P("mp"),
        P("mp", None),
        P(),
    )
    out_specs = (
        P(None, ("dp", "mp"), None),
        P(None, ("dp", "mp"), None),
        P(),
        P(),
        P(None, None, "mp"),
        P("mp", None),
        P(),
        P(),
        P(None, "mp"),
        P("mp"),
        P("mp", None),
        P(),
    )
    return jax.shard_map(
        functools.partial(local, mesh.shape["dp"]),
        mesh=mesh,
        in_specs=in_specs,
        out_specs=out_specs,
        check_vma=False,
    )
```

```python
import functools
import math

import jax
import jax.numpy as jnp
from jax import lax
from jax.experimental import pallas as pl
from jax.experimental.pallas import tpu as pltpu
from jax.sharding import PartitionSpec as P

HD = 64
TOK_DEV = 1024
HALF = TOK_DEV // 2
EDGE = 16
CLEAN_OWN = HALF
NOISY_BASE = 2 * HALF + EDGE
NOISY_OWN = NOISY_BASE + EDGE
KEY_ROWS = NOISY_OWN + HALF + EDGE
TILE = 128
TILES = HALF // TILE
WINDOW = TILE + 2 * EDGE
KEY_TILE = 192
LANES = 128
HIDDEN_TILE = 256
ROW_TILE = 256

epsilon = 1e-05
neg_large = -1e30
to_base2 = 0.125 * math.log2(math.e)
f32 = jnp.float32
bf16 = jnp.bfloat16

NN = (((1,), (0,)), ((), ()))
NT = (((1,), (1,)), ((), ()))


def dot(left, right, dims=NN):
    return lax.dot_general(left, right, dims, preferred_element_type=f32)


def low_lanes(shape):
    return lax.broadcasted_iota(jnp.int32, shape, 1) < HD


def turn(values, cosine, sine):
    lane = lax.broadcasted_iota(jnp.int32, values.shape, 1)
    first_half = (lane & (HD - 1)) < HD // 2
    swapped = jnp.where(
        first_half,
        pltpu.roll(values, LANES - HD // 2, 1),
        pltpu.roll(values, HD // 2, 1),
    )
    return values * cosine + swapped * sine


def project_rows(rows, w_ref, cosine, sine, q_ref, k_ref, v_ref, at):
    for part, out_ref in ((0, q_ref), (1, k_ref)):
        field = dot(rows, w_ref[part])
        for pair in range(field.shape[1] // LANES):
            cols = slice(pair * LANES, (pair + 1) * LANES)
            out_ref[at, cols] = turn(field[:, cols], cosine, sine).astype(bf16)
    v_ref[at, :] = dot(rows, w_ref[2]).astype(bf16)


def project_kernel(rows_ref, w_ref, cos_ref, sin_ref, q_ref, k_ref, v_ref):
    at = slice(0, rows_ref.shape[0])
    project_rows(rows_ref[...], w_ref, cos_ref[...], sin_ref[...], q_ref, k_ref, v_ref, at)


def project(rows, weights, cosine, sine):
    count, width = rows.shape
    cols = weights.shape[2]
    step = count // 3
    row_spec = pl.BlockSpec((step, width), lambda i: (i, 0))
    table_spec = pl.BlockSpec((step, LANES), lambda i: (i, 0))
    out_spec = pl.BlockSpec((step, cols), lambda i: (i, 0))
    shape = jax.ShapeDtypeStruct((count, cols), bf16)
    return pl.pallas_call(
        project_kernel,
        grid=(3,),
        in_specs=[
            row_spec,
            pl.BlockSpec(weights.shape, lambda i: (0, 0, 0)),
            table_spec,
            table_spec,
        ],
        out_specs=[out_spec] * 3,
        out_shape=[shape] * 3,
        name="project",
        cost_estimate=pl.CostEstimate(
            flops=2 * count * width * 3 * cols,
            bytes_accessed=2 * (count * (width + 3 * cols) + 3 * width * cols),
            transcendentals=0,
        ),
    )(rows, weights, cosine, sine)


def normal(values):
    average = jnp.mean(values, axis=-1, keepdims=True)
    centred = values - average
    variance = jnp.mean(centred * centred, axis=-1, keepdims=True)
    scale = lax.rsqrt(variance + epsilon)
    return centred * scale, scale


def enter_kernel(
    tokens_ref,
    context_ref,
    vectors_ref,
    w_ref,
    cos_ref,
    sin_ref,
    rows_ref,
    rows_t_ref,
    q_ref,
    k_ref,
    v_ref,
):
    def norm(values):
        unit = normal(values.astype(f32))[0]
        return (unit * vectors_ref[0:1, :] + vectors_ref[1:2, :]).astype(bf16)

    def blocks(i, _):
        source = pl.ds(pl.multiple_of(i * TILE, TILE), TILE)
        rows_ref[source, :] = norm(context_ref[source, :])
        at = pl.ds(pl.multiple_of(CLEAN_OWN + i * TILE, TILE), TILE)
        rows_ref[at, :] = norm(tokens_ref[1, source, :])
        at = pl.ds(pl.multiple_of(NOISY_OWN + i * TILE, EDGE), TILE)
        rows_ref[at, :] = norm(tokens_ref[0, source, :])
        return 0

    lax.fori_loop(0, TILES, blocks, 0)
    rows_ref[2 * HALF : NOISY_BASE, :] = rows_ref[:EDGE, :]
    edge = norm(context_ref[HALF:, :])
    rows_ref[NOISY_BASE:NOISY_OWN, :] = edge
    rows_ref[NOISY_OWN + HALF :, :] = edge
    step = KEY_ROWS // 3

    def fields(i, _):
        at = pl.ds(pl.multiple_of(i * step, EDGE), step)
        project_rows(
            rows_ref[at, :], w_ref, cos_ref[at, :], sin_ref[at, :], q_ref, k_ref, v_ref, at
        )
        return 0

    lax.fori_loop(0, 3, fields, 0)
    for c in range(rows_t_ref.shape[0] // LANES):
        cols = slice(c * LANES, (c + 1) * LANES)
        rows_t_ref[cols, :] = rows_ref[:, cols].T


def enter(tokens, context, vectors, weights, cosine, sine):
    width, cols = weights.shape[1:]
    vmem = pl.BlockSpec(memory_space=pltpu.VMEM)
    shape = jax.ShapeDtypeStruct
    field = shape((KEY_ROWS, cols), bf16)
    return pl.pallas_call(
        enter_kernel,
        in_specs=[vmem] * 6,
        out_specs=[vmem] * 5,
        out_shape=[shape((KEY_ROWS, width), bf16), shape((width, KEY_ROWS), bf16)] + [field] * 3,
        name="enter",
        cost_estimate=pl.CostEstimate(
            flops=10**10, bytes_accessed=16 * 10**6, transcendentals=0
        ),
    )(tokens, context, vectors, weights, cosine, sine)


def split_heads(rows):
    low = low_lanes(rows.shape)
    zero = jnp.zeros_like(rows)
    return jnp.where(low, rows, zero), jnp.where(low, zero, rows)


def between(shape, offset, low, high):
    index = lax.broadcasted_iota(jnp.int32, shape, 0) + offset
    return jnp.logical_and(index >= low, index < high)


def fold(values, combine):
    rows, cols = values.shape
    groups = values.reshape(rows // 8, 8, cols)
    return combine(groups, axis=0)


def forward_kernel(
    span_ref, clean_ref, noisy_ref, q_ref, k_ref, v_ref, out_ref, lse_ref, bias_ref, window_ref
):
    pairs = q_ref.shape[1] // LANES
    lanes = [slice(p * LANES, (p + 1) * LANES) for p in range(pairs)]

    def one_tile(t, _):
        clean_at = pl.multiple_of(CLEAN_OWN + t * TILE, TILE)
        noisy_at = pl.multiple_of(NOISY_OWN + t * TILE, EDGE)
        window_at = pl.multiple_of(NOISY_BASE + t * TILE, EDGE)
        key_low, key_high = clean_ref[t, 0:1, :], clean_ref[t, 1:2, :]
        own_low, own_high = noisy_ref[t, 0:1, :], noisy_ref[t, 1:2, :]
        allowed = between((WINDOW, TILE), 0, own_low, own_high)
        window_ref[...] = jnp.where(allowed, 0.0, neg_large)
        first_key, trips = span_ref[t, 0], span_ref[t, 1]
        queries, tops = [], []
        for cols in lanes:
            query = jnp.concatenate(
                [q_ref[pl.ds(noisy_at, TILE), cols], q_ref[pl.ds(clean_at, TILE), cols]], axis=0
            )
            heads = split_heads(query)
            queries += heads
            keys = k_ref[pl.ds(window_at, WINDOW), cols]
            for head in range(2):
                scores = dot(keys, heads[head][:TILE], NT) + window_ref[...]
                top = fold(scores, jnp.max)
                tops.append(
                    jnp.concatenate([top, jnp.full((8, TILE), neg_large, f32)], axis=1)
                )

        def first_pass(j, tops):
            at = pl.multiple_of(first_key + j * KEY_TILE, EDGE)
            allowed = between((KEY_TILE, 2 * TILE), at, key_low, key_high)
            bias_ref[j] = jnp.where(allowed, 0.0, neg_large)
            after = []
            for p, cols in enumerate(lanes):
                keys = k_ref[pl.ds(at, KEY_TILE), cols]
                for head in range(2):
                    scores = dot(keys, queries[2 * p + head], NT) + bias_ref[j]
                    after.append(jnp.maximum(tops[2 * p + head], fold(scores, jnp.max)))
            return tuple(after)

        tops = lax.fori_loop(0, trips, first_pass, tuple(tops))
        tops = [jnp.max(top, axis=0, keepdims=True) * to_base2 for top in tops]
        state = []
        keys = [k_ref[pl.ds(window_at, WINDOW), cols] for cols in lanes]
        values_t = [v_ref[pl.ds(window_at, WINDOW), cols].T for cols in lanes]
        scores = dot(keys[0], queries[0][:TILE], NT)
        late = None
        for h in range(2 * pairs):
            if h + 1 < 2 * pairs:
                ahead = dot(keys[(h + 1) // 2], queries[h + 1][:TILE], NT)
            expo = jnp.exp2(scores * to_base2 - tops[h][:, :TILE] + window_ref[...])
            if late is not None:
                state.append(jnp.concatenate([late, jnp.zeros((HD, TILE), f32)], axis=1))
            total = fold(expo, jnp.sum)
            state.append(jnp.concatenate([total, jnp.zeros((8, TILE), f32)], axis=1))
            side = slice(h % 2 * HD, (h % 2 + 1) * HD)
            late = dot(values_t[h // 2][side], expo.astype(bf16))
            scores = ahead
        state.append(jnp.concatenate([late, jnp.zeros((HD, TILE), f32)], axis=1))

        def second_pass(j, state):
            at = pl.multiple_of(first_key + j * KEY_TILE, EDGE)
            keys = [k_ref[pl.ds(at, KEY_TILE), cols] for cols in lanes]
            values_t = [v_ref[pl.ds(at, KEY_TILE), cols].T for cols in lanes]
            after = list(state)
            scores = dot(keys[0], queries[0], NT)
            late = None
            for h in range(2 * pairs):
                ahead = dot(keys[(h + 1) // 2], queries[h + 1], NT) if h + 1 < 2 * pairs else None
                expo = jnp.exp2(scores * to_base2 - tops[h] + bias_ref[j])
                after[2 * h] = state[2 * h] + fold(expo, jnp.sum)
                if late is not None:
                    after[2 * h - 1] = state[2 * h - 1] + late
                side = slice(h % 2 * HD, (h % 2 + 1) * HD)
                late = dot(values_t[h // 2][side], expo.astype(bf16))
                scores = ahead
            after[-1] = state[-1] + late
            return tuple(after)

        state = lax.fori_loop(0, trips, second_pass, tuple(state))
        low_at = pl.ds(pl.multiple_of(t * TILE, TILE), TILE)
        high_at = pl.ds(pl.multiple_of(HALF + t * TILE, TILE), TILE)
        for p, cols in enumerate(lanes):
            halves = []
            for head in range(2):
                h = 2 * p + head
                total = jnp.sum(state[2 * h], axis=0, keepdims=True)
                halves.append(state[2 * h + 1] / total)
                lse_ref[p, t, head : head + 1, :] = tops[h] + jnp.log2(total)
            pair = jnp.concatenate(halves, axis=0).T.astype(bf16)
            out_ref[low_at, cols] = pair[:TILE]
            out_ref[high_at, cols] = pair[TILE:]
        return 0

    lax.fori_loop(0, TILES, one_tile, 0)


def attend_forward(spans, clean_bounds, noisy_bounds, query, keys, values):
    count, cols = query.shape
    pairs = cols // LANES
    vmem = pl.BlockSpec(memory_space=pltpu.VMEM)
    work = pairs * 2 * 2 * HALF * TOK_DEV
    return pl.pallas_call(
        forward_kernel,
        in_specs=[pl.BlockSpec(memory_space=pltpu.SMEM)] + [vmem] * 5,
        out_specs=[vmem] * 2,
        out_shape=[
            jax.ShapeDtypeStruct((TOK_DEV, cols), bf16),
            jax.ShapeDtypeStruct((pairs, TILES, 2, 2 * TILE), f32),
        ],
        scratch_shapes=[
            pltpu.VMEM((NOISY_BASE // KEY_TILE + 1, KEY_TILE, 2 * TILE), f32),
            pltpu.VMEM((WINDOW, TILE), f32),
        ],
        name="attend_forward",
        cost_estimate=pl.CostEstimate(
            flops=4 * work * HD, bytes_accessed=8 * count * cols, transcendentals=work
        ),
    )(spans, clean_bounds, noisy_bounds, query, keys, values)


def backward_kernel(
    span_ref,
    clean_ref,
    noisy_ref,
    q_ref,
    k_ref,
    v_ref,
    o_ref,
    d_ref,
    lse_ref,
    cos_ref,
    sin_ref,
    *refs,
):
    rows_ref, out_ref, grad_ref, dk_ref, dv_ref, bias_ref = refs if len(refs) == 6 else (
        None,
        refs[0],
        None,
        *refs[1:],
    )
    pairs = q_ref.shape[1] // LANES
    lanes = [slice(p * LANES, (p + 1) * LANES) for p in range(pairs)]
    dk_ref[...] = jnp.zeros_like(dk_ref)
    dv_ref[...] = jnp.zeros_like(dv_ref)
    out_ref[0] = jnp.zeros_like(out_ref[0])

    def one_tile(t, _):
        clean_at = pl.multiple_of(CLEAN_OWN + t * TILE, TILE)
        noisy_at = pl.multiple_of(NOISY_OWN + t * TILE, EDGE)
        window_at = pl.multiple_of(NOISY_BASE + t * TILE, EDGE)
        low_at = pl.multiple_of(t * TILE, TILE)
        high_at = pl.multiple_of(HALF + t * TILE, TILE)
        key_low, key_high = clean_ref[t, 0:1, :], clean_ref[t, 1:2, :]
        own_low, own_high = noisy_ref[t, 0:1, :], noisy_ref[t, 1:2, :]
        queries, d_outs, inners, lses = [], [], [], []
        for p, cols in enumerate(lanes):

            def both(ref, low, high):
                return jnp.concatenate(
                    [ref[pl.ds(low, TILE), cols], ref[pl.ds(high, TILE), cols]], axis=0
                )

            queries.append(split_heads(both(q_ref, noisy_at, clean_at)))
            d_rows = both(d_ref, low_at, high_at)
            o_rows = both(o_ref, low_at, high_at)
            product = (d_rows.astype(f32) * o_rows.astype(f32)).T
            d_outs.append(split_heads(d_rows))
            inners.append(
                [
                    jnp.sum(product[head * HD : (head + 1) * HD], axis=0, keepdims=True) * 0.125
                    for head in range(2)
                ]
            )
            lses.append([lse_ref[p, t, head : head + 1, :] for head in range(2)])

        def accumulate(at, rows, cols, allowed, d_query):
            bias_ref[:rows, :cols] = jnp.where(allowed, 0.0, neg_large)
            after = list(d_query)
            keys = [k_ref[pl.ds(at, rows), span] for span in lanes]
            eighth = [v_ref[pl.ds(at, rows), span] * jnp.asarray(0.125, bf16) for span in lanes]
            keys_t = [part.T for part in keys]
            stack = lambda parts: jnp.concatenate([part[:cols] for part in parts], axis=0)

            def begin(h):
                p, head = h // 2, h % 2
                return (
                    dot(keys[p], queries[p][head][:cols], NT),
                    dot(eighth[p], d_outs[p][head][:cols], NT),
                )

            def finish_pair(p, weights, d_scores):
                span = lanes[p]
                for head in range(2):
                    side = slice(head * HD, (head + 1) * HD)
                    h = 2 * p + head
                    after[h] = d_query[h] + dot(keys_t[p][side], d_scores[head])
                dv_ref[pl.ds(at, rows), span] += dot(
                    jnp.concatenate(weights, axis=1), stack(d_outs[p])
                )
                dk_ref[pl.ds(at, rows), span] += dot(
                    jnp.concatenate(d_scores, axis=1), stack(queries[p])
                )

            ready = begin(0)
            held = None
            weights, d_scores = [], []
            for h in range(2 * pairs):
                ahead = begin(h + 1) if h + 1 < 2 * pairs else None
                p, head = h // 2, h % 2
                scores = ready[0] * to_base2 - lses[p][head][:, :cols] + bias_ref[:rows, :cols]
                probs = jnp.exp2(scores)
                d_score = (probs * (ready[1] - inners[p][head][:, :cols])).astype(bf16)
                weights.append(probs.astype(bf16))
                d_scores.append(d_score)
                if held is not None:
                    finish_pair(*held)
                    held = None
                if head == 1:
                    held = (p, weights, d_scores)
                    weights, d_scores = [], []
                ready = ahead
            finish_pair(*held)
            return tuple(after)

        allowed = between((WINDOW, TILE), 0, own_low, own_high)
        zero = jnp.zeros((HD, TILE), f32)
        start = accumulate(window_at, WINDOW, TILE, allowed, (zero,) * (2 * pairs))
        start = tuple(jnp.concatenate([part, zero], axis=1) for part in start)
        first_key, trips = span_ref[t, 0], span_ref[t, 1]

        def one_step(j, d_query):
            at = pl.multiple_of(first_key + j * KEY_TILE, EDGE)
            allowed = between((KEY_TILE, 2 * TILE), at, key_low, key_high)
            return accumulate(at, KEY_TILE, 2 * TILE, allowed, d_query)

        d_query = lax.fori_loop(0, trips, one_step, start)
        for p, span in enumerate(lanes):
            pair = jnp.concatenate(d_query[2 * p : 2 * p + 2], axis=0).T
            for at, part in ((noisy_at, pair[:TILE]), (clean_at, pair[TILE:])):
                turned = turn(part, cos_ref[pl.ds(at, TILE), :], -sin_ref[pl.ds(at, TILE), :])
                out_ref[0, pl.ds(at, TILE), span] = turned.astype(bf16)
        return 0

    lax.fori_loop(0, TILES, one_tile, 0)
    step = KEY_ROWS // 9

    def finish(i, _):
        rows = pl.ds(pl.multiple_of(i * step, EDGE), step)
        for span in lanes:
            out_ref[1, rows, span] = turn(
                dk_ref[rows, span], cos_ref[rows, :], -sin_ref[rows, :]
            ).astype(bf16)
        out_ref[2, rows, :] = dv_ref[rows, :].astype(bf16)
        return 0

    lax.fori_loop(0, 9, finish, 0)

    def weight_rows(i, _):
        rows = pl.ds(pl.multiple_of(i * ROW_TILE, LANES), ROW_TILE)
        for c in range(3):
            grad_ref[c, rows, :] = dot(rows_ref[rows, :], out_ref[c]).astype(bf16)
        return 0

    if rows_ref is not None:
        lax.fori_loop(0, rows_ref.shape[0] // ROW_TILE, weight_rows, 0)


def attend_backward(
    spans,
    clean_bounds,
    noisy_bounds,
    query,
    keys,
    values,
    attended,
    d_attended,
    lse,
    cosine,
    sine,
    *rows_t,
):
    count, cols = query.shape
    vmem = pl.BlockSpec(memory_space=pltpu.VMEM)
    return pl.pallas_call(
        backward_kernel,
        in_specs=[pl.BlockSpec(memory_space=pltpu.SMEM)] + [vmem] * (10 + len(rows_t)),
        out_specs=[vmem] * (1 + len(rows_t)),
        scratch_shapes=[
            pltpu.VMEM((count, cols), f32),
            pltpu.VMEM((count, cols), f32),
            pltpu.VMEM((max(KEY_TILE, WINDOW), 2 * TILE), f32),
        ],
        out_shape=[
            jax.ShapeDtypeStruct((3, count, cols), bf16),
            *[jax.ShapeDtypeStruct((3, rows.shape[0], cols), bf16) for rows in rows_t],
        ],
        name="attend_backward",
        cost_estimate=pl.CostEstimate(
            flops=36 * 10**9, bytes_accessed=36 * 10**6, transcendentals=6 * 10**6
        ),
    )(
        spans,
        clean_bounds,
        noisy_bounds,
        query,
        keys,
        values,
        attended,
        d_attended,
        lse,
        cosine,
        sine,
        *rows_t,
    )


PIECES = 16
MESH = pl.DeviceIdType.MESH


def flip(value, mask):
    result = value
    for b in range(mask.bit_length()):
        if mask >> b & 1:
            result = result + (1 << b) * (1 - 2 * ((value // (1 << b)) % 2))
    return result


class Exchange:
    def __init__(self, bits, count, rows, width, back=True):
        self.bits, self.count, self.rows, self.width = bits, count, rows, width
        self.back = back
        self.half, self.quarter, self.piece = rows // 2, rows // 4, rows // PIECES
        self.extra = list(range(4, bits))

    def slots(self):
        return 8 + 2 * (6 if self.back else 4) + (3 if self.extra else 0)

    def scratch(self):
        k, w = self.count, self.width
        cross = k if not self.back else 1
        shapes = [
            pltpu.VMEM((k, 2 - self.back, self.half, w), bf16),
            pltpu.VMEM((cross, self.half, w), bf16),
            pltpu.VMEM((cross, self.half, w), bf16),
            pltpu.VMEM((k, self.quarter, w), bf16),
            pltpu.VMEM((k, self.quarter, w), bf16),
            pltpu.VMEM((k, self.quarter, w), f32),
            pltpu.VMEM((k, 3, self.piece, w), bf16),
            pltpu.VMEM((k, 3, self.piece, w), bf16),
        ]
        lanes_of = (1, 0, 1, 3, 3, 1, 1) if self.back else (2, 1, 1, 3, 0, 0, 0)
        for lanes in [lanes for lanes in lanes_of if lanes]:
            shapes += [pltpu.SemaphoreType.DMA((k, lanes))] * 2
        if self.extra:
            n = len(self.extra)
            shapes += [pltpu.VMEM((k, 2 * n, self.piece, w), bf16)]
            shapes += [pltpu.SemaphoreType.DMA((k, n))] * 2
        return shapes

    def bind(self, place, part, refs):
        (self.a_in, self.b_out, self.b_in, self.c_out, self.c_in, self.keep) = refs[:6]
        self.d_out, self.d_in = refs[6:8]
        names = "acdefg" if self.back else "abcd"
        self.sems = {name: (refs[8 + 2 * i], refs[9 + 2 * i]) for i, name in enumerate(names)}
        if self.extra:
            at = 8 + 2 * len(names)
            self.x_buf, self.x_send, self.x_recv = refs[at : at + 3]
        self.place, self.part = place, part
        self.core, self.x, self.z = place % 2, (place // 2) % 2, (place // 4) % 4
        self.sibling = {"dp": flip(place, 1)}
        self.beside = {"dp": flip(place, 2)}
        self.across = {"mp": 1 - part}
        self.peers = [{"dp": flip(place, j << 2)} for j in range(1, 4)]
        self.partners = [self.sibling, self.beside, self.across] + self.peers
        self.partners += [{"dp": flip(place, 1 << b)} for b in self.extra]
        return self

    def greet(self):
        barrier = pltpu.get_barrier_semaphore()
        for partner in self.partners:
            pl.semaphore_signal(barrier, inc=1, device_id=partner, device_id_type=MESH)
        pl.semaphore_wait(barrier, len(self.partners))

    def copy(self, name, k, lane, source, target, device):
        out, into = self.sems[name]
        return pltpu.make_async_remote_copy(
            src_ref=source,
            dst_ref=target,
            send_sem=out.at[k, lane],
            recv_sem=into.at[k, lane],
            device_id=device,
            device_id_type=MESH,
        )

    def rows_at(self, start, size):
        return pl.ds(pl.multiple_of(start, PIECES), size)

    def copy_a(self, k, lane, grads):
        source = grads.at[k, self.rows_at((1 - self.core) * self.half, self.half)]
        return self.copy("a", k, lane, source, self.a_in.at[k, lane], self.sibling)

    def copy_b(self, k):
        return self.copy("b", k, 0, self.b_out.at[k], self.b_in.at[k], self.across)

    def copy_c(self, k):
        return self.copy("c", k, 0, self.c_out.at[k], self.c_in.at[k], self.beside)

    def copy_d(self, k, j):
        return self.copy("d", k, j, self.d_out.at[k, j], self.d_in.at[k, j], self.peers[j])

    def spot(self, change=0):
        start = self.core * self.half + self.x * self.quarter
        return self.rows_at(start + flip(self.z, change) * self.piece, self.piece)

    def copy_e(self, k, j, full):
        rows = full.at[k, self.spot()]
        return self.copy("e", k, j, rows, rows, self.peers[j])

    def copy_f(self, k, full):
        start = self.core * self.half + self.x * self.quarter
        rows = full.at[k, self.rows_at(start, self.quarter)]
        return self.copy("f", k, 0, rows, rows, self.beside)

    def copy_g(self, k, full):
        rows = full.at[k, self.rows_at(self.core * self.half, self.half)]
        return self.copy("g", k, 0, rows, rows, self.sibling)

    def start_a(self, k, lane, grads):
        self.copy_a(k, lane, grads).start()

    def stage_b(self, k, others):
        self.copy_a(k, 0, others).wait()
        mine = others[k, self.rows_at(self.core * self.half, self.half), :].astype(f32)
        self.b_out[k] = (mine + self.a_in[k, 0].astype(f32)).astype(bf16)
        self.copy_b(k).start()

    def stage_c(self, k, grads, crossed=None):
        lane = 0 if self.back else 1
        self.copy_a(k, lane, grads).wait()
        if not self.back:
            self.copy_b(k).wait()

        def total(which):
            inner = which * self.quarter
            rows = self.rows_at(inner, self.quarter)
            mine = grads[k, self.rows_at(self.core * self.half + inner, self.quarter), :]
            got = self.a_in[k, lane, rows, :].astype(f32)
            if not self.back:
                got = got + self.b_in[k, rows, :].astype(f32)
            elif crossed is not None:
                got = got + crossed(rows)
            return mine.astype(f32) + got

        self.c_out[k] = total(1 - self.x).astype(bf16)
        self.copy_c(k).start()
        self.keep[k] = total(self.x)

    def stage_d(self, k):
        self.copy_c(k).wait()
        for j in range(4):
            rows = self.rows_at(flip(self.z, j) * self.piece, self.piece)
            total = self.keep[k, rows, :] + self.c_in[k, rows, :].astype(f32)
            if j:
                self.d_out[k, j - 1] = total.astype(bf16)
                self.copy_d(k, j - 1).start()
            else:
                self.keep[k, rows, :] = total

    def gather_d(self, k):
        rows = self.rows_at(self.z * self.piece, self.piece)
        total = self.keep[k, rows, :]
        for j in range(3):
            self.copy_d(k, j).wait()
            total = total + self.d_in[k, j].astype(f32)
        for i, b in enumerate(self.extra):
            mine = self.x_buf.at[k, 2 * i]
            mine[...] = total.astype(bf16)
            swap = pltpu.make_async_remote_copy(
                src_ref=mine,
                dst_ref=self.x_buf.at[k, 2 * i + 1],
                send_sem=self.x_send.at[k, i],
                recv_sem=self.x_recv.at[k, i],
                device_id={"dp": flip(self.place, 1 << b)},
                device_id_type=MESH,
            )
            swap.start()
            swap.wait()
            total = total.astype(bf16).astype(f32) + self.x_buf[k, 2 * i + 1].astype(f32)
        return total.astype(bf16)

    def stage_e(self, k, full):
        full[k, self.spot(), :] = self.gather_d(k)
        for j in range(3):
            self.copy_e(k, j, full).start()

    def stage_f(self, k, full):
        for j in range(3):
            self.copy_e(k, j, full).wait()
        self.copy_f(k, full).start()

    def stage_g(self, k, full):
        self.copy_f(k, full).wait()
        self.copy_g(k, full).start()

    def stage_h(self, k, full):
        self.copy_g(k, full).wait()


def at_step(step, count, action):
    @pl.when(jnp.logical_and(step >= 0, step < count))
    def _():
        action(step)


def middle_kernel(exchanges, tiles, *refs):
    (
        x_ref,
        att_ref,
        att2_ref,
        wout_ref,
        wout2_ref,
        dy_ref,
        vectors_ref,
        bup_ref,
        up_mine,
        up_here,
        up_beside,
        down_mine,
        down_here,
        out_hbm,
        mid_hbm,
        datt_hbm,
        datt2_hbm,
        gout_ref,
        gout2_ref,
        gbup_ref,
        small_ref,
        pieces_ref,
        up_there,
        down_there,
        pass_up,
        pass_down,
        up_buf,
        down_buf,
        load_sem,
        n2_ref,
        total_ref,
        dn2_ref,
        act_ref,
        dpre_ref,
        n2_t,
        bup_other,
        bias_sem,
        out_ref,
        mid_ref,
        datt_ref,
        datt2_ref,
        store_sem,
        down_grad,
        up_grad,
        *rest,
    ) = refs
    place, part = lax.axis_index("dp"), lax.axis_index("mp")
    ex = exchanges[0].bind(place, part, rest)
    ex_up = exchanges[1].bind(place, part, rest[exchanges[0].slots() :])
    sides = ((ex, down_grad), (ex_up, up_grad))
    core = ex.core
    count = tiles // 2
    rows_all = x_ref.shape[0]
    blocks = rows_all // ROW_TILE
    width = x_ref.shape[1]
    lanes = width // 2

    def which(i):
        other = jnp.logical_or(i == 0, jnp.logical_and(i % 2 == 1, i < tiles - 1))
        mine = jnp.where(i == tiles - 1, count - 1, i // 2 - 1)
        return other, jnp.where(other, (i + 1) // 2, mine)

    quarter = width // 4
    strip = HIDDEN_TILE // 2
    held = 2 * core + ex.x
    kept = 2 * core + 1 - ex.x

    def load_up(i, source, h):
        target = up_buf.at[i % 2, h * quarter : (h + 1) * quarter]
        return pltpu.make_async_copy(source, target, load_sem.at[i % 2, h])

    def load_down(i, source, h):
        target = down_buf.at[i % 2, h * strip : (h + 1) * strip]
        return pltpu.make_async_copy(source, target, load_sem.at[i % 2, 4 + h])

    def hand_up(k, part_of):
        cols = pl.ds(pl.multiple_of(k * HIDDEN_TILE, HIDDEN_TILE), HIDDEN_TILE)
        side = ex.x if part_of == 0 else 1 - ex.x
        rows = pl.ds(pl.multiple_of(side * quarter, EDGE), quarter)
        return pltpu.make_async_remote_copy(
            src_ref=(up_here, up_beside)[part_of].at[:, cols],
            dst_ref=up_there.at[k, rows],
            send_sem=pass_up.at[k, 2 * part_of],
            recv_sem=pass_up.at[k, 2 * part_of + 1],
            device_id=ex.sibling,
            device_id_type=MESH,
        )

    def hand_down(b):
        return pltpu.make_async_remote_copy(
            src_ref=down_here.at[strip_rows(b)],
            dst_ref=down_there.at[b],
            send_sem=pass_down.at[b, 0],
            recv_sem=pass_down.at[b, 1],
            device_id=ex.sibling,
            device_id_type=MESH,
        )

    def strip_rows(b):
        return pl.ds(pl.multiple_of(b * strip, strip), strip)

    def start_loads(i):
        other, k = which(i)
        mine = jnp.logical_not(other)
        cols = pl.ds(pl.multiple_of(k * HIDDEN_TILE, HIDDEN_TILE), HIDDEN_TILE)

        @pl.when(other)
        def _():
            hand_up(k, 0).wait()
            hand_up(k, 1).wait()

        for h in range(4):

            @pl.when(mine)
            def _():
                load_up(i, up_mine.at[h * quarter : (h + 1) * quarter, cols], h).start()

            @pl.when(jnp.logical_and(other, held == h))
            def _():
                load_up(i, up_here.at[:, cols], h).start()

            @pl.when(jnp.logical_and(other, kept == h))
            def _():
                load_up(i, up_beside.at[:, cols], h).start()

            @pl.when(jnp.logical_and(other, core != h // 2))
            def _():
                rows = slice(h % 2 * quarter, (h % 2 + 1) * quarter)
                load_up(i, up_there.at[k, rows], h).start()

        for h in range(2):
            b = 2 * k + h
            inner = b % count

            @pl.when(mine)
            def _():
                load_down(i, down_mine.at[strip_rows(b), :], h).start()

            @pl.when(jnp.logical_and(other, core == b // count))
            def _():
                load_down(i, down_here.at[strip_rows(inner), :], h).start()

            @pl.when(jnp.logical_and(other, core != b // count))
            def _():
                hand_down(inner).wait_recv()
                load_down(i, down_there.at[inner], h).start()

    def wait_loads(i):
        for h in range(4):
            load_up(i, up_mine.at[:quarter, :HIDDEN_TILE], h).wait()
        for h in range(2):
            load_down(i, down_mine.at[:strip, :], h).wait()

    ex.greet()
    bias_swap = pltpu.make_async_remote_copy(
        src_ref=bup_ref,
        dst_ref=bup_other,
        send_sem=bias_sem.at[0],
        recv_sem=bias_sem.at[1],
        device_id=ex.across,
        device_id_type=MESH,
    )
    bias_swap.start()

    def hand(k, _):
        hand_up(k, 0).start()
        hand_up(k, 1).start()
        hand_down(k).start()
        return 0

    lax.fori_loop(0, count, hand, 0)

    def prologue(r, _):
        rows = pl.ds(pl.multiple_of(r * ROW_TILE, ROW_TILE), ROW_TILE)
        branch = dot(att_ref[rows, :], wout_ref[...]) + dot(att2_ref[rows, :], wout2_ref[...])
        mid = x_ref[rows, :].astype(f32) + branch
        mid_ref[rows, :] = mid
        unit = normal(mid)[0]
        n2_ref[rows, :] = (unit * vectors_ref[2:3, :] + vectors_ref[3:4, :]).astype(bf16)
        total_ref[rows, :] = mid + vectors_ref[4:5, :]
        dn2_ref[rows, :] = jnp.zeros((ROW_TILE, width), f32)
        return 0

    lax.fori_loop(0, blocks, prologue, 0)
    start_loads(0)
    for c in range(width // LANES):
        cols = slice(c * LANES, (c + 1) * LANES)
        n2_t[cols, :] = n2_ref[:, cols].T
    n2_t[width:, :] = jnp.ones((PIECES, rows_all), bf16)
    bias_swap.wait()

    def tile(i):
        other, k = which(i)
        slot = i % 2
        wait_loads(i)

        @pl.when(i + 1 < tiles)
        def _():
            start_loads(i + 1)

        up, down = up_buf.at[slot], down_buf.at[slot]
        bias_at = jnp.where(other, k, count + k)
        bias = jnp.where(other, bup_other[k], bup_ref[k])
        linear = 0.7978845608028654
        cubic = linear * 0.044715
        for r in range(blocks):
            rows = slice(r * ROW_TILE, (r + 1) * ROW_TILE)
            pre = dot(n2_ref[rows, :], up[...]) + bias
            d_act = dot(dy_ref[rows, :], down[...], NT)
            square = pre * pre
            bend = jnp.tanh(pre * (square * cubic + linear))
            gate = 0.5 * bend + 0.5
            full_act = pre * gate
            slope = gate + (full_act - full_act * gate) * (square * (6.0 * cubic) + 2.0 * linear)
            act_ref[rows, :] = full_act.astype(bf16)
            dpre_ref[rows, :] = (d_act * slope).astype(bf16)
        total_ref[...] += dot(act_ref[...], down[...])
        dn2_ref[...] += dot(dpre_ref[...], up[...], NT)
        down_grad[k] = dot(act_ref[...].T, dy_ref[...]).astype(bf16)

        def start(lane):
            for side, grad in sides:
                side.start_a(k, lane, grad)

        by_rows = dot(n2_t[...], dpre_ref[...])
        up_grad[k] = by_rows[:width].astype(bf16)
        gbup_ref[bias_at] = by_rows[width : width + 1]
        pl.when(other)(functools.partial(start, 0))
        pl.when(jnp.logical_not(other))(functools.partial(start, 1))

    def each(k, when, action):
        @pl.when(jnp.logical_and(when, jnp.logical_and(k >= 0, k < count)))
        def _():
            for n, (side, grad) in enumerate(sides):
                action(n, side, grad, k)

    def stage_b(n, side, grad, k):
        side.stage_b(k, grad)

    def stage_c(n, side, grad, k):
        side.stage_c(k, grad)

    def stage_d(n, side, grad, k):
        side.stage_d(k)

    def arrive(n, side, grad, k):
        piece = side.gather_d(k)
        if n == 0:
            pieces_ref[k] = piece
        else:
            for c in range(width // HIDDEN_TILE):
                cols = slice(c * HIDDEN_TILE, (c + 1) * HIDDEN_TILE)
                pieces_ref[count + k, :, cols] = piece[c * PIECES : (c + 1) * PIECES]

    def steps(i):
        even = i % 2 == 0
        odd = jnp.logical_not(even)
        each((i - 5) // 2, odd, arrive)
        each((i - 4) // 2, even, stage_d)
        each((i - 3) // 2, odd, stage_c)
        each(i // 2, even, stage_b)

    def epilogue(r, _):
        rows = pl.ds(pl.multiple_of(r * ROW_TILE, ROW_TILE), ROW_TILE)
        out_ref[rows, :] = total_ref[rows, :].astype(bf16)
        unit, scale = normal(mid_ref[rows, :])
        d_rows = dn2_ref[rows, :]
        dy = dy_ref[rows, :].astype(f32)
        lean = d_rows * vectors_ref[2:3, :]
        d_mid = dy + scale * (
            lean
            - jnp.mean(lean, axis=-1, keepdims=True)
            - unit * jnp.mean(lean * unit, axis=-1, keepdims=True)
        )
        mid_ref[rows, :] = d_mid
        d_branch = d_mid.astype(bf16)
        n2_ref[rows, :] = d_branch
        datt_ref[rows, :] = dot(d_branch, wout_ref[...], NT).astype(bf16)
        datt2_ref[rows, :] = dot(d_branch, wout2_ref[...], NT).astype(bf16)
        add = lambda values: jnp.sum(values, axis=0, keepdims=True)
        small_ref[0:1, :] += add(d_rows * unit)
        small_ref[1:2, :] += add(d_rows)
        small_ref[2:3, :] += add(dy)
        return 0

    def out_grads():
        for source, target in ((att_ref, gout_ref), (att2_ref, gout2_ref)):
            grad = dot(source[...].T, n2_ref[...]).astype(bf16)
            for a in range(wout_ref.shape[0] // LANES):
                for b in range(2):
                    rows = slice(a * LANES, (a + 1) * LANES)
                    cols = slice(b * lanes, (b + 1) * lanes)
                    spread = slice(a * lanes, (a + 1) * lanes)
                    target[b * LANES : (b + 1) * LANES, spread] = grad[rows, cols]

    def main(i, _):
        pl.when(i < tiles)(functools.partial(tile, i))

        @pl.when(jnp.logical_and(i >= tiles, i < tiles + 2))
        def _():
            first = (i - tiles) * (blocks // 2)
            lax.fori_loop(first, first + blocks // 2, epilogue, 0)

        @pl.when(i == tiles + 2)
        def _():
            for store in stores:
                store.start()
            out_grads()

        steps(i)
        return 0

    small_ref[...] = jnp.zeros_like(small_ref)
    stores = [
        pltpu.make_async_copy(source, target, store_sem.at[n])
        for n, (source, target) in enumerate(
            (
                (datt2_ref, datt2_hbm),
                (out_ref, out_hbm),
                (mid_ref, mid_hbm),
                (datt_ref, datt_hbm),
            )
        )
    ]
    lax.fori_loop(0, tiles + 4, main, 0)
    for store in stores:
        store.wait()

    def handed(slot, _):
        hand_down(slot).wait_send()
        return 0

    lax.fori_loop(0, count, handed, 0)


def middle(bits, x, att, att2, wout, wout2, dy, vectors, bup, ups, downs):
    rows, width = x.shape
    hidden = ups[0].shape[1]
    count = hidden // HIDDEN_TILE
    tiles = 2 * count
    exchanges = (
        Exchange(bits, count, HIDDEN_TILE, width, False),
        Exchange(bits, count, width, HIDDEN_TILE, False),
    )
    vmem = pl.BlockSpec(memory_space=pltpu.VMEM)
    hbm = pl.BlockSpec(memory_space=pl.ANY)
    shape = jax.ShapeDtypeStruct
    depth = wout.shape[0]
    return pl.pallas_call(
        functools.partial(middle_kernel, exchanges, tiles),
        in_specs=[vmem] * 8 + [hbm] * 5,
        out_specs=[hbm] * 4 + [vmem] * 5,
        out_shape=[
            shape((rows, width), bf16),
            shape((rows, width), f32),
            shape(att.shape, bf16),
            shape(att2.shape, bf16),
            shape((2 * LANES, depth // LANES * width // 2), bf16),
            shape((2 * LANES, depth // LANES * width // 2), bf16),
            shape((tiles, 1, HIDDEN_TILE), f32),
            shape((8, width), f32),
            shape((2 * count, PIECES, width), bf16),
        ],
        scratch_shapes=[
            pltpu.VMEM((count, width // 2, HIDDEN_TILE), bf16),
            pltpu.VMEM((count, HIDDEN_TILE // 2, width), bf16),
            pltpu.SemaphoreType.DMA((count, 4)),
            pltpu.SemaphoreType.DMA((count, 2)),
            pltpu.VMEM((2, width, HIDDEN_TILE), bf16),
            pltpu.VMEM((2, HIDDEN_TILE, width), bf16),
            pltpu.SemaphoreType.DMA((2, 6)),
            pltpu.VMEM((rows, width), bf16),
            pltpu.VMEM((rows, width), f32),
            pltpu.VMEM((rows, width), f32),
            pltpu.VMEM((rows, HIDDEN_TILE), bf16),
            pltpu.VMEM((rows, HIDDEN_TILE), bf16),
            pltpu.VMEM((width + PIECES, rows), bf16),
            pltpu.VMEM(bup.shape, f32),
            pltpu.SemaphoreType.DMA((2,)),
            pltpu.VMEM((rows, width), bf16),
            pltpu.VMEM((rows, width), f32),
            pltpu.VMEM(att.shape, bf16),
            pltpu.VMEM(att2.shape, bf16),
            pltpu.SemaphoreType.DMA((4,)),
            pltpu.VMEM((count, HIDDEN_TILE, width), bf16),
            pltpu.VMEM((count, width, HIDDEN_TILE), bf16),
        ]
        + exchanges[0].scratch()
        + exchanges[1].scratch(),
        compiler_params=pltpu.CompilerParams(
            collective_id=0, has_side_effects=True, vmem_limit_bytes=67043328
        ),
        name="middle",
        cost_estimate=pl.CostEstimate(
            flops=60 * 10**9, bytes_accessed=40 * 10**6, transcendentals=4 * 10**6
        ),
    )(x, att, att2, wout, wout2, dy, vectors, bup, *ups, *downs)


def leave_kernel(exchange, *refs):
    (
        rows_hbm,
        mine_out_ref,
        crossed_ref,
        crossed_out_ref,
        d_hbm,
        d2_hbm,
        w_hbm,
        w2_hbm,
        tokens_ref,
        context_ref,
        vectors_ref,
        dmid_hbm,
        small_ref,
        small2_ref,
        gqkv_ref,
        gout_ref,
        back_ref,
        sums_ref,
        full_ref,
        out_buf,
        rows_t_ref,
        d_ref,
        d2_ref,
        w_ref,
        w2_ref,
        dmid_ref,
        load_sem,
        rows_ref,
        give_ref,
        take_ref,
        swap_sem,
        norm_ref,
        near_ref,
        far_ref,
        near_sem,
        far_sem,
        *rest,
    ) = refs
    place, part = lax.axis_index("dp"), lax.axis_index("mp")
    ex = exchange.bind(place, part, rest)
    count, bits = ex.count, ex.bits
    loads = [
        pltpu.make_async_copy(source, target, load_sem.at[n])
        for n, (source, target) in enumerate(
            (
                (d_hbm, d_ref),
                (rows_hbm, rows_t_ref),
                (w_hbm, w_ref),
                (w2_hbm, w2_ref),
                (d2_hbm, d2_ref),
                (dmid_hbm, dmid_ref),
            )
        )
    ]
    for load in loads:
        load.start()
    near_id = part * 4 + place % 4
    near = [
        {"dp": flip(place, j % 4), "mp": part if j < 4 else 1 - part} for j in range(1, 8)
    ]
    ex.partners += [near[j - 1] for j in (3, 5, 6, 7)]
    ex.greet()

    lanes = d_ref.shape[2]
    split = mine_out_ref.shape[1] // lanes
    for r in range(split):
        cols = slice(r * lanes, (r + 1) * lanes)
        total = mine_out_ref[:, cols].astype(f32) + crossed_out_ref[:, cols].astype(f32)
        out_buf[r] = total.astype(bf16)
        ex.start_a(r, 0, out_buf)
    step = KEY_ROWS // 3

    def back_rows(n):
        rows = pl.ds(pl.multiple_of(n * step, EDGE), step)
        total = 0.0
        for grads, weights in ((d_ref, w_ref), (d2_ref, w2_ref)):
            for c in range(3):
                total = total + dot(grads[c, rows, :], weights[c], NT)
        rows_ref[rows, :] = total

    def grad_chunk(c):
        for r in range(split):
            rows = slice(r * ROW_TILE, (r + 1) * ROW_TILE)
            k = (c + 1) * split + r
            out_buf[k] = dot(rows_t_ref[rows, :], d_ref[c]).astype(bf16)
            ex.start_a(k, 0, out_buf)

    def stage_c(k):
        @pl.when(k >= split)
        def _():
            ex.stage_c(k, out_buf, lambda rows: crossed_ref[k - split, rows, :].astype(f32))

        @pl.when(k < split)
        def _():
            ex.stage_c(k, out_buf)

    def arrive(k):
        ex.stage_h(k, full_ref)

        @pl.when(k < split)
        def _():
            rows = pl.ds(pl.multiple_of(k * LANES, LANES), LANES)
            for b in range(2):
                piece = full_ref[k, b * LANES : (b + 1) * LANES, :]
                gout_ref[rows, b * lanes : (b + 1) * lanes] = piece

        @pl.when(k >= split)
        def _():
            n = k - split
            rows = pl.ds(pl.multiple_of(n % split * ROW_TILE, ROW_TILE), ROW_TILE)
            gqkv_ref[n // split, rows, :] = full_ref[k]

    def group(g, action):
        @pl.when(jnp.logical_and(g >= 0, g < count // split))
        def _():
            lax.fori_loop(g * split, (g + 1) * split, lambda k, _: (action(k), 0)[1], 0)

    def steps(i):
        group(i - 5, arrive)
        group(i - 4, lambda k: ex.stage_g(k, full_ref))
        group(i - 3, lambda k: ex.stage_f(k, full_ref))
        group(i - 2, lambda k: ex.stage_e(k, full_ref))
        group(i - 1, lambda k: ex.stage_d(k))
        group(i, stage_c)

    width = tokens_ref.shape[1]

    def swap(rows, lane):
        return pltpu.make_async_remote_copy(
            src_ref=give_ref.at[rows],
            dst_ref=take_ref.at[rows],
            send_sem=swap_sem.at[lane, 0],
            recv_sem=swap_sem.at[lane, 1],
            device_id=ex.across,
            device_id_type=MESH,
        )

    def sums_of(d_rows, units):
        add = lambda values: jnp.sum(values, axis=0, keepdims=True)
        norm_ref[0:1, :] += add(d_rows * units)
        norm_ref[1:2, :] += add(d_rows)

    main = slice(0, HALF)
    edges = slice(HALF, HALF + 2 * EDGE)
    parts = tokens_ref.shape[0] // TILE
    lead = small_ref.shape[0] - 2
    bias = lead - 3
    norm_ref[...] = jnp.zeros_like(norm_ref)
    for load in loads[:2]:
        load.wait()

    def own_at(b):
        start = jnp.where(b < TILES, NOISY_OWN + b * TILE, CLEAN_OWN + (b - TILES) * TILE)
        return pl.ds(pl.multiple_of(start, EDGE), TILE)

    def tokens_at(b):
        return pl.ds(pl.multiple_of(b * TILE, TILE), TILE)

    def ready():
        for load in loads[2:5]:
            load.wait()

    def give_main():
        give_ref[main, :] = rows_ref[main, :].astype(bf16)
        swap(main, 0).start()

    def give_edges():
        side = rows_ref[NOISY_BASE:NOISY_OWN, :] + rows_ref[NOISY_OWN + HALF :, :]
        after = rows_ref[2 * HALF : NOISY_BASE, :]
        give_ref[HALF : HALF + EDGE, :] = after.astype(bf16)
        give_ref[HALF + EDGE :, :] = side.astype(bf16)
        swap(edges, 1).start()
        sums_of(after, normal(context_ref[:EDGE, :].astype(f32))[0])
        sums_of(side, normal(context_ref[HALF:, :].astype(f32))[0])

    def tell_near():
        def context_sums(b, _):
            rows = tokens_at(b)
            sums_of(rows_ref[rows, :], normal(context_ref[rows, :].astype(f32))[0])
            return 0

        lax.fori_loop(0, HALF // TILE, context_sums, 0)

        def own_sums(b, _):
            sums_of(rows_ref[own_at(b), :], normal(tokens_ref[tokens_at(b), :].astype(f32))[0])
            return 0

        lax.fori_loop(0, parts, own_sums, 0)
        mine = near_ref.at[near_id]
        mine[:lead, :] = small_ref[:lead, :]
        mine[lead : lead + 2, :] = norm_ref[:2, :]
        mine[lead + 2 : lead + 2 + bias, :] = small2_ref[:bias, :]
        rest_rows = 16 - lead - 2 - bias
        mine[16 - rest_rows :, :] = jnp.zeros((rest_rows, width), f32)
        for j in range(1, 8):
            near_copy(j).start()

    def near_copy(j):
        return pltpu.make_async_remote_copy(
            src_ref=near_ref.at[near_id],
            dst_ref=near_ref.at[near_id],
            send_sem=near_sem.at[j, 0],
            recv_sem=near_sem.at[j, 1],
            device_id=near[j - 1],
            device_id_type=MESH,
        )

    def near_got(j):
        came = (part + j // 4) % 2 * 4 + flip(place % 4, j % 4)
        return pltpu.make_async_remote_copy(
            src_ref=near_ref.at[came],
            dst_ref=near_ref.at[came],
            send_sem=near_sem.at[j, 0],
            recv_sem=near_sem.at[j, 1],
            device_id=near[j - 1],
            device_id_type=MESH,
        )

    def far_copy(j, at):
        return pltpu.make_async_remote_copy(
            src_ref=far_ref.at[at],
            dst_ref=far_ref.at[at],
            send_sem=far_sem.at[j, 0],
            recv_sem=far_sem.at[j, 1],
            device_id=ex.peers[j - 1],
            device_id_type=MESH,
        )

    def tell_far():
        for j in range(1, 8):
            near_copy(j).wait_send()
            near_got(j).wait_recv()
        total = near_ref[0]
        for j in range(1, 8):
            total = total + near_ref[j]
        plane = near_ref[part * 4]
        other = near_ref[(1 - part) * 4]
        for j in range(1, 4):
            plane = plane + near_ref[part * 4 + j]
            other = other + near_ref[(1 - part) * 4 + j]
        spot = far_ref.at[ex.z]
        spot[...] = total
        spot[:bias, :] = plane[:bias] + other[lead + 2 : lead + 2 + bias]
        for j in range(1, 4):
            far_copy(j, ex.z).start()

    def take_back():
        loads[5].wait()
        swap(main, 0).wait()
        swap(edges, 1).wait()
        clean = slice(CLEAN_OWN, CLEAN_OWN + HALF)
        rows_ref[clean, :] += take_ref[main, :].astype(f32)
        begin = slice(CLEAN_OWN, CLEAN_OWN + EDGE)
        rows_ref[begin, :] += take_ref[HALF : HALF + EDGE, :].astype(f32)
        edge = pl.ds(pl.multiple_of(NOISY_OWN + (1 - part) * (HALF - EDGE), EDGE), EDGE)
        rows_ref[edge, :] += take_ref[HALF + EDGE :, :].astype(f32)

    def norm_back(b):
        rows = tokens_at(b)
        unit, scale = normal(tokens_ref[rows, :].astype(f32))
        lean = rows_ref[own_at(b), :] * vectors_ref[0:1, :]
        back_ref[rows, :] = dmid_ref[rows, :] + scale * (
            lean
            - jnp.mean(lean, axis=-1, keepdims=True)
            - unit * jnp.mean(lean * unit, axis=-1, keepdims=True)
        )

    def end_far():
        for j in range(1, 4):
            far_copy(j, ex.z).wait_send()
            far_copy(j, flip(ex.z, j)).wait_recv()
        total = far_ref[0]
        for j in range(1, 4):
            total = total + far_ref[j]
        for i, b in enumerate(ex.extra):
            far_ref[4 + 2 * i] = total
            trade = pltpu.make_async_remote_copy(
                src_ref=far_ref.at[4 + 2 * i],
                dst_ref=far_ref.at[5 + 2 * i],
                send_sem=far_sem.at[4 + i, 0],
                recv_sem=far_sem.at[4 + i, 1],
                device_id={"dp": flip(place, 1 << b)},
                device_id_type=MESH,
            )
            trade.start()
            trade.wait()
            total = total + far_ref[5 + 2 * i]
        sums_ref[...] = total

    groups = count // split - 1
    actions = {
        groups: give_main,
        groups + 2: give_edges,
        groups + 3: tell_near,
        groups + 4: tell_far,
        groups + 5: take_back,
    }
    begin_back = groups + 6

    def phase(p, _):
        @pl.when(p < groups)
        def _():
            grad_chunk(p)

        pl.when(p == groups)(ready)

        @pl.when(jnp.logical_and(p >= groups, p < groups + 3))
        def _():
            back_rows(p - groups)

        for n, action in actions.items():
            pl.when(p == n)(action)
        block = 2 * (p - begin_back)

        @pl.when(jnp.logical_and(block >= 0, block < parts))
        def _():
            lax.fori_loop(block, block + 2, lambda b, _: (norm_back(b), 0)[1], 0)

        pl.when(block == parts)(end_far)
        steps(p)
        return 0

    lax.fori_loop(0, begin_back + parts // 2 + 1, phase, 0)


def leave(bits, rows_t, mine, crossed, d_fields, weights, tokens, context, vectors, d_mid, small, small2):
    rows, cols = ROW_TILE, d_fields[0].shape[2]
    total = mine.shape[1] // cols + crossed[0].shape[0]
    exchange = Exchange(bits, total, rows, cols)
    count, width = tokens.shape
    vmem = pl.BlockSpec(memory_space=pltpu.VMEM)
    hbm = pl.BlockSpec(memory_space=pl.ANY)
    shape = jax.ShapeDtypeStruct
    return pl.pallas_call(
        functools.partial(leave_kernel, exchange),
        in_specs=[hbm] + [vmem] * 3 + [hbm] * 4 + [vmem] * 3 + [hbm] + [vmem] * 2,
        out_specs=[vmem] * 4,
        out_shape=[
            shape(weights[0].shape, bf16),
            shape((d_fields[0].shape[2], width), bf16),
            shape((count, width), f32),
            shape((16, width), f32),
        ],
        scratch_shapes=[
            pltpu.VMEM((total, rows, cols), bf16),
            pltpu.VMEM((total, rows, cols), bf16),
            pltpu.VMEM(rows_t.shape, bf16),
            pltpu.VMEM(d_fields[0].shape, bf16),
            pltpu.VMEM(d_fields[1].shape, bf16),
            pltpu.VMEM(weights[0].shape, bf16),
            pltpu.VMEM(weights[1].shape, bf16),
            pltpu.VMEM(d_mid.shape, f32),
            pltpu.SemaphoreType.DMA((6,)),
            pltpu.VMEM((KEY_ROWS, width), f32),
            pltpu.VMEM((HALF + 2 * EDGE, width), bf16),
            pltpu.VMEM((HALF + 2 * EDGE, width), bf16),
            pltpu.SemaphoreType.DMA((2, 2)),
            pltpu.VMEM((8, width), f32),
            pltpu.VMEM((8, 16, width), f32),
            pltpu.VMEM((4 + 2 * len(exchange.extra), 16, width), f32),
            pltpu.SemaphoreType.DMA((8, 2)),
            pltpu.SemaphoreType.DMA((4 + len(exchange.extra), 2)),
        ]
        + exchange.scratch(),
        compiler_params=pltpu.CompilerParams(
            collective_id=1, has_side_effects=True, vmem_limit_bytes=67043328
        ),
        name="leave",
        cost_estimate=pl.CostEstimate(
            flops=40 * 10**9, bytes_accessed=40 * 10**6, transcendentals=0
        ),
    )(
        rows_t, mine, *crossed, *d_fields, *weights, tokens, context, vectors, d_mid, small, small2
    )


def assemble_kernel(core_ref, down_mine, up_mine, down_got, up_got, down_ref, up_ref):
    core = core_ref[0]
    block = down_mine.shape[1]
    lanes = up_ref.shape[1]
    parts = down_mine.shape[2] // lanes
    deep = block * parts
    for side, down, up in ((core, down_mine, up_mine), (1 - core, down_got, up_got)):
        rows = pl.ds(pl.multiple_of(side * block, block), block)
        down_ref[rows, :] = down[0].astype(f32)
        for n in range(block // PIECES):
            for c in range(parts):
                at = side * deep + (n * parts + c) * PIECES
                rows = pl.ds(pl.multiple_of(at, PIECES), PIECES)
                piece = up[0, n * PIECES : (n + 1) * PIECES, c * lanes : (c + 1) * lanes]
                up_ref[rows, :] = piece.astype(f32)


def assemble(core, gathered, moved):
    tiles, half, width = gathered.shape
    count = tiles // 2
    down_spec = pl.BlockSpec((1, half, width), lambda k, c: (k, 0, 0))
    up_spec = pl.BlockSpec((1, half, width), lambda k, c: (count + k, 0, 0))
    hidden = count * 2 * half
    return pl.pallas_call(
        assemble_kernel,
        grid_spec=pltpu.PrefetchScalarGridSpec(
            num_scalar_prefetch=1,
            grid=(count,),
            in_specs=[down_spec, up_spec, down_spec, up_spec],
            out_specs=[
                pl.BlockSpec((2 * half, width), lambda k, c: (k, 0)),
                pl.BlockSpec((width, 2 * half), lambda k, c: (0, k)),
            ],
        ),
        out_shape=[
            jax.ShapeDtypeStruct((hidden, width), f32),
            jax.ShapeDtypeStruct((width, hidden), f32),
        ],
        name="assemble",
        cost_estimate=pl.CostEstimate(
            flops=10**6, bytes_accessed=14 * 10**6, transcendentals=0
        ),
    )(core, gathered, gathered, moved, moved)


def key_layout(seq_lengths, block_len, part):
    index = jnp.arange(KEY_ROWS, dtype=jnp.int32)
    own = part * HALF
    token = jnp.where(
        index < NOISY_BASE, index + (own - HALF), index - NOISY_BASE + (own - EDGE)
    )
    ends = jnp.cumsum(seq_lengths)
    passed = token[:, None] >= ends[None, :]
    starts = jnp.sum(jnp.where(passed, seq_lengths[None, :], 0), axis=1)
    lengths_here = jnp.where(passed, 0, ends[None, :])
    stops = jnp.min(jnp.where(passed, TOK_DEV, lengths_here), axis=1)
    positions = token - starts
    block_start = starts + positions // block_len * block_len
    block_stop = jnp.minimum(block_start + block_len, stops)
    mine = slice(CLEAN_OWN, CLEAN_OWN + HALF)
    low, start, stop = starts[mine], block_start[mine], block_stop[mine]
    to_clean = own - HALF
    tiles = lambda column: column.reshape(TILES, 1, TILE)
    clean_bounds = jnp.concatenate(
        [
            jnp.concatenate([tiles(low - to_clean), tiles(low - to_clean)], axis=2),
            jnp.concatenate([tiles(start - to_clean), tiles(stop - to_clean)], axis=2),
        ],
        axis=1,
    )
    to_window = own - EDGE + TILE * jnp.arange(TILES, dtype=jnp.int32)[:, None, None]
    noisy_bounds = jnp.concatenate(
        [tiles(start) - to_window, tiles(stop) - to_window], axis=1
    )
    first = jnp.min(clean_bounds[:, 0], axis=1) // EDGE * EDGE
    last = jnp.max(clean_bounds[:, 1], axis=1)
    trips = (last - first + KEY_TILE - 1) // KEY_TILE
    spans = jnp.stack([first, trips], axis=1)
    lane = jnp.arange(LANES, dtype=jnp.int32)
    frequency = jnp.exp(
        (lane % (HD // 2)).astype(f32) * (-math.log(10000.0) / (HD // 2))
    )
    angles = positions.astype(f32)[:, None] * frequency[None, :]
    sign = jnp.where(lane % HD < HD // 2, -1.0, 1.0)
    return spans, clean_bounds, noisy_bounds, jnp.cos(angles), jnp.sin(angles) * sign


def in_order(bit, mine, theirs, axis=0):
    order = bit == 0
    return jnp.concatenate(
        [jnp.where(order, mine, theirs), jnp.where(order, theirs, mine)], axis=axis
    )


def tie(first, second):
    return lax.optimization_barrier((first, second))


def local(
    dp_size,
    tokens,
    lengths,
    block_size,
    cotangent,
    ln1_gain,
    ln1_bias,
    w_qkv,
    w_out,
    ln2_gain,
    ln2_bias,
    w_up,
    b_up,
    w_down,
    b_down,
):
    width = tokens.shape[2]
    part = lax.axis_index("mp")
    place = lax.axis_index("dp")
    bits = dp_size.bit_length() - 1
    core = place & 1

    def across(array):
        return lax.ppermute(array, "mp", [(0, 1), (1, 0)])

    def sibling(array):
        return lax.ppermute(array, "dp", [(i, i ^ 1) for i in range(dp_size)])

    def beside(array):
        return lax.ppermute(array, "dp", [(i, i ^ 2) for i in range(dp_size)])

    edge = jnp.where(part == 0, tokens[0, HALF - EDGE :], tokens[0, :EDGE])
    context = across(jnp.concatenate([tokens[1], edge], axis=0))
    qkv_mine = w_qkv.transpose(1, 0, 2)
    side = (place >> 1) & 1

    def quarter_of(array, axis=0):
        size = array.shape[axis] // 4
        return lax.dynamic_slice_in_dim(array, (2 * core + side) * size, size, axis)

    def half_of(array):
        size = array.shape[0] // 2
        return lax.dynamic_slice_in_dim(array, core * size, size, 0)

    quarters = [quarter_of(qkv_mine, 1), quarter_of(w_up), half_of(w_down), half_of(w_out)]
    layout = key_layout(lengths[0], block_size[0], part)
    vectors = jnp.stack([ln1_gain, ln1_bias, ln2_gain, ln2_bias, b_down])
    context, (quarters, layout, vectors) = tie(context, (quarters, layout, vectors))
    qkv_here, up_here, down_here, out_here = [across(piece) for piece in quarters]

    spans, clean_bounds, noisy_bounds, cosine, sine = layout
    normed1, normed1_t, *fields = enter(tokens, context, vectors, qkv_mine, cosine, sine)
    qkv_here, fields = tie(qkv_here, fields)
    qkv_beside = beside(qkv_here)
    mine = [*fields, *attend_forward(spans, clean_bounds, noisy_bounds, *fields)]
    (qkv_here, qkv_beside, up_here), _ = tie((qkv_here, qkv_beside, up_here), mine[3])
    qkv_half = in_order(side, qkv_here, qkv_beside, axis=1)
    qkv_other = in_order(core, qkv_half, sibling(qkv_half), axis=1)
    up_beside = beside(up_here)
    fields = project(normed1, qkv_other, cosine, sine)
    other = [*fields, *attend_forward(spans, clean_bounds, noisy_bounds, *fields)]
    (out_here, up_here, up_beside, down_here), _ = tie(
        (out_here, up_here, up_beside, down_here), other[3]
    )
    out_other = in_order(core, out_here, sibling(out_here))
    bias_all = b_up.astype(f32).reshape(-1, 1, HIDDEN_TILE)

    x_rows = tokens.reshape(TOK_DEV, width)
    out, d_mid, d_att, d_att2, grad_out, grad_out2, grad_bias, norms, pieces = middle(
        bits,
        x_rows,
        mine[3],
        other[3],
        w_out,
        out_other,
        cotangent.reshape(TOK_DEV, width),
        vectors,
        bias_all,
        (w_up, up_here, up_beside),
        (w_down, down_here),
    )
    hidden = b_up.shape[0]

    crossed_out = across(grad_out2)
    spread = [(b, min(2, min(bits, 4) - b)) for b in range(2, min(bits, 4), 2)]
    gathered = pieces
    ((first_bit, n),) = spread
    moved = [
        lax.ppermute(gathered, "dp", [(i, i ^ (k << first_bit)) for i in range(dp_size)])
        for k in range(1, 1 << n)
    ]

    def backward(saved, d_attended, spans, *rows_t):
        query, keys, values, attended, lse = saved
        return attend_backward(
            spans,
            clean_bounds,
            noisy_bounds,
            query,
            keys,
            values,
            attended,
            d_attended,
            lse,
            cosine,
            sine,
            *rows_t,
        )

    d_fields2, grad2 = backward(other, d_att2, spans, normed1_t)
    grad2 = grad2.reshape(-1, ROW_TILE, grad2.shape[2])
    low_bit, high_bit = (place >> 2) & 1, (place >> 3) & 1
    moved, _ = tie(moved, grad2)
    gathered = in_order(
        high_bit,
        in_order(low_bit, gathered, moved[0], 1),
        in_order(low_bit, moved[1], moved[2], 1),
        1,
    )
    half = ROW_TILE // 2
    part_of = lambda array, which: lax.dynamic_slice_in_dim(array, which * half, half, 1)
    got = sibling(part_of(grad2, 1 - core))
    crossing = (part_of(grad2, core).astype(f32) + got.astype(f32)).astype(bf16)
    (crossing, gathered), spans = tie((crossing, gathered), spans)
    crossed = across(crossing)
    moved = beside(gathered)
    (d_fields1,) = backward(mine, d_att, spans)
    moved, d_fields1 = tie(moved, d_fields1)
    gathered = in_order(side, gathered, moved, 1)
    gathered, d_fields1 = tie(gathered, d_fields1)
    moved = sibling(gathered)
    lead = hidden // width
    bias2, bias1 = grad_bias.reshape(2, lead, width)
    shared = jnp.concatenate([norms[:3], jnp.zeros((2, width), f32)], axis=0)
    grad_qkv, grad_out, grad_tokens, sums = leave(
        bits,
        normed1_t,
        grad_out,
        (crossed, crossed_out),
        (d_fields1, d_fields2),
        (qkv_mine, qkv_other),
        x_rows,
        context,
        vectors,
        d_mid,
        jnp.concatenate([bias1, shared], axis=0),
        jnp.concatenate([bias2, shared], axis=0),
    )
    moved, _ = tie(moved, grad_qkv)
    grad_down, grad_up = assemble(core.reshape(1), gathered, moved)
    return (
        out.reshape(tokens.shape),
        grad_tokens.reshape(tokens.shape),
        sums[lead + 3],
        sums[lead + 4],
        grad_qkv.transpose(1, 0, 2).astype(f32),
        grad_out.astype(f32),
        sums[lead],
        sums[lead + 1],
        grad_up,
        sums[:lead].reshape(hidden),
        grad_down,
        sums[lead + 2],
    )


def solution(mesh):
    in_specs = (
        P(None, ("dp", "mp"), None),
        P("dp", None),
        P(),
        P(None, ("dp", "mp"), None),
        P(),
        P(),
        P(None, None, "mp"),
        P("mp", None),
        P(),
        P(),
        P(None, "mp"),
        P("mp"),
        P("mp", None),
        P(),
    )
    out_specs = (
        P(None, ("dp", "mp"), None),
        P(None, ("dp", "mp"), None),
        P(),
        P(),
        P(None, None, "mp"),
        P("mp", None),
        P(),
        P(),
        P(None, "mp"),
        P("mp"),
        P("mp", None),
        P(),
    )
    return jax.shard_map(
        functools.partial(local, mesh.shape["dp"]),
        mesh=mesh,
        in_specs=in_specs,
        out_specs=out_specs,
        check_vma=False,
    )
```

```python
import functools
import math

import jax
import jax.numpy as jnp
from jax import lax
from jax.experimental import pallas as pl
from jax.experimental.pallas import tpu as pltpu
from jax.sharding import PartitionSpec as P

HD = 64
TOK_DEV = 1024
HALF = TOK_DEV // 2
EDGE = 16
CLEAN_OWN = HALF
NOISY_BASE = 2 * HALF + EDGE
NOISY_OWN = NOISY_BASE + EDGE
KEY_ROWS = NOISY_OWN + HALF + EDGE
TILE = 128
TILES = HALF // TILE
WINDOW = TILE + 2 * EDGE
KEY_TILE = 192
LANES = 128
HIDDEN_TILE = 256
ROW_TILE = 256

epsilon = 1e-05
neg_large = -1e30
to_base2 = 0.125 * math.log2(math.e)
f32 = jnp.float32
bf16 = jnp.bfloat16

NN = (((1,), (0,)), ((), ()))
NT = (((1,), (1,)), ((), ()))


def dot(left, right, dims=NN):
    return lax.dot_general(left, right, dims, preferred_element_type=f32)


def low_lanes(shape):
    return lax.broadcasted_iota(jnp.int32, shape, 1) < HD


def turn(values, cosine, sine):
    lane = lax.broadcasted_iota(jnp.int32, values.shape, 1)
    first_half = (lane & (HD - 1)) < HD // 2
    swapped = jnp.where(
        first_half,
        pltpu.roll(values, LANES - HD // 2, 1),
        pltpu.roll(values, HD // 2, 1),
    )
    return values * cosine + swapped * sine


def project_rows(rows, w_ref, cosine, sine, q_ref, k_ref, v_ref, at):
    for part, out_ref in ((0, q_ref), (1, k_ref)):
        field = dot(rows, w_ref[part])
        for pair in range(field.shape[1] // LANES):
            cols = slice(pair * LANES, (pair + 1) * LANES)
            out_ref[at, cols] = turn(field[:, cols], cosine, sine).astype(bf16)
    v_ref[at, :] = dot(rows, w_ref[2]).astype(bf16)


def project_kernel(rows_ref, w_ref, cos_ref, sin_ref, q_ref, k_ref, v_ref):
    at = slice(0, rows_ref.shape[0])
    project_rows(rows_ref[...], w_ref, cos_ref[...], sin_ref[...], q_ref, k_ref, v_ref, at)


def project(rows, weights, cosine, sine):
    count, width = rows.shape
    cols = weights.shape[2]
    step = count // 3
    row_spec = pl.BlockSpec((step, width), lambda i: (i, 0))
    table_spec = pl.BlockSpec((step, LANES), lambda i: (i, 0))
    out_spec = pl.BlockSpec((step, cols), lambda i: (i, 0))
    shape = jax.ShapeDtypeStruct((count, cols), bf16)
    return pl.pallas_call(
        project_kernel,
        grid=(3,),
        in_specs=[
            row_spec,
            pl.BlockSpec(weights.shape, lambda i: (0, 0, 0)),
            table_spec,
            table_spec,
        ],
        out_specs=[out_spec] * 3,
        out_shape=[shape] * 3,
        name="project",
        cost_estimate=pl.CostEstimate(
            flops=2 * count * width * 3 * cols,
            bytes_accessed=2 * (count * (width + 3 * cols) + 3 * width * cols),
            transcendentals=0,
        ),
    )(rows, weights, cosine, sine)


def normal(values):
    average = jnp.mean(values, axis=-1, keepdims=True)
    centred = values - average
    variance = jnp.mean(centred * centred, axis=-1, keepdims=True)
    scale = lax.rsqrt(variance + epsilon)
    return centred * scale, scale


def enter_kernel(
    tokens_ref,
    context_ref,
    vectors_ref,
    w_ref,
    cos_ref,
    sin_ref,
    rows_ref,
    rows_t_ref,
    q_ref,
    k_ref,
    v_ref,
):
    def norm(values):
        unit = normal(values.astype(f32))[0]
        return (unit * vectors_ref[0:1, :] + vectors_ref[1:2, :]).astype(bf16)

    def blocks(i, _):
        source = pl.ds(pl.multiple_of(i * TILE, TILE), TILE)
        rows_ref[source, :] = norm(context_ref[source, :])
        at = pl.ds(pl.multiple_of(CLEAN_OWN + i * TILE, TILE), TILE)
        rows_ref[at, :] = norm(tokens_ref[1, source, :])
        at = pl.ds(pl.multiple_of(NOISY_OWN + i * TILE, EDGE), TILE)
        rows_ref[at, :] = norm(tokens_ref[0, source, :])
        return 0

    lax.fori_loop(0, TILES, blocks, 0)
    rows_ref[2 * HALF : NOISY_BASE, :] = rows_ref[:EDGE, :]
    edge = norm(context_ref[HALF:, :])
    rows_ref[NOISY_BASE:NOISY_OWN, :] = edge
    rows_ref[NOISY_OWN + HALF :, :] = edge
    step = KEY_ROWS // 3

    def fields(i, _):
        at = pl.ds(pl.multiple_of(i * step, EDGE), step)
        project_rows(
            rows_ref[at, :], w_ref, cos_ref[at, :], sin_ref[at, :], q_ref, k_ref, v_ref, at
        )
        return 0

    lax.fori_loop(0, 3, fields, 0)
    for c in range(rows_t_ref.shape[0] // LANES):
        cols = slice(c * LANES, (c + 1) * LANES)
        rows_t_ref[cols, :] = rows_ref[:, cols].T


def enter(tokens, context, vectors, weights, cosine, sine):
    width, cols = weights.shape[1:]
    vmem = pl.BlockSpec(memory_space=pltpu.VMEM)
    shape = jax.ShapeDtypeStruct
    field = shape((KEY_ROWS, cols), bf16)
    return pl.pallas_call(
        enter_kernel,
        in_specs=[vmem] * 6,
        out_specs=[vmem] * 5,
        out_shape=[shape((KEY_ROWS, width), bf16), shape((width, KEY_ROWS), bf16)] + [field] * 3,
        name="enter",
        cost_estimate=pl.CostEstimate(
            flops=10**10, bytes_accessed=16 * 10**6, transcendentals=0
        ),
    )(tokens, context, vectors, weights, cosine, sine)


def split_heads(rows):
    low = low_lanes(rows.shape)
    zero = jnp.zeros_like(rows)
    return jnp.where(low, rows, zero), jnp.where(low, zero, rows)


def between(shape, offset, low, high):
    index = lax.broadcasted_iota(jnp.int32, shape, 0) + offset
    return jnp.logical_and(index >= low, index < high)


def fold(values, combine):
    rows, cols = values.shape
    groups = values.reshape(rows // 8, 8, cols)
    return combine(groups, axis=0)


def forward_kernel(
    span_ref, clean_ref, noisy_ref, q_ref, k_ref, v_ref, out_ref, lse_ref, bias_ref, window_ref
):
    pairs = q_ref.shape[1] // LANES
    lanes = [slice(p * LANES, (p + 1) * LANES) for p in range(pairs)]

    def one_tile(t, _):
        clean_at = pl.multiple_of(CLEAN_OWN + t * TILE, TILE)
        noisy_at = pl.multiple_of(NOISY_OWN + t * TILE, EDGE)
        window_at = pl.multiple_of(NOISY_BASE + t * TILE, EDGE)
        key_low, key_high = clean_ref[t, 0:1, :], clean_ref[t, 1:2, :]
        own_low, own_high = noisy_ref[t, 0:1, :], noisy_ref[t, 1:2, :]
        allowed = between((WINDOW, TILE), 0, own_low, own_high)
        window_ref[...] = jnp.where(allowed, 0.0, neg_large)
        first_key, trips = span_ref[t, 0], span_ref[t, 1]
        queries, tops = [], []
        for cols in lanes:
            query = jnp.concatenate(
                [q_ref[pl.ds(noisy_at, TILE), cols], q_ref[pl.ds(clean_at, TILE), cols]], axis=0
            )
            heads = split_heads(query)
            queries += heads
            keys = k_ref[pl.ds(window_at, WINDOW), cols]
            for head in range(2):
                scores = dot(keys, heads[head][:TILE], NT) + window_ref[...]
                top = fold(scores, jnp.max)
                tops.append(
                    jnp.concatenate([top, jnp.full((8, TILE), neg_large, f32)], axis=1)
                )

        def first_pass(j, tops):
            at = pl.multiple_of(first_key + j * KEY_TILE, EDGE)
            allowed = between((KEY_TILE, 2 * TILE), at, key_low, key_high)
            bias_ref[j] = jnp.where(allowed, 0.0, neg_large)
            after = []
            for p, cols in enumerate(lanes):
                keys = k_ref[pl.ds(at, KEY_TILE), cols]
                for head in range(2):
                    scores = dot(keys, queries[2 * p + head], NT) + bias_ref[j]
                    after.append(jnp.maximum(tops[2 * p + head], fold(scores, jnp.max)))
            return tuple(after)

        tops = lax.fori_loop(0, trips, first_pass, tuple(tops))
        tops = [jnp.max(top, axis=0, keepdims=True) * to_base2 for top in tops]
        state = []
        keys = [k_ref[pl.ds(window_at, WINDOW), cols] for cols in lanes]
        values_t = [v_ref[pl.ds(window_at, WINDOW), cols].T for cols in lanes]
        scores = dot(keys[0], queries[0][:TILE], NT)
        late = None
        for h in range(2 * pairs):
            if h + 1 < 2 * pairs:
                ahead = dot(keys[(h + 1) // 2], queries[h + 1][:TILE], NT)
            expo = jnp.exp2(scores * to_base2 - tops[h][:, :TILE] + window_ref[...])
            if late is not None:
                state.append(jnp.concatenate([late, jnp.zeros((HD, TILE), f32)], axis=1))
            total = fold(expo, jnp.sum)
            state.append(jnp.concatenate([total, jnp.zeros((8, TILE), f32)], axis=1))
            side = slice(h % 2 * HD, (h % 2 + 1) * HD)
            late = dot(values_t[h // 2][side], expo.astype(bf16))
            scores = ahead
        state.append(jnp.concatenate([late, jnp.zeros((HD, TILE), f32)], axis=1))

        def second_pass(j, state):
            at = pl.multiple_of(first_key + j * KEY_TILE, EDGE)
            keys = [k_ref[pl.ds(at, KEY_TILE), cols] for cols in lanes]
            values_t = [v_ref[pl.ds(at, KEY_TILE), cols].T for cols in lanes]
            after = list(state)
            scores = dot(keys[0], queries[0], NT)
            late = None
            for h in range(2 * pairs):
                ahead = dot(keys[(h + 1) // 2], queries[h + 1], NT) if h + 1 < 2 * pairs else None
                expo = jnp.exp2(scores * to_base2 - tops[h] + bias_ref[j])
                after[2 * h] = state[2 * h] + fold(expo, jnp.sum)
                if late is not None:
                    after[2 * h - 1] = state[2 * h - 1] + late
                side = slice(h % 2 * HD, (h % 2 + 1) * HD)
                late = dot(values_t[h // 2][side], expo.astype(bf16))
                scores = ahead
            after[-1] = state[-1] + late
            return tuple(after)

        state = lax.fori_loop(0, trips, second_pass, tuple(state))
        low_at = pl.ds(pl.multiple_of(t * TILE, TILE), TILE)
        high_at = pl.ds(pl.multiple_of(HALF + t * TILE, TILE), TILE)
        for p, cols in enumerate(lanes):
            halves = []
            for head in range(2):
                h = 2 * p + head
                total = jnp.sum(state[2 * h], axis=0, keepdims=True)
                halves.append(state[2 * h + 1] / total)
                lse_ref[p, t, head : head + 1, :] = tops[h] + jnp.log2(total)
            pair = jnp.concatenate(halves, axis=0).T.astype(bf16)
            out_ref[low_at, cols] = pair[:TILE]
            out_ref[high_at, cols] = pair[TILE:]
        return 0

    lax.fori_loop(0, TILES, one_tile, 0)


def attend_forward(spans, clean_bounds, noisy_bounds, query, keys, values):
    count, cols = query.shape
    pairs = cols // LANES
    vmem = pl.BlockSpec(memory_space=pltpu.VMEM)
    work = pairs * 2 * 2 * HALF * TOK_DEV
    return pl.pallas_call(
        forward_kernel,
        in_specs=[pl.BlockSpec(memory_space=pltpu.SMEM)] + [vmem] * 5,
        out_specs=[vmem] * 2,
        out_shape=[
            jax.ShapeDtypeStruct((TOK_DEV, cols), bf16),
            jax.ShapeDtypeStruct((pairs, TILES, 2, 2 * TILE), f32),
        ],
        scratch_shapes=[
            pltpu.VMEM((NOISY_BASE // KEY_TILE + 1, KEY_TILE, 2 * TILE), f32),
            pltpu.VMEM((WINDOW, TILE), f32),
        ],
        name="attend_forward",
        cost_estimate=pl.CostEstimate(
            flops=4 * work * HD, bytes_accessed=8 * count * cols, transcendentals=work
        ),
    )(spans, clean_bounds, noisy_bounds, query, keys, values)


def backward_kernel(
    giving,
    span_ref,
    clean_ref,
    noisy_ref,
    q_ref,
    k_ref,
    v_ref,
    o_ref,
    d_ref,
    lse_ref,
    cos_ref,
    sin_ref,
    *refs,
):
    if giving:
        d2_hbm, w_hbm, w2_hbm, out_ref, give_ref, *refs = refs
        dk_ref, dv_ref, bias_ref, d2_ref, w_ref, w2_ref, load_sem = refs
        loads = [(w_hbm, w_ref), (w2_hbm, w2_ref)]
        loads += [(d2_hbm.at[c, :HALF], d2_ref.at[c]) for c in range(3)]
        loads = [
            pltpu.make_async_copy(source, target, load_sem.at[n])
            for n, (source, target) in enumerate(loads)
        ]
        for load in loads:
            load.start()
    else:
        rows_ref, out_ref, grad_ref, dk_ref, dv_ref, bias_ref = refs
    pairs = q_ref.shape[1] // LANES
    lanes = [slice(p * LANES, (p + 1) * LANES) for p in range(pairs)]
    dk_ref[...] = jnp.zeros_like(dk_ref)
    dv_ref[...] = jnp.zeros_like(dv_ref)
    out_ref[0] = jnp.zeros_like(out_ref[0])

    def one_tile(t, _):
        clean_at = pl.multiple_of(CLEAN_OWN + t * TILE, TILE)
        noisy_at = pl.multiple_of(NOISY_OWN + t * TILE, EDGE)
        window_at = pl.multiple_of(NOISY_BASE + t * TILE, EDGE)
        low_at = pl.multiple_of(t * TILE, TILE)
        high_at = pl.multiple_of(HALF + t * TILE, TILE)
        key_low, key_high = clean_ref[t, 0:1, :], clean_ref[t, 1:2, :]
        own_low, own_high = noisy_ref[t, 0:1, :], noisy_ref[t, 1:2, :]
        queries, d_outs, inners, lses = [], [], [], []
        for p, cols in enumerate(lanes):

            def both(ref, low, high):
                return jnp.concatenate(
                    [ref[pl.ds(low, TILE), cols], ref[pl.ds(high, TILE), cols]], axis=0
                )

            queries.append(split_heads(both(q_ref, noisy_at, clean_at)))
            d_rows = both(d_ref, low_at, high_at)
            o_rows = both(o_ref, low_at, high_at)
            product = (d_rows.astype(f32) * o_rows.astype(f32)).T
            d_outs.append(split_heads(d_rows))
            inners.append(
                [
                    jnp.sum(product[head * HD : (head + 1) * HD], axis=0, keepdims=True) * 0.125
                    for head in range(2)
                ]
            )
            lses.append([lse_ref[p, t, head : head + 1, :] for head in range(2)])

        def accumulate(at, rows, cols, allowed, d_query):
            bias_ref[:rows, :cols] = jnp.where(allowed, 0.0, neg_large)
            after = list(d_query)
            keys = [k_ref[pl.ds(at, rows), span] for span in lanes]
            eighth = [v_ref[pl.ds(at, rows), span] * jnp.asarray(0.125, bf16) for span in lanes]
            keys_t = [part.T for part in keys]
            stack = lambda parts: jnp.concatenate([part[:cols] for part in parts], axis=0)

            def begin(h):
                p, head = h // 2, h % 2
                return (
                    dot(keys[p], queries[p][head][:cols], NT),
                    dot(eighth[p], d_outs[p][head][:cols], NT),
                )

            def finish_pair(p, weights, d_scores):
                span = lanes[p]
                for head in range(2):
                    side = slice(head * HD, (head + 1) * HD)
                    h = 2 * p + head
                    after[h] = d_query[h] + dot(keys_t[p][side], d_scores[head])
                dv_ref[pl.ds(at, rows), span] += dot(
                    jnp.concatenate(weights, axis=1), stack(d_outs[p])
                )
                dk_ref[pl.ds(at, rows), span] += dot(
                    jnp.concatenate(d_scores, axis=1), stack(queries[p])
                )

            ready = begin(0)
            held = None
            weights, d_scores = [], []
            for h in range(2 * pairs):
                ahead = begin(h + 1) if h + 1 < 2 * pairs else None
                p, head = h // 2, h % 2
                scores = ready[0] * to_base2 - lses[p][head][:, :cols] + bias_ref[:rows, :cols]
                probs = jnp.exp2(scores)
                d_score = (probs * (ready[1] - inners[p][head][:, :cols])).astype(bf16)
                weights.append(probs.astype(bf16))
                d_scores.append(d_score)
                if held is not None:
                    finish_pair(*held)
                    held = None
                if head == 1:
                    held = (p, weights, d_scores)
                    weights, d_scores = [], []
                ready = ahead
            finish_pair(*held)
            return tuple(after)

        allowed = between((WINDOW, TILE), 0, own_low, own_high)
        zero = jnp.zeros((HD, TILE), f32)
        start = accumulate(window_at, WINDOW, TILE, allowed, (zero,) * (2 * pairs))
        start = tuple(jnp.concatenate([part, zero], axis=1) for part in start)
        first_key, trips = span_ref[t, 0], span_ref[t, 1]

        def one_step(j, d_query):
            at = pl.multiple_of(first_key + j * KEY_TILE, EDGE)
            allowed = between((KEY_TILE, 2 * TILE), at, key_low, key_high)
            return accumulate(at, KEY_TILE, 2 * TILE, allowed, d_query)

        d_query = lax.fori_loop(0, trips, one_step, start)
        for p, span in enumerate(lanes):
            pair = jnp.concatenate(d_query[2 * p : 2 * p + 2], axis=0).T
            for at, part in ((noisy_at, pair[:TILE]), (clean_at, pair[TILE:])):
                turned = turn(part, cos_ref[pl.ds(at, TILE), :], -sin_ref[pl.ds(at, TILE), :])
                out_ref[0, pl.ds(at, TILE), span] = turned.astype(bf16)
        return 0

    lax.fori_loop(0, TILES, one_tile, 0)
    step = KEY_ROWS // 9

    def finish(i, _):
        rows = pl.ds(pl.multiple_of(i * step, EDGE), step)
        for span in lanes:
            out_ref[1, rows, span] = turn(
                dk_ref[rows, span], cos_ref[rows, :], -sin_ref[rows, :]
            ).astype(bf16)
        out_ref[2, rows, :] = dv_ref[rows, :].astype(bf16)
        return 0

    lax.fori_loop(0, 9, finish, 0)

    def weight_rows(i, _):
        rows = pl.ds(pl.multiple_of(i * ROW_TILE, LANES), ROW_TILE)
        for c in range(3):
            grad_ref[c, rows, :] = dot(rows_ref[rows, :], out_ref[c]).astype(bf16)
        return 0

    if giving:
        for load in loads:
            load.wait()
        total = 0.0
        for c in range(3):
            total = total + dot(out_ref[c, :HALF, :], w_ref[c], NT) + dot(d2_ref[c], w2_ref[c], NT)
        give_ref[...] = total
    else:
        lax.fori_loop(0, rows_ref.shape[0] // ROW_TILE, weight_rows, 0)


def attend_backward(
    spans,
    clean_bounds,
    noisy_bounds,
    query,
    keys,
    values,
    attended,
    d_attended,
    lse,
    cosine,
    sine,
    rest,
):
    count, cols = query.shape
    vmem = pl.BlockSpec(memory_space=pltpu.VMEM)
    hbm = pl.BlockSpec(memory_space=pl.ANY)
    shape = jax.ShapeDtypeStruct
    giving = len(rest) > 1
    if giving:
        width = rest[1].shape[1]
        second = shape((HALF, width), f32)
        scratch = [
            pltpu.VMEM((3, HALF, cols), bf16),
            pltpu.VMEM(rest[1].shape, bf16),
            pltpu.VMEM(rest[2].shape, bf16),
            pltpu.SemaphoreType.DMA((5,)),
        ]
    else:
        second = shape((3, rest[0].shape[0], cols), bf16)
        scratch = []
    return pl.pallas_call(
        functools.partial(backward_kernel, giving),
        in_specs=[pl.BlockSpec(memory_space=pltpu.SMEM)]
        + [vmem] * 10
        + [hbm if giving else vmem] * len(rest),
        out_specs=[vmem] * 2,
        scratch_shapes=[
            pltpu.VMEM((count, cols), f32),
            pltpu.VMEM((count, cols), f32),
            pltpu.VMEM((max(KEY_TILE, WINDOW), 2 * TILE), f32),
        ]
        + scratch,
        out_shape=[shape((3, count, cols), bf16), second],
        name="attend_backward",
        cost_estimate=pl.CostEstimate(
            flops=36 * 10**9, bytes_accessed=36 * 10**6, transcendentals=6 * 10**6
        ),
    )(
        spans,
        clean_bounds,
        noisy_bounds,
        query,
        keys,
        values,
        attended,
        d_attended,
        lse,
        cosine,
        sine,
        *rest,
    )


PIECES = 16
MESH = pl.DeviceIdType.MESH


def flip(value, mask):
    result = value
    for b in range(mask.bit_length()):
        if mask >> b & 1:
            result = result + (1 << b) * (1 - 2 * ((value // (1 << b)) % 2))
    return result


class Exchange:
    def __init__(self, bits, count, rows, width, back=True):
        self.bits, self.count, self.rows, self.width = bits, count, rows, width
        self.back = back
        self.half, self.quarter, self.piece = rows // 2, rows // 4, rows // PIECES
        self.extra = list(range(4, bits))

    def slots(self):
        return 8 + 2 * (6 if self.back else 4) + (3 if self.extra else 0)

    def scratch(self):
        k, w = self.count, self.width
        cross = k if not self.back else 1
        shapes = [
            pltpu.VMEM((k, 2 - self.back, self.half, w), bf16),
            pltpu.VMEM((cross, self.half, w), bf16),
            pltpu.VMEM((cross, self.half, w), bf16),
            pltpu.VMEM((k, self.quarter, w), bf16),
            pltpu.VMEM((k, self.quarter, w), bf16),
            pltpu.VMEM((k, self.quarter, w), f32),
            pltpu.VMEM((k, 3, self.piece, w), bf16),
            pltpu.VMEM((k, 3, self.piece, w), bf16),
        ]
        lanes_of = (1, 0, 1, 3, 3, 1, 1) if self.back else (2, 1, 1, 3, 0, 0, 0)
        for lanes in [lanes for lanes in lanes_of if lanes]:
            shapes += [pltpu.SemaphoreType.DMA((k, lanes))] * 2
        if self.extra:
            n = len(self.extra)
            shapes += [pltpu.VMEM((k, 2 * n, self.piece, w), bf16)]
            shapes += [pltpu.SemaphoreType.DMA((k, n))] * 2
        return shapes

    def bind(self, place, part, refs):
        (self.a_in, self.b_out, self.b_in, self.c_out, self.c_in, self.keep) = refs[:6]
        self.d_out, self.d_in = refs[6:8]
        names = "acdefg" if self.back else "abcd"
        self.sems = {name: (refs[8 + 2 * i], refs[9 + 2 * i]) for i, name in enumerate(names)}
        if self.extra:
            at = 8 + 2 * len(names)
            self.x_buf, self.x_send, self.x_recv = refs[at : at + 3]
        self.place, self.part = place, part
        self.core, self.x, self.z = place % 2, (place // 2) % 2, (place // 4) % 4
        self.sibling = {"dp": flip(place, 1)}
        self.beside = {"dp": flip(place, 2)}
        self.across = {"mp": 1 - part}
        self.peers = [{"dp": flip(place, j << 2)} for j in range(1, 4)]
        self.partners = [self.sibling, self.beside, self.across] + self.peers
        self.partners += [{"dp": flip(place, 1 << b)} for b in self.extra]
        return self

    def greet(self):
        barrier = pltpu.get_barrier_semaphore()
        for partner in self.partners:
            pl.semaphore_signal(barrier, inc=1, device_id=partner, device_id_type=MESH)
        pl.semaphore_wait(barrier, len(self.partners))

    def copy(self, name, k, lane, source, target, device):
        out, into = self.sems[name]
        return pltpu.make_async_remote_copy(
            src_ref=source,
            dst_ref=target,
            send_sem=out.at[k, lane],
            recv_sem=into.at[k, lane],
            device_id=device,
            device_id_type=MESH,
        )

    def rows_at(self, start, size):
        return pl.ds(pl.multiple_of(start, PIECES), size)

    def copy_a(self, k, lane, grads):
        source = grads.at[k, self.rows_at((1 - self.core) * self.half, self.half)]
        return self.copy("a", k, lane, source, self.a_in.at[k, lane], self.sibling)

    def copy_b(self, k):
        return self.copy("b", k, 0, self.b_out.at[k], self.b_in.at[k], self.across)

    def copy_c(self, k):
        return self.copy("c", k, 0, self.c_out.at[k], self.c_in.at[k], self.beside)

    def copy_d(self, k, j):
        return self.copy("d", k, j, self.d_out.at[k, j], self.d_in.at[k, j], self.peers[j])

    def spot(self, change=0):
        start = self.core * self.half + self.x * self.quarter
        return self.rows_at(start + flip(self.z, change) * self.piece, self.piece)

    def copy_e(self, k, j, full):
        rows = full.at[k, self.spot()]
        return self.copy("e", k, j, rows, rows, self.peers[j])

    def copy_f(self, k, full):
        start = self.core * self.half + self.x * self.quarter
        rows = full.at[k, self.rows_at(start, self.quarter)]
        return self.copy("f", k, 0, rows, rows, self.beside)

    def copy_g(self, k, full):
        rows = full.at[k, self.rows_at(self.core * self.half, self.half)]
        return self.copy("g", k, 0, rows, rows, self.sibling)

    def start_a(self, k, lane, grads):
        self.copy_a(k, lane, grads).start()

    def stage_b(self, k, others):
        self.copy_a(k, 0, others).wait()
        mine = others[k, self.rows_at(self.core * self.half, self.half), :].astype(f32)
        self.b_out[k] = (mine + self.a_in[k, 0].astype(f32)).astype(bf16)
        self.copy_b(k).start()

    def stage_c(self, k, grads, crossed=None):
        lane = 0 if self.back else 1
        self.copy_a(k, lane, grads).wait()
        if not self.back:
            self.copy_b(k).wait()

        def total(which):
            inner = which * self.quarter
            rows = self.rows_at(inner, self.quarter)
            mine = grads[k, self.rows_at(self.core * self.half + inner, self.quarter), :]
            got = self.a_in[k, lane, rows, :].astype(f32)
            if not self.back:
                got = got + self.b_in[k, rows, :].astype(f32)
            elif crossed is not None:
                got = got + crossed(rows)
            return mine.astype(f32) + got

        self.c_out[k] = total(1 - self.x).astype(bf16)
        self.copy_c(k).start()
        self.keep[k] = total(self.x)

    def stage_d(self, k):
        self.copy_c(k).wait()
        for j in range(4):
            rows = self.rows_at(flip(self.z, j) * self.piece, self.piece)
            total = self.keep[k, rows, :] + self.c_in[k, rows, :].astype(f32)
            if j:
                self.d_out[k, j - 1] = total.astype(bf16)
                self.copy_d(k, j - 1).start()
            else:
                self.keep[k, rows, :] = total

    def gather_d(self, k):
        rows = self.rows_at(self.z * self.piece, self.piece)
        total = self.keep[k, rows, :]
        for j in range(3):
            self.copy_d(k, j).wait()
            total = total + self.d_in[k, j].astype(f32)
        for i, b in enumerate(self.extra):
            mine = self.x_buf.at[k, 2 * i]
            mine[...] = total.astype(bf16)
            swap = pltpu.make_async_remote_copy(
                src_ref=mine,
                dst_ref=self.x_buf.at[k, 2 * i + 1],
                send_sem=self.x_send.at[k, i],
                recv_sem=self.x_recv.at[k, i],
                device_id={"dp": flip(self.place, 1 << b)},
                device_id_type=MESH,
            )
            swap.start()
            swap.wait()
            total = total.astype(bf16).astype(f32) + self.x_buf[k, 2 * i + 1].astype(f32)
        return total.astype(bf16)

    def stage_e(self, k, full):
        full[k, self.spot(), :] = self.gather_d(k)
        for j in range(3):
            self.copy_e(k, j, full).start()

    def stage_f(self, k, full):
        for j in range(3):
            self.copy_e(k, j, full).wait()
        self.copy_f(k, full).start()

    def stage_g(self, k, full):
        self.copy_f(k, full).wait()
        self.copy_g(k, full).start()

    def stage_h(self, k, full):
        self.copy_g(k, full).wait()


def at_step(step, count, action):
    @pl.when(jnp.logical_and(step >= 0, step < count))
    def _():
        action(step)


def middle_kernel(exchanges, tiles, *refs):
    (
        x_ref,
        att_ref,
        att2_ref,
        wout_ref,
        wout2_ref,
        dy_ref,
        vectors_ref,
        bup_ref,
        up_mine,
        up_here,
        up_beside,
        down_mine,
        down_here,
        out_hbm,
        mid_hbm,
        datt_hbm,
        datt2_hbm,
        gout_ref,
        gout2_ref,
        gbup_ref,
        small_ref,
        pieces_ref,
        up_there,
        down_there,
        pass_up,
        pass_down,
        up_buf,
        down_buf,
        load_sem,
        n2_ref,
        total_ref,
        dn2_ref,
        act_ref,
        dpre_ref,
        n2_t,
        bup_other,
        bias_sem,
        out_ref,
        mid_ref,
        datt_ref,
        datt2_ref,
        store_sem,
        down_grad,
        up_grad,
        *rest,
    ) = refs
    place, part = lax.axis_index("dp"), lax.axis_index("mp")
    ex = exchanges[0].bind(place, part, rest)
    ex_up = exchanges[1].bind(place, part, rest[exchanges[0].slots() :])
    sides = ((ex, down_grad), (ex_up, up_grad))
    core = ex.core
    count = tiles // 2
    rows_all = x_ref.shape[0]
    blocks = rows_all // ROW_TILE
    width = x_ref.shape[1]
    lanes = width // 2

    def which(i):
        other = jnp.logical_or(i == 0, jnp.logical_and(i % 2 == 1, i < tiles - 1))
        mine = jnp.where(i == tiles - 1, count - 1, i // 2 - 1)
        return other, jnp.where(other, (i + 1) // 2, mine)

    quarter = width // 4
    strip = HIDDEN_TILE // 2
    held = 2 * core + ex.x
    kept = 2 * core + 1 - ex.x

    def load_up(i, source, h):
        target = up_buf.at[i % 2, h * quarter : (h + 1) * quarter]
        return pltpu.make_async_copy(source, target, load_sem.at[i % 2, h])

    def load_down(i, source, h):
        target = down_buf.at[i % 2, h * strip : (h + 1) * strip]
        return pltpu.make_async_copy(source, target, load_sem.at[i % 2, 4 + h])

    def hand_up(k, part_of):
        cols = pl.ds(pl.multiple_of(k * HIDDEN_TILE, HIDDEN_TILE), HIDDEN_TILE)
        side = ex.x if part_of == 0 else 1 - ex.x
        rows = pl.ds(pl.multiple_of(side * quarter, EDGE), quarter)
        return pltpu.make_async_remote_copy(
            src_ref=(up_here, up_beside)[part_of].at[:, cols],
            dst_ref=up_there.at[k, rows],
            send_sem=pass_up.at[k, 2 * part_of],
            recv_sem=pass_up.at[k, 2 * part_of + 1],
            device_id=ex.sibling,
            device_id_type=MESH,
        )

    def hand_down(b):
        return pltpu.make_async_remote_copy(
            src_ref=down_here.at[strip_rows(b)],
            dst_ref=down_there.at[b],
            send_sem=pass_down.at[b, 0],
            recv_sem=pass_down.at[b, 1],
            device_id=ex.sibling,
            device_id_type=MESH,
        )

    def strip_rows(b):
        return pl.ds(pl.multiple_of(b * strip, strip), strip)

    def start_loads(i):
        other, k = which(i)
        mine = jnp.logical_not(other)
        cols = pl.ds(pl.multiple_of(k * HIDDEN_TILE, HIDDEN_TILE), HIDDEN_TILE)

        @pl.when(other)
        def _():
            hand_up(k, 0).wait()
            hand_up(k, 1).wait()

        for h in range(4):

            @pl.when(mine)
            def _():
                load_up(i, up_mine.at[h * quarter : (h + 1) * quarter, cols], h).start()

            @pl.when(jnp.logical_and(other, held == h))
            def _():
                load_up(i, up_here.at[:, cols], h).start()

            @pl.when(jnp.logical_and(other, kept == h))
            def _():
                load_up(i, up_beside.at[:, cols], h).start()

            @pl.when(jnp.logical_and(other, core != h // 2))
            def _():
                rows = slice(h % 2 * quarter, (h % 2 + 1) * quarter)
                load_up(i, up_there.at[k, rows], h).start()

        for h in range(2):
            b = 2 * k + h
            inner = b % count

            @pl.when(mine)
            def _():
                load_down(i, down_mine.at[strip_rows(b), :], h).start()

            @pl.when(jnp.logical_and(other, core == b // count))
            def _():
                load_down(i, down_here.at[strip_rows(inner), :], h).start()

            @pl.when(jnp.logical_and(other, core != b // count))
            def _():
                hand_down(inner).wait_recv()
                load_down(i, down_there.at[inner], h).start()

    def wait_loads(i):
        for h in range(4):
            load_up(i, up_mine.at[:quarter, :HIDDEN_TILE], h).wait()
        for h in range(2):
            load_down(i, down_mine.at[:strip, :], h).wait()

    ex.greet()
    bias_swap = pltpu.make_async_remote_copy(
        src_ref=bup_ref,
        dst_ref=bup_other,
        send_sem=bias_sem.at[0],
        recv_sem=bias_sem.at[1],
        device_id=ex.across,
        device_id_type=MESH,
    )
    bias_swap.start()

    def hand(k, _):
        hand_up(k, 0).start()
        hand_up(k, 1).start()
        hand_down(k).start()
        return 0

    lax.fori_loop(0, count, hand, 0)

    def prologue(n, _):
        prologue_block(2 * n)
        prologue_block(2 * n + 1)
        return 0

    def prologue_block(r):
        rows = pl.ds(pl.multiple_of(r * ROW_TILE, ROW_TILE), ROW_TILE)
        branch = dot(att_ref[rows, :], wout_ref[...]) + dot(att2_ref[rows, :], wout2_ref[...])
        mid = x_ref[rows, :].astype(f32) + branch
        mid_ref[rows, :] = mid
        unit = normal(mid)[0]
        n2_ref[rows, :] = (unit * vectors_ref[2:3, :] + vectors_ref[3:4, :]).astype(bf16)
        total_ref[rows, :] = mid + vectors_ref[4:5, :]
        dn2_ref[rows, :] = jnp.zeros((ROW_TILE, width), f32)

    lax.fori_loop(0, blocks // 2, prologue, 0)
    start_loads(0)
    for c in range(width // LANES):
        cols = slice(c * LANES, (c + 1) * LANES)
        n2_t[cols, :] = n2_ref[:, cols].T
    n2_t[width:, :] = jnp.ones((PIECES, rows_all), bf16)
    bias_swap.wait()

    def tile(i):
        other, k = which(i)
        slot = i % 2
        wait_loads(i)

        @pl.when(i + 1 < tiles)
        def _():
            start_loads(i + 1)

        up, down = up_buf.at[slot], down_buf.at[slot]
        bias_at = jnp.where(other, k, count + k)
        bias = jnp.where(other, bup_other[k], bup_ref[k])
        linear = 0.7978845608028654
        cubic = linear * 0.044715
        for r in range(blocks):
            rows = slice(r * ROW_TILE, (r + 1) * ROW_TILE)
            pre = dot(n2_ref[rows, :], up[...]) + bias
            d_act = dot(dy_ref[rows, :], down[...], NT)
            square = pre * pre
            bend = jnp.tanh(pre * (square * cubic + linear))
            gate = 0.5 * bend + 0.5
            full_act = pre * gate
            slope = gate + (full_act - full_act * gate) * (square * (6.0 * cubic) + 2.0 * linear)
            act_ref[rows, :] = full_act.astype(bf16)
            dpre_ref[rows, :] = (d_act * slope).astype(bf16)
        total_ref[...] += dot(act_ref[...], down[...])
        dn2_ref[...] += dot(dpre_ref[...], up[...], NT)
        down_grad[k] = dot(act_ref[...].T, dy_ref[...]).astype(bf16)

        def start(lane):
            for side, grad in sides:
                side.start_a(k, lane, grad)

        by_rows = dot(n2_t[...], dpre_ref[...])
        up_grad[k] = by_rows[:width].astype(bf16)
        gbup_ref[bias_at] = by_rows[width : width + 1]
        pl.when(other)(functools.partial(start, 0))
        pl.when(jnp.logical_not(other))(functools.partial(start, 1))

    def each(k, when, action):
        @pl.when(jnp.logical_and(when, jnp.logical_and(k >= 0, k < count)))
        def _():
            for n, (side, grad) in enumerate(sides):
                action(n, side, grad, k)

    def stage_b(n, side, grad, k):
        side.stage_b(k, grad)

    def stage_c(n, side, grad, k):
        side.stage_c(k, grad)

    def stage_d(n, side, grad, k):
        side.stage_d(k)

    def arrive(n, side, grad, k):
        piece = side.gather_d(k)
        if n == 0:
            pieces_ref[k] = piece
        else:
            for c in range(width // HIDDEN_TILE):
                cols = slice(c * HIDDEN_TILE, (c + 1) * HIDDEN_TILE)
                pieces_ref[count + k, :, cols] = piece[c * PIECES : (c + 1) * PIECES]

    def steps(i):
        even = i % 2 == 0
        odd = jnp.logical_not(even)
        each((i - 5) // 2, odd, arrive)
        each((i - 4) // 2, even, stage_d)
        each((i - 3) // 2, odd, stage_c)
        each(i // 2, even, stage_b)

    def epilogue(r, _):
        rows = pl.ds(pl.multiple_of(r * ROW_TILE, ROW_TILE), ROW_TILE)
        out_ref[rows, :] = total_ref[rows, :].astype(bf16)
        unit, scale = normal(mid_ref[rows, :])
        d_rows = dn2_ref[rows, :]
        dy = dy_ref[rows, :].astype(f32)
        lean = d_rows * vectors_ref[2:3, :]
        d_mid = dy + scale * (
            lean
            - jnp.mean(lean, axis=-1, keepdims=True)
            - unit * jnp.mean(lean * unit, axis=-1, keepdims=True)
        )
        mid_ref[rows, :] = d_mid
        d_branch = d_mid.astype(bf16)
        n2_ref[rows, :] = d_branch
        datt_ref[rows, :] = dot(d_branch, wout_ref[...], NT).astype(bf16)
        datt2_ref[rows, :] = dot(d_branch, wout2_ref[...], NT).astype(bf16)
        add = lambda values: jnp.sum(values, axis=0, keepdims=True)
        small_ref[0:1, :] += add(d_rows * unit)
        small_ref[1:2, :] += add(d_rows)
        small_ref[2:3, :] += add(dy)
        return 0

    def out_grads():
        for source, target in ((att_ref, gout_ref), (att2_ref, gout2_ref)):
            grad = dot(source[...].T, n2_ref[...]).astype(bf16)
            for a in range(wout_ref.shape[0] // LANES):
                for b in range(2):
                    rows = slice(a * LANES, (a + 1) * LANES)
                    cols = slice(b * lanes, (b + 1) * lanes)
                    spread = slice(a * lanes, (a + 1) * lanes)
                    target[b * LANES : (b + 1) * LANES, spread] = grad[rows, cols]

    def main(i, _):
        pl.when(i < tiles)(functools.partial(tile, i))

        @pl.when(jnp.logical_and(i >= tiles, i < tiles + 2))
        def _():
            first = (i - tiles) * (blocks // 2)
            lax.fori_loop(first, first + blocks // 2, epilogue, 0)

        @pl.when(i == tiles + 2)
        def _():
            for store in stores:
                store.start()
            out_grads()

        steps(i)
        return 0

    small_ref[...] = jnp.zeros_like(small_ref)
    stores = [
        pltpu.make_async_copy(source, target, store_sem.at[n])
        for n, (source, target) in enumerate(
            (
                (datt2_ref, datt2_hbm),
                (out_ref, out_hbm),
                (mid_ref, mid_hbm),
                (datt_ref, datt_hbm),
            )
        )
    ]
    lax.fori_loop(0, tiles + 4, main, 0)
    for store in stores:
        store.wait()

    def handed(slot, _):
        hand_down(slot).wait_send()
        return 0

    lax.fori_loop(0, count, handed, 0)


def middle(bits, x, att, att2, wout, wout2, dy, vectors, bup, ups, downs):
    rows, width = x.shape
    hidden = ups[0].shape[1]
    count = hidden // HIDDEN_TILE
    tiles = 2 * count
    exchanges = (
        Exchange(bits, count, HIDDEN_TILE, width, False),
        Exchange(bits, count, width, HIDDEN_TILE, False),
    )
    vmem = pl.BlockSpec(memory_space=pltpu.VMEM)
    hbm = pl.BlockSpec(memory_space=pl.ANY)
    shape = jax.ShapeDtypeStruct
    depth = wout.shape[0]
    return pl.pallas_call(
        functools.partial(middle_kernel, exchanges, tiles),
        in_specs=[vmem] * 8 + [hbm] * 5,
        out_specs=[hbm] * 4 + [vmem] * 5,
        out_shape=[
            shape((rows, width), bf16),
            shape((rows, width), f32),
            shape(att.shape, bf16),
            shape(att2.shape, bf16),
            shape((2 * LANES, depth // LANES * width // 2), bf16),
            shape((2 * LANES, depth // LANES * width // 2), bf16),
            shape((tiles, 1, HIDDEN_TILE), f32),
            shape((8, width), f32),
            shape((2 * count, PIECES, width), bf16),
        ],
        scratch_shapes=[
            pltpu.VMEM((count, width // 2, HIDDEN_TILE), bf16),
            pltpu.VMEM((count, HIDDEN_TILE // 2, width), bf16),
            pltpu.SemaphoreType.DMA((count, 4)),
            pltpu.SemaphoreType.DMA((count, 2)),
            pltpu.VMEM((2, width, HIDDEN_TILE), bf16),
            pltpu.VMEM((2, HIDDEN_TILE, width), bf16),
            pltpu.SemaphoreType.DMA((2, 6)),
            pltpu.VMEM((rows, width), bf16),
            pltpu.VMEM((rows, width), f32),
            pltpu.VMEM((rows, width), f32),
            pltpu.VMEM((rows, HIDDEN_TILE), bf16),
            pltpu.VMEM((rows, HIDDEN_TILE), bf16),
            pltpu.VMEM((width + PIECES, rows), bf16),
            pltpu.VMEM(bup.shape, f32),
            pltpu.SemaphoreType.DMA((2,)),
            pltpu.VMEM((rows, width), bf16),
            pltpu.VMEM((rows, width), f32),
            pltpu.VMEM(att.shape, bf16),
            pltpu.VMEM(att2.shape, bf16),
            pltpu.SemaphoreType.DMA((4,)),
            pltpu.VMEM((count, HIDDEN_TILE, width), bf16),
            pltpu.VMEM((count, width, HIDDEN_TILE), bf16),
        ]
        + exchanges[0].scratch()
        + exchanges[1].scratch(),
        compiler_params=pltpu.CompilerParams(
            collective_id=0, has_side_effects=True, vmem_limit_bytes=67043328
        ),
        name="middle",
        cost_estimate=pl.CostEstimate(
            flops=60 * 10**9, bytes_accessed=40 * 10**6, transcendentals=4 * 10**6
        ),
    )(x, att, att2, wout, wout2, dy, vectors, bup, *ups, *downs)


def leave_kernel(exchange, *refs):
    (
        rows_hbm,
        mine_out_ref,
        crossed_ref,
        crossed_out_ref,
        d_hbm,
        d2_hbm,
        w_hbm,
        w2_hbm,
        tokens_ref,
        context_ref,
        given_ref,
        vectors_ref,
        dmid_hbm,
        small_ref,
        small2_ref,
        gqkv_ref,
        gout_ref,
        back_ref,
        sums_ref,
        full_ref,
        out_buf,
        rows_t_ref,
        d_ref,
        d2_ref,
        w_ref,
        w2_ref,
        dmid_ref,
        load_sem,
        rows_ref,
        give_ref,
        take_ref,
        swap_sem,
        norm_ref,
        near_ref,
        far_ref,
        near_sem,
        far_sem,
        *rest,
    ) = refs
    place, part = lax.axis_index("dp"), lax.axis_index("mp")
    ex = exchange.bind(place, part, rest)
    count, bits = ex.count, ex.bits
    loads = [
        pltpu.make_async_copy(source, target, load_sem.at[n])
        for n, (source, target) in enumerate(
            (
                (d_hbm, d_ref),
                (rows_hbm, rows_t_ref),
                (w_hbm, w_ref),
                (w2_hbm, w2_ref),
                (d2_hbm, d2_ref),
                (dmid_hbm, dmid_ref),
            )
        )
    ]
    for load in loads:
        load.start()
    near_id = part * 4 + place % 4
    near = [
        {"dp": flip(place, j % 4), "mp": part if j < 4 else 1 - part} for j in range(1, 8)
    ]
    ex.partners += [near[j - 1] for j in (3, 5, 6, 7)]
    ex.greet()

    lanes = d_ref.shape[2]
    split = mine_out_ref.shape[1] // lanes
    for r in range(split):
        cols = slice(r * lanes, (r + 1) * lanes)
        total = mine_out_ref[:, cols].astype(f32) + crossed_out_ref[:, cols].astype(f32)
        out_buf[r] = total.astype(bf16)
        ex.start_a(r, 0, out_buf)
    step = HALF + 2 * EDGE

    def back_rows(n):
        start = CLEAN_OWN + n * (KEY_ROWS - step - CLEAN_OWN)
        rows = pl.ds(pl.multiple_of(start, EDGE), step)
        total = 0.0
        for grads, weights in ((d_ref, w_ref), (d2_ref, w2_ref)):
            for c in range(3):
                total = total + dot(grads[c, rows, :], weights[c], NT)
        rows_ref[rows, :] = total

    def grad_chunk(c):
        for r in range(split):
            rows = slice(r * ROW_TILE, (r + 1) * ROW_TILE)
            k = (c + 1) * split + r
            out_buf[k] = dot(rows_t_ref[rows, :], d_ref[c]).astype(bf16)
            ex.start_a(k, 0, out_buf)

    def stage_c(k):
        @pl.when(k >= split)
        def _():
            ex.stage_c(k, out_buf, lambda rows: crossed_ref[k - split, rows, :].astype(f32))

        @pl.when(k < split)
        def _():
            ex.stage_c(k, out_buf)

    def arrive(k):
        ex.stage_h(k, full_ref)

        @pl.when(k < split)
        def _():
            rows = pl.ds(pl.multiple_of(k * LANES, LANES), LANES)
            for b in range(2):
                piece = full_ref[k, b * LANES : (b + 1) * LANES, :]
                gout_ref[rows, b * lanes : (b + 1) * lanes] = piece

        @pl.when(k >= split)
        def _():
            n = k - split
            rows = pl.ds(pl.multiple_of(n % split * ROW_TILE, ROW_TILE), ROW_TILE)
            gqkv_ref[n // split, rows, :] = full_ref[k]

    def group(g, action):
        @pl.when(jnp.logical_and(g >= 0, g < count // split))
        def _():
            lax.fori_loop(g * split, (g + 1) * split, lambda k, _: (action(k), 0)[1], 0)

    def steps(i):
        group(i - 5, arrive)
        group(i - 4, lambda k: ex.stage_g(k, full_ref))
        group(i - 3, lambda k: ex.stage_f(k, full_ref))
        group(i - 2, lambda k: ex.stage_e(k, full_ref))
        group(i - 1, lambda k: ex.stage_d(k))
        group(i, stage_c)

    width = tokens_ref.shape[1]

    def swap(rows, lane):
        return pltpu.make_async_remote_copy(
            src_ref=give_ref.at[rows],
            dst_ref=take_ref.at[rows],
            send_sem=swap_sem.at[lane, 0],
            recv_sem=swap_sem.at[lane, 1],
            device_id=ex.across,
            device_id_type=MESH,
        )

    def sums_of(d_rows, units):
        add = lambda values: jnp.sum(values, axis=0, keepdims=True)
        norm_ref[0:1, :] += add(d_rows * units)
        norm_ref[1:2, :] += add(d_rows)

    main = slice(0, HALF)
    edges = slice(HALF, HALF + 2 * EDGE)
    parts = tokens_ref.shape[0] // TILE
    lead = small_ref.shape[0] - 2
    bias = lead - 3
    norm_ref[...] = jnp.zeros_like(norm_ref)
    for load in loads[:2]:
        load.wait()

    def own_at(b):
        start = jnp.where(b < TILES, NOISY_OWN + b * TILE, CLEAN_OWN + (b - TILES) * TILE)
        return pl.ds(pl.multiple_of(start, EDGE), TILE)

    def tokens_at(b):
        return pl.ds(pl.multiple_of(b * TILE, TILE), TILE)

    def ready():
        for load in loads[2:5]:
            load.wait()

    give_ref[main, :] = given_ref[...].astype(bf16)
    swap(main, 0).start()

    def give_edges():
        side = rows_ref[NOISY_BASE:NOISY_OWN, :] + rows_ref[NOISY_OWN + HALF :, :]
        after = rows_ref[2 * HALF : NOISY_BASE, :]
        give_ref[HALF : HALF + EDGE, :] = after.astype(bf16)
        give_ref[HALF + EDGE :, :] = side.astype(bf16)
        swap(edges, 1).start()
        sums_of(after, normal(context_ref[:EDGE, :].astype(f32))[0])
        sums_of(side, normal(context_ref[HALF:, :].astype(f32))[0])

    def tell_near():
        def context_sums(b, _):
            rows = tokens_at(b)
            sums_of(given_ref[rows, :], normal(context_ref[rows, :].astype(f32))[0])
            return 0

        lax.fori_loop(0, HALF // TILE, context_sums, 0)

        def own_sums(b, _):
            sums_of(rows_ref[own_at(b), :], normal(tokens_ref[tokens_at(b), :].astype(f32))[0])
            return 0

        lax.fori_loop(0, parts, own_sums, 0)
        mine = near_ref.at[near_id]
        mine[:lead, :] = small_ref[:lead, :]
        mine[lead : lead + 2, :] = norm_ref[:2, :]
        mine[lead + 2 : lead + 2 + bias, :] = small2_ref[:bias, :]
        rest_rows = 16 - lead - 2 - bias
        mine[16 - rest_rows :, :] = jnp.zeros((rest_rows, width), f32)
        for j in range(1, 8):
            near_copy(j).start()

    def near_copy(j):
        return pltpu.make_async_remote_copy(
            src_ref=near_ref.at[near_id],
            dst_ref=near_ref.at[near_id],
            send_sem=near_sem.at[j, 0],
            recv_sem=near_sem.at[j, 1],
            device_id=near[j - 1],
            device_id_type=MESH,
        )

    def near_got(j):
        came = (part + j // 4) % 2 * 4 + flip(place % 4, j % 4)
        return pltpu.make_async_remote_copy(
            src_ref=near_ref.at[came],
            dst_ref=near_ref.at[came],
            send_sem=near_sem.at[j, 0],
            recv_sem=near_sem.at[j, 1],
            device_id=near[j - 1],
            device_id_type=MESH,
        )

    def far_copy(j, at):
        return pltpu.make_async_remote_copy(
            src_ref=far_ref.at[at],
            dst_ref=far_ref.at[at],
            send_sem=far_sem.at[j, 0],
            recv_sem=far_sem.at[j, 1],
            device_id=ex.peers[j - 1],
            device_id_type=MESH,
        )

    def tell_far():
        for j in range(1, 8):
            near_copy(j).wait_send()
            near_got(j).wait_recv()
        total = near_ref[0]
        for j in range(1, 8):
            total = total + near_ref[j]
        plane = near_ref[part * 4]
        other = near_ref[(1 - part) * 4]
        for j in range(1, 4):
            plane = plane + near_ref[part * 4 + j]
            other = other + near_ref[(1 - part) * 4 + j]
        spot = far_ref.at[ex.z]
        spot[...] = total
        spot[:bias, :] = plane[:bias] + other[lead + 2 : lead + 2 + bias]
        for j in range(1, 4):
            far_copy(j, ex.z).start()

    def take_back():
        loads[5].wait()
        swap(main, 0).wait()
        swap(edges, 1).wait()
        clean = slice(CLEAN_OWN, CLEAN_OWN + HALF)
        rows_ref[clean, :] += take_ref[main, :].astype(f32)
        begin = slice(CLEAN_OWN, CLEAN_OWN + EDGE)
        rows_ref[begin, :] += take_ref[HALF : HALF + EDGE, :].astype(f32)
        edge = pl.ds(pl.multiple_of(NOISY_OWN + (1 - part) * (HALF - EDGE), EDGE), EDGE)
        rows_ref[edge, :] += take_ref[HALF + EDGE :, :].astype(f32)

    def norm_back(b):
        rows = tokens_at(b)
        unit, scale = normal(tokens_ref[rows, :].astype(f32))
        lean = rows_ref[own_at(b), :] * vectors_ref[0:1, :]
        back_ref[rows, :] = dmid_ref[rows, :] + scale * (
            lean
            - jnp.mean(lean, axis=-1, keepdims=True)
            - unit * jnp.mean(lean * unit, axis=-1, keepdims=True)
        )

    def end_far():
        for j in range(1, 4):
            far_copy(j, ex.z).wait_send()
            far_copy(j, flip(ex.z, j)).wait_recv()
        total = far_ref[0]
        for j in range(1, 4):
            total = total + far_ref[j]
        for i, b in enumerate(ex.extra):
            far_ref[4 + 2 * i] = total
            trade = pltpu.make_async_remote_copy(
                src_ref=far_ref.at[4 + 2 * i],
                dst_ref=far_ref.at[5 + 2 * i],
                send_sem=far_sem.at[4 + i, 0],
                recv_sem=far_sem.at[4 + i, 1],
                device_id={"dp": flip(place, 1 << b)},
                device_id_type=MESH,
            )
            trade.start()
            trade.wait()
            total = total + far_ref[5 + 2 * i]
        sums_ref[...] = total

    groups = count // split - 1
    actions = {
        groups + 1: give_edges,
        groups + 2: tell_near,
        groups + 3: tell_far,
        groups + 4: take_back,
    }
    begin_back = groups + 5

    def phase(p, _):
        @pl.when(p < groups)
        def _():
            grad_chunk(p)

        pl.when(p == groups)(ready)

        @pl.when(jnp.logical_and(p >= groups, p < groups + 2))
        def _():
            back_rows(p - groups)

        for n, action in actions.items():
            pl.when(p == n)(action)
        block = 2 * (p - begin_back)

        @pl.when(jnp.logical_and(block >= 0, block < parts))
        def _():
            lax.fori_loop(block, block + 2, lambda b, _: (norm_back(b), 0)[1], 0)

        pl.when(block == parts)(end_far)
        steps(p)
        return 0

    lax.fori_loop(0, begin_back + parts // 2 + 1, phase, 0)


def leave(bits, rows_t, mine, crossed, d_fields, weights, tokens, context, given, vectors, d_mid, small, small2):
    rows, cols = ROW_TILE, d_fields[0].shape[2]
    total = mine.shape[1] // cols + crossed[0].shape[0]
    exchange = Exchange(bits, total, rows, cols)
    count, width = tokens.shape
    vmem = pl.BlockSpec(memory_space=pltpu.VMEM)
    hbm = pl.BlockSpec(memory_space=pl.ANY)
    shape = jax.ShapeDtypeStruct
    return pl.pallas_call(
        functools.partial(leave_kernel, exchange),
        in_specs=[hbm] + [vmem] * 3 + [hbm] * 4 + [vmem] * 4 + [hbm] + [vmem] * 2,
        out_specs=[vmem] * 4,
        out_shape=[
            shape(weights[0].shape, bf16),
            shape((d_fields[0].shape[2], width), bf16),
            shape((count, width), f32),
            shape((16, width), f32),
        ],
        scratch_shapes=[
            pltpu.VMEM((total, rows, cols), bf16),
            pltpu.VMEM((total, rows, cols), bf16),
            pltpu.VMEM(rows_t.shape, bf16),
            pltpu.VMEM(d_fields[0].shape, bf16),
            pltpu.VMEM(d_fields[1].shape, bf16),
            pltpu.VMEM(weights[0].shape, bf16),
            pltpu.VMEM(weights[1].shape, bf16),
            pltpu.VMEM(d_mid.shape, f32),
            pltpu.SemaphoreType.DMA((6,)),
            pltpu.VMEM((KEY_ROWS, width), f32),
            pltpu.VMEM((HALF + 2 * EDGE, width), bf16),
            pltpu.VMEM((HALF + 2 * EDGE, width), bf16),
            pltpu.SemaphoreType.DMA((2, 2)),
            pltpu.VMEM((8, width), f32),
            pltpu.VMEM((8, 16, width), f32),
            pltpu.VMEM((4 + 2 * len(exchange.extra), 16, width), f32),
            pltpu.SemaphoreType.DMA((8, 2)),
            pltpu.SemaphoreType.DMA((4 + len(exchange.extra), 2)),
        ]
        + exchange.scratch(),
        compiler_params=pltpu.CompilerParams(
            collective_id=1, has_side_effects=True, vmem_limit_bytes=67043328
        ),
        name="leave",
        cost_estimate=pl.CostEstimate(
            flops=40 * 10**9, bytes_accessed=40 * 10**6, transcendentals=0
        ),
    )(
        rows_t, mine, *crossed, *d_fields, *weights, tokens, context, given, vectors, d_mid, small, small2
    )


def assemble_kernel(core_ref, down_mine, up_mine, down_got, up_got, down_ref, up_ref):
    core = core_ref[0]
    block = down_mine.shape[1]
    lanes = up_ref.shape[1]
    parts = down_mine.shape[2] // lanes
    deep = block * parts
    for side, down, up in ((core, down_mine, up_mine), (1 - core, down_got, up_got)):
        rows = pl.ds(pl.multiple_of(side * block, block), block)
        down_ref[rows, :] = down[0].astype(f32)
        for n in range(block // PIECES):
            for c in range(parts):
                at = side * deep + (n * parts + c) * PIECES
                rows = pl.ds(pl.multiple_of(at, PIECES), PIECES)
                piece = up[0, n * PIECES : (n + 1) * PIECES, c * lanes : (c + 1) * lanes]
                up_ref[rows, :] = piece.astype(f32)


def assemble(core, gathered, moved):
    tiles, half, width = gathered.shape
    count = tiles // 2
    down_spec = pl.BlockSpec((1, half, width), lambda k, c: (k, 0, 0))
    up_spec = pl.BlockSpec((1, half, width), lambda k, c: (count + k, 0, 0))
    hidden = count * 2 * half
    return pl.pallas_call(
        assemble_kernel,
        grid_spec=pltpu.PrefetchScalarGridSpec(
            num_scalar_prefetch=1,
            grid=(count,),
            in_specs=[down_spec, up_spec, down_spec, up_spec],
            out_specs=[
                pl.BlockSpec((2 * half, width), lambda k, c: (k, 0)),
                pl.BlockSpec((width, 2 * half), lambda k, c: (0, k)),
            ],
        ),
        out_shape=[
            jax.ShapeDtypeStruct((hidden, width), f32),
            jax.ShapeDtypeStruct((width, hidden), f32),
        ],
        name="assemble",
        cost_estimate=pl.CostEstimate(
            flops=10**6, bytes_accessed=14 * 10**6, transcendentals=0
        ),
    )(core, gathered, gathered, moved, moved)


def key_layout(seq_lengths, block_len, part):
    index = jnp.arange(KEY_ROWS, dtype=jnp.int32)
    own = part * HALF
    token = jnp.where(
        index < NOISY_BASE, index + (own - HALF), index - NOISY_BASE + (own - EDGE)
    )
    ends = jnp.cumsum(seq_lengths)
    passed = token[:, None] >= ends[None, :]
    starts = jnp.sum(jnp.where(passed, seq_lengths[None, :], 0), axis=1)
    lengths_here = jnp.where(passed, 0, ends[None, :])
    stops = jnp.min(jnp.where(passed, TOK_DEV, lengths_here), axis=1)
    positions = token - starts
    block_start = starts + positions // block_len * block_len
    block_stop = jnp.minimum(block_start + block_len, stops)
    mine = slice(CLEAN_OWN, CLEAN_OWN + HALF)
    low, start, stop = starts[mine], block_start[mine], block_stop[mine]
    to_clean = own - HALF
    tiles = lambda column: column.reshape(TILES, 1, TILE)
    clean_bounds = jnp.concatenate(
        [
            jnp.concatenate([tiles(low - to_clean), tiles(low - to_clean)], axis=2),
            jnp.concatenate([tiles(start - to_clean), tiles(stop - to_clean)], axis=2),
        ],
        axis=1,
    )
    to_window = own - EDGE + TILE * jnp.arange(TILES, dtype=jnp.int32)[:, None, None]
    noisy_bounds = jnp.concatenate(
        [tiles(start) - to_window, tiles(stop) - to_window], axis=1
    )
    first = jnp.min(clean_bounds[:, 0], axis=1) // EDGE * EDGE
    last = jnp.max(clean_bounds[:, 1], axis=1)
    trips = (last - first + KEY_TILE - 1) // KEY_TILE
    spans = jnp.stack([first, trips], axis=1)
    lane = jnp.arange(LANES, dtype=jnp.int32)
    frequency = jnp.exp(
        (lane % (HD // 2)).astype(f32) * (-math.log(10000.0) / (HD // 2))
    )
    angles = positions.astype(f32)[:, None] * frequency[None, :]
    sign = jnp.where(lane % HD < HD // 2, -1.0, 1.0)
    return spans, clean_bounds, noisy_bounds, jnp.cos(angles), jnp.sin(angles) * sign


def in_order(bit, mine, theirs, axis=0):
    order = bit == 0
    return jnp.concatenate(
        [jnp.where(order, mine, theirs), jnp.where(order, theirs, mine)], axis=axis
    )


def tie(first, second):
    return lax.optimization_barrier((first, second))


def local(
    dp_size,
    tokens,
    lengths,
    block_size,
    cotangent,
    ln1_gain,
    ln1_bias,
    w_qkv,
    w_out,
    ln2_gain,
    ln2_bias,
    w_up,
    b_up,
    w_down,
    b_down,
):
    width = tokens.shape[2]
    part = lax.axis_index("mp")
    place = lax.axis_index("dp")
    bits = dp_size.bit_length() - 1
    core = place & 1

    def across(array):
        return lax.ppermute(array, "mp", [(0, 1), (1, 0)])

    def sibling(array):
        return lax.ppermute(array, "dp", [(i, i ^ 1) for i in range(dp_size)])

    def beside(array):
        return lax.ppermute(array, "dp", [(i, i ^ 2) for i in range(dp_size)])

    edge = jnp.where(part == 0, tokens[0, HALF - EDGE :], tokens[0, :EDGE])
    context = across(jnp.concatenate([tokens[1], edge], axis=0))
    qkv_mine = w_qkv.transpose(1, 0, 2)
    side = (place >> 1) & 1

    def quarter_of(array, axis=0):
        size = array.shape[axis] // 4
        return lax.dynamic_slice_in_dim(array, (2 * core + side) * size, size, axis)

    def half_of(array):
        size = array.shape[0] // 2
        return lax.dynamic_slice_in_dim(array, core * size, size, 0)

    quarters = [quarter_of(qkv_mine, 1), quarter_of(w_up), half_of(w_down), half_of(w_out)]
    layout = key_layout(lengths[0], block_size[0], part)
    vectors = jnp.stack([ln1_gain, ln1_bias, ln2_gain, ln2_bias, b_down])
    context, (quarters, layout, vectors) = tie(context, (quarters, layout, vectors))
    qkv_here, up_here, down_here, out_here = [across(piece) for piece in quarters]

    spans, clean_bounds, noisy_bounds, cosine, sine = layout
    normed1, normed1_t, *fields = enter(tokens, context, vectors, qkv_mine, cosine, sine)
    qkv_here, fields = tie(qkv_here, fields)
    qkv_beside = beside(qkv_here)
    mine = [*fields, *attend_forward(spans, clean_bounds, noisy_bounds, *fields)]
    (qkv_here, qkv_beside, up_here), _ = tie((qkv_here, qkv_beside, up_here), mine[3])
    qkv_half = in_order(side, qkv_here, qkv_beside, axis=1)
    qkv_other = in_order(core, qkv_half, sibling(qkv_half), axis=1)
    up_beside = beside(up_here)
    fields = project(normed1, qkv_other, cosine, sine)
    other = [*fields, *attend_forward(spans, clean_bounds, noisy_bounds, *fields)]
    (out_here, up_here, up_beside, down_here), _ = tie(
        (out_here, up_here, up_beside, down_here), other[3]
    )
    out_other = in_order(core, out_here, sibling(out_here))
    bias_all = b_up.astype(f32).reshape(-1, 1, HIDDEN_TILE)

    x_rows = tokens.reshape(TOK_DEV, width)
    out, d_mid, d_att, d_att2, grad_out, grad_out2, grad_bias, norms, pieces = middle(
        bits,
        x_rows,
        mine[3],
        other[3],
        w_out,
        out_other,
        cotangent.reshape(TOK_DEV, width),
        vectors,
        bias_all,
        (w_up, up_here, up_beside),
        (w_down, down_here),
    )
    hidden = b_up.shape[0]

    crossed_out = across(grad_out2)
    spread = [(b, min(2, min(bits, 4) - b)) for b in range(2, min(bits, 4), 2)]
    gathered = pieces
    ((first_bit, n),) = spread
    moved = [
        lax.ppermute(gathered, "dp", [(i, i ^ (k << first_bit)) for i in range(dp_size)])
        for k in range(1, 1 << n)
    ]

    def backward(saved, d_attended, spans, *rest):
        query, keys, values, attended, lse = saved
        return attend_backward(
            spans,
            clean_bounds,
            noisy_bounds,
            query,
            keys,
            values,
            attended,
            d_attended,
            lse,
            cosine,
            sine,
            rest,
        )

    d_fields2, grad2 = backward(other, d_att2, spans, normed1_t)
    grad2 = grad2.reshape(-1, ROW_TILE, grad2.shape[2])
    low_bit, high_bit = (place >> 2) & 1, (place >> 3) & 1
    moved, _ = tie(moved, grad2)
    gathered = in_order(
        high_bit,
        in_order(low_bit, gathered, moved[0], 1),
        in_order(low_bit, moved[1], moved[2], 1),
        1,
    )
    half = ROW_TILE // 2
    part_of = lambda array, which: lax.dynamic_slice_in_dim(array, which * half, half, 1)
    got = sibling(part_of(grad2, 1 - core))
    crossing = (part_of(grad2, core).astype(f32) + got.astype(f32)).astype(bf16)
    (crossing, gathered), spans = tie((crossing, gathered), spans)
    crossed = across(crossing)
    moved = beside(gathered)
    d_fields1, given = backward(mine, d_att, spans, d_fields2, qkv_mine, qkv_other)
    moved, d_fields1 = tie(moved, d_fields1)
    gathered = in_order(side, gathered, moved, 1)
    gathered, d_fields1 = tie(gathered, d_fields1)
    moved = sibling(gathered)
    lead = hidden // width
    bias2, bias1 = grad_bias.reshape(2, lead, width)
    shared = jnp.concatenate([norms[:3], jnp.zeros((2, width), f32)], axis=0)
    grad_qkv, grad_out, grad_tokens, sums = leave(
        bits,
        normed1_t,
        grad_out,
        (crossed, crossed_out),
        (d_fields1, d_fields2),
        (qkv_mine, qkv_other),
        x_rows,
        context,
        given,
        vectors,
        d_mid,
        jnp.concatenate([bias1, shared], axis=0),
        jnp.concatenate([bias2, shared], axis=0),
    )
    moved, _ = tie(moved, grad_qkv)
    grad_down, grad_up = assemble(core.reshape(1), gathered, moved)
    return (
        out.reshape(tokens.shape),
        grad_tokens.reshape(tokens.shape),
        sums[lead + 3],
        sums[lead + 4],
        grad_qkv.transpose(1, 0, 2).astype(f32),
        grad_out.astype(f32),
        sums[lead],
        sums[lead + 1],
        grad_up,
        sums[:lead].reshape(hidden),
        grad_down,
        sums[lead + 2],
    )


def solution(mesh):
    in_specs = (
        P(None, ("dp", "mp"), None),
        P("dp", None),
        P(),
        P(None, ("dp", "mp"), None),
        P(),
        P(),
        P(None, None, "mp"),
        P("mp", None),
        P(),
        P(),
        P(None, "mp"),
        P("mp"),
        P("mp", None),
        P(),
    )
    out_specs = (
        P(None, ("dp", "mp"), None),
        P(None, ("dp", "mp"), None),
        P(),
        P(),
        P(None, None, "mp"),
        P("mp", None),
        P(),
        P(),
        P(None, "mp"),
        P("mp"),
        P("mp", None),
        P(),
    )
    return jax.shard_map(
        functools.partial(local, mesh.shape["dp"]),
        mesh=mesh,
        in_specs=in_specs,
        out_specs=out_specs,
        check_vma=False,
    )
```

```python
import functools
import math

import jax
import jax.numpy as jnp
from jax import lax
from jax.experimental import pallas as pl
from jax.experimental.pallas import tpu as pltpu
from jax.sharding import PartitionSpec as P

HD = 64
TOK_DEV = 1024
HALF = TOK_DEV // 2
EDGE = 16
CLEAN_OWN = HALF
NOISY_BASE = 2 * HALF + EDGE
NOISY_OWN = NOISY_BASE + EDGE
KEY_ROWS = NOISY_OWN + HALF + EDGE
TILE = 128
TILES = HALF // TILE
WINDOW = TILE + 2 * EDGE
KEY_TILE = 192
LANES = 128
HIDDEN_TILE = 256
ROW_TILE = 256

epsilon = 1e-05
neg_large = -1e30
to_base2 = 0.125 * math.log2(math.e)
f32 = jnp.float32
bf16 = jnp.bfloat16

NN = (((1,), (0,)), ((), ()))
NT = (((1,), (1,)), ((), ()))


def dot(left, right, dims=NN):
    return lax.dot_general(left, right, dims, preferred_element_type=f32)


def low_lanes(shape):
    return lax.broadcasted_iota(jnp.int32, shape, 1) < HD


def turn(values, cosine, sine):
    lane = lax.broadcasted_iota(jnp.int32, values.shape, 1)
    first_half = (lane & (HD - 1)) < HD // 2
    swapped = jnp.where(
        first_half,
        pltpu.roll(values, LANES - HD // 2, 1),
        pltpu.roll(values, HD // 2, 1),
    )
    return values * cosine + swapped * sine


def project_rows(rows, w_ref, cosine, sine, q_ref, k_ref, v_ref, at):
    for part, out_ref in ((0, q_ref), (1, k_ref)):
        field = dot(rows, w_ref[part])
        for pair in range(field.shape[1] // LANES):
            cols = slice(pair * LANES, (pair + 1) * LANES)
            out_ref[at, cols] = turn(field[:, cols], cosine, sine).astype(bf16)
    v_ref[at, :] = dot(rows, w_ref[2]).astype(bf16)


def project_kernel(rows_ref, w_ref, cos_ref, sin_ref, q_ref, k_ref, v_ref):
    at = slice(0, rows_ref.shape[0])
    project_rows(rows_ref[...], w_ref, cos_ref[...], sin_ref[...], q_ref, k_ref, v_ref, at)


def project(rows, weights, cosine, sine):
    count, width = rows.shape
    cols = weights.shape[2]
    step = count // 3
    row_spec = pl.BlockSpec((step, width), lambda i: (i, 0))
    table_spec = pl.BlockSpec((step, LANES), lambda i: (i, 0))
    out_spec = pl.BlockSpec((step, cols), lambda i: (i, 0))
    shape = jax.ShapeDtypeStruct((count, cols), bf16)
    return pl.pallas_call(
        project_kernel,
        grid=(3,),
        in_specs=[
            row_spec,
            pl.BlockSpec(weights.shape, lambda i: (0, 0, 0)),
            table_spec,
            table_spec,
        ],
        out_specs=[out_spec] * 3,
        out_shape=[shape] * 3,
        name="project",
        cost_estimate=pl.CostEstimate(
            flops=2 * count * width * 3 * cols,
            bytes_accessed=2 * (count * (width + 3 * cols) + 3 * width * cols),
            transcendentals=0,
        ),
    )(rows, weights, cosine, sine)


def normal(values):
    average = jnp.mean(values, axis=-1, keepdims=True)
    centred = values - average
    variance = jnp.mean(centred * centred, axis=-1, keepdims=True)
    scale = lax.rsqrt(variance + epsilon)
    return centred * scale, scale


def enter_kernel(
    tokens_ref,
    context_ref,
    vectors_ref,
    w_ref,
    cos_ref,
    sin_ref,
    rows_ref,
    rows_t_ref,
    q_ref,
    k_ref,
    v_ref,
):
    def norm(values):
        unit = normal(values.astype(f32))[0]
        return (unit * vectors_ref[0:1, :] + vectors_ref[1:2, :]).astype(bf16)

    def blocks(i, _):
        source = pl.ds(pl.multiple_of(i * TILE, TILE), TILE)
        rows_ref[source, :] = norm(context_ref[source, :])
        at = pl.ds(pl.multiple_of(CLEAN_OWN + i * TILE, TILE), TILE)
        rows_ref[at, :] = norm(tokens_ref[1, source, :])
        at = pl.ds(pl.multiple_of(NOISY_OWN + i * TILE, EDGE), TILE)
        rows_ref[at, :] = norm(tokens_ref[0, source, :])
        return 0

    lax.fori_loop(0, TILES, blocks, 0)
    rows_ref[2 * HALF : NOISY_BASE, :] = rows_ref[:EDGE, :]
    edge = norm(context_ref[HALF:, :])
    rows_ref[NOISY_BASE:NOISY_OWN, :] = edge
    rows_ref[NOISY_OWN + HALF :, :] = edge
    step = KEY_ROWS // 3

    def fields(i, _):
        at = pl.ds(pl.multiple_of(i * step, EDGE), step)
        project_rows(
            rows_ref[at, :], w_ref, cos_ref[at, :], sin_ref[at, :], q_ref, k_ref, v_ref, at
        )
        return 0

    lax.fori_loop(0, 3, fields, 0)
    for c in range(rows_t_ref.shape[0] // LANES):
        cols = slice(c * LANES, (c + 1) * LANES)
        rows_t_ref[cols, :] = rows_ref[:, cols].T


def enter(tokens, context, vectors, weights, cosine, sine):
    width, cols = weights.shape[1:]
    vmem = pl.BlockSpec(memory_space=pltpu.VMEM)
    shape = jax.ShapeDtypeStruct
    field = shape((KEY_ROWS, cols), bf16)
    return pl.pallas_call(
        enter_kernel,
        in_specs=[vmem] * 6,
        out_specs=[vmem] * 5,
        out_shape=[shape((KEY_ROWS, width), bf16), shape((width, KEY_ROWS), bf16)] + [field] * 3,
        name="enter",
        cost_estimate=pl.CostEstimate(
            flops=10**10, bytes_accessed=16 * 10**6, transcendentals=0
        ),
    )(tokens, context, vectors, weights, cosine, sine)


def split_heads(rows):
    low = low_lanes(rows.shape)
    zero = jnp.zeros_like(rows)
    return jnp.where(low, rows, zero), jnp.where(low, zero, rows)


def between(shape, offset, low, high):
    index = lax.broadcasted_iota(jnp.int32, shape, 0) + offset
    return jnp.logical_and(index >= low, index < high)


def fold(values, combine):
    rows, cols = values.shape
    groups = values.reshape(rows // 8, 8, cols)
    return combine(groups, axis=0)


def forward_kernel(
    span_ref, clean_ref, noisy_ref, q_ref, k_ref, v_ref, out_ref, lse_ref, bias_ref, window_ref
):
    pairs = q_ref.shape[1] // LANES
    lanes = [slice(p * LANES, (p + 1) * LANES) for p in range(pairs)]

    def one_tile(t, _):
        clean_at = pl.multiple_of(CLEAN_OWN + t * TILE, TILE)
        noisy_at = pl.multiple_of(NOISY_OWN + t * TILE, EDGE)
        window_at = pl.multiple_of(NOISY_BASE + t * TILE, EDGE)
        key_low, key_high = clean_ref[t, 0:1, :], clean_ref[t, 1:2, :]
        own_low, own_high = noisy_ref[t, 0:1, :], noisy_ref[t, 1:2, :]
        allowed = between((WINDOW, TILE), 0, own_low, own_high)
        window_ref[...] = jnp.where(allowed, 0.0, neg_large)
        first_key, trips = span_ref[t, 0], span_ref[t, 1]
        queries, tops = [], []
        for cols in lanes:
            query = jnp.concatenate(
                [q_ref[pl.ds(noisy_at, TILE), cols], q_ref[pl.ds(clean_at, TILE), cols]], axis=0
            )
            heads = split_heads(query)
            queries += heads
            keys = k_ref[pl.ds(window_at, WINDOW), cols]
            for head in range(2):
                scores = dot(keys, heads[head][:TILE], NT) + window_ref[...]
                top = fold(scores, jnp.max)
                tops.append(
                    jnp.concatenate([top, jnp.full((8, TILE), neg_large, f32)], axis=1)
                )

        def first_pass(j, tops):
            at = pl.multiple_of(first_key + j * KEY_TILE, EDGE)
            allowed = between((KEY_TILE, 2 * TILE), at, key_low, key_high)
            bias_ref[j] = jnp.where(allowed, 0.0, neg_large)
            after = []
            for p, cols in enumerate(lanes):
                keys = k_ref[pl.ds(at, KEY_TILE), cols]
                for head in range(2):
                    scores = dot(keys, queries[2 * p + head], NT) + bias_ref[j]
                    after.append(jnp.maximum(tops[2 * p + head], fold(scores, jnp.max)))
            return tuple(after)

        tops = lax.fori_loop(0, trips, first_pass, tuple(tops))
        tops = [jnp.max(top, axis=0, keepdims=True) * to_base2 for top in tops]
        state = []
        keys = [k_ref[pl.ds(window_at, WINDOW), cols] for cols in lanes]
        values_t = [v_ref[pl.ds(window_at, WINDOW), cols].T for cols in lanes]
        scores = dot(keys[0], queries[0][:TILE], NT)
        late = None
        for h in range(2 * pairs):
            if h + 1 < 2 * pairs:
                ahead = dot(keys[(h + 1) // 2], queries[h + 1][:TILE], NT)
            expo = jnp.exp2(scores * to_base2 - tops[h][:, :TILE] + window_ref[...])
            if late is not None:
                state.append(jnp.concatenate([late, jnp.zeros((HD, TILE), f32)], axis=1))
            total = fold(expo, jnp.sum)
            state.append(jnp.concatenate([total, jnp.zeros((8, TILE), f32)], axis=1))
            side = slice(h % 2 * HD, (h % 2 + 1) * HD)
            late = dot(values_t[h // 2][side], expo.astype(bf16))
            scores = ahead
        state.append(jnp.concatenate([late, jnp.zeros((HD, TILE), f32)], axis=1))

        def second_pass(j, state):
            at = pl.multiple_of(first_key + j * KEY_TILE, EDGE)
            keys = [k_ref[pl.ds(at, KEY_TILE), cols] for cols in lanes]
            values_t = [v_ref[pl.ds(at, KEY_TILE), cols].T for cols in lanes]
            after = list(state)
            scores = dot(keys[0], queries[0], NT)
            late = None
            for h in range(2 * pairs):
                ahead = dot(keys[(h + 1) // 2], queries[h + 1], NT) if h + 1 < 2 * pairs else None
                expo = jnp.exp2(scores * to_base2 - tops[h] + bias_ref[j])
                after[2 * h] = state[2 * h] + fold(expo, jnp.sum)
                if late is not None:
                    after[2 * h - 1] = state[2 * h - 1] + late
                side = slice(h % 2 * HD, (h % 2 + 1) * HD)
                late = dot(values_t[h // 2][side], expo.astype(bf16))
                scores = ahead
            after[-1] = state[-1] + late
            return tuple(after)

        state = lax.fori_loop(0, trips, second_pass, tuple(state))
        low_at = pl.ds(pl.multiple_of(t * TILE, TILE), TILE)
        high_at = pl.ds(pl.multiple_of(HALF + t * TILE, TILE), TILE)
        for p, cols in enumerate(lanes):
            halves = []
            for head in range(2):
                h = 2 * p + head
                total = jnp.sum(state[2 * h], axis=0, keepdims=True)
                halves.append(state[2 * h + 1] / total)
                lse_ref[p, t, head : head + 1, :] = tops[h] + jnp.log2(total)
            pair = jnp.concatenate(halves, axis=0).T.astype(bf16)
            out_ref[low_at, cols] = pair[:TILE]
            out_ref[high_at, cols] = pair[TILE:]
        return 0

    lax.fori_loop(0, TILES, one_tile, 0)


def attend_forward(spans, clean_bounds, noisy_bounds, query, keys, values):
    count, cols = query.shape
    pairs = cols // LANES
    vmem = pl.BlockSpec(memory_space=pltpu.VMEM)
    work = pairs * 2 * 2 * HALF * TOK_DEV
    return pl.pallas_call(
        forward_kernel,
        in_specs=[pl.BlockSpec(memory_space=pltpu.SMEM)] + [vmem] * 5,
        out_specs=[vmem] * 2,
        out_shape=[
            jax.ShapeDtypeStruct((TOK_DEV, cols), bf16),
            jax.ShapeDtypeStruct((pairs, TILES, 2, 2 * TILE), f32),
        ],
        scratch_shapes=[
            pltpu.VMEM((NOISY_BASE // KEY_TILE + 1, KEY_TILE, 2 * TILE), f32),
            pltpu.VMEM((WINDOW, TILE), f32),
        ],
        name="attend_forward",
        cost_estimate=pl.CostEstimate(
            flops=4 * work * HD, bytes_accessed=8 * count * cols, transcendentals=work
        ),
    )(spans, clean_bounds, noisy_bounds, query, keys, values)


def backward_kernel(
    giving,
    span_ref,
    clean_ref,
    noisy_ref,
    q_ref,
    k_ref,
    v_ref,
    o_ref,
    d_ref,
    lse_ref,
    cos_ref,
    sin_ref,
    *refs,
):
    if giving:
        d2_hbm, w_hbm, w2_hbm, out_ref, give_ref, *refs = refs
        dk_ref, dv_ref, bias_ref, d2_ref, w_ref, w2_ref, load_sem = refs
        loads = [(w_hbm, w_ref), (w2_hbm, w2_ref)]
        loads += [(d2_hbm.at[c, :HALF], d2_ref.at[c]) for c in range(3)]
        loads = [
            pltpu.make_async_copy(source, target, load_sem.at[n])
            for n, (source, target) in enumerate(loads)
        ]
        for load in loads:
            load.start()
    else:
        rows_ref, out_ref, grad_ref, dk_ref, dv_ref, bias_ref = refs
    pairs = q_ref.shape[1] // LANES
    lanes = [slice(p * LANES, (p + 1) * LANES) for p in range(pairs)]
    dk_ref[...] = jnp.zeros_like(dk_ref)
    dv_ref[...] = jnp.zeros_like(dv_ref)
    out_ref[0] = jnp.zeros_like(out_ref[0])

    def one_tile(t, _):
        clean_at = pl.multiple_of(CLEAN_OWN + t * TILE, TILE)
        noisy_at = pl.multiple_of(NOISY_OWN + t * TILE, EDGE)
        window_at = pl.multiple_of(NOISY_BASE + t * TILE, EDGE)
        low_at = pl.multiple_of(t * TILE, TILE)
        high_at = pl.multiple_of(HALF + t * TILE, TILE)
        key_low, key_high = clean_ref[t, 0:1, :], clean_ref[t, 1:2, :]
        own_low, own_high = noisy_ref[t, 0:1, :], noisy_ref[t, 1:2, :]
        queries, d_outs, inners, lses = [], [], [], []
        for p, cols in enumerate(lanes):

            def both(ref, low, high):
                return jnp.concatenate(
                    [ref[pl.ds(low, TILE), cols], ref[pl.ds(high, TILE), cols]], axis=0
                )

            queries.append(split_heads(both(q_ref, noisy_at, clean_at)))
            d_rows = both(d_ref, low_at, high_at)
            o_rows = both(o_ref, low_at, high_at)
            product = (d_rows.astype(f32) * o_rows.astype(f32)).T
            d_outs.append(split_heads(d_rows))
            inners.append(
                [
                    jnp.sum(product[head * HD : (head + 1) * HD], axis=0, keepdims=True) * 0.125
                    for head in range(2)
                ]
            )
            lses.append([lse_ref[p, t, head : head + 1, :] for head in range(2)])

        def accumulate(at, rows, cols, allowed, d_query):
            bias_ref[:rows, :cols] = jnp.where(allowed, 0.0, neg_large)
            after = list(d_query)
            keys = [k_ref[pl.ds(at, rows), span] for span in lanes]
            eighth = [v_ref[pl.ds(at, rows), span] * jnp.asarray(0.125, bf16) for span in lanes]
            keys_t = [part.T for part in keys]
            stack = lambda parts: jnp.concatenate([part[:cols] for part in parts], axis=0)

            def begin(h):
                p, head = h // 2, h % 2
                return (
                    dot(keys[p], queries[p][head][:cols], NT),
                    dot(eighth[p], d_outs[p][head][:cols], NT),
                )

            def finish_pair(p, weights, d_scores):
                span = lanes[p]
                for head in range(2):
                    side = slice(head * HD, (head + 1) * HD)
                    h = 2 * p + head
                    after[h] = d_query[h] + dot(keys_t[p][side], d_scores[head])
                dv_ref[pl.ds(at, rows), span] += dot(
                    jnp.concatenate(weights, axis=1), stack(d_outs[p])
                )
                dk_ref[pl.ds(at, rows), span] += dot(
                    jnp.concatenate(d_scores, axis=1), stack(queries[p])
                )

            ready = begin(0)
            held = None
            weights, d_scores = [], []
            for h in range(2 * pairs):
                ahead = begin(h + 1) if h + 1 < 2 * pairs else None
                p, head = h // 2, h % 2
                scores = ready[0] * to_base2 - lses[p][head][:, :cols] + bias_ref[:rows, :cols]
                probs = jnp.exp2(scores)
                d_score = (probs * (ready[1] - inners[p][head][:, :cols])).astype(bf16)
                weights.append(probs.astype(bf16))
                d_scores.append(d_score)
                if held is not None:
                    finish_pair(*held)
                    held = None
                if head == 1:
                    held = (p, weights, d_scores)
                    weights, d_scores = [], []
                ready = ahead
            finish_pair(*held)
            return tuple(after)

        allowed = between((WINDOW, TILE), 0, own_low, own_high)
        zero = jnp.zeros((HD, TILE), f32)
        start = accumulate(window_at, WINDOW, TILE, allowed, (zero,) * (2 * pairs))
        start = tuple(jnp.concatenate([part, zero], axis=1) for part in start)
        first_key, trips = span_ref[t, 0], span_ref[t, 1]

        def one_step(j, d_query):
            at = pl.multiple_of(first_key + j * KEY_TILE, EDGE)
            allowed = between((KEY_TILE, 2 * TILE), at, key_low, key_high)
            return accumulate(at, KEY_TILE, 2 * TILE, allowed, d_query)

        d_query = lax.fori_loop(0, trips, one_step, start)
        for p, span in enumerate(lanes):
            pair = jnp.concatenate(d_query[2 * p : 2 * p + 2], axis=0).T
            for at, part in ((noisy_at, pair[:TILE]), (clean_at, pair[TILE:])):
                turned = turn(part, cos_ref[pl.ds(at, TILE), :], -sin_ref[pl.ds(at, TILE), :])
                out_ref[0, pl.ds(at, TILE), span] = turned.astype(bf16)
        return 0

    lax.fori_loop(0, TILES, one_tile, 0)
    step = KEY_ROWS // 9

    def finish(i, _):
        rows = pl.ds(pl.multiple_of(i * step, EDGE), step)
        for span in lanes:
            out_ref[1, rows, span] = turn(
                dk_ref[rows, span], cos_ref[rows, :], -sin_ref[rows, :]
            ).astype(bf16)
        out_ref[2, rows, :] = dv_ref[rows, :].astype(bf16)
        return 0

    lax.fori_loop(0, 9, finish, 0)

    def weight_rows(i, _):
        rows = pl.ds(pl.multiple_of(i * ROW_TILE, LANES), ROW_TILE)
        for c in range(3):
            grad_ref[c, rows, :] = dot(rows_ref[rows, :], out_ref[c]).astype(bf16)
        return 0

    if giving:
        for load in loads:
            load.wait()
        total = 0.0
        for c in range(3):
            total = total + dot(out_ref[c, :HALF, :], w_ref[c], NT) + dot(d2_ref[c], w2_ref[c], NT)
        give_ref[...] = total
    else:
        lax.fori_loop(0, rows_ref.shape[0] // ROW_TILE, weight_rows, 0)


def attend_backward(
    spans,
    clean_bounds,
    noisy_bounds,
    query,
    keys,
    values,
    attended,
    d_attended,
    lse,
    cosine,
    sine,
    rest,
):
    count, cols = query.shape
    vmem = pl.BlockSpec(memory_space=pltpu.VMEM)
    hbm = pl.BlockSpec(memory_space=pl.ANY)
    shape = jax.ShapeDtypeStruct
    giving = len(rest) > 1
    if giving:
        width = rest[1].shape[1]
        second = shape((HALF, width), f32)
        scratch = [
            pltpu.VMEM((3, HALF, cols), bf16),
            pltpu.VMEM(rest[1].shape, bf16),
            pltpu.VMEM(rest[2].shape, bf16),
            pltpu.SemaphoreType.DMA((5,)),
        ]
    else:
        second = shape((3, rest[0].shape[0], cols), bf16)
        scratch = []
    return pl.pallas_call(
        functools.partial(backward_kernel, giving),
        in_specs=[pl.BlockSpec(memory_space=pltpu.SMEM)]
        + [vmem] * 10
        + [hbm if giving else vmem] * len(rest),
        out_specs=[vmem] * 2,
        scratch_shapes=[
            pltpu.VMEM((count, cols), f32),
            pltpu.VMEM((count, cols), f32),
            pltpu.VMEM((max(KEY_TILE, WINDOW), 2 * TILE), f32),
        ]
        + scratch,
        out_shape=[shape((3, count, cols), bf16), second],
        name="attend_backward",
        cost_estimate=pl.CostEstimate(
            flops=36 * 10**9, bytes_accessed=36 * 10**6, transcendentals=6 * 10**6
        ),
    )(
        spans,
        clean_bounds,
        noisy_bounds,
        query,
        keys,
        values,
        attended,
        d_attended,
        lse,
        cosine,
        sine,
        *rest,
    )


PIECES = 16
MESH = pl.DeviceIdType.MESH


def flip(value, mask):
    result = value
    for b in range(mask.bit_length()):
        if mask >> b & 1:
            result = result + (1 << b) * (1 - 2 * ((value // (1 << b)) % 2))
    return result


class Exchange:
    def __init__(self, bits, count, rows, width, back=True):
        self.bits, self.count, self.rows, self.width = bits, count, rows, width
        self.back = back
        self.half, self.quarter, self.piece = rows // 2, rows // 4, rows // PIECES
        self.extra = list(range(4, bits))

    def slots(self):
        return 8 + 2 * (6 if self.back else 4) + (3 if self.extra else 0)

    def scratch(self):
        k, w = self.count, self.width
        cross = k if not self.back else 1
        shapes = [
            pltpu.VMEM((k, 2 - self.back, self.half, w), bf16),
            pltpu.VMEM((cross, self.half, w), bf16),
            pltpu.VMEM((cross, self.half, w), bf16),
            pltpu.VMEM((k, self.quarter, w), bf16),
            pltpu.VMEM((k, self.quarter, w), bf16),
            pltpu.VMEM((k, self.quarter, w), f32),
            pltpu.VMEM((k, 3, self.piece, w), bf16),
            pltpu.VMEM((k, 3, self.piece, w), bf16),
        ]
        lanes_of = (1, 0, 1, 3, 3, 1, 1) if self.back else (2, 1, 1, 3, 0, 0, 0)
        for lanes in [lanes for lanes in lanes_of if lanes]:
            shapes += [pltpu.SemaphoreType.DMA((k, lanes))] * 2
        if self.extra:
            n = len(self.extra)
            shapes += [pltpu.VMEM((k, 2 * n, self.piece, w), bf16)]
            shapes += [pltpu.SemaphoreType.DMA((k, n))] * 2
        return shapes

    def bind(self, place, part, refs):
        (self.a_in, self.b_out, self.b_in, self.c_out, self.c_in, self.keep) = refs[:6]
        self.d_out, self.d_in = refs[6:8]
        names = "acdefg" if self.back else "abcd"
        self.sems = {name: (refs[8 + 2 * i], refs[9 + 2 * i]) for i, name in enumerate(names)}
        if self.extra:
            at = 8 + 2 * len(names)
            self.x_buf, self.x_send, self.x_recv = refs[at : at + 3]
        self.place, self.part = place, part
        self.core, self.x, self.z = place % 2, (place // 2) % 2, (place // 4) % 4
        self.sibling = {"dp": flip(place, 1)}
        self.beside = {"dp": flip(place, 2)}
        self.across = {"mp": 1 - part}
        self.peers = [{"dp": flip(place, j << 2)} for j in range(1, 4)]
        self.partners = [self.sibling, self.beside, self.across] + self.peers
        self.partners += [{"dp": flip(place, 1 << b)} for b in self.extra]
        return self

    def greet(self):
        barrier = pltpu.get_barrier_semaphore()
        for partner in self.partners:
            pl.semaphore_signal(barrier, inc=1, device_id=partner, device_id_type=MESH)
        pl.semaphore_wait(barrier, len(self.partners))

    def copy(self, name, k, lane, source, target, device):
        out, into = self.sems[name]
        return pltpu.make_async_remote_copy(
            src_ref=source,
            dst_ref=target,
            send_sem=out.at[k, lane],
            recv_sem=into.at[k, lane],
            device_id=device,
            device_id_type=MESH,
        )

    def rows_at(self, start, size):
        return pl.ds(pl.multiple_of(start, PIECES), size)

    def copy_a(self, k, lane, grads):
        source = grads.at[k, self.rows_at((1 - self.core) * self.half, self.half)]
        return self.copy("a", k, lane, source, self.a_in.at[k, lane], self.sibling)

    def copy_b(self, k):
        return self.copy("b", k, 0, self.b_out.at[k], self.b_in.at[k], self.across)

    def copy_c(self, k):
        return self.copy("c", k, 0, self.c_out.at[k], self.c_in.at[k], self.beside)

    def copy_d(self, k, j):
        return self.copy("d", k, j, self.d_out.at[k, j], self.d_in.at[k, j], self.peers[j])

    def spot(self, change=0):
        start = self.core * self.half + self.x * self.quarter
        return self.rows_at(start + flip(self.z, change) * self.piece, self.piece)

    def copy_e(self, k, j, full):
        rows = full.at[k, self.spot()]
        return self.copy("e", k, j, rows, rows, self.peers[j])

    def copy_f(self, k, full):
        start = self.core * self.half + self.x * self.quarter
        rows = full.at[k, self.rows_at(start, self.quarter)]
        return self.copy("f", k, 0, rows, rows, self.beside)

    def copy_g(self, k, full):
        rows = full.at[k, self.rows_at(self.core * self.half, self.half)]
        return self.copy("g", k, 0, rows, rows, self.sibling)

    def start_a(self, k, lane, grads):
        self.copy_a(k, lane, grads).start()

    def stage_b(self, k, others):
        self.copy_a(k, 0, others).wait()
        mine = others[k, self.rows_at(self.core * self.half, self.half), :].astype(f32)
        self.b_out[k] = (mine + self.a_in[k, 0].astype(f32)).astype(bf16)
        self.copy_b(k).start()

    def stage_c(self, k, grads, crossed=None):
        lane = 0 if self.back else 1
        self.copy_a(k, lane, grads).wait()
        if not self.back:
            self.copy_b(k).wait()

        def total(which):
            inner = which * self.quarter
            rows = self.rows_at(inner, self.quarter)
            mine = grads[k, self.rows_at(self.core * self.half + inner, self.quarter), :]
            got = self.a_in[k, lane, rows, :].astype(f32)
            if not self.back:
                got = got + self.b_in[k, rows, :].astype(f32)
            elif crossed is not None:
                got = got + crossed(rows)
            return mine.astype(f32) + got

        self.c_out[k] = total(1 - self.x).astype(bf16)
        self.copy_c(k).start()
        self.keep[k] = total(self.x)

    def stage_d(self, k):
        self.copy_c(k).wait()
        for j in range(4):
            rows = self.rows_at(flip(self.z, j) * self.piece, self.piece)
            total = self.keep[k, rows, :] + self.c_in[k, rows, :].astype(f32)
            if j:
                self.d_out[k, j - 1] = total.astype(bf16)
                self.copy_d(k, j - 1).start()
            else:
                self.keep[k, rows, :] = total

    def gather_d(self, k):
        rows = self.rows_at(self.z * self.piece, self.piece)
        total = self.keep[k, rows, :]
        for j in range(3):
            self.copy_d(k, j).wait()
            total = total + self.d_in[k, j].astype(f32)
        for i, b in enumerate(self.extra):
            mine = self.x_buf.at[k, 2 * i]
            mine[...] = total.astype(bf16)
            swap = pltpu.make_async_remote_copy(
                src_ref=mine,
                dst_ref=self.x_buf.at[k, 2 * i + 1],
                send_sem=self.x_send.at[k, i],
                recv_sem=self.x_recv.at[k, i],
                device_id={"dp": flip(self.place, 1 << b)},
                device_id_type=MESH,
            )
            swap.start()
            swap.wait()
            total = total.astype(bf16).astype(f32) + self.x_buf[k, 2 * i + 1].astype(f32)
        return total.astype(bf16)

    def stage_e(self, k, full):
        full[k, self.spot(), :] = self.gather_d(k)
        for j in range(3):
            self.copy_e(k, j, full).start()

    def stage_f(self, k, full):
        for j in range(3):
            self.copy_e(k, j, full).wait()
        self.copy_f(k, full).start()

    def stage_g(self, k, full):
        self.copy_f(k, full).wait()
        self.copy_g(k, full).start()

    def stage_h(self, k, full):
        self.copy_g(k, full).wait()


def at_step(step, count, action):
    @pl.when(jnp.logical_and(step >= 0, step < count))
    def _():
        action(step)


def middle_kernel(exchanges, tiles, *refs):
    (
        x_ref,
        att_ref,
        att2_ref,
        wout_ref,
        wout2_ref,
        dy_ref,
        vectors_ref,
        bup_ref,
        up_mine,
        up_here,
        up_beside,
        down_mine,
        down_here,
        out_hbm,
        mid_hbm,
        datt_hbm,
        datt2_hbm,
        gout_ref,
        gout2_ref,
        gbup_ref,
        small_ref,
        pieces_ref,
        up_there,
        down_there,
        pass_up,
        pass_down,
        up_buf,
        down_buf,
        load_sem,
        n2_ref,
        total_ref,
        dn2_ref,
        act_ref,
        dpre_ref,
        n2_t,
        bup_other,
        bias_sem,
        out_ref,
        mid_ref,
        datt_ref,
        datt2_ref,
        store_sem,
        down_grad,
        up_grad,
        *rest,
    ) = refs
    place, part = lax.axis_index("dp"), lax.axis_index("mp")
    ex = exchanges[0].bind(place, part, rest)
    ex_up = exchanges[1].bind(place, part, rest[exchanges[0].slots() :])
    sides = ((ex, down_grad), (ex_up, up_grad))
    core = ex.core
    count = tiles // 2
    rows_all = x_ref.shape[0]
    blocks = rows_all // ROW_TILE
    width = x_ref.shape[1]
    lanes = width // 2

    def which(i):
        other = jnp.logical_or(i == 0, jnp.logical_and(i % 2 == 1, i < tiles - 1))
        mine = jnp.where(i == tiles - 1, count - 1, i // 2 - 1)
        return other, jnp.where(other, (i + 1) // 2, mine)

    quarter = width // 4
    strip = HIDDEN_TILE // 2
    held = 2 * core + ex.x
    kept = 2 * core + 1 - ex.x

    def load_up(i, source, h):
        target = up_buf.at[i % 2, h * quarter : (h + 1) * quarter]
        return pltpu.make_async_copy(source, target, load_sem.at[i % 2, h])

    def load_down(i, source, h):
        target = down_buf.at[i % 2, h * strip : (h + 1) * strip]
        return pltpu.make_async_copy(source, target, load_sem.at[i % 2, 4 + h])

    def hand_up(k, part_of):
        cols = pl.ds(pl.multiple_of(k * HIDDEN_TILE, HIDDEN_TILE), HIDDEN_TILE)
        side = ex.x if part_of == 0 else 1 - ex.x
        rows = pl.ds(pl.multiple_of(side * quarter, EDGE), quarter)
        return pltpu.make_async_remote_copy(
            src_ref=(up_here, up_beside)[part_of].at[:, cols],
            dst_ref=up_there.at[k, rows],
            send_sem=pass_up.at[k, 2 * part_of],
            recv_sem=pass_up.at[k, 2 * part_of + 1],
            device_id=ex.sibling,
            device_id_type=MESH,
        )

    def hand_down(b):
        return pltpu.make_async_remote_copy(
            src_ref=down_here.at[strip_rows(b)],
            dst_ref=down_there.at[b],
            send_sem=pass_down.at[b, 0],
            recv_sem=pass_down.at[b, 1],
            device_id=ex.sibling,
            device_id_type=MESH,
        )

    def strip_rows(b):
        return pl.ds(pl.multiple_of(b * strip, strip), strip)

    def start_loads(i):
        other, k = which(i)
        mine = jnp.logical_not(other)
        cols = pl.ds(pl.multiple_of(k * HIDDEN_TILE, HIDDEN_TILE), HIDDEN_TILE)

        @pl.when(other)
        def _():
            hand_up(k, 0).wait()
            hand_up(k, 1).wait()

        for h in range(4):

            @pl.when(mine)
            def _():
                load_up(i, up_mine.at[h * quarter : (h + 1) * quarter, cols], h).start()

            @pl.when(jnp.logical_and(other, held == h))
            def _():
                load_up(i, up_here.at[:, cols], h).start()

            @pl.when(jnp.logical_and(other, kept == h))
            def _():
                load_up(i, up_beside.at[:, cols], h).start()

            @pl.when(jnp.logical_and(other, core != h // 2))
            def _():
                rows = slice(h % 2 * quarter, (h % 2 + 1) * quarter)
                load_up(i, up_there.at[k, rows], h).start()

        for h in range(2):
            b = 2 * k + h
            inner = b % count

            @pl.when(mine)
            def _():
                load_down(i, down_mine.at[strip_rows(b), :], h).start()

            @pl.when(jnp.logical_and(other, core == b // count))
            def _():
                load_down(i, down_here.at[strip_rows(inner), :], h).start()

            @pl.when(jnp.logical_and(other, core != b // count))
            def _():
                hand_down(inner).wait_recv()
                load_down(i, down_there.at[inner], h).start()

    def wait_loads(i):
        for h in range(4):
            load_up(i, up_mine.at[:quarter, :HIDDEN_TILE], h).wait()
        for h in range(2):
            load_down(i, down_mine.at[:strip, :], h).wait()

    ex.greet()
    bias_swap = pltpu.make_async_remote_copy(
        src_ref=bup_ref,
        dst_ref=bup_other,
        send_sem=bias_sem.at[0],
        recv_sem=bias_sem.at[1],
        device_id=ex.across,
        device_id_type=MESH,
    )
    bias_swap.start()

    def hand(k, _):
        hand_up(k, 0).start()
        hand_up(k, 1).start()
        hand_down(k).start()
        return 0

    lax.fori_loop(0, count, hand, 0)

    def prologue(n, _):
        prologue_block(2 * n)
        prologue_block(2 * n + 1)
        return 0

    def prologue_block(r):
        rows = pl.ds(pl.multiple_of(r * ROW_TILE, ROW_TILE), ROW_TILE)
        branch = dot(att_ref[rows, :], wout_ref[...]) + dot(att2_ref[rows, :], wout2_ref[...])
        mid = x_ref[rows, :].astype(f32) + branch
        mid_ref[rows, :] = mid
        unit = normal(mid)[0]
        n2_ref[rows, :] = (unit * vectors_ref[2:3, :] + vectors_ref[3:4, :]).astype(bf16)
        total_ref[rows, :] = mid + vectors_ref[4:5, :]
        dn2_ref[rows, :] = jnp.zeros((ROW_TILE, width), f32)

    lax.fori_loop(0, blocks // 2, prologue, 0)
    start_loads(0)
    for c in range(width // LANES):
        cols = slice(c * LANES, (c + 1) * LANES)
        n2_t[cols, :] = n2_ref[:, cols].T
    n2_t[width:, :] = jnp.ones((PIECES, rows_all), bf16)
    bias_swap.wait()

    def tile(i):
        other, k = which(i)
        slot = i % 2
        wait_loads(i)

        @pl.when(i + 1 < tiles)
        def _():
            start_loads(i + 1)

        up, down = up_buf.at[slot], down_buf.at[slot]
        bias_at = jnp.where(other, k, count + k)
        bias = jnp.where(other, bup_other[k], bup_ref[k])
        linear = 0.7978845608028654
        cubic = linear * 0.044715
        for r in range(blocks):
            rows = slice(r * ROW_TILE, (r + 1) * ROW_TILE)
            pre = dot(n2_ref[rows, :], up[...]) + bias
            d_act = dot(dy_ref[rows, :], down[...], NT)
            square = pre * pre
            bend = jnp.tanh(pre * (square * cubic + linear))
            gate = 0.5 * bend + 0.5
            full_act = pre * gate
            slope = gate + (full_act - full_act * gate) * (square * (6.0 * cubic) + 2.0 * linear)
            act_ref[rows, :] = full_act.astype(bf16)
            dpre_ref[rows, :] = (d_act * slope).astype(bf16)
        total_ref[...] += dot(act_ref[...], down[...])
        dn2_ref[...] += dot(dpre_ref[...], up[...], NT)
        down_grad[k] = dot(act_ref[...].T, dy_ref[...]).astype(bf16)

        def start(lane):
            for side, grad in sides:
                side.start_a(k, lane, grad)

        by_rows = dot(n2_t[...], dpre_ref[...])
        up_grad[k] = by_rows[:width].astype(bf16)
        gbup_ref[bias_at] = by_rows[width : width + 1]
        pl.when(other)(functools.partial(start, 0))
        pl.when(jnp.logical_not(other))(functools.partial(start, 1))

    def each(k, when, action):
        @pl.when(jnp.logical_and(when, jnp.logical_and(k >= 0, k < count)))
        def _():
            for n, (side, grad) in enumerate(sides):
                action(n, side, grad, k)

    def stage_b(n, side, grad, k):
        side.stage_b(k, grad)

    def stage_c(n, side, grad, k):
        side.stage_c(k, grad)

    def stage_d(n, side, grad, k):
        side.stage_d(k)

    def arrive(n, side, grad, k):
        piece = side.gather_d(k)
        if n == 0:
            pieces_ref[k] = piece
        else:
            for c in range(width // HIDDEN_TILE):
                cols = slice(c * HIDDEN_TILE, (c + 1) * HIDDEN_TILE)
                pieces_ref[count + k, :, cols] = piece[c * PIECES : (c + 1) * PIECES]

    def steps(i):
        even = i % 2 == 0
        odd = jnp.logical_not(even)
        each((i - 5) // 2, odd, arrive)
        each((i - 4) // 2, even, stage_d)
        each((i - 3) // 2, odd, stage_c)
        each(i // 2, even, stage_b)

    def epilogue(r, _):
        rows = pl.ds(pl.multiple_of(r * ROW_TILE, ROW_TILE), ROW_TILE)
        out_ref[rows, :] = total_ref[rows, :].astype(bf16)
        unit, scale = normal(mid_ref[rows, :])
        d_rows = dn2_ref[rows, :]
        dy = dy_ref[rows, :].astype(f32)
        lean = d_rows * vectors_ref[2:3, :]
        d_mid = dy + scale * (
            lean
            - jnp.mean(lean, axis=-1, keepdims=True)
            - unit * jnp.mean(lean * unit, axis=-1, keepdims=True)
        )
        mid_ref[rows, :] = d_mid
        d_branch = d_mid.astype(bf16)
        n2_ref[rows, :] = d_branch
        datt_ref[rows, :] = dot(d_branch, wout_ref[...], NT).astype(bf16)
        datt2_ref[rows, :] = dot(d_branch, wout2_ref[...], NT).astype(bf16)
        add = lambda values: jnp.sum(values, axis=0, keepdims=True)
        small_ref[0:1, :] += add(d_rows * unit)
        small_ref[1:2, :] += add(d_rows)
        small_ref[2:3, :] += add(dy)
        return 0

    def out_grads():
        for source, target in ((att_ref, gout_ref), (att2_ref, gout2_ref)):
            grad = dot(source[...].T, n2_ref[...]).astype(bf16)
            for a in range(wout_ref.shape[0] // LANES):
                for b in range(2):
                    rows = slice(a * LANES, (a + 1) * LANES)
                    cols = slice(b * lanes, (b + 1) * lanes)
                    spread = slice(a * lanes, (a + 1) * lanes)
                    target[b * LANES : (b + 1) * LANES, spread] = grad[rows, cols]

    def main(i, _):
        pl.when(i < tiles)(functools.partial(tile, i))

        @pl.when(jnp.logical_and(i >= tiles, i < tiles + 2))
        def _():
            first = (i - tiles) * (blocks // 2)
            lax.fori_loop(first, first + blocks // 2, epilogue, 0)

        @pl.when(i == tiles + 2)
        def _():
            for store in stores:
                store.start()
            out_grads()

        steps(i)
        return 0

    small_ref[...] = jnp.zeros_like(small_ref)
    stores = [
        pltpu.make_async_copy(source, target, store_sem.at[n])
        for n, (source, target) in enumerate(
            (
                (datt2_ref, datt2_hbm),
                (out_ref, out_hbm),
                (mid_ref, mid_hbm),
                (datt_ref, datt_hbm),
            )
        )
    ]
    lax.fori_loop(0, tiles + 4, main, 0)
    for store in stores:
        store.wait()

    def handed(slot, _):
        hand_down(slot).wait_send()
        return 0

    lax.fori_loop(0, count, handed, 0)


def middle(bits, x, att, att2, wout, wout2, dy, vectors, bup, ups, downs):
    rows, width = x.shape
    hidden = ups[0].shape[1]
    count = hidden // HIDDEN_TILE
    tiles = 2 * count
    exchanges = (
        Exchange(bits, count, HIDDEN_TILE, width, False),
        Exchange(bits, count, width, HIDDEN_TILE, False),
    )
    vmem = pl.BlockSpec(memory_space=pltpu.VMEM)
    hbm = pl.BlockSpec(memory_space=pl.ANY)
    shape = jax.ShapeDtypeStruct
    depth = wout.shape[0]
    return pl.pallas_call(
        functools.partial(middle_kernel, exchanges, tiles),
        in_specs=[vmem] * 8 + [hbm] * 5,
        out_specs=[hbm] * 4 + [vmem] * 5,
        out_shape=[
            shape((rows, width), bf16),
            shape((rows, width), f32),
            shape(att.shape, bf16),
            shape(att2.shape, bf16),
            shape((2 * LANES, depth // LANES * width // 2), bf16),
            shape((2 * LANES, depth // LANES * width // 2), bf16),
            shape((tiles, 1, HIDDEN_TILE), f32),
            shape((8, width), f32),
            shape((2 * count, PIECES, width), bf16),
        ],
        scratch_shapes=[
            pltpu.VMEM((count, width // 2, HIDDEN_TILE), bf16),
            pltpu.VMEM((count, HIDDEN_TILE // 2, width), bf16),
            pltpu.SemaphoreType.DMA((count, 4)),
            pltpu.SemaphoreType.DMA((count, 2)),
            pltpu.VMEM((2, width, HIDDEN_TILE), bf16),
            pltpu.VMEM((2, HIDDEN_TILE, width), bf16),
            pltpu.SemaphoreType.DMA((2, 6)),
            pltpu.VMEM((rows, width), bf16),
            pltpu.VMEM((rows, width), f32),
            pltpu.VMEM((rows, width), f32),
            pltpu.VMEM((rows, HIDDEN_TILE), bf16),
            pltpu.VMEM((rows, HIDDEN_TILE), bf16),
            pltpu.VMEM((width + PIECES, rows), bf16),
            pltpu.VMEM(bup.shape, f32),
            pltpu.SemaphoreType.DMA((2,)),
            pltpu.VMEM((rows, width), bf16),
            pltpu.VMEM((rows, width), f32),
            pltpu.VMEM(att.shape, bf16),
            pltpu.VMEM(att2.shape, bf16),
            pltpu.SemaphoreType.DMA((4,)),
            pltpu.VMEM((count, HIDDEN_TILE, width), bf16),
            pltpu.VMEM((count, width, HIDDEN_TILE), bf16),
        ]
        + exchanges[0].scratch()
        + exchanges[1].scratch(),
        compiler_params=pltpu.CompilerParams(
            collective_id=0, has_side_effects=True, vmem_limit_bytes=67043328
        ),
        name="middle",
        cost_estimate=pl.CostEstimate(
            flops=60 * 10**9, bytes_accessed=40 * 10**6, transcendentals=4 * 10**6
        ),
    )(x, att, att2, wout, wout2, dy, vectors, bup, *ups, *downs)


def leave_kernel(exchange, *refs):
    (
        rows_hbm,
        mine_out_ref,
        crossed_ref,
        crossed_out_ref,
        d_hbm,
        d2_hbm,
        w_hbm,
        w2_hbm,
        tokens_ref,
        context_ref,
        given_ref,
        vectors_ref,
        dmid_hbm,
        small_ref,
        small2_ref,
        gqkv_ref,
        gout_ref,
        back_ref,
        sums_ref,
        full_ref,
        out_buf,
        rows_t_ref,
        d_ref,
        d2_ref,
        w_ref,
        w2_ref,
        dmid_ref,
        load_sem,
        rows_ref,
        give_ref,
        take_ref,
        swap_sem,
        norm_ref,
        *rest,
    ) = refs
    early, late, rest = rest[:4], rest[4:8], rest[8:]
    place, part = lax.axis_index("dp"), lax.axis_index("mp")
    ex = exchange.bind(place, part, rest)
    count, bits = ex.count, ex.bits
    loads = [
        pltpu.make_async_copy(source, target, load_sem.at[n])
        for n, (source, target) in enumerate(
            (
                (d_hbm, d_ref),
                (rows_hbm, rows_t_ref),
                (w_hbm, w_ref),
                (w2_hbm, w2_ref),
                (d2_hbm, d2_ref),
                (dmid_hbm, dmid_ref),
            )
        )
    ]
    for load in loads:
        load.start()
    near_id = part * 4 + place % 4
    near = [
        {"dp": flip(place, j % 4), "mp": part if j < 4 else 1 - part} for j in range(1, 8)
    ]
    ex.partners += [near[j - 1] for j in (3, 5, 6, 7)]
    ex.greet()

    lanes = d_ref.shape[2]
    split = mine_out_ref.shape[1] // lanes
    for r in range(split):
        cols = slice(r * lanes, (r + 1) * lanes)
        total = mine_out_ref[:, cols].astype(f32) + crossed_out_ref[:, cols].astype(f32)
        out_buf[r] = total.astype(bf16)
        ex.start_a(r, 0, out_buf)
    step = HALF + 2 * EDGE

    def back_rows(n):
        start = CLEAN_OWN + n * (KEY_ROWS - step - CLEAN_OWN)
        rows = pl.ds(pl.multiple_of(start, EDGE), step)
        total = 0.0
        for grads, weights in ((d_ref, w_ref), (d2_ref, w2_ref)):
            for c in range(3):
                total = total + dot(grads[c, rows, :], weights[c], NT)
        rows_ref[rows, :] = total

    def grad_chunk(c):
        for r in range(split):
            rows = slice(r * ROW_TILE, (r + 1) * ROW_TILE)
            k = (c + 1) * split + r
            out_buf[k] = dot(rows_t_ref[rows, :], d_ref[c]).astype(bf16)
            ex.start_a(k, 0, out_buf)

    def stage_c(k):
        @pl.when(k >= split)
        def _():
            ex.stage_c(k, out_buf, lambda rows: crossed_ref[k - split, rows, :].astype(f32))

        @pl.when(k < split)
        def _():
            ex.stage_c(k, out_buf)

    def arrive(k):
        ex.stage_h(k, full_ref)

        @pl.when(k < split)
        def _():
            rows = pl.ds(pl.multiple_of(k * LANES, LANES), LANES)
            for b in range(2):
                piece = full_ref[k, b * LANES : (b + 1) * LANES, :]
                gout_ref[rows, b * lanes : (b + 1) * lanes] = piece

        @pl.when(k >= split)
        def _():
            n = k - split
            rows = pl.ds(pl.multiple_of(n % split * ROW_TILE, ROW_TILE), ROW_TILE)
            gqkv_ref[n // split, rows, :] = full_ref[k]

    def group(g, action):
        @pl.when(jnp.logical_and(g >= 0, g < count // split))
        def _():
            lax.fori_loop(g * split, (g + 1) * split, lambda k, _: (action(k), 0)[1], 0)

    def steps(i):
        group(i - 5, arrive)
        group(i - 4, lambda k: ex.stage_g(k, full_ref))
        group(i - 3, lambda k: ex.stage_f(k, full_ref))
        group(i - 2, lambda k: ex.stage_e(k, full_ref))
        group(i - 1, lambda k: ex.stage_d(k))
        group(i, stage_c)

    width = tokens_ref.shape[1]

    def swap(rows, lane):
        return pltpu.make_async_remote_copy(
            src_ref=give_ref.at[rows],
            dst_ref=take_ref.at[rows],
            send_sem=swap_sem.at[lane, 0],
            recv_sem=swap_sem.at[lane, 1],
            device_id=ex.across,
            device_id_type=MESH,
        )

    def sums_of(d_rows, units):
        add = lambda values: jnp.sum(values, axis=0, keepdims=True)
        norm_ref[0:1, :] += add(d_rows * units)
        norm_ref[1:2, :] += add(d_rows)

    main = slice(0, HALF)
    edges = slice(HALF, HALF + 2 * EDGE)
    parts = tokens_ref.shape[0] // TILE
    lead = small_ref.shape[0] - 2
    bias = lead - 3
    norm_ref[...] = jnp.zeros_like(norm_ref)
    for load in loads[:2]:
        load.wait()

    def own_at(b):
        start = jnp.where(b < TILES, NOISY_OWN + b * TILE, CLEAN_OWN + (b - TILES) * TILE)
        return pl.ds(pl.multiple_of(start, EDGE), TILE)

    def tokens_at(b):
        return pl.ds(pl.multiple_of(b * TILE, TILE), TILE)

    def ready():
        for load in loads[2:5]:
            load.wait()

    give_ref[main, :] = given_ref[...].astype(bf16)
    swap(main, 0).start()

    def give_edges():
        side = rows_ref[NOISY_BASE:NOISY_OWN, :] + rows_ref[NOISY_OWN + HALF :, :]
        after = rows_ref[2 * HALF : NOISY_BASE, :]
        give_ref[HALF : HALF + EDGE, :] = after.astype(bf16)
        give_ref[HALF + EDGE :, :] = side.astype(bf16)
        swap(edges, 1).start()
        sums_of(after, normal(context_ref[:EDGE, :].astype(f32))[0])
        sums_of(side, normal(context_ref[HALF:, :].astype(f32))[0])

    def tell_near():
        def context_sums(b, _):
            rows = tokens_at(b)
            sums_of(given_ref[rows, :], normal(context_ref[rows, :].astype(f32))[0])
            return 0

        lax.fori_loop(0, HALF // TILE, context_sums, 0)

        def own_sums(b, _):
            sums_of(rows_ref[own_at(b), :], normal(tokens_ref[tokens_at(b), :].astype(f32))[0])
            return 0

        lax.fori_loop(0, parts, own_sums, 0)
        mine = late[0].at[near_id]
        mine[...] = norm_ref[...]
        start_near(late)

    def near_copy(group, j, at):
        near_ref, _, near_sem, _ = group
        return pltpu.make_async_remote_copy(
            src_ref=near_ref.at[at],
            dst_ref=near_ref.at[at],
            send_sem=near_sem.at[j, 0],
            recv_sem=near_sem.at[j, 1],
            device_id=near[j - 1],
            device_id_type=MESH,
        )

    def far_copy(group, j, at):
        _, far_ref, _, far_sem = group
        return pltpu.make_async_remote_copy(
            src_ref=far_ref.at[at],
            dst_ref=far_ref.at[at],
            send_sem=far_sem.at[j, 0],
            recv_sem=far_sem.at[j, 1],
            device_id=ex.peers[j - 1],
            device_id_type=MESH,
        )

    def start_near(group):
        for j in range(1, 8):
            near_copy(group, j, near_id).start()

    def near_sum(group, places):
        total = group[0][places[0]]
        for at in places[1:]:
            total = total + group[0][at]
        return total

    def wait_near(group):
        for j in range(1, 8):
            near_copy(group, j, near_id).wait_send()
            came = (part + j // 4) % 2 * 4 + flip(place % 4, j % 4)
            near_copy(group, j, came).wait_recv()

    def start_far(group):
        for j in range(1, 4):
            far_copy(group, j, ex.z).start()

    def far_sum(group):
        far_ref, far_sem = group[1], group[3]
        for j in range(1, 4):
            far_copy(group, j, ex.z).wait_send()
            far_copy(group, j, flip(ex.z, j)).wait_recv()
        total = far_ref[0]
        for j in range(1, 4):
            total = total + far_ref[j]
        for i, b in enumerate(ex.extra):
            far_ref[4 + 2 * i] = total
            trade = pltpu.make_async_remote_copy(
                src_ref=far_ref.at[4 + 2 * i],
                dst_ref=far_ref.at[5 + 2 * i],
                send_sem=far_sem.at[4 + i, 0],
                recv_sem=far_sem.at[4 + i, 1],
                device_id={"dp": flip(place, 1 << b)},
                device_id_type=MESH,
            )
            trade.start()
            trade.wait()
            total = total + far_ref[5 + 2 * i]
        return total

    def early_near():
        mine = early[0].at[near_id]
        mine[:lead, :] = small_ref[:lead, :]
        mine[lead : lead + bias, :] = small2_ref[:bias, :]
        mine[lead + bias :, :] = jnp.zeros((16 - lead - bias, width), f32)
        start_near(early)

    def early_far():
        wait_near(early)
        spot = early[1].at[ex.z]
        spot[...] = near_sum(early, range(8))
        plane = near_sum(early, [part * 4 + j for j in range(4)])
        other = near_sum(early, [(1 - part) * 4 + j for j in range(4)])
        spot[:bias, :] = plane[:bias] + other[lead : lead + bias]
        start_far(early)

    def early_end():
        sums_ref[...] = far_sum(early)

    def late_far():
        wait_near(late)
        late[1][ex.z] = near_sum(late, range(8))
        start_far(late)

    def late_end():
        sums_ref[lead : lead + 2, :] = far_sum(late)[:2]

    def take_back():
        loads[5].wait()
        swap(main, 0).wait()
        swap(edges, 1).wait()
        clean = slice(CLEAN_OWN, CLEAN_OWN + HALF)
        rows_ref[clean, :] += take_ref[main, :].astype(f32)
        begin = slice(CLEAN_OWN, CLEAN_OWN + EDGE)
        rows_ref[begin, :] += take_ref[HALF : HALF + EDGE, :].astype(f32)
        edge = pl.ds(pl.multiple_of(NOISY_OWN + (1 - part) * (HALF - EDGE), EDGE), EDGE)
        rows_ref[edge, :] += take_ref[HALF + EDGE :, :].astype(f32)

    def norm_back(b):
        rows = tokens_at(b)
        unit, scale = normal(tokens_ref[rows, :].astype(f32))
        lean = rows_ref[own_at(b), :] * vectors_ref[0:1, :]
        back_ref[rows, :] = dmid_ref[rows, :] + scale * (
            lean
            - jnp.mean(lean, axis=-1, keepdims=True)
            - unit * jnp.mean(lean * unit, axis=-1, keepdims=True)
        )

    def middle_step():
        take_back()
        early_far()

    def last_step():
        late_far()
        early_end()

    groups = count // split - 1
    actions = {
        0: early_near,
        groups + 1: give_edges,
        groups + 2: tell_near,
        groups + 3: middle_step,
        groups + 6: last_step,
    }
    begin_back = groups + 4

    def phase(p, _):
        @pl.when(p < groups)
        def _():
            grad_chunk(p)

        pl.when(p == groups)(ready)

        @pl.when(jnp.logical_and(p >= groups, p < groups + 2))
        def _():
            back_rows(p - groups)

        for n, action in actions.items():
            pl.when(p == n)(action)
        block = 2 * (p - begin_back)

        @pl.when(jnp.logical_and(block >= 0, block < parts))
        def _():
            lax.fori_loop(block, block + 2, lambda b, _: (norm_back(b), 0)[1], 0)

        pl.when(block == parts)(late_end)
        steps(p)
        return 0

    lax.fori_loop(0, begin_back + parts // 2 + 1, phase, 0)


def leave(bits, rows_t, mine, crossed, d_fields, weights, tokens, context, given, vectors, d_mid, small, small2):
    rows, cols = ROW_TILE, d_fields[0].shape[2]
    total = mine.shape[1] // cols + crossed[0].shape[0]
    exchange = Exchange(bits, total, rows, cols)
    count, width = tokens.shape
    vmem = pl.BlockSpec(memory_space=pltpu.VMEM)
    hbm = pl.BlockSpec(memory_space=pl.ANY)
    shape = jax.ShapeDtypeStruct
    return pl.pallas_call(
        functools.partial(leave_kernel, exchange),
        in_specs=[hbm] + [vmem] * 3 + [hbm] * 4 + [vmem] * 4 + [hbm] + [vmem] * 2,
        out_specs=[vmem] * 4,
        out_shape=[
            shape(weights[0].shape, bf16),
            shape((d_fields[0].shape[2], width), bf16),
            shape((count, width), f32),
            shape((16, width), f32),
        ],
        scratch_shapes=[
            pltpu.VMEM((total, rows, cols), bf16),
            pltpu.VMEM((total, rows, cols), bf16),
            pltpu.VMEM(rows_t.shape, bf16),
            pltpu.VMEM(d_fields[0].shape, bf16),
            pltpu.VMEM(d_fields[1].shape, bf16),
            pltpu.VMEM(weights[0].shape, bf16),
            pltpu.VMEM(weights[1].shape, bf16),
            pltpu.VMEM(d_mid.shape, f32),
            pltpu.SemaphoreType.DMA((6,)),
            pltpu.VMEM((KEY_ROWS, width), f32),
            pltpu.VMEM((HALF + 2 * EDGE, width), bf16),
            pltpu.VMEM((HALF + 2 * EDGE, width), bf16),
            pltpu.SemaphoreType.DMA((2, 2)),
            pltpu.VMEM((8, width), f32),
        ]
        + [
            spec
            for depth in (16, 8)
            for spec in (
                pltpu.VMEM((8, depth, width), f32),
                pltpu.VMEM((4 + 2 * len(exchange.extra), depth, width), f32),
                pltpu.SemaphoreType.DMA((8, 2)),
                pltpu.SemaphoreType.DMA((4 + len(exchange.extra), 2)),
            )
        ]
        + exchange.scratch(),
        compiler_params=pltpu.CompilerParams(
            collective_id=1, has_side_effects=True, vmem_limit_bytes=67043328
        ),
        name="leave",
        cost_estimate=pl.CostEstimate(
            flops=40 * 10**9, bytes_accessed=40 * 10**6, transcendentals=0
        ),
    )(
        rows_t, mine, *crossed, *d_fields, *weights, tokens, context, given, vectors, d_mid, small, small2
    )


def assemble_kernel(core_ref, down_mine, up_mine, down_got, up_got, down_ref, up_ref):
    core = core_ref[0]
    block = down_mine.shape[1]
    lanes = up_ref.shape[1]
    parts = down_mine.shape[2] // lanes
    deep = block * parts
    for side, down, up in ((core, down_mine, up_mine), (1 - core, down_got, up_got)):
        rows = pl.ds(pl.multiple_of(side * block, block), block)
        down_ref[rows, :] = down[0].astype(f32)
        for n in range(block // PIECES):
            for c in range(parts):
                at = side * deep + (n * parts + c) * PIECES
                rows = pl.ds(pl.multiple_of(at, PIECES), PIECES)
                piece = up[0, n * PIECES : (n + 1) * PIECES, c * lanes : (c + 1) * lanes]
                up_ref[rows, :] = piece.astype(f32)


def assemble(core, gathered, moved):
    tiles, half, width = gathered.shape
    count = tiles // 2
    down_spec = pl.BlockSpec((1, half, width), lambda k, c: (k, 0, 0))
    up_spec = pl.BlockSpec((1, half, width), lambda k, c: (count + k, 0, 0))
    hidden = count * 2 * half
    return pl.pallas_call(
        assemble_kernel,
        grid_spec=pltpu.PrefetchScalarGridSpec(
            num_scalar_prefetch=1,
            grid=(count,),
            in_specs=[down_spec, up_spec, down_spec, up_spec],
            out_specs=[
                pl.BlockSpec((2 * half, width), lambda k, c: (k, 0)),
                pl.BlockSpec((width, 2 * half), lambda k, c: (0, k)),
            ],
        ),
        out_shape=[
            jax.ShapeDtypeStruct((hidden, width), f32),
            jax.ShapeDtypeStruct((width, hidden), f32),
        ],
        name="assemble",
        cost_estimate=pl.CostEstimate(
            flops=10**6, bytes_accessed=14 * 10**6, transcendentals=0
        ),
    )(core, gathered, gathered, moved, moved)


def key_layout(seq_lengths, block_len, part):
    index = jnp.arange(KEY_ROWS, dtype=jnp.int32)
    own = part * HALF
    token = jnp.where(
        index < NOISY_BASE, index + (own - HALF), index - NOISY_BASE + (own - EDGE)
    )
    ends = jnp.cumsum(seq_lengths)
    passed = token[:, None] >= ends[None, :]
    starts = jnp.sum(jnp.where(passed, seq_lengths[None, :], 0), axis=1)
    lengths_here = jnp.where(passed, 0, ends[None, :])
    stops = jnp.min(jnp.where(passed, TOK_DEV, lengths_here), axis=1)
    positions = token - starts
    block_start = starts + positions // block_len * block_len
    block_stop = jnp.minimum(block_start + block_len, stops)
    mine = slice(CLEAN_OWN, CLEAN_OWN + HALF)
    low, start, stop = starts[mine], block_start[mine], block_stop[mine]
    to_clean = own - HALF
    tiles = lambda column: column.reshape(TILES, 1, TILE)
    clean_bounds = jnp.concatenate(
        [
            jnp.concatenate([tiles(low - to_clean), tiles(low - to_clean)], axis=2),
            jnp.concatenate([tiles(start - to_clean), tiles(stop - to_clean)], axis=2),
        ],
        axis=1,
    )
    to_window = own - EDGE + TILE * jnp.arange(TILES, dtype=jnp.int32)[:, None, None]
    noisy_bounds = jnp.concatenate(
        [tiles(start) - to_window, tiles(stop) - to_window], axis=1
    )
    first = jnp.min(clean_bounds[:, 0], axis=1) // EDGE * EDGE
    last = jnp.max(clean_bounds[:, 1], axis=1)
    trips = (last - first + KEY_TILE - 1) // KEY_TILE
    spans = jnp.stack([first, trips], axis=1)
    lane = jnp.arange(LANES, dtype=jnp.int32)
    frequency = jnp.exp(
        (lane % (HD // 2)).astype(f32) * (-math.log(10000.0) / (HD // 2))
    )
    angles = positions.astype(f32)[:, None] * frequency[None, :]
    sign = jnp.where(lane % HD < HD // 2, -1.0, 1.0)
    return spans, clean_bounds, noisy_bounds, jnp.cos(angles), jnp.sin(angles) * sign


def in_order(bit, mine, theirs, axis=0):
    order = bit == 0
    return jnp.concatenate(
        [jnp.where(order, mine, theirs), jnp.where(order, theirs, mine)], axis=axis
    )


def tie(first, second):
    return lax.optimization_barrier((first, second))


def local(
    dp_size,
    tokens,
    lengths,
    block_size,
    cotangent,
    ln1_gain,
    ln1_bias,
    w_qkv,
    w_out,
    ln2_gain,
    ln2_bias,
    w_up,
    b_up,
    w_down,
    b_down,
):
    width = tokens.shape[2]
    part = lax.axis_index("mp")
    place = lax.axis_index("dp")
    bits = dp_size.bit_length() - 1
    core = place & 1

    def across(array):
        return lax.ppermute(array, "mp", [(0, 1), (1, 0)])

    def sibling(array):
        return lax.ppermute(array, "dp", [(i, i ^ 1) for i in range(dp_size)])

    def beside(array):
        return lax.ppermute(array, "dp", [(i, i ^ 2) for i in range(dp_size)])

    edge = jnp.where(part == 0, tokens[0, HALF - EDGE :], tokens[0, :EDGE])
    context = across(jnp.concatenate([tokens[1], edge], axis=0))
    qkv_mine = w_qkv.transpose(1, 0, 2)
    side = (place >> 1) & 1

    def quarter_of(array, axis=0):
        size = array.shape[axis] // 4
        return lax.dynamic_slice_in_dim(array, (2 * core + side) * size, size, axis)

    def half_of(array):
        size = array.shape[0] // 2
        return lax.dynamic_slice_in_dim(array, core * size, size, 0)

    quarters = [quarter_of(qkv_mine, 1), quarter_of(w_up), half_of(w_down), half_of(w_out)]
    layout = key_layout(lengths[0], block_size[0], part)
    vectors = jnp.stack([ln1_gain, ln1_bias, ln2_gain, ln2_bias, b_down])
    context, (quarters, layout, vectors) = tie(context, (quarters, layout, vectors))
    qkv_here, up_here, down_here, out_here = [across(piece) for piece in quarters]

    spans, clean_bounds, noisy_bounds, cosine, sine = layout
    normed1, normed1_t, *fields = enter(tokens, context, vectors, qkv_mine, cosine, sine)
    qkv_here, fields = tie(qkv_here, fields)
    qkv_beside = beside(qkv_here)
    mine = [*fields, *attend_forward(spans, clean_bounds, noisy_bounds, *fields)]
    (qkv_here, qkv_beside, up_here), _ = tie((qkv_here, qkv_beside, up_here), mine[3])
    qkv_half = in_order(side, qkv_here, qkv_beside, axis=1)
    qkv_other = in_order(core, qkv_half, sibling(qkv_half), axis=1)
    up_beside = beside(up_here)
    fields = project(normed1, qkv_other, cosine, sine)
    other = [*fields, *attend_forward(spans, clean_bounds, noisy_bounds, *fields)]
    (out_here, up_here, up_beside, down_here), _ = tie(
        (out_here, up_here, up_beside, down_here), other[3]
    )
    out_other = in_order(core, out_here, sibling(out_here))
    bias_all = b_up.astype(f32).reshape(-1, 1, HIDDEN_TILE)

    x_rows = tokens.reshape(TOK_DEV, width)
    out, d_mid, d_att, d_att2, grad_out, grad_out2, grad_bias, norms, pieces = middle(
        bits,
        x_rows,
        mine[3],
        other[3],
        w_out,
        out_other,
        cotangent.reshape(TOK_DEV, width),
        vectors,
        bias_all,
        (w_up, up_here, up_beside),
        (w_down, down_here),
    )
    hidden = b_up.shape[0]

    crossed_out = across(grad_out2)
    spread = [(b, min(2, min(bits, 4) - b)) for b in range(2, min(bits, 4), 2)]
    gathered = pieces
    ((first_bit, n),) = spread
    moved = [
        lax.ppermute(gathered, "dp", [(i, i ^ (k << first_bit)) for i in range(dp_size)])
        for k in range(1, 1 << n)
    ]

    def backward(saved, d_attended, spans, *rest):
        query, keys, values, attended, lse = saved
        return attend_backward(
            spans,
            clean_bounds,
            noisy_bounds,
            query,
            keys,
            values,
            attended,
            d_attended,
            lse,
            cosine,
            sine,
            rest,
        )

    d_fields2, grad2 = backward(other, d_att2, spans, normed1_t)
    grad2 = grad2.reshape(-1, ROW_TILE, grad2.shape[2])
    low_bit, high_bit = (place >> 2) & 1, (place >> 3) & 1
    moved, _ = tie(moved, grad2)
    gathered = in_order(
        high_bit,
        in_order(low_bit, gathered, moved[0], 1),
        in_order(low_bit, moved[1], moved[2], 1),
        1,
    )
    half = ROW_TILE // 2
    part_of = lambda array, which: lax.dynamic_slice_in_dim(array, which * half, half, 1)
    got = sibling(part_of(grad2, 1 - core))
    crossing = (part_of(grad2, core).astype(f32) + got.astype(f32)).astype(bf16)
    (crossing, gathered), spans = tie((crossing, gathered), spans)
    crossed = across(crossing)
    moved = beside(gathered)
    d_fields1, given = backward(mine, d_att, spans, d_fields2, qkv_mine, qkv_other)
    moved, d_fields1 = tie(moved, d_fields1)
    gathered = in_order(side, gathered, moved, 1)
    gathered, d_fields1 = tie(gathered, d_fields1)
    moved = sibling(gathered)
    lead = hidden // width
    bias2, bias1 = grad_bias.reshape(2, lead, width)
    shared = jnp.concatenate([norms[:3], jnp.zeros((2, width), f32)], axis=0)
    grad_qkv, grad_out, grad_tokens, sums = leave(
        bits,
        normed1_t,
        grad_out,
        (crossed, crossed_out),
        (d_fields1, d_fields2),
        (qkv_mine, qkv_other),
        x_rows,
        context,
        given,
        vectors,
        d_mid,
        jnp.concatenate([bias1, shared], axis=0),
        jnp.concatenate([bias2, shared], axis=0),
    )
    moved, _ = tie(moved, grad_qkv)
    grad_down, grad_up = assemble(core.reshape(1), gathered, moved)
    return (
        out.reshape(tokens.shape),
        grad_tokens.reshape(tokens.shape),
        sums[lead + 3],
        sums[lead + 4],
        grad_qkv.transpose(1, 0, 2).astype(f32),
        grad_out.astype(f32),
        sums[lead],
        sums[lead + 1],
        grad_up,
        sums[:lead].reshape(hidden),
        grad_down,
        sums[lead + 2],
    )


def solution(mesh):
    in_specs = (
        P(None, ("dp", "mp"), None),
        P("dp", None),
        P(),
        P(None, ("dp", "mp"), None),
        P(),
        P(),
        P(None, None, "mp"),
        P("mp", None),
        P(),
        P(),
        P(None, "mp"),
        P("mp"),
        P("mp", None),
        P(),
    )
    out_specs = (
        P(None, ("dp", "mp"), None),
        P(None, ("dp", "mp"), None),
        P(),
        P(),
        P(None, None, "mp"),
        P("mp", None),
        P(),
        P(),
        P(None, "mp"),
        P("mp"),
        P("mp", None),
        P(),
    )
    return jax.shard_map(
        functools.partial(local, mesh.shape["dp"]),
        mesh=mesh,
        in_specs=in_specs,
        out_specs=out_specs,
        check_vma=False,
    )
```

```python
import functools
import math

import jax
import jax.numpy as jnp
from jax import lax
from jax.experimental import pallas as pl
from jax.experimental.pallas import tpu as pltpu
from jax.sharding import PartitionSpec as P

HD = 64
TOK_DEV = 1024
HALF = TOK_DEV // 2
EDGE = 16
CLEAN_OWN = HALF
NOISY_BASE = 2 * HALF + EDGE
NOISY_OWN = NOISY_BASE + EDGE
KEY_ROWS = NOISY_OWN + HALF + EDGE
TILE = 128
TILES = HALF // TILE
WINDOW = TILE + 2 * EDGE
KEY_TILE = 192
LANES = 128
HIDDEN_TILE = 256
ROW_TILE = 256

epsilon = 1e-05
neg_large = -1e30
to_base2 = 0.125 * math.log2(math.e)
f32 = jnp.float32
bf16 = jnp.bfloat16

NN = (((1,), (0,)), ((), ()))
NT = (((1,), (1,)), ((), ()))


def dot(left, right, dims=NN):
    return lax.dot_general(left, right, dims, preferred_element_type=f32)


def low_lanes(shape):
    return lax.broadcasted_iota(jnp.int32, shape, 1) < HD


def turn(values, cosine, sine):
    lane = lax.broadcasted_iota(jnp.int32, values.shape, 1)
    first_half = (lane & (HD - 1)) < HD // 2
    swapped = jnp.where(
        first_half,
        pltpu.roll(values, LANES - HD // 2, 1),
        pltpu.roll(values, HD // 2, 1),
    )
    return values * cosine + swapped * sine


def project_rows(rows, w_ref, cosine, sine, q_ref, k_ref, v_ref, at):
    for part, out_ref in ((0, q_ref), (1, k_ref)):
        field = dot(rows, w_ref[part])
        for pair in range(field.shape[1] // LANES):
            cols = slice(pair * LANES, (pair + 1) * LANES)
            out_ref[at, cols] = turn(field[:, cols], cosine, sine).astype(bf16)
    v_ref[at, :] = dot(rows, w_ref[2]).astype(bf16)


def project_kernel(rows_ref, w_ref, cos_ref, sin_ref, q_ref, k_ref, v_ref):
    at = slice(0, rows_ref.shape[0])
    project_rows(rows_ref[...], w_ref, cos_ref[...], sin_ref[...], q_ref, k_ref, v_ref, at)


def project(rows, weights, cosine, sine):
    count, width = rows.shape
    cols = weights.shape[2]
    step = count // 3
    row_spec = pl.BlockSpec((step, width), lambda i: (i, 0))
    table_spec = pl.BlockSpec((step, LANES), lambda i: (i, 0))
    out_spec = pl.BlockSpec((step, cols), lambda i: (i, 0))
    shape = jax.ShapeDtypeStruct((count, cols), bf16)
    return pl.pallas_call(
        project_kernel,
        grid=(3,),
        in_specs=[
            row_spec,
            pl.BlockSpec(weights.shape, lambda i: (0, 0, 0)),
            table_spec,
            table_spec,
        ],
        out_specs=[out_spec] * 3,
        out_shape=[shape] * 3,
        name="project",
        cost_estimate=pl.CostEstimate(
            flops=2 * count * width * 3 * cols,
            bytes_accessed=2 * (count * (width + 3 * cols) + 3 * width * cols),
            transcendentals=0,
        ),
    )(rows, weights, cosine, sine)


def normal(values):
    average = jnp.mean(values, axis=-1, keepdims=True)
    centred = values - average
    variance = jnp.mean(centred * centred, axis=-1, keepdims=True)
    scale = lax.rsqrt(variance + epsilon)
    return centred * scale, scale


def enter_kernel(
    tokens_ref,
    context_ref,
    vectors_ref,
    w_ref,
    cos_ref,
    sin_ref,
    rows_ref,
    rows_t_ref,
    q_ref,
    k_ref,
    v_ref,
):
    def norm(values):
        unit = normal(values.astype(f32))[0]
        return (unit * vectors_ref[0:1, :] + vectors_ref[1:2, :]).astype(bf16)

    def blocks(i, _):
        source = pl.ds(pl.multiple_of(i * TILE, TILE), TILE)
        rows_ref[source, :] = norm(context_ref[source, :])
        at = pl.ds(pl.multiple_of(CLEAN_OWN + i * TILE, TILE), TILE)
        rows_ref[at, :] = norm(tokens_ref[1, source, :])
        at = pl.ds(pl.multiple_of(NOISY_OWN + i * TILE, EDGE), TILE)
        rows_ref[at, :] = norm(tokens_ref[0, source, :])
        return 0

    lax.fori_loop(0, TILES, blocks, 0)
    rows_ref[2 * HALF : NOISY_BASE, :] = rows_ref[:EDGE, :]
    edge = norm(context_ref[HALF:, :])
    rows_ref[NOISY_BASE:NOISY_OWN, :] = edge
    rows_ref[NOISY_OWN + HALF :, :] = edge
    step = KEY_ROWS // 3

    def fields(i, _):
        at = pl.ds(pl.multiple_of(i * step, EDGE), step)
        project_rows(
            rows_ref[at, :], w_ref, cos_ref[at, :], sin_ref[at, :], q_ref, k_ref, v_ref, at
        )
        return 0

    lax.fori_loop(0, 3, fields, 0)
    for c in range(rows_t_ref.shape[0] // LANES):
        cols = slice(c * LANES, (c + 1) * LANES)
        rows_t_ref[cols, :] = rows_ref[:, cols].T


def enter(tokens, context, vectors, weights, cosine, sine):
    width, cols = weights.shape[1:]
    vmem = pl.BlockSpec(memory_space=pltpu.VMEM)
    shape = jax.ShapeDtypeStruct
    field = shape((KEY_ROWS, cols), bf16)
    return pl.pallas_call(
        enter_kernel,
        in_specs=[vmem] * 6,
        out_specs=[vmem] * 5,
        out_shape=[shape((KEY_ROWS, width), bf16), shape((width, KEY_ROWS), bf16)] + [field] * 3,
        name="enter",
        cost_estimate=pl.CostEstimate(
            flops=10**10, bytes_accessed=16 * 10**6, transcendentals=0
        ),
    )(tokens, context, vectors, weights, cosine, sine)


def split_heads(rows):
    low = low_lanes(rows.shape)
    zero = jnp.zeros_like(rows)
    return jnp.where(low, rows, zero), jnp.where(low, zero, rows)


def between(shape, offset, low, high):
    index = lax.broadcasted_iota(jnp.int32, shape, 0) + offset
    return jnp.logical_and(index >= low, index < high)


def fold(values, combine):
    rows, cols = values.shape
    groups = values.reshape(rows // 8, 8, cols)
    return combine(groups, axis=0)


def forward_kernel(
    span_ref, clean_ref, noisy_ref, q_ref, k_ref, v_ref, out_ref, lse_ref, bias_ref, window_ref
):
    pairs = q_ref.shape[1] // LANES
    lanes = [slice(p * LANES, (p + 1) * LANES) for p in range(pairs)]

    def one_tile(t, _):
        clean_at = pl.multiple_of(CLEAN_OWN + t * TILE, TILE)
        noisy_at = pl.multiple_of(NOISY_OWN + t * TILE, EDGE)
        window_at = pl.multiple_of(NOISY_BASE + t * TILE, EDGE)
        key_low, key_high = clean_ref[t, 0:1, :], clean_ref[t, 1:2, :]
        own_low, own_high = noisy_ref[t, 0:1, :], noisy_ref[t, 1:2, :]
        allowed = between((WINDOW, TILE), 0, own_low, own_high)
        window_ref[...] = jnp.where(allowed, 0.0, neg_large)
        first_key, trips = span_ref[t, 0], span_ref[t, 1]
        queries, tops = [], []
        for cols in lanes:
            query = jnp.concatenate(
                [q_ref[pl.ds(noisy_at, TILE), cols], q_ref[pl.ds(clean_at, TILE), cols]], axis=0
            )
            heads = split_heads(query)
            queries += heads
            keys = k_ref[pl.ds(window_at, WINDOW), cols]
            for head in range(2):
                scores = dot(keys, heads[head][:TILE], NT) + window_ref[...]
                top = fold(scores, jnp.max)
                tops.append(
                    jnp.concatenate([top, jnp.full((8, TILE), neg_large, f32)], axis=1)
                )

        def first_pass(j, tops):
            at = pl.multiple_of(first_key + j * KEY_TILE, EDGE)
            allowed = between((KEY_TILE, 2 * TILE), at, key_low, key_high)
            bias_ref[j] = jnp.where(allowed, 0.0, neg_large)
            after = []
            for p, cols in enumerate(lanes):
                keys = k_ref[pl.ds(at, KEY_TILE), cols]
                for head in range(2):
                    scores = dot(keys, queries[2 * p + head], NT) + bias_ref[j]
                    after.append(jnp.maximum(tops[2 * p + head], fold(scores, jnp.max)))
            return tuple(after)

        tops = lax.fori_loop(0, trips, first_pass, tuple(tops))
        tops = [jnp.max(top, axis=0, keepdims=True) * to_base2 for top in tops]
        state = []
        keys = [k_ref[pl.ds(window_at, WINDOW), cols] for cols in lanes]
        values_t = [v_ref[pl.ds(window_at, WINDOW), cols].T for cols in lanes]
        scores = dot(keys[0], queries[0][:TILE], NT)
        late = None
        for h in range(2 * pairs):
            if h + 1 < 2 * pairs:
                ahead = dot(keys[(h + 1) // 2], queries[h + 1][:TILE], NT)
            expo = jnp.exp2(scores * to_base2 - tops[h][:, :TILE] + window_ref[...])
            if late is not None:
                state.append(jnp.concatenate([late, jnp.zeros((HD, TILE), f32)], axis=1))
            total = fold(expo, jnp.sum)
            state.append(jnp.concatenate([total, jnp.zeros((8, TILE), f32)], axis=1))
            side = slice(h % 2 * HD, (h % 2 + 1) * HD)
            late = dot(values_t[h // 2][side], expo.astype(bf16))
            scores = ahead
        state.append(jnp.concatenate([late, jnp.zeros((HD, TILE), f32)], axis=1))

        def second_pass(j, state):
            at = pl.multiple_of(first_key + j * KEY_TILE, EDGE)
            keys = [k_ref[pl.ds(at, KEY_TILE), cols] for cols in lanes]
            values_t = [v_ref[pl.ds(at, KEY_TILE), cols].T for cols in lanes]
            after = list(state)
            scores = dot(keys[0], queries[0], NT)
            late = None
            for h in range(2 * pairs):
                ahead = dot(keys[(h + 1) // 2], queries[h + 1], NT) if h + 1 < 2 * pairs else None
                expo = jnp.exp2(scores * to_base2 - tops[h] + bias_ref[j])
                after[2 * h] = state[2 * h] + fold(expo, jnp.sum)
                if late is not None:
                    after[2 * h - 1] = state[2 * h - 1] + late
                side = slice(h % 2 * HD, (h % 2 + 1) * HD)
                late = dot(values_t[h // 2][side], expo.astype(bf16))
                scores = ahead
            after[-1] = state[-1] + late
            return tuple(after)

        state = lax.fori_loop(0, trips, second_pass, tuple(state))
        low_at = pl.ds(pl.multiple_of(t * TILE, TILE), TILE)
        high_at = pl.ds(pl.multiple_of(HALF + t * TILE, TILE), TILE)
        for p, cols in enumerate(lanes):
            halves = []
            for head in range(2):
                h = 2 * p + head
                total = jnp.sum(state[2 * h], axis=0, keepdims=True)
                halves.append(state[2 * h + 1] / total)
                lse_ref[p, t, head : head + 1, :] = tops[h] + jnp.log2(total)
            pair = jnp.concatenate(halves, axis=0).T.astype(bf16)
            out_ref[low_at, cols] = pair[:TILE]
            out_ref[high_at, cols] = pair[TILE:]
        return 0

    lax.fori_loop(0, TILES, one_tile, 0)


def attend_forward(spans, clean_bounds, noisy_bounds, query, keys, values):
    count, cols = query.shape
    pairs = cols // LANES
    vmem = pl.BlockSpec(memory_space=pltpu.VMEM)
    work = pairs * 2 * 2 * HALF * TOK_DEV
    return pl.pallas_call(
        forward_kernel,
        in_specs=[pl.BlockSpec(memory_space=pltpu.SMEM)] + [vmem] * 5,
        out_specs=[vmem] * 2,
        out_shape=[
            jax.ShapeDtypeStruct((TOK_DEV, cols), bf16),
            jax.ShapeDtypeStruct((pairs, TILES, 2, 2 * TILE), f32),
        ],
        scratch_shapes=[
            pltpu.VMEM((NOISY_BASE // KEY_TILE + 1, KEY_TILE, 2 * TILE), f32),
            pltpu.VMEM((WINDOW, TILE), f32),
        ],
        name="attend_forward",
        cost_estimate=pl.CostEstimate(
            flops=4 * work * HD, bytes_accessed=8 * count * cols, transcendentals=work
        ),
    )(spans, clean_bounds, noisy_bounds, query, keys, values)


def backward_kernel(
    giving,
    span_ref,
    clean_ref,
    noisy_ref,
    q_ref,
    k_ref,
    v_ref,
    o_ref,
    d_ref,
    lse_ref,
    cos_ref,
    sin_ref,
    *refs,
):
    if giving:
        d2_hbm, w_hbm, w2_hbm, out_ref, give_ref, *refs = refs
        dk_ref, dv_ref, bias_ref, d2_ref, w_ref, w2_ref, load_sem = refs
        loads = [(w_hbm, w_ref), (w2_hbm, w2_ref)]
        loads += [(d2_hbm.at[c, :HALF], d2_ref.at[c]) for c in range(3)]
        loads = [
            pltpu.make_async_copy(source, target, load_sem.at[n])
            for n, (source, target) in enumerate(loads)
        ]
        for load in loads:
            load.start()
    else:
        rows_ref, out_ref, grad_ref, dk_ref, dv_ref, bias_ref = refs
    pairs = q_ref.shape[1] // LANES
    lanes = [slice(p * LANES, (p + 1) * LANES) for p in range(pairs)]
    dk_ref[...] = jnp.zeros_like(dk_ref)
    dv_ref[...] = jnp.zeros_like(dv_ref)
    out_ref[0] = jnp.zeros_like(out_ref[0])

    def one_tile(t, _):
        clean_at = pl.multiple_of(CLEAN_OWN + t * TILE, TILE)
        noisy_at = pl.multiple_of(NOISY_OWN + t * TILE, EDGE)
        window_at = pl.multiple_of(NOISY_BASE + t * TILE, EDGE)
        low_at = pl.multiple_of(t * TILE, TILE)
        high_at = pl.multiple_of(HALF + t * TILE, TILE)
        key_low, key_high = clean_ref[t, 0:1, :], clean_ref[t, 1:2, :]
        own_low, own_high = noisy_ref[t, 0:1, :], noisy_ref[t, 1:2, :]
        queries, d_outs, inners, lses = [], [], [], []
        for p, cols in enumerate(lanes):

            def both(ref, low, high):
                return jnp.concatenate(
                    [ref[pl.ds(low, TILE), cols], ref[pl.ds(high, TILE), cols]], axis=0
                )

            queries.append(split_heads(both(q_ref, noisy_at, clean_at)))
            d_rows = both(d_ref, low_at, high_at)
            o_rows = both(o_ref, low_at, high_at)
            product = (d_rows.astype(f32) * o_rows.astype(f32)).T
            d_outs.append(split_heads(d_rows))
            inners.append(
                [
                    jnp.sum(product[head * HD : (head + 1) * HD], axis=0, keepdims=True) * 0.125
                    for head in range(2)
                ]
            )
            lses.append([lse_ref[p, t, head : head + 1, :] for head in range(2)])

        def accumulate(at, rows, cols, allowed, d_query):
            bias_ref[:rows, :cols] = jnp.where(allowed, 0.0, neg_large)
            after = list(d_query)
            keys = [k_ref[pl.ds(at, rows), span] for span in lanes]
            eighth = [v_ref[pl.ds(at, rows), span] * jnp.asarray(0.125, bf16) for span in lanes]
            keys_t = [part.T for part in keys]
            stack = lambda parts: jnp.concatenate([part[:cols] for part in parts], axis=0)

            def begin(h):
                p, head = h // 2, h % 2
                return (
                    dot(keys[p], queries[p][head][:cols], NT),
                    dot(eighth[p], d_outs[p][head][:cols], NT),
                )

            def finish_pair(p, weights, d_scores):
                span = lanes[p]
                for head in range(2):
                    side = slice(head * HD, (head + 1) * HD)
                    h = 2 * p + head
                    after[h] = d_query[h] + dot(keys_t[p][side], d_scores[head])
                dv_ref[pl.ds(at, rows), span] += dot(
                    jnp.concatenate(weights, axis=1), stack(d_outs[p])
                )
                dk_ref[pl.ds(at, rows), span] += dot(
                    jnp.concatenate(d_scores, axis=1), stack(queries[p])
                )

            ready = begin(0)
            held = None
            weights, d_scores = [], []
            for h in range(2 * pairs):
                ahead = begin(h + 1) if h + 1 < 2 * pairs else None
                p, head = h // 2, h % 2
                scores = ready[0] * to_base2 - lses[p][head][:, :cols] + bias_ref[:rows, :cols]
                probs = jnp.exp2(scores)
                d_score = (probs * (ready[1] - inners[p][head][:, :cols])).astype(bf16)
                weights.append(probs.astype(bf16))
                d_scores.append(d_score)
                if held is not None:
                    finish_pair(*held)
                    held = None
                if head == 1:
                    held = (p, weights, d_scores)
                    weights, d_scores = [], []
                ready = ahead
            finish_pair(*held)
            return tuple(after)

        allowed = between((WINDOW, TILE), 0, own_low, own_high)
        zero = jnp.zeros((HD, TILE), f32)
        start = accumulate(window_at, WINDOW, TILE, allowed, (zero,) * (2 * pairs))
        start = tuple(jnp.concatenate([part, zero], axis=1) for part in start)
        first_key, trips = span_ref[t, 0], span_ref[t, 1]

        def one_step(j, d_query):
            at = pl.multiple_of(first_key + j * KEY_TILE, EDGE)
            allowed = between((KEY_TILE, 2 * TILE), at, key_low, key_high)
            return accumulate(at, KEY_TILE, 2 * TILE, allowed, d_query)

        d_query = lax.fori_loop(0, trips, one_step, start)
        for p, span in enumerate(lanes):
            pair = jnp.concatenate(d_query[2 * p : 2 * p + 2], axis=0).T
            for at, part in ((noisy_at, pair[:TILE]), (clean_at, pair[TILE:])):
                turned = turn(part, cos_ref[pl.ds(at, TILE), :], -sin_ref[pl.ds(at, TILE), :])
                out_ref[0, pl.ds(at, TILE), span] = turned.astype(bf16)
        return 0

    lax.fori_loop(0, TILES, one_tile, 0)
    step = KEY_ROWS // 9

    def finish(i, _):
        rows = pl.ds(pl.multiple_of(i * step, EDGE), step)
        for span in lanes:
            out_ref[1, rows, span] = turn(
                dk_ref[rows, span], cos_ref[rows, :], -sin_ref[rows, :]
            ).astype(bf16)
        out_ref[2, rows, :] = dv_ref[rows, :].astype(bf16)
        return 0

    lax.fori_loop(0, 9, finish, 0)

    def weight_rows(i, _):
        rows = pl.ds(pl.multiple_of(i * ROW_TILE, LANES), ROW_TILE)
        for c in range(3):
            grad_ref[c, rows, :] = dot(rows_ref[rows, :], out_ref[c]).astype(bf16)
        return 0

    if giving:
        for load in loads:
            load.wait()
        total = 0.0
        for c in range(3):
            total = total + dot(out_ref[c, :HALF, :], w_ref[c], NT) + dot(d2_ref[c], w2_ref[c], NT)
        give_ref[...] = total
    else:
        lax.fori_loop(0, rows_ref.shape[0] // ROW_TILE, weight_rows, 0)


def attend_backward(
    spans,
    clean_bounds,
    noisy_bounds,
    query,
    keys,
    values,
    attended,
    d_attended,
    lse,
    cosine,
    sine,
    rest,
):
    count, cols = query.shape
    vmem = pl.BlockSpec(memory_space=pltpu.VMEM)
    hbm = pl.BlockSpec(memory_space=pl.ANY)
    shape = jax.ShapeDtypeStruct
    giving = len(rest) > 1
    if giving:
        width = rest[1].shape[1]
        second = shape((HALF, width), f32)
        scratch = [
            pltpu.VMEM((3, HALF, cols), bf16),
            pltpu.VMEM(rest[1].shape, bf16),
            pltpu.VMEM(rest[2].shape, bf16),
            pltpu.SemaphoreType.DMA((5,)),
        ]
    else:
        second = shape((3, rest[0].shape[0], cols), bf16)
        scratch = []
    return pl.pallas_call(
        functools.partial(backward_kernel, giving),
        in_specs=[pl.BlockSpec(memory_space=pltpu.SMEM)]
        + [vmem] * 10
        + [hbm if giving else vmem] * len(rest),
        out_specs=[vmem] * 2,
        scratch_shapes=[
            pltpu.VMEM((count, cols), f32),
            pltpu.VMEM((count, cols), f32),
            pltpu.VMEM((max(KEY_TILE, WINDOW), 2 * TILE), f32),
        ]
        + scratch,
        out_shape=[shape((3, count, cols), bf16), second],
        name="attend_backward",
        cost_estimate=pl.CostEstimate(
            flops=36 * 10**9, bytes_accessed=36 * 10**6, transcendentals=6 * 10**6
        ),
    )(
        spans,
        clean_bounds,
        noisy_bounds,
        query,
        keys,
        values,
        attended,
        d_attended,
        lse,
        cosine,
        sine,
        *rest,
    )


PIECES = 16
MESH = pl.DeviceIdType.MESH


def flip(value, mask):
    result = value
    for b in range(mask.bit_length()):
        if mask >> b & 1:
            result = result + (1 << b) * (1 - 2 * ((value // (1 << b)) % 2))
    return result


class Exchange:
    def __init__(self, bits, count, rows, width, back=True):
        self.bits, self.count, self.rows, self.width = bits, count, rows, width
        self.back = back
        self.half, self.quarter, self.piece = rows // 2, rows // 4, rows // PIECES
        self.extra = list(range(4, bits))

    def slots(self):
        return 8 + 2 * (6 if self.back else 4) + (3 if self.extra else 0)

    def scratch(self):
        k, w = self.count, self.width
        cross = k if not self.back else 1
        shapes = [
            pltpu.VMEM((k, 2 - self.back, self.half, w), bf16),
            pltpu.VMEM((cross, self.half, w), bf16),
            pltpu.VMEM((cross, self.half, w), bf16),
            pltpu.VMEM((k, self.quarter, w), bf16),
            pltpu.VMEM((k, self.quarter, w), bf16),
            pltpu.VMEM((k, self.quarter, w), f32),
            pltpu.VMEM((k, 3, self.piece, w), bf16),
            pltpu.VMEM((k, 3, self.piece, w), bf16),
        ]
        lanes_of = (1, 0, 1, 3, 3, 1, 1) if self.back else (2, 1, 1, 3, 0, 0, 0)
        for lanes in [lanes for lanes in lanes_of if lanes]:
            shapes += [pltpu.SemaphoreType.DMA((k, lanes))] * 2
        if self.extra:
            n = len(self.extra)
            shapes += [pltpu.VMEM((k, 2 * n, self.piece, w), bf16)]
            shapes += [pltpu.SemaphoreType.DMA((k, n))] * 2
        return shapes

    def bind(self, place, part, refs):
        (self.a_in, self.b_out, self.b_in, self.c_out, self.c_in, self.keep) = refs[:6]
        self.d_out, self.d_in = refs[6:8]
        names = "acdefg" if self.back else "abcd"
        self.sems = {name: (refs[8 + 2 * i], refs[9 + 2 * i]) for i, name in enumerate(names)}
        if self.extra:
            at = 8 + 2 * len(names)
            self.x_buf, self.x_send, self.x_recv = refs[at : at + 3]
        self.place, self.part = place, part
        self.core, self.x, self.z = place % 2, (place // 2) % 2, (place // 4) % 4
        self.sibling = {"dp": flip(place, 1)}
        self.beside = {"dp": flip(place, 2)}
        self.across = {"mp": 1 - part}
        self.peers = [{"dp": flip(place, j << 2)} for j in range(1, 4)]
        self.partners = [self.sibling, self.beside, self.across] + self.peers
        self.partners += [{"dp": flip(place, 1 << b)} for b in self.extra]
        return self

    def greet(self):
        barrier = pltpu.get_barrier_semaphore()
        for partner in self.partners:
            pl.semaphore_signal(barrier, inc=1, device_id=partner, device_id_type=MESH)
        pl.semaphore_wait(barrier, len(self.partners))

    def copy(self, name, k, lane, source, target, device):
        out, into = self.sems[name]
        return pltpu.make_async_remote_copy(
            src_ref=source,
            dst_ref=target,
            send_sem=out.at[k, lane],
            recv_sem=into.at[k, lane],
            device_id=device,
            device_id_type=MESH,
        )

    def rows_at(self, start, size):
        return pl.ds(pl.multiple_of(start, PIECES), size)

    def copy_a(self, k, lane, grads):
        source = grads.at[k, self.rows_at((1 - self.core) * self.half, self.half)]
        return self.copy("a", k, lane, source, self.a_in.at[k, lane], self.sibling)

    def copy_b(self, k):
        return self.copy("b", k, 0, self.b_out.at[k], self.b_in.at[k], self.across)

    def copy_c(self, k):
        return self.copy("c", k, 0, self.c_out.at[k], self.c_in.at[k], self.beside)

    def copy_d(self, k, j):
        return self.copy("d", k, j, self.d_out.at[k, j], self.d_in.at[k, j], self.peers[j])

    def spot(self, change=0):
        start = self.core * self.half + self.x * self.quarter
        return self.rows_at(start + flip(self.z, change) * self.piece, self.piece)

    def copy_e(self, k, j, full):
        rows = full.at[k, self.spot()]
        return self.copy("e", k, j, rows, rows, self.peers[j])

    def copy_f(self, k, full):
        start = self.core * self.half + self.x * self.quarter
        rows = full.at[k, self.rows_at(start, self.quarter)]
        return self.copy("f", k, 0, rows, rows, self.beside)

    def copy_g(self, k, full):
        rows = full.at[k, self.rows_at(self.core * self.half, self.half)]
        return self.copy("g", k, 0, rows, rows, self.sibling)

    def start_a(self, k, lane, grads):
        self.copy_a(k, lane, grads).start()

    def stage_b(self, k, others):
        self.copy_a(k, 0, others).wait()
        mine = others[k, self.rows_at(self.core * self.half, self.half), :].astype(f32)
        self.b_out[k] = (mine + self.a_in[k, 0].astype(f32)).astype(bf16)
        self.copy_b(k).start()

    def stage_c(self, k, grads, crossed=None):
        lane = 0 if self.back else 1
        self.copy_a(k, lane, grads).wait()
        if not self.back:
            self.copy_b(k).wait()

        def total(which):
            inner = which * self.quarter
            rows = self.rows_at(inner, self.quarter)
            mine = grads[k, self.rows_at(self.core * self.half + inner, self.quarter), :]
            got = self.a_in[k, lane, rows, :].astype(f32)
            if not self.back:
                got = got + self.b_in[k, rows, :].astype(f32)
            elif crossed is not None:
                got = got + crossed(rows)
            return mine.astype(f32) + got

        self.c_out[k] = total(1 - self.x).astype(bf16)
        self.copy_c(k).start()
        self.keep[k] = total(self.x)

    def stage_d(self, k):
        self.copy_c(k).wait()
        for j in range(4):
            rows = self.rows_at(flip(self.z, j) * self.piece, self.piece)
            total = self.keep[k, rows, :] + self.c_in[k, rows, :].astype(f32)
            if j:
                self.d_out[k, j - 1] = total.astype(bf16)
                self.copy_d(k, j - 1).start()
            else:
                self.keep[k, rows, :] = total

    def gather_d(self, k):
        rows = self.rows_at(self.z * self.piece, self.piece)
        total = self.keep[k, rows, :]
        for j in range(3):
            self.copy_d(k, j).wait()
            total = total + self.d_in[k, j].astype(f32)
        for i, b in enumerate(self.extra):
            mine = self.x_buf.at[k, 2 * i]
            mine[...] = total.astype(bf16)
            swap = pltpu.make_async_remote_copy(
                src_ref=mine,
                dst_ref=self.x_buf.at[k, 2 * i + 1],
                send_sem=self.x_send.at[k, i],
                recv_sem=self.x_recv.at[k, i],
                device_id={"dp": flip(self.place, 1 << b)},
                device_id_type=MESH,
            )
            swap.start()
            swap.wait()
            total = total.astype(bf16).astype(f32) + self.x_buf[k, 2 * i + 1].astype(f32)
        return total.astype(bf16)

    def stage_e(self, k, full):
        full[k, self.spot(), :] = self.gather_d(k)
        for j in range(3):
            self.copy_e(k, j, full).start()

    def stage_f(self, k, full):
        for j in range(3):
            self.copy_e(k, j, full).wait()
        self.copy_f(k, full).start()

    def stage_g(self, k, full):
        self.copy_f(k, full).wait()
        self.copy_g(k, full).start()

    def stage_h(self, k, full):
        self.copy_g(k, full).wait()


def at_step(step, count, action):
    @pl.when(jnp.logical_and(step >= 0, step < count))
    def _():
        action(step)


def middle_kernel(exchanges, tiles, *refs):
    (
        x_ref,
        att_ref,
        att2_ref,
        wout_ref,
        wout2_ref,
        dy_ref,
        vectors_ref,
        bup_ref,
        up_mine,
        up_here,
        up_beside,
        down_mine,
        down_here,
        out_hbm,
        mid_hbm,
        datt_hbm,
        datt2_hbm,
        gout_ref,
        gout2_ref,
        gbup_ref,
        small_ref,
        pieces_ref,
        up_there,
        down_there,
        pass_up,
        pass_down,
        up_buf,
        down_buf,
        load_sem,
        n2_ref,
        total_ref,
        dn2_ref,
        act_ref,
        dpre_ref,
        n2_t,
        bup_other,
        bias_sem,
        out_ref,
        mid_ref,
        datt_ref,
        datt2_ref,
        store_sem,
        down_grad,
        up_grad,
        *rest,
    ) = refs
    place, part = lax.axis_index("dp"), lax.axis_index("mp")
    ex = exchanges[0].bind(place, part, rest)
    ex_up = exchanges[1].bind(place, part, rest[exchanges[0].slots() :])
    sides = ((ex, down_grad), (ex_up, up_grad))
    core = ex.core
    count = tiles // 2
    rows_all = x_ref.shape[0]
    blocks = rows_all // ROW_TILE
    width = x_ref.shape[1]
    lanes = width // 2

    def which(i):
        other = jnp.logical_or(i == 0, jnp.logical_and(i % 2 == 1, i < tiles - 1))
        mine = jnp.where(i == tiles - 1, count - 1, i // 2 - 1)
        return other, jnp.where(other, (i + 1) // 2, mine)

    quarter = width // 4
    strip = HIDDEN_TILE // 2
    held = 2 * core + ex.x
    kept = 2 * core + 1 - ex.x

    def load_up(i, source, h):
        target = up_buf.at[i % 2, h * quarter : (h + 1) * quarter]
        return pltpu.make_async_copy(source, target, load_sem.at[i % 2, h])

    def load_down(i, source, h):
        target = down_buf.at[i % 2, h * strip : (h + 1) * strip]
        return pltpu.make_async_copy(source, target, load_sem.at[i % 2, 4 + h])

    def hand_up(k, part_of):
        cols = pl.ds(pl.multiple_of(k * HIDDEN_TILE, HIDDEN_TILE), HIDDEN_TILE)
        side = ex.x if part_of == 0 else 1 - ex.x
        rows = pl.ds(pl.multiple_of(side * quarter, EDGE), quarter)
        return pltpu.make_async_remote_copy(
            src_ref=(up_here, up_beside)[part_of].at[:, cols],
            dst_ref=up_there.at[k, rows],
            send_sem=pass_up.at[k, 2 * part_of],
            recv_sem=pass_up.at[k, 2 * part_of + 1],
            device_id=ex.sibling,
            device_id_type=MESH,
        )

    def hand_down(b):
        return pltpu.make_async_remote_copy(
            src_ref=down_here.at[strip_rows(b)],
            dst_ref=down_there.at[b],
            send_sem=pass_down.at[b, 0],
            recv_sem=pass_down.at[b, 1],
            device_id=ex.sibling,
            device_id_type=MESH,
        )

    def strip_rows(b):
        return pl.ds(pl.multiple_of(b * strip, strip), strip)

    def start_loads(i):
        other, k = which(i)
        mine = jnp.logical_not(other)
        cols = pl.ds(pl.multiple_of(k * HIDDEN_TILE, HIDDEN_TILE), HIDDEN_TILE)

        @pl.when(other)
        def _():
            hand_up(k, 0).wait()
            hand_up(k, 1).wait()

        for h in range(4):

            @pl.when(mine)
            def _():
                load_up(i, up_mine.at[h * quarter : (h + 1) * quarter, cols], h).start()

            @pl.when(jnp.logical_and(other, held == h))
            def _():
                load_up(i, up_here.at[:, cols], h).start()

            @pl.when(jnp.logical_and(other, kept == h))
            def _():
                load_up(i, up_beside.at[:, cols], h).start()

            @pl.when(jnp.logical_and(other, core != h // 2))
            def _():
                rows = slice(h % 2 * quarter, (h % 2 + 1) * quarter)
                load_up(i, up_there.at[k, rows], h).start()

        for h in range(2):
            b = 2 * k + h
            inner = b % count

            @pl.when(mine)
            def _():
                load_down(i, down_mine.at[strip_rows(b), :], h).start()

            @pl.when(jnp.logical_and(other, core == b // count))
            def _():
                load_down(i, down_here.at[strip_rows(inner), :], h).start()

            @pl.when(jnp.logical_and(other, core != b // count))
            def _():
                hand_down(inner).wait_recv()
                load_down(i, down_there.at[inner], h).start()

    def wait_loads(i):
        for h in range(4):
            load_up(i, up_mine.at[:quarter, :HIDDEN_TILE], h).wait()
        for h in range(2):
            load_down(i, down_mine.at[:strip, :], h).wait()

    ex.greet()
    bias_swap = pltpu.make_async_remote_copy(
        src_ref=bup_ref,
        dst_ref=bup_other,
        send_sem=bias_sem.at[0],
        recv_sem=bias_sem.at[1],
        device_id=ex.across,
        device_id_type=MESH,
    )
    bias_swap.start()

    def hand(k, _):
        hand_up(k, 0).start()
        hand_up(k, 1).start()
        hand_down(k).start()
        return 0

    lax.fori_loop(0, count, hand, 0)

    def prologue(n, _):
        prologue_block(2 * n)
        prologue_block(2 * n + 1)
        return 0

    def prologue_block(r):
        rows = pl.ds(pl.multiple_of(r * ROW_TILE, ROW_TILE), ROW_TILE)
        branch = dot(att_ref[rows, :], wout_ref[...]) + dot(att2_ref[rows, :], wout2_ref[...])
        mid = x_ref[rows, :].astype(f32) + branch
        mid_ref[rows, :] = mid
        unit = normal(mid)[0]
        n2_ref[rows, :] = (unit * vectors_ref[2:3, :] + vectors_ref[3:4, :]).astype(bf16)
        total_ref[rows, :] = mid + vectors_ref[4:5, :]
        dn2_ref[rows, :] = jnp.zeros((ROW_TILE, width), f32)

    lax.fori_loop(0, blocks // 2, prologue, 0)
    start_loads(0)
    for c in range(width // LANES):
        cols = slice(c * LANES, (c + 1) * LANES)
        n2_t[cols, :] = n2_ref[:, cols].T
    n2_t[width:, :] = jnp.ones((PIECES, rows_all), bf16)
    bias_swap.wait()

    def tile(i):
        other, k = which(i)
        slot = i % 2
        wait_loads(i)

        @pl.when(i + 1 < tiles)
        def _():
            start_loads(i + 1)

        up, down = up_buf.at[slot], down_buf.at[slot]
        bias_at = jnp.where(other, k, count + k)
        bias = jnp.where(other, bup_other[k], bup_ref[k])
        linear = 0.7978845608028654
        cubic = linear * 0.044715
        for r in range(blocks):
            rows = slice(r * ROW_TILE, (r + 1) * ROW_TILE)
            pre = dot(n2_ref[rows, :], up[...]) + bias
            d_act = dot(dy_ref[rows, :], down[...], NT)
            square = pre * pre
            bend = jnp.tanh(pre * (square * cubic + linear))
            gate = 0.5 * bend + 0.5
            full_act = pre * gate
            slope = gate + (full_act - full_act * gate) * (square * (6.0 * cubic) + 2.0 * linear)
            act_ref[rows, :] = full_act.astype(bf16)
            dpre_ref[rows, :] = (d_act * slope).astype(bf16)
        total_ref[...] += dot(act_ref[...], down[...])
        dn2_ref[...] += dot(dpre_ref[...], up[...], NT)
        down_grad[k] = dot(act_ref[...].T, dy_ref[...]).astype(bf16)

        def start(lane):
            for side, grad in sides:
                side.start_a(k, lane, grad)

        by_rows = dot(n2_t[...], dpre_ref[...])
        up_grad[k] = by_rows[:width].astype(bf16)
        gbup_ref[bias_at] = by_rows[width : width + 1]
        pl.when(other)(functools.partial(start, 0))
        pl.when(jnp.logical_not(other))(functools.partial(start, 1))

    def each(k, when, action):
        @pl.when(jnp.logical_and(when, jnp.logical_and(k >= 0, k < count)))
        def _():
            for n, (side, grad) in enumerate(sides):
                action(n, side, grad, k)

    def stage_b(n, side, grad, k):
        side.stage_b(k, grad)

    def stage_c(n, side, grad, k):
        side.stage_c(k, grad)

    def stage_d(n, side, grad, k):
        side.stage_d(k)

    def arrive(n, side, grad, k):
        piece = side.gather_d(k)
        if n == 0:
            pieces_ref[k] = piece
        else:
            for c in range(width // HIDDEN_TILE):
                cols = slice(c * HIDDEN_TILE, (c + 1) * HIDDEN_TILE)
                pieces_ref[count + k, :, cols] = piece[c * PIECES : (c + 1) * PIECES]

    def steps(i):
        even = i % 2 == 0
        odd = jnp.logical_not(even)
        each((i - 5) // 2, odd, arrive)
        each((i - 4) // 2, even, stage_d)
        each((i - 3) // 2, odd, stage_c)
        each(i // 2, even, stage_b)

    def epilogue(r, _):
        rows = pl.ds(pl.multiple_of(r * ROW_TILE, ROW_TILE), ROW_TILE)
        out_ref[rows, :] = total_ref[rows, :].astype(bf16)
        unit, scale = normal(mid_ref[rows, :])
        d_rows = dn2_ref[rows, :]
        dy = dy_ref[rows, :].astype(f32)
        lean = d_rows * vectors_ref[2:3, :]
        d_mid = dy + scale * (
            lean
            - jnp.mean(lean, axis=-1, keepdims=True)
            - unit * jnp.mean(lean * unit, axis=-1, keepdims=True)
        )
        mid_ref[rows, :] = d_mid
        d_branch = d_mid.astype(bf16)
        n2_ref[rows, :] = d_branch
        datt_ref[rows, :] = dot(d_branch, wout_ref[...], NT).astype(bf16)
        datt2_ref[rows, :] = dot(d_branch, wout2_ref[...], NT).astype(bf16)
        add = lambda values: jnp.sum(values, axis=0, keepdims=True)
        small_ref[0:1, :] += add(d_rows * unit)
        small_ref[1:2, :] += add(d_rows)
        small_ref[2:3, :] += add(dy)
        return 0

    def out_grads():
        for source, target in ((att_ref, gout_ref), (att2_ref, gout2_ref)):
            grad = dot(source[...].T, n2_ref[...]).astype(bf16)
            for a in range(wout_ref.shape[0] // LANES):
                for b in range(2):
                    rows = slice(a * LANES, (a + 1) * LANES)
                    cols = slice(b * lanes, (b + 1) * lanes)
                    spread = slice(a * lanes, (a + 1) * lanes)
                    target[b * LANES : (b + 1) * LANES, spread] = grad[rows, cols]

    def main(i, _):
        pl.when(i < tiles)(functools.partial(tile, i))

        @pl.when(jnp.logical_and(i >= tiles, i < tiles + 2))
        def _():
            first = (i - tiles) * (blocks // 2)
            lax.fori_loop(first, first + blocks // 2, epilogue, 0)

        @pl.when(i == tiles + 2)
        def _():
            for store in stores:
                store.start()
            out_grads()

        steps(i)
        return 0

    small_ref[...] = jnp.zeros_like(small_ref)
    stores = [
        pltpu.make_async_copy(source, target, store_sem.at[n])
        for n, (source, target) in enumerate(
            (
                (datt2_ref, datt2_hbm),
                (out_ref, out_hbm),
                (mid_ref, mid_hbm),
                (datt_ref, datt_hbm),
            )
        )
    ]
    lax.fori_loop(0, tiles + 4, main, 0)
    for store in stores:
        store.wait()

    def handed(slot, _):
        hand_down(slot).wait_send()
        return 0

    lax.fori_loop(0, count, handed, 0)


def middle(bits, x, att, att2, wout, wout2, dy, vectors, bup, ups, downs):
    rows, width = x.shape
    hidden = ups[0].shape[1]
    count = hidden // HIDDEN_TILE
    tiles = 2 * count
    exchanges = (
        Exchange(bits, count, HIDDEN_TILE, width, False),
        Exchange(bits, count, width, HIDDEN_TILE, False),
    )
    vmem = pl.BlockSpec(memory_space=pltpu.VMEM)
    hbm = pl.BlockSpec(memory_space=pl.ANY)
    shape = jax.ShapeDtypeStruct
    depth = wout.shape[0]
    return pl.pallas_call(
        functools.partial(middle_kernel, exchanges, tiles),
        in_specs=[vmem] * 8 + [hbm] * 5,
        out_specs=[hbm] * 4 + [vmem] * 5,
        out_shape=[
            shape((rows, width), bf16),
            shape((rows, width), f32),
            shape(att.shape, bf16),
            shape(att2.shape, bf16),
            shape((2 * LANES, depth // LANES * width // 2), bf16),
            shape((2 * LANES, depth // LANES * width // 2), bf16),
            shape((tiles, 1, HIDDEN_TILE), f32),
            shape((8, width), f32),
            shape((2 * count, PIECES, width), bf16),
        ],
        scratch_shapes=[
            pltpu.VMEM((count, width // 2, HIDDEN_TILE), bf16),
            pltpu.VMEM((count, HIDDEN_TILE // 2, width), bf16),
            pltpu.SemaphoreType.DMA((count, 4)),
            pltpu.SemaphoreType.DMA((count, 2)),
            pltpu.VMEM((2, width, HIDDEN_TILE), bf16),
            pltpu.VMEM((2, HIDDEN_TILE, width), bf16),
            pltpu.SemaphoreType.DMA((2, 6)),
            pltpu.VMEM((rows, width), bf16),
            pltpu.VMEM((rows, width), f32),
            pltpu.VMEM((rows, width), f32),
            pltpu.VMEM((rows, HIDDEN_TILE), bf16),
            pltpu.VMEM((rows, HIDDEN_TILE), bf16),
            pltpu.VMEM((width + PIECES, rows), bf16),
            pltpu.VMEM(bup.shape, f32),
            pltpu.SemaphoreType.DMA((2,)),
            pltpu.VMEM((rows, width), bf16),
            pltpu.VMEM((rows, width), f32),
            pltpu.VMEM(att.shape, bf16),
            pltpu.VMEM(att2.shape, bf16),
            pltpu.SemaphoreType.DMA((4,)),
            pltpu.VMEM((count, HIDDEN_TILE, width), bf16),
            pltpu.VMEM((count, width, HIDDEN_TILE), bf16),
        ]
        + exchanges[0].scratch()
        + exchanges[1].scratch(),
        compiler_params=pltpu.CompilerParams(
            collective_id=0, has_side_effects=True, vmem_limit_bytes=67043328
        ),
        name="middle",
        cost_estimate=pl.CostEstimate(
            flops=60 * 10**9, bytes_accessed=40 * 10**6, transcendentals=4 * 10**6
        ),
    )(x, att, att2, wout, wout2, dy, vectors, bup, *ups, *downs)


def leave_kernel(exchange, *refs):
    (
        rows_hbm,
        mine_out_ref,
        crossed_ref,
        crossed_out_ref,
        d_hbm,
        d2_hbm,
        w_hbm,
        w2_hbm,
        tokens_ref,
        context_ref,
        given_ref,
        vectors_ref,
        dmid_hbm,
        small_ref,
        small2_ref,
        gqkv_ref,
        gout_ref,
        back_ref,
        sums_ref,
        full_ref,
        out_buf,
        rows_t_ref,
        d_ref,
        d2_ref,
        w_ref,
        w2_ref,
        dmid_ref,
        load_sem,
        rows_ref,
        give_ref,
        take_ref,
        swap_sem,
        norm_ref,
        near_ref,
        far_ref,
        near_sem,
        far_sem,
        *rest,
    ) = refs
    place, part = lax.axis_index("dp"), lax.axis_index("mp")
    ex = exchange.bind(place, part, rest)
    count, bits = ex.count, ex.bits
    loads = [
        pltpu.make_async_copy(source, target, load_sem.at[n])
        for n, (source, target) in enumerate(
            (
                (d_hbm, d_ref),
                (rows_hbm, rows_t_ref),
                (w_hbm, w_ref),
                (w2_hbm, w2_ref),
                (d2_hbm, d2_ref),
                (dmid_hbm, dmid_ref),
            )
        )
    ]
    for load in loads:
        load.start()
    near_id = part * 4 + place % 4
    near = [
        {"dp": flip(place, j % 4), "mp": part if j < 4 else 1 - part} for j in range(1, 8)
    ]
    ex.partners += [near[j - 1] for j in (3, 5, 6, 7)]
    ex.greet()

    lanes = d_ref.shape[2]
    split = mine_out_ref.shape[1] // lanes
    for r in range(split):
        cols = slice(r * lanes, (r + 1) * lanes)
        total = mine_out_ref[:, cols].astype(f32) + crossed_out_ref[:, cols].astype(f32)
        out_buf[r] = total.astype(bf16)
        ex.start_a(r, 0, out_buf)
    step = HALF + 2 * EDGE

    def back_rows(n):
        start = CLEAN_OWN + n * (KEY_ROWS - step - CLEAN_OWN)
        rows = pl.ds(pl.multiple_of(start, EDGE), step)
        total = 0.0
        for grads, weights in ((d_ref, w_ref), (d2_ref, w2_ref)):
            for c in range(3):
                total = total + dot(grads[c, rows, :], weights[c], NT)
        rows_ref[rows, :] = total

    def grad_chunk(c):
        for r in range(split):
            rows = slice(r * ROW_TILE, (r + 1) * ROW_TILE)
            k = (c + 1) * split + r
            out_buf[k] = dot(rows_t_ref[rows, :], d_ref[c]).astype(bf16)
            ex.start_a(k, 0, out_buf)

    def stage_c(k):
        @pl.when(k >= split)
        def _():
            ex.stage_c(k, out_buf, lambda rows: crossed_ref[k - split, rows, :].astype(f32))

        @pl.when(k < split)
        def _():
            ex.stage_c(k, out_buf)

    def arrive(k):
        ex.stage_h(k, full_ref)

        @pl.when(k < split)
        def _():
            rows = pl.ds(pl.multiple_of(k * LANES, LANES), LANES)
            for b in range(2):
                piece = full_ref[k, b * LANES : (b + 1) * LANES, :]
                gout_ref[rows, b * lanes : (b + 1) * lanes] = piece

        @pl.when(k >= split)
        def _():
            n = k - split
            rows = pl.ds(pl.multiple_of(n % split * ROW_TILE, ROW_TILE), ROW_TILE)
            gqkv_ref[n // split, rows, :] = full_ref[k]

    def group(g, action):
        @pl.when(jnp.logical_and(g >= 0, g < count // split))
        def _():
            lax.fori_loop(g * split, (g + 1) * split, lambda k, _: (action(k), 0)[1], 0)

    def steps(i):
        group(i - 5, arrive)
        group(i - 4, lambda k: ex.stage_g(k, full_ref))
        group(i - 3, lambda k: ex.stage_f(k, full_ref))
        group(i - 2, lambda k: ex.stage_e(k, full_ref))
        group(i - 1, lambda k: ex.stage_d(k))
        group(i, stage_c)

    width = tokens_ref.shape[1]

    def swap(rows, lane):
        return pltpu.make_async_remote_copy(
            src_ref=give_ref.at[rows],
            dst_ref=take_ref.at[rows],
            send_sem=swap_sem.at[lane, 0],
            recv_sem=swap_sem.at[lane, 1],
            device_id=ex.across,
            device_id_type=MESH,
        )

    def sums_of(d_rows, units):
        add = lambda values: jnp.sum(values, axis=0, keepdims=True)
        norm_ref[0:1, :] += add(d_rows * units)
        norm_ref[1:2, :] += add(d_rows)

    main = slice(0, HALF)
    edges = slice(HALF, HALF + 2 * EDGE)
    parts = tokens_ref.shape[0] // TILE
    lead = small_ref.shape[0] - 2
    bias = lead - 3
    norm_ref[...] = jnp.zeros_like(norm_ref)
    for load in loads[:2]:
        load.wait()

    def own_at(b):
        start = jnp.where(b < TILES, NOISY_OWN + b * TILE, CLEAN_OWN + (b - TILES) * TILE)
        return pl.ds(pl.multiple_of(start, EDGE), TILE)

    def tokens_at(b):
        return pl.ds(pl.multiple_of(b * TILE, TILE), TILE)

    def ready():
        for load in loads[2:5]:
            load.wait()

    give_ref[main, :] = given_ref[...].astype(bf16)
    swap(main, 0).start()

    def give_edges():
        side = rows_ref[NOISY_BASE:NOISY_OWN, :] + rows_ref[NOISY_OWN + HALF :, :]
        after = rows_ref[2 * HALF : NOISY_BASE, :]
        give_ref[HALF : HALF + EDGE, :] = after.astype(bf16)
        give_ref[HALF + EDGE :, :] = side.astype(bf16)
        swap(edges, 1).start()
        sums_of(after, normal(context_ref[:EDGE, :].astype(f32))[0])
        sums_of(side, normal(context_ref[HALF:, :].astype(f32))[0])

    def tell_near():
        def context_sums(b, _):
            rows = tokens_at(b)
            sums_of(given_ref[rows, :], normal(context_ref[rows, :].astype(f32))[0])
            return 0

        lax.fori_loop(0, HALF // TILE, context_sums, 0)

        def own_sums(b, _):
            sums_of(rows_ref[own_at(b), :], normal(tokens_ref[tokens_at(b), :].astype(f32))[0])
            return 0

        lax.fori_loop(0, parts, own_sums, 0)
        blank = jnp.zeros((16 - lead - 2 - bias, width), f32)
        near_ref[near_id] = jnp.concatenate(
            [small_ref[:lead, :], norm_ref[:2, :], small2_ref[:bias, :], blank], axis=0
        ).astype(bf16)
        for j in range(1, 8):
            near_copy(j).start()

    def near_copy(j):
        return pltpu.make_async_remote_copy(
            src_ref=near_ref.at[near_id],
            dst_ref=near_ref.at[near_id],
            send_sem=near_sem.at[j, 0],
            recv_sem=near_sem.at[j, 1],
            device_id=near[j - 1],
            device_id_type=MESH,
        )

    def near_got(j):
        came = (part + j // 4) % 2 * 4 + flip(place % 4, j % 4)
        return pltpu.make_async_remote_copy(
            src_ref=near_ref.at[came],
            dst_ref=near_ref.at[came],
            send_sem=near_sem.at[j, 0],
            recv_sem=near_sem.at[j, 1],
            device_id=near[j - 1],
            device_id_type=MESH,
        )

    def far_copy(j, at):
        return pltpu.make_async_remote_copy(
            src_ref=far_ref.at[at],
            dst_ref=far_ref.at[at],
            send_sem=far_sem.at[j, 0],
            recv_sem=far_sem.at[j, 1],
            device_id=ex.peers[j - 1],
            device_id_type=MESH,
        )

    def tell_far():
        for j in range(1, 8):
            near_copy(j).wait_send()
            near_got(j).wait_recv()
        near_sum = lambda at: sum(near_ref[at + j].astype(f32) for j in range(1, 4)) + near_ref[
            at
        ].astype(f32)
        plane, other = near_sum(part * 4), near_sum((1 - part) * 4)
        total = near_sum(0) + near_sum(4)
        mixed = plane[:bias] + other[lead + 2 : lead + 2 + bias]
        far_ref[ex.z] = jnp.concatenate([mixed, total[bias:]], axis=0).astype(bf16)
        for j in range(1, 4):
            far_copy(j, ex.z).start()

    def take_back():
        loads[5].wait()
        swap(main, 0).wait()
        swap(edges, 1).wait()
        clean = slice(CLEAN_OWN, CLEAN_OWN + HALF)
        rows_ref[clean, :] += take_ref[main, :].astype(f32)
        begin = slice(CLEAN_OWN, CLEAN_OWN + EDGE)
        rows_ref[begin, :] += take_ref[HALF : HALF + EDGE, :].astype(f32)
        edge = pl.ds(pl.multiple_of(NOISY_OWN + (1 - part) * (HALF - EDGE), EDGE), EDGE)
        rows_ref[edge, :] += take_ref[HALF + EDGE :, :].astype(f32)

    def norm_back(b):
        rows = tokens_at(b)
        unit, scale = normal(tokens_ref[rows, :].astype(f32))
        lean = rows_ref[own_at(b), :] * vectors_ref[0:1, :]
        back_ref[rows, :] = dmid_ref[rows, :] + scale * (
            lean
            - jnp.mean(lean, axis=-1, keepdims=True)
            - unit * jnp.mean(lean * unit, axis=-1, keepdims=True)
        )

    def end_far():
        for j in range(1, 4):
            far_copy(j, ex.z).wait_send()
            far_copy(j, flip(ex.z, j)).wait_recv()
        total = far_ref[0].astype(f32)
        for j in range(1, 4):
            total = total + far_ref[j].astype(f32)
        for i, b in enumerate(ex.extra):
            total = total.astype(bf16).astype(f32)
            far_ref[4 + 2 * i] = total.astype(bf16)
            trade = pltpu.make_async_remote_copy(
                src_ref=far_ref.at[4 + 2 * i],
                dst_ref=far_ref.at[5 + 2 * i],
                send_sem=far_sem.at[4 + i, 0],
                recv_sem=far_sem.at[4 + i, 1],
                device_id={"dp": flip(place, 1 << b)},
                device_id_type=MESH,
            )
            trade.start()
            trade.wait()
            total = total + far_ref[5 + 2 * i].astype(f32)
        sums_ref[...] = total

    groups = count // split - 1
    actions = {
        groups + 1: give_edges,
        groups + 2: tell_near,
        groups + 3: take_back,
        groups + 6: tell_far,
    }
    begin_back = groups + 4

    def phase(p, _):
        @pl.when(p < groups)
        def _():
            grad_chunk(p)

        pl.when(p == groups)(ready)

        @pl.when(jnp.logical_and(p >= groups, p < groups + 2))
        def _():
            back_rows(p - groups)

        for n, action in actions.items():
            pl.when(p == n)(action)
        block = 2 * (p - begin_back)

        @pl.when(jnp.logical_and(block >= 0, block < parts))
        def _():
            lax.fori_loop(block, block + 2, lambda b, _: (norm_back(b), 0)[1], 0)

        pl.when(block == parts)(end_far)
        steps(p)
        return 0

    lax.fori_loop(0, begin_back + parts // 2 + 1, phase, 0)


def leave(bits, rows_t, mine, crossed, d_fields, weights, tokens, context, given, vectors, d_mid, small, small2):
    rows, cols = ROW_TILE, d_fields[0].shape[2]
    total = mine.shape[1] // cols + crossed[0].shape[0]
    exchange = Exchange(bits, total, rows, cols)
    count, width = tokens.shape
    vmem = pl.BlockSpec(memory_space=pltpu.VMEM)
    hbm = pl.BlockSpec(memory_space=pl.ANY)
    shape = jax.ShapeDtypeStruct
    return pl.pallas_call(
        functools.partial(leave_kernel, exchange),
        in_specs=[hbm] + [vmem] * 3 + [hbm] * 4 + [vmem] * 4 + [hbm] + [vmem] * 2,
        out_specs=[vmem] * 4,
        out_shape=[
            shape(weights[0].shape, bf16),
            shape((d_fields[0].shape[2], width), bf16),
            shape((count, width), f32),
            shape((16, width), f32),
        ],
        scratch_shapes=[
            pltpu.VMEM((total, rows, cols), bf16),
            pltpu.VMEM((total, rows, cols), bf16),
            pltpu.VMEM(rows_t.shape, bf16),
            pltpu.VMEM(d_fields[0].shape, bf16),
            pltpu.VMEM(d_fields[1].shape, bf16),
            pltpu.VMEM(weights[0].shape, bf16),
            pltpu.VMEM(weights[1].shape, bf16),
            pltpu.VMEM(d_mid.shape, f32),
            pltpu.SemaphoreType.DMA((6,)),
            pltpu.VMEM((KEY_ROWS, width), f32),
            pltpu.VMEM((HALF + 2 * EDGE, width), bf16),
            pltpu.VMEM((HALF + 2 * EDGE, width), bf16),
            pltpu.SemaphoreType.DMA((2, 2)),
            pltpu.VMEM((8, width), f32),
            pltpu.VMEM((8, 16, width), bf16),
            pltpu.VMEM((4 + 2 * len(exchange.extra), 16, width), bf16),
            pltpu.SemaphoreType.DMA((8, 2)),
            pltpu.SemaphoreType.DMA((4 + len(exchange.extra), 2)),
        ]
        + exchange.scratch(),
        compiler_params=pltpu.CompilerParams(
            collective_id=1, has_side_effects=True, vmem_limit_bytes=67043328
        ),
        name="leave",
        cost_estimate=pl.CostEstimate(
            flops=40 * 10**9, bytes_accessed=40 * 10**6, transcendentals=0
        ),
    )(
        rows_t, mine, *crossed, *d_fields, *weights, tokens, context, given, vectors, d_mid, small, small2
    )


def assemble_kernel(core_ref, down_mine, up_mine, down_got, up_got, down_ref, up_ref):
    core = core_ref[0]
    block = down_mine.shape[1]
    lanes = up_ref.shape[1]
    parts = down_mine.shape[2] // lanes
    deep = block * parts
    for side, down, up in ((core, down_mine, up_mine), (1 - core, down_got, up_got)):
        rows = pl.ds(pl.multiple_of(side * block, block), block)
        down_ref[rows, :] = down[0].astype(f32)
        for n in range(block // PIECES):
            for c in range(parts):
                at = side * deep + (n * parts + c) * PIECES
                rows = pl.ds(pl.multiple_of(at, PIECES), PIECES)
                piece = up[0, n * PIECES : (n + 1) * PIECES, c * lanes : (c + 1) * lanes]
                up_ref[rows, :] = piece.astype(f32)


def assemble(core, gathered, moved):
    tiles, half, width = gathered.shape
    count = tiles // 2
    down_spec = pl.BlockSpec((1, half, width), lambda k, c: (k, 0, 0))
    up_spec = pl.BlockSpec((1, half, width), lambda k, c: (count + k, 0, 0))
    hidden = count * 2 * half
    return pl.pallas_call(
        assemble_kernel,
        grid_spec=pltpu.PrefetchScalarGridSpec(
            num_scalar_prefetch=1,
            grid=(count,),
            in_specs=[down_spec, up_spec, down_spec, up_spec],
            out_specs=[
                pl.BlockSpec((2 * half, width), lambda k, c: (k, 0)),
                pl.BlockSpec((width, 2 * half), lambda k, c: (0, k)),
            ],
        ),
        out_shape=[
            jax.ShapeDtypeStruct((hidden, width), f32),
            jax.ShapeDtypeStruct((width, hidden), f32),
        ],
        name="assemble",
        cost_estimate=pl.CostEstimate(
            flops=10**6, bytes_accessed=14 * 10**6, transcendentals=0
        ),
    )(core, gathered, gathered, moved, moved)


def key_layout(seq_lengths, block_len, part):
    index = jnp.arange(KEY_ROWS, dtype=jnp.int32)
    own = part * HALF
    token = jnp.where(
        index < NOISY_BASE, index + (own - HALF), index - NOISY_BASE + (own - EDGE)
    )
    ends = jnp.cumsum(seq_lengths)
    passed = token[:, None] >= ends[None, :]
    starts = jnp.sum(jnp.where(passed, seq_lengths[None, :], 0), axis=1)
    lengths_here = jnp.where(passed, 0, ends[None, :])
    stops = jnp.min(jnp.where(passed, TOK_DEV, lengths_here), axis=1)
    positions = token - starts
    block_start = starts + positions // block_len * block_len
    block_stop = jnp.minimum(block_start + block_len, stops)
    mine = slice(CLEAN_OWN, CLEAN_OWN + HALF)
    low, start, stop = starts[mine], block_start[mine], block_stop[mine]
    to_clean = own - HALF
    tiles = lambda column: column.reshape(TILES, 1, TILE)
    clean_bounds = jnp.concatenate(
        [
            jnp.concatenate([tiles(low - to_clean), tiles(low - to_clean)], axis=2),
            jnp.concatenate([tiles(start - to_clean), tiles(stop - to_clean)], axis=2),
        ],
        axis=1,
    )
    to_window = own - EDGE + TILE * jnp.arange(TILES, dtype=jnp.int32)[:, None, None]
    noisy_bounds = jnp.concatenate(
        [tiles(start) - to_window, tiles(stop) - to_window], axis=1
    )
    first = jnp.min(clean_bounds[:, 0], axis=1) // EDGE * EDGE
    last = jnp.max(clean_bounds[:, 1], axis=1)
    trips = (last - first + KEY_TILE - 1) // KEY_TILE
    spans = jnp.stack([first, trips], axis=1)
    lane = jnp.arange(LANES, dtype=jnp.int32)
    frequency = jnp.exp(
        (lane % (HD // 2)).astype(f32) * (-math.log(10000.0) / (HD // 2))
    )
    angles = positions.astype(f32)[:, None] * frequency[None, :]
    sign = jnp.where(lane % HD < HD // 2, -1.0, 1.0)
    return spans, clean_bounds, noisy_bounds, jnp.cos(angles), jnp.sin(angles) * sign


def in_order(bit, mine, theirs, axis=0):
    order = bit == 0
    return jnp.concatenate(
        [jnp.where(order, mine, theirs), jnp.where(order, theirs, mine)], axis=axis
    )


def tie(first, second):
    return lax.optimization_barrier((first, second))


def local(
    dp_size,
    tokens,
    lengths,
    block_size,
    cotangent,
    ln1_gain,
    ln1_bias,
    w_qkv,
    w_out,
    ln2_gain,
    ln2_bias,
    w_up,
    b_up,
    w_down,
    b_down,
):
    width = tokens.shape[2]
    part = lax.axis_index("mp")
    place = lax.axis_index("dp")
    bits = dp_size.bit_length() - 1
    core = place & 1

    def across(array):
        return lax.ppermute(array, "mp", [(0, 1), (1, 0)])

    def sibling(array):
        return lax.ppermute(array, "dp", [(i, i ^ 1) for i in range(dp_size)])

    def beside(array):
        return lax.ppermute(array, "dp", [(i, i ^ 2) for i in range(dp_size)])

    edge = jnp.where(part == 0, tokens[0, HALF - EDGE :], tokens[0, :EDGE])
    context = across(jnp.concatenate([tokens[1], edge], axis=0))
    qkv_mine = w_qkv.transpose(1, 0, 2)
    side = (place >> 1) & 1

    def quarter_of(array, axis=0):
        size = array.shape[axis] // 4
        return lax.dynamic_slice_in_dim(array, (2 * core + side) * size, size, axis)

    def half_of(array):
        size = array.shape[0] // 2
        return lax.dynamic_slice_in_dim(array, core * size, size, 0)

    quarters = [quarter_of(qkv_mine, 1), quarter_of(w_up), half_of(w_down), half_of(w_out)]
    layout = key_layout(lengths[0], block_size[0], part)
    vectors = jnp.stack([ln1_gain, ln1_bias, ln2_gain, ln2_bias, b_down])
    context, (quarters, layout, vectors) = tie(context, (quarters, layout, vectors))
    qkv_here, up_here, down_here, out_here = [across(piece) for piece in quarters]

    spans, clean_bounds, noisy_bounds, cosine, sine = layout
    normed1, normed1_t, *fields = enter(tokens, context, vectors, qkv_mine, cosine, sine)
    qkv_here, fields = tie(qkv_here, fields)
    qkv_beside = beside(qkv_here)
    mine = [*fields, *attend_forward(spans, clean_bounds, noisy_bounds, *fields)]
    (qkv_here, qkv_beside, up_here), _ = tie((qkv_here, qkv_beside, up_here), mine[3])
    qkv_half = in_order(side, qkv_here, qkv_beside, axis=1)
    qkv_other = in_order(core, qkv_half, sibling(qkv_half), axis=1)
    up_beside = beside(up_here)
    fields = project(normed1, qkv_other, cosine, sine)
    other = [*fields, *attend_forward(spans, clean_bounds, noisy_bounds, *fields)]
    (out_here, up_here, up_beside, down_here), _ = tie(
        (out_here, up_here, up_beside, down_here), other[3]
    )
    out_other = in_order(core, out_here, sibling(out_here))
    bias_all = b_up.astype(f32).reshape(-1, 1, HIDDEN_TILE)

    x_rows = tokens.reshape(TOK_DEV, width)
    out, d_mid, d_att, d_att2, grad_out, grad_out2, grad_bias, norms, pieces = middle(
        bits,
        x_rows,
        mine[3],
        other[3],
        w_out,
        out_other,
        cotangent.reshape(TOK_DEV, width),
        vectors,
        bias_all,
        (w_up, up_here, up_beside),
        (w_down, down_here),
    )
    hidden = b_up.shape[0]

    crossed_out = across(grad_out2)
    spread = [(b, min(2, min(bits, 4) - b)) for b in range(2, min(bits, 4), 2)]
    gathered = pieces
    ((first_bit, n),) = spread
    moved = [
        lax.ppermute(gathered, "dp", [(i, i ^ (k << first_bit)) for i in range(dp_size)])
        for k in range(1, 1 << n)
    ]

    def backward(saved, d_attended, spans, *rest):
        query, keys, values, attended, lse = saved
        return attend_backward(
            spans,
            clean_bounds,
            noisy_bounds,
            query,
            keys,
            values,
            attended,
            d_attended,
            lse,
            cosine,
            sine,
            rest,
        )

    d_fields2, grad2 = backward(other, d_att2, spans, normed1_t)
    grad2 = grad2.reshape(-1, ROW_TILE, grad2.shape[2])
    low_bit, high_bit = (place >> 2) & 1, (place >> 3) & 1
    moved, _ = tie(moved, grad2)
    gathered = in_order(
        high_bit,
        in_order(low_bit, gathered, moved[0], 1),
        in_order(low_bit, moved[1], moved[2], 1),
        1,
    )
    half = ROW_TILE // 2
    part_of = lambda array, which: lax.dynamic_slice_in_dim(array, which * half, half, 1)
    got = sibling(part_of(grad2, 1 - core))
    crossing = (part_of(grad2, core).astype(f32) + got.astype(f32)).astype(bf16)
    (crossing, gathered), spans = tie((crossing, gathered), spans)
    crossed = across(crossing)
    moved = beside(gathered)
    d_fields1, given = backward(mine, d_att, spans, d_fields2, qkv_mine, qkv_other)
    moved, d_fields1 = tie(moved, d_fields1)
    gathered = in_order(side, gathered, moved, 1)
    gathered, d_fields1 = tie(gathered, d_fields1)
    moved = sibling(gathered)
    lead = hidden // width
    bias2, bias1 = grad_bias.reshape(2, lead, width)
    shared = jnp.concatenate([norms[:3], jnp.zeros((2, width), f32)], axis=0)
    grad_qkv, grad_out, grad_tokens, sums = leave(
        bits,
        normed1_t,
        grad_out,
        (crossed, crossed_out),
        (d_fields1, d_fields2),
        (qkv_mine, qkv_other),
        x_rows,
        context,
        given,
        vectors,
        d_mid,
        jnp.concatenate([bias1, shared], axis=0),
        jnp.concatenate([bias2, shared], axis=0),
    )
    moved, _ = tie(moved, grad_qkv)
    grad_down, grad_up = assemble(core.reshape(1), gathered, moved)
    return (
        out.reshape(tokens.shape),
        grad_tokens.reshape(tokens.shape),
        sums[lead + 3],
        sums[lead + 4],
        grad_qkv.transpose(1, 0, 2).astype(f32),
        grad_out.astype(f32),
        sums[lead],
        sums[lead + 1],
        grad_up,
        sums[:lead].reshape(hidden),
        grad_down,
        sums[lead + 2],
    )


def solution(mesh):
    in_specs = (
        P(None, ("dp", "mp"), None),
        P("dp", None),
        P(),
        P(None, ("dp", "mp"), None),
        P(),
        P(),
        P(None, None, "mp"),
        P("mp", None),
        P(),
        P(),
        P(None, "mp"),
        P("mp"),
        P("mp", None),
        P(),
    )
    out_specs = (
        P(None, ("dp", "mp"), None),
        P(None, ("dp", "mp"), None),
        P(),
        P(),
        P(None, None, "mp"),
        P("mp", None),
        P(),
        P(),
        P(None, "mp"),
        P("mp"),
        P("mp", None),
        P(),
    )
    return jax.shard_map(
        functools.partial(local, mesh.shape["dp"]),
        mesh=mesh,
        in_specs=in_specs,
        out_specs=out_specs,
        check_vma=False,
    )
```

```python
import functools
import math

import jax
import jax.numpy as jnp
from jax import lax
from jax.experimental import pallas as pl
from jax.experimental.pallas import tpu as pltpu
from jax.sharding import PartitionSpec as P

HD = 64
TOK_DEV = 1024
HALF = TOK_DEV // 2
EDGE = 16
CLEAN_OWN = HALF
NOISY_BASE = 2 * HALF + EDGE
NOISY_OWN = NOISY_BASE + EDGE
KEY_ROWS = NOISY_OWN + HALF + EDGE
TILE = 128
TILES = HALF // TILE
WINDOW = TILE + 2 * EDGE
KEY_TILE = 192
LANES = 128
HIDDEN_TILE = 256
ROW_TILE = 256

epsilon = 1e-05
neg_large = -1e30
to_base2 = 0.125 * math.log2(math.e)
f32 = jnp.float32
bf16 = jnp.bfloat16

NN = (((1,), (0,)), ((), ()))
NT = (((1,), (1,)), ((), ()))


def dot(left, right, dims=NN):
    return lax.dot_general(left, right, dims, preferred_element_type=f32)


def low_lanes(shape):
    return lax.broadcasted_iota(jnp.int32, shape, 1) < HD


def turn(values, cosine, sine):
    lane = lax.broadcasted_iota(jnp.int32, values.shape, 1)
    first_half = (lane & (HD - 1)) < HD // 2
    swapped = jnp.where(
        first_half,
        pltpu.roll(values, LANES - HD // 2, 1),
        pltpu.roll(values, HD // 2, 1),
    )
    return values * cosine + swapped * sine


def project_rows(rows, w_ref, cosine, sine, q_ref, k_ref, v_ref, at):
    for part, out_ref in ((0, q_ref), (1, k_ref)):
        field = dot(rows, w_ref[part])
        for pair in range(field.shape[1] // LANES):
            cols = slice(pair * LANES, (pair + 1) * LANES)
            out_ref[at, cols] = turn(field[:, cols], cosine, sine).astype(bf16)
    v_ref[at, :] = dot(rows, w_ref[2]).astype(bf16)


def project_kernel(rows_ref, w_ref, cos_ref, sin_ref, q_ref, k_ref, v_ref):
    at = slice(0, rows_ref.shape[0])
    project_rows(rows_ref[...], w_ref, cos_ref[...], sin_ref[...], q_ref, k_ref, v_ref, at)


def project(rows, weights, cosine, sine):
    count, width = rows.shape
    cols = weights.shape[2]
    step = count // 3
    row_spec = pl.BlockSpec((step, width), lambda i: (i, 0))
    table_spec = pl.BlockSpec((step, LANES), lambda i: (i, 0))
    out_spec = pl.BlockSpec((step, cols), lambda i: (i, 0))
    shape = jax.ShapeDtypeStruct((count, cols), bf16)
    return pl.pallas_call(
        project_kernel,
        grid=(3,),
        in_specs=[
            row_spec,
            pl.BlockSpec(weights.shape, lambda i: (0, 0, 0)),
            table_spec,
            table_spec,
        ],
        out_specs=[out_spec] * 3,
        out_shape=[shape] * 3,
        name="project",
        cost_estimate=pl.CostEstimate(
            flops=2 * count * width * 3 * cols,
            bytes_accessed=2 * (count * (width + 3 * cols) + 3 * width * cols),
            transcendentals=0,
        ),
    )(rows, weights, cosine, sine)


def normal(values):
    average = jnp.mean(values, axis=-1, keepdims=True)
    centred = values - average
    variance = jnp.mean(centred * centred, axis=-1, keepdims=True)
    scale = lax.rsqrt(variance + epsilon)
    return centred * scale, scale


def enter_kernel(
    tokens_ref,
    context_ref,
    vectors_ref,
    w_ref,
    cos_ref,
    sin_ref,
    rows_ref,
    rows_t_ref,
    q_ref,
    k_ref,
    v_ref,
):
    def norm(values):
        unit = normal(values.astype(f32))[0]
        return (unit * vectors_ref[0:1, :] + vectors_ref[1:2, :]).astype(bf16)

    def blocks(i, _):
        source = pl.ds(pl.multiple_of(i * TILE, TILE), TILE)
        rows_ref[source, :] = norm(context_ref[source, :])
        at = pl.ds(pl.multiple_of(CLEAN_OWN + i * TILE, TILE), TILE)
        rows_ref[at, :] = norm(tokens_ref[1, source, :])
        at = pl.ds(pl.multiple_of(NOISY_OWN + i * TILE, EDGE), TILE)
        rows_ref[at, :] = norm(tokens_ref[0, source, :])
        return 0

    lax.fori_loop(0, TILES, blocks, 0)
    rows_ref[2 * HALF : NOISY_BASE, :] = rows_ref[:EDGE, :]
    edge = norm(context_ref[HALF:, :])
    rows_ref[NOISY_BASE:NOISY_OWN, :] = edge
    rows_ref[NOISY_OWN + HALF :, :] = edge
    step = KEY_ROWS // 3

    def fields(i, _):
        at = pl.ds(pl.multiple_of(i * step, EDGE), step)
        project_rows(
            rows_ref[at, :], w_ref, cos_ref[at, :], sin_ref[at, :], q_ref, k_ref, v_ref, at
        )
        return 0

    lax.fori_loop(0, 3, fields, 0)
    for c in range(rows_t_ref.shape[0] // LANES):
        cols = slice(c * LANES, (c + 1) * LANES)
        rows_t_ref[cols, :] = rows_ref[:, cols].T


def enter(tokens, context, vectors, weights, cosine, sine):
    width, cols = weights.shape[1:]
    vmem = pl.BlockSpec(memory_space=pltpu.VMEM)
    shape = jax.ShapeDtypeStruct
    field = shape((KEY_ROWS, cols), bf16)
    return pl.pallas_call(
        enter_kernel,
        in_specs=[vmem] * 6,
        out_specs=[vmem] * 5,
        out_shape=[shape((KEY_ROWS, width), bf16), shape((width, KEY_ROWS), bf16)] + [field] * 3,
        name="enter",
        cost_estimate=pl.CostEstimate(
            flops=10**10, bytes_accessed=16 * 10**6, transcendentals=0
        ),
    )(tokens, context, vectors, weights, cosine, sine)


def split_heads(rows):
    low = low_lanes(rows.shape)
    zero = jnp.zeros_like(rows)
    return jnp.where(low, rows, zero), jnp.where(low, zero, rows)


def between(shape, offset, low, high):
    index = lax.broadcasted_iota(jnp.int32, shape, 0) + offset
    return jnp.logical_and(index >= low, index < high)


def fold(values, combine):
    rows, cols = values.shape
    groups = values.reshape(rows // 8, 8, cols)
    return combine(groups, axis=0)


def forward_kernel(
    span_ref, clean_ref, noisy_ref, q_ref, k_ref, v_ref, out_ref, lse_ref, bias_ref, window_ref
):
    pairs = q_ref.shape[1] // LANES
    lanes = [slice(p * LANES, (p + 1) * LANES) for p in range(pairs)]

    def one_tile(t, _):
        clean_at = pl.multiple_of(CLEAN_OWN + t * TILE, TILE)
        noisy_at = pl.multiple_of(NOISY_OWN + t * TILE, EDGE)
        window_at = pl.multiple_of(NOISY_BASE + t * TILE, EDGE)
        key_low, key_high = clean_ref[t, 0:1, :], clean_ref[t, 1:2, :]
        own_low, own_high = noisy_ref[t, 0:1, :], noisy_ref[t, 1:2, :]
        allowed = between((WINDOW, TILE), 0, own_low, own_high)
        window_ref[...] = jnp.where(allowed, 0.0, neg_large)
        first_key, trips = span_ref[t, 0], span_ref[t, 1]
        queries, tops = [], []
        for cols in lanes:
            query = jnp.concatenate(
                [q_ref[pl.ds(noisy_at, TILE), cols], q_ref[pl.ds(clean_at, TILE), cols]], axis=0
            )
            heads = split_heads(query)
            queries += heads
            keys = k_ref[pl.ds(window_at, WINDOW), cols]
            for head in range(2):
                scores = dot(keys, heads[head][:TILE], NT) + window_ref[...]
                top = fold(scores, jnp.max)
                tops.append(
                    jnp.concatenate([top, jnp.full((8, TILE), neg_large, f32)], axis=1)
                )

        def first_pass(j, tops):
            at = pl.multiple_of(first_key + j * KEY_TILE, EDGE)
            allowed = between((KEY_TILE, 2 * TILE), at, key_low, key_high)
            bias_ref[j] = jnp.where(allowed, 0.0, neg_large)
            after = []
            for p, cols in enumerate(lanes):
                keys = k_ref[pl.ds(at, KEY_TILE), cols]
                for head in range(2):
                    scores = dot(keys, queries[2 * p + head], NT) + bias_ref[j]
                    after.append(jnp.maximum(tops[2 * p + head], fold(scores, jnp.max)))
            return tuple(after)

        tops = lax.fori_loop(0, trips, first_pass, tuple(tops))
        tops = [jnp.max(top, axis=0, keepdims=True) * to_base2 for top in tops]
        state = []
        keys = [k_ref[pl.ds(window_at, WINDOW), cols] for cols in lanes]
        values_t = [v_ref[pl.ds(window_at, WINDOW), cols].T for cols in lanes]
        scores = dot(keys[0], queries[0][:TILE], NT)
        late = None
        for h in range(2 * pairs):
            if h + 1 < 2 * pairs:
                ahead = dot(keys[(h + 1) // 2], queries[h + 1][:TILE], NT)
            expo = jnp.exp2(scores * to_base2 - tops[h][:, :TILE] + window_ref[...])
            if late is not None:
                state.append(jnp.concatenate([late, jnp.zeros((HD, TILE), f32)], axis=1))
            total = fold(expo, jnp.sum)
            state.append(jnp.concatenate([total, jnp.zeros((8, TILE), f32)], axis=1))
            side = slice(h % 2 * HD, (h % 2 + 1) * HD)
            late = dot(values_t[h // 2][side], expo.astype(bf16))
            scores = ahead
        state.append(jnp.concatenate([late, jnp.zeros((HD, TILE), f32)], axis=1))

        def second_pass(j, state):
            at = pl.multiple_of(first_key + j * KEY_TILE, EDGE)
            keys = [k_ref[pl.ds(at, KEY_TILE), cols] for cols in lanes]
            values_t = [v_ref[pl.ds(at, KEY_TILE), cols].T for cols in lanes]
            after = list(state)
            scores = dot(keys[0], queries[0], NT)
            late = None
            for h in range(2 * pairs):
                ahead = dot(keys[(h + 1) // 2], queries[h + 1], NT) if h + 1 < 2 * pairs else None
                expo = jnp.exp2(scores * to_base2 - tops[h] + bias_ref[j])
                after[2 * h] = state[2 * h] + fold(expo, jnp.sum)
                if late is not None:
                    after[2 * h - 1] = state[2 * h - 1] + late
                side = slice(h % 2 * HD, (h % 2 + 1) * HD)
                late = dot(values_t[h // 2][side], expo.astype(bf16))
                scores = ahead
            after[-1] = state[-1] + late
            return tuple(after)

        state = lax.fori_loop(0, trips, second_pass, tuple(state))
        low_at = pl.ds(pl.multiple_of(t * TILE, TILE), TILE)
        high_at = pl.ds(pl.multiple_of(HALF + t * TILE, TILE), TILE)
        for p, cols in enumerate(lanes):
            halves = []
            for head in range(2):
                h = 2 * p + head
                total = jnp.sum(state[2 * h], axis=0, keepdims=True)
                halves.append(state[2 * h + 1] / total)
                lse_ref[p, t, head : head + 1, :] = tops[h] + jnp.log2(total)
            pair = jnp.concatenate(halves, axis=0).T.astype(bf16)
            out_ref[low_at, cols] = pair[:TILE]
            out_ref[high_at, cols] = pair[TILE:]
        return 0

    lax.fori_loop(0, TILES, one_tile, 0)


def attend_forward(spans, clean_bounds, noisy_bounds, query, keys, values):
    count, cols = query.shape
    pairs = cols // LANES
    vmem = pl.BlockSpec(memory_space=pltpu.VMEM)
    work = pairs * 2 * 2 * HALF * TOK_DEV
    return pl.pallas_call(
        forward_kernel,
        in_specs=[pl.BlockSpec(memory_space=pltpu.SMEM)] + [vmem] * 5,
        out_specs=[vmem] * 2,
        out_shape=[
            jax.ShapeDtypeStruct((TOK_DEV, cols), bf16),
            jax.ShapeDtypeStruct((pairs, TILES, 2, 2 * TILE), f32),
        ],
        scratch_shapes=[
            pltpu.VMEM((NOISY_BASE // KEY_TILE + 1, KEY_TILE, 2 * TILE), f32),
            pltpu.VMEM((WINDOW, TILE), f32),
        ],
        name="attend_forward",
        cost_estimate=pl.CostEstimate(
            flops=4 * work * HD, bytes_accessed=8 * count * cols, transcendentals=work
        ),
    )(spans, clean_bounds, noisy_bounds, query, keys, values)


def backward_kernel(
    giving,
    span_ref,
    clean_ref,
    noisy_ref,
    q_ref,
    k_ref,
    v_ref,
    o_ref,
    d_ref,
    lse_ref,
    cos_ref,
    sin_ref,
    *refs,
):
    if giving:
        d2_hbm, w_hbm, w2_hbm, out_ref, give_ref, low_ref, *refs = refs
        dk_ref, dv_ref, bias_ref, d2_ref, w_ref, w2_ref, load_sem = refs
        loads = [(w_hbm, w_ref), (w2_hbm, w2_ref)]
        loads += [(d2_hbm.at[c, :HALF], d2_ref.at[c]) for c in range(3)]
        loads = [
            pltpu.make_async_copy(source, target, load_sem.at[n])
            for n, (source, target) in enumerate(loads)
        ]
        for load in loads:
            load.start()
    else:
        rows_ref, out_ref, grad_ref, dk_ref, dv_ref, bias_ref = refs
    pairs = q_ref.shape[1] // LANES
    lanes = [slice(p * LANES, (p + 1) * LANES) for p in range(pairs)]
    dk_ref[...] = jnp.zeros_like(dk_ref)
    dv_ref[...] = jnp.zeros_like(dv_ref)
    out_ref[0] = jnp.zeros_like(out_ref[0])

    def one_tile(t, _):
        clean_at = pl.multiple_of(CLEAN_OWN + t * TILE, TILE)
        noisy_at = pl.multiple_of(NOISY_OWN + t * TILE, EDGE)
        window_at = pl.multiple_of(NOISY_BASE + t * TILE, EDGE)
        low_at = pl.multiple_of(t * TILE, TILE)
        high_at = pl.multiple_of(HALF + t * TILE, TILE)
        key_low, key_high = clean_ref[t, 0:1, :], clean_ref[t, 1:2, :]
        own_low, own_high = noisy_ref[t, 0:1, :], noisy_ref[t, 1:2, :]
        queries, d_outs, inners, lses = [], [], [], []
        for p, cols in enumerate(lanes):

            def both(ref, low, high):
                return jnp.concatenate(
                    [ref[pl.ds(low, TILE), cols], ref[pl.ds(high, TILE), cols]], axis=0
                )

            queries.append(split_heads(both(q_ref, noisy_at, clean_at)))
            d_rows = both(d_ref, low_at, high_at)
            o_rows = both(o_ref, low_at, high_at)
            product = (d_rows.astype(f32) * o_rows.astype(f32)).T
            d_outs.append(split_heads(d_rows))
            inners.append(
                [
                    jnp.sum(product[head * HD : (head + 1) * HD], axis=0, keepdims=True) * 0.125
                    for head in range(2)
                ]
            )
            lses.append([lse_ref[p, t, head : head + 1, :] for head in range(2)])

        def accumulate(at, rows, cols, allowed, d_query):
            bias_ref[:rows, :cols] = jnp.where(allowed, 0.0, neg_large)
            after = list(d_query)
            keys = [k_ref[pl.ds(at, rows), span] for span in lanes]
            eighth = [v_ref[pl.ds(at, rows), span] * jnp.asarray(0.125, bf16) for span in lanes]
            keys_t = [part.T for part in keys]
            stack = lambda parts: jnp.concatenate([part[:cols] for part in parts], axis=0)

            def begin(h):
                p, head = h // 2, h % 2
                return (
                    dot(keys[p], queries[p][head][:cols], NT),
                    dot(eighth[p], d_outs[p][head][:cols], NT),
                )

            def finish_pair(p, weights, d_scores):
                span = lanes[p]
                for head in range(2):
                    side = slice(head * HD, (head + 1) * HD)
                    h = 2 * p + head
                    after[h] = d_query[h] + dot(keys_t[p][side], d_scores[head])
                dv_ref[pl.ds(at, rows), span] += dot(
                    jnp.concatenate(weights, axis=1), stack(d_outs[p])
                )
                dk_ref[pl.ds(at, rows), span] += dot(
                    jnp.concatenate(d_scores, axis=1), stack(queries[p])
                )

            ready = begin(0)
            held = None
            weights, d_scores = [], []
            for h in range(2 * pairs):
                ahead = begin(h + 1) if h + 1 < 2 * pairs else None
                p, head = h // 2, h % 2
                scores = ready[0] * to_base2 - lses[p][head][:, :cols] + bias_ref[:rows, :cols]
                probs = jnp.exp2(scores)
                d_score = (probs * (ready[1] - inners[p][head][:, :cols])).astype(bf16)
                weights.append(probs.astype(bf16))
                d_scores.append(d_score)
                if held is not None:
                    finish_pair(*held)
                    held = None
                if head == 1:
                    held = (p, weights, d_scores)
                    weights, d_scores = [], []
                ready = ahead
            finish_pair(*held)
            return tuple(after)

        allowed = between((WINDOW, TILE), 0, own_low, own_high)
        zero = jnp.zeros((HD, TILE), f32)
        start = accumulate(window_at, WINDOW, TILE, allowed, (zero,) * (2 * pairs))
        start = tuple(jnp.concatenate([part, zero], axis=1) for part in start)
        first_key, trips = span_ref[t, 0], span_ref[t, 1]

        def one_step(j, d_query):
            at = pl.multiple_of(first_key + j * KEY_TILE, EDGE)
            allowed = between((KEY_TILE, 2 * TILE), at, key_low, key_high)
            return accumulate(at, KEY_TILE, 2 * TILE, allowed, d_query)

        d_query = lax.fori_loop(0, trips, one_step, start)
        for p, span in enumerate(lanes):
            pair = jnp.concatenate(d_query[2 * p : 2 * p + 2], axis=0).T
            for at, part in ((noisy_at, pair[:TILE]), (clean_at, pair[TILE:])):
                turned = turn(part, cos_ref[pl.ds(at, TILE), :], -sin_ref[pl.ds(at, TILE), :])
                out_ref[0, pl.ds(at, TILE), span] = turned.astype(bf16)
        return 0

    lax.fori_loop(0, TILES, one_tile, 0)
    step = KEY_ROWS // 9

    def finish(i, _):
        rows = pl.ds(pl.multiple_of(i * step, EDGE), step)
        for span in lanes:
            out_ref[1, rows, span] = turn(
                dk_ref[rows, span], cos_ref[rows, :], -sin_ref[rows, :]
            ).astype(bf16)
        out_ref[2, rows, :] = dv_ref[rows, :].astype(bf16)
        return 0

    lax.fori_loop(0, 9, finish, 0)

    def weight_rows(i, _):
        rows = pl.ds(pl.multiple_of(i * ROW_TILE, LANES), ROW_TILE)
        for c in range(3):
            grad_ref[c, rows, :] = dot(rows_ref[rows, :], out_ref[c]).astype(bf16)
        return 0

    if giving:
        for load in loads:
            load.wait()
        total = 0.0
        for c in range(3):
            total = total + dot(out_ref[c, :HALF, :], w_ref[c], NT) + dot(d2_ref[c], w2_ref[c], NT)
        give_ref[...] = total
        low_ref[...] = total.astype(bf16)
    else:
        lax.fori_loop(0, rows_ref.shape[0] // ROW_TILE, weight_rows, 0)


def attend_backward(
    spans,
    clean_bounds,
    noisy_bounds,
    query,
    keys,
    values,
    attended,
    d_attended,
    lse,
    cosine,
    sine,
    rest,
):
    count, cols = query.shape
    vmem = pl.BlockSpec(memory_space=pltpu.VMEM)
    hbm = pl.BlockSpec(memory_space=pl.ANY)
    shape = jax.ShapeDtypeStruct
    giving = len(rest) > 1
    if giving:
        width = rest[1].shape[1]
        second = [shape((HALF, width), f32), shape((HALF, width), bf16)]
        scratch = [
            pltpu.VMEM((3, HALF, cols), bf16),
            pltpu.VMEM(rest[1].shape, bf16),
            pltpu.VMEM(rest[2].shape, bf16),
            pltpu.SemaphoreType.DMA((5,)),
        ]
    else:
        second = [shape((3, rest[0].shape[0], cols), bf16)]
        scratch = []
    return pl.pallas_call(
        functools.partial(backward_kernel, giving),
        in_specs=[pl.BlockSpec(memory_space=pltpu.SMEM)]
        + [vmem] * 10
        + [hbm if giving else vmem] * len(rest),
        out_specs=[vmem] * (1 + len(second)),
        scratch_shapes=[
            pltpu.VMEM((count, cols), f32),
            pltpu.VMEM((count, cols), f32),
            pltpu.VMEM((max(KEY_TILE, WINDOW), 2 * TILE), f32),
        ]
        + scratch,
        out_shape=[shape((3, count, cols), bf16)] + second,
        name="attend_backward",
        cost_estimate=pl.CostEstimate(
            flops=36 * 10**9, bytes_accessed=36 * 10**6, transcendentals=6 * 10**6
        ),
    )(
        spans,
        clean_bounds,
        noisy_bounds,
        query,
        keys,
        values,
        attended,
        d_attended,
        lse,
        cosine,
        sine,
        *rest,
    )


PIECES = 16
MESH = pl.DeviceIdType.MESH


def flip(value, mask):
    result = value
    for b in range(mask.bit_length()):
        if mask >> b & 1:
            result = result + (1 << b) * (1 - 2 * ((value // (1 << b)) % 2))
    return result


class Exchange:
    def __init__(self, bits, count, rows, width, back=True):
        self.bits, self.count, self.rows, self.width = bits, count, rows, width
        self.back = back
        self.half, self.quarter, self.piece = rows // 2, rows // 4, rows // PIECES
        self.extra = list(range(4, bits))

    def slots(self):
        return 8 + 2 * (6 if self.back else 4) + (3 if self.extra else 0)

    def scratch(self):
        k, w = self.count, self.width
        cross = k if not self.back else 1
        shapes = [
            pltpu.VMEM((k, 2 - self.back, self.half, w), bf16),
            pltpu.VMEM((cross, self.half, w), bf16),
            pltpu.VMEM((cross, self.half, w), bf16),
            pltpu.VMEM((k, self.quarter, w), bf16),
            pltpu.VMEM((k, self.quarter, w), bf16),
            pltpu.VMEM((k, self.quarter, w), f32),
            pltpu.VMEM((k, 3, self.piece, w), bf16),
            pltpu.VMEM((k, 3, self.piece, w), bf16),
        ]
        lanes_of = (1, 0, 1, 3, 3, 1, 1) if self.back else (2, 1, 1, 3, 0, 0, 0)
        for lanes in [lanes for lanes in lanes_of if lanes]:
            shapes += [pltpu.SemaphoreType.DMA((k, lanes))] * 2
        if self.extra:
            n = len(self.extra)
            shapes += [pltpu.VMEM((k, 2 * n, self.piece, w), bf16)]
            shapes += [pltpu.SemaphoreType.DMA((k, n))] * 2
        return shapes

    def bind(self, place, part, refs):
        (self.a_in, self.b_out, self.b_in, self.c_out, self.c_in, self.keep) = refs[:6]
        self.d_out, self.d_in = refs[6:8]
        names = "acdefg" if self.back else "abcd"
        self.sems = {name: (refs[8 + 2 * i], refs[9 + 2 * i]) for i, name in enumerate(names)}
        if self.extra:
            at = 8 + 2 * len(names)
            self.x_buf, self.x_send, self.x_recv = refs[at : at + 3]
        self.place, self.part = place, part
        self.core, self.x, self.z = place % 2, (place // 2) % 2, (place // 4) % 4
        self.sibling = {"dp": flip(place, 1)}
        self.beside = {"dp": flip(place, 2)}
        self.across = {"mp": 1 - part}
        self.peers = [{"dp": flip(place, j << 2)} for j in range(1, 4)]
        self.partners = [self.sibling, self.beside, self.across] + self.peers
        self.partners += [{"dp": flip(place, 1 << b)} for b in self.extra]
        return self

    def greet(self):
        barrier = pltpu.get_barrier_semaphore()
        for partner in self.partners:
            pl.semaphore_signal(barrier, inc=1, device_id=partner, device_id_type=MESH)
        pl.semaphore_wait(barrier, len(self.partners))

    def copy(self, name, k, lane, source, target, device):
        out, into = self.sems[name]
        return pltpu.make_async_remote_copy(
            src_ref=source,
            dst_ref=target,
            send_sem=out.at[k, lane],
            recv_sem=into.at[k, lane],
            device_id=device,
            device_id_type=MESH,
        )

    def rows_at(self, start, size):
        return pl.ds(pl.multiple_of(start, PIECES), size)

    def copy_a(self, k, lane, grads):
        source = grads.at[k, self.rows_at((1 - self.core) * self.half, self.half)]
        return self.copy("a", k, lane, source, self.a_in.at[k, lane], self.sibling)

    def copy_b(self, k):
        return self.copy("b", k, 0, self.b_out.at[k], self.b_in.at[k], self.across)

    def copy_c(self, k):
        return self.copy("c", k, 0, self.c_out.at[k], self.c_in.at[k], self.beside)

    def copy_d(self, k, j):
        return self.copy("d", k, j, self.d_out.at[k, j], self.d_in.at[k, j], self.peers[j])

    def spot(self, change=0):
        start = self.core * self.half + self.x * self.quarter
        return self.rows_at(start + flip(self.z, change) * self.piece, self.piece)

    def copy_e(self, k, j, full):
        rows = full.at[k, self.spot()]
        return self.copy("e", k, j, rows, rows, self.peers[j])

    def copy_f(self, k, full):
        start = self.core * self.half + self.x * self.quarter
        rows = full.at[k, self.rows_at(start, self.quarter)]
        return self.copy("f", k, 0, rows, rows, self.beside)

    def copy_g(self, k, full):
        rows = full.at[k, self.rows_at(self.core * self.half, self.half)]
        return self.copy("g", k, 0, rows, rows, self.sibling)

    def start_a(self, k, lane, grads):
        self.copy_a(k, lane, grads).start()

    def stage_b(self, k, others):
        self.copy_a(k, 0, others).wait()
        mine = others[k, self.rows_at(self.core * self.half, self.half), :].astype(f32)
        self.b_out[k] = (mine + self.a_in[k, 0].astype(f32)).astype(bf16)
        self.copy_b(k).start()

    def stage_c(self, k, grads, crossed=None):
        lane = 0 if self.back else 1
        self.copy_a(k, lane, grads).wait()
        if not self.back:
            self.copy_b(k).wait()

        def total(which):
            inner = which * self.quarter
            rows = self.rows_at(inner, self.quarter)
            mine = grads[k, self.rows_at(self.core * self.half + inner, self.quarter), :]
            got = self.a_in[k, lane, rows, :].astype(f32)
            if not self.back:
                got = got + self.b_in[k, rows, :].astype(f32)
            elif crossed is not None:
                got = got + crossed(rows)
            return mine.astype(f32) + got

        self.c_out[k] = total(1 - self.x).astype(bf16)
        self.copy_c(k).start()
        self.keep[k] = total(self.x)

    def stage_d(self, k):
        self.copy_c(k).wait()
        for j in range(4):
            rows = self.rows_at(flip(self.z, j) * self.piece, self.piece)
            total = self.keep[k, rows, :] + self.c_in[k, rows, :].astype(f32)
            if j:
                self.d_out[k, j - 1] = total.astype(bf16)
                self.copy_d(k, j - 1).start()
            else:
                self.keep[k, rows, :] = total

    def gather_d(self, k):
        rows = self.rows_at(self.z * self.piece, self.piece)
        total = self.keep[k, rows, :]
        for j in range(3):
            self.copy_d(k, j).wait()
            total = total + self.d_in[k, j].astype(f32)
        for i, b in enumerate(self.extra):
            mine = self.x_buf.at[k, 2 * i]
            mine[...] = total.astype(bf16)
            swap = pltpu.make_async_remote_copy(
                src_ref=mine,
                dst_ref=self.x_buf.at[k, 2 * i + 1],
                send_sem=self.x_send.at[k, i],
                recv_sem=self.x_recv.at[k, i],
                device_id={"dp": flip(self.place, 1 << b)},
                device_id_type=MESH,
            )
            swap.start()
            swap.wait()
            total = total.astype(bf16).astype(f32) + self.x_buf[k, 2 * i + 1].astype(f32)
        return total.astype(bf16)

    def stage_e(self, k, full):
        full[k, self.spot(), :] = self.gather_d(k)
        for j in range(3):
            self.copy_e(k, j, full).start()

    def stage_f(self, k, full):
        for j in range(3):
            self.copy_e(k, j, full).wait()
        self.copy_f(k, full).start()

    def stage_g(self, k, full):
        self.copy_f(k, full).wait()
        self.copy_g(k, full).start()

    def stage_h(self, k, full):
        self.copy_g(k, full).wait()


def at_step(step, count, action):
    @pl.when(jnp.logical_and(step >= 0, step < count))
    def _():
        action(step)


def middle_kernel(exchanges, tiles, *refs):
    (
        x_ref,
        att_ref,
        att2_ref,
        wout_ref,
        wout2_ref,
        dy_ref,
        vectors_ref,
        bup_ref,
        up_mine,
        up_here,
        up_beside,
        down_mine,
        down_here,
        out_hbm,
        mid_hbm,
        datt_hbm,
        datt2_hbm,
        gout_ref,
        gout2_ref,
        gbup_ref,
        small_ref,
        pieces_ref,
        up_there,
        down_there,
        pass_up,
        pass_down,
        up_buf,
        down_buf,
        load_sem,
        n2_ref,
        total_ref,
        dn2_ref,
        act_ref,
        dpre_ref,
        n2_t,
        bup_other,
        bias_sem,
        out_ref,
        mid_ref,
        datt_ref,
        datt2_ref,
        store_sem,
        down_grad,
        up_grad,
        *rest,
    ) = refs
    place, part = lax.axis_index("dp"), lax.axis_index("mp")
    ex = exchanges[0].bind(place, part, rest)
    ex_up = exchanges[1].bind(place, part, rest[exchanges[0].slots() :])
    sides = ((ex, down_grad), (ex_up, up_grad))
    core = ex.core
    count = tiles // 2
    rows_all = x_ref.shape[0]
    blocks = rows_all // ROW_TILE
    width = x_ref.shape[1]
    lanes = width // 2

    def which(i):
        other = jnp.logical_or(i == 0, jnp.logical_and(i % 2 == 1, i < tiles - 1))
        mine = jnp.where(i == tiles - 1, count - 1, i // 2 - 1)
        return other, jnp.where(other, (i + 1) // 2, mine)

    quarter = width // 4
    strip = HIDDEN_TILE // 2
    held = 2 * core + ex.x
    kept = 2 * core + 1 - ex.x

    def load_up(i, source, h):
        target = up_buf.at[i % 2, h * quarter : (h + 1) * quarter]
        return pltpu.make_async_copy(source, target, load_sem.at[i % 2, h])

    def load_down(i, source, h):
        target = down_buf.at[i % 2, h * strip : (h + 1) * strip]
        return pltpu.make_async_copy(source, target, load_sem.at[i % 2, 4 + h])

    def hand_up(k, part_of):
        cols = pl.ds(pl.multiple_of(k * HIDDEN_TILE, HIDDEN_TILE), HIDDEN_TILE)
        side = ex.x if part_of == 0 else 1 - ex.x
        rows = pl.ds(pl.multiple_of(side * quarter, EDGE), quarter)
        return pltpu.make_async_remote_copy(
            src_ref=(up_here, up_beside)[part_of].at[:, cols],
            dst_ref=up_there.at[k, rows],
            send_sem=pass_up.at[k, 2 * part_of],
            recv_sem=pass_up.at[k, 2 * part_of + 1],
            device_id=ex.sibling,
            device_id_type=MESH,
        )

    def hand_down(b):
        return pltpu.make_async_remote_copy(
            src_ref=down_here.at[strip_rows(b)],
            dst_ref=down_there.at[b],
            send_sem=pass_down.at[b, 0],
            recv_sem=pass_down.at[b, 1],
            device_id=ex.sibling,
            device_id_type=MESH,
        )

    def strip_rows(b):
        return pl.ds(pl.multiple_of(b * strip, strip), strip)

    def start_loads(i):
        other, k = which(i)
        mine = jnp.logical_not(other)
        cols = pl.ds(pl.multiple_of(k * HIDDEN_TILE, HIDDEN_TILE), HIDDEN_TILE)

        @pl.when(other)
        def _():
            hand_up(k, 0).wait()
            hand_up(k, 1).wait()

        for h in range(4):

            @pl.when(mine)
            def _():
                load_up(i, up_mine.at[h * quarter : (h + 1) * quarter, cols], h).start()

            @pl.when(jnp.logical_and(other, held == h))
            def _():
                load_up(i, up_here.at[:, cols], h).start()

            @pl.when(jnp.logical_and(other, kept == h))
            def _():
                load_up(i, up_beside.at[:, cols], h).start()

            @pl.when(jnp.logical_and(other, core != h // 2))
            def _():
                rows = slice(h % 2 * quarter, (h % 2 + 1) * quarter)
                load_up(i, up_there.at[k, rows], h).start()

        for h in range(2):
            b = 2 * k + h
            inner = b % count

            @pl.when(mine)
            def _():
                load_down(i, down_mine.at[strip_rows(b), :], h).start()

            @pl.when(jnp.logical_and(other, core == b // count))
            def _():
                load_down(i, down_here.at[strip_rows(inner), :], h).start()

            @pl.when(jnp.logical_and(other, core != b // count))
            def _():
                hand_down(inner).wait_recv()
                load_down(i, down_there.at[inner], h).start()

    def wait_loads(i):
        for h in range(4):
            load_up(i, up_mine.at[:quarter, :HIDDEN_TILE], h).wait()
        for h in range(2):
            load_down(i, down_mine.at[:strip, :], h).wait()

    ex.greet()
    bias_swap = pltpu.make_async_remote_copy(
        src_ref=bup_ref,
        dst_ref=bup_other,
        send_sem=bias_sem.at[0],
        recv_sem=bias_sem.at[1],
        device_id=ex.across,
        device_id_type=MESH,
    )
    bias_swap.start()

    def hand(k, _):
        hand_up(k, 0).start()
        hand_up(k, 1).start()
        hand_down(k).start()
        return 0

    lax.fori_loop(0, count, hand, 0)

    def prologue(n, _):
        prologue_block(2 * n)
        prologue_block(2 * n + 1)
        return 0

    def prologue_block(r):
        rows = pl.ds(pl.multiple_of(r * ROW_TILE, ROW_TILE), ROW_TILE)
        branch = dot(att_ref[rows, :], wout_ref[...]) + dot(att2_ref[rows, :], wout2_ref[...])
        mid = x_ref[rows, :].astype(f32) + branch
        mid_ref[rows, :] = mid
        unit = normal(mid)[0]
        n2_ref[rows, :] = (unit * vectors_ref[2:3, :] + vectors_ref[3:4, :]).astype(bf16)
        total_ref[rows, :] = mid + vectors_ref[4:5, :]
        dn2_ref[rows, :] = jnp.zeros((ROW_TILE, width), f32)

    lax.fori_loop(0, blocks // 2, prologue, 0)
    start_loads(0)
    for c in range(width // LANES):
        cols = slice(c * LANES, (c + 1) * LANES)
        n2_t[cols, :] = n2_ref[:, cols].T
    n2_t[width:, :] = jnp.ones((PIECES, rows_all), bf16)
    bias_swap.wait()

    def tile(i):
        other, k = which(i)
        slot = i % 2
        wait_loads(i)

        @pl.when(i + 1 < tiles)
        def _():
            start_loads(i + 1)

        up, down = up_buf.at[slot], down_buf.at[slot]
        bias_at = jnp.where(other, k, count + k)
        bias = jnp.where(other, bup_other[k], bup_ref[k])
        linear = 0.7978845608028654
        cubic = linear * 0.044715
        for r in range(blocks):
            rows = slice(r * ROW_TILE, (r + 1) * ROW_TILE)
            pre = dot(n2_ref[rows, :], up[...]) + bias
            d_act = dot(dy_ref[rows, :], down[...], NT)
            square = pre * pre
            bend = jnp.tanh(pre * (square * cubic + linear))
            gate = 0.5 * bend + 0.5
            full_act = pre * gate
            slope = gate + (full_act - full_act * gate) * (square * (6.0 * cubic) + 2.0 * linear)
            act_ref[rows, :] = full_act.astype(bf16)
            dpre_ref[rows, :] = (d_act * slope).astype(bf16)
        total_ref[...] += dot(act_ref[...], down[...])
        dn2_ref[...] += dot(dpre_ref[...], up[...], NT)
        down_grad[k] = dot(act_ref[...].T, dy_ref[...]).astype(bf16)

        def start(lane):
            for side, grad in sides:
                side.start_a(k, lane, grad)

        by_rows = dot(n2_t[...], dpre_ref[...])
        up_grad[k] = by_rows[:width].astype(bf16)
        gbup_ref[bias_at] = by_rows[width : width + 1]
        pl.when(other)(functools.partial(start, 0))
        pl.when(jnp.logical_not(other))(functools.partial(start, 1))

    def each(k, when, action):
        @pl.when(jnp.logical_and(when, jnp.logical_and(k >= 0, k < count)))
        def _():
            for n, (side, grad) in enumerate(sides):
                action(n, side, grad, k)

    def stage_b(n, side, grad, k):
        side.stage_b(k, grad)

    def stage_c(n, side, grad, k):
        side.stage_c(k, grad)

    def stage_d(n, side, grad, k):
        side.stage_d(k)

    def arrive(n, side, grad, k):
        piece = side.gather_d(k)
        if n == 0:
            pieces_ref[k] = piece
        else:
            for c in range(width // HIDDEN_TILE):
                cols = slice(c * HIDDEN_TILE, (c + 1) * HIDDEN_TILE)
                pieces_ref[count + k, :, cols] = piece[c * PIECES : (c + 1) * PIECES]

    def steps(i):
        even = i % 2 == 0
        odd = jnp.logical_not(even)
        each((i - 5) // 2, odd, arrive)
        each((i - 4) // 2, even, stage_d)
        each((i - 3) // 2, odd, stage_c)
        each(i // 2, even, stage_b)

    def epilogue(r, _):
        rows = pl.ds(pl.multiple_of(r * ROW_TILE, ROW_TILE), ROW_TILE)
        out_ref[rows, :] = total_ref[rows, :].astype(bf16)
        unit, scale = normal(mid_ref[rows, :])
        d_rows = dn2_ref[rows, :]
        dy = dy_ref[rows, :].astype(f32)
        lean = d_rows * vectors_ref[2:3, :]
        d_mid = dy + scale * (
            lean
            - jnp.mean(lean, axis=-1, keepdims=True)
            - unit * jnp.mean(lean * unit, axis=-1, keepdims=True)
        )
        mid_ref[rows, :] = d_mid
        d_branch = d_mid.astype(bf16)
        n2_ref[rows, :] = d_branch
        datt_ref[rows, :] = dot(d_branch, wout_ref[...], NT).astype(bf16)
        datt2_ref[rows, :] = dot(d_branch, wout2_ref[...], NT).astype(bf16)
        add = lambda values: jnp.sum(values, axis=0, keepdims=True)
        small_ref[0:1, :] += add(d_rows * unit)
        small_ref[1:2, :] += add(d_rows)
        small_ref[2:3, :] += add(dy)
        return 0

    def out_grads():
        for source, target in ((att_ref, gout_ref), (att2_ref, gout2_ref)):
            grad = dot(source[...].T, n2_ref[...]).astype(bf16)
            for a in range(wout_ref.shape[0] // LANES):
                for b in range(2):
                    rows = slice(a * LANES, (a + 1) * LANES)
                    cols = slice(b * lanes, (b + 1) * lanes)
                    spread = slice(a * lanes, (a + 1) * lanes)
                    target[b * LANES : (b + 1) * LANES, spread] = grad[rows, cols]

    def main(i, _):
        pl.when(i < tiles)(functools.partial(tile, i))

        @pl.when(jnp.logical_and(i >= tiles, i < tiles + 2))
        def _():
            first = (i - tiles) * (blocks // 2)
            lax.fori_loop(first, first + blocks // 2, epilogue, 0)

        @pl.when(i == tiles + 2)
        def _():
            for store in stores:
                store.start()
            out_grads()

        steps(i)
        return 0

    small_ref[...] = jnp.zeros_like(small_ref)
    stores = [
        pltpu.make_async_copy(source, target, store_sem.at[n])
        for n, (source, target) in enumerate(
            (
                (datt2_ref, datt2_hbm),
                (out_ref, out_hbm),
                (mid_ref, mid_hbm),
                (datt_ref, datt_hbm),
            )
        )
    ]
    lax.fori_loop(0, tiles + 4, main, 0)
    for store in stores:
        store.wait()

    def handed(slot, _):
        hand_down(slot).wait_send()
        return 0

    lax.fori_loop(0, count, handed, 0)


def middle(bits, x, att, att2, wout, wout2, dy, vectors, bup, ups, downs):
    rows, width = x.shape
    hidden = ups[0].shape[1]
    count = hidden // HIDDEN_TILE
    tiles = 2 * count
    exchanges = (
        Exchange(bits, count, HIDDEN_TILE, width, False),
        Exchange(bits, count, width, HIDDEN_TILE, False),
    )
    vmem = pl.BlockSpec(memory_space=pltpu.VMEM)
    hbm = pl.BlockSpec(memory_space=pl.ANY)
    shape = jax.ShapeDtypeStruct
    depth = wout.shape[0]
    return pl.pallas_call(
        functools.partial(middle_kernel, exchanges, tiles),
        in_specs=[vmem] * 8 + [hbm] * 5,
        out_specs=[hbm] * 4 + [vmem] * 5,
        out_shape=[
            shape((rows, width), bf16),
            shape((rows, width), f32),
            shape(att.shape, bf16),
            shape(att2.shape, bf16),
            shape((2 * LANES, depth // LANES * width // 2), bf16),
            shape((2 * LANES, depth // LANES * width // 2), bf16),
            shape((tiles, 1, HIDDEN_TILE), f32),
            shape((8, width), f32),
            shape((2 * count, PIECES, width), bf16),
        ],
        scratch_shapes=[
            pltpu.VMEM((count, width // 2, HIDDEN_TILE), bf16),
            pltpu.VMEM((count, HIDDEN_TILE // 2, width), bf16),
            pltpu.SemaphoreType.DMA((count, 4)),
            pltpu.SemaphoreType.DMA((count, 2)),
            pltpu.VMEM((2, width, HIDDEN_TILE), bf16),
            pltpu.VMEM((2, HIDDEN_TILE, width), bf16),
            pltpu.SemaphoreType.DMA((2, 6)),
            pltpu.VMEM((rows, width), bf16),
            pltpu.VMEM((rows, width), f32),
            pltpu.VMEM((rows, width), f32),
            pltpu.VMEM((rows, HIDDEN_TILE), bf16),
            pltpu.VMEM((rows, HIDDEN_TILE), bf16),
            pltpu.VMEM((width + PIECES, rows), bf16),
            pltpu.VMEM(bup.shape, f32),
            pltpu.SemaphoreType.DMA((2,)),
            pltpu.VMEM((rows, width), bf16),
            pltpu.VMEM((rows, width), f32),
            pltpu.VMEM(att.shape, bf16),
            pltpu.VMEM(att2.shape, bf16),
            pltpu.SemaphoreType.DMA((4,)),
            pltpu.VMEM((count, HIDDEN_TILE, width), bf16),
            pltpu.VMEM((count, width, HIDDEN_TILE), bf16),
        ]
        + exchanges[0].scratch()
        + exchanges[1].scratch(),
        compiler_params=pltpu.CompilerParams(
            collective_id=0, has_side_effects=True, vmem_limit_bytes=67043328
        ),
        name="middle",
        cost_estimate=pl.CostEstimate(
            flops=60 * 10**9, bytes_accessed=40 * 10**6, transcendentals=4 * 10**6
        ),
    )(x, att, att2, wout, wout2, dy, vectors, bup, *ups, *downs)


def leave_kernel(exchange, *refs):
    (
        rows_hbm,
        mine_out_ref,
        crossed_ref,
        crossed_out_ref,
        d_hbm,
        d2_hbm,
        w_hbm,
        w2_hbm,
        tokens_ref,
        context_ref,
        given_ref,
        small_ref,
        small2_ref,
        gqkv_ref,
        gout_ref,
        back_hbm,
        sums_ref,
        full_ref,
        out_buf,
        rows_t_ref,
        d_ref,
        d2_ref,
        w_ref,
        w2_ref,
        load_sem,
        rows_ref,
        give_ref,
        take_ref,
        swap_sem,
        back_sem,
        norm_ref,
        near_ref,
        far_ref,
        near_sem,
        far_sem,
        *rest,
    ) = refs
    place, part = lax.axis_index("dp"), lax.axis_index("mp")
    ex = exchange.bind(place, part, rest)
    count, bits = ex.count, ex.bits
    loads = [
        pltpu.make_async_copy(source, target, load_sem.at[n])
        for n, (source, target) in enumerate(
            (
                (d_hbm, d_ref),
                (rows_hbm, rows_t_ref),
                (w_hbm, w_ref),
                (w2_hbm, w2_ref),
                (d2_hbm, d2_ref),
            )
        )
    ]
    for load in loads:
        load.start()
    near_id = part * 4 + place % 4
    near = [
        {"dp": flip(place, j % 4), "mp": part if j < 4 else 1 - part} for j in range(1, 8)
    ]
    ex.partners += [near[j - 1] for j in (3, 5, 6, 7)]
    ex.greet()

    lanes = d_ref.shape[2]
    split = mine_out_ref.shape[1] // lanes
    for r in range(split):
        cols = slice(r * lanes, (r + 1) * lanes)
        total = mine_out_ref[:, cols].astype(f32) + crossed_out_ref[:, cols].astype(f32)
        out_buf[r] = total.astype(bf16)
        ex.start_a(r, 0, out_buf)
    step = HALF + 2 * EDGE

    def back_rows(n):
        start = CLEAN_OWN + n * (KEY_ROWS - step - CLEAN_OWN)
        rows = pl.ds(pl.multiple_of(start, EDGE), step)
        total = 0.0
        for grads, weights in ((d_ref, w_ref), (d2_ref, w2_ref)):
            for c in range(3):
                total = total + dot(grads[c, rows, :], weights[c], NT)
        rows_ref[rows, :] = total

    def grad_chunk(c):
        for r in range(split):
            rows = slice(r * ROW_TILE, (r + 1) * ROW_TILE)
            k = (c + 1) * split + r
            out_buf[k] = dot(rows_t_ref[rows, :], d_ref[c]).astype(bf16)
            ex.start_a(k, 0, out_buf)

    def stage_c(k):
        @pl.when(k >= split)
        def _():
            ex.stage_c(k, out_buf, lambda rows: crossed_ref[k - split, rows, :].astype(f32))

        @pl.when(k < split)
        def _():
            ex.stage_c(k, out_buf)

    def arrive(k):
        ex.stage_h(k, full_ref)

        @pl.when(k < split)
        def _():
            rows = pl.ds(pl.multiple_of(k * LANES, LANES), LANES)
            for b in range(2):
                piece = full_ref[k, b * LANES : (b + 1) * LANES, :]
                gout_ref[rows, b * lanes : (b + 1) * lanes] = piece

        @pl.when(k >= split)
        def _():
            n = k - split
            rows = pl.ds(pl.multiple_of(n % split * ROW_TILE, ROW_TILE), ROW_TILE)
            gqkv_ref[n // split, rows, :] = full_ref[k]

    def group(g, action):
        @pl.when(jnp.logical_and(g >= 0, g < count // split))
        def _():
            lax.fori_loop(g * split, (g + 1) * split, lambda k, _: (action(k), 0)[1], 0)

    def steps(i):
        group(i - 5, arrive)
        group(i - 4, lambda k: ex.stage_g(k, full_ref))
        group(i - 3, lambda k: ex.stage_f(k, full_ref))
        group(i - 2, lambda k: ex.stage_e(k, full_ref))
        group(i - 1, lambda k: ex.stage_d(k))
        group(i, stage_c)

    width = tokens_ref.shape[1]

    def swap():
        return pltpu.make_async_remote_copy(
            src_ref=give_ref,
            dst_ref=take_ref,
            send_sem=swap_sem.at[0],
            recv_sem=swap_sem.at[1],
            device_id=ex.across,
            device_id_type=MESH,
        )

    def sums_of(d_rows, units):
        add = lambda values: jnp.sum(values, axis=0, keepdims=True)
        norm_ref[0:1, :] += add(d_rows * units)
        norm_ref[1:2, :] += add(d_rows)

    parts = tokens_ref.shape[0] // TILE
    lead = small_ref.shape[0] - 2
    bias = lead - 3
    norm_ref[...] = jnp.zeros_like(norm_ref)
    for load in loads[:2]:
        load.wait()

    def own_at(b):
        start = jnp.where(b < TILES, NOISY_OWN + b * TILE, CLEAN_OWN + (b - TILES) * TILE)
        return pl.ds(pl.multiple_of(start, EDGE), TILE)

    def tokens_at(b):
        return pl.ds(pl.multiple_of(b * TILE, TILE), TILE)

    def ready():
        for load in loads[2:5]:
            load.wait()

    def give_edges():
        side = rows_ref[NOISY_BASE:NOISY_OWN, :] + rows_ref[NOISY_OWN + HALF :, :]
        after = rows_ref[2 * HALF : NOISY_BASE, :]
        give_ref[:EDGE, :] = after.astype(bf16)
        give_ref[EDGE:, :] = side.astype(bf16)
        swap().start()
        sums_of(after, normal(context_ref[:EDGE, :].astype(f32))[0])
        sums_of(side, normal(context_ref[HALF:, :].astype(f32))[0])

    def tell_near():
        def context_sums(b, _):
            rows = tokens_at(b)
            sums_of(given_ref[rows, :], normal(context_ref[rows, :].astype(f32))[0])
            return 0

        lax.fori_loop(0, HALF // TILE, context_sums, 0)

        def own_sums(b, _):
            sums_of(rows_ref[own_at(b), :], normal(tokens_ref[tokens_at(b), :].astype(f32))[0])
            return 0

        lax.fori_loop(0, parts, own_sums, 0)
        blank = jnp.zeros((16 - lead - 2 - bias, width), f32)
        near_ref[near_id] = jnp.concatenate(
            [small_ref[:lead, :], norm_ref[:2, :], small2_ref[:bias, :], blank], axis=0
        ).astype(bf16)
        for j in range(1, 8):
            near_copy(j).start()

    def near_copy(j):
        return pltpu.make_async_remote_copy(
            src_ref=near_ref.at[near_id],
            dst_ref=near_ref.at[near_id],
            send_sem=near_sem.at[j, 0],
            recv_sem=near_sem.at[j, 1],
            device_id=near[j - 1],
            device_id_type=MESH,
        )

    def near_got(j):
        came = (part + j // 4) % 2 * 4 + flip(place % 4, j % 4)
        return pltpu.make_async_remote_copy(
            src_ref=near_ref.at[came],
            dst_ref=near_ref.at[came],
            send_sem=near_sem.at[j, 0],
            recv_sem=near_sem.at[j, 1],
            device_id=near[j - 1],
            device_id_type=MESH,
        )

    def far_copy(j, at):
        return pltpu.make_async_remote_copy(
            src_ref=far_ref.at[at],
            dst_ref=far_ref.at[at],
            send_sem=far_sem.at[j, 0],
            recv_sem=far_sem.at[j, 1],
            device_id=ex.peers[j - 1],
            device_id_type=MESH,
        )

    def tell_far():
        for j in range(1, 8):
            near_copy(j).wait_send()
            near_got(j).wait_recv()
        near_sum = lambda at: sum(near_ref[at + j].astype(f32) for j in range(1, 4)) + near_ref[
            at
        ].astype(f32)
        plane, other = near_sum(part * 4), near_sum((1 - part) * 4)
        total = near_sum(0) + near_sum(4)
        mixed = plane[:bias] + other[lead + 2 : lead + 2 + bias]
        far_ref[ex.z] = jnp.concatenate([mixed, total[bias:]], axis=0).astype(bf16)
        for j in range(1, 4):
            far_copy(j, ex.z).start()

    halves = [
        pltpu.make_async_copy(
            rows_ref.at[start : start + HALF],
            back_hbm.at[n * HALF : (n + 1) * HALF],
            back_sem.at[n],
        )
        for n, start in enumerate((NOISY_OWN, CLEAN_OWN))
    ]

    def take_back():
        swap().wait()
        begin = slice(CLEAN_OWN, CLEAN_OWN + EDGE)
        rows_ref[begin, :] += take_ref[:EDGE, :].astype(f32)
        edge = pl.ds(pl.multiple_of(NOISY_OWN + (1 - part) * (HALF - EDGE), EDGE), EDGE)
        rows_ref[edge, :] += take_ref[EDGE:, :].astype(f32)
        for half in halves:
            half.start()

    def end_far():
        for j in range(1, 4):
            far_copy(j, ex.z).wait_send()
            far_copy(j, flip(ex.z, j)).wait_recv()
        total = far_ref[0].astype(f32)
        for j in range(1, 4):
            total = total + far_ref[j].astype(f32)
        for i, b in enumerate(ex.extra):
            total = total.astype(bf16).astype(f32)
            far_ref[4 + 2 * i] = total.astype(bf16)
            trade = pltpu.make_async_remote_copy(
                src_ref=far_ref.at[4 + 2 * i],
                dst_ref=far_ref.at[5 + 2 * i],
                send_sem=far_sem.at[4 + i, 0],
                recv_sem=far_sem.at[4 + i, 1],
                device_id={"dp": flip(place, 1 << b)},
                device_id_type=MESH,
            )
            trade.start()
            trade.wait()
            total = total + far_ref[5 + 2 * i].astype(f32)
        sums_ref[...] = total

    groups = count // split - 1
    actions = {
        groups + 1: give_edges,
        groups + 2: tell_near,
        groups + 3: take_back,
        groups + 4: tell_far,
        groups + 6: end_far,
    }

    def phase(p, _):
        @pl.when(p < groups)
        def _():
            grad_chunk(p)

        pl.when(p == groups)(ready)

        @pl.when(jnp.logical_and(p >= groups, p < groups + 2))
        def _():
            back_rows(p - groups)

        for n, action in actions.items():
            pl.when(p == n)(action)
        steps(p)
        return 0

    lax.fori_loop(0, groups + 7, phase, 0)
    for half in halves:
        half.wait()


def leave(bits, rows_t, mine, crossed, d_fields, weights, tokens, context, given, small, small2):
    rows, cols = ROW_TILE, d_fields[0].shape[2]
    total = mine.shape[1] // cols + crossed[0].shape[0]
    exchange = Exchange(bits, total, rows, cols)
    count, width = tokens.shape
    vmem = pl.BlockSpec(memory_space=pltpu.VMEM)
    hbm = pl.BlockSpec(memory_space=pl.ANY)
    shape = jax.ShapeDtypeStruct
    return pl.pallas_call(
        functools.partial(leave_kernel, exchange),
        in_specs=[hbm] + [vmem] * 3 + [hbm] * 4 + [vmem] * 5,
        out_specs=[vmem] * 2 + [hbm, vmem],
        out_shape=[
            shape(weights[0].shape, bf16),
            shape((d_fields[0].shape[2], width), bf16),
            shape((count, width), f32),
            shape((16, width), f32),
        ],
        scratch_shapes=[
            pltpu.VMEM((total, rows, cols), bf16),
            pltpu.VMEM((total, rows, cols), bf16),
            pltpu.VMEM(rows_t.shape, bf16),
            pltpu.VMEM(d_fields[0].shape, bf16),
            pltpu.VMEM(d_fields[1].shape, bf16),
            pltpu.VMEM(weights[0].shape, bf16),
            pltpu.VMEM(weights[1].shape, bf16),
            pltpu.SemaphoreType.DMA((5,)),
            pltpu.VMEM((KEY_ROWS, width), f32),
            pltpu.VMEM((2 * EDGE, width), bf16),
            pltpu.VMEM((2 * EDGE, width), bf16),
            pltpu.SemaphoreType.DMA((2,)),
            pltpu.SemaphoreType.DMA((2,)),
            pltpu.VMEM((8, width), f32),
            pltpu.VMEM((8, 16, width), bf16),
            pltpu.VMEM((4 + 2 * len(exchange.extra), 16, width), bf16),
            pltpu.SemaphoreType.DMA((8, 2)),
            pltpu.SemaphoreType.DMA((4 + len(exchange.extra), 2)),
        ]
        + exchange.scratch(),
        compiler_params=pltpu.CompilerParams(
            collective_id=1, has_side_effects=True, vmem_limit_bytes=67043328
        ),
        name="leave",
        cost_estimate=pl.CostEstimate(
            flops=40 * 10**9, bytes_accessed=40 * 10**6, transcendentals=0
        ),
    )(
        rows_t, mine, *crossed, *d_fields, *weights, tokens, context, given, small, small2
    )


def finish_kernel(rows_ref, got_ref, tokens_ref, vectors_ref, dmid_ref, out_ref):
    clean = pl.program_id(0) >= pl.num_programs(0) // 2
    got = jnp.where(clean, got_ref[...].astype(f32), 0.0)
    unit, scale = normal(tokens_ref[...].astype(f32))
    lean = (rows_ref[...] + got) * vectors_ref[0:1, :]
    out_ref[...] = dmid_ref[...] + scale * (
        lean
        - jnp.mean(lean, axis=-1, keepdims=True)
        - unit * jnp.mean(lean * unit, axis=-1, keepdims=True)
    )


def finish(rows, got, tokens, vectors, d_mid):
    count, width = rows.shape
    spec = pl.BlockSpec((ROW_TILE, width), lambda b: (b, 0))
    half = count // ROW_TILE // 2
    return pl.pallas_call(
        finish_kernel,
        grid=(count // ROW_TILE,),
        in_specs=[
            spec,
            pl.BlockSpec((ROW_TILE, width), lambda b: (jnp.maximum(b - half, 0), 0)),
            spec,
            pl.BlockSpec(vectors.shape, lambda b: (0, 0)),
            spec,
        ],
        out_specs=spec,
        out_shape=jax.ShapeDtypeStruct((count, width), f32),
        name="finish",
        cost_estimate=pl.CostEstimate(
            flops=10**7, bytes_accessed=12 * 10**6, transcendentals=0
        ),
    )(rows, got, tokens, vectors, d_mid)


def assemble_kernel(core_ref, down_mine, up_mine, down_got, up_got, down_ref, up_ref):
    core = core_ref[0]
    block = down_mine.shape[1]
    lanes = up_ref.shape[1]
    parts = down_mine.shape[2] // lanes
    deep = block * parts
    for side, down, up in ((core, down_mine, up_mine), (1 - core, down_got, up_got)):
        rows = pl.ds(pl.multiple_of(side * block, block), block)
        down_ref[rows, :] = down[0].astype(f32)
        for n in range(block // PIECES):
            for c in range(parts):
                at = side * deep + (n * parts + c) * PIECES
                rows = pl.ds(pl.multiple_of(at, PIECES), PIECES)
                piece = up[0, n * PIECES : (n + 1) * PIECES, c * lanes : (c + 1) * lanes]
                up_ref[rows, :] = piece.astype(f32)


def assemble(core, gathered, moved):
    tiles, half, width = gathered.shape
    count = tiles // 2
    down_spec = pl.BlockSpec((1, half, width), lambda k, c: (k, 0, 0))
    up_spec = pl.BlockSpec((1, half, width), lambda k, c: (count + k, 0, 0))
    hidden = count * 2 * half
    return pl.pallas_call(
        assemble_kernel,
        grid_spec=pltpu.PrefetchScalarGridSpec(
            num_scalar_prefetch=1,
            grid=(count,),
            in_specs=[down_spec, up_spec, down_spec, up_spec],
            out_specs=[
                pl.BlockSpec((2 * half, width), lambda k, c: (k, 0)),
                pl.BlockSpec((width, 2 * half), lambda k, c: (0, k)),
            ],
        ),
        out_shape=[
            jax.ShapeDtypeStruct((hidden, width), f32),
            jax.ShapeDtypeStruct((width, hidden), f32),
        ],
        name="assemble",
        cost_estimate=pl.CostEstimate(
            flops=10**6, bytes_accessed=14 * 10**6, transcendentals=0
        ),
    )(core, gathered, gathered, moved, moved)


def key_layout(seq_lengths, block_len, part):
    index = jnp.arange(KEY_ROWS, dtype=jnp.int32)
    own = part * HALF
    token = jnp.where(
        index < NOISY_BASE, index + (own - HALF), index - NOISY_BASE + (own - EDGE)
    )
    ends = jnp.cumsum(seq_lengths)
    passed = token[:, None] >= ends[None, :]
    starts = jnp.sum(jnp.where(passed, seq_lengths[None, :], 0), axis=1)
    lengths_here = jnp.where(passed, 0, ends[None, :])
    stops = jnp.min(jnp.where(passed, TOK_DEV, lengths_here), axis=1)
    positions = token - starts
    block_start = starts + positions // block_len * block_len
    block_stop = jnp.minimum(block_start + block_len, stops)
    mine = slice(CLEAN_OWN, CLEAN_OWN + HALF)
    low, start, stop = starts[mine], block_start[mine], block_stop[mine]
    to_clean = own - HALF
    tiles = lambda column: column.reshape(TILES, 1, TILE)
    clean_bounds = jnp.concatenate(
        [
            jnp.concatenate([tiles(low - to_clean), tiles(low - to_clean)], axis=2),
            jnp.concatenate([tiles(start - to_clean), tiles(stop - to_clean)], axis=2),
        ],
        axis=1,
    )
    to_window = own - EDGE + TILE * jnp.arange(TILES, dtype=jnp.int32)[:, None, None]
    noisy_bounds = jnp.concatenate(
        [tiles(start) - to_window, tiles(stop) - to_window], axis=1
    )
    first = jnp.min(clean_bounds[:, 0], axis=1) // EDGE * EDGE
    last = jnp.max(clean_bounds[:, 1], axis=1)
    trips = (last - first + KEY_TILE - 1) // KEY_TILE
    spans = jnp.stack([first, trips], axis=1)
    lane = jnp.arange(LANES, dtype=jnp.int32)
    frequency = jnp.exp(
        (lane % (HD // 2)).astype(f32) * (-math.log(10000.0) / (HD // 2))
    )
    angles = positions.astype(f32)[:, None] * frequency[None, :]
    sign = jnp.where(lane % HD < HD // 2, -1.0, 1.0)
    return spans, clean_bounds, noisy_bounds, jnp.cos(angles), jnp.sin(angles) * sign


def in_order(bit, mine, theirs, axis=0):
    order = bit == 0
    return jnp.concatenate(
        [jnp.where(order, mine, theirs), jnp.where(order, theirs, mine)], axis=axis
    )


def tie(first, second):
    return lax.optimization_barrier((first, second))


def local(
    dp_size,
    tokens,
    lengths,
    block_size,
    cotangent,
    ln1_gain,
    ln1_bias,
    w_qkv,
    w_out,
    ln2_gain,
    ln2_bias,
    w_up,
    b_up,
    w_down,
    b_down,
):
    width = tokens.shape[2]
    part = lax.axis_index("mp")
    place = lax.axis_index("dp")
    bits = dp_size.bit_length() - 1
    core = place & 1

    def across(array):
        return lax.ppermute(array, "mp", [(0, 1), (1, 0)])

    def sibling(array):
        return lax.ppermute(array, "dp", [(i, i ^ 1) for i in range(dp_size)])

    def beside(array):
        return lax.ppermute(array, "dp", [(i, i ^ 2) for i in range(dp_size)])

    edge = jnp.where(part == 0, tokens[0, HALF - EDGE :], tokens[0, :EDGE])
    context = across(jnp.concatenate([tokens[1], edge], axis=0))
    qkv_mine = w_qkv.transpose(1, 0, 2)
    side = (place >> 1) & 1

    def quarter_of(array, axis=0):
        size = array.shape[axis] // 4
        return lax.dynamic_slice_in_dim(array, (2 * core + side) * size, size, axis)

    def half_of(array):
        size = array.shape[0] // 2
        return lax.dynamic_slice_in_dim(array, core * size, size, 0)

    quarters = [quarter_of(qkv_mine, 1), quarter_of(w_up), half_of(w_down), half_of(w_out)]
    layout = key_layout(lengths[0], block_size[0], part)
    vectors = jnp.stack([ln1_gain, ln1_bias, ln2_gain, ln2_bias, b_down])
    context, (quarters, layout, vectors) = tie(context, (quarters, layout, vectors))
    qkv_here, up_here, down_here, out_here = [across(piece) for piece in quarters]

    spans, clean_bounds, noisy_bounds, cosine, sine = layout
    normed1, normed1_t, *fields = enter(tokens, context, vectors, qkv_mine, cosine, sine)
    qkv_here, fields = tie(qkv_here, fields)
    qkv_beside = beside(qkv_here)
    mine = [*fields, *attend_forward(spans, clean_bounds, noisy_bounds, *fields)]
    (qkv_here, qkv_beside, up_here), _ = tie((qkv_here, qkv_beside, up_here), mine[3])
    qkv_half = in_order(side, qkv_here, qkv_beside, axis=1)
    qkv_other = in_order(core, qkv_half, sibling(qkv_half), axis=1)
    up_beside = beside(up_here)
    fields = project(normed1, qkv_other, cosine, sine)
    other = [*fields, *attend_forward(spans, clean_bounds, noisy_bounds, *fields)]
    (out_here, up_here, up_beside, down_here), _ = tie(
        (out_here, up_here, up_beside, down_here), other[3]
    )
    out_other = in_order(core, out_here, sibling(out_here))
    bias_all = b_up.astype(f32).reshape(-1, 1, HIDDEN_TILE)

    x_rows = tokens.reshape(TOK_DEV, width)
    out, d_mid, d_att, d_att2, grad_out, grad_out2, grad_bias, norms, pieces = middle(
        bits,
        x_rows,
        mine[3],
        other[3],
        w_out,
        out_other,
        cotangent.reshape(TOK_DEV, width),
        vectors,
        bias_all,
        (w_up, up_here, up_beside),
        (w_down, down_here),
    )
    hidden = b_up.shape[0]

    crossed_out = across(grad_out2)
    spread = [(b, min(2, min(bits, 4) - b)) for b in range(2, min(bits, 4), 2)]
    gathered = pieces
    ((first_bit, n),) = spread
    moved = [
        lax.ppermute(gathered, "dp", [(i, i ^ (k << first_bit)) for i in range(dp_size)])
        for k in range(1, 1 << n)
    ]

    def backward(saved, d_attended, spans, *rest):
        query, keys, values, attended, lse = saved
        return attend_backward(
            spans,
            clean_bounds,
            noisy_bounds,
            query,
            keys,
            values,
            attended,
            d_attended,
            lse,
            cosine,
            sine,
            rest,
        )

    d_fields2, grad2 = backward(other, d_att2, spans, normed1_t)
    grad2 = grad2.reshape(-1, ROW_TILE, grad2.shape[2])
    low_bit, high_bit = (place >> 2) & 1, (place >> 3) & 1
    moved, _ = tie(moved, grad2)
    gathered = in_order(
        high_bit,
        in_order(low_bit, gathered, moved[0], 1),
        in_order(low_bit, moved[1], moved[2], 1),
        1,
    )
    half = ROW_TILE // 2
    part_of = lambda array, which: lax.dynamic_slice_in_dim(array, which * half, half, 1)
    got = sibling(part_of(grad2, 1 - core))
    crossing = (part_of(grad2, core).astype(f32) + got.astype(f32)).astype(bf16)
    (crossing, gathered), spans = tie((crossing, gathered), spans)
    crossed = across(crossing)
    moved = beside(gathered)
    d_fields1, given, give = backward(mine, d_att, spans, d_fields2, qkv_mine, qkv_other)
    took = across(give)
    moved, d_fields1 = tie(moved, d_fields1)
    gathered = in_order(side, gathered, moved, 1)
    gathered, d_fields1 = tie(gathered, d_fields1)
    moved = sibling(gathered)
    lead = hidden // width
    bias2, bias1 = grad_bias.reshape(2, lead, width)
    shared = jnp.concatenate([norms[:3], jnp.zeros((2, width), f32)], axis=0)
    grad_qkv, grad_out, d_rows, sums = leave(
        bits,
        normed1_t,
        grad_out,
        (crossed, crossed_out),
        (d_fields1, d_fields2),
        (qkv_mine, qkv_other),
        x_rows,
        context,
        given,
        jnp.concatenate([bias1, shared], axis=0),
        jnp.concatenate([bias2, shared], axis=0),
    )
    (moved, took), grad_qkv = tie((moved, took), grad_qkv)
    grad_tokens = finish(d_rows, took, x_rows, vectors, d_mid)
    grad_down, grad_up = assemble(core.reshape(1), gathered, moved)
    return (
        out.reshape(tokens.shape),
        grad_tokens.reshape(tokens.shape),
        sums[lead + 3],
        sums[lead + 4],
        grad_qkv.transpose(1, 0, 2).astype(f32),
        grad_out.astype(f32),
        sums[lead],
        sums[lead + 1],
        grad_up,
        sums[:lead].reshape(hidden),
        grad_down,
        sums[lead + 2],
    )


def solution(mesh):
    in_specs = (
        P(None, ("dp", "mp"), None),
        P("dp", None),
        P(),
        P(None, ("dp", "mp"), None),
        P(),
        P(),
        P(None, None, "mp"),
        P("mp", None),
        P(),
        P(),
        P(None, "mp"),
        P("mp"),
        P("mp", None),
        P(),
    )
    out_specs = (
        P(None, ("dp", "mp"), None),
        P(None, ("dp", "mp"), None),
        P(),
        P(),
        P(None, None, "mp"),
        P("mp", None),
        P(),
        P(),
        P(None, "mp"),
        P("mp"),
        P("mp", None),
        P(),
    )
    return jax.shard_map(
        functools.partial(local, mesh.shape["dp"]),
        mesh=mesh,
        in_specs=in_specs,
        out_specs=out_specs,
        check_vma=False,
    )
```

```python
import functools
import math

import jax
import jax.numpy as jnp
from jax import lax
from jax.experimental import pallas as pl
from jax.experimental.pallas import tpu as pltpu
from jax.sharding import PartitionSpec as P

HD = 64
TOK_DEV = 1024
HALF = TOK_DEV // 2
EDGE = 16
CLEAN_OWN = HALF
NOISY_BASE = 2 * HALF + EDGE
NOISY_OWN = NOISY_BASE + EDGE
KEY_ROWS = NOISY_OWN + HALF + EDGE
TILE = 128
TILES = HALF // TILE
WINDOW = TILE + 2 * EDGE
KEY_TILE = 192
LANES = 128
HIDDEN_TILE = 256
ROW_TILE = 256

epsilon = 1e-05
neg_large = -1e30
to_base2 = 0.125 * math.log2(math.e)
f32 = jnp.float32
bf16 = jnp.bfloat16

NN = (((1,), (0,)), ((), ()))
NT = (((1,), (1,)), ((), ()))


def dot(left, right, dims=NN):
    return lax.dot_general(left, right, dims, preferred_element_type=f32)


def low_lanes(shape):
    return lax.broadcasted_iota(jnp.int32, shape, 1) < HD


def turn(values, cosine, sine):
    lane = lax.broadcasted_iota(jnp.int32, values.shape, 1)
    first_half = (lane & (HD - 1)) < HD // 2
    swapped = jnp.where(
        first_half,
        pltpu.roll(values, LANES - HD // 2, 1),
        pltpu.roll(values, HD // 2, 1),
    )
    return values * cosine + swapped * sine


def project_rows(rows, w_ref, cosine, sine, q_ref, k_ref, v_ref, at):
    for part, out_ref in ((0, q_ref), (1, k_ref)):
        field = dot(rows, w_ref[part])
        for pair in range(field.shape[1] // LANES):
            cols = slice(pair * LANES, (pair + 1) * LANES)
            out_ref[at, cols] = turn(field[:, cols], cosine, sine).astype(bf16)
    v_ref[at, :] = dot(rows, w_ref[2]).astype(bf16)


def project_kernel(rows_ref, w_ref, cos_ref, sin_ref, q_ref, k_ref, v_ref):
    at = slice(0, rows_ref.shape[0])
    project_rows(rows_ref[...], w_ref, cos_ref[...], sin_ref[...], q_ref, k_ref, v_ref, at)


def project(rows, weights, cosine, sine):
    count, width = rows.shape
    cols = weights.shape[2]
    step = count // 3
    row_spec = pl.BlockSpec((step, width), lambda i: (i, 0))
    table_spec = pl.BlockSpec((step, LANES), lambda i: (i, 0))
    out_spec = pl.BlockSpec((step, cols), lambda i: (i, 0))
    shape = jax.ShapeDtypeStruct((count, cols), bf16)
    return pl.pallas_call(
        project_kernel,
        grid=(3,),
        in_specs=[
            row_spec,
            pl.BlockSpec(weights.shape, lambda i: (0, 0, 0)),
            table_spec,
            table_spec,
        ],
        out_specs=[out_spec] * 3,
        out_shape=[shape] * 3,
        name="project",
        cost_estimate=pl.CostEstimate(
            flops=2 * count * width * 3 * cols,
            bytes_accessed=2 * (count * (width + 3 * cols) + 3 * width * cols),
            transcendentals=0,
        ),
    )(rows, weights, cosine, sine)


def normal(values):
    average = jnp.mean(values, axis=-1, keepdims=True)
    centred = values - average
    variance = jnp.mean(centred * centred, axis=-1, keepdims=True)
    scale = lax.rsqrt(variance + epsilon)
    return centred * scale, scale


def enter_kernel(
    tokens_ref,
    context_ref,
    vectors_ref,
    w_ref,
    cos_ref,
    sin_ref,
    rows_ref,
    rows_t_ref,
    q_ref,
    k_ref,
    v_ref,
):
    def norm(values):
        unit = normal(values.astype(f32))[0]
        return (unit * vectors_ref[0:1, :] + vectors_ref[1:2, :]).astype(bf16)

    def blocks(i, _):
        source = pl.ds(pl.multiple_of(i * TILE, TILE), TILE)
        rows_ref[source, :] = norm(context_ref[source, :])
        at = pl.ds(pl.multiple_of(CLEAN_OWN + i * TILE, TILE), TILE)
        rows_ref[at, :] = norm(tokens_ref[1, source, :])
        at = pl.ds(pl.multiple_of(NOISY_OWN + i * TILE, EDGE), TILE)
        rows_ref[at, :] = norm(tokens_ref[0, source, :])
        return 0

    lax.fori_loop(0, TILES, blocks, 0)
    rows_ref[2 * HALF : NOISY_BASE, :] = rows_ref[:EDGE, :]
    edge = norm(context_ref[HALF:, :])
    rows_ref[NOISY_BASE:NOISY_OWN, :] = edge
    rows_ref[NOISY_OWN + HALF :, :] = edge
    step = KEY_ROWS // 3

    def fields(i, _):
        at = pl.ds(pl.multiple_of(i * step, EDGE), step)
        project_rows(
            rows_ref[at, :], w_ref, cos_ref[at, :], sin_ref[at, :], q_ref, k_ref, v_ref, at
        )
        return 0

    lax.fori_loop(0, 3, fields, 0)
    for c in range(rows_t_ref.shape[0] // LANES):
        cols = slice(c * LANES, (c + 1) * LANES)
        rows_t_ref[cols, :] = rows_ref[:, cols].T


def enter(tokens, context, vectors, weights, cosine, sine):
    width, cols = weights.shape[1:]
    vmem = pl.BlockSpec(memory_space=pltpu.VMEM)
    shape = jax.ShapeDtypeStruct
    field = shape((KEY_ROWS, cols), bf16)
    return pl.pallas_call(
        enter_kernel,
        in_specs=[vmem] * 6,
        out_specs=[vmem] * 5,
        out_shape=[shape((KEY_ROWS, width), bf16), shape((width, KEY_ROWS), bf16)] + [field] * 3,
        name="enter",
        cost_estimate=pl.CostEstimate(
            flops=10**10, bytes_accessed=16 * 10**6, transcendentals=0
        ),
    )(tokens, context, vectors, weights, cosine, sine)


def split_heads(rows):
    low = low_lanes(rows.shape)
    zero = jnp.zeros_like(rows)
    return jnp.where(low, rows, zero), jnp.where(low, zero, rows)


def between(shape, offset, low, high):
    index = lax.broadcasted_iota(jnp.int32, shape, 0) + offset
    return jnp.logical_and(index >= low, index < high)


def fold(values, combine):
    rows, cols = values.shape
    groups = values.reshape(rows // 8, 8, cols)
    return combine(groups, axis=0)


def forward_kernel(
    span_ref, clean_ref, noisy_ref, q_ref, k_ref, v_ref, out_ref, lse_ref, bias_ref, window_ref
):
    pairs = q_ref.shape[1] // LANES
    lanes = [slice(p * LANES, (p + 1) * LANES) for p in range(pairs)]

    def one_tile(t, _):
        clean_at = pl.multiple_of(CLEAN_OWN + t * TILE, TILE)
        noisy_at = pl.multiple_of(NOISY_OWN + t * TILE, EDGE)
        window_at = pl.multiple_of(NOISY_BASE + t * TILE, EDGE)
        key_low, key_high = clean_ref[t, 0:1, :], clean_ref[t, 1:2, :]
        own_low, own_high = noisy_ref[t, 0:1, :], noisy_ref[t, 1:2, :]
        allowed = between((WINDOW, TILE), 0, own_low, own_high)
        window_ref[...] = jnp.where(allowed, 0.0, neg_large)
        first_key, trips = span_ref[t, 0], span_ref[t, 1]
        queries, tops = [], []
        for cols in lanes:
            query = jnp.concatenate(
                [q_ref[pl.ds(noisy_at, TILE), cols], q_ref[pl.ds(clean_at, TILE), cols]], axis=0
            )
            heads = split_heads(query)
            queries += heads
            keys = k_ref[pl.ds(window_at, WINDOW), cols]
            for head in range(2):
                scores = dot(keys, heads[head][:TILE], NT) + window_ref[...]
                top = fold(scores, jnp.max)
                tops.append(
                    jnp.concatenate([top, jnp.full((8, TILE), neg_large, f32)], axis=1)
                )

        def first_pass(j, tops):
            at = pl.multiple_of(first_key + j * KEY_TILE, EDGE)
            allowed = between((KEY_TILE, 2 * TILE), at, key_low, key_high)
            bias_ref[j] = jnp.where(allowed, 0.0, neg_large)
            after = []
            for p, cols in enumerate(lanes):
                keys = k_ref[pl.ds(at, KEY_TILE), cols]
                for head in range(2):
                    scores = dot(keys, queries[2 * p + head], NT) + bias_ref[j]
                    after.append(jnp.maximum(tops[2 * p + head], fold(scores, jnp.max)))
            return tuple(after)

        tops = lax.fori_loop(0, trips, first_pass, tuple(tops))
        tops = [jnp.max(top, axis=0, keepdims=True) * to_base2 for top in tops]
        state = []
        keys = [k_ref[pl.ds(window_at, WINDOW), cols] for cols in lanes]
        values_t = [v_ref[pl.ds(window_at, WINDOW), cols].T for cols in lanes]
        scores = dot(keys[0], queries[0][:TILE], NT)
        late = None
        for h in range(2 * pairs):
            if h + 1 < 2 * pairs:
                ahead = dot(keys[(h + 1) // 2], queries[h + 1][:TILE], NT)
            expo = jnp.exp2(scores * to_base2 - tops[h][:, :TILE] + window_ref[...])
            if late is not None:
                state.append(jnp.concatenate([late, jnp.zeros((HD, TILE), f32)], axis=1))
            total = fold(expo, jnp.sum)
            state.append(jnp.concatenate([total, jnp.zeros((8, TILE), f32)], axis=1))
            side = slice(h % 2 * HD, (h % 2 + 1) * HD)
            late = dot(values_t[h // 2][side], expo.astype(bf16))
            scores = ahead
        state.append(jnp.concatenate([late, jnp.zeros((HD, TILE), f32)], axis=1))

        def second_pass(j, state):
            at = pl.multiple_of(first_key + j * KEY_TILE, EDGE)
            keys = [k_ref[pl.ds(at, KEY_TILE), cols] for cols in lanes]
            values_t = [v_ref[pl.ds(at, KEY_TILE), cols].T for cols in lanes]
            after = list(state)
            scores = dot(keys[0], queries[0], NT)
            late = None
            for h in range(2 * pairs):
                ahead = dot(keys[(h + 1) // 2], queries[h + 1], NT) if h + 1 < 2 * pairs else None
                expo = jnp.exp2(scores * to_base2 - tops[h] + bias_ref[j])
                after[2 * h] = state[2 * h] + fold(expo, jnp.sum)
                if late is not None:
                    after[2 * h - 1] = state[2 * h - 1] + late
                side = slice(h % 2 * HD, (h % 2 + 1) * HD)
                late = dot(values_t[h // 2][side], expo.astype(bf16))
                scores = ahead
            after[-1] = state[-1] + late
            return tuple(after)

        state = lax.fori_loop(0, trips, second_pass, tuple(state))
        low_at = pl.ds(pl.multiple_of(t * TILE, TILE), TILE)
        high_at = pl.ds(pl.multiple_of(HALF + t * TILE, TILE), TILE)
        for p, cols in enumerate(lanes):
            halves = []
            for head in range(2):
                h = 2 * p + head
                total = jnp.sum(state[2 * h], axis=0, keepdims=True)
                halves.append(state[2 * h + 1] / total)
                lse_ref[p, t, head : head + 1, :] = tops[h] + jnp.log2(total)
            pair = jnp.concatenate(halves, axis=0).T.astype(bf16)
            out_ref[low_at, cols] = pair[:TILE]
            out_ref[high_at, cols] = pair[TILE:]
        return 0

    lax.fori_loop(0, TILES, one_tile, 0)


def attend_forward(spans, clean_bounds, noisy_bounds, query, keys, values):
    count, cols = query.shape
    pairs = cols // LANES
    vmem = pl.BlockSpec(memory_space=pltpu.VMEM)
    work = pairs * 2 * 2 * HALF * TOK_DEV
    return pl.pallas_call(
        forward_kernel,
        in_specs=[pl.BlockSpec(memory_space=pltpu.SMEM)] + [vmem] * 5,
        out_specs=[vmem] * 2,
        out_shape=[
            jax.ShapeDtypeStruct((TOK_DEV, cols), bf16),
            jax.ShapeDtypeStruct((pairs, TILES, 2, 2 * TILE), f32),
        ],
        scratch_shapes=[
            pltpu.VMEM((NOISY_BASE // KEY_TILE + 1, KEY_TILE, 2 * TILE), f32),
            pltpu.VMEM((WINDOW, TILE), f32),
        ],
        name="attend_forward",
        cost_estimate=pl.CostEstimate(
            flops=4 * work * HD, bytes_accessed=8 * count * cols, transcendentals=work
        ),
    )(spans, clean_bounds, noisy_bounds, query, keys, values)


def backward_kernel(
    giving,
    span_ref,
    clean_ref,
    noisy_ref,
    q_ref,
    k_ref,
    v_ref,
    o_ref,
    d_ref,
    lse_ref,
    cos_ref,
    sin_ref,
    *refs,
):
    if giving:
        d2_hbm, w_hbm, w2_hbm, out_ref, give_ref, low_ref, *refs = refs
        dk_ref, dv_ref, bias_ref, d2_ref, w_ref, w2_ref, load_sem = refs
        loads = [(w_hbm, w_ref), (w2_hbm, w2_ref)]
        loads += [(d2_hbm.at[c, :HALF], d2_ref.at[c]) for c in range(3)]
        loads = [
            pltpu.make_async_copy(source, target, load_sem.at[n])
            for n, (source, target) in enumerate(loads)
        ]
        for load in loads:
            load.start()
    else:
        rows_ref, out_ref, grad_ref, dk_ref, dv_ref, bias_ref = refs
    pairs = q_ref.shape[1] // LANES
    lanes = [slice(p * LANES, (p + 1) * LANES) for p in range(pairs)]
    dk_ref[...] = jnp.zeros_like(dk_ref)
    dv_ref[...] = jnp.zeros_like(dv_ref)
    out_ref[0] = jnp.zeros_like(out_ref[0])

    def one_tile(t, _):
        clean_at = pl.multiple_of(CLEAN_OWN + t * TILE, TILE)
        noisy_at = pl.multiple_of(NOISY_OWN + t * TILE, EDGE)
        window_at = pl.multiple_of(NOISY_BASE + t * TILE, EDGE)
        low_at = pl.multiple_of(t * TILE, TILE)
        high_at = pl.multiple_of(HALF + t * TILE, TILE)
        key_low, key_high = clean_ref[t, 0:1, :], clean_ref[t, 1:2, :]
        own_low, own_high = noisy_ref[t, 0:1, :], noisy_ref[t, 1:2, :]
        queries, d_outs, inners, lses = [], [], [], []
        for p, cols in enumerate(lanes):

            def both(ref, low, high):
                return jnp.concatenate(
                    [ref[pl.ds(low, TILE), cols], ref[pl.ds(high, TILE), cols]], axis=0
                )

            queries.append(split_heads(both(q_ref, noisy_at, clean_at)))
            d_rows = both(d_ref, low_at, high_at)
            o_rows = both(o_ref, low_at, high_at)
            product = (d_rows.astype(f32) * o_rows.astype(f32)).T
            d_outs.append(split_heads(d_rows))
            inners.append(
                [
                    jnp.sum(product[head * HD : (head + 1) * HD], axis=0, keepdims=True) * 0.125
                    for head in range(2)
                ]
            )
            lses.append([lse_ref[p, t, head : head + 1, :] for head in range(2)])

        def accumulate(at, rows, cols, allowed, d_query):
            bias_ref[:rows, :cols] = jnp.where(allowed, 0.0, neg_large)
            after = list(d_query)
            keys = [k_ref[pl.ds(at, rows), span] for span in lanes]
            eighth = [v_ref[pl.ds(at, rows), span] * jnp.asarray(0.125, bf16) for span in lanes]
            keys_t = [part.T for part in keys]
            stack = lambda parts: jnp.concatenate([part[:cols] for part in parts], axis=0)

            def begin(h):
                p, head = h // 2, h % 2
                return (
                    dot(keys[p], queries[p][head][:cols], NT),
                    dot(eighth[p], d_outs[p][head][:cols], NT),
                )

            def finish_pair(p, weights, d_scores):
                span = lanes[p]
                for head in range(2):
                    side = slice(head * HD, (head + 1) * HD)
                    h = 2 * p + head
                    after[h] = d_query[h] + dot(keys_t[p][side], d_scores[head])
                dv_ref[pl.ds(at, rows), span] += dot(
                    jnp.concatenate(weights, axis=1), stack(d_outs[p])
                )
                dk_ref[pl.ds(at, rows), span] += dot(
                    jnp.concatenate(d_scores, axis=1), stack(queries[p])
                )

            ready = begin(0)
            held = None
            weights, d_scores = [], []
            for h in range(2 * pairs):
                ahead = begin(h + 1) if h + 1 < 2 * pairs else None
                p, head = h // 2, h % 2
                scores = ready[0] * to_base2 - lses[p][head][:, :cols] + bias_ref[:rows, :cols]
                probs = jnp.exp2(scores)
                d_score = (probs * (ready[1] - inners[p][head][:, :cols])).astype(bf16)
                weights.append(probs.astype(bf16))
                d_scores.append(d_score)
                if held is not None:
                    finish_pair(*held)
                    held = None
                if head == 1:
                    held = (p, weights, d_scores)
                    weights, d_scores = [], []
                ready = ahead
            finish_pair(*held)
            return tuple(after)

        allowed = between((WINDOW, TILE), 0, own_low, own_high)
        zero = jnp.zeros((HD, TILE), f32)
        start = accumulate(window_at, WINDOW, TILE, allowed, (zero,) * (2 * pairs))
        start = tuple(jnp.concatenate([part, zero], axis=1) for part in start)
        first_key, trips = span_ref[t, 0], span_ref[t, 1]

        def one_step(j, d_query):
            at = pl.multiple_of(first_key + j * KEY_TILE, EDGE)
            allowed = between((KEY_TILE, 2 * TILE), at, key_low, key_high)
            return accumulate(at, KEY_TILE, 2 * TILE, allowed, d_query)

        d_query = lax.fori_loop(0, trips, one_step, start)
        for p, span in enumerate(lanes):
            pair = jnp.concatenate(d_query[2 * p : 2 * p + 2], axis=0).T
            for at, part in ((noisy_at, pair[:TILE]), (clean_at, pair[TILE:])):
                turned = turn(part, cos_ref[pl.ds(at, TILE), :], -sin_ref[pl.ds(at, TILE), :])
                out_ref[0, pl.ds(at, TILE), span] = turned.astype(bf16)
        return 0

    lax.fori_loop(0, TILES, one_tile, 0)
    step = KEY_ROWS // 9

    def finish(i, _):
        rows = pl.ds(pl.multiple_of(i * step, EDGE), step)
        for span in lanes:
            out_ref[1, rows, span] = turn(
                dk_ref[rows, span], cos_ref[rows, :], -sin_ref[rows, :]
            ).astype(bf16)
        out_ref[2, rows, :] = dv_ref[rows, :].astype(bf16)
        return 0

    lax.fori_loop(0, 9, finish, 0)

    def weight_rows(i, _):
        rows = pl.ds(pl.multiple_of(i * ROW_TILE, LANES), ROW_TILE)
        for c in range(3):
            grad_ref[c, rows, :] = dot(rows_ref[rows, :], out_ref[c]).astype(bf16)
        return 0

    if giving:
        for load in loads:
            load.wait()
        total = 0.0
        for c in range(3):
            total = total + dot(out_ref[c, :HALF, :], w_ref[c], NT) + dot(d2_ref[c], w2_ref[c], NT)
        give_ref[...] = total
        low_ref[...] = total.astype(bf16)
    else:
        lax.fori_loop(0, rows_ref.shape[0] // ROW_TILE, weight_rows, 0)


def attend_backward(
    spans,
    clean_bounds,
    noisy_bounds,
    query,
    keys,
    values,
    attended,
    d_attended,
    lse,
    cosine,
    sine,
    rest,
):
    count, cols = query.shape
    vmem = pl.BlockSpec(memory_space=pltpu.VMEM)
    hbm = pl.BlockSpec(memory_space=pl.ANY)
    shape = jax.ShapeDtypeStruct
    giving = len(rest) > 1
    if giving:
        width = rest[1].shape[1]
        second = [shape((HALF, width), f32), shape((HALF, width), bf16)]
        scratch = [
            pltpu.VMEM((3, HALF, cols), bf16),
            pltpu.VMEM(rest[1].shape, bf16),
            pltpu.VMEM(rest[2].shape, bf16),
            pltpu.SemaphoreType.DMA((5,)),
        ]
    else:
        second = [shape((3, rest[0].shape[0], cols), bf16)]
        scratch = []
    return pl.pallas_call(
        functools.partial(backward_kernel, giving),
        in_specs=[pl.BlockSpec(memory_space=pltpu.SMEM)]
        + [vmem] * 10
        + [hbm if giving else vmem] * len(rest),
        out_specs=[vmem] * (1 + len(second)),
        scratch_shapes=[
            pltpu.VMEM((count, cols), f32),
            pltpu.VMEM((count, cols), f32),
            pltpu.VMEM((max(KEY_TILE, WINDOW), 2 * TILE), f32),
        ]
        + scratch,
        out_shape=[shape((3, count, cols), bf16)] + second,
        name="attend_backward",
        cost_estimate=pl.CostEstimate(
            flops=36 * 10**9, bytes_accessed=36 * 10**6, transcendentals=6 * 10**6
        ),
    )(
        spans,
        clean_bounds,
        noisy_bounds,
        query,
        keys,
        values,
        attended,
        d_attended,
        lse,
        cosine,
        sine,
        *rest,
    )


PIECES = 16
MESH = pl.DeviceIdType.MESH


def flip(value, mask):
    result = value
    for b in range(mask.bit_length()):
        if mask >> b & 1:
            result = result + (1 << b) * (1 - 2 * ((value // (1 << b)) % 2))
    return result


class Exchange:
    def __init__(self, bits, count, rows, width, back=True):
        self.bits, self.count, self.rows, self.width = bits, count, rows, width
        self.back = back
        self.half, self.quarter, self.piece = rows // 2, rows // 4, rows // PIECES
        self.extra = list(range(4, bits))

    def slots(self):
        return 8 + 2 * (6 if self.back else 4) + (3 if self.extra else 0)

    def scratch(self):
        k, w = self.count, self.width
        cross = k if not self.back else 1
        shapes = [
            pltpu.VMEM((k, 2 - self.back, self.half, w), bf16),
            pltpu.VMEM((cross, self.half, w), bf16),
            pltpu.VMEM((cross, self.half, w), bf16),
            pltpu.VMEM((k, self.quarter, w), bf16),
            pltpu.VMEM((k, self.quarter, w), bf16),
            pltpu.VMEM((k, self.quarter, w), f32),
            pltpu.VMEM((k, 3, self.piece, w), bf16),
            pltpu.VMEM((k, 3, self.piece, w), bf16),
        ]
        lanes_of = (1, 0, 1, 3, 3, 1, 1) if self.back else (2, 1, 1, 3, 0, 0, 0)
        for lanes in [lanes for lanes in lanes_of if lanes]:
            shapes += [pltpu.SemaphoreType.DMA((k, lanes))] * 2
        if self.extra:
            n = len(self.extra)
            shapes += [pltpu.VMEM((k, 2 * n, self.piece, w), bf16)]
            shapes += [pltpu.SemaphoreType.DMA((k, n))] * 2
        return shapes

    def bind(self, place, part, refs):
        (self.a_in, self.b_out, self.b_in, self.c_out, self.c_in, self.keep) = refs[:6]
        self.d_out, self.d_in = refs[6:8]
        names = "acdefg" if self.back else "abcd"
        self.sems = {name: (refs[8 + 2 * i], refs[9 + 2 * i]) for i, name in enumerate(names)}
        if self.extra:
            at = 8 + 2 * len(names)
            self.x_buf, self.x_send, self.x_recv = refs[at : at + 3]
        self.place, self.part = place, part
        self.core, self.x, self.z = place % 2, (place // 2) % 2, (place // 4) % 4
        self.sibling = {"dp": flip(place, 1)}
        self.beside = {"dp": flip(place, 2)}
        self.across = {"mp": 1 - part}
        self.peers = [{"dp": flip(place, j << 2)} for j in range(1, 4)]
        self.partners = [self.sibling, self.beside, self.across] + self.peers
        self.partners += [{"dp": flip(place, 1 << b)} for b in self.extra]
        return self

    def greet(self):
        barrier = pltpu.get_barrier_semaphore()
        for partner in self.partners:
            pl.semaphore_signal(barrier, inc=1, device_id=partner, device_id_type=MESH)
        pl.semaphore_wait(barrier, len(self.partners))

    def copy(self, name, k, lane, source, target, device):
        out, into = self.sems[name]
        return pltpu.make_async_remote_copy(
            src_ref=source,
            dst_ref=target,
            send_sem=out.at[k, lane],
            recv_sem=into.at[k, lane],
            device_id=device,
            device_id_type=MESH,
        )

    def rows_at(self, start, size):
        return pl.ds(pl.multiple_of(start, PIECES), size)

    def copy_a(self, k, lane, grads):
        source = grads.at[k, self.rows_at((1 - self.core) * self.half, self.half)]
        return self.copy("a", k, lane, source, self.a_in.at[k, lane], self.sibling)

    def copy_b(self, k):
        return self.copy("b", k, 0, self.b_out.at[k], self.b_in.at[k], self.across)

    def copy_c(self, k):
        return self.copy("c", k, 0, self.c_out.at[k], self.c_in.at[k], self.beside)

    def copy_d(self, k, j):
        return self.copy("d", k, j, self.d_out.at[k, j], self.d_in.at[k, j], self.peers[j])

    def spot(self, change=0):
        start = self.core * self.half + self.x * self.quarter
        return self.rows_at(start + flip(self.z, change) * self.piece, self.piece)

    def copy_e(self, k, j, full):
        rows = full.at[k, self.spot()]
        return self.copy("e", k, j, rows, rows, self.peers[j])

    def copy_f(self, k, full):
        start = self.core * self.half + self.x * self.quarter
        rows = full.at[k, self.rows_at(start, self.quarter)]
        return self.copy("f", k, 0, rows, rows, self.beside)

    def copy_g(self, k, full):
        rows = full.at[k, self.rows_at(self.core * self.half, self.half)]
        return self.copy("g", k, 0, rows, rows, self.sibling)

    def start_a(self, k, lane, grads):
        self.copy_a(k, lane, grads).start()

    def stage_b(self, k, others):
        self.copy_a(k, 0, others).wait()
        mine = others[k, self.rows_at(self.core * self.half, self.half), :].astype(f32)
        self.b_out[k] = (mine + self.a_in[k, 0].astype(f32)).astype(bf16)
        self.copy_b(k).start()

    def stage_c(self, k, grads, crossed=None):
        lane = 0 if self.back else 1
        self.copy_a(k, lane, grads).wait()
        if not self.back:
            self.copy_b(k).wait()

        def total(which):
            inner = which * self.quarter
            rows = self.rows_at(inner, self.quarter)
            mine = grads[k, self.rows_at(self.core * self.half + inner, self.quarter), :]
            got = self.a_in[k, lane, rows, :].astype(f32)
            if not self.back:
                got = got + self.b_in[k, rows, :].astype(f32)
            elif crossed is not None:
                got = got + crossed(rows)
            return mine.astype(f32) + got

        self.c_out[k] = total(1 - self.x).astype(bf16)
        self.copy_c(k).start()
        self.keep[k] = total(self.x)

    def stage_d(self, k):
        self.copy_c(k).wait()
        for j in range(4):
            rows = self.rows_at(flip(self.z, j) * self.piece, self.piece)
            total = self.keep[k, rows, :] + self.c_in[k, rows, :].astype(f32)
            if j:
                self.d_out[k, j - 1] = total.astype(bf16)
                self.copy_d(k, j - 1).start()
            else:
                self.keep[k, rows, :] = total

    def gather_d(self, k):
        rows = self.rows_at(self.z * self.piece, self.piece)
        total = self.keep[k, rows, :]
        for j in range(3):
            self.copy_d(k, j).wait()
            total = total + self.d_in[k, j].astype(f32)
        for i, b in enumerate(self.extra):
            mine = self.x_buf.at[k, 2 * i]
            mine[...] = total.astype(bf16)
            swap = pltpu.make_async_remote_copy(
                src_ref=mine,
                dst_ref=self.x_buf.at[k, 2 * i + 1],
                send_sem=self.x_send.at[k, i],
                recv_sem=self.x_recv.at[k, i],
                device_id={"dp": flip(self.place, 1 << b)},
                device_id_type=MESH,
            )
            swap.start()
            swap.wait()
            total = total.astype(bf16).astype(f32) + self.x_buf[k, 2 * i + 1].astype(f32)
        return total.astype(bf16)

    def stage_e(self, k, full):
        full[k, self.spot(), :] = self.gather_d(k)
        for j in range(3):
            self.copy_e(k, j, full).start()

    def stage_f(self, k, full):
        for j in range(3):
            self.copy_e(k, j, full).wait()
        self.copy_f(k, full).start()

    def stage_g(self, k, full):
        self.copy_f(k, full).wait()
        self.copy_g(k, full).start()

    def stage_h(self, k, full):
        self.copy_g(k, full).wait()


def at_step(step, count, action):
    @pl.when(jnp.logical_and(step >= 0, step < count))
    def _():
        action(step)


def middle_kernel(exchanges, tiles, *refs):
    (
        x_ref,
        att_ref,
        att2_ref,
        wout_ref,
        wout2_ref,
        dy_ref,
        vectors_ref,
        bup_ref,
        up_mine,
        up_here,
        up_beside,
        down_mine,
        down_here,
        out_hbm,
        mid_hbm,
        datt_hbm,
        datt2_hbm,
        gout_ref,
        gout2_ref,
        gbup_ref,
        small_ref,
        pieces_ref,
        up_there,
        down_there,
        pass_up,
        pass_down,
        up_buf,
        down_buf,
        load_sem,
        n2_ref,
        total_ref,
        dn2_ref,
        act_ref,
        dpre_ref,
        n2_t,
        bup_other,
        bias_sem,
        out_ref,
        mid_ref,
        datt_ref,
        datt2_ref,
        store_sem,
        down_grad,
        up_grad,
        *rest,
    ) = refs
    place, part = lax.axis_index("dp"), lax.axis_index("mp")
    ex = exchanges[0].bind(place, part, rest)
    ex_up = exchanges[1].bind(place, part, rest[exchanges[0].slots() :])
    sides = ((ex, down_grad), (ex_up, up_grad))
    core = ex.core
    count = tiles // 2
    rows_all = x_ref.shape[0]
    blocks = rows_all // ROW_TILE
    width = x_ref.shape[1]
    lanes = width // 2

    def which(i):
        other = jnp.logical_or(i == 0, jnp.logical_and(i % 2 == 1, i < tiles - 1))
        mine = jnp.where(i == tiles - 1, count - 1, i // 2 - 1)
        return other, jnp.where(other, (i + 1) // 2, mine)

    quarter = width // 4
    strip = HIDDEN_TILE // 2
    held = 2 * core + ex.x
    kept = 2 * core + 1 - ex.x

    def load_up(i, source, h):
        target = up_buf.at[i % 2, h * quarter : (h + 1) * quarter]
        return pltpu.make_async_copy(source, target, load_sem.at[i % 2, h])

    def load_down(i, source, h):
        target = down_buf.at[i % 2, h * strip : (h + 1) * strip]
        return pltpu.make_async_copy(source, target, load_sem.at[i % 2, 4 + h])

    def hand_up(k, part_of):
        cols = pl.ds(pl.multiple_of(k * HIDDEN_TILE, HIDDEN_TILE), HIDDEN_TILE)
        side = ex.x if part_of == 0 else 1 - ex.x
        rows = pl.ds(pl.multiple_of(side * quarter, EDGE), quarter)
        return pltpu.make_async_remote_copy(
            src_ref=(up_here, up_beside)[part_of].at[:, cols],
            dst_ref=up_there.at[k, rows],
            send_sem=pass_up.at[k, 2 * part_of],
            recv_sem=pass_up.at[k, 2 * part_of + 1],
            device_id=ex.sibling,
            device_id_type=MESH,
        )

    def hand_down(b):
        return pltpu.make_async_remote_copy(
            src_ref=down_here.at[strip_rows(b)],
            dst_ref=down_there.at[b],
            send_sem=pass_down.at[b, 0],
            recv_sem=pass_down.at[b, 1],
            device_id=ex.sibling,
            device_id_type=MESH,
        )

    def strip_rows(b):
        return pl.ds(pl.multiple_of(b * strip, strip), strip)

    def start_loads(i):
        other, k = which(i)
        mine = jnp.logical_not(other)
        cols = pl.ds(pl.multiple_of(k * HIDDEN_TILE, HIDDEN_TILE), HIDDEN_TILE)

        @pl.when(other)
        def _():
            hand_up(k, 0).wait()
            hand_up(k, 1).wait()

        for h in range(4):

            @pl.when(mine)
            def _():
                load_up(i, up_mine.at[h * quarter : (h + 1) * quarter, cols], h).start()

            @pl.when(jnp.logical_and(other, held == h))
            def _():
                load_up(i, up_here.at[:, cols], h).start()

            @pl.when(jnp.logical_and(other, kept == h))
            def _():
                load_up(i, up_beside.at[:, cols], h).start()

            @pl.when(jnp.logical_and(other, core != h // 2))
            def _():
                rows = slice(h % 2 * quarter, (h % 2 + 1) * quarter)
                load_up(i, up_there.at[k, rows], h).start()

        for h in range(2):
            b = 2 * k + h
            inner = b % count

            @pl.when(mine)
            def _():
                load_down(i, down_mine.at[strip_rows(b), :], h).start()

            @pl.when(jnp.logical_and(other, core == b // count))
            def _():
                load_down(i, down_here.at[strip_rows(inner), :], h).start()

            @pl.when(jnp.logical_and(other, core != b // count))
            def _():
                hand_down(inner).wait_recv()
                load_down(i, down_there.at[inner], h).start()

    def wait_loads(i):
        for h in range(4):
            load_up(i, up_mine.at[:quarter, :HIDDEN_TILE], h).wait()
        for h in range(2):
            load_down(i, down_mine.at[:strip, :], h).wait()

    ex.greet()
    bias_swap = pltpu.make_async_remote_copy(
        src_ref=bup_ref,
        dst_ref=bup_other,
        send_sem=bias_sem.at[0],
        recv_sem=bias_sem.at[1],
        device_id=ex.across,
        device_id_type=MESH,
    )
    bias_swap.start()

    def hand(k, _):
        hand_up(k, 0).start()
        hand_up(k, 1).start()
        hand_down(k).start()
        return 0

    lax.fori_loop(0, count, hand, 0)

    def prologue(n, _):
        prologue_block(2 * n)
        prologue_block(2 * n + 1)
        return 0

    def prologue_block(r):
        rows = pl.ds(pl.multiple_of(r * ROW_TILE, ROW_TILE), ROW_TILE)
        branch = dot(att_ref[rows, :], wout_ref[...]) + dot(att2_ref[rows, :], wout2_ref[...])
        mid = x_ref[rows, :].astype(f32) + branch
        mid_ref[rows, :] = mid
        unit = normal(mid)[0]
        n2_ref[rows, :] = (unit * vectors_ref[2:3, :] + vectors_ref[3:4, :]).astype(bf16)
        total_ref[rows, :] = mid + vectors_ref[4:5, :]
        dn2_ref[rows, :] = jnp.zeros((ROW_TILE, width), f32)

    lax.fori_loop(0, blocks // 2, prologue, 0)
    start_loads(0)
    for c in range(width // LANES):
        cols = slice(c * LANES, (c + 1) * LANES)
        n2_t[cols, :] = n2_ref[:, cols].T
    n2_t[width:, :] = jnp.ones((PIECES, rows_all), bf16)
    bias_swap.wait()

    def tile(i):
        other, k = which(i)
        slot = i % 2
        wait_loads(i)

        @pl.when(i + 1 < tiles)
        def _():
            start_loads(i + 1)

        up, down = up_buf.at[slot], down_buf.at[slot]
        bias_at = jnp.where(other, k, count + k)
        bias = jnp.where(other, bup_other[k], bup_ref[k])
        linear = 0.7978845608028654
        cubic = linear * 0.044715
        for r in range(blocks):
            rows = slice(r * ROW_TILE, (r + 1) * ROW_TILE)
            pre = dot(n2_ref[rows, :], up[...]) + bias
            d_act = dot(dy_ref[rows, :], down[...], NT)
            square = pre * pre
            bend = jnp.tanh(pre * (square * cubic + linear))
            gate = 0.5 * bend + 0.5
            full_act = pre * gate
            slope = gate + (full_act - full_act * gate) * (square * (6.0 * cubic) + 2.0 * linear)
            act_ref[rows, :] = full_act.astype(bf16)
            dpre_ref[rows, :] = (d_act * slope).astype(bf16)
        total_ref[...] += dot(act_ref[...], down[...])
        dn2_ref[...] += dot(dpre_ref[...], up[...], NT)
        down_grad[k] = dot(act_ref[...].T, dy_ref[...]).astype(bf16)

        def start(lane):
            for side, grad in sides:
                side.start_a(k, lane, grad)

        by_rows = dot(n2_t[...], dpre_ref[...])
        up_grad[k] = by_rows[:width].astype(bf16)
        gbup_ref[bias_at] = by_rows[width : width + 1]
        pl.when(other)(functools.partial(start, 0))
        pl.when(jnp.logical_not(other))(functools.partial(start, 1))

    def each(k, when, action):
        @pl.when(jnp.logical_and(when, jnp.logical_and(k >= 0, k < count)))
        def _():
            for n, (side, grad) in enumerate(sides):
                action(n, side, grad, k)

    def stage_b(n, side, grad, k):
        side.stage_b(k, grad)

    def stage_c(n, side, grad, k):
        side.stage_c(k, grad)

    def stage_d(n, side, grad, k):
        side.stage_d(k)

    def arrive(n, side, grad, k):
        piece = side.gather_d(k)
        if n == 0:
            pieces_ref[k] = piece
        else:
            for c in range(width // HIDDEN_TILE):
                cols = slice(c * HIDDEN_TILE, (c + 1) * HIDDEN_TILE)
                pieces_ref[count + k, :, cols] = piece[c * PIECES : (c + 1) * PIECES]

    def steps(i):
        even = i % 2 == 0
        odd = jnp.logical_not(even)
        each((i - 5) // 2, odd, arrive)
        each((i - 4) // 2, even, stage_d)
        each((i - 3) // 2, odd, stage_c)
        each(i // 2, even, stage_b)

    def epilogue(r, _):
        rows = pl.ds(pl.multiple_of(r * ROW_TILE, ROW_TILE), ROW_TILE)
        out_ref[rows, :] = total_ref[rows, :].astype(bf16)
        unit, scale = normal(mid_ref[rows, :])
        d_rows = dn2_ref[rows, :]
        dy = dy_ref[rows, :].astype(f32)
        lean = d_rows * vectors_ref[2:3, :]
        d_mid = dy + scale * (
            lean
            - jnp.mean(lean, axis=-1, keepdims=True)
            - unit * jnp.mean(lean * unit, axis=-1, keepdims=True)
        )
        mid_ref[rows, :] = d_mid
        d_branch = d_mid.astype(bf16)
        n2_ref[rows, :] = d_branch
        datt_ref[rows, :] = dot(d_branch, wout_ref[...], NT).astype(bf16)
        datt2_ref[rows, :] = dot(d_branch, wout2_ref[...], NT).astype(bf16)
        add = lambda values: jnp.sum(values, axis=0, keepdims=True)
        small_ref[0:1, :] += add(d_rows * unit)
        small_ref[1:2, :] += add(d_rows)
        small_ref[2:3, :] += add(dy)
        return 0

    def out_grads():
        for source, target in ((att_ref, gout_ref), (att2_ref, gout2_ref)):
            grad = dot(source[...].T, n2_ref[...]).astype(bf16)
            for a in range(wout_ref.shape[0] // LANES):
                for b in range(2):
                    rows = slice(a * LANES, (a + 1) * LANES)
                    cols = slice(b * lanes, (b + 1) * lanes)
                    spread = slice(a * lanes, (a + 1) * lanes)
                    target[b * LANES : (b + 1) * LANES, spread] = grad[rows, cols]

    def main(i, _):
        pl.when(i < tiles)(functools.partial(tile, i))

        @pl.when(jnp.logical_and(i >= tiles, i < tiles + 2))
        def _():
            first = (i - tiles) * (blocks // 2)
            lax.fori_loop(first, first + blocks // 2, epilogue, 0)

        @pl.when(i == tiles + 2)
        def _():
            for store in stores:
                store.start()
            out_grads()

        steps(i)
        return 0

    small_ref[...] = jnp.zeros_like(small_ref)
    stores = [
        pltpu.make_async_copy(source, target, store_sem.at[n])
        for n, (source, target) in enumerate(
            (
                (datt2_ref, datt2_hbm),
                (out_ref, out_hbm),
                (mid_ref, mid_hbm),
                (datt_ref, datt_hbm),
            )
        )
    ]
    lax.fori_loop(0, tiles + 4, main, 0)
    for store in stores:
        store.wait()

    def handed(slot, _):
        hand_down(slot).wait_send()
        return 0

    lax.fori_loop(0, count, handed, 0)


def middle(bits, x, att, att2, wout, wout2, dy, vectors, bup, ups, downs):
    rows, width = x.shape
    hidden = ups[0].shape[1]
    count = hidden // HIDDEN_TILE
    tiles = 2 * count
    exchanges = (
        Exchange(bits, count, HIDDEN_TILE, width, False),
        Exchange(bits, count, width, HIDDEN_TILE, False),
    )
    vmem = pl.BlockSpec(memory_space=pltpu.VMEM)
    hbm = pl.BlockSpec(memory_space=pl.ANY)
    shape = jax.ShapeDtypeStruct
    depth = wout.shape[0]
    return pl.pallas_call(
        functools.partial(middle_kernel, exchanges, tiles),
        in_specs=[vmem] * 8 + [hbm] * 5,
        out_specs=[hbm] * 4 + [vmem] * 5,
        out_shape=[
            shape((rows, width), bf16),
            shape((rows, width), f32),
            shape(att.shape, bf16),
            shape(att2.shape, bf16),
            shape((2 * LANES, depth // LANES * width // 2), bf16),
            shape((2 * LANES, depth // LANES * width // 2), bf16),
            shape((tiles, 1, HIDDEN_TILE), f32),
            shape((8, width), f32),
            shape((2 * count, PIECES, width), bf16),
        ],
        scratch_shapes=[
            pltpu.VMEM((count, width // 2, HIDDEN_TILE), bf16),
            pltpu.VMEM((count, HIDDEN_TILE // 2, width), bf16),
            pltpu.SemaphoreType.DMA((count, 4)),
            pltpu.SemaphoreType.DMA((count, 2)),
            pltpu.VMEM((2, width, HIDDEN_TILE), bf16),
            pltpu.VMEM((2, HIDDEN_TILE, width), bf16),
            pltpu.SemaphoreType.DMA((2, 6)),
            pltpu.VMEM((rows, width), bf16),
            pltpu.VMEM((rows, width), f32),
            pltpu.VMEM((rows, width), f32),
            pltpu.VMEM((rows, HIDDEN_TILE), bf16),
            pltpu.VMEM((rows, HIDDEN_TILE), bf16),
            pltpu.VMEM((width + PIECES, rows), bf16),
            pltpu.VMEM(bup.shape, f32),
            pltpu.SemaphoreType.DMA((2,)),
            pltpu.VMEM((rows, width), bf16),
            pltpu.VMEM((rows, width), f32),
            pltpu.VMEM(att.shape, bf16),
            pltpu.VMEM(att2.shape, bf16),
            pltpu.SemaphoreType.DMA((4,)),
            pltpu.VMEM((count, HIDDEN_TILE, width), bf16),
            pltpu.VMEM((count, width, HIDDEN_TILE), bf16),
        ]
        + exchanges[0].scratch()
        + exchanges[1].scratch(),
        compiler_params=pltpu.CompilerParams(
            collective_id=0, has_side_effects=True, vmem_limit_bytes=67043328
        ),
        name="middle",
        cost_estimate=pl.CostEstimate(
            flops=60 * 10**9, bytes_accessed=40 * 10**6, transcendentals=4 * 10**6
        ),
    )(x, att, att2, wout, wout2, dy, vectors, bup, *ups, *downs)


def leave_kernel(exchange, *refs):
    (
        rows_hbm,
        mine_out_ref,
        crossed_ref,
        crossed_out_ref,
        d_hbm,
        d2_hbm,
        w_hbm,
        w2_hbm,
        tokens_ref,
        context_ref,
        given_ref,
        small_ref,
        small2_ref,
        gqkv_ref,
        gout_ref,
        back_hbm,
        sums_ref,
        full_ref,
        out_buf,
        rows_t_ref,
        d_ref,
        d2_ref,
        w_ref,
        w2_ref,
        load_sem,
        rows_ref,
        give_ref,
        take_ref,
        swap_sem,
        back_sem,
        norm_ref,
        near_ref,
        far_ref,
        near_sem,
        far_sem,
        *rest,
    ) = refs
    place, part = lax.axis_index("dp"), lax.axis_index("mp")
    ex = exchange.bind(place, part, rest)
    count, bits = ex.count, ex.bits
    loads = [
        pltpu.make_async_copy(source, target, load_sem.at[n])
        for n, (source, target) in enumerate(
            (
                (d_hbm, d_ref),
                (rows_hbm, rows_t_ref),
                (w_hbm, w_ref),
                (w2_hbm, w2_ref),
                (d2_hbm, d2_ref),
            )
        )
    ]
    for load in loads:
        load.start()
    near_id = part * 4 + place % 4
    near = [
        {"dp": flip(place, j % 4), "mp": part if j < 4 else 1 - part} for j in range(1, 8)
    ]
    ex.partners += [near[j - 1] for j in (3, 5, 6, 7)]
    ex.greet()

    lanes = d_ref.shape[2]
    split = mine_out_ref.shape[1] // lanes
    for r in range(split):
        cols = slice(r * lanes, (r + 1) * lanes)
        total = mine_out_ref[:, cols].astype(f32) + crossed_out_ref[:, cols].astype(f32)
        out_buf[r] = total.astype(bf16)
        ex.start_a(r, 0, out_buf)
    step = HALF + 2 * EDGE

    def back_rows(n):
        start = CLEAN_OWN + n * (KEY_ROWS - step - CLEAN_OWN)
        rows = pl.ds(pl.multiple_of(start, EDGE), step)
        total = 0.0
        for grads, weights in ((d_ref, w_ref), (d2_ref, w2_ref)):
            for c in range(3):
                total = total + dot(grads[c, rows, :], weights[c], NT)
        rows_ref[rows, :] = total

    def grad_chunk(c):
        for r in range(split):
            rows = slice(r * ROW_TILE, (r + 1) * ROW_TILE)
            k = (c + 1) * split + r
            out_buf[k] = dot(rows_t_ref[rows, :], d_ref[c]).astype(bf16)
            ex.start_a(k, 0, out_buf)

    def stage_c(k):
        @pl.when(k >= split)
        def _():
            ex.stage_c(k, out_buf, lambda rows: crossed_ref[k - split, rows, :].astype(f32))

        @pl.when(k < split)
        def _():
            ex.stage_c(k, out_buf)

    def arrive(k):
        ex.stage_h(k, full_ref)

        @pl.when(k < split)
        def _():
            rows = pl.ds(pl.multiple_of(k * LANES, LANES), LANES)
            for b in range(2):
                piece = full_ref[k, b * LANES : (b + 1) * LANES, :]
                gout_ref[rows, b * lanes : (b + 1) * lanes] = piece

        @pl.when(k >= split)
        def _():
            n = k - split
            rows = pl.ds(pl.multiple_of(n % split * ROW_TILE, ROW_TILE), ROW_TILE)
            gqkv_ref[n // split, rows, :] = full_ref[k]

    def group(g, action):
        @pl.when(jnp.logical_and(g >= 0, g < count // split))
        def _():
            lax.fori_loop(g * split, (g + 1) * split, lambda k, _: (action(k), 0)[1], 0)

    def steps(i):
        group(i - 5, arrive)
        group(i - 4, lambda k: ex.stage_g(k, full_ref))
        group(i - 3, lambda k: ex.stage_f(k, full_ref))
        group(i - 2, lambda k: ex.stage_e(k, full_ref))
        group(i - 1, lambda k: ex.stage_d(k))
        group(i, stage_c)

    width = tokens_ref.shape[1]

    def swap():
        return pltpu.make_async_remote_copy(
            src_ref=give_ref,
            dst_ref=take_ref,
            send_sem=swap_sem.at[0],
            recv_sem=swap_sem.at[1],
            device_id=ex.across,
            device_id_type=MESH,
        )

    def sums_of(d_rows, units):
        add = lambda values: jnp.sum(values, axis=0, keepdims=True)
        norm_ref[0:1, :] += add(d_rows * units)
        norm_ref[1:2, :] += add(d_rows)

    parts = tokens_ref.shape[0] // TILE
    lead = small_ref.shape[0] - 2
    bias = lead - 3
    norm_ref[...] = jnp.zeros_like(norm_ref)
    for load in loads[:2]:
        load.wait()

    def own_at(b):
        start = jnp.where(b < TILES, NOISY_OWN + b * TILE, CLEAN_OWN + (b - TILES) * TILE)
        return pl.ds(pl.multiple_of(start, EDGE), TILE)

    def tokens_at(b):
        return pl.ds(pl.multiple_of(b * TILE, TILE), TILE)

    def ready():
        for load in loads[2:5]:
            load.wait()

    def give_edges():
        side = rows_ref[NOISY_BASE:NOISY_OWN, :] + rows_ref[NOISY_OWN + HALF :, :]
        after = rows_ref[2 * HALF : NOISY_BASE, :]
        give_ref[:EDGE, :] = after.astype(bf16)
        give_ref[EDGE:, :] = side.astype(bf16)
        swap().start()
        sums_of(after, normal(context_ref[:EDGE, :].astype(f32))[0])
        sums_of(side, normal(context_ref[HALF:, :].astype(f32))[0])

    def tell_near():
        def context_sums(b, _):
            rows = tokens_at(b)
            sums_of(given_ref[rows, :], normal(context_ref[rows, :].astype(f32))[0])
            return 0

        lax.fori_loop(0, HALF // TILE, context_sums, 0)

        def own_sums(b, _):
            sums_of(rows_ref[own_at(b), :], normal(tokens_ref[tokens_at(b), :].astype(f32))[0])
            return 0

        lax.fori_loop(0, parts, own_sums, 0)
        blank = jnp.zeros((16 - lead - 2 - bias, width), f32)
        near_ref[near_id] = jnp.concatenate(
            [small_ref[:lead, :], norm_ref[:2, :], small2_ref[:bias, :], blank], axis=0
        ).astype(bf16)
        for j in range(1, 8):
            near_copy(j).start()

    def near_copy(j):
        return pltpu.make_async_remote_copy(
            src_ref=near_ref.at[near_id],
            dst_ref=near_ref.at[near_id],
            send_sem=near_sem.at[j, 0],
            recv_sem=near_sem.at[j, 1],
            device_id=near[j - 1],
            device_id_type=MESH,
        )

    def near_got(j):
        came = (part + j // 4) % 2 * 4 + flip(place % 4, j % 4)
        return pltpu.make_async_remote_copy(
            src_ref=near_ref.at[came],
            dst_ref=near_ref.at[came],
            send_sem=near_sem.at[j, 0],
            recv_sem=near_sem.at[j, 1],
            device_id=near[j - 1],
            device_id_type=MESH,
        )

    def far_copy(j, at):
        return pltpu.make_async_remote_copy(
            src_ref=far_ref.at[at],
            dst_ref=far_ref.at[at],
            send_sem=far_sem.at[j, 0],
            recv_sem=far_sem.at[j, 1],
            device_id=ex.peers[j - 1],
            device_id_type=MESH,
        )

    def tell_far():
        for j in range(1, 8):
            near_copy(j).wait_send()
            near_got(j).wait_recv()
        near_sum = lambda at: sum(near_ref[at + j].astype(f32) for j in range(1, 4)) + near_ref[
            at
        ].astype(f32)
        plane, other = near_sum(part * 4), near_sum((1 - part) * 4)
        total = near_sum(0) + near_sum(4)
        mixed = plane[:bias] + other[lead + 2 : lead + 2 + bias]
        far_ref[ex.z] = jnp.concatenate([mixed, total[bias:]], axis=0).astype(bf16)
        for j in range(1, 4):
            far_copy(j, ex.z).start()

    halves = [
        pltpu.make_async_copy(
            rows_ref.at[start : start + HALF],
            back_hbm.at[n * HALF : (n + 1) * HALF],
            back_sem.at[n],
        )
        for n, start in enumerate((NOISY_OWN, CLEAN_OWN))
    ]

    def take_back():
        swap().wait()
        begin = slice(CLEAN_OWN, CLEAN_OWN + EDGE)
        rows_ref[begin, :] += take_ref[:EDGE, :].astype(f32)
        edge = pl.ds(pl.multiple_of(NOISY_OWN + (1 - part) * (HALF - EDGE), EDGE), EDGE)
        rows_ref[edge, :] += take_ref[EDGE:, :].astype(f32)
        for half in halves:
            half.start()

    def end_far():
        for j in range(1, 4):
            far_copy(j, ex.z).wait_send()
            far_copy(j, flip(ex.z, j)).wait_recv()
        total = far_ref[0].astype(f32)
        for j in range(1, 4):
            total = total + far_ref[j].astype(f32)
        for i, b in enumerate(ex.extra):
            total = total.astype(bf16).astype(f32)
            far_ref[4 + 2 * i] = total.astype(bf16)
            trade = pltpu.make_async_remote_copy(
                src_ref=far_ref.at[4 + 2 * i],
                dst_ref=far_ref.at[5 + 2 * i],
                send_sem=far_sem.at[4 + i, 0],
                recv_sem=far_sem.at[4 + i, 1],
                device_id={"dp": flip(place, 1 << b)},
                device_id_type=MESH,
            )
            trade.start()
            trade.wait()
            total = total + far_ref[5 + 2 * i].astype(f32)
        sums_ref[...] = total

    groups = count // split - 1
    actions = {
        groups + 1: give_edges,
        groups + 2: tell_near,
        groups + 3: take_back,
        groups + 4: tell_far,
        groups + 6: end_far,
    }

    def phase(p, _):
        @pl.when(p < groups)
        def _():
            grad_chunk(p)

        pl.when(p == groups)(ready)

        @pl.when(jnp.logical_and(p >= groups, p < groups + 2))
        def _():
            back_rows(p - groups)

        for n, action in actions.items():
            pl.when(p == n)(action)
        steps(p)
        return 0

    lax.fori_loop(0, groups + 7, phase, 0)
    for half in halves:
        half.wait()


def leave(bits, rows_t, mine, crossed, d_fields, weights, tokens, context, given, small, small2):
    rows, cols = ROW_TILE, d_fields[0].shape[2]
    total = mine.shape[1] // cols + crossed[0].shape[0]
    exchange = Exchange(bits, total, rows, cols)
    count, width = tokens.shape
    vmem = pl.BlockSpec(memory_space=pltpu.VMEM)
    hbm = pl.BlockSpec(memory_space=pl.ANY)
    shape = jax.ShapeDtypeStruct
    return pl.pallas_call(
        functools.partial(leave_kernel, exchange),
        in_specs=[hbm] + [vmem] * 3 + [hbm] * 4 + [vmem] * 5,
        out_specs=[vmem] * 2 + [hbm, vmem],
        out_shape=[
            shape(weights[0].shape, bf16),
            shape((d_fields[0].shape[2], width), bf16),
            shape((count, width), f32),
            shape((16, width), f32),
        ],
        scratch_shapes=[
            pltpu.VMEM((total, rows, cols), bf16),
            pltpu.VMEM((total, rows, cols), bf16),
            pltpu.VMEM(rows_t.shape, bf16),
            pltpu.VMEM(d_fields[0].shape, bf16),
            pltpu.VMEM(d_fields[1].shape, bf16),
            pltpu.VMEM(weights[0].shape, bf16),
            pltpu.VMEM(weights[1].shape, bf16),
            pltpu.SemaphoreType.DMA((5,)),
            pltpu.VMEM((KEY_ROWS, width), f32),
            pltpu.VMEM((2 * EDGE, width), bf16),
            pltpu.VMEM((2 * EDGE, width), bf16),
            pltpu.SemaphoreType.DMA((2,)),
            pltpu.SemaphoreType.DMA((2,)),
            pltpu.VMEM((8, width), f32),
            pltpu.VMEM((8, 16, width), bf16),
            pltpu.VMEM((4 + 2 * len(exchange.extra), 16, width), bf16),
            pltpu.SemaphoreType.DMA((8, 2)),
            pltpu.SemaphoreType.DMA((4 + len(exchange.extra), 2)),
        ]
        + exchange.scratch(),
        compiler_params=pltpu.CompilerParams(
            collective_id=1, has_side_effects=True, vmem_limit_bytes=67043328
        ),
        name="leave",
        cost_estimate=pl.CostEstimate(
            flops=40 * 10**9, bytes_accessed=40 * 10**6, transcendentals=0
        ),
    )(
        rows_t, mine, *crossed, *d_fields, *weights, tokens, context, given, small, small2
    )


def finish_kernel(rows_ref, got_ref, tokens_ref, vectors_ref, dmid_ref, out_ref):
    clean = pl.program_id(0) >= pl.num_programs(0) // 2
    got = jnp.where(clean, got_ref[...].astype(f32), 0.0)
    unit, scale = normal(tokens_ref[...].astype(f32))
    lean = (rows_ref[...] + got) * vectors_ref[0:1, :]
    out_ref[...] = dmid_ref[...] + scale * (
        lean
        - jnp.mean(lean, axis=-1, keepdims=True)
        - unit * jnp.mean(lean * unit, axis=-1, keepdims=True)
    )


def finish(rows, got, tokens, vectors, d_mid):
    count, width = rows.shape
    spec = pl.BlockSpec((TILE, width), lambda b: (b, 0))
    half = count // TILE // 2
    return pl.pallas_call(
        finish_kernel,
        grid=(count // TILE,),
        in_specs=[
            spec,
            pl.BlockSpec((TILE, width), lambda b: (jnp.maximum(b - half, 0), 0)),
            spec,
            pl.BlockSpec(vectors.shape, lambda b: (0, 0)),
            spec,
        ],
        out_specs=spec,
        out_shape=jax.ShapeDtypeStruct((count, width), f32),
        name="finish",
        cost_estimate=pl.CostEstimate(
            flops=10**7, bytes_accessed=12 * 10**6, transcendentals=0
        ),
    )(rows, got, tokens, vectors, d_mid)


def assemble_kernel(
    core_ref, down_mine, up_mine, down_got, up_got, qkv_low, out_low, down_ref, up_ref, qkv_ref, out_ref
):
    qkv_ref[...] = qkv_low[...].astype(f32)
    out_ref[...] = out_low[...].astype(f32)
    core = core_ref[0]
    block = down_mine.shape[1]
    lanes = up_ref.shape[1]
    parts = down_mine.shape[2] // lanes
    deep = block * parts
    for side, down, up in ((core, down_mine, up_mine), (1 - core, down_got, up_got)):
        rows = pl.ds(pl.multiple_of(side * block, block), block)
        down_ref[rows, :] = down[0].astype(f32)
        for n in range(block // PIECES):
            for c in range(parts):
                at = side * deep + (n * parts + c) * PIECES
                rows = pl.ds(pl.multiple_of(at, PIECES), PIECES)
                piece = up[0, n * PIECES : (n + 1) * PIECES, c * lanes : (c + 1) * lanes]
                up_ref[rows, :] = piece.astype(f32)


def assemble(core, gathered, moved, qkv, out):
    tiles, half, width = gathered.shape
    count = tiles // 2
    down_spec = pl.BlockSpec((1, half, width), lambda k, c: (k, 0, 0))
    up_spec = pl.BlockSpec((1, half, width), lambda k, c: (count + k, 0, 0))
    hidden = count * 2 * half
    qkv_spec = pl.BlockSpec((qkv.shape[0] // count, qkv.shape[1]), lambda k, c: (k, 0))
    out_spec = pl.BlockSpec((out.shape[0] // count, out.shape[1]), lambda k, c: (k, 0))
    return pl.pallas_call(
        assemble_kernel,
        grid_spec=pltpu.PrefetchScalarGridSpec(
            num_scalar_prefetch=1,
            grid=(count,),
            in_specs=[down_spec, up_spec, down_spec, up_spec, qkv_spec, out_spec],
            out_specs=[
                pl.BlockSpec((2 * half, width), lambda k, c: (k, 0)),
                pl.BlockSpec((width, 2 * half), lambda k, c: (0, k)),
                qkv_spec,
                out_spec,
            ],
        ),
        out_shape=[
            jax.ShapeDtypeStruct((hidden, width), f32),
            jax.ShapeDtypeStruct((width, hidden), f32),
            jax.ShapeDtypeStruct(qkv.shape, f32),
            jax.ShapeDtypeStruct(out.shape, f32),
        ],
        name="assemble",
        cost_estimate=pl.CostEstimate(
            flops=10**6, bytes_accessed=14 * 10**6, transcendentals=0
        ),
    )(core, gathered, gathered, moved, moved, qkv, out)


def key_layout(seq_lengths, block_len, part):
    index = jnp.arange(KEY_ROWS, dtype=jnp.int32)
    own = part * HALF
    token = jnp.where(
        index < NOISY_BASE, index + (own - HALF), index - NOISY_BASE + (own - EDGE)
    )
    ends = jnp.cumsum(seq_lengths)
    passed = token[:, None] >= ends[None, :]
    starts = jnp.sum(jnp.where(passed, seq_lengths[None, :], 0), axis=1)
    lengths_here = jnp.where(passed, 0, ends[None, :])
    stops = jnp.min(jnp.where(passed, TOK_DEV, lengths_here), axis=1)
    positions = token - starts
    block_start = starts + positions // block_len * block_len
    block_stop = jnp.minimum(block_start + block_len, stops)
    mine = slice(CLEAN_OWN, CLEAN_OWN + HALF)
    low, start, stop = starts[mine], block_start[mine], block_stop[mine]
    to_clean = own - HALF
    tiles = lambda column: column.reshape(TILES, 1, TILE)
    clean_bounds = jnp.concatenate(
        [
            jnp.concatenate([tiles(low - to_clean), tiles(low - to_clean)], axis=2),
            jnp.concatenate([tiles(start - to_clean), tiles(stop - to_clean)], axis=2),
        ],
        axis=1,
    )
    to_window = own - EDGE + TILE * jnp.arange(TILES, dtype=jnp.int32)[:, None, None]
    noisy_bounds = jnp.concatenate(
        [tiles(start) - to_window, tiles(stop) - to_window], axis=1
    )
    first = jnp.min(clean_bounds[:, 0], axis=1) // EDGE * EDGE
    last = jnp.max(clean_bounds[:, 1], axis=1)
    trips = (last - first + KEY_TILE - 1) // KEY_TILE
    spans = jnp.stack([first, trips], axis=1)
    lane = jnp.arange(LANES, dtype=jnp.int32)
    frequency = jnp.exp(
        (lane % (HD // 2)).astype(f32) * (-math.log(10000.0) / (HD // 2))
    )
    angles = positions.astype(f32)[:, None] * frequency[None, :]
    sign = jnp.where(lane % HD < HD // 2, -1.0, 1.0)
    return spans, clean_bounds, noisy_bounds, jnp.cos(angles), jnp.sin(angles) * sign


def in_order(bit, mine, theirs, axis=0):
    order = bit == 0
    return jnp.concatenate(
        [jnp.where(order, mine, theirs), jnp.where(order, theirs, mine)], axis=axis
    )


def tie(first, second):
    return lax.optimization_barrier((first, second))


def local(
    dp_size,
    tokens,
    lengths,
    block_size,
    cotangent,
    ln1_gain,
    ln1_bias,
    w_qkv,
    w_out,
    ln2_gain,
    ln2_bias,
    w_up,
    b_up,
    w_down,
    b_down,
):
    width = tokens.shape[2]
    part = lax.axis_index("mp")
    place = lax.axis_index("dp")
    bits = dp_size.bit_length() - 1
    core = place & 1

    def across(array):
        return lax.ppermute(array, "mp", [(0, 1), (1, 0)])

    def sibling(array):
        return lax.ppermute(array, "dp", [(i, i ^ 1) for i in range(dp_size)])

    def beside(array):
        return lax.ppermute(array, "dp", [(i, i ^ 2) for i in range(dp_size)])

    edge = jnp.where(part == 0, tokens[0, HALF - EDGE :], tokens[0, :EDGE])
    context = across(jnp.concatenate([tokens[1], edge], axis=0))
    qkv_mine = w_qkv.transpose(1, 0, 2)
    side = (place >> 1) & 1

    def quarter_of(array, axis=0):
        size = array.shape[axis] // 4
        return lax.dynamic_slice_in_dim(array, (2 * core + side) * size, size, axis)

    def half_of(array):
        size = array.shape[0] // 2
        return lax.dynamic_slice_in_dim(array, core * size, size, 0)

    quarters = [quarter_of(qkv_mine, 1), quarter_of(w_up), half_of(w_down), half_of(w_out)]
    layout = key_layout(lengths[0], block_size[0], part)
    vectors = jnp.stack([ln1_gain, ln1_bias, ln2_gain, ln2_bias, b_down])
    context, (quarters, layout, vectors) = tie(context, (quarters, layout, vectors))
    qkv_here, up_here, down_here, out_here = [across(piece) for piece in quarters]

    spans, clean_bounds, noisy_bounds, cosine, sine = layout
    normed1, normed1_t, *fields = enter(tokens, context, vectors, qkv_mine, cosine, sine)
    qkv_here, fields = tie(qkv_here, fields)
    qkv_beside = beside(qkv_here)
    mine = [*fields, *attend_forward(spans, clean_bounds, noisy_bounds, *fields)]
    (qkv_here, qkv_beside, up_here, out_here), _ = tie(
        (qkv_here, qkv_beside, up_here, out_here), mine[3]
    )
    out_there = sibling(out_here)
    qkv_half = in_order(side, qkv_here, qkv_beside, axis=1)
    qkv_other = in_order(core, qkv_half, sibling(qkv_half), axis=1)
    up_beside = beside(up_here)
    fields = project(normed1, qkv_other, cosine, sine)
    (out_here, out_there), fields = tie((out_here, out_there), fields)
    out_other = in_order(core, out_here, out_there)
    out_other, fields = tie(out_other, fields)
    other = [*fields, *attend_forward(spans, clean_bounds, noisy_bounds, *fields)]
    (up_here, up_beside, down_here), _ = tie((up_here, up_beside, down_here), other[3])
    bias_all = b_up.astype(f32).reshape(-1, 1, HIDDEN_TILE)

    x_rows = tokens.reshape(TOK_DEV, width)
    out, d_mid, d_att, d_att2, grad_out, grad_out2, grad_bias, norms, pieces = middle(
        bits,
        x_rows,
        mine[3],
        other[3],
        w_out,
        out_other,
        cotangent.reshape(TOK_DEV, width),
        vectors,
        bias_all,
        (w_up, up_here, up_beside),
        (w_down, down_here),
    )
    hidden = b_up.shape[0]

    crossed_out = across(grad_out2)
    spread = [(b, min(2, min(bits, 4) - b)) for b in range(2, min(bits, 4), 2)]
    gathered = pieces
    ((first_bit, n),) = spread
    moved = [
        lax.ppermute(gathered, "dp", [(i, i ^ (k << first_bit)) for i in range(dp_size)])
        for k in range(1, 1 << n)
    ]

    def backward(saved, d_attended, spans, *rest):
        query, keys, values, attended, lse = saved
        return attend_backward(
            spans,
            clean_bounds,
            noisy_bounds,
            query,
            keys,
            values,
            attended,
            d_attended,
            lse,
            cosine,
            sine,
            rest,
        )

    d_fields2, grad2 = backward(other, d_att2, spans, normed1_t)
    grad2 = grad2.reshape(-1, ROW_TILE, grad2.shape[2])
    low_bit, high_bit = (place >> 2) & 1, (place >> 3) & 1
    moved, _ = tie(moved, grad2)
    gathered = in_order(
        high_bit,
        in_order(low_bit, gathered, moved[0], 1),
        in_order(low_bit, moved[1], moved[2], 1),
        1,
    )
    half = ROW_TILE // 2
    part_of = lambda array, which: lax.dynamic_slice_in_dim(array, which * half, half, 1)
    got = sibling(part_of(grad2, 1 - core))
    crossing = (part_of(grad2, core).astype(f32) + got.astype(f32)).astype(bf16)
    (crossing, gathered), spans = tie((crossing, gathered), spans)
    crossed = across(crossing)
    moved = beside(gathered)
    d_fields1, given, give = backward(mine, d_att, spans, d_fields2, qkv_mine, qkv_other)
    took = across(give)
    moved, d_fields1 = tie(moved, d_fields1)
    gathered = in_order(side, gathered, moved, 1)
    gathered, d_fields1 = tie(gathered, d_fields1)
    moved = sibling(gathered)
    lead = hidden // width
    bias2, bias1 = grad_bias.reshape(2, lead, width)
    shared = jnp.concatenate([norms[:3], jnp.zeros((2, width), f32)], axis=0)
    grad_qkv, grad_out, d_rows, sums = leave(
        bits,
        normed1_t,
        grad_out,
        (crossed, crossed_out),
        (d_fields1, d_fields2),
        (qkv_mine, qkv_other),
        x_rows,
        context,
        given,
        jnp.concatenate([bias1, shared], axis=0),
        jnp.concatenate([bias2, shared], axis=0),
    )
    (moved, took), grad_qkv = tie((moved, took), grad_qkv)
    grad_tokens = finish(d_rows, took, x_rows, vectors, d_mid)
    grad_down, grad_up, grad_qkv, grad_out = assemble(
        core.reshape(1), gathered, moved, grad_qkv.reshape(-1, grad_qkv.shape[2]), grad_out
    )
    return (
        out.reshape(tokens.shape),
        grad_tokens.reshape(tokens.shape),
        sums[lead + 3],
        sums[lead + 4],
        grad_qkv.reshape(qkv_mine.shape).transpose(1, 0, 2),
        grad_out,
        sums[lead],
        sums[lead + 1],
        grad_up,
        sums[:lead].reshape(hidden),
        grad_down,
        sums[lead + 2],
    )


def solution(mesh):
    in_specs = (
        P(None, ("dp", "mp"), None),
        P("dp", None),
        P(),
        P(None, ("dp", "mp"), None),
        P(),
        P(),
        P(None, None, "mp"),
        P("mp", None),
        P(),
        P(),
        P(None, "mp"),
        P("mp"),
        P("mp", None),
        P(),
    )
    out_specs = (
        P(None, ("dp", "mp"), None),
        P(None, ("dp", "mp"), None),
        P(),
        P(),
        P(None, None, "mp"),
        P("mp", None),
        P(),
        P(),
        P(None, "mp"),
        P("mp"),
        P("mp", None),
        P(),
    )
    return jax.shard_map(
        functools.partial(local, mesh.shape["dp"]),
        mesh=mesh,
        in_specs=in_specs,
        out_specs=out_specs,
        check_vma=False,
    )
```

```python
import functools
import math

import jax
import jax.numpy as jnp
from jax import lax
from jax.experimental import pallas as pl
from jax.experimental.pallas import tpu as pltpu
from jax.sharding import PartitionSpec as P

HD = 64
TOK_DEV = 1024
HALF = TOK_DEV // 2
EDGE = 16
CLEAN_OWN = HALF
NOISY_BASE = 2 * HALF + EDGE
NOISY_OWN = NOISY_BASE + EDGE
KEY_ROWS = NOISY_OWN + HALF + EDGE
TILE = 128
TILES = HALF // TILE
WINDOW = TILE + 2 * EDGE
KEY_TILE = 192
LANES = 128
HIDDEN_TILE = 256
ROW_TILE = 256

epsilon = 1e-05
neg_large = -1e30
to_base2 = 0.125 * math.log2(math.e)
f32 = jnp.float32
bf16 = jnp.bfloat16

NN = (((1,), (0,)), ((), ()))
NT = (((1,), (1,)), ((), ()))


def dot(left, right, dims=NN):
    return lax.dot_general(left, right, dims, preferred_element_type=f32)


def low_lanes(shape):
    return lax.broadcasted_iota(jnp.int32, shape, 1) < HD


def turn(values, cosine, sine):
    lane = lax.broadcasted_iota(jnp.int32, values.shape, 1)
    first_half = (lane & (HD - 1)) < HD // 2
    swapped = jnp.where(
        first_half,
        pltpu.roll(values, LANES - HD // 2, 1),
        pltpu.roll(values, HD // 2, 1),
    )
    return values * cosine + swapped * sine


def project_rows(rows, w_ref, cosine, sine, q_ref, k_ref, v_ref, at):
    for part, out_ref in ((0, q_ref), (1, k_ref)):
        field = dot(rows, w_ref[part])
        for pair in range(field.shape[1] // LANES):
            cols = slice(pair * LANES, (pair + 1) * LANES)
            out_ref[at, cols] = turn(field[:, cols], cosine, sine).astype(bf16)
    v_ref[at, :] = dot(rows, w_ref[2]).astype(bf16)


def project_kernel(rows_ref, w_ref, cos_ref, sin_ref, q_ref, k_ref, v_ref):
    at = slice(0, rows_ref.shape[0])
    project_rows(rows_ref[...], w_ref, cos_ref[...], sin_ref[...], q_ref, k_ref, v_ref, at)


def project(rows, weights, cosine, sine):
    count, width = rows.shape
    cols = weights.shape[2]
    step = count // 3
    row_spec = pl.BlockSpec((step, width), lambda i: (i, 0))
    table_spec = pl.BlockSpec((step, LANES), lambda i: (i, 0))
    out_spec = pl.BlockSpec((step, cols), lambda i: (i, 0))
    shape = jax.ShapeDtypeStruct((count, cols), bf16)
    return pl.pallas_call(
        project_kernel,
        grid=(3,),
        in_specs=[
            row_spec,
            pl.BlockSpec(weights.shape, lambda i: (0, 0, 0)),
            table_spec,
            table_spec,
        ],
        out_specs=[out_spec] * 3,
        out_shape=[shape] * 3,
        name="project",
        cost_estimate=pl.CostEstimate(
            flops=2 * count * width * 3 * cols,
            bytes_accessed=2 * (count * (width + 3 * cols) + 3 * width * cols),
            transcendentals=0,
        ),
    )(rows, weights, cosine, sine)


def normal(values):
    average = jnp.mean(values, axis=-1, keepdims=True)
    centred = values - average
    variance = jnp.mean(centred * centred, axis=-1, keepdims=True)
    scale = lax.rsqrt(variance + epsilon)
    return centred * scale, scale


def enter_kernel(
    tokens_ref,
    context_ref,
    vectors_ref,
    w_ref,
    cos_ref,
    sin_ref,
    rows_ref,
    rows_t_ref,
    q_ref,
    k_ref,
    v_ref,
):
    def norm(values):
        unit = normal(values.astype(f32))[0]
        return (unit * vectors_ref[0:1, :] + vectors_ref[1:2, :]).astype(bf16)

    def blocks(i, _):
        source = pl.ds(pl.multiple_of(i * TILE, TILE), TILE)
        rows_ref[source, :] = norm(context_ref[source, :])
        at = pl.ds(pl.multiple_of(CLEAN_OWN + i * TILE, TILE), TILE)
        rows_ref[at, :] = norm(tokens_ref[1, source, :])
        at = pl.ds(pl.multiple_of(NOISY_OWN + i * TILE, EDGE), TILE)
        rows_ref[at, :] = norm(tokens_ref[0, source, :])
        return 0

    lax.fori_loop(0, TILES, blocks, 0)
    rows_ref[2 * HALF : NOISY_BASE, :] = rows_ref[:EDGE, :]
    edge = norm(context_ref[HALF:, :])
    rows_ref[NOISY_BASE:NOISY_OWN, :] = edge
    rows_ref[NOISY_OWN + HALF :, :] = edge
    step = KEY_ROWS // 3

    def fields(i, _):
        at = pl.ds(pl.multiple_of(i * step, EDGE), step)
        project_rows(
            rows_ref[at, :], w_ref, cos_ref[at, :], sin_ref[at, :], q_ref, k_ref, v_ref, at
        )
        return 0

    lax.fori_loop(0, 3, fields, 0)
    for c in range(rows_t_ref.shape[0] // LANES):
        cols = slice(c * LANES, (c + 1) * LANES)
        rows_t_ref[cols, :] = rows_ref[:, cols].T


def enter(tokens, context, vectors, weights, cosine, sine):
    width, cols = weights.shape[1:]
    vmem = pl.BlockSpec(memory_space=pltpu.VMEM)
    shape = jax.ShapeDtypeStruct
    field = shape((KEY_ROWS, cols), bf16)
    return pl.pallas_call(
        enter_kernel,
        in_specs=[vmem] * 6,
        out_specs=[vmem] * 5,
        out_shape=[shape((KEY_ROWS, width), bf16), shape((width, KEY_ROWS), bf16)] + [field] * 3,
        name="enter",
        cost_estimate=pl.CostEstimate(
            flops=10**10, bytes_accessed=16 * 10**6, transcendentals=0
        ),
    )(tokens, context, vectors, weights, cosine, sine)


def split_heads(rows):
    low = low_lanes(rows.shape)
    zero = jnp.zeros_like(rows)
    return jnp.where(low, rows, zero), jnp.where(low, zero, rows)


def between(shape, offset, low, high):
    index = lax.broadcasted_iota(jnp.int32, shape, 0) + offset
    return jnp.logical_and(index >= low, index < high)


def fold(values, combine):
    rows, cols = values.shape
    groups = values.reshape(rows // 8, 8, cols)
    return combine(groups, axis=0)


def forward_kernel(
    span_ref, clean_ref, noisy_ref, q_ref, k_ref, v_ref, out_ref, lse_ref, bias_ref, window_ref
):
    pairs = q_ref.shape[1] // LANES
    lanes = [slice(p * LANES, (p + 1) * LANES) for p in range(pairs)]

    def one_tile(t, _):
        clean_at = pl.multiple_of(CLEAN_OWN + t * TILE, TILE)
        noisy_at = pl.multiple_of(NOISY_OWN + t * TILE, EDGE)
        window_at = pl.multiple_of(NOISY_BASE + t * TILE, EDGE)
        key_low, key_high = clean_ref[t, 0:1, :], clean_ref[t, 1:2, :]
        own_low, own_high = noisy_ref[t, 0:1, :], noisy_ref[t, 1:2, :]
        allowed = between((WINDOW, TILE), 0, own_low, own_high)
        window_ref[...] = jnp.where(allowed, 0.0, neg_large)
        first_key, trips = span_ref[t, 0], span_ref[t, 1]
        queries, tops = [], []
        for cols in lanes:
            query = jnp.concatenate(
                [q_ref[pl.ds(noisy_at, TILE), cols], q_ref[pl.ds(clean_at, TILE), cols]], axis=0
            )
            heads = split_heads(query)
            queries += heads
            keys = k_ref[pl.ds(window_at, WINDOW), cols]
            for head in range(2):
                scores = dot(keys, heads[head][:TILE], NT) + window_ref[...]
                top = fold(scores, jnp.max)
                tops.append(
                    jnp.concatenate([top, jnp.full((8, TILE), neg_large, f32)], axis=1)
                )

        def first_pass(j, tops):
            at = pl.multiple_of(first_key + j * KEY_TILE, EDGE)
            allowed = between((KEY_TILE, 2 * TILE), at, key_low, key_high)
            bias_ref[j] = jnp.where(allowed, 0.0, neg_large)
            after = []
            for p, cols in enumerate(lanes):
                keys = k_ref[pl.ds(at, KEY_TILE), cols]
                for head in range(2):
                    scores = dot(keys, queries[2 * p + head], NT) + bias_ref[j]
                    after.append(jnp.maximum(tops[2 * p + head], fold(scores, jnp.max)))
            return tuple(after)

        tops = lax.fori_loop(0, trips, first_pass, tuple(tops))
        tops = [jnp.max(top, axis=0, keepdims=True) * to_base2 for top in tops]
        state = []
        keys = [k_ref[pl.ds(window_at, WINDOW), cols] for cols in lanes]
        values_t = [v_ref[pl.ds(window_at, WINDOW), cols].T for cols in lanes]
        scores = dot(keys[0], queries[0][:TILE], NT)
        late = None
        for h in range(2 * pairs):
            if h + 1 < 2 * pairs:
                ahead = dot(keys[(h + 1) // 2], queries[h + 1][:TILE], NT)
            expo = jnp.exp2(scores * to_base2 - tops[h][:, :TILE] + window_ref[...])
            if late is not None:
                state.append(jnp.concatenate([late, jnp.zeros((HD, TILE), f32)], axis=1))
            total = fold(expo, jnp.sum)
            state.append(jnp.concatenate([total, jnp.zeros((8, TILE), f32)], axis=1))
            side = slice(h % 2 * HD, (h % 2 + 1) * HD)
            late = dot(values_t[h // 2][side], expo.astype(bf16))
            scores = ahead
        state.append(jnp.concatenate([late, jnp.zeros((HD, TILE), f32)], axis=1))

        def second_pass(j, state):
            at = pl.multiple_of(first_key + j * KEY_TILE, EDGE)
            keys = [k_ref[pl.ds(at, KEY_TILE), cols] for cols in lanes]
            values_t = [v_ref[pl.ds(at, KEY_TILE), cols].T for cols in lanes]
            after = list(state)
            scores = dot(keys[0], queries[0], NT)
            late = None
            for h in range(2 * pairs):
                ahead = dot(keys[(h + 1) // 2], queries[h + 1], NT) if h + 1 < 2 * pairs else None
                expo = jnp.exp2(scores * to_base2 - tops[h] + bias_ref[j])
                after[2 * h] = state[2 * h] + fold(expo, jnp.sum)
                if late is not None:
                    after[2 * h - 1] = state[2 * h - 1] + late
                side = slice(h % 2 * HD, (h % 2 + 1) * HD)
                late = dot(values_t[h // 2][side], expo.astype(bf16))
                scores = ahead
            after[-1] = state[-1] + late
            return tuple(after)

        state = lax.fori_loop(0, trips, second_pass, tuple(state))
        low_at = pl.ds(pl.multiple_of(t * TILE, TILE), TILE)
        high_at = pl.ds(pl.multiple_of(HALF + t * TILE, TILE), TILE)
        for p, cols in enumerate(lanes):
            halves = []
            for head in range(2):
                h = 2 * p + head
                total = jnp.sum(state[2 * h], axis=0, keepdims=True)
                halves.append(state[2 * h + 1] / total)
                lse_ref[p, t, head : head + 1, :] = tops[h] + jnp.log2(total)
            pair = jnp.concatenate(halves, axis=0).T.astype(bf16)
            out_ref[low_at, cols] = pair[:TILE]
            out_ref[high_at, cols] = pair[TILE:]
        return 0

    lax.fori_loop(0, TILES, one_tile, 0)


def attend_forward(spans, clean_bounds, noisy_bounds, query, keys, values):
    count, cols = query.shape
    pairs = cols // LANES
    vmem = pl.BlockSpec(memory_space=pltpu.VMEM)
    work = pairs * 2 * 2 * HALF * TOK_DEV
    return pl.pallas_call(
        forward_kernel,
        in_specs=[pl.BlockSpec(memory_space=pltpu.SMEM)] + [vmem] * 5,
        out_specs=[vmem] * 2,
        out_shape=[
            jax.ShapeDtypeStruct((TOK_DEV, cols), bf16),
            jax.ShapeDtypeStruct((pairs, TILES, 2, 2 * TILE), f32),
        ],
        scratch_shapes=[
            pltpu.VMEM((NOISY_BASE // KEY_TILE + 1, KEY_TILE, 2 * TILE), f32),
            pltpu.VMEM((WINDOW, TILE), f32),
        ],
        name="attend_forward",
        cost_estimate=pl.CostEstimate(
            flops=4 * work * HD, bytes_accessed=8 * count * cols, transcendentals=work
        ),
    )(spans, clean_bounds, noisy_bounds, query, keys, values)


def backward_kernel(
    giving,
    span_ref,
    clean_ref,
    noisy_ref,
    q_ref,
    k_ref,
    v_ref,
    o_ref,
    d_ref,
    lse_ref,
    cos_ref,
    sin_ref,
    *refs,
):
    if giving:
        d2_hbm, w_hbm, w2_hbm, out_ref, give_ref, low_ref, *refs = refs
        dk_ref, dv_ref, bias_ref, d2_ref, w_ref, w2_ref, load_sem = refs
        loads = [(w_hbm, w_ref), (w2_hbm, w2_ref)]
        loads += [(d2_hbm.at[c, :HALF], d2_ref.at[c]) for c in range(3)]
        loads = [
            pltpu.make_async_copy(source, target, load_sem.at[n])
            for n, (source, target) in enumerate(loads)
        ]
        for load in loads:
            load.start()
    else:
        rows_ref, out_ref, grad_ref, dk_ref, dv_ref, bias_ref = refs
    pairs = q_ref.shape[1] // LANES
    lanes = [slice(p * LANES, (p + 1) * LANES) for p in range(pairs)]
    dk_ref[...] = jnp.zeros_like(dk_ref)
    dv_ref[...] = jnp.zeros_like(dv_ref)
    out_ref[0] = jnp.zeros_like(out_ref[0])

    def one_tile(t, _):
        clean_at = pl.multiple_of(CLEAN_OWN + t * TILE, TILE)
        noisy_at = pl.multiple_of(NOISY_OWN + t * TILE, EDGE)
        window_at = pl.multiple_of(NOISY_BASE + t * TILE, EDGE)
        low_at = pl.multiple_of(t * TILE, TILE)
        high_at = pl.multiple_of(HALF + t * TILE, TILE)
        key_low, key_high = clean_ref[t, 0:1, :], clean_ref[t, 1:2, :]
        own_low, own_high = noisy_ref[t, 0:1, :], noisy_ref[t, 1:2, :]
        queries, d_outs, inners, lses = [], [], [], []
        for p, cols in enumerate(lanes):

            def both(ref, low, high):
                return jnp.concatenate(
                    [ref[pl.ds(low, TILE), cols], ref[pl.ds(high, TILE), cols]], axis=0
                )

            queries.append(split_heads(both(q_ref, noisy_at, clean_at)))
            d_rows = both(d_ref, low_at, high_at)
            o_rows = both(o_ref, low_at, high_at)
            product = (d_rows.astype(f32) * o_rows.astype(f32)).T
            d_outs.append(split_heads(d_rows))
            inners.append(
                [
                    jnp.sum(product[head * HD : (head + 1) * HD], axis=0, keepdims=True) * 0.125
                    for head in range(2)
                ]
            )
            lses.append([lse_ref[p, t, head : head + 1, :] for head in range(2)])

        def accumulate(at, rows, cols, allowed, d_query):
            bias_ref[:rows, :cols] = jnp.where(allowed, 0.0, neg_large)
            after = list(d_query)
            keys = [k_ref[pl.ds(at, rows), span] for span in lanes]
            eighth = [v_ref[pl.ds(at, rows), span] * jnp.asarray(0.125, bf16) for span in lanes]
            keys_t = [part.T for part in keys]
            stack = lambda parts: jnp.concatenate([part[:cols] for part in parts], axis=0)

            def begin(h):
                p, head = h // 2, h % 2
                return (
                    dot(keys[p], queries[p][head][:cols], NT),
                    dot(eighth[p], d_outs[p][head][:cols], NT),
                )

            def finish_pair(p, weights, d_scores):
                span = lanes[p]
                for head in range(2):
                    side = slice(head * HD, (head + 1) * HD)
                    h = 2 * p + head
                    after[h] = d_query[h] + dot(keys_t[p][side], d_scores[head])
                dv_ref[pl.ds(at, rows), span] += dot(
                    jnp.concatenate(weights, axis=1), stack(d_outs[p])
                )
                dk_ref[pl.ds(at, rows), span] += dot(
                    jnp.concatenate(d_scores, axis=1), stack(queries[p])
                )

            ready = begin(0)
            held = None
            weights, d_scores = [], []
            for h in range(2 * pairs):
                ahead = begin(h + 1) if h + 1 < 2 * pairs else None
                p, head = h // 2, h % 2
                scores = ready[0] * to_base2 - lses[p][head][:, :cols] + bias_ref[:rows, :cols]
                probs = jnp.exp2(scores)
                d_score = (probs * (ready[1] - inners[p][head][:, :cols])).astype(bf16)
                weights.append(probs.astype(bf16))
                d_scores.append(d_score)
                if held is not None:
                    finish_pair(*held)
                    held = None
                if head == 1:
                    held = (p, weights, d_scores)
                    weights, d_scores = [], []
                ready = ahead
            finish_pair(*held)
            return tuple(after)

        allowed = between((WINDOW, TILE), 0, own_low, own_high)
        zero = jnp.zeros((HD, TILE), f32)
        start = accumulate(window_at, WINDOW, TILE, allowed, (zero,) * (2 * pairs))
        start = tuple(jnp.concatenate([part, zero], axis=1) for part in start)
        first_key, trips = span_ref[t, 0], span_ref[t, 1]

        def one_step(j, d_query):
            at = pl.multiple_of(first_key + j * KEY_TILE, EDGE)
            allowed = between((KEY_TILE, 2 * TILE), at, key_low, key_high)
            return accumulate(at, KEY_TILE, 2 * TILE, allowed, d_query)

        d_query = lax.fori_loop(0, trips, one_step, start)
        for p, span in enumerate(lanes):
            pair = jnp.concatenate(d_query[2 * p : 2 * p + 2], axis=0).T
            for at, part in ((noisy_at, pair[:TILE]), (clean_at, pair[TILE:])):
                turned = turn(part, cos_ref[pl.ds(at, TILE), :], -sin_ref[pl.ds(at, TILE), :])
                out_ref[0, pl.ds(at, TILE), span] = turned.astype(bf16)
        return 0

    lax.fori_loop(0, TILES, one_tile, 0)
    step = KEY_ROWS // 9

    def finish(i, _):
        rows = pl.ds(pl.multiple_of(i * step, EDGE), step)
        for span in lanes:
            out_ref[1, rows, span] = turn(
                dk_ref[rows, span], cos_ref[rows, :], -sin_ref[rows, :]
            ).astype(bf16)
        out_ref[2, rows, :] = dv_ref[rows, :].astype(bf16)
        return 0

    lax.fori_loop(0, 9, finish, 0)

    def weight_rows(i, _):
        rows = pl.ds(pl.multiple_of(i * ROW_TILE, LANES), ROW_TILE)
        for c in range(3):
            grad_ref[c, rows, :] = dot(rows_ref[rows, :], out_ref[c]).astype(bf16)
        return 0

    if giving:
        for load in loads:
            load.wait()
        total = 0.0
        for c in range(3):
            total = total + dot(out_ref[c, :HALF, :], w_ref[c], NT) + dot(d2_ref[c], w2_ref[c], NT)
        give_ref[...] = total
        low_ref[...] = total.astype(bf16)
    else:
        lax.fori_loop(0, rows_ref.shape[0] // ROW_TILE, weight_rows, 0)


def attend_backward(
    spans,
    clean_bounds,
    noisy_bounds,
    query,
    keys,
    values,
    attended,
    d_attended,
    lse,
    cosine,
    sine,
    rest,
):
    count, cols = query.shape
    vmem = pl.BlockSpec(memory_space=pltpu.VMEM)
    hbm = pl.BlockSpec(memory_space=pl.ANY)
    shape = jax.ShapeDtypeStruct
    giving = len(rest) > 1
    if giving:
        width = rest[1].shape[1]
        second = [shape((HALF, width), f32), shape((HALF, width), bf16)]
        scratch = [
            pltpu.VMEM((3, HALF, cols), bf16),
            pltpu.VMEM(rest[1].shape, bf16),
            pltpu.VMEM(rest[2].shape, bf16),
            pltpu.SemaphoreType.DMA((5,)),
        ]
    else:
        second = [shape((3, rest[0].shape[0], cols), bf16)]
        scratch = []
    return pl.pallas_call(
        functools.partial(backward_kernel, giving),
        in_specs=[pl.BlockSpec(memory_space=pltpu.SMEM)]
        + [vmem] * 10
        + [hbm if giving else vmem] * len(rest),
        out_specs=[vmem] * (1 + len(second)),
        scratch_shapes=[
            pltpu.VMEM((count, cols), f32),
            pltpu.VMEM((count, cols), f32),
            pltpu.VMEM((max(KEY_TILE, WINDOW), 2 * TILE), f32),
        ]
        + scratch,
        out_shape=[shape((3, count, cols), bf16)] + second,
        name="attend_backward",
        cost_estimate=pl.CostEstimate(
            flops=36 * 10**9, bytes_accessed=36 * 10**6, transcendentals=6 * 10**6
        ),
    )(
        spans,
        clean_bounds,
        noisy_bounds,
        query,
        keys,
        values,
        attended,
        d_attended,
        lse,
        cosine,
        sine,
        *rest,
    )


PIECES = 16
MESH = pl.DeviceIdType.MESH


def flip(value, mask):
    result = value
    for b in range(mask.bit_length()):
        if mask >> b & 1:
            result = result + (1 << b) * (1 - 2 * ((value // (1 << b)) % 2))
    return result


class Exchange:
    def __init__(self, bits, count, rows, width, back=True):
        self.bits, self.count, self.rows, self.width = bits, count, rows, width
        self.back = back
        self.half, self.quarter, self.piece = rows // 2, rows // 4, rows // PIECES
        self.extra = list(range(4, bits))

    def slots(self):
        return 8 + 2 * (6 if self.back else 4) + (3 if self.extra else 0)

    def scratch(self):
        k, w = self.count, self.width
        cross = k if not self.back else 1
        shapes = [
            pltpu.VMEM((k, 2 - self.back, self.half, w), bf16),
            pltpu.VMEM((cross, self.half, w), bf16),
            pltpu.VMEM((cross, self.half, w), bf16),
            pltpu.VMEM((k, self.quarter, w), bf16),
            pltpu.VMEM((k, self.quarter, w), bf16),
            pltpu.VMEM((k, self.quarter, w), f32),
            pltpu.VMEM((k, 3, self.piece, w), bf16),
            pltpu.VMEM((k, 3, self.piece, w), bf16),
        ]
        lanes_of = (1, 0, 1, 3, 3, 1, 1) if self.back else (2, 1, 1, 3, 0, 0, 0)
        for lanes in [lanes for lanes in lanes_of if lanes]:
            shapes += [pltpu.SemaphoreType.DMA((k, lanes))] * 2
        if self.extra:
            n = len(self.extra)
            shapes += [pltpu.VMEM((k, 2 * n, self.piece, w), bf16)]
            shapes += [pltpu.SemaphoreType.DMA((k, n))] * 2
        return shapes

    def bind(self, place, part, refs):
        (self.a_in, self.b_out, self.b_in, self.c_out, self.c_in, self.keep) = refs[:6]
        self.d_out, self.d_in = refs[6:8]
        names = "acdefg" if self.back else "abcd"
        self.sems = {name: (refs[8 + 2 * i], refs[9 + 2 * i]) for i, name in enumerate(names)}
        if self.extra:
            at = 8 + 2 * len(names)
            self.x_buf, self.x_send, self.x_recv = refs[at : at + 3]
        self.place, self.part = place, part
        self.core, self.x, self.z = place % 2, (place // 2) % 2, (place // 4) % 4
        self.sibling = {"dp": flip(place, 1)}
        self.beside = {"dp": flip(place, 2)}
        self.across = {"mp": 1 - part}
        self.peers = [{"dp": flip(place, j << 2)} for j in range(1, 4)]
        self.partners = [self.sibling, self.beside, self.across] + self.peers
        self.partners += [{"dp": flip(place, 1 << b)} for b in self.extra]
        return self

    def greet(self):
        barrier = pltpu.get_barrier_semaphore()
        for partner in self.partners:
            pl.semaphore_signal(barrier, inc=1, device_id=partner, device_id_type=MESH)
        pl.semaphore_wait(barrier, len(self.partners))

    def copy(self, name, k, lane, source, target, device):
        out, into = self.sems[name]
        return pltpu.make_async_remote_copy(
            src_ref=source,
            dst_ref=target,
            send_sem=out.at[k, lane],
            recv_sem=into.at[k, lane],
            device_id=device,
            device_id_type=MESH,
        )

    def rows_at(self, start, size):
        return pl.ds(pl.multiple_of(start, PIECES), size)

    def copy_a(self, k, lane, grads):
        source = grads.at[k, self.rows_at((1 - self.core) * self.half, self.half)]
        return self.copy("a", k, lane, source, self.a_in.at[k, lane], self.sibling)

    def copy_b(self, k):
        return self.copy("b", k, 0, self.b_out.at[k], self.b_in.at[k], self.across)

    def copy_c(self, k):
        return self.copy("c", k, 0, self.c_out.at[k], self.c_in.at[k], self.beside)

    def copy_d(self, k, j):
        return self.copy("d", k, j, self.d_out.at[k, j], self.d_in.at[k, j], self.peers[j])

    def spot(self, change=0):
        start = self.core * self.half + self.x * self.quarter
        return self.rows_at(start + flip(self.z, change) * self.piece, self.piece)

    def copy_e(self, k, j, full):
        rows = full.at[k, self.spot()]
        return self.copy("e", k, j, rows, rows, self.peers[j])

    def copy_f(self, k, full):
        start = self.core * self.half + self.x * self.quarter
        rows = full.at[k, self.rows_at(start, self.quarter)]
        return self.copy("f", k, 0, rows, rows, self.beside)

    def copy_g(self, k, full):
        rows = full.at[k, self.rows_at(self.core * self.half, self.half)]
        return self.copy("g", k, 0, rows, rows, self.sibling)

    def start_a(self, k, lane, grads):
        self.copy_a(k, lane, grads).start()

    def stage_b(self, k, others):
        self.copy_a(k, 0, others).wait()
        mine = others[k, self.rows_at(self.core * self.half, self.half), :].astype(f32)
        self.b_out[k] = (mine + self.a_in[k, 0].astype(f32)).astype(bf16)
        self.copy_b(k).start()

    def stage_c(self, k, grads, crossed=None):
        lane = 0 if self.back else 1
        self.copy_a(k, lane, grads).wait()
        if not self.back:
            self.copy_b(k).wait()

        def total(which):
            inner = which * self.quarter
            rows = self.rows_at(inner, self.quarter)
            mine = grads[k, self.rows_at(self.core * self.half + inner, self.quarter), :]
            got = self.a_in[k, lane, rows, :].astype(f32)
            if not self.back:
                got = got + self.b_in[k, rows, :].astype(f32)
            elif crossed is not None:
                got = got + crossed(rows)
            return mine.astype(f32) + got

        self.c_out[k] = total(1 - self.x).astype(bf16)
        self.copy_c(k).start()
        self.keep[k] = total(self.x)

    def stage_d(self, k):
        self.copy_c(k).wait()
        for j in range(4):
            rows = self.rows_at(flip(self.z, j) * self.piece, self.piece)
            total = self.keep[k, rows, :] + self.c_in[k, rows, :].astype(f32)
            if j:
                self.d_out[k, j - 1] = total.astype(bf16)
                self.copy_d(k, j - 1).start()
            else:
                self.keep[k, rows, :] = total

    def gather_d(self, k):
        rows = self.rows_at(self.z * self.piece, self.piece)
        total = self.keep[k, rows, :]
        for j in range(3):
            self.copy_d(k, j).wait()
            total = total + self.d_in[k, j].astype(f32)
        for i, b in enumerate(self.extra):
            mine = self.x_buf.at[k, 2 * i]
            mine[...] = total.astype(bf16)
            swap = pltpu.make_async_remote_copy(
                src_ref=mine,
                dst_ref=self.x_buf.at[k, 2 * i + 1],
                send_sem=self.x_send.at[k, i],
                recv_sem=self.x_recv.at[k, i],
                device_id={"dp": flip(self.place, 1 << b)},
                device_id_type=MESH,
            )
            swap.start()
            swap.wait()
            total = total.astype(bf16).astype(f32) + self.x_buf[k, 2 * i + 1].astype(f32)
        return total.astype(bf16)

    def stage_e(self, k, full):
        full[k, self.spot(), :] = self.gather_d(k)
        for j in range(3):
            self.copy_e(k, j, full).start()

    def stage_f(self, k, full):
        for j in range(3):
            self.copy_e(k, j, full).wait()
        self.copy_f(k, full).start()

    def stage_g(self, k, full):
        self.copy_f(k, full).wait()
        self.copy_g(k, full).start()

    def stage_h(self, k, full):
        self.copy_g(k, full).wait()


def at_step(step, count, action):
    @pl.when(jnp.logical_and(step >= 0, step < count))
    def _():
        action(step)


def middle_kernel(exchanges, tiles, *refs):
    (
        x_ref,
        att_ref,
        att2_ref,
        wout_ref,
        wout2_ref,
        dy_ref,
        vectors_ref,
        bup_ref,
        up_mine,
        up_here,
        up_beside,
        down_mine,
        down_here,
        out_hbm,
        mid_hbm,
        datt_hbm,
        datt2_hbm,
        gout_ref,
        gout2_ref,
        gbup_ref,
        small_ref,
        pieces_ref,
        up_there,
        down_there,
        pass_up,
        pass_down,
        up_buf,
        down_buf,
        load_sem,
        n2_ref,
        total_ref,
        dn2_ref,
        act_ref,
        dpre_ref,
        n2_t,
        bup_other,
        bias_sem,
        out_ref,
        mid_ref,
        datt_ref,
        datt2_ref,
        store_sem,
        down_grad,
        up_grad,
        *rest,
    ) = refs
    place, part = lax.axis_index("dp"), lax.axis_index("mp")
    ex = exchanges[0].bind(place, part, rest)
    ex_up = exchanges[1].bind(place, part, rest[exchanges[0].slots() :])
    sides = ((ex, down_grad), (ex_up, up_grad))
    core = ex.core
    count = tiles // 2
    rows_all = x_ref.shape[0]
    blocks = rows_all // ROW_TILE
    width = x_ref.shape[1]
    lanes = width // 2

    def which(i):
        other = jnp.logical_or(i == 0, jnp.logical_and(i % 2 == 1, i < tiles - 1))
        mine = jnp.where(i == tiles - 1, count - 1, i // 2 - 1)
        return other, jnp.where(other, (i + 1) // 2, mine)

    quarter = width // 4
    strip = HIDDEN_TILE // 2
    held = 2 * core + ex.x
    kept = 2 * core + 1 - ex.x

    def load_up(i, source, h):
        target = up_buf.at[i % 2, h * quarter : (h + 1) * quarter]
        return pltpu.make_async_copy(source, target, load_sem.at[i % 2, h])

    def load_down(i, source, h):
        target = down_buf.at[i % 2, h * strip : (h + 1) * strip]
        return pltpu.make_async_copy(source, target, load_sem.at[i % 2, 4 + h])

    def hand_up(k, part_of):
        cols = pl.ds(pl.multiple_of(k * HIDDEN_TILE, HIDDEN_TILE), HIDDEN_TILE)
        side = ex.x if part_of == 0 else 1 - ex.x
        rows = pl.ds(pl.multiple_of(side * quarter, EDGE), quarter)
        return pltpu.make_async_remote_copy(
            src_ref=(up_here, up_beside)[part_of].at[:, cols],
            dst_ref=up_there.at[k, rows],
            send_sem=pass_up.at[k, 2 * part_of],
            recv_sem=pass_up.at[k, 2 * part_of + 1],
            device_id=ex.sibling,
            device_id_type=MESH,
        )

    def hand_down(b):
        return pltpu.make_async_remote_copy(
            src_ref=down_here.at[strip_rows(b)],
            dst_ref=down_there.at[b],
            send_sem=pass_down.at[b, 0],
            recv_sem=pass_down.at[b, 1],
            device_id=ex.sibling,
            device_id_type=MESH,
        )

    def strip_rows(b):
        return pl.ds(pl.multiple_of(b * strip, strip), strip)

    def start_loads(i):
        other, k = which(i)
        mine = jnp.logical_not(other)
        cols = pl.ds(pl.multiple_of(k * HIDDEN_TILE, HIDDEN_TILE), HIDDEN_TILE)

        @pl.when(other)
        def _():
            hand_up(k, 0).wait()
            hand_up(k, 1).wait()

        for h in range(4):

            @pl.when(mine)
            def _():
                load_up(i, up_mine.at[h * quarter : (h + 1) * quarter, cols], h).start()

            @pl.when(jnp.logical_and(other, held == h))
            def _():
                load_up(i, up_here.at[:, cols], h).start()

            @pl.when(jnp.logical_and(other, kept == h))
            def _():
                load_up(i, up_beside.at[:, cols], h).start()

            @pl.when(jnp.logical_and(other, core != h // 2))
            def _():
                rows = slice(h % 2 * quarter, (h % 2 + 1) * quarter)
                load_up(i, up_there.at[k, rows], h).start()

        for h in range(2):
            b = 2 * k + h
            inner = b % count

            @pl.when(mine)
            def _():
                load_down(i, down_mine.at[strip_rows(b), :], h).start()

            @pl.when(jnp.logical_and(other, core == b // count))
            def _():
                load_down(i, down_here.at[strip_rows(inner), :], h).start()

            @pl.when(jnp.logical_and(other, core != b // count))
            def _():
                hand_down(inner).wait_recv()
                load_down(i, down_there.at[inner], h).start()

    def wait_loads(i):
        for h in range(4):
            load_up(i, up_mine.at[:quarter, :HIDDEN_TILE], h).wait()
        for h in range(2):
            load_down(i, down_mine.at[:strip, :], h).wait()

    ex.greet()
    bias_swap = pltpu.make_async_remote_copy(
        src_ref=bup_ref,
        dst_ref=bup_other,
        send_sem=bias_sem.at[0],
        recv_sem=bias_sem.at[1],
        device_id=ex.across,
        device_id_type=MESH,
    )
    bias_swap.start()

    def hand(k, _):
        hand_up(k, 0).start()
        hand_up(k, 1).start()
        hand_down(k).start()
        return 0

    lax.fori_loop(0, count, hand, 0)

    def prologue(n, _):
        prologue_block(2 * n)
        prologue_block(2 * n + 1)
        return 0

    def prologue_block(r):
        rows = pl.ds(pl.multiple_of(r * ROW_TILE, ROW_TILE), ROW_TILE)
        branch = dot(att_ref[rows, :], wout_ref[...]) + dot(att2_ref[rows, :], wout2_ref[...])
        mid = x_ref[rows, :].astype(f32) + branch
        mid_ref[rows, :] = mid
        unit = normal(mid)[0]
        n2_ref[rows, :] = (unit * vectors_ref[2:3, :] + vectors_ref[3:4, :]).astype(bf16)
        total_ref[rows, :] = mid + vectors_ref[4:5, :]
        dn2_ref[rows, :] = jnp.zeros((ROW_TILE, width), f32)

    lax.fori_loop(0, blocks // 2, prologue, 0)
    start_loads(0)
    for c in range(width // LANES):
        cols = slice(c * LANES, (c + 1) * LANES)
        n2_t[cols, :] = n2_ref[:, cols].T
    n2_t[width:, :] = jnp.ones((PIECES, rows_all), bf16)
    bias_swap.wait()

    def tile(i):
        other, k = which(i)
        slot = i % 2
        wait_loads(i)

        @pl.when(i + 1 < tiles)
        def _():
            start_loads(i + 1)

        up, down = up_buf.at[slot], down_buf.at[slot]
        bias_at = jnp.where(other, k, count + k)
        bias = jnp.where(other, bup_other[k], bup_ref[k])
        linear = 0.7978845608028654
        cubic = linear * 0.044715
        for r in range(blocks):
            rows = slice(r * ROW_TILE, (r + 1) * ROW_TILE)
            pre = dot(n2_ref[rows, :], up[...]) + bias
            d_act = dot(dy_ref[rows, :], down[...], NT)
            square = pre * pre
            bend = jnp.tanh(pre * (square * cubic + linear))
            gate = 0.5 * bend + 0.5
            full_act = pre * gate
            slope = gate + (full_act - full_act * gate) * (square * (6.0 * cubic) + 2.0 * linear)
            act_ref[rows, :] = full_act.astype(bf16)
            dpre_ref[rows, :] = (d_act * slope).astype(bf16)
        total_ref[...] += dot(act_ref[...], down[...])
        dn2_ref[...] += dot(dpre_ref[...], up[...], NT)
        down_grad[k] = dot(act_ref[...].T, dy_ref[...]).astype(bf16)

        def start(lane):
            for side, grad in sides:
                side.start_a(k, lane, grad)

        by_rows = dot(n2_t[...], dpre_ref[...])
        up_grad[k] = by_rows[:width].astype(bf16)
        gbup_ref[bias_at] = by_rows[width : width + 1]
        pl.when(other)(functools.partial(start, 0))
        pl.when(jnp.logical_not(other))(functools.partial(start, 1))

    def each(k, when, action):
        @pl.when(jnp.logical_and(when, jnp.logical_and(k >= 0, k < count)))
        def _():
            for n, (side, grad) in enumerate(sides):
                action(n, side, grad, k)

    def stage_b(n, side, grad, k):
        side.stage_b(k, grad)

    def stage_c(n, side, grad, k):
        side.stage_c(k, grad)

    def stage_d(n, side, grad, k):
        side.stage_d(k)

    def arrive(n, side, grad, k):
        piece = side.gather_d(k)
        if n == 0:
            pieces_ref[k] = piece
        else:
            for c in range(width // HIDDEN_TILE):
                cols = slice(c * HIDDEN_TILE, (c + 1) * HIDDEN_TILE)
                pieces_ref[count + k, :, cols] = piece[c * PIECES : (c + 1) * PIECES]

    def steps(i):
        even = i % 2 == 0
        odd = jnp.logical_not(even)
        each((i - 5) // 2, odd, arrive)
        each((i - 4) // 2, even, stage_d)
        each((i - 3) // 2, odd, stage_c)
        each(i // 2, even, stage_b)

    def epilogue(r):
        rows = pl.ds(pl.multiple_of(r * ROW_TILE, ROW_TILE), ROW_TILE)
        out_ref[rows, :] = total_ref[rows, :].astype(bf16)
        unit, scale = normal(mid_ref[rows, :])
        d_rows = dn2_ref[rows, :]
        dy = dy_ref[rows, :].astype(f32)
        lean = d_rows * vectors_ref[2:3, :]
        d_mid = dy + scale * (
            lean
            - jnp.mean(lean, axis=-1, keepdims=True)
            - unit * jnp.mean(lean * unit, axis=-1, keepdims=True)
        )
        mid_ref[rows, :] = d_mid
        d_branch = d_mid.astype(bf16)
        n2_ref[rows, :] = d_branch
        datt_ref[rows, :] = dot(d_branch, wout_ref[...], NT).astype(bf16)
        datt2_ref[rows, :] = dot(d_branch, wout2_ref[...], NT).astype(bf16)
        add = lambda values: jnp.sum(values, axis=0, keepdims=True)
        small_ref[0:1, :] += add(d_rows * unit)
        small_ref[1:2, :] += add(d_rows)
        small_ref[2:3, :] += add(dy)

    def out_grads():
        for source, target in ((att_ref, gout_ref), (att2_ref, gout2_ref)):
            grad = dot(source[...].T, n2_ref[...]).astype(bf16)
            for a in range(wout_ref.shape[0] // LANES):
                for b in range(2):
                    rows = slice(a * LANES, (a + 1) * LANES)
                    cols = slice(b * lanes, (b + 1) * lanes)
                    spread = slice(a * lanes, (a + 1) * lanes)
                    target[b * LANES : (b + 1) * LANES, spread] = grad[rows, cols]

    def main(i, _):
        pl.when(i < tiles)(functools.partial(tile, i))

        @pl.when(jnp.logical_and(i >= tiles, i < tiles + 2))
        def _():
            first = (i - tiles) * (blocks // 2)
            for r in range(blocks // 2):
                epilogue(first + r)

        @pl.when(i == tiles + 2)
        def _():
            for store in stores:
                store.start()
            out_grads()

        steps(i)
        return 0

    small_ref[...] = jnp.zeros_like(small_ref)
    stores = [
        pltpu.make_async_copy(source, target, store_sem.at[n])
        for n, (source, target) in enumerate(
            (
                (datt2_ref, datt2_hbm),
                (out_ref, out_hbm),
                (mid_ref, mid_hbm),
                (datt_ref, datt_hbm),
            )
        )
    ]
    lax.fori_loop(0, tiles + 4, main, 0)
    for store in stores:
        store.wait()

    def handed(slot, _):
        hand_down(slot).wait_send()
        return 0

    lax.fori_loop(0, count, handed, 0)


def middle(bits, x, att, att2, wout, wout2, dy, vectors, bup, ups, downs):
    rows, width = x.shape
    hidden = ups[0].shape[1]
    count = hidden // HIDDEN_TILE
    tiles = 2 * count
    exchanges = (
        Exchange(bits, count, HIDDEN_TILE, width, False),
        Exchange(bits, count, width, HIDDEN_TILE, False),
    )
    vmem = pl.BlockSpec(memory_space=pltpu.VMEM)
    hbm = pl.BlockSpec(memory_space=pl.ANY)
    shape = jax.ShapeDtypeStruct
    depth = wout.shape[0]
    return pl.pallas_call(
        functools.partial(middle_kernel, exchanges, tiles),
        in_specs=[vmem] * 8 + [hbm] * 5,
        out_specs=[hbm] * 4 + [vmem] * 5,
        out_shape=[
            shape((rows, width), bf16),
            shape((rows, width), f32),
            shape(att.shape, bf16),
            shape(att2.shape, bf16),
            shape((2 * LANES, depth // LANES * width // 2), bf16),
            shape((2 * LANES, depth // LANES * width // 2), bf16),
            shape((tiles, 1, HIDDEN_TILE), f32),
            shape((8, width), f32),
            shape((2 * count, PIECES, width), bf16),
        ],
        scratch_shapes=[
            pltpu.VMEM((count, width // 2, HIDDEN_TILE), bf16),
            pltpu.VMEM((count, HIDDEN_TILE // 2, width), bf16),
            pltpu.SemaphoreType.DMA((count, 4)),
            pltpu.SemaphoreType.DMA((count, 2)),
            pltpu.VMEM((2, width, HIDDEN_TILE), bf16),
            pltpu.VMEM((2, HIDDEN_TILE, width), bf16),
            pltpu.SemaphoreType.DMA((2, 6)),
            pltpu.VMEM((rows, width), bf16),
            pltpu.VMEM((rows, width), f32),
            pltpu.VMEM((rows, width), f32),
            pltpu.VMEM((rows, HIDDEN_TILE), bf16),
            pltpu.VMEM((rows, HIDDEN_TILE), bf16),
            pltpu.VMEM((width + PIECES, rows), bf16),
            pltpu.VMEM(bup.shape, f32),
            pltpu.SemaphoreType.DMA((2,)),
            pltpu.VMEM((rows, width), bf16),
            pltpu.VMEM((rows, width), f32),
            pltpu.VMEM(att.shape, bf16),
            pltpu.VMEM(att2.shape, bf16),
            pltpu.SemaphoreType.DMA((4,)),
            pltpu.VMEM((count, HIDDEN_TILE, width), bf16),
            pltpu.VMEM((count, width, HIDDEN_TILE), bf16),
        ]
        + exchanges[0].scratch()
        + exchanges[1].scratch(),
        compiler_params=pltpu.CompilerParams(
            collective_id=0, has_side_effects=True, vmem_limit_bytes=67043328
        ),
        name="middle",
        cost_estimate=pl.CostEstimate(
            flops=60 * 10**9, bytes_accessed=40 * 10**6, transcendentals=4 * 10**6
        ),
    )(x, att, att2, wout, wout2, dy, vectors, bup, *ups, *downs)


def leave_kernel(exchange, *refs):
    (
        rows_hbm,
        mine_out_ref,
        crossed_ref,
        crossed_out_ref,
        d_hbm,
        d2_hbm,
        w_hbm,
        w2_hbm,
        tokens_ref,
        context_ref,
        given_ref,
        small_ref,
        small2_ref,
        gqkv_ref,
        gout_ref,
        back_hbm,
        sums_ref,
        full_ref,
        out_buf,
        rows_t_ref,
        d_ref,
        d2_ref,
        w_ref,
        w2_ref,
        load_sem,
        rows_ref,
        give_ref,
        take_ref,
        swap_sem,
        back_sem,
        norm_ref,
        near_ref,
        far_ref,
        near_sem,
        far_sem,
        *rest,
    ) = refs
    place, part = lax.axis_index("dp"), lax.axis_index("mp")
    ex = exchange.bind(place, part, rest)
    count, bits = ex.count, ex.bits
    loads = [
        pltpu.make_async_copy(source, target, load_sem.at[n])
        for n, (source, target) in enumerate(
            (
                (d_hbm, d_ref),
                (rows_hbm, rows_t_ref),
                (w_hbm, w_ref),
                (w2_hbm, w2_ref),
                (d2_hbm, d2_ref),
            )
        )
    ]
    for load in loads:
        load.start()
    near_id = part * 4 + place % 4
    near = [
        {"dp": flip(place, j % 4), "mp": part if j < 4 else 1 - part} for j in range(1, 8)
    ]
    ex.partners += [near[j - 1] for j in (3, 5, 6, 7)]
    ex.greet()

    lanes = d_ref.shape[2]
    split = mine_out_ref.shape[1] // lanes
    for r in range(split):
        cols = slice(r * lanes, (r + 1) * lanes)
        total = mine_out_ref[:, cols].astype(f32) + crossed_out_ref[:, cols].astype(f32)
        out_buf[r] = total.astype(bf16)
        ex.start_a(r, 0, out_buf)
    step = HALF + 2 * EDGE

    def back_rows(n):
        start = CLEAN_OWN + n * (KEY_ROWS - step - CLEAN_OWN)
        rows = pl.ds(pl.multiple_of(start, EDGE), step)
        total = 0.0
        for grads, weights in ((d_ref, w_ref), (d2_ref, w2_ref)):
            for c in range(3):
                total = total + dot(grads[c, rows, :], weights[c], NT)
        rows_ref[rows, :] = total

    def grad_chunk(c):
        for r in range(split):
            rows = slice(r * ROW_TILE, (r + 1) * ROW_TILE)
            k = (c + 1) * split + r
            out_buf[k] = dot(rows_t_ref[rows, :], d_ref[c]).astype(bf16)
            ex.start_a(k, 0, out_buf)

    def stage_c(k):
        @pl.when(k >= split)
        def _():
            ex.stage_c(k, out_buf, lambda rows: crossed_ref[k - split, rows, :].astype(f32))

        @pl.when(k < split)
        def _():
            ex.stage_c(k, out_buf)

    def arrive(k):
        ex.stage_h(k, full_ref)

        @pl.when(k < split)
        def _():
            rows = pl.ds(pl.multiple_of(k * LANES, LANES), LANES)
            for b in range(2):
                piece = full_ref[k, b * LANES : (b + 1) * LANES, :]
                gout_ref[rows, b * lanes : (b + 1) * lanes] = piece

        @pl.when(k >= split)
        def _():
            n = k - split
            rows = pl.ds(pl.multiple_of(n % split * ROW_TILE, ROW_TILE), ROW_TILE)
            gqkv_ref[n // split, rows, :] = full_ref[k]

    def group(g, action):
        @pl.when(jnp.logical_and(g >= 0, g < count // split))
        def _():
            lax.fori_loop(g * split, (g + 1) * split, lambda k, _: (action(k), 0)[1], 0)

    def steps(i):
        group(i - 5, arrive)
        group(i - 4, lambda k: ex.stage_g(k, full_ref))
        group(i - 3, lambda k: ex.stage_f(k, full_ref))
        group(i - 2, lambda k: ex.stage_e(k, full_ref))
        group(i - 1, lambda k: ex.stage_d(k))
        group(i, stage_c)

    width = tokens_ref.shape[1]

    def swap():
        return pltpu.make_async_remote_copy(
            src_ref=give_ref,
            dst_ref=take_ref,
            send_sem=swap_sem.at[0],
            recv_sem=swap_sem.at[1],
            device_id=ex.across,
            device_id_type=MESH,
        )

    def sums_of(d_rows, units):
        add = lambda values: jnp.sum(values, axis=0, keepdims=True)
        norm_ref[0:1, :] += add(d_rows * units)
        norm_ref[1:2, :] += add(d_rows)

    parts = tokens_ref.shape[0] // TILE
    lead = small_ref.shape[0] - 2
    bias = lead - 3
    norm_ref[...] = jnp.zeros_like(norm_ref)
    for load in loads[:2]:
        load.wait()

    def own_at(b):
        start = jnp.where(b < TILES, NOISY_OWN + b * TILE, CLEAN_OWN + (b - TILES) * TILE)
        return pl.ds(pl.multiple_of(start, EDGE), TILE)

    def tokens_at(b):
        return pl.ds(pl.multiple_of(b * TILE, TILE), TILE)

    def ready():
        for load in loads[2:5]:
            load.wait()

    def give_edges():
        side = rows_ref[NOISY_BASE:NOISY_OWN, :] + rows_ref[NOISY_OWN + HALF :, :]
        after = rows_ref[2 * HALF : NOISY_BASE, :]
        give_ref[:EDGE, :] = after.astype(bf16)
        give_ref[EDGE:, :] = side.astype(bf16)
        swap().start()
        sums_of(after, normal(context_ref[:EDGE, :].astype(f32))[0])
        sums_of(side, normal(context_ref[HALF:, :].astype(f32))[0])

    def tell_near():
        def context_sums(b, _):
            rows = tokens_at(b)
            sums_of(given_ref[rows, :], normal(context_ref[rows, :].astype(f32))[0])
            return 0

        lax.fori_loop(0, HALF // TILE, context_sums, 0)

        def own_sums(b, _):
            sums_of(rows_ref[own_at(b), :], normal(tokens_ref[tokens_at(b), :].astype(f32))[0])
            return 0

        lax.fori_loop(0, parts, own_sums, 0)
        blank = jnp.zeros((16 - lead - 2 - bias, width), f32)
        near_ref[near_id] = jnp.concatenate(
            [small_ref[:lead, :], norm_ref[:2, :], small2_ref[:bias, :], blank], axis=0
        ).astype(bf16)
        for j in range(1, 8):
            near_copy(j).start()

    def near_copy(j):
        return pltpu.make_async_remote_copy(
            src_ref=near_ref.at[near_id],
            dst_ref=near_ref.at[near_id],
            send_sem=near_sem.at[j, 0],
            recv_sem=near_sem.at[j, 1],
            device_id=near[j - 1],
            device_id_type=MESH,
        )

    def near_got(j):
        came = (part + j // 4) % 2 * 4 + flip(place % 4, j % 4)
        return pltpu.make_async_remote_copy(
            src_ref=near_ref.at[came],
            dst_ref=near_ref.at[came],
            send_sem=near_sem.at[j, 0],
            recv_sem=near_sem.at[j, 1],
            device_id=near[j - 1],
            device_id_type=MESH,
        )

    def far_copy(j, at):
        return pltpu.make_async_remote_copy(
            src_ref=far_ref.at[at],
            dst_ref=far_ref.at[at],
            send_sem=far_sem.at[j, 0],
            recv_sem=far_sem.at[j, 1],
            device_id=ex.peers[j - 1],
            device_id_type=MESH,
        )

    def tell_far():
        for j in range(1, 8):
            near_copy(j).wait_send()
            near_got(j).wait_recv()
        near_sum = lambda at: sum(near_ref[at + j].astype(f32) for j in range(1, 4)) + near_ref[
            at
        ].astype(f32)
        plane, other = near_sum(part * 4), near_sum((1 - part) * 4)
        total = near_sum(0) + near_sum(4)
        mixed = plane[:bias] + other[lead + 2 : lead + 2 + bias]
        far_ref[ex.z] = jnp.concatenate([mixed, total[bias:]], axis=0).astype(bf16)
        for j in range(1, 4):
            far_copy(j, ex.z).start()

    halves = [
        pltpu.make_async_copy(
            rows_ref.at[start : start + HALF],
            back_hbm.at[n * HALF : (n + 1) * HALF],
            back_sem.at[n],
        )
        for n, start in enumerate((NOISY_OWN, CLEAN_OWN))
    ]

    def take_back():
        swap().wait()
        begin = slice(CLEAN_OWN, CLEAN_OWN + EDGE)
        rows_ref[begin, :] += take_ref[:EDGE, :].astype(f32)
        edge = pl.ds(pl.multiple_of(NOISY_OWN + (1 - part) * (HALF - EDGE), EDGE), EDGE)
        rows_ref[edge, :] += take_ref[EDGE:, :].astype(f32)
        for half in halves:
            half.start()

    def end_far():
        for j in range(1, 4):
            far_copy(j, ex.z).wait_send()
            far_copy(j, flip(ex.z, j)).wait_recv()
        total = far_ref[0].astype(f32)
        for j in range(1, 4):
            total = total + far_ref[j].astype(f32)
        for i, b in enumerate(ex.extra):
            total = total.astype(bf16).astype(f32)
            far_ref[4 + 2 * i] = total.astype(bf16)
            trade = pltpu.make_async_remote_copy(
                src_ref=far_ref.at[4 + 2 * i],
                dst_ref=far_ref.at[5 + 2 * i],
                send_sem=far_sem.at[4 + i, 0],
                recv_sem=far_sem.at[4 + i, 1],
                device_id={"dp": flip(place, 1 << b)},
                device_id_type=MESH,
            )
            trade.start()
            trade.wait()
            total = total + far_ref[5 + 2 * i].astype(f32)
        sums_ref[...] = total

    groups = count // split - 1
    actions = {
        groups + 1: give_edges,
        groups + 2: tell_near,
        groups + 3: take_back,
        groups + 4: tell_far,
        groups + 6: end_far,
    }

    def phase(p, _):
        @pl.when(p < groups)
        def _():
            grad_chunk(p)

        pl.when(p == groups)(ready)

        @pl.when(jnp.logical_and(p >= groups, p < groups + 2))
        def _():
            back_rows(p - groups)

        for n, action in actions.items():
            pl.when(p == n)(action)
        steps(p)
        return 0

    lax.fori_loop(0, groups + 7, phase, 0)
    for half in halves:
        half.wait()


def leave(bits, rows_t, mine, crossed, d_fields, weights, tokens, context, given, small, small2):
    rows, cols = ROW_TILE, d_fields[0].shape[2]
    total = mine.shape[1] // cols + crossed[0].shape[0]
    exchange = Exchange(bits, total, rows, cols)
    count, width = tokens.shape
    vmem = pl.BlockSpec(memory_space=pltpu.VMEM)
    hbm = pl.BlockSpec(memory_space=pl.ANY)
    shape = jax.ShapeDtypeStruct
    return pl.pallas_call(
        functools.partial(leave_kernel, exchange),
        in_specs=[hbm] + [vmem] * 3 + [hbm] * 4 + [vmem] * 5,
        out_specs=[vmem] * 2 + [hbm, vmem],
        out_shape=[
            shape(weights[0].shape, bf16),
            shape((d_fields[0].shape[2], width), bf16),
            shape((count, width), f32),
            shape((16, width), f32),
        ],
        scratch_shapes=[
            pltpu.VMEM((total, rows, cols), bf16),
            pltpu.VMEM((total, rows, cols), bf16),
            pltpu.VMEM(rows_t.shape, bf16),
            pltpu.VMEM(d_fields[0].shape, bf16),
            pltpu.VMEM(d_fields[1].shape, bf16),
            pltpu.VMEM(weights[0].shape, bf16),
            pltpu.VMEM(weights[1].shape, bf16),
            pltpu.SemaphoreType.DMA((5,)),
            pltpu.VMEM((KEY_ROWS, width), f32),
            pltpu.VMEM((2 * EDGE, width), bf16),
            pltpu.VMEM((2 * EDGE, width), bf16),
            pltpu.SemaphoreType.DMA((2,)),
            pltpu.SemaphoreType.DMA((2,)),
            pltpu.VMEM((8, width), f32),
            pltpu.VMEM((8, 16, width), bf16),
            pltpu.VMEM((4 + 2 * len(exchange.extra), 16, width), bf16),
            pltpu.SemaphoreType.DMA((8, 2)),
            pltpu.SemaphoreType.DMA((4 + len(exchange.extra), 2)),
        ]
        + exchange.scratch(),
        compiler_params=pltpu.CompilerParams(
            collective_id=1, has_side_effects=True, vmem_limit_bytes=67043328
        ),
        name="leave",
        cost_estimate=pl.CostEstimate(
            flops=40 * 10**9, bytes_accessed=40 * 10**6, transcendentals=0
        ),
    )(
        rows_t, mine, *crossed, *d_fields, *weights, tokens, context, given, small, small2
    )


def finish_kernel(rows_ref, got_ref, tokens_ref, vectors_ref, dmid_ref, out_ref):
    clean = pl.program_id(0) >= pl.num_programs(0) // 2
    got = jnp.where(clean, got_ref[...].astype(f32), 0.0)
    unit, scale = normal(tokens_ref[...].astype(f32))
    lean = (rows_ref[...] + got) * vectors_ref[0:1, :]
    out_ref[...] = dmid_ref[...] + scale * (
        lean
        - jnp.mean(lean, axis=-1, keepdims=True)
        - unit * jnp.mean(lean * unit, axis=-1, keepdims=True)
    )


def finish(rows, got, tokens, vectors, d_mid):
    count, width = rows.shape
    spec = pl.BlockSpec((ROW_TILE, width), lambda b: (b, 0))
    half = count // ROW_TILE // 2
    return pl.pallas_call(
        finish_kernel,
        grid=(count // ROW_TILE,),
        in_specs=[
            spec,
            pl.BlockSpec((ROW_TILE, width), lambda b: (jnp.maximum(b - half, 0), 0)),
            spec,
            pl.BlockSpec(vectors.shape, lambda b: (0, 0)),
            spec,
        ],
        out_specs=spec,
        out_shape=jax.ShapeDtypeStruct((count, width), f32),
        name="finish",
        cost_estimate=pl.CostEstimate(
            flops=10**7, bytes_accessed=12 * 10**6, transcendentals=0
        ),
    )(rows, got, tokens, vectors, d_mid)


def assemble_kernel(
    core_ref, down_mine, up_mine, down_got, up_got, qkv_low, out_low, down_ref, up_ref, qkv_ref, out_ref
):
    qkv_ref[...] = qkv_low[...].astype(f32)
    out_ref[...] = out_low[...].astype(f32)
    core = core_ref[0]
    block = down_mine.shape[1]
    lanes = up_ref.shape[1]
    parts = down_mine.shape[2] // lanes
    deep = block * parts
    for side, down, up in ((core, down_mine, up_mine), (1 - core, down_got, up_got)):
        rows = pl.ds(pl.multiple_of(side * block, block), block)
        down_ref[rows, :] = down[0].astype(f32)
        for n in range(block // PIECES):
            for c in range(parts):
                at = side * deep + (n * parts + c) * PIECES
                rows = pl.ds(pl.multiple_of(at, PIECES), PIECES)
                piece = up[0, n * PIECES : (n + 1) * PIECES, c * lanes : (c + 1) * lanes]
                up_ref[rows, :] = piece.astype(f32)


def assemble(core, gathered, moved, qkv, out):
    tiles, half, width = gathered.shape
    count = tiles // 2
    down_spec = pl.BlockSpec((1, half, width), lambda k, c: (k, 0, 0))
    up_spec = pl.BlockSpec((1, half, width), lambda k, c: (count + k, 0, 0))
    hidden = count * 2 * half
    qkv_spec = pl.BlockSpec((qkv.shape[0] // count, qkv.shape[1]), lambda k, c: (k, 0))
    out_spec = pl.BlockSpec((out.shape[0] // count, out.shape[1]), lambda k, c: (k, 0))
    return pl.pallas_call(
        assemble_kernel,
        grid_spec=pltpu.PrefetchScalarGridSpec(
            num_scalar_prefetch=1,
            grid=(count,),
            in_specs=[down_spec, up_spec, down_spec, up_spec, qkv_spec, out_spec],
            out_specs=[
                pl.BlockSpec((2 * half, width), lambda k, c: (k, 0)),
                pl.BlockSpec((width, 2 * half), lambda k, c: (0, k)),
                qkv_spec,
                out_spec,
            ],
        ),
        out_shape=[
            jax.ShapeDtypeStruct((hidden, width), f32),
            jax.ShapeDtypeStruct((width, hidden), f32),
            jax.ShapeDtypeStruct(qkv.shape, f32),
            jax.ShapeDtypeStruct(out.shape, f32),
        ],
        name="assemble",
        cost_estimate=pl.CostEstimate(
            flops=10**6, bytes_accessed=14 * 10**6, transcendentals=0
        ),
    )(core, gathered, gathered, moved, moved, qkv, out)


def key_layout(seq_lengths, block_len, part):
    index = jnp.arange(KEY_ROWS, dtype=jnp.int32)
    own = part * HALF
    token = jnp.where(
        index < NOISY_BASE, index + (own - HALF), index - NOISY_BASE + (own - EDGE)
    )
    ends = jnp.cumsum(seq_lengths)
    passed = token[:, None] >= ends[None, :]
    starts = jnp.sum(jnp.where(passed, seq_lengths[None, :], 0), axis=1)
    lengths_here = jnp.where(passed, 0, ends[None, :])
    stops = jnp.min(jnp.where(passed, TOK_DEV, lengths_here), axis=1)
    positions = token - starts
    block_start = starts + positions // block_len * block_len
    block_stop = jnp.minimum(block_start + block_len, stops)
    mine = slice(CLEAN_OWN, CLEAN_OWN + HALF)
    low, start, stop = starts[mine], block_start[mine], block_stop[mine]
    to_clean = own - HALF
    tiles = lambda column: column.reshape(TILES, 1, TILE)
    clean_bounds = jnp.concatenate(
        [
            jnp.concatenate([tiles(low - to_clean), tiles(low - to_clean)], axis=2),
            jnp.concatenate([tiles(start - to_clean), tiles(stop - to_clean)], axis=2),
        ],
        axis=1,
    )
    to_window = own - EDGE + TILE * jnp.arange(TILES, dtype=jnp.int32)[:, None, None]
    noisy_bounds = jnp.concatenate(
        [tiles(start) - to_window, tiles(stop) - to_window], axis=1
    )
    first = jnp.min(clean_bounds[:, 0], axis=1) // EDGE * EDGE
    last = jnp.max(clean_bounds[:, 1], axis=1)
    trips = (last - first + KEY_TILE - 1) // KEY_TILE
    spans = jnp.stack([first, trips], axis=1)
    lane = jnp.arange(LANES, dtype=jnp.int32)
    frequency = jnp.exp(
        (lane % (HD // 2)).astype(f32) * (-math.log(10000.0) / (HD // 2))
    )
    angles = positions.astype(f32)[:, None] * frequency[None, :]
    sign = jnp.where(lane % HD < HD // 2, -1.0, 1.0)
    return spans, clean_bounds, noisy_bounds, jnp.cos(angles), jnp.sin(angles) * sign


def in_order(bit, mine, theirs, axis=0):
    order = bit == 0
    return jnp.concatenate(
        [jnp.where(order, mine, theirs), jnp.where(order, theirs, mine)], axis=axis
    )


def tie(first, second):
    return lax.optimization_barrier((first, second))


def local(
    dp_size,
    tokens,
    lengths,
    block_size,
    cotangent,
    ln1_gain,
    ln1_bias,
    w_qkv,
    w_out,
    ln2_gain,
    ln2_bias,
    w_up,
    b_up,
    w_down,
    b_down,
):
    width = tokens.shape[2]
    part = lax.axis_index("mp")
    place = lax.axis_index("dp")
    bits = dp_size.bit_length() - 1
    core = place & 1

    def across(array):
        return lax.ppermute(array, "mp", [(0, 1), (1, 0)])

    def sibling(array):
        return lax.ppermute(array, "dp", [(i, i ^ 1) for i in range(dp_size)])

    def beside(array):
        return lax.ppermute(array, "dp", [(i, i ^ 2) for i in range(dp_size)])

    edge = jnp.where(part == 0, tokens[0, HALF - EDGE :], tokens[0, :EDGE])
    context = across(jnp.concatenate([tokens[1], edge], axis=0))
    qkv_mine = w_qkv.transpose(1, 0, 2)
    side = (place >> 1) & 1

    def quarter_of(array, axis=0):
        size = array.shape[axis] // 4
        return lax.dynamic_slice_in_dim(array, (2 * core + side) * size, size, axis)

    def half_of(array):
        size = array.shape[0] // 2
        return lax.dynamic_slice_in_dim(array, core * size, size, 0)

    quarters = [quarter_of(qkv_mine, 1), quarter_of(w_up), half_of(w_down), half_of(w_out)]
    layout = key_layout(lengths[0], block_size[0], part)
    vectors = jnp.stack([ln1_gain, ln1_bias, ln2_gain, ln2_bias, b_down])
    context, (quarters, layout, vectors) = tie(context, (quarters, layout, vectors))
    qkv_here, up_here, down_here, out_here = [across(piece) for piece in quarters]

    spans, clean_bounds, noisy_bounds, cosine, sine = layout
    normed1, normed1_t, *fields = enter(tokens, context, vectors, qkv_mine, cosine, sine)
    qkv_here, fields = tie(qkv_here, fields)
    qkv_beside = beside(qkv_here)
    mine = [*fields, *attend_forward(spans, clean_bounds, noisy_bounds, *fields)]
    (qkv_here, qkv_beside, up_here, out_here), _ = tie(
        (qkv_here, qkv_beside, up_here, out_here), mine[3]
    )
    out_there = sibling(out_here)
    qkv_half = in_order(side, qkv_here, qkv_beside, axis=1)
    qkv_other = in_order(core, qkv_half, sibling(qkv_half), axis=1)
    up_beside = beside(up_here)
    fields = project(normed1, qkv_other, cosine, sine)
    (out_here, out_there), fields = tie((out_here, out_there), fields)
    out_other = in_order(core, out_here, out_there)
    out_other, fields = tie(out_other, fields)
    other = [*fields, *attend_forward(spans, clean_bounds, noisy_bounds, *fields)]
    (up_here, up_beside, down_here), _ = tie((up_here, up_beside, down_here), other[3])
    bias_all = b_up.astype(f32).reshape(-1, 1, HIDDEN_TILE)

    x_rows = tokens.reshape(TOK_DEV, width)
    out, d_mid, d_att, d_att2, grad_out, grad_out2, grad_bias, norms, pieces = middle(
        bits,
        x_rows,
        mine[3],
        other[3],
        w_out,
        out_other,
        cotangent.reshape(TOK_DEV, width),
        vectors,
        bias_all,
        (w_up, up_here, up_beside),
        (w_down, down_here),
    )
    hidden = b_up.shape[0]

    crossed_out = across(grad_out2)
    spread = [(b, min(2, min(bits, 4) - b)) for b in range(2, min(bits, 4), 2)]
    gathered = pieces
    ((first_bit, n),) = spread
    moved = [
        lax.ppermute(gathered, "dp", [(i, i ^ (k << first_bit)) for i in range(dp_size)])
        for k in range(1, 1 << n)
    ]

    def backward(saved, d_attended, spans, *rest):
        query, keys, values, attended, lse = saved
        return attend_backward(
            spans,
            clean_bounds,
            noisy_bounds,
            query,
            keys,
            values,
            attended,
            d_attended,
            lse,
            cosine,
            sine,
            rest,
        )

    d_fields2, grad2 = backward(other, d_att2, spans, normed1_t)
    grad2 = grad2.reshape(-1, ROW_TILE, grad2.shape[2])
    low_bit, high_bit = (place >> 2) & 1, (place >> 3) & 1
    moved, _ = tie(moved, grad2)
    gathered = in_order(
        high_bit,
        in_order(low_bit, gathered, moved[0], 1),
        in_order(low_bit, moved[1], moved[2], 1),
        1,
    )
    half = ROW_TILE // 2
    part_of = lambda array, which: lax.dynamic_slice_in_dim(array, which * half, half, 1)
    got = sibling(part_of(grad2, 1 - core))
    crossing = (part_of(grad2, core).astype(f32) + got.astype(f32)).astype(bf16)
    (crossing, gathered), spans = tie((crossing, gathered), spans)
    crossed = across(crossing)
    moved = beside(gathered)
    d_fields1, given, give = backward(mine, d_att, spans, d_fields2, qkv_mine, qkv_other)
    took = across(give)
    moved, d_fields1 = tie(moved, d_fields1)
    gathered = in_order(side, gathered, moved, 1)
    gathered, d_fields1 = tie(gathered, d_fields1)
    moved = sibling(gathered)
    lead = hidden // width
    bias2, bias1 = grad_bias.reshape(2, lead, width)
    shared = jnp.concatenate([norms[:3], jnp.zeros((2, width), f32)], axis=0)
    grad_qkv, grad_out, d_rows, sums = leave(
        bits,
        normed1_t,
        grad_out,
        (crossed, crossed_out),
        (d_fields1, d_fields2),
        (qkv_mine, qkv_other),
        x_rows,
        context,
        given,
        jnp.concatenate([bias1, shared], axis=0),
        jnp.concatenate([bias2, shared], axis=0),
    )
    (moved, took), grad_qkv = tie((moved, took), grad_qkv)
    grad_tokens = finish(d_rows, took, x_rows, vectors, d_mid)
    grad_down, grad_up, grad_qkv, grad_out = assemble(
        core.reshape(1), gathered, moved, grad_qkv.reshape(-1, grad_qkv.shape[2]), grad_out
    )
    return (
        out.reshape(tokens.shape),
        grad_tokens.reshape(tokens.shape),
        sums[lead + 3],
        sums[lead + 4],
        grad_qkv.reshape(qkv_mine.shape).transpose(1, 0, 2),
        grad_out,
        sums[lead],
        sums[lead + 1],
        grad_up,
        sums[:lead].reshape(hidden),
        grad_down,
        sums[lead + 2],
    )


def solution(mesh):
    in_specs = (
        P(None, ("dp", "mp"), None),
        P("dp", None),
        P(),
        P(None, ("dp", "mp"), None),
        P(),
        P(),
        P(None, None, "mp"),
        P("mp", None),
        P(),
        P(),
        P(None, "mp"),
        P("mp"),
        P("mp", None),
        P(),
    )
    out_specs = (
        P(None, ("dp", "mp"), None),
        P(None, ("dp", "mp"), None),
        P(),
        P(),
        P(None, None, "mp"),
        P("mp", None),
        P(),
        P(),
        P(None, "mp"),
        P("mp"),
        P("mp", None),
        P(),
    )
    return jax.shard_map(
        functools.partial(local, mesh.shape["dp"]),
        mesh=mesh,
        in_specs=in_specs,
        out_specs=out_specs,
        check_vma=False,
    )
```

```python
import functools
import math

import jax
import jax.numpy as jnp
from jax import lax
from jax.experimental import pallas as pl
from jax.experimental.pallas import tpu as pltpu
from jax.sharding import PartitionSpec as P

HD = 64
TOK_DEV = 1024
HALF = TOK_DEV // 2
EDGE = 16
CLEAN_OWN = HALF
NOISY_BASE = 2 * HALF + EDGE
NOISY_OWN = NOISY_BASE + EDGE
KEY_ROWS = NOISY_OWN + HALF + EDGE
TILE = 128
TILES = HALF // TILE
WINDOW = TILE + 2 * EDGE
KEY_TILE = 192
LANES = 128
HIDDEN_TILE = 256
ROW_TILE = 256

epsilon = 1e-05
neg_large = -1e30
to_base2 = 0.125 * math.log2(math.e)
f32 = jnp.float32
bf16 = jnp.bfloat16

NN = (((1,), (0,)), ((), ()))
NT = (((1,), (1,)), ((), ()))


def dot(left, right, dims=NN):
    return lax.dot_general(left, right, dims, preferred_element_type=f32)


def low_lanes(shape):
    return lax.broadcasted_iota(jnp.int32, shape, 1) < HD


def turn(values, cosine, sine):
    lane = lax.broadcasted_iota(jnp.int32, values.shape, 1)
    first_half = (lane & (HD - 1)) < HD // 2
    swapped = jnp.where(
        first_half,
        pltpu.roll(values, LANES - HD // 2, 1),
        pltpu.roll(values, HD // 2, 1),
    )
    return values * cosine + swapped * sine


def project_rows(rows, w_ref, cosine, sine, q_ref, k_ref, v_ref, at):
    for part, out_ref in ((0, q_ref), (1, k_ref)):
        field = dot(rows, w_ref[part])
        for pair in range(field.shape[1] // LANES):
            cols = slice(pair * LANES, (pair + 1) * LANES)
            out_ref[at, cols] = turn(field[:, cols], cosine, sine).astype(bf16)
    v_ref[at, :] = dot(rows, w_ref[2]).astype(bf16)


def project_kernel(rows_ref, w_ref, cos_ref, sin_ref, q_ref, k_ref, v_ref):
    at = slice(0, rows_ref.shape[0])
    project_rows(rows_ref[...], w_ref, cos_ref[...], sin_ref[...], q_ref, k_ref, v_ref, at)


def project(rows, weights, cosine, sine):
    count, width = rows.shape
    cols = weights.shape[2]
    step = count // 3
    row_spec = pl.BlockSpec((step, width), lambda i: (i, 0))
    table_spec = pl.BlockSpec((step, LANES), lambda i: (i, 0))
    out_spec = pl.BlockSpec((step, cols), lambda i: (i, 0))
    shape = jax.ShapeDtypeStruct((count, cols), bf16)
    return pl.pallas_call(
        project_kernel,
        grid=(3,),
        in_specs=[
            row_spec,
            pl.BlockSpec(weights.shape, lambda i: (0, 0, 0)),
            table_spec,
            table_spec,
        ],
        out_specs=[out_spec] * 3,
        out_shape=[shape] * 3,
        name="project",
        cost_estimate=pl.CostEstimate(
            flops=2 * count * width * 3 * cols,
            bytes_accessed=2 * (count * (width + 3 * cols) + 3 * width * cols),
            transcendentals=0,
        ),
    )(rows, weights, cosine, sine)


def normal(values):
    average = jnp.mean(values, axis=-1, keepdims=True)
    centred = values - average
    variance = jnp.mean(centred * centred, axis=-1, keepdims=True)
    scale = lax.rsqrt(variance + epsilon)
    return centred * scale, scale


def enter_kernel(
    tokens_ref,
    context_ref,
    vectors_ref,
    w_ref,
    cos_ref,
    sin_ref,
    rows_ref,
    rows_t_ref,
    q_ref,
    k_ref,
    v_ref,
):
    def norm(values):
        unit = normal(values.astype(f32))[0]
        return (unit * vectors_ref[0:1, :] + vectors_ref[1:2, :]).astype(bf16)

    def blocks(i, _):
        source = pl.ds(pl.multiple_of(i * TILE, TILE), TILE)
        rows_ref[source, :] = norm(context_ref[source, :])
        at = pl.ds(pl.multiple_of(CLEAN_OWN + i * TILE, TILE), TILE)
        rows_ref[at, :] = norm(tokens_ref[1, source, :])
        at = pl.ds(pl.multiple_of(NOISY_OWN + i * TILE, EDGE), TILE)
        rows_ref[at, :] = norm(tokens_ref[0, source, :])
        return 0

    lax.fori_loop(0, TILES, blocks, 0)
    rows_ref[2 * HALF : NOISY_BASE, :] = rows_ref[:EDGE, :]
    edge = norm(context_ref[HALF:, :])
    rows_ref[NOISY_BASE:NOISY_OWN, :] = edge
    rows_ref[NOISY_OWN + HALF :, :] = edge
    step = KEY_ROWS // 3

    def fields(i, _):
        at = pl.ds(pl.multiple_of(i * step, EDGE), step)
        project_rows(
            rows_ref[at, :], w_ref, cos_ref[at, :], sin_ref[at, :], q_ref, k_ref, v_ref, at
        )
        return 0

    lax.fori_loop(0, 3, fields, 0)
    for c in range(rows_t_ref.shape[0] // LANES):
        cols = slice(c * LANES, (c + 1) * LANES)
        rows_t_ref[cols, :] = rows_ref[:, cols].T


def enter(tokens, context, vectors, weights, cosine, sine):
    width, cols = weights.shape[1:]
    vmem = pl.BlockSpec(memory_space=pltpu.VMEM)
    shape = jax.ShapeDtypeStruct
    field = shape((KEY_ROWS, cols), bf16)
    return pl.pallas_call(
        enter_kernel,
        in_specs=[vmem] * 6,
        out_specs=[vmem] * 5,
        out_shape=[shape((KEY_ROWS, width), bf16), shape((width, KEY_ROWS), bf16)] + [field] * 3,
        name="enter",
        cost_estimate=pl.CostEstimate(
            flops=10**10, bytes_accessed=16 * 10**6, transcendentals=0
        ),
    )(tokens, context, vectors, weights, cosine, sine)


def split_heads(rows):
    low = low_lanes(rows.shape)
    zero = jnp.zeros_like(rows)
    return jnp.where(low, rows, zero), jnp.where(low, zero, rows)


def between(shape, offset, low, high):
    index = lax.broadcasted_iota(jnp.int32, shape, 0) + offset
    return jnp.logical_and(index >= low, index < high)


def fold(values, combine):
    rows, cols = values.shape
    groups = values.reshape(rows // 8, 8, cols)
    return combine(groups, axis=0)


def forward_kernel(
    span_ref, clean_ref, noisy_ref, q_ref, k_ref, v_ref, out_ref, lse_ref, bias_ref, window_ref
):
    pairs = q_ref.shape[1] // LANES
    lanes = [slice(p * LANES, (p + 1) * LANES) for p in range(pairs)]

    def one_tile(t, _):
        clean_at = pl.multiple_of(CLEAN_OWN + t * TILE, TILE)
        noisy_at = pl.multiple_of(NOISY_OWN + t * TILE, EDGE)
        window_at = pl.multiple_of(NOISY_BASE + t * TILE, EDGE)
        key_low, key_high = clean_ref[t, 0:1, :], clean_ref[t, 1:2, :]
        own_low, own_high = noisy_ref[t, 0:1, :], noisy_ref[t, 1:2, :]
        allowed = between((WINDOW, TILE), 0, own_low, own_high)
        window_ref[...] = jnp.where(allowed, 0.0, neg_large)
        first_key, trips = span_ref[t, 0], span_ref[t, 1]
        queries, tops = [], []
        for cols in lanes:
            query = jnp.concatenate(
                [q_ref[pl.ds(noisy_at, TILE), cols], q_ref[pl.ds(clean_at, TILE), cols]], axis=0
            )
            heads = split_heads(query)
            queries += heads
            keys = k_ref[pl.ds(window_at, WINDOW), cols]
            for head in range(2):
                scores = dot(keys, heads[head][:TILE], NT) + window_ref[...]
                top = fold(scores, jnp.max)
                tops.append(
                    jnp.concatenate([top, jnp.full((8, TILE), neg_large, f32)], axis=1)
                )

        def first_pass(j, tops):
            at = pl.multiple_of(first_key + j * KEY_TILE, EDGE)
            allowed = between((KEY_TILE, 2 * TILE), at, key_low, key_high)
            bias_ref[j] = jnp.where(allowed, 0.0, neg_large)
            after = []
            for p, cols in enumerate(lanes):
                keys = k_ref[pl.ds(at, KEY_TILE), cols]
                for head in range(2):
                    scores = dot(keys, queries[2 * p + head], NT) + bias_ref[j]
                    after.append(jnp.maximum(tops[2 * p + head], fold(scores, jnp.max)))
            return tuple(after)

        tops = lax.fori_loop(0, trips, first_pass, tuple(tops))
        tops = [jnp.max(top, axis=0, keepdims=True) * to_base2 for top in tops]
        state = []
        keys = [k_ref[pl.ds(window_at, WINDOW), cols] for cols in lanes]
        values_t = [v_ref[pl.ds(window_at, WINDOW), cols].T for cols in lanes]
        scores = dot(keys[0], queries[0][:TILE], NT)
        late = None
        for h in range(2 * pairs):
            if h + 1 < 2 * pairs:
                ahead = dot(keys[(h + 1) // 2], queries[h + 1][:TILE], NT)
            expo = jnp.exp2(scores * to_base2 - tops[h][:, :TILE] + window_ref[...])
            if late is not None:
                state.append(jnp.concatenate([late, jnp.zeros((HD, TILE), f32)], axis=1))
            total = fold(expo, jnp.sum)
            state.append(jnp.concatenate([total, jnp.zeros((8, TILE), f32)], axis=1))
            side = slice(h % 2 * HD, (h % 2 + 1) * HD)
            late = dot(values_t[h // 2][side], expo.astype(bf16))
            scores = ahead
        state.append(jnp.concatenate([late, jnp.zeros((HD, TILE), f32)], axis=1))

        def second_pass(j, state):
            at = pl.multiple_of(first_key + j * KEY_TILE, EDGE)
            keys = [k_ref[pl.ds(at, KEY_TILE), cols] for cols in lanes]
            values_t = [v_ref[pl.ds(at, KEY_TILE), cols].T for cols in lanes]
            after = list(state)
            scores = dot(keys[0], queries[0], NT)
            late = None
            for h in range(2 * pairs):
                ahead = dot(keys[(h + 1) // 2], queries[h + 1], NT) if h + 1 < 2 * pairs else None
                expo = jnp.exp2(scores * to_base2 - tops[h] + bias_ref[j])
                after[2 * h] = state[2 * h] + fold(expo, jnp.sum)
                if late is not None:
                    after[2 * h - 1] = state[2 * h - 1] + late
                side = slice(h % 2 * HD, (h % 2 + 1) * HD)
                late = dot(values_t[h // 2][side], expo.astype(bf16))
                scores = ahead
            after[-1] = state[-1] + late
            return tuple(after)

        state = lax.fori_loop(0, trips, second_pass, tuple(state))
        low_at = pl.ds(pl.multiple_of(t * TILE, TILE), TILE)
        high_at = pl.ds(pl.multiple_of(HALF + t * TILE, TILE), TILE)
        for p, cols in enumerate(lanes):
            halves = []
            for head in range(2):
                h = 2 * p + head
                total = jnp.sum(state[2 * h], axis=0, keepdims=True)
                halves.append(state[2 * h + 1] / total)
                lse_ref[p, t, head : head + 1, :] = tops[h] + jnp.log2(total)
            pair = jnp.concatenate(halves, axis=0).T.astype(bf16)
            out_ref[low_at, cols] = pair[:TILE]
            out_ref[high_at, cols] = pair[TILE:]
        return 0

    lax.fori_loop(0, TILES, one_tile, 0)


def attend_forward(spans, clean_bounds, noisy_bounds, query, keys, values):
    count, cols = query.shape
    pairs = cols // LANES
    vmem = pl.BlockSpec(memory_space=pltpu.VMEM)
    work = pairs * 2 * 2 * HALF * TOK_DEV
    return pl.pallas_call(
        forward_kernel,
        in_specs=[pl.BlockSpec(memory_space=pltpu.SMEM)] + [vmem] * 5,
        out_specs=[vmem] * 2,
        out_shape=[
            jax.ShapeDtypeStruct((TOK_DEV, cols), bf16),
            jax.ShapeDtypeStruct((pairs, TILES, 2, 2 * TILE), f32),
        ],
        scratch_shapes=[
            pltpu.VMEM((NOISY_BASE // KEY_TILE + 1, KEY_TILE, 2 * TILE), f32),
            pltpu.VMEM((WINDOW, TILE), f32),
        ],
        name="attend_forward",
        cost_estimate=pl.CostEstimate(
            flops=4 * work * HD, bytes_accessed=8 * count * cols, transcendentals=work
        ),
    )(spans, clean_bounds, noisy_bounds, query, keys, values)


def backward_kernel(
    giving,
    span_ref,
    clean_ref,
    noisy_ref,
    q_ref,
    k_ref,
    v_ref,
    o_ref,
    d_ref,
    lse_ref,
    cos_ref,
    sin_ref,
    *refs,
):
    if giving:
        d2_hbm, w_hbm, w2_hbm, out_ref, give_ref, low_ref, *refs = refs
        dk_ref, dv_ref, bias_ref, d2_ref, w_ref, w2_ref, load_sem = refs
        loads = [(w_hbm, w_ref), (w2_hbm, w2_ref)]
        loads += [(d2_hbm.at[c, :HALF], d2_ref.at[c]) for c in range(3)]
        loads = [
            pltpu.make_async_copy(source, target, load_sem.at[n])
            for n, (source, target) in enumerate(loads)
        ]
        for load in loads:
            load.start()
    else:
        rows_hbm, out_ref, grad_ref, dk_ref, dv_ref, bias_ref, rows_ref, load_sem = refs
        load_rows = pltpu.make_async_copy(rows_hbm, rows_ref, load_sem.at[0])
        load_rows.start()
    pairs = q_ref.shape[1] // LANES
    lanes = [slice(p * LANES, (p + 1) * LANES) for p in range(pairs)]
    dk_ref[...] = jnp.zeros_like(dk_ref)
    dv_ref[...] = jnp.zeros_like(dv_ref)
    out_ref[0] = jnp.zeros_like(out_ref[0])

    def one_tile(t, _):
        clean_at = pl.multiple_of(CLEAN_OWN + t * TILE, TILE)
        noisy_at = pl.multiple_of(NOISY_OWN + t * TILE, EDGE)
        window_at = pl.multiple_of(NOISY_BASE + t * TILE, EDGE)
        low_at = pl.multiple_of(t * TILE, TILE)
        high_at = pl.multiple_of(HALF + t * TILE, TILE)
        key_low, key_high = clean_ref[t, 0:1, :], clean_ref[t, 1:2, :]
        own_low, own_high = noisy_ref[t, 0:1, :], noisy_ref[t, 1:2, :]
        queries, d_outs, inners, lses = [], [], [], []
        for p, cols in enumerate(lanes):

            def both(ref, low, high):
                return jnp.concatenate(
                    [ref[pl.ds(low, TILE), cols], ref[pl.ds(high, TILE), cols]], axis=0
                )

            queries.append(split_heads(both(q_ref, noisy_at, clean_at)))
            d_rows = both(d_ref, low_at, high_at)
            o_rows = both(o_ref, low_at, high_at)
            product = (d_rows.astype(f32) * o_rows.astype(f32)).T
            d_outs.append(split_heads(d_rows))
            inners.append(
                [
                    jnp.sum(product[head * HD : (head + 1) * HD], axis=0, keepdims=True) * 0.125
                    for head in range(2)
                ]
            )
            lses.append([lse_ref[p, t, head : head + 1, :] for head in range(2)])

        def accumulate(at, rows, cols, allowed, d_query):
            bias_ref[:rows, :cols] = jnp.where(allowed, 0.0, neg_large)
            after = list(d_query)
            keys = [k_ref[pl.ds(at, rows), span] for span in lanes]
            eighth = [v_ref[pl.ds(at, rows), span] * jnp.asarray(0.125, bf16) for span in lanes]
            keys_t = [part.T for part in keys]
            stack = lambda parts: jnp.concatenate([part[:cols] for part in parts], axis=0)

            def begin(h):
                p, head = h // 2, h % 2
                return (
                    dot(keys[p], queries[p][head][:cols], NT),
                    dot(eighth[p], d_outs[p][head][:cols], NT),
                )

            def finish_pair(p, weights, d_scores):
                span = lanes[p]
                for head in range(2):
                    side = slice(head * HD, (head + 1) * HD)
                    h = 2 * p + head
                    after[h] = d_query[h] + dot(keys_t[p][side], d_scores[head])
                dv_ref[pl.ds(at, rows), span] += dot(
                    jnp.concatenate(weights, axis=1), stack(d_outs[p])
                )
                dk_ref[pl.ds(at, rows), span] += dot(
                    jnp.concatenate(d_scores, axis=1), stack(queries[p])
                )

            ready = begin(0)
            held = None
            weights, d_scores = [], []
            for h in range(2 * pairs):
                ahead = begin(h + 1) if h + 1 < 2 * pairs else None
                p, head = h // 2, h % 2
                scores = ready[0] * to_base2 - lses[p][head][:, :cols] + bias_ref[:rows, :cols]
                probs = jnp.exp2(scores)
                d_score = (probs * (ready[1] - inners[p][head][:, :cols])).astype(bf16)
                weights.append(probs.astype(bf16))
                d_scores.append(d_score)
                if held is not None:
                    finish_pair(*held)
                    held = None
                if head == 1:
                    held = (p, weights, d_scores)
                    weights, d_scores = [], []
                ready = ahead
            finish_pair(*held)
            return tuple(after)

        allowed = between((WINDOW, TILE), 0, own_low, own_high)
        zero = jnp.zeros((HD, TILE), f32)
        start = accumulate(window_at, WINDOW, TILE, allowed, (zero,) * (2 * pairs))
        start = tuple(jnp.concatenate([part, zero], axis=1) for part in start)
        first_key, trips = span_ref[t, 0], span_ref[t, 1]

        def one_step(j, d_query):
            at = pl.multiple_of(first_key + j * KEY_TILE, EDGE)
            allowed = between((KEY_TILE, 2 * TILE), at, key_low, key_high)
            return accumulate(at, KEY_TILE, 2 * TILE, allowed, d_query)

        d_query = lax.fori_loop(0, trips, one_step, start)
        for p, span in enumerate(lanes):
            pair = jnp.concatenate(d_query[2 * p : 2 * p + 2], axis=0).T
            for at, part in ((noisy_at, pair[:TILE]), (clean_at, pair[TILE:])):
                turned = turn(part, cos_ref[pl.ds(at, TILE), :], -sin_ref[pl.ds(at, TILE), :])
                out_ref[0, pl.ds(at, TILE), span] = turned.astype(bf16)
        return 0

    lax.fori_loop(0, TILES, one_tile, 0)
    step = KEY_ROWS // 9

    def finish(i, _):
        rows = pl.ds(pl.multiple_of(i * step, EDGE), step)
        for span in lanes:
            out_ref[1, rows, span] = turn(
                dk_ref[rows, span], cos_ref[rows, :], -sin_ref[rows, :]
            ).astype(bf16)
        out_ref[2, rows, :] = dv_ref[rows, :].astype(bf16)
        return 0

    lax.fori_loop(0, 9, finish, 0)

    def weight_rows(i, _):
        rows = pl.ds(pl.multiple_of(i * ROW_TILE, LANES), ROW_TILE)
        for c in range(3):
            grad_ref[c, rows, :] = dot(rows_ref[rows, :], out_ref[c]).astype(bf16)
        return 0

    if giving:
        for load in loads:
            load.wait()
        total = 0.0
        for c in range(3):
            total = total + dot(out_ref[c, :HALF, :], w_ref[c], NT) + dot(d2_ref[c], w2_ref[c], NT)
        give_ref[...] = total
        low_ref[...] = total.astype(bf16)
    else:
        load_rows.wait()
        lax.fori_loop(0, rows_ref.shape[0] // ROW_TILE, weight_rows, 0)


def attend_backward(
    spans,
    clean_bounds,
    noisy_bounds,
    query,
    keys,
    values,
    attended,
    d_attended,
    lse,
    cosine,
    sine,
    rest,
):
    count, cols = query.shape
    vmem = pl.BlockSpec(memory_space=pltpu.VMEM)
    hbm = pl.BlockSpec(memory_space=pl.ANY)
    shape = jax.ShapeDtypeStruct
    giving = len(rest) > 1
    if giving:
        width = rest[1].shape[1]
        second = [shape((HALF, width), f32), shape((HALF, width), bf16)]
        scratch = [
            pltpu.VMEM((3, HALF, cols), bf16),
            pltpu.VMEM(rest[1].shape, bf16),
            pltpu.VMEM(rest[2].shape, bf16),
            pltpu.SemaphoreType.DMA((5,)),
        ]
    else:
        second = [shape((3, rest[0].shape[0], cols), bf16)]
        scratch = [pltpu.VMEM(rest[0].shape, bf16), pltpu.SemaphoreType.DMA((1,))]
    return pl.pallas_call(
        functools.partial(backward_kernel, giving),
        in_specs=[pl.BlockSpec(memory_space=pltpu.SMEM)]
        + [vmem] * 10
        + [hbm] * len(rest),
        out_specs=[vmem] * (1 + len(second)),
        scratch_shapes=[
            pltpu.VMEM((count, cols), f32),
            pltpu.VMEM((count, cols), f32),
            pltpu.VMEM((max(KEY_TILE, WINDOW), 2 * TILE), f32),
        ]
        + scratch,
        out_shape=[shape((3, count, cols), bf16)] + second,
        name="attend_backward",
        cost_estimate=pl.CostEstimate(
            flops=36 * 10**9, bytes_accessed=36 * 10**6, transcendentals=6 * 10**6
        ),
    )(
        spans,
        clean_bounds,
        noisy_bounds,
        query,
        keys,
        values,
        attended,
        d_attended,
        lse,
        cosine,
        sine,
        *rest,
    )


PIECES = 16
MESH = pl.DeviceIdType.MESH


def flip(value, mask):
    result = value
    for b in range(mask.bit_length()):
        if mask >> b & 1:
            result = result + (1 << b) * (1 - 2 * ((value // (1 << b)) % 2))
    return result


class Exchange:
    def __init__(self, bits, count, rows, width, back=True):
        self.bits, self.count, self.rows, self.width = bits, count, rows, width
        self.back = back
        self.half, self.quarter, self.piece = rows // 2, rows // 4, rows // PIECES
        self.extra = list(range(4, bits))

    def slots(self):
        return 8 + 2 * (6 if self.back else 4) + (3 if self.extra else 0)

    def scratch(self):
        k, w = self.count, self.width
        cross = k if not self.back else 1
        shapes = [
            pltpu.VMEM((k, 2 - self.back, self.half, w), bf16),
            pltpu.VMEM((cross, self.half, w), bf16),
            pltpu.VMEM((cross, self.half, w), bf16),
            pltpu.VMEM((k, self.quarter, w), bf16),
            pltpu.VMEM((k, self.quarter, w), bf16),
            pltpu.VMEM((k, self.quarter, w), f32),
            pltpu.VMEM((k, 3, self.piece, w), bf16),
            pltpu.VMEM((k, 3, self.piece, w), bf16),
        ]
        lanes_of = (1, 0, 1, 3, 3, 1, 1) if self.back else (2, 1, 1, 3, 0, 0, 0)
        for lanes in [lanes for lanes in lanes_of if lanes]:
            shapes += [pltpu.SemaphoreType.DMA((k, lanes))] * 2
        if self.extra:
            n = len(self.extra)
            shapes += [pltpu.VMEM((k, 2 * n, self.piece, w), bf16)]
            shapes += [pltpu.SemaphoreType.DMA((k, n))] * 2
        return shapes

    def bind(self, place, part, refs):
        (self.a_in, self.b_out, self.b_in, self.c_out, self.c_in, self.keep) = refs[:6]
        self.d_out, self.d_in = refs[6:8]
        names = "acdefg" if self.back else "abcd"
        self.sems = {name: (refs[8 + 2 * i], refs[9 + 2 * i]) for i, name in enumerate(names)}
        if self.extra:
            at = 8 + 2 * len(names)
            self.x_buf, self.x_send, self.x_recv = refs[at : at + 3]
        self.place, self.part = place, part
        self.core, self.x, self.z = place % 2, (place // 2) % 2, (place // 4) % 4
        self.sibling = {"dp": flip(place, 1)}
        self.beside = {"dp": flip(place, 2)}
        self.across = {"mp": 1 - part}
        self.peers = [{"dp": flip(place, j << 2)} for j in range(1, 4)]
        self.partners = [self.sibling, self.beside, self.across] + self.peers
        self.partners += [{"dp": flip(place, 1 << b)} for b in self.extra]
        return self

    def greet(self):
        barrier = pltpu.get_barrier_semaphore()
        for partner in self.partners:
            pl.semaphore_signal(barrier, inc=1, device_id=partner, device_id_type=MESH)
        pl.semaphore_wait(barrier, len(self.partners))

    def copy(self, name, k, lane, source, target, device):
        out, into = self.sems[name]
        return pltpu.make_async_remote_copy(
            src_ref=source,
            dst_ref=target,
            send_sem=out.at[k, lane],
            recv_sem=into.at[k, lane],
            device_id=device,
            device_id_type=MESH,
        )

    def rows_at(self, start, size):
        return pl.ds(pl.multiple_of(start, PIECES), size)

    def copy_a(self, k, lane, grads):
        source = grads.at[k, self.rows_at((1 - self.core) * self.half, self.half)]
        return self.copy("a", k, lane, source, self.a_in.at[k, lane], self.sibling)

    def copy_b(self, k):
        return self.copy("b", k, 0, self.b_out.at[k], self.b_in.at[k], self.across)

    def copy_c(self, k):
        return self.copy("c", k, 0, self.c_out.at[k], self.c_in.at[k], self.beside)

    def copy_d(self, k, j):
        return self.copy("d", k, j, self.d_out.at[k, j], self.d_in.at[k, j], self.peers[j])

    def spot(self, change=0):
        start = self.core * self.half + self.x * self.quarter
        return self.rows_at(start + flip(self.z, change) * self.piece, self.piece)

    def copy_e(self, k, j, full):
        rows = full.at[k, self.spot()]
        return self.copy("e", k, j, rows, rows, self.peers[j])

    def copy_f(self, k, full):
        start = self.core * self.half + self.x * self.quarter
        rows = full.at[k, self.rows_at(start, self.quarter)]
        return self.copy("f", k, 0, rows, rows, self.beside)

    def copy_g(self, k, full):
        rows = full.at[k, self.rows_at(self.core * self.half, self.half)]
        return self.copy("g", k, 0, rows, rows, self.sibling)

    def start_a(self, k, lane, grads):
        self.copy_a(k, lane, grads).start()

    def stage_b(self, k, others):
        self.copy_a(k, 0, others).wait()
        mine = others[k, self.rows_at(self.core * self.half, self.half), :].astype(f32)
        self.b_out[k] = (mine + self.a_in[k, 0].astype(f32)).astype(bf16)
        self.copy_b(k).start()

    def stage_c(self, k, grads, crossed=None):
        lane = 0 if self.back else 1
        self.copy_a(k, lane, grads).wait()
        if not self.back:
            self.copy_b(k).wait()

        def total(which):
            inner = which * self.quarter
            rows = self.rows_at(inner, self.quarter)
            mine = grads[k, self.rows_at(self.core * self.half + inner, self.quarter), :]
            got = self.a_in[k, lane, rows, :].astype(f32)
            if not self.back:
                got = got + self.b_in[k, rows, :].astype(f32)
            elif crossed is not None:
                got = got + crossed(rows)
            return mine.astype(f32) + got

        self.c_out[k] = total(1 - self.x).astype(bf16)
        self.copy_c(k).start()
        self.keep[k] = total(self.x)

    def stage_d(self, k):
        self.copy_c(k).wait()
        for j in range(4):
            rows = self.rows_at(flip(self.z, j) * self.piece, self.piece)
            total = self.keep[k, rows, :] + self.c_in[k, rows, :].astype(f32)
            if j:
                self.d_out[k, j - 1] = total.astype(bf16)
                self.copy_d(k, j - 1).start()
            else:
                self.keep[k, rows, :] = total

    def gather_d(self, k):
        rows = self.rows_at(self.z * self.piece, self.piece)
        total = self.keep[k, rows, :]
        for j in range(3):
            self.copy_d(k, j).wait()
            total = total + self.d_in[k, j].astype(f32)
        for i, b in enumerate(self.extra):
            mine = self.x_buf.at[k, 2 * i]
            mine[...] = total.astype(bf16)
            swap = pltpu.make_async_remote_copy(
                src_ref=mine,
                dst_ref=self.x_buf.at[k, 2 * i + 1],
                send_sem=self.x_send.at[k, i],
                recv_sem=self.x_recv.at[k, i],
                device_id={"dp": flip(self.place, 1 << b)},
                device_id_type=MESH,
            )
            swap.start()
            swap.wait()
            total = total.astype(bf16).astype(f32) + self.x_buf[k, 2 * i + 1].astype(f32)
        return total.astype(bf16)

    def stage_e(self, k, full):
        full[k, self.spot(), :] = self.gather_d(k)
        for j in range(3):
            self.copy_e(k, j, full).start()

    def stage_f(self, k, full):
        for j in range(3):
            self.copy_e(k, j, full).wait()
        self.copy_f(k, full).start()

    def stage_g(self, k, full):
        self.copy_f(k, full).wait()
        self.copy_g(k, full).start()

    def stage_h(self, k, full):
        self.copy_g(k, full).wait()


def at_step(step, count, action):
    @pl.when(jnp.logical_and(step >= 0, step < count))
    def _():
        action(step)


def middle_kernel(exchanges, tiles, *refs):
    (
        x_ref,
        att_ref,
        att2_ref,
        wout_ref,
        wout2_ref,
        dy_ref,
        vectors_ref,
        bup_ref,
        up_mine,
        up_here,
        up_beside,
        down_mine,
        down_here,
        out_hbm,
        mid_hbm,
        datt_hbm,
        datt2_hbm,
        gout_ref,
        gout2_ref,
        gbup_ref,
        small_ref,
        pieces_ref,
        up_there,
        down_there,
        pass_up,
        pass_down,
        up_buf,
        down_buf,
        load_sem,
        n2_ref,
        total_ref,
        dn2_ref,
        act_ref,
        dpre_ref,
        n2_t,
        bup_other,
        bias_sem,
        out_ref,
        mid_ref,
        datt_ref,
        datt2_ref,
        store_sem,
        down_grad,
        up_grad,
        *rest,
    ) = refs
    place, part = lax.axis_index("dp"), lax.axis_index("mp")
    ex = exchanges[0].bind(place, part, rest)
    ex_up = exchanges[1].bind(place, part, rest[exchanges[0].slots() :])
    sides = ((ex, down_grad), (ex_up, up_grad))
    core = ex.core
    count = tiles // 2
    rows_all = x_ref.shape[0]
    blocks = rows_all // ROW_TILE
    width = x_ref.shape[1]
    lanes = width // 2

    def which(i):
        other = jnp.logical_or(i == 0, jnp.logical_and(i % 2 == 1, i < tiles - 1))
        mine = jnp.where(i == tiles - 1, count - 1, i // 2 - 1)
        return other, jnp.where(other, (i + 1) // 2, mine)

    quarter = width // 4
    strip = HIDDEN_TILE // 2
    held = 2 * core + ex.x
    kept = 2 * core + 1 - ex.x

    def load_up(i, source, h):
        target = up_buf.at[i % 2, h * quarter : (h + 1) * quarter]
        return pltpu.make_async_copy(source, target, load_sem.at[i % 2, h])

    def load_down(i, source, h):
        target = down_buf.at[i % 2, h * strip : (h + 1) * strip]
        return pltpu.make_async_copy(source, target, load_sem.at[i % 2, 4 + h])

    def hand_up(k, part_of):
        cols = pl.ds(pl.multiple_of(k * HIDDEN_TILE, HIDDEN_TILE), HIDDEN_TILE)
        side = ex.x if part_of == 0 else 1 - ex.x
        rows = pl.ds(pl.multiple_of(side * quarter, EDGE), quarter)
        return pltpu.make_async_remote_copy(
            src_ref=(up_here, up_beside)[part_of].at[:, cols],
            dst_ref=up_there.at[k, rows],
            send_sem=pass_up.at[k, 2 * part_of],
            recv_sem=pass_up.at[k, 2 * part_of + 1],
            device_id=ex.sibling,
            device_id_type=MESH,
        )

    def hand_down(b):
        return pltpu.make_async_remote_copy(
            src_ref=down_here.at[strip_rows(b)],
            dst_ref=down_there.at[b],
            send_sem=pass_down.at[b, 0],
            recv_sem=pass_down.at[b, 1],
            device_id=ex.sibling,
            device_id_type=MESH,
        )

    def strip_rows(b):
        return pl.ds(pl.multiple_of(b * strip, strip), strip)

    def start_loads(i):
        other, k = which(i)
        mine = jnp.logical_not(other)
        cols = pl.ds(pl.multiple_of(k * HIDDEN_TILE, HIDDEN_TILE), HIDDEN_TILE)

        @pl.when(other)
        def _():
            hand_up(k, 0).wait()
            hand_up(k, 1).wait()

        for h in range(4):

            @pl.when(mine)
            def _():
                load_up(i, up_mine.at[h * quarter : (h + 1) * quarter, cols], h).start()

            @pl.when(jnp.logical_and(other, held == h))
            def _():
                load_up(i, up_here.at[:, cols], h).start()

            @pl.when(jnp.logical_and(other, kept == h))
            def _():
                load_up(i, up_beside.at[:, cols], h).start()

            @pl.when(jnp.logical_and(other, core != h // 2))
            def _():
                rows = slice(h % 2 * quarter, (h % 2 + 1) * quarter)
                load_up(i, up_there.at[k, rows], h).start()

        for h in range(2):
            b = 2 * k + h
            inner = b % count

            @pl.when(mine)
            def _():
                load_down(i, down_mine.at[strip_rows(b), :], h).start()

            @pl.when(jnp.logical_and(other, core == b // count))
            def _():
                load_down(i, down_here.at[strip_rows(inner), :], h).start()

            @pl.when(jnp.logical_and(other, core != b // count))
            def _():
                hand_down(inner).wait_recv()
                load_down(i, down_there.at[inner], h).start()

    def wait_loads(i):
        for h in range(4):
            load_up(i, up_mine.at[:quarter, :HIDDEN_TILE], h).wait()
        for h in range(2):
            load_down(i, down_mine.at[:strip, :], h).wait()

    ex.greet()
    bias_swap = pltpu.make_async_remote_copy(
        src_ref=bup_ref,
        dst_ref=bup_other,
        send_sem=bias_sem.at[0],
        recv_sem=bias_sem.at[1],
        device_id=ex.across,
        device_id_type=MESH,
    )
    bias_swap.start()

    def hand(k, _):
        hand_up(k, 0).start()
        hand_up(k, 1).start()
        hand_down(k).start()
        return 0

    lax.fori_loop(0, count, hand, 0)

    def prologue(n, _):
        prologue_block(2 * n)
        prologue_block(2 * n + 1)
        return 0

    def prologue_block(r):
        rows = pl.ds(pl.multiple_of(r * ROW_TILE, ROW_TILE), ROW_TILE)
        branch = dot(att_ref[rows, :], wout_ref[...]) + dot(att2_ref[rows, :], wout2_ref[...])
        mid = x_ref[rows, :].astype(f32) + branch
        mid_ref[rows, :] = mid
        unit = normal(mid)[0]
        n2_ref[rows, :] = (unit * vectors_ref[2:3, :] + vectors_ref[3:4, :]).astype(bf16)
        total_ref[rows, :] = mid + vectors_ref[4:5, :]
        dn2_ref[rows, :] = jnp.zeros((ROW_TILE, width), f32)

    lax.fori_loop(0, blocks // 2, prologue, 0)
    start_loads(0)
    for c in range(width // LANES):
        cols = slice(c * LANES, (c + 1) * LANES)
        n2_t[cols, :] = n2_ref[:, cols].T
    n2_t[width:, :] = jnp.ones((PIECES, rows_all), bf16)
    bias_swap.wait()

    def tile(i):
        other, k = which(i)
        slot = i % 2
        wait_loads(i)

        @pl.when(i + 1 < tiles)
        def _():
            start_loads(i + 1)

        up, down = up_buf.at[slot], down_buf.at[slot]
        bias_at = jnp.where(other, k, count + k)
        bias = jnp.where(other, bup_other[k], bup_ref[k])
        linear = 0.7978845608028654
        cubic = linear * 0.044715
        for r in range(blocks):
            rows = slice(r * ROW_TILE, (r + 1) * ROW_TILE)
            pre = dot(n2_ref[rows, :], up[...]) + bias
            d_act = dot(dy_ref[rows, :], down[...], NT)
            square = pre * pre
            bend = jnp.tanh(pre * (square * cubic + linear))
            gate = 0.5 * bend + 0.5
            full_act = pre * gate
            slope = gate + (full_act - full_act * gate) * (square * (6.0 * cubic) + 2.0 * linear)
            act_ref[rows, :] = full_act.astype(bf16)
            dpre_ref[rows, :] = (d_act * slope).astype(bf16)
        total_ref[...] += dot(act_ref[...], down[...])
        dn2_ref[...] += dot(dpre_ref[...], up[...], NT)
        down_grad[k] = dot(act_ref[...].T, dy_ref[...]).astype(bf16)

        def start(lane):
            for side, grad in sides:
                side.start_a(k, lane, grad)

        by_rows = dot(n2_t[...], dpre_ref[...])
        up_grad[k] = by_rows[:width].astype(bf16)
        gbup_ref[bias_at] = by_rows[width : width + 1]
        pl.when(other)(functools.partial(start, 0))
        pl.when(jnp.logical_not(other))(functools.partial(start, 1))

    def each(k, when, action):
        @pl.when(jnp.logical_and(when, jnp.logical_and(k >= 0, k < count)))
        def _():
            for n, (side, grad) in enumerate(sides):
                action(n, side, grad, k)

    def stage_b(n, side, grad, k):
        side.stage_b(k, grad)

    def stage_c(n, side, grad, k):
        side.stage_c(k, grad)

    def stage_d(n, side, grad, k):
        side.stage_d(k)

    def arrive(n, side, grad, k):
        piece = side.gather_d(k)
        if n == 0:
            pieces_ref[k] = piece
        else:
            for c in range(width // HIDDEN_TILE):
                cols = slice(c * HIDDEN_TILE, (c + 1) * HIDDEN_TILE)
                pieces_ref[count + k, :, cols] = piece[c * PIECES : (c + 1) * PIECES]

    def steps(i):
        even = i % 2 == 0
        odd = jnp.logical_not(even)
        each((i - 5) // 2, odd, arrive)
        each((i - 4) // 2, even, stage_d)
        each((i - 3) // 2, odd, stage_c)
        each(i // 2, even, stage_b)

    def epilogue(r):
        rows = pl.ds(pl.multiple_of(r * ROW_TILE, ROW_TILE), ROW_TILE)
        out_ref[rows, :] = total_ref[rows, :].astype(bf16)
        unit, scale = normal(mid_ref[rows, :])
        d_rows = dn2_ref[rows, :]
        dy = dy_ref[rows, :].astype(f32)
        lean = d_rows * vectors_ref[2:3, :]
        d_mid = dy + scale * (
            lean
            - jnp.mean(lean, axis=-1, keepdims=True)
            - unit * jnp.mean(lean * unit, axis=-1, keepdims=True)
        )
        mid_ref[rows, :] = d_mid
        d_branch = d_mid.astype(bf16)
        n2_ref[rows, :] = d_branch
        datt_ref[rows, :] = dot(d_branch, wout_ref[...], NT).astype(bf16)
        datt2_ref[rows, :] = dot(d_branch, wout2_ref[...], NT).astype(bf16)
        add = lambda values: jnp.sum(values, axis=0, keepdims=True)
        small_ref[0:1, :] += add(d_rows * unit)
        small_ref[1:2, :] += add(d_rows)
        small_ref[2:3, :] += add(dy)

    def out_grads():
        for source, target in ((att_ref, gout_ref), (att2_ref, gout2_ref)):
            grad = dot(source[...].T, n2_ref[...]).astype(bf16)
            for a in range(wout_ref.shape[0] // LANES):
                for b in range(2):
                    rows = slice(a * LANES, (a + 1) * LANES)
                    cols = slice(b * lanes, (b + 1) * lanes)
                    spread = slice(a * lanes, (a + 1) * lanes)
                    target[b * LANES : (b + 1) * LANES, spread] = grad[rows, cols]

    def main(i, _):
        pl.when(i < tiles)(functools.partial(tile, i))

        @pl.when(jnp.logical_and(i >= tiles, i < tiles + 2))
        def _():
            first = (i - tiles) * (blocks // 2)
            for r in range(blocks // 2):
                epilogue(first + r)

        @pl.when(i == tiles + 2)
        def _():
            for store in stores:
                store.start()
            out_grads()

        steps(i)
        return 0

    small_ref[...] = jnp.zeros_like(small_ref)
    stores = [
        pltpu.make_async_copy(source, target, store_sem.at[n])
        for n, (source, target) in enumerate(
            (
                (datt2_ref, datt2_hbm),
                (out_ref, out_hbm),
                (mid_ref, mid_hbm),
                (datt_ref, datt_hbm),
            )
        )
    ]
    lax.fori_loop(0, tiles + 4, main, 0)
    for store in stores:
        store.wait()

    def handed(slot, _):
        hand_down(slot).wait_send()
        return 0

    lax.fori_loop(0, count, handed, 0)


def middle(bits, x, att, att2, wout, wout2, dy, vectors, bup, ups, downs):
    rows, width = x.shape
    hidden = ups[0].shape[1]
    count = hidden // HIDDEN_TILE
    tiles = 2 * count
    exchanges = (
        Exchange(bits, count, HIDDEN_TILE, width, False),
        Exchange(bits, count, width, HIDDEN_TILE, False),
    )
    vmem = pl.BlockSpec(memory_space=pltpu.VMEM)
    hbm = pl.BlockSpec(memory_space=pl.ANY)
    shape = jax.ShapeDtypeStruct
    depth = wout.shape[0]
    return pl.pallas_call(
        functools.partial(middle_kernel, exchanges, tiles),
        in_specs=[vmem] * 8 + [hbm] * 5,
        out_specs=[hbm] * 4 + [vmem] * 5,
        out_shape=[
            shape((rows, width), bf16),
            shape((rows, width), f32),
            shape(att.shape, bf16),
            shape(att2.shape, bf16),
            shape((2 * LANES, depth // LANES * width // 2), bf16),
            shape((2 * LANES, depth // LANES * width // 2), bf16),
            shape((tiles, 1, HIDDEN_TILE), f32),
            shape((8, width), f32),
            shape((2 * count, PIECES, width), bf16),
        ],
        scratch_shapes=[
            pltpu.VMEM((count, width // 2, HIDDEN_TILE), bf16),
            pltpu.VMEM((count, HIDDEN_TILE // 2, width), bf16),
            pltpu.SemaphoreType.DMA((count, 4)),
            pltpu.SemaphoreType.DMA((count, 2)),
            pltpu.VMEM((2, width, HIDDEN_TILE), bf16),
            pltpu.VMEM((2, HIDDEN_TILE, width), bf16),
            pltpu.SemaphoreType.DMA((2, 6)),
            pltpu.VMEM((rows, width), bf16),
            pltpu.VMEM((rows, width), f32),
            pltpu.VMEM((rows, width), f32),
            pltpu.VMEM((rows, HIDDEN_TILE), bf16),
            pltpu.VMEM((rows, HIDDEN_TILE), bf16),
            pltpu.VMEM((width + PIECES, rows), bf16),
            pltpu.VMEM(bup.shape, f32),
            pltpu.SemaphoreType.DMA((2,)),
            pltpu.VMEM((rows, width), bf16),
            pltpu.VMEM((rows, width), f32),
            pltpu.VMEM(att.shape, bf16),
            pltpu.VMEM(att2.shape, bf16),
            pltpu.SemaphoreType.DMA((4,)),
            pltpu.VMEM((count, HIDDEN_TILE, width), bf16),
            pltpu.VMEM((count, width, HIDDEN_TILE), bf16),
        ]
        + exchanges[0].scratch()
        + exchanges[1].scratch(),
        compiler_params=pltpu.CompilerParams(
            collective_id=0, has_side_effects=True, vmem_limit_bytes=67043328
        ),
        name="middle",
        cost_estimate=pl.CostEstimate(
            flops=60 * 10**9, bytes_accessed=40 * 10**6, transcendentals=4 * 10**6
        ),
    )(x, att, att2, wout, wout2, dy, vectors, bup, *ups, *downs)


def leave_kernel(exchange, *refs):
    (
        rows_hbm,
        mine_out_ref,
        crossed_ref,
        crossed_out_ref,
        d_hbm,
        d2_hbm,
        w_hbm,
        w2_hbm,
        tokens_hbm,
        context_hbm,
        given_hbm,
        small_ref,
        small2_ref,
        gqkv_ref,
        gout_ref,
        back_hbm,
        sums_ref,
        full_ref,
        out_buf,
        rows_t_ref,
        d_ref,
        d2_ref,
        w_ref,
        w2_ref,
        tokens_ref,
        context_ref,
        given_ref,
        load_sem,
        rows_ref,
        give_ref,
        take_ref,
        swap_sem,
        back_sem,
        norm_ref,
        near_ref,
        far_ref,
        near_sem,
        far_sem,
        *rest,
    ) = refs
    place, part = lax.axis_index("dp"), lax.axis_index("mp")
    ex = exchange.bind(place, part, rest)
    count, bits = ex.count, ex.bits
    loads = [
        pltpu.make_async_copy(source, target, load_sem.at[n])
        for n, (source, target) in enumerate(
            (
                (d_hbm, d_ref),
                (rows_hbm, rows_t_ref),
                (w_hbm, w_ref),
                (w2_hbm, w2_ref),
                (d2_hbm, d2_ref),
                (tokens_hbm, tokens_ref),
                (context_hbm, context_ref),
                (given_hbm, given_ref),
            )
        )
    ]
    for load in loads:
        load.start()
    near_id = part * 4 + place % 4
    near = [
        {"dp": flip(place, j % 4), "mp": part if j < 4 else 1 - part} for j in range(1, 8)
    ]
    ex.partners += [near[j - 1] for j in (3, 5, 6, 7)]
    ex.greet()

    lanes = d_ref.shape[2]
    split = mine_out_ref.shape[1] // lanes
    for r in range(split):
        cols = slice(r * lanes, (r + 1) * lanes)
        total = mine_out_ref[:, cols].astype(f32) + crossed_out_ref[:, cols].astype(f32)
        out_buf[r] = total.astype(bf16)
        ex.start_a(r, 0, out_buf)
    step = HALF + 2 * EDGE

    def back_rows(n):
        start = CLEAN_OWN + n * (KEY_ROWS - step - CLEAN_OWN)
        rows = pl.ds(pl.multiple_of(start, EDGE), step)
        total = 0.0
        for grads, weights in ((d_ref, w_ref), (d2_ref, w2_ref)):
            for c in range(3):
                total = total + dot(grads[c, rows, :], weights[c], NT)
        rows_ref[rows, :] = total

    def grad_chunk(c):
        for r in range(split):
            rows = slice(r * ROW_TILE, (r + 1) * ROW_TILE)
            k = (c + 1) * split + r
            out_buf[k] = dot(rows_t_ref[rows, :], d_ref[c]).astype(bf16)
            ex.start_a(k, 0, out_buf)

    def stage_c(k):
        @pl.when(k >= split)
        def _():
            ex.stage_c(k, out_buf, lambda rows: crossed_ref[k - split, rows, :].astype(f32))

        @pl.when(k < split)
        def _():
            ex.stage_c(k, out_buf)

    def arrive(k):
        ex.stage_h(k, full_ref)

        @pl.when(k < split)
        def _():
            rows = pl.ds(pl.multiple_of(k * LANES, LANES), LANES)
            for b in range(2):
                piece = full_ref[k, b * LANES : (b + 1) * LANES, :]
                gout_ref[rows, b * lanes : (b + 1) * lanes] = piece

        @pl.when(k >= split)
        def _():
            n = k - split
            rows = pl.ds(pl.multiple_of(n % split * ROW_TILE, ROW_TILE), ROW_TILE)
            gqkv_ref[n // split, rows, :] = full_ref[k]

    def group(g, action):
        @pl.when(jnp.logical_and(g >= 0, g < count // split))
        def _():
            lax.fori_loop(g * split, (g + 1) * split, lambda k, _: (action(k), 0)[1], 0)

    def steps(i):
        group(i - 5, arrive)
        group(i - 4, lambda k: ex.stage_g(k, full_ref))
        group(i - 3, lambda k: ex.stage_f(k, full_ref))
        group(i - 2, lambda k: ex.stage_e(k, full_ref))
        group(i - 1, lambda k: ex.stage_d(k))
        group(i, stage_c)

    width = tokens_ref.shape[1]

    def swap():
        return pltpu.make_async_remote_copy(
            src_ref=give_ref,
            dst_ref=take_ref,
            send_sem=swap_sem.at[0],
            recv_sem=swap_sem.at[1],
            device_id=ex.across,
            device_id_type=MESH,
        )

    def sums_of(d_rows, units):
        add = lambda values: jnp.sum(values, axis=0, keepdims=True)
        norm_ref[0:1, :] += add(d_rows * units)
        norm_ref[1:2, :] += add(d_rows)

    parts = tokens_ref.shape[0] // TILE
    lead = small_ref.shape[0] - 2
    bias = lead - 3
    norm_ref[...] = jnp.zeros_like(norm_ref)
    for load in loads[:2]:
        load.wait()

    def own_at(b):
        start = jnp.where(b < TILES, NOISY_OWN + b * TILE, CLEAN_OWN + (b - TILES) * TILE)
        return pl.ds(pl.multiple_of(start, EDGE), TILE)

    def tokens_at(b):
        return pl.ds(pl.multiple_of(b * TILE, TILE), TILE)

    def ready():
        for load in loads[2:]:
            load.wait()

    def give_edges():
        side = rows_ref[NOISY_BASE:NOISY_OWN, :] + rows_ref[NOISY_OWN + HALF :, :]
        after = rows_ref[2 * HALF : NOISY_BASE, :]
        give_ref[:EDGE, :] = after.astype(bf16)
        give_ref[EDGE:, :] = side.astype(bf16)
        swap().start()
        sums_of(after, normal(context_ref[:EDGE, :].astype(f32))[0])
        sums_of(side, normal(context_ref[HALF:, :].astype(f32))[0])

    def tell_near():
        def context_sums(b, _):
            rows = tokens_at(b)
            sums_of(given_ref[rows, :], normal(context_ref[rows, :].astype(f32))[0])
            return 0

        lax.fori_loop(0, HALF // TILE, context_sums, 0)

        def own_sums(b, _):
            sums_of(rows_ref[own_at(b), :], normal(tokens_ref[tokens_at(b), :].astype(f32))[0])
            return 0

        lax.fori_loop(0, parts, own_sums, 0)
        blank = jnp.zeros((16 - lead - 2 - bias, width), f32)
        near_ref[near_id] = jnp.concatenate(
            [small_ref[:lead, :], norm_ref[:2, :], small2_ref[:bias, :], blank], axis=0
        ).astype(bf16)
        for j in range(1, 8):
            near_copy(j).start()

    def near_copy(j):
        return pltpu.make_async_remote_copy(
            src_ref=near_ref.at[near_id],
            dst_ref=near_ref.at[near_id],
            send_sem=near_sem.at[j, 0],
            recv_sem=near_sem.at[j, 1],
            device_id=near[j - 1],
            device_id_type=MESH,
        )

    def near_got(j):
        came = (part + j // 4) % 2 * 4 + flip(place % 4, j % 4)
        return pltpu.make_async_remote_copy(
            src_ref=near_ref.at[came],
            dst_ref=near_ref.at[came],
            send_sem=near_sem.at[j, 0],
            recv_sem=near_sem.at[j, 1],
            device_id=near[j - 1],
            device_id_type=MESH,
        )

    def far_copy(j, at):
        return pltpu.make_async_remote_copy(
            src_ref=far_ref.at[at],
            dst_ref=far_ref.at[at],
            send_sem=far_sem.at[j, 0],
            recv_sem=far_sem.at[j, 1],
            device_id=ex.peers[j - 1],
            device_id_type=MESH,
        )

    def tell_far():
        for j in range(1, 8):
            near_copy(j).wait_send()
            near_got(j).wait_recv()
        near_sum = lambda at: sum(near_ref[at + j].astype(f32) for j in range(1, 4)) + near_ref[
            at
        ].astype(f32)
        plane, other = near_sum(part * 4), near_sum((1 - part) * 4)
        total = near_sum(0) + near_sum(4)
        mixed = plane[:bias] + other[lead + 2 : lead + 2 + bias]
        far_ref[ex.z] = jnp.concatenate([mixed, total[bias:]], axis=0).astype(bf16)
        for j in range(1, 4):
            far_copy(j, ex.z).start()

    halves = [
        pltpu.make_async_copy(
            rows_ref.at[start : start + HALF],
            back_hbm.at[n * HALF : (n + 1) * HALF],
            back_sem.at[n],
        )
        for n, start in enumerate((NOISY_OWN, CLEAN_OWN))
    ]

    def take_back():
        swap().wait()
        begin = slice(CLEAN_OWN, CLEAN_OWN + EDGE)
        rows_ref[begin, :] += take_ref[:EDGE, :].astype(f32)
        edge = pl.ds(pl.multiple_of(NOISY_OWN + (1 - part) * (HALF - EDGE), EDGE), EDGE)
        rows_ref[edge, :] += take_ref[EDGE:, :].astype(f32)
        for half in halves:
            half.start()

    def end_far():
        for j in range(1, 4):
            far_copy(j, ex.z).wait_send()
            far_copy(j, flip(ex.z, j)).wait_recv()
        total = far_ref[0].astype(f32)
        for j in range(1, 4):
            total = total + far_ref[j].astype(f32)
        for i, b in enumerate(ex.extra):
            total = total.astype(bf16).astype(f32)
            far_ref[4 + 2 * i] = total.astype(bf16)
            trade = pltpu.make_async_remote_copy(
                src_ref=far_ref.at[4 + 2 * i],
                dst_ref=far_ref.at[5 + 2 * i],
                send_sem=far_sem.at[4 + i, 0],
                recv_sem=far_sem.at[4 + i, 1],
                device_id={"dp": flip(place, 1 << b)},
                device_id_type=MESH,
            )
            trade.start()
            trade.wait()
            total = total + far_ref[5 + 2 * i].astype(f32)
        sums_ref[...] = total

    groups = count // split - 1
    actions = {
        groups + 1: give_edges,
        groups + 2: tell_near,
        groups + 3: take_back,
        groups + 4: tell_far,
        groups + 6: end_far,
    }

    def phase(p, _):
        @pl.when(p < groups)
        def _():
            grad_chunk(p)

        pl.when(p == groups)(ready)

        @pl.when(jnp.logical_and(p >= groups, p < groups + 2))
        def _():
            back_rows(p - groups)

        for n, action in actions.items():
            pl.when(p == n)(action)
        steps(p)
        return 0

    lax.fori_loop(0, groups + 7, phase, 0)
    for half in halves:
        half.wait()


def leave(bits, rows_t, mine, crossed, d_fields, weights, tokens, context, given, small, small2):
    rows, cols = ROW_TILE, d_fields[0].shape[2]
    total = mine.shape[1] // cols + crossed[0].shape[0]
    exchange = Exchange(bits, total, rows, cols)
    count, width = tokens.shape
    vmem = pl.BlockSpec(memory_space=pltpu.VMEM)
    hbm = pl.BlockSpec(memory_space=pl.ANY)
    shape = jax.ShapeDtypeStruct
    return pl.pallas_call(
        functools.partial(leave_kernel, exchange),
        in_specs=[hbm] + [vmem] * 3 + [hbm] * 7 + [vmem] * 2,
        out_specs=[vmem] * 2 + [hbm, vmem],
        out_shape=[
            shape(weights[0].shape, bf16),
            shape((d_fields[0].shape[2], width), bf16),
            shape((count, width), f32),
            shape((16, width), f32),
        ],
        scratch_shapes=[
            pltpu.VMEM((total, rows, cols), bf16),
            pltpu.VMEM((total, rows, cols), bf16),
            pltpu.VMEM(rows_t.shape, bf16),
            pltpu.VMEM(d_fields[0].shape, bf16),
            pltpu.VMEM(d_fields[1].shape, bf16),
            pltpu.VMEM(weights[0].shape, bf16),
            pltpu.VMEM(weights[1].shape, bf16),
            pltpu.VMEM(tokens.shape, bf16),
            pltpu.VMEM(context.shape, bf16),
            pltpu.VMEM(given.shape, f32),
            pltpu.SemaphoreType.DMA((8,)),
            pltpu.VMEM((KEY_ROWS, width), f32),
            pltpu.VMEM((2 * EDGE, width), bf16),
            pltpu.VMEM((2 * EDGE, width), bf16),
            pltpu.SemaphoreType.DMA((2,)),
            pltpu.SemaphoreType.DMA((2,)),
            pltpu.VMEM((8, width), f32),
            pltpu.VMEM((8, 16, width), bf16),
            pltpu.VMEM((4 + 2 * len(exchange.extra), 16, width), bf16),
            pltpu.SemaphoreType.DMA((8, 2)),
            pltpu.SemaphoreType.DMA((4 + len(exchange.extra), 2)),
        ]
        + exchange.scratch(),
        compiler_params=pltpu.CompilerParams(
            collective_id=1, has_side_effects=True, vmem_limit_bytes=67043328
        ),
        name="leave",
        cost_estimate=pl.CostEstimate(
            flops=40 * 10**9, bytes_accessed=40 * 10**6, transcendentals=0
        ),
    )(
        rows_t, mine, *crossed, *d_fields, *weights, tokens, context, given, small, small2
    )


def finish_kernel(rows_ref, got_ref, tokens_ref, vectors_ref, dmid_ref, out_ref):
    clean = pl.program_id(0) >= pl.num_programs(0) // 2
    got = jnp.where(clean, got_ref[...].astype(f32), 0.0)
    unit, scale = normal(tokens_ref[...].astype(f32))
    lean = (rows_ref[...] + got) * vectors_ref[0:1, :]
    out_ref[...] = dmid_ref[...] + scale * (
        lean
        - jnp.mean(lean, axis=-1, keepdims=True)
        - unit * jnp.mean(lean * unit, axis=-1, keepdims=True)
    )


def finish(rows, got, tokens, vectors, d_mid):
    count, width = rows.shape
    spec = pl.BlockSpec((ROW_TILE, width), lambda b: (b, 0))
    half = count // ROW_TILE // 2
    return pl.pallas_call(
        finish_kernel,
        grid=(count // ROW_TILE,),
        in_specs=[
            spec,
            pl.BlockSpec((ROW_TILE, width), lambda b: (jnp.maximum(b - half, 0), 0)),
            spec,
            pl.BlockSpec(vectors.shape, lambda b: (0, 0)),
            spec,
        ],
        out_specs=spec,
        out_shape=jax.ShapeDtypeStruct((count, width), f32),
        name="finish",
        cost_estimate=pl.CostEstimate(
            flops=10**7, bytes_accessed=12 * 10**6, transcendentals=0
        ),
    )(rows, got, tokens, vectors, d_mid)


def assemble_kernel(
    core_ref, down_mine, up_mine, down_got, up_got, qkv_low, out_low, down_ref, up_ref, qkv_ref, out_ref
):
    qkv_ref[...] = qkv_low[...].astype(f32)
    out_ref[...] = out_low[...].astype(f32)
    core = core_ref[0]
    block = down_mine.shape[1]
    lanes = up_ref.shape[1]
    parts = down_mine.shape[2] // lanes
    deep = block * parts
    for side, down, up in ((core, down_mine, up_mine), (1 - core, down_got, up_got)):
        rows = pl.ds(pl.multiple_of(side * block, block), block)
        down_ref[rows, :] = down[0].astype(f32)
        for n in range(block // PIECES):
            for c in range(parts):
                at = side * deep + (n * parts + c) * PIECES
                rows = pl.ds(pl.multiple_of(at, PIECES), PIECES)
                piece = up[0, n * PIECES : (n + 1) * PIECES, c * lanes : (c + 1) * lanes]
                up_ref[rows, :] = piece.astype(f32)


def assemble(core, gathered, moved, qkv, out):
    tiles, half, width = gathered.shape
    count = tiles // 2
    down_spec = pl.BlockSpec((1, half, width), lambda k, c: (k, 0, 0))
    up_spec = pl.BlockSpec((1, half, width), lambda k, c: (count + k, 0, 0))
    hidden = count * 2 * half
    qkv_spec = pl.BlockSpec((qkv.shape[0] // count, qkv.shape[1]), lambda k, c: (k, 0))
    out_spec = pl.BlockSpec((out.shape[0] // count, out.shape[1]), lambda k, c: (k, 0))
    return pl.pallas_call(
        assemble_kernel,
        grid_spec=pltpu.PrefetchScalarGridSpec(
            num_scalar_prefetch=1,
            grid=(count,),
            in_specs=[down_spec, up_spec, down_spec, up_spec, qkv_spec, out_spec],
            out_specs=[
                pl.BlockSpec((2 * half, width), lambda k, c: (k, 0)),
                pl.BlockSpec((width, 2 * half), lambda k, c: (0, k)),
                qkv_spec,
                out_spec,
            ],
        ),
        out_shape=[
            jax.ShapeDtypeStruct((hidden, width), f32),
            jax.ShapeDtypeStruct((width, hidden), f32),
            jax.ShapeDtypeStruct(qkv.shape, f32),
            jax.ShapeDtypeStruct(out.shape, f32),
        ],
        name="assemble",
        cost_estimate=pl.CostEstimate(
            flops=10**6, bytes_accessed=14 * 10**6, transcendentals=0
        ),
    )(core, gathered, gathered, moved, moved, qkv, out)


def key_layout(seq_lengths, block_len, part):
    index = jnp.arange(KEY_ROWS, dtype=jnp.int32)
    own = part * HALF
    token = jnp.where(
        index < NOISY_BASE, index + (own - HALF), index - NOISY_BASE + (own - EDGE)
    )
    ends = jnp.cumsum(seq_lengths)
    passed = token[:, None] >= ends[None, :]
    starts = jnp.sum(jnp.where(passed, seq_lengths[None, :], 0), axis=1)
    lengths_here = jnp.where(passed, 0, ends[None, :])
    stops = jnp.min(jnp.where(passed, TOK_DEV, lengths_here), axis=1)
    positions = token - starts
    block_start = starts + positions // block_len * block_len
    block_stop = jnp.minimum(block_start + block_len, stops)
    mine = slice(CLEAN_OWN, CLEAN_OWN + HALF)
    low, start, stop = starts[mine], block_start[mine], block_stop[mine]
    to_clean = own - HALF
    tiles = lambda column: column.reshape(TILES, 1, TILE)
    clean_bounds = jnp.concatenate(
        [
            jnp.concatenate([tiles(low - to_clean), tiles(low - to_clean)], axis=2),
            jnp.concatenate([tiles(start - to_clean), tiles(stop - to_clean)], axis=2),
        ],
        axis=1,
    )
    to_window = own - EDGE + TILE * jnp.arange(TILES, dtype=jnp.int32)[:, None, None]
    noisy_bounds = jnp.concatenate(
        [tiles(start) - to_window, tiles(stop) - to_window], axis=1
    )
    first = jnp.min(clean_bounds[:, 0], axis=1) // EDGE * EDGE
    last = jnp.max(clean_bounds[:, 1], axis=1)
    trips = (last - first + KEY_TILE - 1) // KEY_TILE
    spans = jnp.stack([first, trips], axis=1)
    lane = jnp.arange(LANES, dtype=jnp.int32)
    frequency = jnp.exp(
        (lane % (HD // 2)).astype(f32) * (-math.log(10000.0) / (HD // 2))
    )
    angles = positions.astype(f32)[:, None] * frequency[None, :]
    sign = jnp.where(lane % HD < HD // 2, -1.0, 1.0)
    return spans, clean_bounds, noisy_bounds, jnp.cos(angles), jnp.sin(angles) * sign


def in_order(bit, mine, theirs, axis=0):
    order = bit == 0
    return jnp.concatenate(
        [jnp.where(order, mine, theirs), jnp.where(order, theirs, mine)], axis=axis
    )


def tie(first, second):
    return lax.optimization_barrier((first, second))


def local(
    dp_size,
    tokens,
    lengths,
    block_size,
    cotangent,
    ln1_gain,
    ln1_bias,
    w_qkv,
    w_out,
    ln2_gain,
    ln2_bias,
    w_up,
    b_up,
    w_down,
    b_down,
):
    width = tokens.shape[2]
    part = lax.axis_index("mp")
    place = lax.axis_index("dp")
    bits = dp_size.bit_length() - 1
    core = place & 1

    def across(array):
        return lax.ppermute(array, "mp", [(0, 1), (1, 0)])

    def sibling(array):
        return lax.ppermute(array, "dp", [(i, i ^ 1) for i in range(dp_size)])

    def beside(array):
        return lax.ppermute(array, "dp", [(i, i ^ 2) for i in range(dp_size)])

    edge = jnp.where(part == 0, tokens[0, HALF - EDGE :], tokens[0, :EDGE])
    context = across(jnp.concatenate([tokens[1], edge], axis=0))
    qkv_mine = w_qkv.transpose(1, 0, 2)
    side = (place >> 1) & 1

    def quarter_of(array, axis=0):
        size = array.shape[axis] // 4
        return lax.dynamic_slice_in_dim(array, (2 * core + side) * size, size, axis)

    def half_of(array):
        size = array.shape[0] // 2
        return lax.dynamic_slice_in_dim(array, core * size, size, 0)

    quarters = [quarter_of(qkv_mine, 1), quarter_of(w_up), half_of(w_down), half_of(w_out)]
    layout = key_layout(lengths[0], block_size[0], part)
    vectors = jnp.stack([ln1_gain, ln1_bias, ln2_gain, ln2_bias, b_down])
    context, (quarters, layout, vectors) = tie(context, (quarters, layout, vectors))
    qkv_here, up_here, down_here, out_here = [across(piece) for piece in quarters]

    spans, clean_bounds, noisy_bounds, cosine, sine = layout
    normed1, normed1_t, *fields = enter(tokens, context, vectors, qkv_mine, cosine, sine)
    qkv_here, fields = tie(qkv_here, fields)
    qkv_beside = beside(qkv_here)
    mine = [*fields, *attend_forward(spans, clean_bounds, noisy_bounds, *fields)]
    (qkv_here, qkv_beside, up_here, out_here), _ = tie(
        (qkv_here, qkv_beside, up_here, out_here), mine[3]
    )
    out_there = sibling(out_here)
    qkv_half = in_order(side, qkv_here, qkv_beside, axis=1)
    qkv_other = in_order(core, qkv_half, sibling(qkv_half), axis=1)
    up_beside = beside(up_here)
    fields = project(normed1, qkv_other, cosine, sine)
    (out_here, out_there), fields = tie((out_here, out_there), fields)
    out_other = in_order(core, out_here, out_there)
    out_other, fields = tie(out_other, fields)
    other = [*fields, *attend_forward(spans, clean_bounds, noisy_bounds, *fields)]
    (up_here, up_beside, down_here), _ = tie((up_here, up_beside, down_here), other[3])
    bias_all = b_up.astype(f32).reshape(-1, 1, HIDDEN_TILE)

    x_rows = tokens.reshape(TOK_DEV, width)
    out, d_mid, d_att, d_att2, grad_out, grad_out2, grad_bias, norms, pieces = middle(
        bits,
        x_rows,
        mine[3],
        other[3],
        w_out,
        out_other,
        cotangent.reshape(TOK_DEV, width),
        vectors,
        bias_all,
        (w_up, up_here, up_beside),
        (w_down, down_here),
    )
    hidden = b_up.shape[0]

    crossed_out = across(grad_out2)
    spread = [(b, min(2, min(bits, 4) - b)) for b in range(2, min(bits, 4), 2)]
    gathered = pieces
    ((first_bit, n),) = spread
    moved = [
        lax.ppermute(gathered, "dp", [(i, i ^ (k << first_bit)) for i in range(dp_size)])
        for k in range(1, 1 << n)
    ]

    def backward(saved, d_attended, spans, *rest):
        query, keys, values, attended, lse = saved
        return attend_backward(
            spans,
            clean_bounds,
            noisy_bounds,
            query,
            keys,
            values,
            attended,
            d_attended,
            lse,
            cosine,
            sine,
            rest,
        )

    d_fields2, grad2 = backward(other, d_att2, spans, normed1_t)
    grad2 = grad2.reshape(-1, ROW_TILE, grad2.shape[2])
    low_bit, high_bit = (place >> 2) & 1, (place >> 3) & 1
    moved, _ = tie(moved, grad2)
    gathered = in_order(
        high_bit,
        in_order(low_bit, gathered, moved[0], 1),
        in_order(low_bit, moved[1], moved[2], 1),
        1,
    )
    half = ROW_TILE // 2
    part_of = lambda array, which: lax.dynamic_slice_in_dim(array, which * half, half, 1)
    got = sibling(part_of(grad2, 1 - core))
    crossing = (part_of(grad2, core).astype(f32) + got.astype(f32)).astype(bf16)
    (crossing, gathered), spans = tie((crossing, gathered), spans)
    crossed = across(crossing)
    moved = beside(gathered)
    d_fields1, given, give = backward(mine, d_att, spans, d_fields2, qkv_mine, qkv_other)
    took = across(give)
    moved, d_fields1 = tie(moved, d_fields1)
    gathered = in_order(side, gathered, moved, 1)
    gathered, d_fields1 = tie(gathered, d_fields1)
    moved = sibling(gathered)
    lead = hidden // width
    bias2, bias1 = grad_bias.reshape(2, lead, width)
    shared = jnp.concatenate([norms[:3], jnp.zeros((2, width), f32)], axis=0)
    grad_qkv, grad_out, d_rows, sums = leave(
        bits,
        normed1_t,
        grad_out,
        (crossed, crossed_out),
        (d_fields1, d_fields2),
        (qkv_mine, qkv_other),
        x_rows,
        context,
        given,
        jnp.concatenate([bias1, shared], axis=0),
        jnp.concatenate([bias2, shared], axis=0),
    )
    (moved, took), grad_qkv = tie((moved, took), grad_qkv)
    grad_tokens = finish(d_rows, took, x_rows, vectors, d_mid)
    grad_down, grad_up, grad_qkv, grad_out = assemble(
        core.reshape(1), gathered, moved, grad_qkv.reshape(-1, grad_qkv.shape[2]), grad_out
    )
    return (
        out.reshape(tokens.shape),
        grad_tokens.reshape(tokens.shape),
        sums[lead + 3],
        sums[lead + 4],
        grad_qkv.reshape(qkv_mine.shape).transpose(1, 0, 2),
        grad_out,
        sums[lead],
        sums[lead + 1],
        grad_up,
        sums[:lead].reshape(hidden),
        grad_down,
        sums[lead + 2],
    )


def solution(mesh):
    in_specs = (
        P(None, ("dp", "mp"), None),
        P("dp", None),
        P(),
        P(None, ("dp", "mp"), None),
        P(),
        P(),
        P(None, None, "mp"),
        P("mp", None),
        P(),
        P(),
        P(None, "mp"),
        P("mp"),
        P("mp", None),
        P(),
    )
    out_specs = (
        P(None, ("dp", "mp"), None),
        P(None, ("dp", "mp"), None),
        P(),
        P(),
        P(None, None, "mp"),
        P("mp", None),
        P(),
        P(),
        P(None, "mp"),
        P("mp"),
        P("mp", None),
        P(),
    )
    return jax.shard_map(
        functools.partial(local, mesh.shape["dp"]),
        mesh=mesh,
        in_specs=in_specs,
        out_specs=out_specs,
        check_vma=False,
    )
```
